32 devices in a mesh: dp: 16 (over z, x, core), tensor: 2 (over y).
Axes of the slice: x: 2, y: 2, z: 4, core: 2. Of those that a mesh axis runs over, the one named last changes fastest.
Arguments:
- tokens: bfloat16 [16384, 1024], P('dp'), may hold values from -6 to 6
- lengths: int32 [16, 8], replicated, may hold values from 1 to 384, 768 in all within a row
- pairing: int32 [16, 8], P('dp', 'tensor'), may hold values from 0 to 127
- w_qkv: bfloat16 [3, 1024, 1024], P(None, 'dp', 'tensor'), may hold values from -0.1875 to 0.1875
- b_qv: bfloat16 [2, 1024], P(None, 'tensor'), may hold values from -3 to 3
- w_out: bfloat16 [1024, 1024], P('tensor', 'dp'), may hold values from -0.5 to 0.5
- b_out: bfloat16 [1024], replicated, may hold values from -3 to 3
- ln_gain: bfloat16 [2, 1024], replicated, may hold values from 0.5 to 1.5
- ln_bias: bfloat16 [2, 1024], replicated, may hold values from -3 to 3
- w_up: bfloat16 [1024, 4096], P('dp', 'tensor'), may hold values from -0.1875 to 0.1875
- b_up: bfloat16 [4096], P('tensor'), may hold values from -3 to 3
- w_down: bfloat16 [4096, 1024], P('tensor', 'dp'), may hold values from -0.09375 to 0.09375
- b_down: bfloat16 [1024], replicated, may hold values from -3 to 3
- w_proj: bfloat16 [1024, 128], replicated, may hold values from -0.1875 to 0.1875
- cot: bfloat16 [16384, 1024], P(('dp', 'tensor')), may hold values from -6 to 6
Outputs:
- y_out: bfloat16 [16384, 1024], P(('dp', 'tensor'))
- loss: float32 [16, 8], P('dp', 'tensor')
- x_grad: bfloat16 [16384, 1024], P(('dp', 'tensor'))
- w_qkv_grad: float32 [3, 1024, 1024], P(None, 'dp', 'tensor')
- b_qv_grad: float32 [2, 1024], P(None, 'tensor')
- w_out_grad: float32 [1024, 1024], P('tensor', 'dp')
- b_out_grad: float32 [1024], replicated
- ln_gain_grad: float32 [2, 1024], replicated
- ln_bias_grad: float32 [2, 1024], replicated
- w_up_grad: float32 [1024, 4096], P('dp', 'tensor')
- b_up_grad: float32 [4096], P('tensor')
- w_down_grad: float32 [4096, 1024], P('tensor', 'dp')
- b_down_grad: float32 [1024], replicated
- w_proj_grad: float32 [1024, 128], replicated
The draws below stay inside these ranges and needn't reach their ends.
Inputs may be any that keep to these rules, and one draw needn't show every extreme that they name: lengths[r] are the token counts of row r's 8 documents, which follow its 8 queries of 32 tokens; each row sums to 768 and its largest is 384. pairing[r, q] numbers a document over all rows: its row times 8 plus its place in that row.
All inputs are finite; a program needn't handle non-finite values.
Results may differ from the reference program's by a relative error of at most 0.02.
Values may be sent and summed in bfloat16 or wider, within the bound.
No kernel may reach another device: no remote copies, remote signals or barrier semaphores. Data moves between devices by JAX's collectives and lax.ppermute only.
A program may use at most 192 MiB of HBM per device.

```python
import math
import jax
import jax.numpy as jnp
import numpy as np
from jax import lax

D = 1024
HEADS = 16
HEAD_DIM = 64
FF = 4096
PROJ = 128
TOK_DEV = 1024
QLEN = 32
NQ_ROW = 8
NDOC = 8
ROWS = 16
TOKENS = 16384
DOCS = 128
DOC_MOST = 384


def with_ends(drawn, key, least, high):
    longest = drawn.shape.index(max(drawn.shape))
    spots = []
    for shift in (0, 1):
        where = [jax.random.randint(jax.random.fold_in(key, axis), (), 0, length) for axis, length in enumerate(drawn.shape)]
        where[longest] = (where[longest] + shift) % drawn.shape[longest]
        spots.append(tuple(where))
    return drawn.at[spots[0]].set(least).at[spots[1]].set(high)


def level_of(own_key, extent, pieces, least, top_value):
    level, own = 1.0, jax.random.fold_in(own_key, 6)
    for axis_at, blocks in pieces:
        steps = jnp.exp(jax.random.uniform(jax.random.fold_in(own, axis_at), (blocks,), jnp.float32, least / len(pieces), top_value / len(pieces)))
        level = level * jnp.repeat(steps, extent[axis_at] // blocks).reshape([-1 if axis == axis_at else 1 for axis in range(len(extent))])
    return level


def profile(number_of, total, reach, lean):
    weights = [(1 << 20) // math.isqrt(grade ** lean) + 1 for grade in range(2, number_of + 1)]
    rest, given = total - reach - (number_of - 1), [1] * (number_of - 1)
    while rest > 0:
        candidates = [i for i in range(number_of - 1) if given[i] < reach]
        mass, budget = sum([weights[i] for i in candidates]), rest
        for i in candidates:
            addition = min(reach - given[i], max(1, budget * weights[i] // mass), rest)
            given[i] = given[i] + addition
            rest = rest - addition
    return np.array([reach] + given)


def ragged_sizes(key, amount, total, most, skew):
    if amount == 2:
        one = jax.random.randint(key, (), max(1, total - most), min(most, total - 1) + 1)
        return jnp.stack([one, total - one])
    sizes = jnp.asarray(profile(amount, total, most, skew), jnp.int32)
    twos = (amount - 1) // 2
    giver, sink = sizes[1:1 + 2 * twos:2], sizes[2:2 + 2 * twos:2]
    slack = jnp.minimum(giver - 1, most - sink)
    shifted = jax.random.randint(jax.random.fold_in(key, 1), (twos,), 0, 1 << 20) % (slack + 1)
    sizes = sizes.at[1:1 + 2 * twos:2].set(giver - shifted).at[2:2 + 2 * twos:2].set(sink + shifted)
    return sizes[jax.random.permutation(jax.random.fold_in(key, 2), amount)]


def noise(own_key, extent, scale, bound, split=(), kind=jnp.bfloat16):
    level = level_of(own_key, extent, split, -0.22, 0.18) if split else 1.0
    values = jax.random.normal(own_key, extent, jnp.float32) * scale * level
    return jnp.minimum(jnp.maximum(values, -bound), bound).astype(kind)


def setup_inputs(seed: int = 0) -> dict:
    key_of = jax.random.split(jax.random.key(seed), 16)
    return {
        "tokens": noise(key_of[0], (TOKENS, D), 1.0, 6.0, ((0, 16),)),
        "lengths": jax.vmap(lambda own: ragged_sizes(own, NDOC, TOK_DEV - NQ_ROW * QLEN, DOC_MOST, 2))(jax.random.split(key_of[1], ROWS)).reshape((ROWS, NDOC)).astype(jnp.int32),
        "pairing": with_ends(jax.random.randint(key_of[2], (ROWS, NQ_ROW), 0, DOCS), jax.random.fold_in(key_of[2], 1), 0, DOCS - 1).astype(jnp.int32),
        "w_qkv": noise(key_of[3], (3, D, D), D ** -0.5, 0.1875, ((1, 16), (2, 2))),
        "b_qv": noise(key_of[4], (2, D), 0.5, 3.0, ((1, 2),)),
        "w_out": noise(key_of[5], (D, D), (D // 8) ** -0.5, 0.5, ((0, 2), (1, 16))),
        "b_out": noise(key_of[6], (D,), 0.5, 3.0),
        "ln_gain": jnp.clip(1.0 + 0.1 * jax.random.normal(key_of[7], (2, D), jnp.float32), 0.5, 1.5).astype(jnp.bfloat16),
        "ln_bias": noise(key_of[8], (2, D), 0.5, 3.0),
        "w_up": noise(key_of[9], (D, FF), D ** -0.5, 0.1875, ((0, 16), (1, 2))),
        "b_up": noise(key_of[10], (FF,), 0.5, 3.0, ((0, 2),)),
        "w_down": noise(key_of[11], (FF, D), FF ** -0.5, 0.09375, ((0, 2), (1, 16))),
        "b_down": noise(key_of[12], (D,), 0.5, 3.0),
        "w_proj": noise(key_of[13], (D, PROJ), D ** -0.5, 0.1875),
        "cot": noise(key_of[14], (TOKENS, D), 1.0, 6.0, ((0, 32),)),
    }


EPS_NORM = 1e-05
EPS_EMBED = 1e-06
POOL_TEMP = 0.1
LOSS_TEMP = 0.1
FULL_PRECISION = lax.Precision.HIGHEST
MASKED_SCORE = -1e+30

@jax.custom_vjp
def low(v):
    return lax.optimization_barrier(v.astype(jnp.bfloat16)).astype(jnp.float32)

@jax.custom_vjp
def low_back(v):
    return v

def low_keep(v):
    return (low(v), None)

def low_pass(kept, grad):
    return (grad,)

def back_keep(v):
    return (v, None)

def back_low(kept, grad):
    return (low(grad),)
low.defvjp(low_keep, low_pass)
low_back.defvjp(back_keep, back_low)

def matmul(left, right):
    return jnp.dot(left, right, precision=FULL_PRECISION, preferred_element_type=jnp.float32)

def layer_norm(value, gain, shift):
    centred = value - lax.optimization_barrier(jnp.mean(value, axis=-1, keepdims=True))
    variance = lax.optimization_barrier(jnp.mean(centred * centred, axis=-1, keepdims=True))
    return centred * lax.rsqrt(variance + EPS_NORM) * gain + shift

def segments_of(row_lengths):
    position = jnp.arange(TOK_DEV, dtype=jnp.int32)
    query_span = NQ_ROW * QLEN
    ends = jnp.cumsum(row_lengths).astype(jnp.int32)
    passed = lax.optimization_barrier(jnp.sum((position[:, None] - query_span >= ends[None, :]).astype(jnp.int32), axis=1))
    return jnp.where(position < query_span, position // QLEN, NQ_ROW + passed).astype(jnp.int32)

def split_heads(value):
    return value.reshape(TOK_DEV, HEADS, HEAD_DIM)

def layer_row(x_row, segments, weights):
    w_qkv, b_qv, w_out, b_out, ln_gain, ln_bias, w_up, b_up, w_down, b_down = weights
    queries = low_back(low(matmul(x_row, w_qkv[0]) + b_qv[0]))
    keys_all = low_back(low(matmul(x_row, w_qkv[1])))
    values_all = low_back(low(matmul(x_row, w_qkv[2]) + b_qv[1]))
    scores = jnp.einsum('qhd,khd->hqk', split_heads(queries), split_heads(keys_all), precision=FULL_PRECISION) * HEAD_DIM ** (-0.5)
    scores = low_back(scores)
    same_segment = segments[:, None] == segments[None, :]
    scores = jnp.where(same_segment[None], scores, MASKED_SCORE)
    probs = jax.nn.softmax(scores, axis=-1)
    mixed = jnp.einsum('hqk,khd->qhd', low(probs), split_heads(values_all), precision=FULL_PRECISION)
    heads_out = low_back(low(mixed.reshape(TOK_DEV, D)))
    attended = low_back(matmul(heads_out, w_out) + b_out)
    normed = layer_norm(x_row + attended, ln_gain[0], ln_bias[0])
    up_value = low_back(matmul(low(normed), w_up) + b_up)
    activation = low(jax.nn.gelu(up_value, approximate=False))
    ffn_out = low_back(matmul(activation, w_down) + b_down)
    return layer_norm(normed + ffn_out, ln_gain[1], ln_bias[1])

def pooled_scores(normed_all, queries, doc_ids, sizes):

    def one_row(query_block):
        similar = low_back(jnp.einsum('qlw,tw->qlt', query_block, normed_all, precision=FULL_PRECISION))
        expo = jnp.exp(similar / POOL_TEMP)
        totals = jax.ops.segment_sum(jnp.moveaxis(expo, 2, 0), doc_ids, num_segments=DOCS + 1)[:DOCS]
        pooled = POOL_TEMP * jnp.log(totals / sizes[:, None, None])
        return lax.optimization_barrier(jnp.sum(pooled, axis=2)).T
    return lax.map(jax.checkpoint(one_row), queries).reshape(ROWS * NQ_ROW, DOCS)

def forward(x_all, w_qkv, b_qv, w_out, b_out, ln_gain, ln_bias, w_up, b_up, w_down, b_down, w_proj, segments, doc_ids, sizes, pairs):
    weights = (w_qkv, b_qv, w_out, b_out, ln_gain, ln_bias, w_up, b_up, w_down, b_down)

    def one_layer(inputs):
        return layer_row(inputs[0], inputs[1], weights)
    outputs = lax.map(jax.checkpoint(one_layer), (x_all.reshape(ROWS, TOK_DEV, D), segments))
    embed = low(matmul(low(outputs.reshape(TOKENS, D)), w_proj))
    total_loss = jnp.zeros((ROWS * NQ_ROW,), jnp.float32)
    for width in (PROJ, 3 * PROJ // 4, PROJ // 2):
        part = embed[:, :width]
        normed_all = low(part * lax.rsqrt(lax.optimization_barrier(jnp.sum(part * part, axis=1, keepdims=True)) + EPS_EMBED))
        queries = normed_all.reshape(ROWS, TOK_DEV, width)[:, :NQ_ROW * QLEN].reshape(ROWS, NQ_ROW, QLEN, width)
        logits = pooled_scores(normed_all, queries, doc_ids, sizes) / LOSS_TEMP
        target = jnp.take_along_axis(logits, pairs[:, None], axis=1)[:, 0]
        total_loss = total_loss + jax.nn.logsumexp(logits, axis=1) - target
    return (outputs.reshape(TOKENS, D), total_loss.reshape(ROWS, NQ_ROW))

def reference(tokens, lengths, pairing, w_qkv, b_qv, w_out, b_out, ln_gain, ln_bias, w_up, b_up, w_down, b_down, w_proj, cot):
    segments = jax.vmap(segments_of)(lengths)
    row_base = (jnp.arange(ROWS, dtype=jnp.int32) * NDOC)[:, None]
    doc_ids = jnp.where(segments >= NQ_ROW, row_base + segments - NQ_ROW, DOCS).reshape(-1).astype(jnp.int32)
    sizes = lengths.reshape(-1).astype(jnp.float32)
    pairs = pairing.reshape(-1).astype(jnp.int32)
    floats = tuple((array.astype(jnp.float32) for array in (tokens, w_qkv, b_qv, w_out, b_out, ln_gain, ln_bias, w_up, b_up, w_down, b_down, w_proj)))

    def objective(*params):
        return forward(*params, segments, doc_ids, sizes, pairs)
    (outputs, losses), pullback = jax.vjp(objective, *floats)
    grads = pullback((cot.astype(jnp.float32), jnp.ones_like(losses)))
    return (outputs.astype(jnp.bfloat16), losses, grads[0].astype(jnp.bfloat16), grads[1], grads[2], grads[3], grads[4], grads[5], grads[6], grads[7], grads[8], grads[9], grads[10], grads[11])
```

```python
from functools import partial

import jax
import jax.numpy as jnp
from jax import lax
from jax.experimental import pallas as pl
from jax.experimental.pallas import tpu as pltpu
from jax.sharding import Mesh, PartitionSpec as P

HEAD_DIM = 64
QLEN = 32
NQ_ROW = 8
NDOC = 8


EPS_NORM = 1e-05
EPS_EMBED = 1e-06
POOL_TEMP = 0.1
LOSS_TEMP = 0.1
FULL_PRECISION = lax.Precision.HIGHEST
MASKED_SCORE = -1e30


def shortened(shard):

    def short(part):
        return part.astype(jnp.bfloat16) if part.dtype == jnp.float32 else part

    return jax.tree.map(short, shard)


def contract_rows(left, right, precision=None):
    return lax.dot_general(
        left,
        right,
        (((0,), (0,)), ((), ())),
        precision=precision,
        preferred_element_type=jnp.float32,
    )


def contract_cols(left, right, precision=None):
    return lax.dot_general(
        left,
        right,
        (((1,), (1,)), ((), ())),
        precision=precision,
        preferred_element_type=jnp.float32,
    )


def norm_forward(value, gain, shift):
    centred = value - jnp.mean(value, axis=1, keepdims=True)
    rstd = lax.rsqrt(jnp.mean(centred * centred, axis=1, keepdims=True) + EPS_NORM)
    unit = centred * rstd
    return (unit * gain + shift, unit, rstd)


def norm_backward(grad, unit, rstd, gain):
    scaled = grad * gain
    return rstd * (
        scaled
        - jnp.mean(scaled, axis=1, keepdims=True)
        - unit * jnp.mean(scaled * unit, axis=1, keepdims=True)
    )


def segments_of(row_lengths, token_count):
    position = jnp.arange(token_count, dtype=jnp.int32)
    query_span = NQ_ROW * QLEN
    ends = jnp.cumsum(row_lengths)
    passed = jnp.sum((position[:, None] - query_span >= ends[None, :]).astype(jnp.int32), axis=1)
    return jnp.where(position < query_span, position // QLEN, NQ_ROW + passed)


def normalize_cut(raw, width):
    part = raw[:, :width]
    scale = lax.rsqrt(jnp.sum(part * part, axis=1, keepdims=True) + EPS_EMBED)
    return (part * scale, part, scale)


def normalize_back(grad, part, scale, full_width):
    result = scale * grad - part * (scale * scale * scale) * jnp.sum(
        part * grad, axis=1, keepdims=True
    )
    return jnp.pad(result, ((0, 0), (0, full_width - grad.shape[1])))


def masked_scores(query_block, key_rows, block_segments, segments):
    scores = jnp.einsum(
        "qhd,khd->hqk", query_block, key_rows, preferred_element_type=jnp.float32
    ) * HEAD_DIM ** (-0.5)
    return jnp.where((block_segments[:, None] == segments[None, :])[None], scores, MASKED_SCORE)


def attend_forward(query_rows, key_rows, value_rows, segments, block_rows):
    token_count = query_rows.shape[0]

    def one_block(block_start):
        query_block = lax.dynamic_slice_in_dim(query_rows, block_start, block_rows, 0)
        block_segments = lax.dynamic_slice_in_dim(segments, block_start, block_rows, 0)
        scores = masked_scores(query_block, key_rows, block_segments, segments)
        highest = jnp.max(scores, axis=2, keepdims=True)
        expo = jnp.exp(scores - highest)
        totals = jnp.sum(expo, axis=2, keepdims=True)
        weights = (expo / totals).astype(jnp.bfloat16)
        mixed = jnp.einsum("hqk,khd->qhd", weights, value_rows, preferred_element_type=jnp.float32)
        return (mixed.astype(jnp.bfloat16), (highest + jnp.log(totals))[:, :, 0])

    starts = jnp.arange(token_count // block_rows, dtype=jnp.int32) * block_rows
    mixed, log_totals = lax.map(one_block, starts)
    return (mixed.reshape(token_count, -1), log_totals)


def attend_backward(query_rows, key_rows, value_rows, segments, log_totals, grad_mixed, block_rows):
    token_count, local_heads, head_size = query_rows.shape
    scale = HEAD_DIM ** (-0.5)
    grad_heads = grad_mixed.reshape(token_count, local_heads, head_size)

    def one_block(carried, inputs):
        grad_keys, grad_values = carried
        block_start, block_lse = inputs
        query_block = lax.dynamic_slice_in_dim(query_rows, block_start, block_rows, 0)
        grad_block = lax.dynamic_slice_in_dim(grad_heads, block_start, block_rows, 0)
        block_segments = lax.dynamic_slice_in_dim(segments, block_start, block_rows, 0)
        scores = masked_scores(query_block, key_rows, block_segments, segments)
        probs = jnp.exp(scores - block_lse[:, :, None])
        grad_probs = jnp.einsum(
            "qhd,khd->hqk", grad_block, value_rows, preferred_element_type=jnp.float32
        )
        inner = jnp.sum(probs * grad_probs, axis=2, keepdims=True)
        grad_scores = (probs * (grad_probs - inner)).astype(jnp.bfloat16)
        grad_query = (
            jnp.einsum("hqk,khd->qhd", grad_scores, key_rows, preferred_element_type=jnp.float32)
            * scale
        )
        grad_keys = (
            grad_keys
            + jnp.einsum(
                "hqk,qhd->khd", grad_scores, query_block, preferred_element_type=jnp.float32
            )
            * scale
        )
        grad_values = grad_values + jnp.einsum(
            "hqk,qhd->khd",
            probs.astype(jnp.bfloat16),
            grad_block,
            preferred_element_type=jnp.float32,
        )
        return ((grad_keys, grad_values), grad_query)

    starts = jnp.arange(token_count // block_rows, dtype=jnp.int32) * block_rows
    zero_rows = jnp.zeros(key_rows.shape, jnp.float32)
    (grad_keys, grad_values), grad_queries = lax.scan(
        one_block, (zero_rows, zero_rows), (starts, log_totals)
    )
    flat_width = local_heads * head_size
    return (
        grad_queries.reshape(token_count, flat_width),
        grad_keys.reshape(token_count, flat_width),
        grad_values.reshape(token_count, flat_width),
    )


def local(
    tokens,
    lengths,
    pairing,
    w_qkv,
    b_qv,
    w_out,
    b_out,
    ln_gain,
    ln_bias,
    w_up,
    b_up,
    w_down,
    b_down,
    w_proj,
    cot,
):
    tensor_count = lax.axis_size("tensor")
    tensor_index = lax.axis_index("tensor")
    data_index = lax.axis_index("dp")
    token_count = tokens.shape[0]
    share_rows = token_count // tensor_count
    block_rows = min(512, token_count)
    own_start = tensor_index * share_rows
    full_qkv, full_out, full_up, full_down = (
        lax.all_gather(w_qkv, "dp", axis=1, tiled=True),
        lax.all_gather(w_out, "dp", axis=1, tiled=True),
        lax.all_gather(w_up, "dp", axis=0, tiled=True),
        lax.all_gather(w_down, "dp", axis=1, tiled=True),
    )
    head_width = full_qkv.shape[2]
    local_heads = head_width // HEAD_DIM
    row_lengths = lax.dynamic_index_in_dim(lengths, data_index, 0, keepdims=False)
    segments = segments_of(row_lengths, token_count)
    projected = jnp.einsum("td,kdw->ktw", tokens, full_qkv, preferred_element_type=jnp.float32)
    qv_bias = b_qv.astype(jnp.float32)
    query_rows = (
        (projected[0] + qv_bias[0]).astype(jnp.bfloat16).reshape(token_count, local_heads, HEAD_DIM)
    )
    key_rows = projected[1].astype(jnp.bfloat16).reshape(token_count, local_heads, HEAD_DIM)
    value_rows = (
        (projected[2] + qv_bias[1]).astype(jnp.bfloat16).reshape(token_count, local_heads, HEAD_DIM)
    )
    mixed, log_totals = attend_forward(query_rows, key_rows, value_rows, segments, block_rows)
    attn_terms = jnp.dot(mixed, full_out, preferred_element_type=jnp.float32)
    attn_sum = lax.psum_scatter(
        attn_terms.astype(jnp.bfloat16), "tensor", scatter_dimension=0, tiled=True
    ).astype(jnp.float32)
    own_tokens = lax.dynamic_slice_in_dim(tokens, own_start, share_rows, 0).astype(jnp.float32)
    gains = ln_gain.astype(jnp.float32)
    shifts = ln_bias.astype(jnp.float32)
    normed, unit_one, rstd_one = norm_forward(
        own_tokens + attn_sum + b_out.astype(jnp.float32), gains[0], shifts[0]
    )
    normed_all = lax.all_gather(normed.astype(jnp.bfloat16), "tensor", axis=0, tiled=True)
    up_value = jnp.dot(normed_all, full_up, preferred_element_type=jnp.float32) + b_up.astype(
        jnp.float32
    )
    activation = jax.nn.gelu(up_value, approximate=False).astype(jnp.bfloat16)
    ffn_terms = jnp.dot(activation, full_down, preferred_element_type=jnp.float32)
    ffn_sum = lax.psum_scatter(
        ffn_terms.astype(jnp.bfloat16), "tensor", scatter_dimension=0, tiled=True
    ).astype(jnp.float32)
    result, unit_two, rstd_two = norm_forward(
        normed + ffn_sum + b_down.astype(jnp.float32), gains[1], shifts[1]
    )
    result_low = result.astype(jnp.bfloat16)
    embed = jnp.dot(result_low, w_proj, preferred_element_type=jnp.float32).astype(jnp.bfloat16)
    embed_all = lax.all_gather(embed, ("dp", "tensor"), axis=0, tiled=True)
    row_count = lengths.shape[0]
    proj_width = w_proj.shape[1]
    widths = (proj_width, 3 * proj_width // 4, proj_width // 2)
    per_device = pairing.shape[1]
    query_count = per_device * QLEN
    query_span = NQ_ROW * QLEN
    emb_rows = embed_all.reshape(row_count, token_count, proj_width)
    my_row = lax.dynamic_index_in_dim(emb_rows, data_index, 0, keepdims=False)
    query_raw = lax.dynamic_slice_in_dim(my_row, tensor_index * query_count, query_count, 0).astype(
        jnp.float32
    )
    query_levels = [normalize_cut(query_raw, width) for width in widths]
    query_units = [level_parts[0].astype(jnp.bfloat16) for level_parts in query_levels]
    doc_numbers = jnp.arange(NDOC, dtype=jnp.int32)

    def row_pool(carried, inputs):
        row_emb, lengths_row = inputs
        row_hot = (
            segments_of(lengths_row, token_count)[:, None] == NQ_ROW + doc_numbers[None, :]
        ).astype(jnp.float32)
        row_raw = row_emb.astype(jnp.float32)
        pooled_list = []
        sums_list = []
        for width, query_unit in zip(widths, query_units):
            doc_unit = normalize_cut(row_raw, width)[0].astype(jnp.bfloat16)
            expo = jnp.exp(contract_cols(query_unit, doc_unit) / POOL_TEMP)
            sums = jnp.dot(expo, row_hot, precision=FULL_PRECISION)
            pooled = POOL_TEMP * jnp.log(sums / lengths_row.astype(jnp.float32))
            pooled_list.append(jnp.sum(pooled.reshape(per_device, QLEN, NDOC), axis=1))
            sums_list.append(sums)
        return (carried, (jnp.stack(pooled_list), jnp.stack(sums_list)))

    _, (row_scores, row_sums) = lax.scan(row_pool, 0, (emb_rows, lengths))
    logits = (
        jnp.transpose(row_scores, (2, 1, 0, 3)).reshape(per_device, 3, row_count * NDOC) / LOSS_TEMP
    )
    own_pairs = pairing[0]
    target = jnp.take_along_axis(
        logits, jnp.broadcast_to(own_pairs[:, None, None], (per_device, 3, 1)), axis=2
    )[:, :, 0]
    loss_out = jnp.sum(jax.nn.logsumexp(logits, axis=2) - target, axis=1).reshape(1, per_device)
    picked = (
        jnp.arange(row_count * NDOC, dtype=jnp.int32)[None, None, :] == own_pairs[:, None, None]
    ).astype(jnp.float32)
    grad_logits = (jax.nn.softmax(logits, axis=2) - picked) / LOSS_TEMP
    grad_rows = jnp.transpose(grad_logits.reshape(per_device, 3, row_count, NDOC), (2, 1, 0, 3))
    coefficient = jnp.repeat(grad_rows, QLEN, axis=2) / row_sums

    def row_back(carried, inputs):
        row_emb, lengths_row, row_coef = inputs
        row_hot = (
            segments_of(lengths_row, token_count)[:, None] == NQ_ROW + doc_numbers[None, :]
        ).astype(jnp.float32)
        row_raw = row_emb.astype(jnp.float32)
        new_carried = []
        row_grad = jnp.zeros((token_count, proj_width), jnp.float32)
        for level_index in range(3):
            width = widths[level_index]
            doc_unit_f, doc_part, doc_scale = normalize_cut(row_raw, width)
            doc_unit = doc_unit_f.astype(jnp.bfloat16)
            expo = jnp.exp(contract_cols(query_units[level_index], doc_unit) / POOL_TEMP)
            spread = contract_cols(row_coef[level_index], row_hot, FULL_PRECISION)
            grad_sim = (expo * spread).astype(jnp.bfloat16)
            new_carried.append(
                carried[level_index]
                + jnp.dot(grad_sim, doc_unit, preferred_element_type=jnp.float32)
            )
        return (tuple(new_carried), row_grad)

    zero_query = tuple((jnp.zeros((query_count, width), jnp.float32) for width in widths))
    query_grads, doc_grads = lax.scan(row_back, zero_query, (emb_rows, lengths, coefficient))
    grad_query = jnp.zeros((query_count, proj_width), jnp.float32)
    for level_index in range(3):
        level_parts = query_levels[level_index]
        grad_query = grad_query + normalize_back(
            query_grads[level_index], level_parts[1], level_parts[2], proj_width
        )
    coef_mine = jnp.transpose(coefficient, (2, 1, 0, 3)).reshape(query_count, 3, row_count * NDOC)
    coef_all, grad_query_all = (
        lax.all_gather(shortened(coef_mine), ("dp", "tensor"), axis=0, tiled=True).astype(
            coef_mine.dtype
        ),
        lax.all_gather(
            grad_query.astype(jnp.bfloat16), ("dp", "tensor"), axis=0, tiled=True
        ).astype(grad_query.dtype),
    )
    own_raw = embed.astype(jnp.float32)
    own_segments = lax.dynamic_slice_in_dim(segments, own_start, share_rows, 0)
    own_docs = jnp.where(own_segments >= NQ_ROW, data_index * NDOC + own_segments - NQ_ROW, -1)
    own_hot = (own_docs[:, None] == jnp.arange(row_count * NDOC, dtype=jnp.int32)[None, :]).astype(
        jnp.float32
    )
    queries_all = (
        emb_rows[:, :query_span].reshape(row_count * query_span, proj_width).astype(jnp.float32)
    )
    grad_embed = jnp.zeros((share_rows, proj_width), jnp.float32)
    for level_index in range(3):
        width = widths[level_index]
        query_unit_all = normalize_cut(queries_all, width)[0].astype(jnp.bfloat16)
        doc_unit_f, doc_part, doc_scale = normalize_cut(own_raw, width)
        expo = jnp.exp(contract_cols(query_unit_all, doc_unit_f.astype(jnp.bfloat16)) / POOL_TEMP)
        spread = contract_cols(coef_all[:, level_index], own_hot, FULL_PRECISION)
        grad_sim = (expo * spread).astype(jnp.bfloat16)
        grad_doc = contract_rows(grad_sim, query_unit_all)
        grad_embed = grad_embed + normalize_back(grad_doc, doc_part, doc_scale, proj_width)
    row_query_grads = lax.dynamic_slice_in_dim(
        grad_query_all, data_index * query_span, query_span, 0
    )
    padded = jnp.pad(row_query_grads, ((0, token_count - query_span), (0, 0)))
    grad_embed = grad_embed + lax.dynamic_slice_in_dim(padded, own_start, share_rows, 0)
    proj_float = w_proj.astype(jnp.float32)
    grad_result = cot.astype(jnp.float32) + contract_cols(grad_embed, proj_float, FULL_PRECISION)
    proj_grad = contract_rows(result_low.astype(jnp.float32), grad_embed, FULL_PRECISION)
    gain_two = jnp.sum(grad_result * unit_two, axis=0)
    shift_two = jnp.sum(grad_result, axis=0)
    grad_second = norm_backward(grad_result, unit_two, rstd_two, gains[1])
    grad_ffn = grad_second.astype(jnp.bfloat16)
    down_bias = jnp.sum(grad_ffn.astype(jnp.float32), axis=0)
    grad_ffn_all = lax.all_gather(grad_ffn, "tensor", axis=0, tiled=True)
    grad_act = contract_cols(grad_ffn_all, full_down)
    down_grad = contract_rows(activation, grad_ffn_all)
    _, gelu_pull = jax.vjp(partial(jax.nn.gelu, approximate=False), up_value)
    grad_up = gelu_pull(grad_act)[0].astype(jnp.bfloat16)
    up_bias = jnp.sum(grad_up.astype(jnp.float32), axis=0)
    up_grad = contract_rows(normed_all, grad_up)
    normed_terms = contract_cols(grad_up, full_up)
    grad_normed = (
        lax.psum_scatter(
            normed_terms.astype(jnp.bfloat16), "tensor", scatter_dimension=0, tiled=True
        ).astype(jnp.float32)
        + grad_second
    )
    gain_one = jnp.sum(grad_normed * unit_one, axis=0)
    shift_one = jnp.sum(grad_normed, axis=0)
    grad_first = norm_backward(grad_normed, unit_one, rstd_one, gains[0])
    grad_attn = grad_first.astype(jnp.bfloat16)
    out_bias = jnp.sum(grad_attn.astype(jnp.float32), axis=0)
    grad_attn_all = lax.all_gather(grad_attn, "tensor", axis=0, tiled=True)
    out_grad = contract_rows(mixed, grad_attn_all)
    grad_mixed = contract_cols(grad_attn_all, full_out).astype(jnp.bfloat16)
    grad_q, grad_k, grad_v = attend_backward(
        query_rows, key_rows, value_rows, segments, log_totals, grad_mixed, block_rows
    )
    stacked_grads = jnp.stack(
        [grad_q.astype(jnp.bfloat16), grad_k.astype(jnp.bfloat16), grad_v.astype(jnp.bfloat16)]
    )
    qkv_grad = jnp.einsum("td,ktw->kdw", tokens, stacked_grads, preferred_element_type=jnp.float32)
    input_terms = jnp.einsum(
        "ktw,kdw->td", stacked_grads, full_qkv, preferred_element_type=jnp.float32
    )
    grad_input = (
        lax.psum_scatter(
            input_terms.astype(jnp.bfloat16), "tensor", scatter_dimension=0, tiled=True
        ).astype(jnp.float32)
        + grad_first
    )
    qv_grad = jnp.stack(
        [
            jnp.sum(stacked_grads[0].astype(jnp.float32), axis=0),
            jnp.sum(stacked_grads[2].astype(jnp.float32), axis=0),
        ]
    )
    qkv_part, out_part, up_part, down_part = (
        lax.psum_scatter(
            qkv_grad.astype(jnp.bfloat16), "dp", scatter_dimension=1, tiled=True
        ).astype(jnp.float32),
        lax.psum_scatter(
            out_grad.astype(jnp.bfloat16), "dp", scatter_dimension=1, tiled=True
        ).astype(jnp.float32),
        lax.psum_scatter(
            up_grad.astype(jnp.bfloat16), "dp", scatter_dimension=0, tiled=True
        ).astype(jnp.float32),
        lax.psum_scatter(
            down_grad.astype(jnp.bfloat16), "dp", scatter_dimension=1, tiled=True
        ).astype(jnp.float32),
    )
    gain_sum, shift_sum, out_bias_sum, down_bias_sum, proj_sum = lax.psum(
        (
            jnp.stack([gain_one, gain_two]),
            jnp.stack([shift_one, shift_two]),
            out_bias,
            down_bias,
            proj_grad,
        ),
        ("dp", "tensor"),
    )
    qv_sum, up_bias_sum = lax.psum((qv_grad, up_bias), "dp")
    return (
        result_low,
        loss_out,
        grad_input.astype(jnp.bfloat16),
        qkv_part,
        qv_sum,
        out_part,
        out_bias_sum,
        gain_sum,
        shift_sum,
        up_part,
        up_bias_sum,
        down_part,
        down_bias_sum,
        proj_sum,
    )


SWAP = [(0, 1), (1, 0)]
TURN = [(0, 0), (1, 2), (2, 1), (3, 3)]
RING_UP = [(0, 1), (1, 2), (2, 3), (3, 0)]
RING_DOWN = [(1, 0), (2, 1), (3, 2), (0, 3)]
BF = jnp.bfloat16
F32 = jnp.float32


def dot(left, right):
    return jnp.dot(left, right, preferred_element_type=F32)


def turn(value):
    return lax.ppermute(value, ("c", "y"), TURN)


def swap(value, axis):
    return lax.ppermute(value, axis, SWAP)


def up(value):
    return lax.ppermute(value, "z", RING_UP)


def down(value):
    return lax.ppermute(value, "z", RING_DOWN)


def pair_up(first, second, own_index, axis):
    return jnp.where(
        own_index == 0, jnp.stack([first, second], axis), jnp.stack([second, first], axis)
    )


def gather_z(value, z):
    below, above = up(value), down(value)
    half = value.shape[-2] // 2
    far_low = up(below[..., :half, :])
    far_high = down(above[..., half:, :])
    far = jnp.concatenate([far_low, far_high], axis=-2)
    whole = jnp.zeros((4,) + value.shape, value.dtype)
    for offset, part in ((0, value), (3, below), (1, above), (2, far)):
        whole = lax.dynamic_update_index_in_dim(whole, part, (z + offset) % 4, 0)
    return whole


def gather_blocks(value, order, z, x, y):
    done = []
    for axis in order:
        if axis == "z":
            value = gather_z(value, z)
        else:
            place = sum(1 for name in done if "zxy".index(name) < "zxy".index(axis))
            value = pair_up(value, swap(value, axis), {"x": x, "y": y}[axis], place)
        done.append(axis)
    return value.reshape(-1, value.shape[-1])


def sum_pair(blocks, axis_name, own_index, axis):
    theirs = lax.dynamic_index_in_dim(blocks, 1 - own_index, axis, keepdims=False)
    mine = lax.dynamic_index_in_dim(blocks, own_index, axis, keepdims=False)
    return mine.astype(F32) + swap(theirs.astype(BF), axis_name).astype(F32)


def sum_ring(block_of, z):
    far = block_of((z + 2) % 4).astype(BF)
    half = far.shape[0] // 2
    from_below = up(far[:half])
    from_above = down(far[half:])
    pad = ((0, half),) + ((0, 0),) * (far.ndim - 1)
    pad_high = ((half, 0),) + ((0, 0),) * (far.ndim - 1)
    after = block_of((z + 1) % 4) + jnp.pad(from_below, pad).astype(F32)
    before = block_of((z + 3) % 4) + jnp.pad(from_above, pad_high).astype(F32)
    got_up = up(after.astype(BF))
    got_down = down(before.astype(BF))
    return block_of(z) + got_up.astype(F32) + got_down.astype(F32)


def weight_sum(left, right, order, z, x, y):
    width = right.shape[1]
    if order[0] == "z":

        def block_of(place):
            return contract_rows(lax.dynamic_slice_in_dim(left, place * 256, 256, 1), right)

        own = sum_ring(block_of, z).reshape(2, 2, 64, width)
        own = sum_pair(own, "y", y, 1)
        own = sum_pair(own, "x", x, 0)
    else:

        def half_of(x_place):
            columns = [
                lax.dynamic_slice_in_dim(left, step * 256 + x_place * 128, 128, 1)
                for step in range(4)
            ]
            return contract_rows(jnp.concatenate(columns, axis=1), right)

        theirs = swap(half_of(1 - x).astype(BF), "x")
        own = half_of(x) + theirs.astype(F32)
        own = sum_pair(own.reshape(4, 2, 64, width), "y", y, 1)
        own = sum_ring(lambda place: lax.dynamic_index_in_dim(own, place, 0, keepdims=False), z)
    return turn(own.astype(BF)).astype(F32)


def sum_chips(value, steps):
    for step in steps:
        if step == "0":
            value = value + lax.ppermute(value, "z", [(0, 1), (1, 0), (2, 3), (3, 2)])
        elif step == "1":
            value = value + lax.ppermute(value, "z", [(0, 3), (3, 0), (1, 2), (2, 1)])
        else:
            value = value + swap(value, step)
    return value


def rows_of(value, start, count):
    return lax.dynamic_slice_in_dim(value, start, count, 0)


def local_chip(
    tokens,
    lengths,
    pairing,
    w_qkv,
    b_qv,
    w_out,
    b_out,
    ln_gain,
    ln_bias,
    w_up,
    b_up,
    w_down,
    b_down,
    w_proj,
    cot,
):
    z, x, c, y = (lax.axis_index(name) for name in ("z", "x", "c", "y"))
    chip = 4 * z + 2 * x + y
    token_count, width = tokens.shape
    share = token_count // 2
    own_start, other_start = c * share, (1 - c) * share
    gains, shifts = ln_gain.astype(F32), ln_bias.astype(F32)

    qkv_rows = jnp.concatenate([w_qkv[0], w_qkv[1], w_qkv[2]], axis=1)
    full_qkv = gather_blocks(turn(qkv_rows), "xyz", z, x, y)
    row = jnp.where(c == y, tokens, swap(tokens, "c"))
    bias = turn(jnp.concatenate([b_qv.reshape(-1), b_up])[None])[0].astype(F32)
    full_out = gather_blocks(turn(w_out.T), "xyz", z, x, y)
    full_up = gather_blocks(turn(w_up), "zyx", z, x, y)
    full_down = gather_blocks(turn(w_down.T), "xyz", z, x, y)
    own_cot = turn(cot)
    all_pairs = lax.all_gather(pairing, ("z", "x", "c", "y"), axis=0, tiled=False)

    half_width = w_qkv.shape[2]
    local_heads = half_width // HEAD_DIM
    q_bias, v_bias, up_shift = (
        bias[:half_width],
        bias[half_width : 2 * half_width],
        bias[2 * half_width :],
    )
    row_lengths = lax.dynamic_index_in_dim(lengths, chip, 0, keepdims=False)
    segments = segments_of(row_lengths, token_count)
    projected = dot(row, full_qkv)
    heads_shape = (token_count, local_heads, HEAD_DIM)
    query_rows = (projected[:, :half_width] + q_bias).astype(BF).reshape(heads_shape)
    key_rows = projected[:, half_width : 2 * half_width].astype(BF).reshape(heads_shape)
    value_rows = (projected[:, 2 * half_width :] + v_bias).astype(BF).reshape(heads_shape)
    mixed, log_totals = attend_forward(query_rows, key_rows, value_rows, segments, 512)

    def row_sum(left, weight_t, transposed):
        times = contract_cols if transposed else dot
        theirs = swap(times(left(1), weight_t).astype(BF), "c")
        return times(left(0), weight_t) + theirs.astype(F32)

    def mixed_half(which):
        return rows_of(mixed, other_start if which else own_start, share)

    attn_sum = row_sum(mixed_half, full_out, True)
    own_tokens = rows_of(row, own_start, share).astype(F32)
    normed, unit_one, rstd_one = norm_forward(
        own_tokens + attn_sum + b_out.astype(F32), gains[0], shifts[0]
    )
    normed_low = normed.astype(BF)
    normed_all = jnp.concatenate([normed_low, swap(normed_low, "c")], axis=0)
    up_value = dot(normed_all, full_up) + up_shift
    activation = jax.nn.gelu(up_value, approximate=False).astype(BF)
    ffn_sum = row_sum(
        lambda which: activation[which * share : (which + 1) * share], full_down, True
    )
    result, unit_two, rstd_two = norm_forward(
        normed + ffn_sum + b_down.astype(F32), gains[1], shifts[1]
    )
    result_low = result.astype(BF)
    y_out = turn(result_low)
    embed = dot(result_low, w_proj).astype(BF)

    other_embed = swap(embed, "c")
    row_embed = jnp.where(
        c == 0,
        jnp.concatenate([embed, other_embed], axis=0),
        jnp.concatenate([other_embed, embed], axis=0),
    )
    query_span = NQ_ROW * QLEN
    half_span = query_span // 2
    half_queries = NQ_ROW // 2
    own_queries = rows_of(row_embed, c * half_span, half_span)
    chips = ("z", "x", "y")
    chip_count = lengths.shape[0]
    queries = lax.all_to_all(
        jnp.broadcast_to(own_queries[None], (chip_count,) + own_queries.shape), chips, 0, 0
    ).reshape(chip_count * half_span, -1)
    proj_width = w_proj.shape[1]
    widths = (proj_width, 3 * proj_width // 4, proj_width // 2)
    doc_raw = row_embed[query_span:].astype(F32)
    query_raw = queries.astype(F32)
    hot = (
        segments[query_span:, None] == NQ_ROW + jnp.arange(NDOC, dtype=jnp.int32)[None, :]
    ).astype(F32)
    query_levels = [normalize_cut(query_raw, cut) for cut in widths]
    doc_levels = [normalize_cut(doc_raw, cut) for cut in widths]
    sums_list = []
    for cut in range(3):
        expo = jnp.exp(
            contract_cols(query_levels[cut][0].astype(BF), doc_levels[cut][0].astype(BF))
            / POOL_TEMP
        )
        sums_list.append(jnp.dot(expo, hot, precision=FULL_PRECISION))
    sums = jnp.stack(sums_list)
    pooled = POOL_TEMP * jnp.log(sums / row_lengths.astype(F32))
    query_total = chip_count * half_queries
    own_logits = jnp.sum(pooled.reshape(3, query_total, QLEN, NDOC), axis=2) / LOSS_TEMP
    chip_logits = lax.all_to_all(
        jnp.broadcast_to(own_logits[None], (chip_count,) + own_logits.shape), chips, 0, 0
    )
    logits = jnp.transpose(chip_logits, (1, 2, 0, 3)).reshape(3, query_total, chip_count * NDOC)
    pairs = lax.dynamic_index_in_dim(
        all_pairs.reshape(chip_count, 2, half_queries), c, 1, keepdims=False
    ).reshape(query_total)
    picked = (
        jnp.arange(chip_count * NDOC, dtype=jnp.int32)[None, :] == pairs[:, None]
    ).astype(F32)
    highest = jnp.max(logits, axis=2, keepdims=True)
    shares = jnp.exp(logits - highest)
    total = jnp.sum(shares, axis=2, keepdims=True)
    losses = jnp.sum(
        (highest + jnp.log(total))[:, :, 0] - jnp.sum(logits * picked, axis=2), axis=0
    ).reshape(chip_count, half_queries)
    losses = jnp.where(c == y, losses, swap(losses, "c"))
    loss_out = rows_of(losses, 4 * z + 2 * x + c, 1)
    grad_logits = (shares / total - picked) / LOSS_TEMP
    own_grad = lax.dynamic_slice_in_dim(grad_logits, chip * NDOC, NDOC, 2)
    coefficient = jnp.repeat(own_grad, QLEN, axis=1) / sums
    query_grad = jnp.zeros((chip_count * half_span, proj_width), F32)
    doc_grad = jnp.zeros((token_count - query_span, proj_width), F32)
    for cut in range(3):
        query_unit_f, query_part, query_scale = query_levels[cut]
        doc_unit_f, doc_part, doc_scale = doc_levels[cut]
        query_unit, doc_unit = query_unit_f.astype(BF), doc_unit_f.astype(BF)
        expo = jnp.exp(contract_cols(query_unit, doc_unit) / POOL_TEMP)
        spread = contract_cols(coefficient[cut], hot, FULL_PRECISION)
        grad_sim = (expo * spread).astype(BF)
        query_grad = query_grad + normalize_back(
            dot(grad_sim, doc_unit), query_part, query_scale, proj_width
        )
        doc_grad = doc_grad + normalize_back(
            contract_rows(grad_sim, query_unit), doc_part, doc_scale, proj_width
        )
    grad_blocks = lax.all_to_all(
        query_grad.astype(BF).reshape(chip_count, half_span, proj_width), chips, 0, 0
    )
    own_query_grad = jnp.sum(grad_blocks.astype(F32), axis=0)
    row_grad = jnp.concatenate([jnp.zeros((query_span, proj_width), F32), doc_grad], axis=0)
    row_grad = lax.dynamic_update_slice_in_dim(row_grad, own_query_grad, c * half_span, 0)
    grad_embed = rows_of(row_grad, own_start, share) + swap(
        rows_of(row_grad, other_start, share), "c"
    )

    proj_low = w_proj
    grad_embed_low = grad_embed.astype(BF)
    grad_embed_rest = (grad_embed - grad_embed_low.astype(F32)).astype(BF)
    grad_result = own_cot.astype(F32) + (
        contract_cols(grad_embed_low, proj_low) + contract_cols(grad_embed_rest, proj_low)
    )
    proj_grad = contract_rows(result_low, grad_embed_low) + contract_rows(
        result_low, grad_embed_rest
    )
    gain_two = jnp.sum(grad_result * unit_two, axis=0)
    shift_two = jnp.sum(grad_result, axis=0)
    grad_second = norm_backward(grad_result, unit_two, rstd_two, gains[1])
    grad_ffn = grad_second.astype(BF)
    down_bias = jnp.sum(grad_ffn.astype(F32), axis=0)
    grad_ffn_all = jnp.concatenate([grad_ffn, swap(grad_ffn, "c")], axis=0)
    down_part = weight_sum(grad_ffn_all, activation, "zyx", z, x, y)
    grad_act = dot(grad_ffn_all, full_down)
    _, gelu_pull = jax.vjp(partial(jax.nn.gelu, approximate=False), up_value)
    grad_up = gelu_pull(grad_act)[0].astype(BF)
    up_bias = jnp.sum(grad_up.astype(F32), axis=0)
    up_part = weight_sum(normed_all, grad_up, "xyz", z, x, y)
    grad_normed = (
        row_sum(lambda which: grad_up[which * share : (which + 1) * share], full_up, True)
        + grad_second
    )
    gain_one = jnp.sum(grad_normed * unit_one, axis=0)
    shift_one = jnp.sum(grad_normed, axis=0)
    grad_first = norm_backward(grad_normed, unit_one, rstd_one, gains[0])
    grad_attn = grad_first.astype(BF)
    out_bias = jnp.sum(grad_attn.astype(F32), axis=0)
    other_attn = swap(grad_attn, "c")
    grad_attn_all = jnp.where(
        c == 0,
        jnp.concatenate([grad_attn, other_attn], axis=0),
        jnp.concatenate([other_attn, grad_attn], axis=0),
    )
    out_part = weight_sum(grad_attn_all, mixed, "zyx", z, x, y)
    grad_mixed = dot(grad_attn_all, full_out).astype(BF)
    grad_q, grad_k, grad_v = attend_backward(
        query_rows, key_rows, value_rows, segments, log_totals, grad_mixed, 512
    )
    grads = jnp.concatenate([grad_q.astype(BF), grad_k.astype(BF), grad_v.astype(BF)], axis=1)
    qkv_part = weight_sum(row, grads, "zyx", z, x, y)
    grad_input = turn(
        (
            row_sum(
                lambda which: rows_of(grads, other_start if which else own_start, share),
                full_qkv,
                True,
            )
            + grad_first
        ).astype(BF)
    )

    half_sums = jnp.concatenate(
        [
            jnp.sum(grads[:, :half_width].astype(F32), axis=0),
            jnp.sum(grads[:, 2 * half_width :].astype(F32), axis=0),
            up_bias,
        ]
    ).reshape(-1, 128)
    half_sums = sum_chips(half_sums, "xy01")
    half_sums = jnp.where(c == y, half_sums, swap(half_sums, "c")).reshape(-1)
    shared = jnp.stack([gain_one, gain_two, shift_one, shift_two, out_bias, down_bias])
    shared = sum_chips(shared, "cxy01")
    proj_sum = sum_chips(proj_grad, "cxy01")
    return (
        y_out,
        loss_out,
        grad_input,
        jnp.stack([qkv_part[:, k * half_width : (k + 1) * half_width] for k in range(3)]),
        half_sums[: 2 * half_width].reshape(2, half_width),
        out_part.T,
        shared[4],
        shared[0:2],
        shared[2:4],
        up_part,
        half_sums[2 * half_width :],
        down_part.T,
        shared[5],
        proj_sum,
    )


IN_SPECS = (
    P("dp", None),
    P(),
    P("dp", "tensor"),
    P(None, "dp", "tensor"),
    P(None, "tensor"),
    P("tensor", "dp"),
    P(),
    P(),
    P(),
    P("dp", "tensor"),
    P("tensor"),
    P("tensor", "dp"),
    P(),
    P(),
    P(("dp", "tensor"), None),
)
OUT_SPECS = (
    P(("dp", "tensor"), None),
    P("dp", "tensor"),
    P(("dp", "tensor"), None),
    P(None, "dp", "tensor"),
    P(None, "tensor"),
    P("tensor", "dp"),
    P(),
    P(),
    P(),
    P("dp", "tensor"),
    P("tensor"),
    P("tensor", "dp"),
    P(),
    P(),
)


def solution(mesh):
    if mesh.devices.shape != (16, 2):
        return jax.shard_map(
            local, mesh=mesh, in_specs=IN_SPECS, out_specs=OUT_SPECS, check_vma=False
        )
    names = {"dp": ("z", "x", "c"), "tensor": ("y",)}

    def respec(spec):
        parts = []
        for entry in spec:
            axes = () if entry is None else entry if isinstance(entry, tuple) else (entry,)
            parts.append(tuple(name for axis in axes for name in names[axis]) or None)
        return P(*parts)

    chips = Mesh(mesh.devices.reshape(4, 2, 2, 2), ("z", "x", "c", "y"))
    return jax.shard_map(
        local_chip,
        mesh=chips,
        in_specs=tuple(respec(spec) for spec in IN_SPECS),
        out_specs=tuple(respec(spec) for spec in OUT_SPECS),
        check_vma=False,
    )
```

```python
from functools import partial

import jax
import jax.numpy as jnp
from jax import lax
from jax.experimental import pallas as pl
from jax.experimental.pallas import tpu as pltpu
from jax.sharding import Mesh, PartitionSpec as P

HEAD_DIM = 64
QLEN = 32
NQ_ROW = 8
NDOC = 8


EPS_NORM = 1e-05
EPS_EMBED = 1e-06
POOL_TEMP = 0.1
LOSS_TEMP = 0.1
FULL_PRECISION = lax.Precision.HIGHEST
MASKED_SCORE = -1e30


def shortened(shard):

    def short(part):
        return part.astype(jnp.bfloat16) if part.dtype == jnp.float32 else part

    return jax.tree.map(short, shard)


def contract_rows(left, right, precision=None):
    return lax.dot_general(
        left,
        right,
        (((0,), (0,)), ((), ())),
        precision=precision,
        preferred_element_type=jnp.float32,
    )


def contract_cols(left, right, precision=None):
    return lax.dot_general(
        left,
        right,
        (((1,), (1,)), ((), ())),
        precision=precision,
        preferred_element_type=jnp.float32,
    )


def norm_forward(value, gain, shift):
    centred = value - jnp.mean(value, axis=1, keepdims=True)
    rstd = lax.rsqrt(jnp.mean(centred * centred, axis=1, keepdims=True) + EPS_NORM)
    unit = centred * rstd
    return (unit * gain + shift, unit, rstd)


def norm_backward(grad, unit, rstd, gain):
    scaled = grad * gain
    return rstd * (
        scaled
        - jnp.mean(scaled, axis=1, keepdims=True)
        - unit * jnp.mean(scaled * unit, axis=1, keepdims=True)
    )


def segments_of(row_lengths, token_count):
    position = jnp.arange(token_count, dtype=jnp.int32)
    query_span = NQ_ROW * QLEN
    ends = jnp.cumsum(row_lengths)
    passed = jnp.sum((position[:, None] - query_span >= ends[None, :]).astype(jnp.int32), axis=1)
    return jnp.where(position < query_span, position // QLEN, NQ_ROW + passed)


def normalize_cut(raw, width):
    part = raw[:, :width]
    scale = lax.rsqrt(jnp.sum(part * part, axis=1, keepdims=True) + EPS_EMBED)
    return (part * scale, part, scale)


def normalize_back(grad, part, scale, full_width):
    result = scale * grad - part * (scale * scale * scale) * jnp.sum(
        part * grad, axis=1, keepdims=True
    )
    return jnp.pad(result, ((0, 0), (0, full_width - grad.shape[1])))


def masked_scores(query_block, key_rows, block_segments, segments):
    scores = jnp.einsum(
        "qhd,khd->hqk", query_block, key_rows, preferred_element_type=jnp.float32
    ) * HEAD_DIM ** (-0.5)
    return jnp.where((block_segments[:, None] == segments[None, :])[None], scores, MASKED_SCORE)


def attend_forward(query_rows, key_rows, value_rows, segments, block_rows):
    token_count = query_rows.shape[0]

    def one_block(block_start):
        query_block = lax.dynamic_slice_in_dim(query_rows, block_start, block_rows, 0)
        block_segments = lax.dynamic_slice_in_dim(segments, block_start, block_rows, 0)
        scores = masked_scores(query_block, key_rows, block_segments, segments)
        highest = jnp.max(scores, axis=2, keepdims=True)
        expo = jnp.exp(scores - highest)
        totals = jnp.sum(expo, axis=2, keepdims=True)
        weights = (expo / totals).astype(jnp.bfloat16)
        mixed = jnp.einsum("hqk,khd->qhd", weights, value_rows, preferred_element_type=jnp.float32)
        return (mixed.astype(jnp.bfloat16), (highest + jnp.log(totals))[:, :, 0])

    starts = jnp.arange(token_count // block_rows, dtype=jnp.int32) * block_rows
    mixed, log_totals = lax.map(one_block, starts)
    return (mixed.reshape(token_count, -1), log_totals)


def attend_backward(query_rows, key_rows, value_rows, segments, log_totals, grad_mixed, block_rows):
    token_count, local_heads, head_size = query_rows.shape
    scale = HEAD_DIM ** (-0.5)
    grad_heads = grad_mixed.reshape(token_count, local_heads, head_size)

    def one_block(carried, inputs):
        grad_keys, grad_values = carried
        block_start, block_lse = inputs
        query_block = lax.dynamic_slice_in_dim(query_rows, block_start, block_rows, 0)
        grad_block = lax.dynamic_slice_in_dim(grad_heads, block_start, block_rows, 0)
        block_segments = lax.dynamic_slice_in_dim(segments, block_start, block_rows, 0)
        scores = masked_scores(query_block, key_rows, block_segments, segments)
        probs = jnp.exp(scores - block_lse[:, :, None])
        grad_probs = jnp.einsum(
            "qhd,khd->hqk", grad_block, value_rows, preferred_element_type=jnp.float32
        )
        inner = jnp.sum(probs * grad_probs, axis=2, keepdims=True)
        grad_scores = (probs * (grad_probs - inner)).astype(jnp.bfloat16)
        grad_query = (
            jnp.einsum("hqk,khd->qhd", grad_scores, key_rows, preferred_element_type=jnp.float32)
            * scale
        )
        grad_keys = (
            grad_keys
            + jnp.einsum(
                "hqk,qhd->khd", grad_scores, query_block, preferred_element_type=jnp.float32
            )
            * scale
        )
        grad_values = grad_values + jnp.einsum(
            "hqk,qhd->khd",
            probs.astype(jnp.bfloat16),
            grad_block,
            preferred_element_type=jnp.float32,
        )
        return ((grad_keys, grad_values), grad_query)

    starts = jnp.arange(token_count // block_rows, dtype=jnp.int32) * block_rows
    zero_rows = jnp.zeros(key_rows.shape, jnp.float32)
    (grad_keys, grad_values), grad_queries = lax.scan(
        one_block, (zero_rows, zero_rows), (starts, log_totals)
    )
    flat_width = local_heads * head_size
    return (
        grad_queries.reshape(token_count, flat_width),
        grad_keys.reshape(token_count, flat_width),
        grad_values.reshape(token_count, flat_width),
    )


def local(
    tokens,
    lengths,
    pairing,
    w_qkv,
    b_qv,
    w_out,
    b_out,
    ln_gain,
    ln_bias,
    w_up,
    b_up,
    w_down,
    b_down,
    w_proj,
    cot,
):
    tensor_count = lax.axis_size("tensor")
    tensor_index = lax.axis_index("tensor")
    data_index = lax.axis_index("dp")
    token_count = tokens.shape[0]
    share_rows = token_count // tensor_count
    block_rows = min(512, token_count)
    own_start = tensor_index * share_rows
    full_qkv, full_out, full_up, full_down = (
        lax.all_gather(w_qkv, "dp", axis=1, tiled=True),
        lax.all_gather(w_out, "dp", axis=1, tiled=True),
        lax.all_gather(w_up, "dp", axis=0, tiled=True),
        lax.all_gather(w_down, "dp", axis=1, tiled=True),
    )
    head_width = full_qkv.shape[2]
    local_heads = head_width // HEAD_DIM
    row_lengths = lax.dynamic_index_in_dim(lengths, data_index, 0, keepdims=False)
    segments = segments_of(row_lengths, token_count)
    projected = jnp.einsum("td,kdw->ktw", tokens, full_qkv, preferred_element_type=jnp.float32)
    qv_bias = b_qv.astype(jnp.float32)
    query_rows = (
        (projected[0] + qv_bias[0]).astype(jnp.bfloat16).reshape(token_count, local_heads, HEAD_DIM)
    )
    key_rows = projected[1].astype(jnp.bfloat16).reshape(token_count, local_heads, HEAD_DIM)
    value_rows = (
        (projected[2] + qv_bias[1]).astype(jnp.bfloat16).reshape(token_count, local_heads, HEAD_DIM)
    )
    mixed, log_totals = attend_forward(query_rows, key_rows, value_rows, segments, block_rows)
    attn_terms = jnp.dot(mixed, full_out, preferred_element_type=jnp.float32)
    attn_sum = lax.psum_scatter(
        attn_terms.astype(jnp.bfloat16), "tensor", scatter_dimension=0, tiled=True
    ).astype(jnp.float32)
    own_tokens = lax.dynamic_slice_in_dim(tokens, own_start, share_rows, 0).astype(jnp.float32)
    gains = ln_gain.astype(jnp.float32)
    shifts = ln_bias.astype(jnp.float32)
    normed, unit_one, rstd_one = norm_forward(
        own_tokens + attn_sum + b_out.astype(jnp.float32), gains[0], shifts[0]
    )
    normed_all = lax.all_gather(normed.astype(jnp.bfloat16), "tensor", axis=0, tiled=True)
    up_value = jnp.dot(normed_all, full_up, preferred_element_type=jnp.float32) + b_up.astype(
        jnp.float32
    )
    activation = jax.nn.gelu(up_value, approximate=False).astype(jnp.bfloat16)
    ffn_terms = jnp.dot(activation, full_down, preferred_element_type=jnp.float32)
    ffn_sum = lax.psum_scatter(
        ffn_terms.astype(jnp.bfloat16), "tensor", scatter_dimension=0, tiled=True
    ).astype(jnp.float32)
    result, unit_two, rstd_two = norm_forward(
        normed + ffn_sum + b_down.astype(jnp.float32), gains[1], shifts[1]
    )
    result_low = result.astype(jnp.bfloat16)
    embed = jnp.dot(result_low, w_proj, preferred_element_type=jnp.float32).astype(jnp.bfloat16)
    embed_all = lax.all_gather(embed, ("dp", "tensor"), axis=0, tiled=True)
    row_count = lengths.shape[0]
    proj_width = w_proj.shape[1]
    widths = (proj_width, 3 * proj_width // 4, proj_width // 2)
    per_device = pairing.shape[1]
    query_count = per_device * QLEN
    query_span = NQ_ROW * QLEN
    emb_rows = embed_all.reshape(row_count, token_count, proj_width)
    my_row = lax.dynamic_index_in_dim(emb_rows, data_index, 0, keepdims=False)
    query_raw = lax.dynamic_slice_in_dim(my_row, tensor_index * query_count, query_count, 0).astype(
        jnp.float32
    )
    query_levels = [normalize_cut(query_raw, width) for width in widths]
    query_units = [level_parts[0].astype(jnp.bfloat16) for level_parts in query_levels]
    doc_numbers = jnp.arange(NDOC, dtype=jnp.int32)

    def row_pool(carried, inputs):
        row_emb, lengths_row = inputs
        row_hot = (
            segments_of(lengths_row, token_count)[:, None] == NQ_ROW + doc_numbers[None, :]
        ).astype(jnp.float32)
        row_raw = row_emb.astype(jnp.float32)
        pooled_list = []
        sums_list = []
        for width, query_unit in zip(widths, query_units):
            doc_unit = normalize_cut(row_raw, width)[0].astype(jnp.bfloat16)
            expo = jnp.exp(contract_cols(query_unit, doc_unit) / POOL_TEMP)
            sums = jnp.dot(expo, row_hot, precision=FULL_PRECISION)
            pooled = POOL_TEMP * jnp.log(sums / lengths_row.astype(jnp.float32))
            pooled_list.append(jnp.sum(pooled.reshape(per_device, QLEN, NDOC), axis=1))
            sums_list.append(sums)
        return (carried, (jnp.stack(pooled_list), jnp.stack(sums_list)))

    _, (row_scores, row_sums) = lax.scan(row_pool, 0, (emb_rows, lengths))
    logits = (
        jnp.transpose(row_scores, (2, 1, 0, 3)).reshape(per_device, 3, row_count * NDOC) / LOSS_TEMP
    )
    own_pairs = pairing[0]
    target = jnp.take_along_axis(
        logits, jnp.broadcast_to(own_pairs[:, None, None], (per_device, 3, 1)), axis=2
    )[:, :, 0]
    loss_out = jnp.sum(jax.nn.logsumexp(logits, axis=2) - target, axis=1).reshape(1, per_device)
    picked = (
        jnp.arange(row_count * NDOC, dtype=jnp.int32)[None, None, :] == own_pairs[:, None, None]
    ).astype(jnp.float32)
    grad_logits = (jax.nn.softmax(logits, axis=2) - picked) / LOSS_TEMP
    grad_rows = jnp.transpose(grad_logits.reshape(per_device, 3, row_count, NDOC), (2, 1, 0, 3))
    coefficient = jnp.repeat(grad_rows, QLEN, axis=2) / row_sums

    def row_back(carried, inputs):
        row_emb, lengths_row, row_coef = inputs
        row_hot = (
            segments_of(lengths_row, token_count)[:, None] == NQ_ROW + doc_numbers[None, :]
        ).astype(jnp.float32)
        row_raw = row_emb.astype(jnp.float32)
        new_carried = []
        row_grad = jnp.zeros((token_count, proj_width), jnp.float32)
        for level_index in range(3):
            width = widths[level_index]
            doc_unit_f, doc_part, doc_scale = normalize_cut(row_raw, width)
            doc_unit = doc_unit_f.astype(jnp.bfloat16)
            expo = jnp.exp(contract_cols(query_units[level_index], doc_unit) / POOL_TEMP)
            spread = contract_cols(row_coef[level_index], row_hot, FULL_PRECISION)
            grad_sim = (expo * spread).astype(jnp.bfloat16)
            new_carried.append(
                carried[level_index]
                + jnp.dot(grad_sim, doc_unit, preferred_element_type=jnp.float32)
            )
        return (tuple(new_carried), row_grad)

    zero_query = tuple((jnp.zeros((query_count, width), jnp.float32) for width in widths))
    query_grads, doc_grads = lax.scan(row_back, zero_query, (emb_rows, lengths, coefficient))
    grad_query = jnp.zeros((query_count, proj_width), jnp.float32)
    for level_index in range(3):
        level_parts = query_levels[level_index]
        grad_query = grad_query + normalize_back(
            query_grads[level_index], level_parts[1], level_parts[2], proj_width
        )
    coef_mine = jnp.transpose(coefficient, (2, 1, 0, 3)).reshape(query_count, 3, row_count * NDOC)
    coef_all, grad_query_all = (
        lax.all_gather(shortened(coef_mine), ("dp", "tensor"), axis=0, tiled=True).astype(
            coef_mine.dtype
        ),
        lax.all_gather(
            grad_query.astype(jnp.bfloat16), ("dp", "tensor"), axis=0, tiled=True
        ).astype(grad_query.dtype),
    )
    own_raw = embed.astype(jnp.float32)
    own_segments = lax.dynamic_slice_in_dim(segments, own_start, share_rows, 0)
    own_docs = jnp.where(own_segments >= NQ_ROW, data_index * NDOC + own_segments - NQ_ROW, -1)
    own_hot = (own_docs[:, None] == jnp.arange(row_count * NDOC, dtype=jnp.int32)[None, :]).astype(
        jnp.float32
    )
    queries_all = (
        emb_rows[:, :query_span].reshape(row_count * query_span, proj_width).astype(jnp.float32)
    )
    grad_embed = jnp.zeros((share_rows, proj_width), jnp.float32)
    for level_index in range(3):
        width = widths[level_index]
        query_unit_all = normalize_cut(queries_all, width)[0].astype(jnp.bfloat16)
        doc_unit_f, doc_part, doc_scale = normalize_cut(own_raw, width)
        expo = jnp.exp(contract_cols(query_unit_all, doc_unit_f.astype(jnp.bfloat16)) / POOL_TEMP)
        spread = contract_cols(coef_all[:, level_index], own_hot, FULL_PRECISION)
        grad_sim = (expo * spread).astype(jnp.bfloat16)
        grad_doc = contract_rows(grad_sim, query_unit_all)
        grad_embed = grad_embed + normalize_back(grad_doc, doc_part, doc_scale, proj_width)
    row_query_grads = lax.dynamic_slice_in_dim(
        grad_query_all, data_index * query_span, query_span, 0
    )
    padded = jnp.pad(row_query_grads, ((0, token_count - query_span), (0, 0)))
    grad_embed = grad_embed + lax.dynamic_slice_in_dim(padded, own_start, share_rows, 0)
    proj_float = w_proj.astype(jnp.float32)
    grad_result = cot.astype(jnp.float32) + contract_cols(grad_embed, proj_float, FULL_PRECISION)
    proj_grad = contract_rows(result_low.astype(jnp.float32), grad_embed, FULL_PRECISION)
    gain_two = jnp.sum(grad_result * unit_two, axis=0)
    shift_two = jnp.sum(grad_result, axis=0)
    grad_second = norm_backward(grad_result, unit_two, rstd_two, gains[1])
    grad_ffn = grad_second.astype(jnp.bfloat16)
    down_bias = jnp.sum(grad_ffn.astype(jnp.float32), axis=0)
    grad_ffn_all = lax.all_gather(grad_ffn, "tensor", axis=0, tiled=True)
    grad_act = contract_cols(grad_ffn_all, full_down)
    down_grad = contract_rows(activation, grad_ffn_all)
    _, gelu_pull = jax.vjp(partial(jax.nn.gelu, approximate=False), up_value)
    grad_up = gelu_pull(grad_act)[0].astype(jnp.bfloat16)
    up_bias = jnp.sum(grad_up.astype(jnp.float32), axis=0)
    up_grad = contract_rows(normed_all, grad_up)
    normed_terms = contract_cols(grad_up, full_up)
    grad_normed = (
        lax.psum_scatter(
            normed_terms.astype(jnp.bfloat16), "tensor", scatter_dimension=0, tiled=True
        ).astype(jnp.float32)
        + grad_second
    )
    gain_one = jnp.sum(grad_normed * unit_one, axis=0)
    shift_one = jnp.sum(grad_normed, axis=0)
    grad_first = norm_backward(grad_normed, unit_one, rstd_one, gains[0])
    grad_attn = grad_first.astype(jnp.bfloat16)
    out_bias = jnp.sum(grad_attn.astype(jnp.float32), axis=0)
    grad_attn_all = lax.all_gather(grad_attn, "tensor", axis=0, tiled=True)
    out_grad = contract_rows(mixed, grad_attn_all)
    grad_mixed = contract_cols(grad_attn_all, full_out).astype(jnp.bfloat16)
    grad_q, grad_k, grad_v = attend_backward(
        query_rows, key_rows, value_rows, segments, log_totals, grad_mixed, block_rows
    )
    stacked_grads = jnp.stack(
        [grad_q.astype(jnp.bfloat16), grad_k.astype(jnp.bfloat16), grad_v.astype(jnp.bfloat16)]
    )
    qkv_grad = jnp.einsum("td,ktw->kdw", tokens, stacked_grads, preferred_element_type=jnp.float32)
    input_terms = jnp.einsum(
        "ktw,kdw->td", stacked_grads, full_qkv, preferred_element_type=jnp.float32
    )
    grad_input = (
        lax.psum_scatter(
            input_terms.astype(jnp.bfloat16), "tensor", scatter_dimension=0, tiled=True
        ).astype(jnp.float32)
        + grad_first
    )
    qv_grad = jnp.stack(
        [
            jnp.sum(stacked_grads[0].astype(jnp.float32), axis=0),
            jnp.sum(stacked_grads[2].astype(jnp.float32), axis=0),
        ]
    )
    qkv_part, out_part, up_part, down_part = (
        lax.psum_scatter(
            qkv_grad.astype(jnp.bfloat16), "dp", scatter_dimension=1, tiled=True
        ).astype(jnp.float32),
        lax.psum_scatter(
            out_grad.astype(jnp.bfloat16), "dp", scatter_dimension=1, tiled=True
        ).astype(jnp.float32),
        lax.psum_scatter(
            up_grad.astype(jnp.bfloat16), "dp", scatter_dimension=0, tiled=True
        ).astype(jnp.float32),
        lax.psum_scatter(
            down_grad.astype(jnp.bfloat16), "dp", scatter_dimension=1, tiled=True
        ).astype(jnp.float32),
    )
    gain_sum, shift_sum, out_bias_sum, down_bias_sum, proj_sum = lax.psum(
        (
            jnp.stack([gain_one, gain_two]),
            jnp.stack([shift_one, shift_two]),
            out_bias,
            down_bias,
            proj_grad,
        ),
        ("dp", "tensor"),
    )
    qv_sum, up_bias_sum = lax.psum((qv_grad, up_bias), "dp")
    return (
        result_low,
        loss_out,
        grad_input.astype(jnp.bfloat16),
        qkv_part,
        qv_sum,
        out_part,
        out_bias_sum,
        gain_sum,
        shift_sum,
        up_part,
        up_bias_sum,
        down_part,
        down_bias_sum,
        proj_sum,
    )


SWAP = [(0, 1), (1, 0)]
TURN = [(0, 0), (1, 2), (2, 1), (3, 3)]
RING_UP = [(0, 1), (1, 2), (2, 3), (3, 0)]
RING_DOWN = [(1, 0), (2, 1), (3, 2), (0, 3)]
BF = jnp.bfloat16
F32 = jnp.float32


def dot(left, right):
    return jnp.dot(left, right, preferred_element_type=F32)


def turn(value):
    return lax.ppermute(value, ("c", "y"), TURN)


def swap(value, axis):
    return lax.ppermute(value, axis, SWAP)


def up(value):
    return lax.ppermute(value, "z", RING_UP)


def down(value):
    return lax.ppermute(value, "z", RING_DOWN)


def pair_up(first, second, own_index, axis):
    return jnp.where(
        own_index == 0, jnp.stack([first, second], axis), jnp.stack([second, first], axis)
    )


def gather_z(value, z):
    below, above = up(value), down(value)
    half = value.shape[-2] // 2
    far_low = up(below[..., :half, :])
    far_high = down(above[..., half:, :])
    far = jnp.concatenate([far_low, far_high], axis=-2)
    whole = jnp.zeros((4,) + value.shape, value.dtype)
    for offset, part in ((0, value), (3, below), (1, above), (2, far)):
        whole = lax.dynamic_update_index_in_dim(whole, part, (z + offset) % 4, 0)
    return whole


def gather_blocks(value, order, z, x, y):
    done = []
    for axis in order:
        if axis == "z":
            value = gather_z(value, z)
        else:
            place = sum(1 for name in done if "zxy".index(name) < "zxy".index(axis))
            value = pair_up(value, swap(value, axis), {"x": x, "y": y}[axis], place)
        done.append(axis)
    return value.reshape(-1, value.shape[-1])


def gather_split(value, z, x, y):
    value = gather_z(value, z)
    half = value.shape[-1] // 2
    parts = []
    for part, order in ((value[..., :half], "xy"), (value[..., half:], "yx")):
        for step, axis in enumerate(order):
            place = 1 if axis == "x" or step == 0 else 2
            part = pair_up(part, swap(part, axis), {"x": x, "y": y}[axis], place)
        parts.append(part.reshape(-1, half))
    return parts


def sum_pair(blocks, axis_name, own_index, axis):
    theirs = lax.dynamic_index_in_dim(blocks, 1 - own_index, axis, keepdims=False)
    mine = lax.dynamic_index_in_dim(blocks, own_index, axis, keepdims=False)
    return mine.astype(F32) + swap(theirs.astype(BF), axis_name).astype(F32)


def sum_ring(block_of, z):
    far = block_of((z + 2) % 4).astype(BF)
    half = far.shape[0] // 2
    from_below = up(far[:half])
    from_above = down(far[half:])
    pad = ((0, half),) + ((0, 0),) * (far.ndim - 1)
    pad_high = ((half, 0),) + ((0, 0),) * (far.ndim - 1)
    after = block_of((z + 1) % 4) + jnp.pad(from_below, pad).astype(F32)
    before = block_of((z + 3) % 4) + jnp.pad(from_above, pad_high).astype(F32)
    got_up = up(after.astype(BF))
    got_down = down(before.astype(BF))
    return block_of(z) + got_up.astype(F32) + got_down.astype(F32)


def weight_sum(left, right, order, z, x, y):
    width = right.shape[1]
    if order[0] == "z":

        def block_of(place):
            return contract_rows(lax.dynamic_slice_in_dim(left, place * 256, 256, 1), right)

        own = sum_ring(block_of, z).reshape(2, 2, 64, width)
        own = sum_pair(own, "y", y, 1)
        own = sum_pair(own, "x", x, 0)
    else:

        def half_of(x_place):
            columns = [
                lax.dynamic_slice_in_dim(left, step * 256 + x_place * 128, 128, 1)
                for step in range(4)
            ]
            return contract_rows(jnp.concatenate(columns, axis=1), right)

        theirs = swap(half_of(1 - x).astype(BF), "x")
        own = half_of(x) + theirs.astype(F32)
        own = sum_pair(own.reshape(4, 2, 64, width), "y", y, 1)
        own = sum_ring(lambda place: lax.dynamic_index_in_dim(own, place, 0, keepdims=False), z)
    return turn(own.astype(BF)).astype(F32)


def sum_other(value, step):
    if step == "0":
        return lax.ppermute(value, "z", [(0, 1), (1, 0), (2, 3), (3, 2)])
    if step == "1":
        return lax.ppermute(value, "z", [(0, 3), (3, 0), (1, 2), (2, 1)])
    return swap(value, step)


def sum_chips(value, steps):
    for step in steps:
        value = value + sum_other(value, step)
    return value


def tile_bounds(row_lengths, token_count):
    ends = jnp.cumsum(row_lengths)
    span = NQ_ROW * QLEN
    first = jnp.arange(token_count // TILE, dtype=jnp.int32) * TILE - span
    last = first + TILE - 1
    begin = jnp.max(jnp.where(ends[None, :] <= first[:, None], ends[None, :], 0), axis=1)
    end = jnp.min(jnp.where(ends[None, :] > last[:, None], ends[None, :], token_count), axis=1)
    low = jnp.where(first < 0, 0, (begin + span) // TILE)
    high = jnp.where(first < 0, 1, (end + span + TILE - 1) // TILE)
    return jnp.stack([low, high]).astype(jnp.int32)


def rows_of(value, start, count):
    return lax.dynamic_slice_in_dim(value, start, count, 0)


TILE = 256
NEG = -1e30


def exact(left, right, dims):
    return lax.dot_general(left, right, (dims, ((), ())), preferred_element_type=F32)


def head_masks(value):
    lane = lax.broadcasted_iota(jnp.int32, value.shape, 1)
    zero = jnp.zeros_like(value)
    return (jnp.where(lane < HEAD_DIM, value, zero), jnp.where(lane < HEAD_DIM, zero, value))


def fill_bias(seg_col, seg_row, bias):
    for start in range(0, bias.shape[0], TILE):
        rows = slice(start, start + TILE)
        bias[rows, :] = jnp.where(seg_col[rows, :] == seg_row[...], 0.0, NEG)


def attend_kernel(bounds, q_ref, k_ref, v_ref, seg_col, seg_row, out_ref, lse_ref, bias, held):
    @pl.when(pl.program_id(0) == 0)
    def _():
        fill_bias(seg_col, seg_row, bias)

    for block in range(q_ref.shape[0] // TILE):
        own = slice(block * TILE, (block + 1) * TILE)
        queries = head_masks(q_ref[own, :] * HEAD_DIM**-0.5)

        def score(step, highest):
            rows = pl.ds(pl.multiple_of(step * TILE, TILE), TILE)
            keys, shift = k_ref[rows, :], bias[rows, own]
            fresh = []
            for head in range(2):
                scores = exact(keys, queries[head], ((1,), (1,))) + shift
                held[head, rows, :] = scores
                fresh.append(jnp.maximum(highest[head], jnp.max(scores, axis=0, keepdims=True)))
            return tuple(fresh)

        low = jnp.full((1, TILE), NEG, F32)
        highest = lax.fori_loop(bounds[0, block], bounds[1, block], score, (low, low))

        def mix(step, carried):
            rows = pl.ds(pl.multiple_of(step * TILE, TILE), TILE)
            values = v_ref[rows, :]
            fresh = []
            for head in range(2):
                total, mixed = carried[head]
                expo = jnp.exp(held[head, rows, :] - highest[head])
                fresh.append(
                    (
                        total + jnp.sum(expo, axis=0, keepdims=True),
                        mixed + exact(values, expo.astype(BF), ((0,), (0,))),
                    )
                )
            return tuple(fresh)

        start = (jnp.zeros((1, TILE), F32), jnp.zeros((2 * HEAD_DIM, TILE), F32))
        parts = lax.fori_loop(bounds[0, block], bounds[1, block], mix, (start, start))
        mixed = jnp.concatenate(
            [parts[0][1][:HEAD_DIM] / parts[0][0], parts[1][1][HEAD_DIM:] / parts[1][0]], axis=0
        )
        out_ref[own, :] = jnp.transpose(mixed).astype(BF)
        for head in range(2):
            lse_ref[0, head : head + 1, own] = highest[head] + jnp.log(parts[head][0])


def attend(bounds, qkv, seg_col, seg_row):
    count, wide = qkv.shape
    pairs = wide // 3 // 128
    column = lambda shift: pl.BlockSpec((count, 128), lambda i: (0, shift + i))
    whole = lambda shape: pl.BlockSpec(shape, lambda i: (0, 0))
    return pl.pallas_call(
        attend_kernel,
        grid=(pairs,),
        in_specs=[
            pl.BlockSpec(memory_space=pltpu.SMEM),
            column(0),
            column(pairs),
            column(2 * pairs),
            whole((count, 1)),
            whole((1, count)),
        ],
        out_specs=[column(0), pl.BlockSpec((1, 8, count), lambda i: (i, 0, 0))],
        out_shape=[
            jax.ShapeDtypeStruct((count, wide // 3), BF),
            jax.ShapeDtypeStruct((pairs, 8, count), F32),
        ],
        scratch_shapes=[pltpu.VMEM((count, count), F32), pltpu.VMEM((2, count, TILE), F32)],
        compiler_params=pltpu.CompilerParams(vmem_limit_bytes=40 << 20),
        cost_estimate=pl.CostEstimate(
            flops=4 * pairs * count * count * 128,
            transcendentals=pairs * count * count,
            bytes_accessed=4 * count * wide * 2,
        ),
    )(bounds, qkv, qkv, qkv, seg_col, seg_row)


def attend_back_kernel(
    bounds, q_ref, k_ref, v_ref, out_ref, grad_ref, lse_ref, seg_col, seg_row,
    grads_ref, sums_ref, bias, key_sum, value_sum,
):
    pair = pl.program_id(0)

    @pl.when(pair == 0)
    def _():
        fill_bias(seg_col, seg_row, bias)

    key_sum[...] = jnp.zeros_like(key_sum)
    value_sum[...] = jnp.zeros_like(value_sum)
    columns = [
        pl.ds(pl.multiple_of(part * (grads_ref.shape[1] // 3) + pair * 128, 128), 128) for part in range(3)
    ]
    query_total = jnp.zeros((1, 128), F32)
    picks = head_masks(jnp.ones((8, 128), BF))
    for block in range(q_ref.shape[0] // TILE):
        own = slice(block * TILE, (block + 1) * TILE)
        queries = head_masks(q_ref[own, :] * HEAD_DIM**-0.5)
        grads = head_masks(grad_ref[own, :])
        product = grad_ref[own, :].astype(F32) * out_ref[own, :].astype(F32)
        product_high = product.astype(BF)
        product_low = (product - product_high.astype(F32)).astype(BF)
        inner = [
            (
                exact(picks[head], product_high, ((1,), (1,)))
                + exact(picks[head], product_low, ((1,), (1,)))
            )[0:1]
            for head in range(2)
        ]
        lse = [lse_ref[0, head : head + 1, own] for head in range(2)]

        def step_of(step, carried):
            rows = pl.ds(pl.multiple_of(step * TILE, TILE), TILE)
            keys, values, shift = k_ref[rows, :], v_ref[rows, :], bias[rows, own]
            fresh = []
            key_add = jnp.zeros((TILE, 128), F32)
            value_add = jnp.zeros((TILE, 128), F32)
            for head in range(2):
                scores = exact(keys, queries[head], ((1,), (1,))) + shift
                probs = jnp.exp(scores - lse[head])
                grad_probs = exact(values, grads[head], ((1,), (1,)))
                grad_scores = (probs * (grad_probs - inner[head])).astype(BF)
                value_add = value_add + exact(probs.astype(BF), grads[head], ((1,), (0,)))
                key_add = key_add + exact(grad_scores, queries[head], ((1,), (0,)))
                fresh.append(carried[head] + exact(keys, grad_scores, ((0,), (0,))))
            key_sum[rows, :] += key_add
            value_sum[rows, :] += value_add
            return tuple(fresh)

        start = jnp.zeros((2 * HEAD_DIM, TILE), F32)
        parts = lax.fori_loop(bounds[0, block], bounds[1, block], step_of, (start, start))
        grad_query = jnp.concatenate([parts[0][:HEAD_DIM], parts[1][HEAD_DIM:]], axis=0)
        grad_query = jnp.transpose(grad_query * HEAD_DIM**-0.5).astype(BF)
        grads_ref[own, columns[0]] = grad_query
        query_total = query_total + jnp.sum(grad_query.astype(F32), axis=0, keepdims=True)
    grad_value = value_sum[...].astype(BF)
    grads_ref[:, columns[1]] = key_sum[...].astype(BF)
    grads_ref[:, columns[2]] = grad_value
    sums_ref[0, 0:1, :] = query_total
    sums_ref[0, 1:2, :] = jnp.sum(grad_value.astype(F32), axis=0, keepdims=True)


def attend_back(bounds, qkv, mixed, grad_mixed, lse, seg_col, seg_row):
    count, wide = qkv.shape
    pairs = wide // 3 // 128
    column = lambda shift: pl.BlockSpec((count, 128), lambda i: (0, shift + i))
    whole = lambda shape: pl.BlockSpec(shape, lambda i: (0, 0))
    return pl.pallas_call(
        attend_back_kernel,
        grid=(pairs,),
        in_specs=[
            pl.BlockSpec(memory_space=pltpu.SMEM),
            column(0),
            column(pairs),
            column(2 * pairs),
            column(0),
            column(0),
            pl.BlockSpec((1, 8, count), lambda i: (i, 0, 0)),
            whole((count, 1)),
            whole((1, count)),
        ],
        out_specs=[whole((count, wide)), pl.BlockSpec((1, 8, 128), lambda i: (i, 0, 0))],
        out_shape=[
            jax.ShapeDtypeStruct((count, wide), BF),
            jax.ShapeDtypeStruct((pairs, 8, 128), F32),
        ],
        scratch_shapes=[
            pltpu.VMEM((count, count), F32),
            pltpu.VMEM((count, 128), F32),
            pltpu.VMEM((count, 128), F32),
        ],
        compiler_params=pltpu.CompilerParams(vmem_limit_bytes=40 << 20),
        cost_estimate=pl.CostEstimate(
            flops=10 * pairs * count * count * 128,
            transcendentals=pairs * count * count,
            bytes_accessed=8 * count * wide * 2,
        ),
    )(bounds, qkv, qkv, qkv, mixed, grad_mixed, lse, seg_col, seg_row)


ERFC = (
    -1.26551223, 1.00002368, 0.37409196, 0.09678418, -0.18628806,
    0.27886807, -1.13520398, 1.48851587, -0.82215223, 0.17087277,
)


def gelu_pair(value):
    size = jnp.abs(value) * 0.5**0.5
    ratio = 1.0 / (1.0 + 0.5 * size)
    series = jnp.full_like(value, ERFC[-1])
    for factor in ERFC[-2::-1]:
        series = series * ratio + factor
    bell = jnp.exp(-size * size)
    tail = 0.5 * ratio * bell * jnp.exp(series)
    phi = jnp.where(value < 0.0, tail, 1.0 - tail)
    return (value * phi, phi + value * bell * 0.3989422804014327)


def expand_kernel(x_ref, w_ref, b_ref, act_ref, slope_ref):
    rows = 256
    for start in range(0, x_ref.shape[0], rows):
        part = slice(start, start + rows)
        value = exact(x_ref[part, :], w_ref[...], ((1,), (0,))) + b_ref[...]
        active, slope = gelu_pair(value)
        act_ref[part, :] = active.astype(BF)
        slope_ref[part, :] = slope.astype(BF)


def expand(value, weight, shift):
    count, depth = value.shape
    width = weight.shape[1]
    tile = 256
    return pl.pallas_call(
        expand_kernel,
        grid=(width // tile,),
        in_specs=[
            pl.BlockSpec((count, depth), lambda i: (0, 0)),
            pl.BlockSpec((depth, tile), lambda i: (0, i)),
            pl.BlockSpec((1, tile), lambda i: (0, i)),
        ],
        out_specs=[pl.BlockSpec((count, tile), lambda i: (0, i))] * 2,
        out_shape=[jax.ShapeDtypeStruct((count, width), BF)] * 2,
        compiler_params=pltpu.CompilerParams(vmem_limit_bytes=32 << 20),
        cost_estimate=pl.CostEstimate(
            flops=2 * count * depth * width,
            transcendentals=3 * count * width,
            bytes_accessed=2 * (count * depth + depth * width + 2 * count * width),
        ),
    )(value, weight, shift)


def cut_levels(raw, cuts):
    lane = lax.broadcasted_iota(jnp.int32, raw.shape, 1)
    levels = []
    for cut in cuts:
        part = jnp.where(lane < cut, raw, 0.0)
        scale = lax.rsqrt(jnp.sum(part * part, axis=1, keepdims=True) + EPS_EMBED)
        levels.append(((part * scale).astype(BF), part, scale))
    return levels


def pool_kernel(cuts, span, q_ref, d_ref, seg_ref, out_ref, units, hot):
    @pl.when(pl.program_id(0) == 0)
    def _():
        raw = d_ref[span:, :].astype(F32)
        for level, parts in enumerate(cut_levels(raw, cuts)):
            units[level] = parts[0]
        doc = lax.broadcasted_iota(jnp.int32, hot.shape, 0)
        hot[...] = (seg_ref[:, span:] == NQ_ROW + doc).astype(F32).astype(BF)

    levels = cut_levels(q_ref[...].astype(F32), cuts)
    for level in range(len(cuts)):
        similar = exact(units[level], levels[level][0], ((1,), (1,)))
        expo = jnp.exp(similar * (1.0 / POOL_TEMP))
        high = expo.astype(BF)
        rest = (expo - high.astype(F32)).astype(BF)
        out_ref[level * NDOC : (level + 1) * NDOC, :] = exact(
            hot[...], high, ((1,), (0,))
        ) + exact(hot[...], rest, ((1,), (0,)))


def pool(cuts, span, queries, row_embed, seg_row):
    count, width = queries.shape
    tokens = row_embed.shape[0]
    whole = lambda shape: pl.BlockSpec(shape, lambda i: (0, 0))
    return pl.pallas_call(
        partial(pool_kernel, cuts, span),
        grid=(count // TILE,),
        in_specs=[
            pl.BlockSpec((TILE, width), lambda i: (i, 0)),
            whole((tokens, width)),
            whole((1, tokens)),
        ],
        out_specs=pl.BlockSpec((len(cuts) * NDOC, TILE), lambda i: (0, i)),
        out_shape=jax.ShapeDtypeStruct((len(cuts) * NDOC, count), F32),
        scratch_shapes=[
            pltpu.VMEM((len(cuts), tokens - span, width), BF),
            pltpu.VMEM((NDOC, tokens - span), BF),
        ],
        compiler_params=pltpu.CompilerParams(vmem_limit_bytes=32 << 20),
        cost_estimate=pl.CostEstimate(
            flops=2 * len(cuts) * count * tokens * 256,
            transcendentals=len(cuts) * count * tokens,
            bytes_accessed=2 * (count + tokens) * width,
        ),
    )(queries, row_embed, seg_row)


def level_back(grad, part, scale):
    return scale * grad - part * (scale * scale * scale) * jnp.sum(
        part * grad, axis=1, keepdims=True
    )


def pool_back_kernel(
    cuts, span, q_ref, d_ref, seg_ref, coef_ref, q_out, d_out, units, units_t, hot, sums
):
    step = pl.program_id(0)

    @pl.when(step == 0)
    def _():
        raw = d_ref[span:, :].astype(F32)
        for level, parts in enumerate(cut_levels(raw, cuts)):
            units[level] = parts[0]
            units_t[level] = jnp.transpose(parts[0])
        doc = lax.broadcasted_iota(jnp.int32, hot.shape, 0)
        wanted = NQ_ROW + jnp.where(doc < NDOC, doc, doc - NDOC)
        hot[...] = (seg_ref[:, span:] == wanted).astype(F32).astype(BF)
        sums[...] = jnp.zeros_like(sums)

    levels = cut_levels(q_ref[...].astype(F32), cuts)
    total = jnp.zeros(q_ref.shape, F32)
    for level in range(len(cuts)):
        unit, part, scale = levels[level]
        similar = exact(units[level], unit, ((1,), (1,)))
        coef = coef_ref[level * NDOC : (level + 1) * NDOC, :]
        high = coef.astype(BF).astype(F32)
        both = jnp.concatenate([high, coef - high], axis=0).astype(BF)
        spread = exact(hot[...], both, ((0,), (0,)))
        grad = (jnp.exp(similar * (1.0 / POOL_TEMP)) * spread).astype(BF)
        sums[level] += exact(grad, unit, ((1,), (0,)))
        grad_unit = jnp.transpose(exact(units_t[level], grad, ((1,), (0,))))
        total = total + level_back(grad_unit, part, scale)
    q_out[...] = total.astype(BF)

    @pl.when(step == pl.num_programs(0) - 1)
    def _():
        raw = d_ref[span:, :].astype(F32)
        result = jnp.zeros(raw.shape, F32)
        for level, parts in enumerate(cut_levels(raw, cuts)):
            lane = lax.broadcasted_iota(jnp.int32, raw.shape, 1)
            grad = jnp.where(lane < cuts[level], sums[level], 0.0)
            result = result + level_back(grad, parts[1], parts[2])
        d_out[...] = result


def pool_back(cuts, span, queries, row_embed, seg_row, coef):
    count, width = queries.shape
    tokens = row_embed.shape[0]
    docs = tokens - span
    whole = lambda shape: pl.BlockSpec(shape, lambda i: (0, 0))
    return pl.pallas_call(
        partial(pool_back_kernel, cuts, span),
        grid=(count // TILE,),
        in_specs=[
            pl.BlockSpec((TILE, width), lambda i: (i, 0)),
            whole((tokens, width)),
            whole((1, tokens)),
            pl.BlockSpec((len(cuts) * NDOC, TILE), lambda i: (0, i)),
        ],
        out_specs=[pl.BlockSpec((TILE, width), lambda i: (i, 0)), whole((docs, width))],
        out_shape=[
            jax.ShapeDtypeStruct((count, width), BF),
            jax.ShapeDtypeStruct((docs, width), F32),
        ],
        scratch_shapes=[
            pltpu.VMEM((len(cuts), docs, width), BF),
            pltpu.VMEM((len(cuts), width, docs), BF),
            pltpu.VMEM((2 * NDOC, docs), BF),
            pltpu.VMEM((len(cuts), docs, width), F32),
        ],
        compiler_params=pltpu.CompilerParams(vmem_limit_bytes=32 << 20),
        cost_estimate=pl.CostEstimate(
            flops=2 * len(cuts) * count * docs * 512,
            transcendentals=len(cuts) * count * docs,
            bytes_accessed=4 * (count + tokens) * width,
        ),
    )(queries, row_embed, seg_row, coef)


def local_chip(
    tokens,
    lengths,
    pairing,
    w_qkv,
    b_qv,
    w_out,
    b_out,
    ln_gain,
    ln_bias,
    w_up,
    b_up,
    w_down,
    b_down,
    w_proj,
    cot,
):
    z, x, c, y = (lax.axis_index(name) for name in ("z", "x", "c", "y"))
    chip = 4 * z + 2 * x + y
    token_count, width = tokens.shape
    share = token_count // 2
    own_start, other_start = c * share, (1 - c) * share
    gains, shifts = ln_gain.astype(F32), ln_bias.astype(F32)

    half_width = w_qkv.shape[2]
    qkv_rows = jnp.concatenate([w_qkv[0], w_qkv[1], w_qkv[2]], axis=1)
    full_qkv = gather_blocks(turn(qkv_rows), "xyz", z, x, y)
    row = jnp.where(c == y, tokens, swap(tokens, "c"))
    bias = turn(jnp.concatenate([b_qv.reshape(-1), b_up])[None].astype(F32))
    mid_rows = turn(jnp.concatenate([w_up, w_out.T], axis=1))
    up_wide = w_up.shape[1]
    full_mid = gather_blocks(mid_rows, "zyx", z, x, y)
    full_up, full_out = full_mid[:, :up_wide], full_mid[:, up_wide:]
    full_down = gather_blocks(turn(w_down.T), "xyz", z, x, y)
    own_cot = turn(cot)
    half_queries = NQ_ROW // 2
    chip_count = lengths.shape[0]
    query_total = chip_count * half_queries
    pairs = lax.dynamic_update_slice_in_dim(
        jnp.zeros((1, query_total), F32), turn(pairing).astype(F32), chip * half_queries, 1
    )
    pairs = sum_chips(pairs, "xy01").astype(jnp.int32)

    row_lengths = lax.dynamic_index_in_dim(lengths, chip, 0, keepdims=False)
    segments = segments_of(row_lengths, token_count)
    seg_col, seg_row = segments[:, None], segments[None, :]
    query_span = NQ_ROW * QLEN
    bounds = tile_bounds(row_lengths, token_count)
    qkv_bias = jnp.concatenate(
        [bias[:, :half_width], jnp.zeros_like(bias[:, :half_width]), bias[:, half_width : 2 * half_width]],
        axis=1,
    )
    qkv = (dot(row, full_qkv) + qkv_bias).astype(BF)
    mixed, lse = attend(bounds, qkv, seg_col, seg_row)

    def row_sum(left, weight_t, transposed):
        times = contract_cols if transposed else dot
        theirs = swap(times(left(1), weight_t).astype(BF), "c")
        return times(left(0), weight_t) + theirs.astype(F32)

    def mixed_half(which):
        return rows_of(mixed, other_start if which else own_start, share)

    attn_sum = row_sum(mixed_half, full_out, True)
    own_tokens = rows_of(row, own_start, share).astype(F32)
    normed, unit_one, rstd_one = norm_forward(
        own_tokens + attn_sum + b_out.astype(F32), gains[0], shifts[0]
    )
    normed_low = normed.astype(BF)
    normed_all = jnp.concatenate([normed_low, swap(normed_low, "c")], axis=0)
    activation, slope = expand(normed_all, full_up, bias[:, 2 * half_width :])
    ffn_sum = row_sum(
        lambda which: activation[which * share : (which + 1) * share], full_down, True
    )
    result, unit_two, rstd_two = norm_forward(
        normed + ffn_sum + b_down.astype(F32), gains[1], shifts[1]
    )
    result_low = result.astype(BF)
    y_out = turn(result_low)
    embed = dot(result_low, w_proj).astype(BF)

    other_embed = swap(embed, "c")
    row_embed = jnp.where(
        c == 0,
        jnp.concatenate([embed, other_embed], axis=0),
        jnp.concatenate([other_embed, embed], axis=0),
    )
    half_span = query_span // 2
    own_queries = rows_of(row_embed, c * half_span, half_span)
    chips = ("z", "x", "y")
    queries = lax.all_to_all(
        jnp.broadcast_to(own_queries[None], (chip_count,) + own_queries.shape), chips, 0, 0
    ).reshape(chip_count * half_span, -1)
    proj_width = w_proj.shape[1]
    cuts = (proj_width, 3 * proj_width // 4, proj_width // 2)
    sums = pool(cuts, query_span, queries, row_embed, seg_row)
    doc_sizes = jnp.tile(row_lengths.astype(F32), 3)[:, None]
    group = (
        jnp.arange(query_total * QLEN, dtype=jnp.int32)[:, None] // QLEN
        == jnp.arange(query_total, dtype=jnp.int32)[None, :]
    ).astype(F32)
    pooled = POOL_TEMP * jnp.log(sums / doc_sizes)
    logits = jnp.dot(pooled, group, precision=FULL_PRECISION) / LOSS_TEMP
    logits = logits.reshape(3, NDOC, query_total)
    doc_numbers = chip * NDOC + jnp.arange(NDOC, dtype=jnp.int32)
    picked = (doc_numbers[:, None] == pairs).astype(F32)
    own_high = jnp.max(logits, axis=1)
    own_lse = own_high + jnp.log(jnp.sum(jnp.exp(logits - own_high[:, None]), axis=1))
    own_target = jnp.sum(logits * picked, axis=1)
    notes = jnp.pad(jnp.concatenate([own_lse, own_target], axis=1), ((0, 5), (0, 0)))
    notes = lax.all_to_all(
        jnp.broadcast_to(notes[None], (chip_count,) + notes.shape), chips, 0, 0
    )
    chip_lse = notes[:, :3, :query_total]
    high = jnp.max(chip_lse, axis=0)
    all_lse = high + jnp.log(jnp.sum(jnp.exp(chip_lse - high), axis=0))
    target = jnp.sum(notes[:, :3, query_total:], axis=0)
    losses = jnp.sum(all_lse - target, axis=0).reshape(chip_count, half_queries)
    grad_logits = (jnp.exp(logits - all_lse[:, None]) - picked) / LOSS_TEMP
    coefficient = (
        lax.dot_general(
            grad_logits.reshape(3 * NDOC, query_total),
            group,
            (((1,), (1,)), ((), ())),
            precision=FULL_PRECISION,
        )
        / sums
    )
    losses = jnp.where(c == y, losses, swap(losses, "c"))
    loss_out = rows_of(losses, 4 * z + 2 * x + c, 1)
    query_grad, doc_grad = pool_back(cuts, query_span, queries, row_embed, seg_row, coefficient)
    grad_blocks = lax.all_to_all(
        query_grad.reshape(chip_count, half_span, proj_width), chips, 0, 0
    )
    own_query_grad = jnp.sum(grad_blocks.astype(F32), axis=0)
    row_grad = jnp.concatenate([jnp.zeros((query_span, proj_width), F32), doc_grad], axis=0)
    row_grad = lax.dynamic_update_slice_in_dim(row_grad, own_query_grad, c * half_span, 0)
    grad_embed = rows_of(row_grad, own_start, share) + swap(
        rows_of(row_grad, other_start, share), "c"
    )

    proj_low = w_proj
    grad_embed_low = grad_embed.astype(BF)
    grad_embed_rest = (grad_embed - grad_embed_low.astype(F32)).astype(BF)
    grad_result = own_cot.astype(F32) + (
        contract_cols(grad_embed_low, proj_low) + contract_cols(grad_embed_rest, proj_low)
    )
    proj_grad = contract_rows(result_low, grad_embed_low) + contract_rows(
        result_low, grad_embed_rest
    )
    gain_two = jnp.sum(grad_result * unit_two, axis=0)
    shift_two = jnp.sum(grad_result, axis=0)
    grad_second = norm_backward(grad_result, unit_two, rstd_two, gains[1])
    grad_ffn = grad_second.astype(BF)
    down_bias = jnp.sum(grad_ffn.astype(F32), axis=0)
    grad_ffn_all = jnp.concatenate([grad_ffn, swap(grad_ffn, "c")], axis=0)
    down_part = weight_sum(grad_ffn_all, activation, "zyx", z, x, y)
    grad_up = (dot(grad_ffn_all, full_down) * slope.astype(F32)).astype(BF)
    up_bias = jnp.sum(grad_up.astype(F32), axis=0)
    up_part = weight_sum(normed_all, grad_up, "xyz", z, x, y)
    grad_normed = (
        row_sum(lambda which: grad_up[which * share : (which + 1) * share], full_up, True)
        + grad_second
    )
    gain_one = jnp.sum(grad_normed * unit_one, axis=0)
    shift_one = jnp.sum(grad_normed, axis=0)
    grad_first = norm_backward(grad_normed, unit_one, rstd_one, gains[0])
    grad_attn = grad_first.astype(BF)
    out_bias = jnp.sum(grad_attn.astype(F32), axis=0)
    other_attn = swap(grad_attn, "c")
    grad_attn_all = jnp.where(
        c == 0,
        jnp.concatenate([grad_attn, other_attn], axis=0),
        jnp.concatenate([other_attn, grad_attn], axis=0),
    )
    out_part = weight_sum(grad_attn_all, mixed, "zyx", z, x, y)
    grad_mixed = dot(grad_attn_all, full_out).astype(BF)
    grads, grad_sums = attend_back(bounds, qkv, mixed, grad_mixed, lse, seg_col, seg_row)
    qkv_part = weight_sum(row, grads, "zyx", z, x, y)
    grad_input = turn(
        (
            row_sum(
                lambda which: rows_of(grads, other_start if which else own_start, share),
                full_qkv,
                True,
            )
            + grad_first
        ).astype(BF)
    )

    half_sums = jnp.concatenate(
        [grad_sums[:, 0].reshape(-1), grad_sums[:, 1].reshape(-1), up_bias]
    ).reshape(-1, 128)
    half_sums = sum_chips(half_sums, "xy01")
    half_sums = jnp.where(c == y, half_sums, swap(half_sums, "c")).reshape(-1)
    shared = jnp.stack([gain_one, gain_two, shift_one, shift_two, out_bias, down_bias])
    shared = sum_chips(shared, "cxy01")
    proj_half = rows_of(proj_grad, own_start, share) + swap(
        rows_of(proj_grad, other_start, share), "c"
    )
    for step in ("x", "y", "0", "1"):
        proj_half = proj_half + sum_other(proj_half.astype(BF), step).astype(F32)
    proj_sum = pair_up(proj_half, swap(proj_half, "c"), c, 0).reshape(width, -1)
    return (
        y_out,
        loss_out,
        grad_input,
        jnp.stack([qkv_part[:, k * half_width : (k + 1) * half_width] for k in range(3)]),
        half_sums[: 2 * half_width].reshape(2, half_width),
        out_part.T,
        shared[4],
        shared[0:2],
        shared[2:4],
        up_part,
        half_sums[2 * half_width :],
        down_part.T,
        shared[5],
        proj_sum,
    )


IN_SPECS = (
    P("dp", None),
    P(),
    P("dp", "tensor"),
    P(None, "dp", "tensor"),
    P(None, "tensor"),
    P("tensor", "dp"),
    P(),
    P(),
    P(),
    P("dp", "tensor"),
    P("tensor"),
    P("tensor", "dp"),
    P(),
    P(),
    P(("dp", "tensor"), None),
)
OUT_SPECS = (
    P(("dp", "tensor"), None),
    P("dp", "tensor"),
    P(("dp", "tensor"), None),
    P(None, "dp", "tensor"),
    P(None, "tensor"),
    P("tensor", "dp"),
    P(),
    P(),
    P(),
    P("dp", "tensor"),
    P("tensor"),
    P("tensor", "dp"),
    P(),
    P(),
)


def solution(mesh):
    if mesh.devices.shape != (16, 2):
        return jax.shard_map(
            local, mesh=mesh, in_specs=IN_SPECS, out_specs=OUT_SPECS, check_vma=False
        )
    names = {"dp": ("z", "x", "c"), "tensor": ("y",)}

    def respec(spec):
        parts = []
        for entry in spec:
            axes = () if entry is None else entry if isinstance(entry, tuple) else (entry,)
            parts.append(tuple(name for axis in axes for name in names[axis]) or None)
        return P(*parts)

    chips = Mesh(mesh.devices.reshape(4, 2, 2, 2), ("z", "x", "c", "y"))
    return jax.shard_map(
        local_chip,
        mesh=chips,
        in_specs=tuple(respec(spec) for spec in IN_SPECS),
        out_specs=tuple(respec(spec) for spec in OUT_SPECS),
        check_vma=False,
    )
```

```python
from functools import partial

import jax
import jax.numpy as jnp
from jax import lax
from jax.experimental import pallas as pl
from jax.experimental.pallas import tpu as pltpu
from jax.sharding import Mesh, PartitionSpec as P

HEAD_DIM = 64
QLEN = 32
NQ_ROW = 8
NDOC = 8


EPS_NORM = 1e-05
EPS_EMBED = 1e-06
POOL_TEMP = 0.1
LOSS_TEMP = 0.1
FULL_PRECISION = lax.Precision.HIGHEST
MASKED_SCORE = -1e30


def shortened(shard):

    def short(part):
        return part.astype(jnp.bfloat16) if part.dtype == jnp.float32 else part

    return jax.tree.map(short, shard)


def contract_rows(left, right, precision=None):
    return lax.dot_general(
        left,
        right,
        (((0,), (0,)), ((), ())),
        precision=precision,
        preferred_element_type=jnp.float32,
    )


def contract_cols(left, right, precision=None):
    return lax.dot_general(
        left,
        right,
        (((1,), (1,)), ((), ())),
        precision=precision,
        preferred_element_type=jnp.float32,
    )


def norm_forward(value, gain, shift):
    centred = value - jnp.mean(value, axis=1, keepdims=True)
    rstd = lax.rsqrt(jnp.mean(centred * centred, axis=1, keepdims=True) + EPS_NORM)
    unit = centred * rstd
    return (unit * gain + shift, unit, rstd)


def norm_backward(grad, unit, rstd, gain):
    scaled = grad * gain
    return rstd * (
        scaled
        - jnp.mean(scaled, axis=1, keepdims=True)
        - unit * jnp.mean(scaled * unit, axis=1, keepdims=True)
    )


def segments_of(row_lengths, token_count):
    position = jnp.arange(token_count, dtype=jnp.int32)
    query_span = NQ_ROW * QLEN
    ends = jnp.cumsum(row_lengths)
    passed = jnp.sum((position[:, None] - query_span >= ends[None, :]).astype(jnp.int32), axis=1)
    return jnp.where(position < query_span, position // QLEN, NQ_ROW + passed)


def normalize_cut(raw, width):
    part = raw[:, :width]
    scale = lax.rsqrt(jnp.sum(part * part, axis=1, keepdims=True) + EPS_EMBED)
    return (part * scale, part, scale)


def normalize_back(grad, part, scale, full_width):
    result = scale * grad - part * (scale * scale * scale) * jnp.sum(
        part * grad, axis=1, keepdims=True
    )
    return jnp.pad(result, ((0, 0), (0, full_width - grad.shape[1])))


def masked_scores(query_block, key_rows, block_segments, segments):
    scores = jnp.einsum(
        "qhd,khd->hqk", query_block, key_rows, preferred_element_type=jnp.float32
    ) * HEAD_DIM ** (-0.5)
    return jnp.where((block_segments[:, None] == segments[None, :])[None], scores, MASKED_SCORE)


def attend_forward(query_rows, key_rows, value_rows, segments, block_rows):
    token_count = query_rows.shape[0]

    def one_block(block_start):
        query_block = lax.dynamic_slice_in_dim(query_rows, block_start, block_rows, 0)
        block_segments = lax.dynamic_slice_in_dim(segments, block_start, block_rows, 0)
        scores = masked_scores(query_block, key_rows, block_segments, segments)
        highest = jnp.max(scores, axis=2, keepdims=True)
        expo = jnp.exp(scores - highest)
        totals = jnp.sum(expo, axis=2, keepdims=True)
        weights = (expo / totals).astype(jnp.bfloat16)
        mixed = jnp.einsum("hqk,khd->qhd", weights, value_rows, preferred_element_type=jnp.float32)
        return (mixed.astype(jnp.bfloat16), (highest + jnp.log(totals))[:, :, 0])

    starts = jnp.arange(token_count // block_rows, dtype=jnp.int32) * block_rows
    mixed, log_totals = lax.map(one_block, starts)
    return (mixed.reshape(token_count, -1), log_totals)


def attend_backward(query_rows, key_rows, value_rows, segments, log_totals, grad_mixed, block_rows):
    token_count, local_heads, head_size = query_rows.shape
    scale = HEAD_DIM ** (-0.5)
    grad_heads = grad_mixed.reshape(token_count, local_heads, head_size)

    def one_block(carried, inputs):
        grad_keys, grad_values = carried
        block_start, block_lse = inputs
        query_block = lax.dynamic_slice_in_dim(query_rows, block_start, block_rows, 0)
        grad_block = lax.dynamic_slice_in_dim(grad_heads, block_start, block_rows, 0)
        block_segments = lax.dynamic_slice_in_dim(segments, block_start, block_rows, 0)
        scores = masked_scores(query_block, key_rows, block_segments, segments)
        probs = jnp.exp(scores - block_lse[:, :, None])
        grad_probs = jnp.einsum(
            "qhd,khd->hqk", grad_block, value_rows, preferred_element_type=jnp.float32
        )
        inner = jnp.sum(probs * grad_probs, axis=2, keepdims=True)
        grad_scores = (probs * (grad_probs - inner)).astype(jnp.bfloat16)
        grad_query = (
            jnp.einsum("hqk,khd->qhd", grad_scores, key_rows, preferred_element_type=jnp.float32)
            * scale
        )
        grad_keys = (
            grad_keys
            + jnp.einsum(
                "hqk,qhd->khd", grad_scores, query_block, preferred_element_type=jnp.float32
            )
            * scale
        )
        grad_values = grad_values + jnp.einsum(
            "hqk,qhd->khd",
            probs.astype(jnp.bfloat16),
            grad_block,
            preferred_element_type=jnp.float32,
        )
        return ((grad_keys, grad_values), grad_query)

    starts = jnp.arange(token_count // block_rows, dtype=jnp.int32) * block_rows
    zero_rows = jnp.zeros(key_rows.shape, jnp.float32)
    (grad_keys, grad_values), grad_queries = lax.scan(
        one_block, (zero_rows, zero_rows), (starts, log_totals)
    )
    flat_width = local_heads * head_size
    return (
        grad_queries.reshape(token_count, flat_width),
        grad_keys.reshape(token_count, flat_width),
        grad_values.reshape(token_count, flat_width),
    )


def local(
    tokens,
    lengths,
    pairing,
    w_qkv,
    b_qv,
    w_out,
    b_out,
    ln_gain,
    ln_bias,
    w_up,
    b_up,
    w_down,
    b_down,
    w_proj,
    cot,
):
    tensor_count = lax.axis_size("tensor")
    tensor_index = lax.axis_index("tensor")
    data_index = lax.axis_index("dp")
    token_count = tokens.shape[0]
    share_rows = token_count // tensor_count
    block_rows = min(512, token_count)
    own_start = tensor_index * share_rows
    full_qkv, full_out, full_up, full_down = (
        lax.all_gather(w_qkv, "dp", axis=1, tiled=True),
        lax.all_gather(w_out, "dp", axis=1, tiled=True),
        lax.all_gather(w_up, "dp", axis=0, tiled=True),
        lax.all_gather(w_down, "dp", axis=1, tiled=True),
    )
    head_width = full_qkv.shape[2]
    local_heads = head_width // HEAD_DIM
    row_lengths = lax.dynamic_index_in_dim(lengths, data_index, 0, keepdims=False)
    segments = segments_of(row_lengths, token_count)
    projected = jnp.einsum("td,kdw->ktw", tokens, full_qkv, preferred_element_type=jnp.float32)
    qv_bias = b_qv.astype(jnp.float32)
    query_rows = (
        (projected[0] + qv_bias[0]).astype(jnp.bfloat16).reshape(token_count, local_heads, HEAD_DIM)
    )
    key_rows = projected[1].astype(jnp.bfloat16).reshape(token_count, local_heads, HEAD_DIM)
    value_rows = (
        (projected[2] + qv_bias[1]).astype(jnp.bfloat16).reshape(token_count, local_heads, HEAD_DIM)
    )
    mixed, log_totals = attend_forward(query_rows, key_rows, value_rows, segments, block_rows)
    attn_terms = jnp.dot(mixed, full_out, preferred_element_type=jnp.float32)
    attn_sum = lax.psum_scatter(
        attn_terms.astype(jnp.bfloat16), "tensor", scatter_dimension=0, tiled=True
    ).astype(jnp.float32)
    own_tokens = lax.dynamic_slice_in_dim(tokens, own_start, share_rows, 0).astype(jnp.float32)
    gains = ln_gain.astype(jnp.float32)
    shifts = ln_bias.astype(jnp.float32)
    normed, unit_one, rstd_one = norm_forward(
        own_tokens + attn_sum + b_out.astype(jnp.float32), gains[0], shifts[0]
    )
    normed_all = lax.all_gather(normed.astype(jnp.bfloat16), "tensor", axis=0, tiled=True)
    up_value = jnp.dot(normed_all, full_up, preferred_element_type=jnp.float32) + b_up.astype(
        jnp.float32
    )
    activation = jax.nn.gelu(up_value, approximate=False).astype(jnp.bfloat16)
    ffn_terms = jnp.dot(activation, full_down, preferred_element_type=jnp.float32)
    ffn_sum = lax.psum_scatter(
        ffn_terms.astype(jnp.bfloat16), "tensor", scatter_dimension=0, tiled=True
    ).astype(jnp.float32)
    result, unit_two, rstd_two = norm_forward(
        normed + ffn_sum + b_down.astype(jnp.float32), gains[1], shifts[1]
    )
    result_low = result.astype(jnp.bfloat16)
    embed = jnp.dot(result_low, w_proj, preferred_element_type=jnp.float32).astype(jnp.bfloat16)
    embed_all = lax.all_gather(embed, ("dp", "tensor"), axis=0, tiled=True)
    row_count = lengths.shape[0]
    proj_width = w_proj.shape[1]
    widths = (proj_width, 3 * proj_width // 4, proj_width // 2)
    per_device = pairing.shape[1]
    query_count = per_device * QLEN
    query_span = NQ_ROW * QLEN
    emb_rows = embed_all.reshape(row_count, token_count, proj_width)
    my_row = lax.dynamic_index_in_dim(emb_rows, data_index, 0, keepdims=False)
    query_raw = lax.dynamic_slice_in_dim(my_row, tensor_index * query_count, query_count, 0).astype(
        jnp.float32
    )
    query_levels = [normalize_cut(query_raw, width) for width in widths]
    query_units = [level_parts[0].astype(jnp.bfloat16) for level_parts in query_levels]
    doc_numbers = jnp.arange(NDOC, dtype=jnp.int32)

    def row_pool(carried, inputs):
        row_emb, lengths_row = inputs
        row_hot = (
            segments_of(lengths_row, token_count)[:, None] == NQ_ROW + doc_numbers[None, :]
        ).astype(jnp.float32)
        row_raw = row_emb.astype(jnp.float32)
        pooled_list = []
        sums_list = []
        for width, query_unit in zip(widths, query_units):
            doc_unit = normalize_cut(row_raw, width)[0].astype(jnp.bfloat16)
            expo = jnp.exp(contract_cols(query_unit, doc_unit) / POOL_TEMP)
            sums = jnp.dot(expo, row_hot, precision=FULL_PRECISION)
            pooled = POOL_TEMP * jnp.log(sums / lengths_row.astype(jnp.float32))
            pooled_list.append(jnp.sum(pooled.reshape(per_device, QLEN, NDOC), axis=1))
            sums_list.append(sums)
        return (carried, (jnp.stack(pooled_list), jnp.stack(sums_list)))

    _, (row_scores, row_sums) = lax.scan(row_pool, 0, (emb_rows, lengths))
    logits = (
        jnp.transpose(row_scores, (2, 1, 0, 3)).reshape(per_device, 3, row_count * NDOC) / LOSS_TEMP
    )
    own_pairs = pairing[0]
    target = jnp.take_along_axis(
        logits, jnp.broadcast_to(own_pairs[:, None, None], (per_device, 3, 1)), axis=2
    )[:, :, 0]
    loss_out = jnp.sum(jax.nn.logsumexp(logits, axis=2) - target, axis=1).reshape(1, per_device)
    picked = (
        jnp.arange(row_count * NDOC, dtype=jnp.int32)[None, None, :] == own_pairs[:, None, None]
    ).astype(jnp.float32)
    grad_logits = (jax.nn.softmax(logits, axis=2) - picked) / LOSS_TEMP
    grad_rows = jnp.transpose(grad_logits.reshape(per_device, 3, row_count, NDOC), (2, 1, 0, 3))
    coefficient = jnp.repeat(grad_rows, QLEN, axis=2) / row_sums

    def row_back(carried, inputs):
        row_emb, lengths_row, row_coef = inputs
        row_hot = (
            segments_of(lengths_row, token_count)[:, None] == NQ_ROW + doc_numbers[None, :]
        ).astype(jnp.float32)
        row_raw = row_emb.astype(jnp.float32)
        new_carried = []
        row_grad = jnp.zeros((token_count, proj_width), jnp.float32)
        for level_index in range(3):
            width = widths[level_index]
            doc_unit_f, doc_part, doc_scale = normalize_cut(row_raw, width)
            doc_unit = doc_unit_f.astype(jnp.bfloat16)
            expo = jnp.exp(contract_cols(query_units[level_index], doc_unit) / POOL_TEMP)
            spread = contract_cols(row_coef[level_index], row_hot, FULL_PRECISION)
            grad_sim = (expo * spread).astype(jnp.bfloat16)
            new_carried.append(
                carried[level_index]
                + jnp.dot(grad_sim, doc_unit, preferred_element_type=jnp.float32)
            )
        return (tuple(new_carried), row_grad)

    zero_query = tuple((jnp.zeros((query_count, width), jnp.float32) for width in widths))
    query_grads, doc_grads = lax.scan(row_back, zero_query, (emb_rows, lengths, coefficient))
    grad_query = jnp.zeros((query_count, proj_width), jnp.float32)
    for level_index in range(3):
        level_parts = query_levels[level_index]
        grad_query = grad_query + normalize_back(
            query_grads[level_index], level_parts[1], level_parts[2], proj_width
        )
    coef_mine = jnp.transpose(coefficient, (2, 1, 0, 3)).reshape(query_count, 3, row_count * NDOC)
    coef_all, grad_query_all = (
        lax.all_gather(shortened(coef_mine), ("dp", "tensor"), axis=0, tiled=True).astype(
            coef_mine.dtype
        ),
        lax.all_gather(
            grad_query.astype(jnp.bfloat16), ("dp", "tensor"), axis=0, tiled=True
        ).astype(grad_query.dtype),
    )
    own_raw = embed.astype(jnp.float32)
    own_segments = lax.dynamic_slice_in_dim(segments, own_start, share_rows, 0)
    own_docs = jnp.where(own_segments >= NQ_ROW, data_index * NDOC + own_segments - NQ_ROW, -1)
    own_hot = (own_docs[:, None] == jnp.arange(row_count * NDOC, dtype=jnp.int32)[None, :]).astype(
        jnp.float32
    )
    queries_all = (
        emb_rows[:, :query_span].reshape(row_count * query_span, proj_width).astype(jnp.float32)
    )
    grad_embed = jnp.zeros((share_rows, proj_width), jnp.float32)
    for level_index in range(3):
        width = widths[level_index]
        query_unit_all = normalize_cut(queries_all, width)[0].astype(jnp.bfloat16)
        doc_unit_f, doc_part, doc_scale = normalize_cut(own_raw, width)
        expo = jnp.exp(contract_cols(query_unit_all, doc_unit_f.astype(jnp.bfloat16)) / POOL_TEMP)
        spread = contract_cols(coef_all[:, level_index], own_hot, FULL_PRECISION)
        grad_sim = (expo * spread).astype(jnp.bfloat16)
        grad_doc = contract_rows(grad_sim, query_unit_all)
        grad_embed = grad_embed + normalize_back(grad_doc, doc_part, doc_scale, proj_width)
    row_query_grads = lax.dynamic_slice_in_dim(
        grad_query_all, data_index * query_span, query_span, 0
    )
    padded = jnp.pad(row_query_grads, ((0, token_count - query_span), (0, 0)))
    grad_embed = grad_embed + lax.dynamic_slice_in_dim(padded, own_start, share_rows, 0)
    proj_float = w_proj.astype(jnp.float32)
    grad_result = cot.astype(jnp.float32) + contract_cols(grad_embed, proj_float, FULL_PRECISION)
    proj_grad = contract_rows(result_low.astype(jnp.float32), grad_embed, FULL_PRECISION)
    gain_two = jnp.sum(grad_result * unit_two, axis=0)
    shift_two = jnp.sum(grad_result, axis=0)
    grad_second = norm_backward(grad_result, unit_two, rstd_two, gains[1])
    grad_ffn = grad_second.astype(jnp.bfloat16)
    down_bias = jnp.sum(grad_ffn.astype(jnp.float32), axis=0)
    grad_ffn_all = lax.all_gather(grad_ffn, "tensor", axis=0, tiled=True)
    grad_act = contract_cols(grad_ffn_all, full_down)
    down_grad = contract_rows(activation, grad_ffn_all)
    _, gelu_pull = jax.vjp(partial(jax.nn.gelu, approximate=False), up_value)
    grad_up = gelu_pull(grad_act)[0].astype(jnp.bfloat16)
    up_bias = jnp.sum(grad_up.astype(jnp.float32), axis=0)
    up_grad = contract_rows(normed_all, grad_up)
    normed_terms = contract_cols(grad_up, full_up)
    grad_normed = (
        lax.psum_scatter(
            normed_terms.astype(jnp.bfloat16), "tensor", scatter_dimension=0, tiled=True
        ).astype(jnp.float32)
        + grad_second
    )
    gain_one = jnp.sum(grad_normed * unit_one, axis=0)
    shift_one = jnp.sum(grad_normed, axis=0)
    grad_first = norm_backward(grad_normed, unit_one, rstd_one, gains[0])
    grad_attn = grad_first.astype(jnp.bfloat16)
    out_bias = jnp.sum(grad_attn.astype(jnp.float32), axis=0)
    grad_attn_all = lax.all_gather(grad_attn, "tensor", axis=0, tiled=True)
    out_grad = contract_rows(mixed, grad_attn_all)
    grad_mixed = contract_cols(grad_attn_all, full_out).astype(jnp.bfloat16)
    grad_q, grad_k, grad_v = attend_backward(
        query_rows, key_rows, value_rows, segments, log_totals, grad_mixed, block_rows
    )
    stacked_grads = jnp.stack(
        [grad_q.astype(jnp.bfloat16), grad_k.astype(jnp.bfloat16), grad_v.astype(jnp.bfloat16)]
    )
    qkv_grad = jnp.einsum("td,ktw->kdw", tokens, stacked_grads, preferred_element_type=jnp.float32)
    input_terms = jnp.einsum(
        "ktw,kdw->td", stacked_grads, full_qkv, preferred_element_type=jnp.float32
    )
    grad_input = (
        lax.psum_scatter(
            input_terms.astype(jnp.bfloat16), "tensor", scatter_dimension=0, tiled=True
        ).astype(jnp.float32)
        + grad_first
    )
    qv_grad = jnp.stack(
        [
            jnp.sum(stacked_grads[0].astype(jnp.float32), axis=0),
            jnp.sum(stacked_grads[2].astype(jnp.float32), axis=0),
        ]
    )
    qkv_part, out_part, up_part, down_part = (
        lax.psum_scatter(
            qkv_grad.astype(jnp.bfloat16), "dp", scatter_dimension=1, tiled=True
        ).astype(jnp.float32),
        lax.psum_scatter(
            out_grad.astype(jnp.bfloat16), "dp", scatter_dimension=1, tiled=True
        ).astype(jnp.float32),
        lax.psum_scatter(
            up_grad.astype(jnp.bfloat16), "dp", scatter_dimension=0, tiled=True
        ).astype(jnp.float32),
        lax.psum_scatter(
            down_grad.astype(jnp.bfloat16), "dp", scatter_dimension=1, tiled=True
        ).astype(jnp.float32),
    )
    gain_sum, shift_sum, out_bias_sum, down_bias_sum, proj_sum = lax.psum(
        (
            jnp.stack([gain_one, gain_two]),
            jnp.stack([shift_one, shift_two]),
            out_bias,
            down_bias,
            proj_grad,
        ),
        ("dp", "tensor"),
    )
    qv_sum, up_bias_sum = lax.psum((qv_grad, up_bias), "dp")
    return (
        result_low,
        loss_out,
        grad_input.astype(jnp.bfloat16),
        qkv_part,
        qv_sum,
        out_part,
        out_bias_sum,
        gain_sum,
        shift_sum,
        up_part,
        up_bias_sum,
        down_part,
        down_bias_sum,
        proj_sum,
    )


SWAP = [(0, 1), (1, 0)]
TURN = [(0, 0), (1, 2), (2, 1), (3, 3)]
RING_UP = [(0, 1), (1, 2), (2, 3), (3, 0)]
RING_DOWN = [(1, 0), (2, 1), (3, 2), (0, 3)]
BF = jnp.bfloat16
F32 = jnp.float32


def dot(left, right):
    return jnp.dot(left, right, preferred_element_type=F32)


def turn(value):
    return lax.ppermute(value, ("c", "y"), TURN)


def swap(value, axis):
    return lax.ppermute(value, axis, SWAP)


def up(value):
    return lax.ppermute(value, "z", RING_UP)


def down(value):
    return lax.ppermute(value, "z", RING_DOWN)


def pair_up(first, second, own_index, axis):
    return jnp.where(
        own_index == 0, jnp.stack([first, second], axis), jnp.stack([second, first], axis)
    )


def gather_z(value, z):
    below, above = up(value), down(value)
    half = value.shape[-2] // 2
    far_low = up(below[..., :half, :])
    far_high = down(above[..., half:, :])
    far = jnp.concatenate([far_low, far_high], axis=-2)
    whole = jnp.zeros((4,) + value.shape, value.dtype)
    for offset, part in ((0, value), (3, below), (1, above), (2, far)):
        whole = lax.dynamic_update_index_in_dim(whole, part, (z + offset) % 4, 0)
    return whole


def gather_c(value, c, y, axis):
    got = lax.ppermute(value, ("c", "y"), [(2, 0), (1, 3), (0, 1), (3, 2)])
    cross = lax.ppermute(value, ("c", "y"), [(2, 1), (1, 2)])
    first = jnp.where(c == y, value, got)
    second = jnp.where(c == y, got, cross)
    return pair_up(first, second, c, axis)


def gather_x(value, x, axis):
    return pair_up(value, swap(value, "x"), x, axis)


def flat(value):
    return value.reshape(-1, value.shape[-1])


def tie(value, *others):
    return lax.optimization_barrier((value,) + others)[0]


def sum_c(blocks, c, y):
    axis = blocks.ndim - 3
    mine = lax.dynamic_index_in_dim(blocks, c, axis, keepdims=False)
    other = lax.dynamic_index_in_dim(blocks, 1 - c, axis, keepdims=False)
    other_low = other.astype(BF)
    got = lax.ppermute(
        jnp.where(c == y, other_low, mine.astype(BF)),
        ("c", "y"),
        [(0, 2), (3, 1), (1, 0), (2, 3)],
    )
    cross = lax.ppermute(other_low, ("c", "y"), [(1, 2), (2, 1)])
    return got.astype(F32) + jnp.where(c == y, mine, cross.astype(F32))


def sum_x(blocks, x, axis):
    theirs = lax.dynamic_index_in_dim(blocks, 1 - x, axis, keepdims=False)
    mine = lax.dynamic_index_in_dim(blocks, x, axis, keepdims=False)
    return mine.astype(F32) + swap(theirs.astype(BF), "x").astype(F32)


def sum_ring(block_of, z):
    far = block_of((z + 2) % 4).astype(BF)
    half = far.shape[0] // 2
    from_below = up(far[:half])
    from_above = down(far[half:])
    pad = ((0, half),) + ((0, 0),) * (far.ndim - 1)
    pad_high = ((half, 0),) + ((0, 0),) * (far.ndim - 1)
    after = block_of((z + 1) % 4) + jnp.pad(from_below, pad).astype(F32)
    before = block_of((z + 3) % 4) + jnp.pad(from_above, pad_high).astype(F32)
    got_up = up(after.astype(BF))
    got_down = down(before.astype(BF))
    return block_of(z) + got_up.astype(F32) + got_down.astype(F32)


def weight_sum_z(left, right, z, x, c, y):
    def block_of(place):
        return contract_rows(lax.dynamic_slice_in_dim(left, place * 256, 256, 1), right)

    own = sum_ring(block_of, z).reshape(2, 2, 64, right.shape[1])
    return sum_c(sum_x(own, x, 0), c, y)


def sum_other(value, step):
    if step == "0":
        return lax.ppermute(value, "z", [(0, 1), (1, 0), (2, 3), (3, 2)])
    if step == "1":
        return lax.ppermute(value, "z", [(0, 3), (3, 0), (1, 2), (2, 1)])
    return swap(value, step)


def sum_chips(value, steps):
    for step in steps:
        value = value + sum_other(value, step)
    return value


def tile_bounds(row_lengths, token_count):
    ends = jnp.cumsum(row_lengths)
    span = NQ_ROW * QLEN
    first = jnp.arange(token_count // TILE, dtype=jnp.int32) * TILE - span
    last = first + TILE - 1
    begin = jnp.max(jnp.where(ends[None, :] <= first[:, None], ends[None, :], 0), axis=1)
    end = jnp.min(jnp.where(ends[None, :] > last[:, None], ends[None, :], token_count), axis=1)
    low = jnp.where(first < 0, 0, (begin + span) // TILE)
    high = jnp.where(first < 0, 1, (end + span + TILE - 1) // TILE)
    return jnp.stack([low, high]).astype(jnp.int32)


def rows_of(value, start, count):
    return lax.dynamic_slice_in_dim(value, start, count, 0)


TILE = 256
NEG = -1e30


def exact(left, right, dims):
    return lax.dot_general(left, right, (dims, ((), ())), preferred_element_type=F32)


def head_masks(value):
    lane = lax.broadcasted_iota(jnp.int32, value.shape, 1)
    zero = jnp.zeros_like(value)
    return (jnp.where(lane < HEAD_DIM, value, zero), jnp.where(lane < HEAD_DIM, zero, value))


def fill_bias(seg_col, seg_row, bias):
    for start in range(0, bias.shape[0], TILE):
        rows = slice(start, start + TILE)
        bias[rows, :] = jnp.where(seg_col[rows, :] == seg_row[...], 0.0, NEG)


def attend_kernel(bounds, q_ref, k_ref, v_ref, seg_col, seg_row, out_ref, lse_ref, bias, held):
    @pl.when(pl.program_id(0) == 0)
    def _():
        fill_bias(seg_col, seg_row, bias)

    for block in range(q_ref.shape[0] // TILE):
        own = slice(block * TILE, (block + 1) * TILE)
        queries = head_masks(q_ref[own, :] * HEAD_DIM**-0.5)

        def score(step, highest):
            rows = pl.ds(pl.multiple_of(step * TILE, TILE), TILE)
            keys, shift = k_ref[rows, :], bias[rows, own]
            fresh = []
            for head in range(2):
                scores = exact(keys, queries[head], ((1,), (1,))) + shift
                held[head, rows, :] = scores
                fresh.append(jnp.maximum(highest[head], jnp.max(scores, axis=0, keepdims=True)))
            return tuple(fresh)

        low = jnp.full((1, TILE), NEG, F32)
        highest = lax.fori_loop(bounds[0, block], bounds[1, block], score, (low, low))

        def mix(step, carried):
            rows = pl.ds(pl.multiple_of(step * TILE, TILE), TILE)
            values = v_ref[rows, :]
            fresh = []
            for head in range(2):
                total, mixed = carried[head]
                expo = jnp.exp(held[head, rows, :] - highest[head])
                fresh.append(
                    (
                        total + jnp.sum(expo, axis=0, keepdims=True),
                        mixed + exact(values, expo.astype(BF), ((0,), (0,))),
                    )
                )
            return tuple(fresh)

        start = (jnp.zeros((1, TILE), F32), jnp.zeros((2 * HEAD_DIM, TILE), F32))
        parts = lax.fori_loop(bounds[0, block], bounds[1, block], mix, (start, start))
        mixed = jnp.concatenate(
            [parts[0][1][:HEAD_DIM] / parts[0][0], parts[1][1][HEAD_DIM:] / parts[1][0]], axis=0
        )
        out_ref[own, :] = jnp.transpose(mixed).astype(BF)
        for head in range(2):
            lse_ref[0, head : head + 1, own] = highest[head] + jnp.log(parts[head][0])


def attend(bounds, qkv, seg_col, seg_row):
    count, wide = qkv.shape
    pairs = wide // 3 // 128
    column = lambda shift: pl.BlockSpec((count, 128), lambda i: (0, shift + i))
    whole = lambda shape: pl.BlockSpec(shape, lambda i: (0, 0))
    return pl.pallas_call(
        attend_kernel,
        grid=(pairs,),
        in_specs=[
            pl.BlockSpec(memory_space=pltpu.SMEM),
            column(0),
            column(pairs),
            column(2 * pairs),
            whole((count, 1)),
            whole((1, count)),
        ],
        out_specs=[column(0), pl.BlockSpec((1, 8, count), lambda i: (i, 0, 0))],
        out_shape=[
            jax.ShapeDtypeStruct((count, wide // 3), BF),
            jax.ShapeDtypeStruct((pairs, 8, count), F32),
        ],
        scratch_shapes=[pltpu.VMEM((count, count), F32), pltpu.VMEM((2, count, TILE), F32)],
        compiler_params=pltpu.CompilerParams(vmem_limit_bytes=40 << 20),
        cost_estimate=pl.CostEstimate(
            flops=4 * pairs * count * count * 128,
            transcendentals=pairs * count * count,
            bytes_accessed=4 * count * wide * 2,
        ),
    )(bounds, qkv, qkv, qkv, seg_col, seg_row)


def attend_back_kernel(
    bounds, q_ref, k_ref, v_ref, out_ref, grad_ref, lse_ref, seg_col, seg_row,
    grads_ref, sums_ref, bias, key_sum, value_sum,
):
    pair = pl.program_id(0)

    @pl.when(pair == 0)
    def _():
        fill_bias(seg_col, seg_row, bias)

    key_sum[...] = jnp.zeros_like(key_sum)
    value_sum[...] = jnp.zeros_like(value_sum)
    columns = [
        pl.ds(pl.multiple_of(part * (grads_ref.shape[1] // 3) + pair * 128, 128), 128) for part in range(3)
    ]
    query_total = jnp.zeros((1, 128), F32)
    picks = head_masks(jnp.ones((8, 128), BF))
    for block in range(q_ref.shape[0] // TILE):
        own = slice(block * TILE, (block + 1) * TILE)
        queries = head_masks(q_ref[own, :] * HEAD_DIM**-0.5)
        grads = head_masks(grad_ref[own, :])
        product = grad_ref[own, :].astype(F32) * out_ref[own, :].astype(F32)
        product_high = product.astype(BF)
        product_low = (product - product_high.astype(F32)).astype(BF)
        inner = [
            (
                exact(picks[head], product_high, ((1,), (1,)))
                + exact(picks[head], product_low, ((1,), (1,)))
            )[0:1]
            for head in range(2)
        ]
        lse = [lse_ref[0, head : head + 1, own] for head in range(2)]

        def step_of(step, carried):
            rows = pl.ds(pl.multiple_of(step * TILE, TILE), TILE)
            keys, values, shift = k_ref[rows, :], v_ref[rows, :], bias[rows, own]
            fresh = []
            key_add = jnp.zeros((TILE, 128), F32)
            value_add = jnp.zeros((TILE, 128), F32)
            for head in range(2):
                scores = exact(keys, queries[head], ((1,), (1,))) + shift
                probs = jnp.exp(scores - lse[head])
                grad_probs = exact(values, grads[head], ((1,), (1,)))
                grad_scores = (probs * (grad_probs - inner[head])).astype(BF)
                value_add = value_add + exact(probs.astype(BF), grads[head], ((1,), (0,)))
                key_add = key_add + exact(grad_scores, queries[head], ((1,), (0,)))
                fresh.append(carried[head] + exact(keys, grad_scores, ((0,), (0,))))
            key_sum[rows, :] += key_add
            value_sum[rows, :] += value_add
            return tuple(fresh)

        start = jnp.zeros((2 * HEAD_DIM, TILE), F32)
        parts = lax.fori_loop(bounds[0, block], bounds[1, block], step_of, (start, start))
        grad_query = jnp.concatenate([parts[0][:HEAD_DIM], parts[1][HEAD_DIM:]], axis=0)
        grad_query = jnp.transpose(grad_query * HEAD_DIM**-0.5).astype(BF)
        grads_ref[own, columns[0]] = grad_query
        query_total = query_total + jnp.sum(grad_query.astype(F32), axis=0, keepdims=True)
    grad_value = value_sum[...].astype(BF)
    grads_ref[:, columns[1]] = key_sum[...].astype(BF)
    grads_ref[:, columns[2]] = grad_value
    sums_ref[0, 0:1, :] = query_total
    sums_ref[0, 1:2, :] = jnp.sum(grad_value.astype(F32), axis=0, keepdims=True)


def attend_back(bounds, qkv, mixed, grad_mixed, lse, seg_col, seg_row):
    count, wide = qkv.shape
    pairs = wide // 3 // 128
    column = lambda shift: pl.BlockSpec((count, 128), lambda i: (0, shift + i))
    whole = lambda shape: pl.BlockSpec(shape, lambda i: (0, 0))
    return pl.pallas_call(
        attend_back_kernel,
        grid=(pairs,),
        in_specs=[
            pl.BlockSpec(memory_space=pltpu.SMEM),
            column(0),
            column(pairs),
            column(2 * pairs),
            column(0),
            column(0),
            pl.BlockSpec((1, 8, count), lambda i: (i, 0, 0)),
            whole((count, 1)),
            whole((1, count)),
        ],
        out_specs=[whole((count, wide)), pl.BlockSpec((1, 8, 128), lambda i: (i, 0, 0))],
        out_shape=[
            jax.ShapeDtypeStruct((count, wide), BF),
            jax.ShapeDtypeStruct((pairs, 8, 128), F32),
        ],
        scratch_shapes=[
            pltpu.VMEM((count, count), F32),
            pltpu.VMEM((count, 128), F32),
            pltpu.VMEM((count, 128), F32),
        ],
        compiler_params=pltpu.CompilerParams(vmem_limit_bytes=40 << 20),
        cost_estimate=pl.CostEstimate(
            flops=10 * pairs * count * count * 128,
            transcendentals=pairs * count * count,
            bytes_accessed=8 * count * wide * 2,
        ),
    )(bounds, qkv, qkv, qkv, mixed, grad_mixed, lse, seg_col, seg_row)


ERFC = (
    -1.26551223, 1.00002368, 0.37409196, 0.09678418, -0.18628806,
    0.27886807, -1.13520398, 1.48851587, -0.82215223, 0.17087277,
)


def gelu_pair(value):
    size = jnp.abs(value) * 0.5**0.5
    ratio = 1.0 / (1.0 + 0.5 * size)
    series = jnp.full_like(value, ERFC[-1])
    for factor in ERFC[-2::-1]:
        series = series * ratio + factor
    bell = jnp.exp(-size * size)
    tail = 0.5 * ratio * bell * jnp.exp(series)
    phi = jnp.where(value < 0.0, tail, 1.0 - tail)
    return (value * phi, phi + value * bell * 0.3989422804014327)


def expand_kernel(left_tiles, x_ref, left_ref, right_ref, b_ref, act_ref, slope_ref):
    def fill(w_ref):
        rows = 256
        for start in range(0, x_ref.shape[0], rows):
            part = slice(start, start + rows)
            value = exact(x_ref[part, :], w_ref[...], ((1,), (0,))) + b_ref[...]
            active, slope = gelu_pair(value)
            act_ref[part, :] = active.astype(BF)
            slope_ref[part, :] = slope.astype(BF)

    pl.when(pl.program_id(0) < left_tiles)(lambda: fill(left_ref))
    pl.when(pl.program_id(0) >= left_tiles)(lambda: fill(right_ref))


def expand(value, left, right, shift):
    count, depth = value.shape
    width = shift.shape[1]
    tile = 256
    left_tiles = left.shape[1] // tile
    return pl.pallas_call(
        partial(expand_kernel, left_tiles),
        grid=(width // tile,),
        in_specs=[
            pl.BlockSpec((count, depth), lambda i: (0, 0)),
            pl.BlockSpec((depth, tile), lambda i: (0, jnp.minimum(i, left_tiles - 1))),
            pl.BlockSpec((depth, tile), lambda i: (0, jnp.maximum(i - left_tiles, 0))),
            pl.BlockSpec((1, tile), lambda i: (0, i)),
        ],
        out_specs=[pl.BlockSpec((count, tile), lambda i: (0, i))] * 2,
        out_shape=[jax.ShapeDtypeStruct((count, width), BF)] * 2,
        compiler_params=pltpu.CompilerParams(vmem_limit_bytes=32 << 20),
        cost_estimate=pl.CostEstimate(
            flops=2 * count * depth * width,
            transcendentals=3 * count * width,
            bytes_accessed=2 * (count * depth + depth * width + 2 * count * width),
        ),
    )(value, left, right, shift)


def cut_levels(raw, cuts):
    lane = lax.broadcasted_iota(jnp.int32, raw.shape, 1)
    levels = []
    for cut in cuts:
        part = jnp.where(lane < cut, raw, 0.0)
        scale = lax.rsqrt(jnp.sum(part * part, axis=1, keepdims=True) + EPS_EMBED)
        levels.append(((part * scale).astype(BF), part, scale))
    return levels


def pool_kernel(cuts, span, q_ref, d_ref, seg_ref, out_ref, units, hot):
    @pl.when(pl.program_id(0) == 0)
    def _():
        raw = d_ref[span:, :].astype(F32)
        for level, parts in enumerate(cut_levels(raw, cuts)):
            units[level] = parts[0]
        doc = lax.broadcasted_iota(jnp.int32, hot.shape, 0)
        hot[...] = (seg_ref[:, span:] == NQ_ROW + doc).astype(F32).astype(BF)

    levels = cut_levels(q_ref[...].astype(F32), cuts)
    for level in range(len(cuts)):
        similar = exact(units[level], levels[level][0], ((1,), (1,)))
        expo = jnp.exp(similar * (1.0 / POOL_TEMP))
        high = expo.astype(BF)
        rest = (expo - high.astype(F32)).astype(BF)
        out_ref[level * NDOC : (level + 1) * NDOC, :] = exact(
            hot[...], high, ((1,), (0,))
        ) + exact(hot[...], rest, ((1,), (0,)))


def pool(cuts, span, queries, row_embed, seg_row):
    count, width = queries.shape
    tokens = row_embed.shape[0]
    whole = lambda shape: pl.BlockSpec(shape, lambda i: (0, 0))
    return pl.pallas_call(
        partial(pool_kernel, cuts, span),
        grid=(count // TILE,),
        in_specs=[
            pl.BlockSpec((TILE, width), lambda i: (i, 0)),
            whole((tokens, width)),
            whole((1, tokens)),
        ],
        out_specs=pl.BlockSpec((len(cuts) * NDOC, TILE), lambda i: (0, i)),
        out_shape=jax.ShapeDtypeStruct((len(cuts) * NDOC, count), F32),
        scratch_shapes=[
            pltpu.VMEM((len(cuts), tokens - span, width), BF),
            pltpu.VMEM((NDOC, tokens - span), BF),
        ],
        compiler_params=pltpu.CompilerParams(vmem_limit_bytes=32 << 20),
        cost_estimate=pl.CostEstimate(
            flops=2 * len(cuts) * count * tokens * 256,
            transcendentals=len(cuts) * count * tokens,
            bytes_accessed=2 * (count + tokens) * width,
        ),
    )(queries, row_embed, seg_row)


def level_back(grad, part, scale):
    return scale * grad - part * (scale * scale * scale) * jnp.sum(
        part * grad, axis=1, keepdims=True
    )


def pool_back_kernel(
    cuts, span, q_ref, d_ref, seg_ref, coef_ref, q_out, d_out, units, units_t, hot, sums
):
    step = pl.program_id(0)

    @pl.when(step == 0)
    def _():
        raw = d_ref[span:, :].astype(F32)
        for level, parts in enumerate(cut_levels(raw, cuts)):
            units[level] = parts[0]
            units_t[level] = jnp.transpose(parts[0])
        doc = lax.broadcasted_iota(jnp.int32, hot.shape, 0)
        wanted = NQ_ROW + jnp.where(doc < NDOC, doc, doc - NDOC)
        hot[...] = (seg_ref[:, span:] == wanted).astype(F32).astype(BF)
        sums[...] = jnp.zeros_like(sums)

    levels = cut_levels(q_ref[...].astype(F32), cuts)
    total = jnp.zeros(q_ref.shape, F32)
    for level in range(len(cuts)):
        unit, part, scale = levels[level]
        similar = exact(units[level], unit, ((1,), (1,)))
        coef = coef_ref[level * NDOC : (level + 1) * NDOC, :]
        high = coef.astype(BF).astype(F32)
        both = jnp.concatenate([high, coef - high], axis=0).astype(BF)
        spread = exact(hot[...], both, ((0,), (0,)))
        grad = (jnp.exp(similar * (1.0 / POOL_TEMP)) * spread).astype(BF)
        sums[level] += exact(grad, unit, ((1,), (0,)))
        grad_unit = jnp.transpose(exact(units_t[level], grad, ((1,), (0,))))
        total = total + level_back(grad_unit, part, scale)
    q_out[...] = total.astype(BF)

    @pl.when(step == pl.num_programs(0) - 1)
    def _():
        raw = d_ref[span:, :].astype(F32)
        result = jnp.zeros(raw.shape, F32)
        for level, parts in enumerate(cut_levels(raw, cuts)):
            lane = lax.broadcasted_iota(jnp.int32, raw.shape, 1)
            grad = jnp.where(lane < cuts[level], sums[level], 0.0)
            result = result + level_back(grad, parts[1], parts[2])
        d_out[...] = result


def pool_back(cuts, span, queries, row_embed, seg_row, coef):
    count, width = queries.shape
    tokens = row_embed.shape[0]
    docs = tokens - span
    whole = lambda shape: pl.BlockSpec(shape, lambda i: (0, 0))
    return pl.pallas_call(
        partial(pool_back_kernel, cuts, span),
        grid=(count // TILE,),
        in_specs=[
            pl.BlockSpec((TILE, width), lambda i: (i, 0)),
            whole((tokens, width)),
            whole((1, tokens)),
            pl.BlockSpec((len(cuts) * NDOC, TILE), lambda i: (0, i)),
        ],
        out_specs=[pl.BlockSpec((TILE, width), lambda i: (i, 0)), whole((docs, width))],
        out_shape=[
            jax.ShapeDtypeStruct((count, width), BF),
            jax.ShapeDtypeStruct((docs, width), F32),
        ],
        scratch_shapes=[
            pltpu.VMEM((len(cuts), docs, width), BF),
            pltpu.VMEM((len(cuts), width, docs), BF),
            pltpu.VMEM((2 * NDOC, docs), BF),
            pltpu.VMEM((len(cuts), docs, width), F32),
        ],
        compiler_params=pltpu.CompilerParams(vmem_limit_bytes=32 << 20),
        cost_estimate=pl.CostEstimate(
            flops=2 * len(cuts) * count * docs * 512,
            transcendentals=len(cuts) * count * docs,
            bytes_accessed=4 * (count + tokens) * width,
        ),
    )(queries, row_embed, seg_row, coef)


def local_chip(
    tokens,
    lengths,
    pairing,
    w_qkv,
    b_qv,
    w_out,
    b_out,
    ln_gain,
    ln_bias,
    w_up,
    b_up,
    w_down,
    b_down,
    w_proj,
    cot,
):
    z, x, c, y = (lax.axis_index(name) for name in ("z", "x", "c", "y"))
    chip = 4 * z + 2 * x + y
    token_count, width = tokens.shape
    share = token_count // 2
    own_start, other_start = c * share, (1 - c) * share
    gains, shifts = ln_gain.astype(F32), ln_bias.astype(F32)

    half_width = w_qkv.shape[2]
    up_wide = w_up.shape[1]
    left_wide = (up_wide + half_width) // 2
    qkv_rows = jnp.concatenate([w_qkv[0], w_qkv[1], w_qkv[2]], axis=1)
    mid_rows = jnp.concatenate([w_up, w_out.T], axis=1)
    qkv_rows = gather_c(qkv_rows, c, y, 0)
    mid_rows = gather_z(mid_rows, z)
    down_rows = gather_c(w_down.T, c, y, 0)
    qkv_rows = gather_x(qkv_rows, x, 0)
    down_rows = gather_x(down_rows, x, 0)
    mid_left = gather_x(mid_rows[..., :left_wide], x, 1)
    mid_right = gather_c(mid_rows[..., left_wide:], c, y, 1)
    full_qkv = flat(gather_z(qkv_rows, z))
    mid_left = flat(gather_c(mid_left, c, y, 2))
    mid_right = flat(gather_x(mid_right, x, 1))
    full_out = mid_right[:, up_wide - left_wide :]
    full_down = flat(gather_z(down_rows, z))
    row = jnp.where(c == y, tokens, swap(tokens, "c"))
    bias = jnp.concatenate([b_qv.reshape(-1), b_up])[None].astype(F32)
    bias = jnp.where(c == y, bias, swap(bias, "y"))
    own_cot = turn(cot)
    half_queries = NQ_ROW // 2
    chip_count = lengths.shape[0]
    query_total = chip_count * half_queries
    pairs = lax.dynamic_update_slice_in_dim(
        jnp.zeros((1, 2 * query_total), F32),
        pairing.astype(F32),
        ((4 * z + 2 * x + c) * 2 + y) * half_queries,
        1,
    )
    pairs = sum_chips(pairs, "cxy01").reshape(chip_count, 2, half_queries)
    pairs = lax.dynamic_index_in_dim(pairs, c, 1, keepdims=False).reshape(1, query_total)
    pairs = pairs.astype(jnp.int32)

    row_lengths = lax.dynamic_index_in_dim(lengths, chip, 0, keepdims=False)
    segments = segments_of(row_lengths, token_count)
    seg_col, seg_row = segments[:, None], segments[None, :]
    query_span = NQ_ROW * QLEN
    bounds = tile_bounds(row_lengths, token_count)
    qkv_bias = jnp.concatenate(
        [bias[:, :half_width], jnp.zeros_like(bias[:, :half_width]), bias[:, half_width : 2 * half_width]],
        axis=1,
    )
    qkv = (dot(row, full_qkv) + qkv_bias).astype(BF)
    mixed, lse = attend(bounds, qkv, seg_col, seg_row)
    mixed, own_cot, pairs = lax.optimization_barrier((mixed, own_cot, pairs))

    def row_sum(left, weight_t, transposed):
        times = contract_cols if transposed else dot
        theirs = swap(times(left(1), weight_t).astype(BF), "c")
        return times(left(0), weight_t) + theirs.astype(F32)

    def mixed_half(which):
        return rows_of(mixed, other_start if which else own_start, share)

    attn_sum = row_sum(mixed_half, full_out, True)
    own_tokens = rows_of(row, own_start, share).astype(F32)
    normed, unit_one, rstd_one = norm_forward(
        own_tokens + attn_sum + b_out.astype(F32), gains[0], shifts[0]
    )
    normed_low = normed.astype(BF)
    normed_all = jnp.concatenate([normed_low, swap(normed_low, "c")], axis=0)
    activation, slope = expand(normed_all, mid_left, mid_right, bias[:, 2 * half_width :])
    ffn_sum = row_sum(
        lambda which: activation[which * share : (which + 1) * share], full_down, True
    )
    result, unit_two, rstd_two = norm_forward(
        normed + ffn_sum + b_down.astype(F32), gains[1], shifts[1]
    )
    result_low = result.astype(BF)
    y_out = turn(result_low)
    embed = dot(result_low, w_proj).astype(BF)

    other_embed = swap(embed, "c")
    row_embed = jnp.where(
        c == 0,
        jnp.concatenate([embed, other_embed], axis=0),
        jnp.concatenate([other_embed, embed], axis=0),
    )
    half_span = query_span // 2
    own_queries = rows_of(row_embed, c * half_span, half_span)
    chips = ("z", "x", "y")
    queries = lax.all_to_all(
        jnp.broadcast_to(own_queries[None], (chip_count,) + own_queries.shape), chips, 0, 0
    ).reshape(chip_count * half_span, -1)
    proj_width = w_proj.shape[1]
    cuts = (proj_width, 3 * proj_width // 4, proj_width // 2)
    sums = pool(cuts, query_span, queries, row_embed, seg_row)
    doc_sizes = jnp.tile(row_lengths.astype(F32), 3)[:, None]
    group = (
        jnp.arange(query_total * QLEN, dtype=jnp.int32)[:, None] // QLEN
        == jnp.arange(query_total, dtype=jnp.int32)[None, :]
    ).astype(F32)
    pooled = POOL_TEMP * jnp.log(sums / doc_sizes)
    logits = jnp.dot(pooled, group, precision=FULL_PRECISION) / LOSS_TEMP
    logits = logits.reshape(3, NDOC, query_total)
    doc_numbers = chip * NDOC + jnp.arange(NDOC, dtype=jnp.int32)
    picked = (doc_numbers[:, None] == pairs).astype(F32)
    own_high = jnp.max(logits, axis=1)
    own_lse = own_high + jnp.log(jnp.sum(jnp.exp(logits - own_high[:, None]), axis=1))
    own_target = jnp.sum(logits * picked, axis=1)
    notes = jnp.pad(jnp.concatenate([own_lse, own_target], axis=1), ((0, 5), (0, 0)))
    notes = lax.all_to_all(
        jnp.broadcast_to(notes[None], (chip_count,) + notes.shape), chips, 0, 0
    )
    chip_lse = notes[:, :3, :query_total]
    high = jnp.max(chip_lse, axis=0)
    all_lse = high + jnp.log(jnp.sum(jnp.exp(chip_lse - high), axis=0))
    target = jnp.sum(notes[:, :3, query_total:], axis=0)
    losses = jnp.sum(all_lse - target, axis=0).reshape(chip_count, half_queries)
    grad_logits = (jnp.exp(logits - all_lse[:, None]) - picked) / LOSS_TEMP
    coefficient = (
        lax.dot_general(
            grad_logits.reshape(3 * NDOC, query_total),
            group,
            (((1,), (1,)), ((), ())),
            precision=FULL_PRECISION,
        )
        / sums
    )
    losses = jnp.where(c == y, losses, swap(losses, "c"))
    loss_out = rows_of(losses, 4 * z + 2 * x + c, 1)
    query_grad, doc_grad = pool_back(cuts, query_span, queries, row_embed, seg_row, coefficient)
    grad_blocks = lax.all_to_all(
        query_grad.reshape(chip_count, half_span, proj_width), chips, 0, 0
    )
    own_query_grad = jnp.sum(grad_blocks.astype(F32), axis=0)
    row_grad = jnp.concatenate([jnp.zeros((query_span, proj_width), F32), doc_grad], axis=0)
    row_grad = lax.dynamic_update_slice_in_dim(row_grad, own_query_grad, c * half_span, 0)
    grad_embed = rows_of(row_grad, own_start, share) + swap(
        rows_of(row_grad, other_start, share), "c"
    )

    proj_low = w_proj
    grad_embed_low = grad_embed.astype(BF)
    grad_embed_rest = (grad_embed - grad_embed_low.astype(F32)).astype(BF)
    grad_result = own_cot.astype(F32) + (
        contract_cols(grad_embed_low, proj_low) + contract_cols(grad_embed_rest, proj_low)
    )
    proj_grad = contract_rows(result_low, grad_embed_low) + contract_rows(
        result_low, grad_embed_rest
    )
    gain_two = jnp.sum(grad_result * unit_two, axis=0)
    shift_two = jnp.sum(grad_result, axis=0)
    grad_second = norm_backward(grad_result, unit_two, rstd_two, gains[1])
    grad_ffn = grad_second.astype(BF)
    down_bias = jnp.sum(grad_ffn.astype(F32), axis=0)
    grad_ffn_all = jnp.concatenate([grad_ffn, swap(grad_ffn, "c")], axis=0)
    down_part = weight_sum_z(grad_ffn_all, activation, z, x, c, y)
    grad_up = (dot(grad_ffn_all, full_down) * slope.astype(F32)).astype(BF)
    up_bias = jnp.sum(grad_up.astype(F32), axis=0)
    up_part = weight_sum_z(normed_all, grad_up, z, x, c, y)
    def normed_terms(which):
        part = grad_up[which * share : (which + 1) * share]
        return contract_cols(part[:, :left_wide], mid_left) + contract_cols(
            part[:, left_wide:], mid_right[:, : up_wide - left_wide]
        )

    other_terms = swap(normed_terms(1).astype(BF), "c")
    grad_normed = normed_terms(0) + other_terms.astype(F32) + grad_second
    gain_one = jnp.sum(grad_normed * unit_one, axis=0)
    shift_one = jnp.sum(grad_normed, axis=0)
    grad_first = norm_backward(grad_normed, unit_one, rstd_one, gains[0])
    grad_attn = grad_first.astype(BF)
    out_bias = jnp.sum(grad_attn.astype(F32), axis=0)
    other_attn = swap(grad_attn, "c")
    grad_attn_all = jnp.where(
        c == 0,
        jnp.concatenate([grad_attn, other_attn], axis=0),
        jnp.concatenate([other_attn, grad_attn], axis=0),
    )
    out_part = weight_sum_z(grad_attn_all, mixed, z, x, c, y)
    grad_mixed = dot(grad_attn_all, full_out).astype(BF)
    grads, grad_sums = attend_back(bounds, qkv, mixed, grad_mixed, lse, seg_col, seg_row)
    qkv_part = weight_sum_z(row, grads, z, x, c, y)
    grad_input = turn(
        (
            row_sum(
                lambda which: rows_of(grads, other_start if which else own_start, share),
                full_qkv,
                True,
            )
            + grad_first
        ).astype(BF)
    )

    shared = jnp.stack([gain_one, gain_two, shift_one, shift_two, out_bias, down_bias])
    half_sums = jnp.concatenate(
        [grad_sums[:, 0].reshape(-1), grad_sums[:, 1].reshape(-1), up_bias]
    )
    small = jnp.concatenate([shared.reshape(-1), half_sums]).reshape(-1, 128)
    small = sum_chips(small, "xy01")
    other_small = swap(small, "c")
    shared_rows = 6 * width // 128
    shared = (small[:shared_rows] + other_small[:shared_rows]).reshape(6, width)
    half_sums = jnp.where(c == y, small[shared_rows:], other_small[shared_rows:]).reshape(-1)
    proj_half = rows_of(proj_grad, own_start, share) + swap(
        rows_of(proj_grad, other_start, share), "c"
    )
    for step in ("x", "y", "0", "1"):
        proj_half = proj_half + sum_other(proj_half.astype(BF), step).astype(F32)
    proj_sum = pair_up(proj_half, swap(proj_half, "c"), c, 0).reshape(width, -1)
    return (
        y_out,
        loss_out,
        grad_input,
        jnp.stack([qkv_part[:, k * half_width : (k + 1) * half_width] for k in range(3)]),
        half_sums[: 2 * half_width].reshape(2, half_width),
        out_part.T,
        shared[4],
        shared[0:2],
        shared[2:4],
        up_part,
        half_sums[2 * half_width :],
        down_part.T,
        shared[5],
        proj_sum,
    )


IN_SPECS = (
    P("dp", None),
    P(),
    P("dp", "tensor"),
    P(None, "dp", "tensor"),
    P(None, "tensor"),
    P("tensor", "dp"),
    P(),
    P(),
    P(),
    P("dp", "tensor"),
    P("tensor"),
    P("tensor", "dp"),
    P(),
    P(),
    P(("dp", "tensor"), None),
)
OUT_SPECS = (
    P(("dp", "tensor"), None),
    P("dp", "tensor"),
    P(("dp", "tensor"), None),
    P(None, "dp", "tensor"),
    P(None, "tensor"),
    P("tensor", "dp"),
    P(),
    P(),
    P(),
    P("dp", "tensor"),
    P("tensor"),
    P("tensor", "dp"),
    P(),
    P(),
)


def solution(mesh):
    if mesh.devices.shape != (16, 2):
        return jax.shard_map(
            local, mesh=mesh, in_specs=IN_SPECS, out_specs=OUT_SPECS, check_vma=False
        )
    names = {"dp": ("z", "x", "c"), "tensor": ("y",)}

    def respec(spec):
        parts = []
        for entry in spec:
            axes = () if entry is None else entry if isinstance(entry, tuple) else (entry,)
            parts.append(tuple(name for axis in axes for name in names[axis]) or None)
        return P(*parts)

    chips = Mesh(mesh.devices.reshape(4, 2, 2, 2), ("z", "x", "c", "y"))
    return jax.shard_map(
        local_chip,
        mesh=chips,
        in_specs=tuple(respec(spec) for spec in IN_SPECS),
        out_specs=tuple(respec(spec) for spec in OUT_SPECS),
        check_vma=False,
    )
```

```python
from functools import partial

import jax
import jax.numpy as jnp
from jax import lax
from jax.experimental import pallas as pl
from jax.experimental.pallas import tpu as pltpu
from jax.sharding import Mesh, PartitionSpec as P

HEAD_DIM = 64
QLEN = 32
NQ_ROW = 8
NDOC = 8


EPS_NORM = 1e-05
EPS_EMBED = 1e-06
POOL_TEMP = 0.1
LOSS_TEMP = 0.1
FULL_PRECISION = lax.Precision.HIGHEST
MASKED_SCORE = -1e30


def shortened(shard):

    def short(part):
        return part.astype(jnp.bfloat16) if part.dtype == jnp.float32 else part

    return jax.tree.map(short, shard)


def contract_rows(left, right, precision=None):
    return lax.dot_general(
        left,
        right,
        (((0,), (0,)), ((), ())),
        precision=precision,
        preferred_element_type=jnp.float32,
    )


def contract_cols(left, right, precision=None):
    return lax.dot_general(
        left,
        right,
        (((1,), (1,)), ((), ())),
        precision=precision,
        preferred_element_type=jnp.float32,
    )


def norm_forward(value, gain, shift):
    centred = value - jnp.mean(value, axis=1, keepdims=True)
    rstd = lax.rsqrt(jnp.mean(centred * centred, axis=1, keepdims=True) + EPS_NORM)
    unit = centred * rstd
    return (unit * gain + shift, unit, rstd)


def norm_backward(grad, unit, rstd, gain):
    scaled = grad * gain
    return rstd * (
        scaled
        - jnp.mean(scaled, axis=1, keepdims=True)
        - unit * jnp.mean(scaled * unit, axis=1, keepdims=True)
    )


def segments_of(row_lengths, token_count):
    position = jnp.arange(token_count, dtype=jnp.int32)
    query_span = NQ_ROW * QLEN
    ends = jnp.cumsum(row_lengths)
    passed = jnp.sum((position[:, None] - query_span >= ends[None, :]).astype(jnp.int32), axis=1)
    return jnp.where(position < query_span, position // QLEN, NQ_ROW + passed)


def normalize_cut(raw, width):
    part = raw[:, :width]
    scale = lax.rsqrt(jnp.sum(part * part, axis=1, keepdims=True) + EPS_EMBED)
    return (part * scale, part, scale)


def normalize_back(grad, part, scale, full_width):
    result = scale * grad - part * (scale * scale * scale) * jnp.sum(
        part * grad, axis=1, keepdims=True
    )
    return jnp.pad(result, ((0, 0), (0, full_width - grad.shape[1])))


def masked_scores(query_block, key_rows, block_segments, segments):
    scores = jnp.einsum(
        "qhd,khd->hqk", query_block, key_rows, preferred_element_type=jnp.float32
    ) * HEAD_DIM ** (-0.5)
    return jnp.where((block_segments[:, None] == segments[None, :])[None], scores, MASKED_SCORE)


def attend_forward(query_rows, key_rows, value_rows, segments, block_rows):
    token_count = query_rows.shape[0]

    def one_block(block_start):
        query_block = lax.dynamic_slice_in_dim(query_rows, block_start, block_rows, 0)
        block_segments = lax.dynamic_slice_in_dim(segments, block_start, block_rows, 0)
        scores = masked_scores(query_block, key_rows, block_segments, segments)
        highest = jnp.max(scores, axis=2, keepdims=True)
        expo = jnp.exp(scores - highest)
        totals = jnp.sum(expo, axis=2, keepdims=True)
        weights = (expo / totals).astype(jnp.bfloat16)
        mixed = jnp.einsum("hqk,khd->qhd", weights, value_rows, preferred_element_type=jnp.float32)
        return (mixed.astype(jnp.bfloat16), (highest + jnp.log(totals))[:, :, 0])

    starts = jnp.arange(token_count // block_rows, dtype=jnp.int32) * block_rows
    mixed, log_totals = lax.map(one_block, starts)
    return (mixed.reshape(token_count, -1), log_totals)


def attend_backward(query_rows, key_rows, value_rows, segments, log_totals, grad_mixed, block_rows):
    token_count, local_heads, head_size = query_rows.shape
    scale = HEAD_DIM ** (-0.5)
    grad_heads = grad_mixed.reshape(token_count, local_heads, head_size)

    def one_block(carried, inputs):
        grad_keys, grad_values = carried
        block_start, block_lse = inputs
        query_block = lax.dynamic_slice_in_dim(query_rows, block_start, block_rows, 0)
        grad_block = lax.dynamic_slice_in_dim(grad_heads, block_start, block_rows, 0)
        block_segments = lax.dynamic_slice_in_dim(segments, block_start, block_rows, 0)
        scores = masked_scores(query_block, key_rows, block_segments, segments)
        probs = jnp.exp(scores - block_lse[:, :, None])
        grad_probs = jnp.einsum(
            "qhd,khd->hqk", grad_block, value_rows, preferred_element_type=jnp.float32
        )
        inner = jnp.sum(probs * grad_probs, axis=2, keepdims=True)
        grad_scores = (probs * (grad_probs - inner)).astype(jnp.bfloat16)
        grad_query = (
            jnp.einsum("hqk,khd->qhd", grad_scores, key_rows, preferred_element_type=jnp.float32)
            * scale
        )
        grad_keys = (
            grad_keys
            + jnp.einsum(
                "hqk,qhd->khd", grad_scores, query_block, preferred_element_type=jnp.float32
            )
            * scale
        )
        grad_values = grad_values + jnp.einsum(
            "hqk,qhd->khd",
            probs.astype(jnp.bfloat16),
            grad_block,
            preferred_element_type=jnp.float32,
        )
        return ((grad_keys, grad_values), grad_query)

    starts = jnp.arange(token_count // block_rows, dtype=jnp.int32) * block_rows
    zero_rows = jnp.zeros(key_rows.shape, jnp.float32)
    (grad_keys, grad_values), grad_queries = lax.scan(
        one_block, (zero_rows, zero_rows), (starts, log_totals)
    )
    flat_width = local_heads * head_size
    return (
        grad_queries.reshape(token_count, flat_width),
        grad_keys.reshape(token_count, flat_width),
        grad_values.reshape(token_count, flat_width),
    )


def local(
    tokens,
    lengths,
    pairing,
    w_qkv,
    b_qv,
    w_out,
    b_out,
    ln_gain,
    ln_bias,
    w_up,
    b_up,
    w_down,
    b_down,
    w_proj,
    cot,
):
    tensor_count = lax.axis_size("tensor")
    tensor_index = lax.axis_index("tensor")
    data_index = lax.axis_index("dp")
    token_count = tokens.shape[0]
    share_rows = token_count // tensor_count
    block_rows = min(512, token_count)
    own_start = tensor_index * share_rows
    full_qkv, full_out, full_up, full_down = (
        lax.all_gather(w_qkv, "dp", axis=1, tiled=True),
        lax.all_gather(w_out, "dp", axis=1, tiled=True),
        lax.all_gather(w_up, "dp", axis=0, tiled=True),
        lax.all_gather(w_down, "dp", axis=1, tiled=True),
    )
    head_width = full_qkv.shape[2]
    local_heads = head_width // HEAD_DIM
    row_lengths = lax.dynamic_index_in_dim(lengths, data_index, 0, keepdims=False)
    segments = segments_of(row_lengths, token_count)
    projected = jnp.einsum("td,kdw->ktw", tokens, full_qkv, preferred_element_type=jnp.float32)
    qv_bias = b_qv.astype(jnp.float32)
    query_rows = (
        (projected[0] + qv_bias[0]).astype(jnp.bfloat16).reshape(token_count, local_heads, HEAD_DIM)
    )
    key_rows = projected[1].astype(jnp.bfloat16).reshape(token_count, local_heads, HEAD_DIM)
    value_rows = (
        (projected[2] + qv_bias[1]).astype(jnp.bfloat16).reshape(token_count, local_heads, HEAD_DIM)
    )
    mixed, log_totals = attend_forward(query_rows, key_rows, value_rows, segments, block_rows)
    attn_terms = jnp.dot(mixed, full_out, preferred_element_type=jnp.float32)
    attn_sum = lax.psum_scatter(
        attn_terms.astype(jnp.bfloat16), "tensor", scatter_dimension=0, tiled=True
    ).astype(jnp.float32)
    own_tokens = lax.dynamic_slice_in_dim(tokens, own_start, share_rows, 0).astype(jnp.float32)
    gains = ln_gain.astype(jnp.float32)
    shifts = ln_bias.astype(jnp.float32)
    normed, unit_one, rstd_one = norm_forward(
        own_tokens + attn_sum + b_out.astype(jnp.float32), gains[0], shifts[0]
    )
    normed_all = lax.all_gather(normed.astype(jnp.bfloat16), "tensor", axis=0, tiled=True)
    up_value = jnp.dot(normed_all, full_up, preferred_element_type=jnp.float32) + b_up.astype(
        jnp.float32
    )
    activation = jax.nn.gelu(up_value, approximate=False).astype(jnp.bfloat16)
    ffn_terms = jnp.dot(activation, full_down, preferred_element_type=jnp.float32)
    ffn_sum = lax.psum_scatter(
        ffn_terms.astype(jnp.bfloat16), "tensor", scatter_dimension=0, tiled=True
    ).astype(jnp.float32)
    result, unit_two, rstd_two = norm_forward(
        normed + ffn_sum + b_down.astype(jnp.float32), gains[1], shifts[1]
    )
    result_low = result.astype(jnp.bfloat16)
    embed = jnp.dot(result_low, w_proj, preferred_element_type=jnp.float32).astype(jnp.bfloat16)
    embed_all = lax.all_gather(embed, ("dp", "tensor"), axis=0, tiled=True)
    row_count = lengths.shape[0]
    proj_width = w_proj.shape[1]
    widths = (proj_width, 3 * proj_width // 4, proj_width // 2)
    per_device = pairing.shape[1]
    query_count = per_device * QLEN
    query_span = NQ_ROW * QLEN
    emb_rows = embed_all.reshape(row_count, token_count, proj_width)
    my_row = lax.dynamic_index_in_dim(emb_rows, data_index, 0, keepdims=False)
    query_raw = lax.dynamic_slice_in_dim(my_row, tensor_index * query_count, query_count, 0).astype(
        jnp.float32
    )
    query_levels = [normalize_cut(query_raw, width) for width in widths]
    query_units = [level_parts[0].astype(jnp.bfloat16) for level_parts in query_levels]
    doc_numbers = jnp.arange(NDOC, dtype=jnp.int32)

    def row_pool(carried, inputs):
        row_emb, lengths_row = inputs
        row_hot = (
            segments_of(lengths_row, token_count)[:, None] == NQ_ROW + doc_numbers[None, :]
        ).astype(jnp.float32)
        row_raw = row_emb.astype(jnp.float32)
        pooled_list = []
        sums_list = []
        for width, query_unit in zip(widths, query_units):
            doc_unit = normalize_cut(row_raw, width)[0].astype(jnp.bfloat16)
            expo = jnp.exp(contract_cols(query_unit, doc_unit) / POOL_TEMP)
            sums = jnp.dot(expo, row_hot, precision=FULL_PRECISION)
            pooled = POOL_TEMP * jnp.log(sums / lengths_row.astype(jnp.float32))
            pooled_list.append(jnp.sum(pooled.reshape(per_device, QLEN, NDOC), axis=1))
            sums_list.append(sums)
        return (carried, (jnp.stack(pooled_list), jnp.stack(sums_list)))

    _, (row_scores, row_sums) = lax.scan(row_pool, 0, (emb_rows, lengths))
    logits = (
        jnp.transpose(row_scores, (2, 1, 0, 3)).reshape(per_device, 3, row_count * NDOC) / LOSS_TEMP
    )
    own_pairs = pairing[0]
    target = jnp.take_along_axis(
        logits, jnp.broadcast_to(own_pairs[:, None, None], (per_device, 3, 1)), axis=2
    )[:, :, 0]
    loss_out = jnp.sum(jax.nn.logsumexp(logits, axis=2) - target, axis=1).reshape(1, per_device)
    picked = (
        jnp.arange(row_count * NDOC, dtype=jnp.int32)[None, None, :] == own_pairs[:, None, None]
    ).astype(jnp.float32)
    grad_logits = (jax.nn.softmax(logits, axis=2) - picked) / LOSS_TEMP
    grad_rows = jnp.transpose(grad_logits.reshape(per_device, 3, row_count, NDOC), (2, 1, 0, 3))
    coefficient = jnp.repeat(grad_rows, QLEN, axis=2) / row_sums

    def row_back(carried, inputs):
        row_emb, lengths_row, row_coef = inputs
        row_hot = (
            segments_of(lengths_row, token_count)[:, None] == NQ_ROW + doc_numbers[None, :]
        ).astype(jnp.float32)
        row_raw = row_emb.astype(jnp.float32)
        new_carried = []
        row_grad = jnp.zeros((token_count, proj_width), jnp.float32)
        for level_index in range(3):
            width = widths[level_index]
            doc_unit_f, doc_part, doc_scale = normalize_cut(row_raw, width)
            doc_unit = doc_unit_f.astype(jnp.bfloat16)
            expo = jnp.exp(contract_cols(query_units[level_index], doc_unit) / POOL_TEMP)
            spread = contract_cols(row_coef[level_index], row_hot, FULL_PRECISION)
            grad_sim = (expo * spread).astype(jnp.bfloat16)
            new_carried.append(
                carried[level_index]
                + jnp.dot(grad_sim, doc_unit, preferred_element_type=jnp.float32)
            )
        return (tuple(new_carried), row_grad)

    zero_query = tuple((jnp.zeros((query_count, width), jnp.float32) for width in widths))
    query_grads, doc_grads = lax.scan(row_back, zero_query, (emb_rows, lengths, coefficient))
    grad_query = jnp.zeros((query_count, proj_width), jnp.float32)
    for level_index in range(3):
        level_parts = query_levels[level_index]
        grad_query = grad_query + normalize_back(
            query_grads[level_index], level_parts[1], level_parts[2], proj_width
        )
    coef_mine = jnp.transpose(coefficient, (2, 1, 0, 3)).reshape(query_count, 3, row_count * NDOC)
    coef_all, grad_query_all = (
        lax.all_gather(shortened(coef_mine), ("dp", "tensor"), axis=0, tiled=True).astype(
            coef_mine.dtype
        ),
        lax.all_gather(
            grad_query.astype(jnp.bfloat16), ("dp", "tensor"), axis=0, tiled=True
        ).astype(grad_query.dtype),
    )
    own_raw = embed.astype(jnp.float32)
    own_segments = lax.dynamic_slice_in_dim(segments, own_start, share_rows, 0)
    own_docs = jnp.where(own_segments >= NQ_ROW, data_index * NDOC + own_segments - NQ_ROW, -1)
    own_hot = (own_docs[:, None] == jnp.arange(row_count * NDOC, dtype=jnp.int32)[None, :]).astype(
        jnp.float32
    )
    queries_all = (
        emb_rows[:, :query_span].reshape(row_count * query_span, proj_width).astype(jnp.float32)
    )
    grad_embed = jnp.zeros((share_rows, proj_width), jnp.float32)
    for level_index in range(3):
        width = widths[level_index]
        query_unit_all = normalize_cut(queries_all, width)[0].astype(jnp.bfloat16)
        doc_unit_f, doc_part, doc_scale = normalize_cut(own_raw, width)
        expo = jnp.exp(contract_cols(query_unit_all, doc_unit_f.astype(jnp.bfloat16)) / POOL_TEMP)
        spread = contract_cols(coef_all[:, level_index], own_hot, FULL_PRECISION)
        grad_sim = (expo * spread).astype(jnp.bfloat16)
        grad_doc = contract_rows(grad_sim, query_unit_all)
        grad_embed = grad_embed + normalize_back(grad_doc, doc_part, doc_scale, proj_width)
    row_query_grads = lax.dynamic_slice_in_dim(
        grad_query_all, data_index * query_span, query_span, 0
    )
    padded = jnp.pad(row_query_grads, ((0, token_count - query_span), (0, 0)))
    grad_embed = grad_embed + lax.dynamic_slice_in_dim(padded, own_start, share_rows, 0)
    proj_float = w_proj.astype(jnp.float32)
    grad_result = cot.astype(jnp.float32) + contract_cols(grad_embed, proj_float, FULL_PRECISION)
    proj_grad = contract_rows(result_low.astype(jnp.float32), grad_embed, FULL_PRECISION)
    gain_two = jnp.sum(grad_result * unit_two, axis=0)
    shift_two = jnp.sum(grad_result, axis=0)
    grad_second = norm_backward(grad_result, unit_two, rstd_two, gains[1])
    grad_ffn = grad_second.astype(jnp.bfloat16)
    down_bias = jnp.sum(grad_ffn.astype(jnp.float32), axis=0)
    grad_ffn_all = lax.all_gather(grad_ffn, "tensor", axis=0, tiled=True)
    grad_act = contract_cols(grad_ffn_all, full_down)
    down_grad = contract_rows(activation, grad_ffn_all)
    _, gelu_pull = jax.vjp(partial(jax.nn.gelu, approximate=False), up_value)
    grad_up = gelu_pull(grad_act)[0].astype(jnp.bfloat16)
    up_bias = jnp.sum(grad_up.astype(jnp.float32), axis=0)
    up_grad = contract_rows(normed_all, grad_up)
    normed_terms = contract_cols(grad_up, full_up)
    grad_normed = (
        lax.psum_scatter(
            normed_terms.astype(jnp.bfloat16), "tensor", scatter_dimension=0, tiled=True
        ).astype(jnp.float32)
        + grad_second
    )
    gain_one = jnp.sum(grad_normed * unit_one, axis=0)
    shift_one = jnp.sum(grad_normed, axis=0)
    grad_first = norm_backward(grad_normed, unit_one, rstd_one, gains[0])
    grad_attn = grad_first.astype(jnp.bfloat16)
    out_bias = jnp.sum(grad_attn.astype(jnp.float32), axis=0)
    grad_attn_all = lax.all_gather(grad_attn, "tensor", axis=0, tiled=True)
    out_grad = contract_rows(mixed, grad_attn_all)
    grad_mixed = contract_cols(grad_attn_all, full_out).astype(jnp.bfloat16)
    grad_q, grad_k, grad_v = attend_backward(
        query_rows, key_rows, value_rows, segments, log_totals, grad_mixed, block_rows
    )
    stacked_grads = jnp.stack(
        [grad_q.astype(jnp.bfloat16), grad_k.astype(jnp.bfloat16), grad_v.astype(jnp.bfloat16)]
    )
    qkv_grad = jnp.einsum("td,ktw->kdw", tokens, stacked_grads, preferred_element_type=jnp.float32)
    input_terms = jnp.einsum(
        "ktw,kdw->td", stacked_grads, full_qkv, preferred_element_type=jnp.float32
    )
    grad_input = (
        lax.psum_scatter(
            input_terms.astype(jnp.bfloat16), "tensor", scatter_dimension=0, tiled=True
        ).astype(jnp.float32)
        + grad_first
    )
    qv_grad = jnp.stack(
        [
            jnp.sum(stacked_grads[0].astype(jnp.float32), axis=0),
            jnp.sum(stacked_grads[2].astype(jnp.float32), axis=0),
        ]
    )
    qkv_part, out_part, up_part, down_part = (
        lax.psum_scatter(
            qkv_grad.astype(jnp.bfloat16), "dp", scatter_dimension=1, tiled=True
        ).astype(jnp.float32),
        lax.psum_scatter(
            out_grad.astype(jnp.bfloat16), "dp", scatter_dimension=1, tiled=True
        ).astype(jnp.float32),
        lax.psum_scatter(
            up_grad.astype(jnp.bfloat16), "dp", scatter_dimension=0, tiled=True
        ).astype(jnp.float32),
        lax.psum_scatter(
            down_grad.astype(jnp.bfloat16), "dp", scatter_dimension=1, tiled=True
        ).astype(jnp.float32),
    )
    gain_sum, shift_sum, out_bias_sum, down_bias_sum, proj_sum = lax.psum(
        (
            jnp.stack([gain_one, gain_two]),
            jnp.stack([shift_one, shift_two]),
            out_bias,
            down_bias,
            proj_grad,
        ),
        ("dp", "tensor"),
    )
    qv_sum, up_bias_sum = lax.psum((qv_grad, up_bias), "dp")
    return (
        result_low,
        loss_out,
        grad_input.astype(jnp.bfloat16),
        qkv_part,
        qv_sum,
        out_part,
        out_bias_sum,
        gain_sum,
        shift_sum,
        up_part,
        up_bias_sum,
        down_part,
        down_bias_sum,
        proj_sum,
    )


SWAP = [(0, 1), (1, 0)]
TURN = [(0, 0), (1, 2), (2, 1), (3, 3)]
FAR = [(0, 3), (3, 0), (1, 2), (2, 1)]
NEAR = [(0, 1), (1, 0), (2, 3), (3, 2)]
BF = jnp.bfloat16
F32 = jnp.float32


def dot(left, right):
    return jnp.dot(left, right, preferred_element_type=F32)


def turn(value):
    return lax.ppermute(value, ("c", "y"), TURN)


def swap(value, axis):
    return lax.ppermute(value, axis, SWAP)


def pair_up(first, second, own_index, axis):
    return jnp.where(
        own_index == 0, jnp.stack([first, second], axis), jnp.stack([second, first], axis)
    )


def gather_far(value, z):
    far = lax.ppermute(value, "z", FAR)
    return jnp.where(z < 2, jnp.stack([value, far]), jnp.stack([far, value]))


def gather_near(pair, z):
    other = lax.ppermute(pair, "z", NEAR)
    return jnp.where(
        (z == 0) | (z == 3),
        jnp.stack([pair[0], other[0], other[1], pair[1]]),
        jnp.stack([other[0], pair[0], pair[1], other[1]]),
    )


def gather_c(value, c, y, axis):
    got = lax.ppermute(value, ("c", "y"), [(2, 0), (1, 3), (0, 1), (3, 2)])
    cross = lax.ppermute(value, ("c", "y"), [(2, 1), (1, 2)])
    first = jnp.where(c == y, value, got)
    second = jnp.where(c == y, got, cross)
    return pair_up(first, second, c, axis)


def gather_x(value, x, axis):
    return pair_up(value, swap(value, "x"), x, axis)


def gather_first(value, x, c, y):
    half = value.shape[1] // 2
    return (gather_x(value[:, :half], x, 1), gather_c(value[:, half:], c, y, 1))


def gather_last(parts, x, c, y):
    left = gather_c(parts[0], c, y, 2)
    right = gather_x(parts[1], x, 1)
    return jnp.concatenate([left, right], axis=3).reshape(-1, left.shape[-1])


def tie(value, *others):
    return lax.optimization_barrier((value,) + others)[0]


def sum_c(blocks, c, y):
    axis = blocks.ndim - 3
    mine = lax.dynamic_index_in_dim(blocks, c, axis, keepdims=False)
    other = lax.dynamic_index_in_dim(blocks, 1 - c, axis, keepdims=False)
    other_low = other.astype(BF)
    got = lax.ppermute(
        jnp.where(c == y, other_low, mine.astype(BF)),
        ("c", "y"),
        [(0, 2), (3, 1), (1, 0), (2, 3)],
    )
    cross = lax.ppermute(other_low, ("c", "y"), [(1, 2), (2, 1)])
    return got.astype(F32) + jnp.where(c == y, mine.astype(F32), cross.astype(F32))


def sum_x(blocks, x, axis):
    theirs = lax.dynamic_index_in_dim(blocks, 1 - x, axis, keepdims=False)
    mine = lax.dynamic_index_in_dim(blocks, x, axis, keepdims=False)
    return mine.astype(F32) + swap(theirs.astype(BF), "x").astype(F32)


def sum_z(blocks, z):
    ends = (z == 0) | (z == 3)
    outer, inner = jnp.stack([blocks[0], blocks[3]]), blocks[1:3]
    pair = jnp.where(ends, outer, inner) + lax.ppermute(
        jnp.where(ends, inner, outer).astype(BF), "z", NEAR
    ).astype(F32)
    given = lax.ppermute(jnp.where(z < 2, pair[1], pair[0]).astype(BF), "z", FAR)
    return jnp.where(z < 2, pair[0], pair[1]) + given.astype(F32)


def weight_sum(left, right, z, x, c, y):
    blocks = contract_rows(left, right).astype(BF).reshape(4, 2, 2, 64, right.shape[1])
    low = sum_x(blocks[..., :32, :], x, 1)
    high = sum_c(blocks[..., 32:, :], c, y)
    low = sum_c(low, c, y)
    high = sum_x(high, x, 1)
    return sum_z(jnp.concatenate([low, high], axis=1), z)


def sum_other(value, step):
    if step == "0":
        return lax.ppermute(value, "z", NEAR)
    if step == "1":
        return lax.ppermute(value, "z", FAR)
    return swap(value, step)


def sum_chips(value, steps):
    for step in steps:
        value = value + sum_other(value, step)
    return value


def tile_bounds(row_lengths, token_count):
    ends = jnp.cumsum(row_lengths)
    span = NQ_ROW * QLEN
    first = jnp.arange(token_count // TILE, dtype=jnp.int32) * TILE - span
    last = first + TILE - 1
    begin = jnp.max(jnp.where(ends[None, :] <= first[:, None], ends[None, :], 0), axis=1)
    end = jnp.min(jnp.where(ends[None, :] > last[:, None], ends[None, :], token_count), axis=1)
    low = jnp.where(first < 0, 0, (begin + span) // TILE)
    high = jnp.where(first < 0, 1, (end + span + TILE - 1) // TILE)
    return jnp.stack([low, high]).astype(jnp.int32)


def rows_of(value, start, count):
    return lax.dynamic_slice_in_dim(value, start, count, 0)


TILE = 256
NEG = -1e30


def exact(left, right, dims):
    return lax.dot_general(left, right, (dims, ((), ())), preferred_element_type=F32)


def head_masks(value):
    lane = lax.broadcasted_iota(jnp.int32, value.shape, 1)
    zero = jnp.zeros_like(value)
    return (jnp.where(lane < HEAD_DIM, value, zero), jnp.where(lane < HEAD_DIM, zero, value))


def fill_bias(seg_col, seg_row, bias):
    for start in range(0, bias.shape[0], TILE):
        rows = slice(start, start + TILE)
        bias[rows, :] = jnp.where(seg_col[rows, :] == seg_row[...], 0.0, NEG)


def attend_kernel(bounds, q_ref, k_ref, v_ref, seg_col, seg_row, out_ref, lse_ref, bias, held):
    @pl.when(pl.program_id(0) == 0)
    def _():
        fill_bias(seg_col, seg_row, bias)

    for block in range(q_ref.shape[0] // TILE):
        own = slice(block * TILE, (block + 1) * TILE)
        queries = head_masks(q_ref[own, :] * HEAD_DIM**-0.5)

        def score(step, highest):
            rows = pl.ds(pl.multiple_of(step * TILE, TILE), TILE)
            keys, shift = k_ref[rows, :], bias[rows, own]
            fresh = []
            for head in range(2):
                scores = exact(keys, queries[head], ((1,), (1,))) + shift
                held[head, rows, :] = scores
                fresh.append(jnp.maximum(highest[head], jnp.max(scores, axis=0, keepdims=True)))
            return tuple(fresh)

        low = jnp.full((1, TILE), NEG, F32)
        highest = lax.fori_loop(bounds[0, block], bounds[1, block], score, (low, low))

        def mix(step, carried):
            rows = pl.ds(pl.multiple_of(step * TILE, TILE), TILE)
            values = v_ref[rows, :]
            fresh = []
            for head in range(2):
                total, mixed = carried[head]
                expo = jnp.exp(held[head, rows, :] - highest[head])
                fresh.append(
                    (
                        total + jnp.sum(expo, axis=0, keepdims=True),
                        mixed + exact(values, expo.astype(BF), ((0,), (0,))),
                    )
                )
            return tuple(fresh)

        start = (jnp.zeros((1, TILE), F32), jnp.zeros((2 * HEAD_DIM, TILE), F32))
        parts = lax.fori_loop(bounds[0, block], bounds[1, block], mix, (start, start))
        mixed = jnp.concatenate(
            [parts[0][1][:HEAD_DIM] / parts[0][0], parts[1][1][HEAD_DIM:] / parts[1][0]], axis=0
        )
        out_ref[own, :] = jnp.transpose(mixed).astype(BF)
        for head in range(2):
            lse_ref[0, head : head + 1, own] = highest[head] + jnp.log(parts[head][0])


def attend(bounds, qkv, seg_col, seg_row):
    count, wide = qkv.shape
    pairs = wide // 3 // 128
    column = lambda shift: pl.BlockSpec((count, 128), lambda i: (0, shift + i))
    whole = lambda shape: pl.BlockSpec(shape, lambda i: (0, 0))
    return pl.pallas_call(
        attend_kernel,
        grid=(pairs,),
        in_specs=[
            pl.BlockSpec(memory_space=pltpu.SMEM),
            column(0),
            column(pairs),
            column(2 * pairs),
            whole((count, 1)),
            whole((1, count)),
        ],
        out_specs=[column(0), pl.BlockSpec((1, 8, count), lambda i: (i, 0, 0))],
        out_shape=[
            jax.ShapeDtypeStruct((count, wide // 3), BF),
            jax.ShapeDtypeStruct((pairs, 8, count), F32),
        ],
        scratch_shapes=[pltpu.VMEM((count, count), F32), pltpu.VMEM((2, count, TILE), F32)],
        compiler_params=pltpu.CompilerParams(vmem_limit_bytes=40 << 20),
        cost_estimate=pl.CostEstimate(
            flops=4 * pairs * count * count * 128,
            transcendentals=pairs * count * count,
            bytes_accessed=4 * count * wide * 2,
        ),
    )(bounds, qkv, qkv, qkv, seg_col, seg_row)


def attend_back_kernel(
    bounds, q_ref, k_ref, v_ref, out_ref, grad_ref, lse_ref, seg_col, seg_row,
    grads_ref, sums_ref, bias, key_sum, value_sum,
):
    pair = pl.program_id(0)

    @pl.when(pair == 0)
    def _():
        fill_bias(seg_col, seg_row, bias)

    key_sum[...] = jnp.zeros_like(key_sum)
    value_sum[...] = jnp.zeros_like(value_sum)
    columns = [
        pl.ds(pl.multiple_of(part * (grads_ref.shape[1] // 3) + pair * 128, 128), 128) for part in range(3)
    ]
    query_total = jnp.zeros((1, 128), F32)
    picks = head_masks(jnp.ones((8, 128), BF))
    for block in range(q_ref.shape[0] // TILE):
        own = slice(block * TILE, (block + 1) * TILE)
        queries = head_masks(q_ref[own, :] * HEAD_DIM**-0.5)
        grads = head_masks(grad_ref[own, :])
        product = grad_ref[own, :].astype(F32) * out_ref[own, :].astype(F32)
        product_high = product.astype(BF)
        product_low = (product - product_high.astype(F32)).astype(BF)
        inner = [
            (
                exact(picks[head], product_high, ((1,), (1,)))
                + exact(picks[head], product_low, ((1,), (1,)))
            )[0:1]
            for head in range(2)
        ]
        lse = [lse_ref[0, head : head + 1, own] for head in range(2)]

        def step_of(step, carried):
            rows = pl.ds(pl.multiple_of(step * TILE, TILE), TILE)
            keys, values, shift = k_ref[rows, :], v_ref[rows, :], bias[rows, own]
            fresh = []
            key_add = jnp.zeros((TILE, 128), F32)
            value_add = jnp.zeros((TILE, 128), F32)
            for head in range(2):
                scores = exact(keys, queries[head], ((1,), (1,))) + shift
                probs = jnp.exp(scores - lse[head])
                grad_probs = exact(values, grads[head], ((1,), (1,)))
                grad_scores = (probs * (grad_probs - inner[head])).astype(BF)
                value_add = value_add + exact(probs.astype(BF), grads[head], ((1,), (0,)))
                key_add = key_add + exact(grad_scores, queries[head], ((1,), (0,)))
                fresh.append(carried[head] + exact(keys, grad_scores, ((0,), (0,))))
            key_sum[rows, :] += key_add
            value_sum[rows, :] += value_add
            return tuple(fresh)

        start = jnp.zeros((2 * HEAD_DIM, TILE), F32)
        parts = lax.fori_loop(bounds[0, block], bounds[1, block], step_of, (start, start))
        grad_query = jnp.concatenate([parts[0][:HEAD_DIM], parts[1][HEAD_DIM:]], axis=0)
        grad_query = jnp.transpose(grad_query * HEAD_DIM**-0.5).astype(BF)
        grads_ref[own, columns[0]] = grad_query
        query_total = query_total + jnp.sum(grad_query.astype(F32), axis=0, keepdims=True)
    grad_value = value_sum[...].astype(BF)
    grads_ref[:, columns[1]] = key_sum[...].astype(BF)
    grads_ref[:, columns[2]] = grad_value
    sums_ref[0, 0:1, :] = query_total
    sums_ref[0, 1:2, :] = jnp.sum(grad_value.astype(F32), axis=0, keepdims=True)


def attend_back(bounds, qkv, mixed, grad_mixed, lse, seg_col, seg_row):
    count, wide = qkv.shape
    pairs = wide // 3 // 128
    column = lambda shift: pl.BlockSpec((count, 128), lambda i: (0, shift + i))
    whole = lambda shape: pl.BlockSpec(shape, lambda i: (0, 0))
    return pl.pallas_call(
        attend_back_kernel,
        grid=(pairs,),
        in_specs=[
            pl.BlockSpec(memory_space=pltpu.SMEM),
            column(0),
            column(pairs),
            column(2 * pairs),
            column(0),
            column(0),
            pl.BlockSpec((1, 8, count), lambda i: (i, 0, 0)),
            whole((count, 1)),
            whole((1, count)),
        ],
        out_specs=[whole((count, wide)), pl.BlockSpec((1, 8, 128), lambda i: (i, 0, 0))],
        out_shape=[
            jax.ShapeDtypeStruct((count, wide), BF),
            jax.ShapeDtypeStruct((pairs, 8, 128), F32),
        ],
        scratch_shapes=[
            pltpu.VMEM((count, count), F32),
            pltpu.VMEM((count, 128), F32),
            pltpu.VMEM((count, 128), F32),
        ],
        compiler_params=pltpu.CompilerParams(vmem_limit_bytes=40 << 20),
        cost_estimate=pl.CostEstimate(
            flops=10 * pairs * count * count * 128,
            transcendentals=pairs * count * count,
            bytes_accessed=8 * count * wide * 2,
        ),
    )(bounds, qkv, qkv, qkv, mixed, grad_mixed, lse, seg_col, seg_row)


ERFC = (
    -1.26551223, 1.00002368, 0.37409196, 0.09678418, -0.18628806,
    0.27886807, -1.13520398, 1.48851587, -0.82215223, 0.17087277,
)


def gelu_pair(value):
    size = jnp.abs(value) * 0.5**0.5
    ratio = 1.0 / (1.0 + 0.5 * size)
    series = jnp.full_like(value, ERFC[-1])
    for factor in ERFC[-2::-1]:
        series = series * ratio + factor
    bell = jnp.exp(-size * size)
    tail = 0.5 * ratio * bell * jnp.exp(series)
    phi = jnp.where(value < 0.0, tail, 1.0 - tail)
    return (value * phi, phi + value * bell * 0.3989422804014327)


def expand_kernel(x_ref, w_ref, b_ref, act_ref, slope_ref):
    rows = 256
    for start in range(0, x_ref.shape[0], rows):
        part = slice(start, start + rows)
        value = exact(x_ref[part, :], w_ref[...], ((1,), (0,))) + b_ref[...]
        active, slope = gelu_pair(value)
        act_ref[part, :] = active.astype(BF)
        slope_ref[part, :] = slope.astype(BF)


def expand(value, weight, shift):
    count, depth = value.shape
    width = shift.shape[1]
    tile = 256
    return pl.pallas_call(
        expand_kernel,
        grid=(width // tile,),
        in_specs=[
            pl.BlockSpec((count, depth), lambda i: (0, 0)),
            pl.BlockSpec((depth, tile), lambda i: (0, i)),
            pl.BlockSpec((1, tile), lambda i: (0, i)),
        ],
        out_specs=[pl.BlockSpec((count, tile), lambda i: (0, i))] * 2,
        out_shape=[jax.ShapeDtypeStruct((count, width), BF)] * 2,
        compiler_params=pltpu.CompilerParams(vmem_limit_bytes=32 << 20),
        cost_estimate=pl.CostEstimate(
            flops=2 * count * depth * width,
            transcendentals=3 * count * width,
            bytes_accessed=2 * (count * depth + depth * width + 2 * count * width),
        ),
    )(value, weight, shift)


def cut_levels(raw, cuts):
    lane = lax.broadcasted_iota(jnp.int32, raw.shape, 1)
    levels = []
    for cut in cuts:
        part = jnp.where(lane < cut, raw, 0.0)
        scale = lax.rsqrt(jnp.sum(part * part, axis=1, keepdims=True) + EPS_EMBED)
        levels.append(((part * scale).astype(BF), part, scale))
    return levels


def pool_kernel(cuts, span, q_ref, d_ref, seg_ref, out_ref, units, hot):
    @pl.when(pl.program_id(0) == 0)
    def _():
        raw = d_ref[span:, :].astype(F32)
        for level, parts in enumerate(cut_levels(raw, cuts)):
            units[level] = parts[0]
        doc = lax.broadcasted_iota(jnp.int32, hot.shape, 0)
        hot[...] = (seg_ref[:, span:] == NQ_ROW + doc).astype(F32).astype(BF)

    levels = cut_levels(q_ref[...].astype(F32), cuts)
    for level in range(len(cuts)):
        similar = exact(units[level], levels[level][0], ((1,), (1,)))
        expo = jnp.exp(similar * (1.0 / POOL_TEMP))
        high = expo.astype(BF)
        rest = (expo - high.astype(F32)).astype(BF)
        out_ref[level * NDOC : (level + 1) * NDOC, :] = exact(
            hot[...], high, ((1,), (0,))
        ) + exact(hot[...], rest, ((1,), (0,)))


def pool(cuts, span, queries, row_embed, seg_row):
    count, width = queries.shape
    tokens = row_embed.shape[0]
    whole = lambda shape: pl.BlockSpec(shape, lambda i: (0, 0))
    return pl.pallas_call(
        partial(pool_kernel, cuts, span),
        grid=(count // TILE,),
        in_specs=[
            pl.BlockSpec((TILE, width), lambda i: (i, 0)),
            whole((tokens, width)),
            whole((1, tokens)),
        ],
        out_specs=pl.BlockSpec((len(cuts) * NDOC, TILE), lambda i: (0, i)),
        out_shape=jax.ShapeDtypeStruct((len(cuts) * NDOC, count), F32),
        scratch_shapes=[
            pltpu.VMEM((len(cuts), tokens - span, width), BF),
            pltpu.VMEM((NDOC, tokens - span), BF),
        ],
        compiler_params=pltpu.CompilerParams(vmem_limit_bytes=32 << 20),
        cost_estimate=pl.CostEstimate(
            flops=2 * len(cuts) * count * tokens * 256,
            transcendentals=len(cuts) * count * tokens,
            bytes_accessed=2 * (count + tokens) * width,
        ),
    )(queries, row_embed, seg_row)


def level_back(grad, part, scale):
    return scale * grad - part * (scale * scale * scale) * jnp.sum(
        part * grad, axis=1, keepdims=True
    )


def pool_back_kernel(
    cuts, span, q_ref, d_ref, seg_ref, coef_ref, q_out, d_out, units, units_t, hot, sums
):
    step = pl.program_id(0)

    @pl.when(step == 0)
    def _():
        raw = d_ref[span:, :].astype(F32)
        for level, parts in enumerate(cut_levels(raw, cuts)):
            units[level] = parts[0]
            units_t[level] = jnp.transpose(parts[0])
        doc = lax.broadcasted_iota(jnp.int32, hot.shape, 0)
        wanted = NQ_ROW + jnp.where(doc < NDOC, doc, doc - NDOC)
        hot[...] = (seg_ref[:, span:] == wanted).astype(F32).astype(BF)
        sums[...] = jnp.zeros_like(sums)

    levels = cut_levels(q_ref[...].astype(F32), cuts)
    total = jnp.zeros(q_ref.shape, F32)
    for level in range(len(cuts)):
        unit, part, scale = levels[level]
        similar = exact(units[level], unit, ((1,), (1,)))
        coef = coef_ref[level * NDOC : (level + 1) * NDOC, :]
        high = coef.astype(BF).astype(F32)
        both = jnp.concatenate([high, coef - high], axis=0).astype(BF)
        spread = exact(hot[...], both, ((0,), (0,)))
        grad = (jnp.exp(similar * (1.0 / POOL_TEMP)) * spread).astype(BF)
        sums[level] += exact(grad, unit, ((1,), (0,)))
        grad_unit = jnp.transpose(exact(units_t[level], grad, ((1,), (0,))))
        total = total + level_back(grad_unit, part, scale)
    q_out[...] = total.astype(BF)

    @pl.when(step == pl.num_programs(0) - 1)
    def _():
        raw = d_ref[span:, :].astype(F32)
        result = jnp.zeros(raw.shape, F32)
        for level, parts in enumerate(cut_levels(raw, cuts)):
            lane = lax.broadcasted_iota(jnp.int32, raw.shape, 1)
            grad = jnp.where(lane < cuts[level], sums[level], 0.0)
            result = result + level_back(grad, parts[1], parts[2])
        d_out[...] = result


def pool_back(cuts, span, queries, row_embed, seg_row, coef):
    count, width = queries.shape
    tokens = row_embed.shape[0]
    docs = tokens - span
    whole = lambda shape: pl.BlockSpec(shape, lambda i: (0, 0))
    return pl.pallas_call(
        partial(pool_back_kernel, cuts, span),
        grid=(count // TILE,),
        in_specs=[
            pl.BlockSpec((TILE, width), lambda i: (i, 0)),
            whole((tokens, width)),
            whole((1, tokens)),
            pl.BlockSpec((len(cuts) * NDOC, TILE), lambda i: (0, i)),
        ],
        out_specs=[pl.BlockSpec((TILE, width), lambda i: (i, 0)), whole((docs, width))],
        out_shape=[
            jax.ShapeDtypeStruct((count, width), BF),
            jax.ShapeDtypeStruct((docs, width), F32),
        ],
        scratch_shapes=[
            pltpu.VMEM((len(cuts), docs, width), BF),
            pltpu.VMEM((len(cuts), width, docs), BF),
            pltpu.VMEM((2 * NDOC, docs), BF),
            pltpu.VMEM((len(cuts), docs, width), F32),
        ],
        compiler_params=pltpu.CompilerParams(vmem_limit_bytes=32 << 20),
        cost_estimate=pl.CostEstimate(
            flops=2 * len(cuts) * count * docs * 512,
            transcendentals=len(cuts) * count * docs,
            bytes_accessed=4 * (count + tokens) * width,
        ),
    )(queries, row_embed, seg_row, coef)


def local_chip(
    tokens,
    lengths,
    pairing,
    w_qkv,
    b_qv,
    w_out,
    b_out,
    ln_gain,
    ln_bias,
    w_up,
    b_up,
    w_down,
    b_down,
    w_proj,
    cot,
):
    z, x, c, y = (lax.axis_index(name) for name in ("z", "x", "c", "y"))
    chip = 4 * z + 2 * x + y
    token_count, width = tokens.shape
    share = token_count // 2
    own_start, other_start = c * share, (1 - c) * share
    gains, shifts = ln_gain.astype(F32), ln_bias.astype(F32)

    half_width = w_qkv.shape[2]
    up_wide = w_up.shape[1]
    chip_count = lengths.shape[0]
    half_queries = NQ_ROW // 2
    query_total = chip_count * half_queries
    qkv_rows = jnp.concatenate([w_qkv[0], w_qkv[1], w_qkv[2]], axis=1)
    pair_rows = jnp.pad(pairing.astype(BF), ((0, 63), (0, 128 - half_queries)))
    mid_rows = jnp.concatenate([w_up, w_out.T, pair_rows], axis=1)
    qkv_pair = gather_far(qkv_rows, z)
    mid_pair = gather_far(tie(mid_rows, qkv_pair), z)
    qkv_line = gather_near(qkv_pair, z)
    mid_line = gather_near(mid_pair, z)
    qkv_parts = gather_first(qkv_line, x, c, y)
    down_pair = gather_far(tie(w_down.T, mid_pair), z)
    full_qkv = gather_last(qkv_parts, x, c, y)
    mid_parts = gather_first(tie(mid_line, *qkv_parts), x, c, y)
    down_line = gather_near(down_pair, z)
    full_mid = gather_last(mid_parts, x, c, y)
    down_parts = gather_first(tie(down_line, *mid_parts), x, c, y)
    full_down = gather_last(down_parts, x, c, y)
    full_out = full_mid[:, up_wide : up_wide + half_width]
    pairs = full_mid[:, up_wide + half_width :].reshape(chip_count, 64, 128)
    pairs = pairs[:, 0, :half_queries].astype(jnp.int32).reshape(1, query_total)
    row = jnp.where(c == y, tokens, swap(tokens, "c"))
    bias = jnp.concatenate([b_qv.reshape(-1), b_up])[None].astype(F32)
    bias = jnp.where(c == y, bias, swap(bias, "y"))
    row_lengths = lax.dynamic_index_in_dim(lengths, chip, 0, keepdims=False)
    segments = segments_of(row_lengths, token_count)
    seg_col, seg_row = segments[:, None], segments[None, :]
    query_span = NQ_ROW * QLEN
    bounds = tile_bounds(row_lengths, token_count)
    qkv_bias = jnp.concatenate(
        [bias[:, :half_width], jnp.zeros_like(bias[:, :half_width]), bias[:, half_width : 2 * half_width]],
        axis=1,
    )
    qkv = (dot(row, full_qkv) + qkv_bias).astype(BF)
    mixed, lse = attend(bounds, qkv, seg_col, seg_row)
    own_cot = turn(tie(cot, qkv))

    def row_sum(left, weight_t, transposed):
        times = contract_cols if transposed else dot
        theirs = swap(times(left(1), weight_t).astype(BF), "c")
        return times(left(0), weight_t) + theirs.astype(F32)

    def mixed_half(which):
        return rows_of(mixed, other_start if which else own_start, share)

    attn_sum = row_sum(mixed_half, full_out, True)
    own_tokens = rows_of(row, own_start, share).astype(F32)
    normed, unit_one, rstd_one = norm_forward(
        own_tokens + attn_sum + b_out.astype(F32), gains[0], shifts[0]
    )
    normed_low = normed.astype(BF)
    normed_all = jnp.concatenate([normed_low, swap(normed_low, "c")], axis=0)
    activation, slope = expand(normed_all, full_mid, bias[:, 2 * half_width :])
    ffn_sum = row_sum(
        lambda which: activation[which * share : (which + 1) * share], full_down, True
    )
    result, unit_two, rstd_two = norm_forward(
        normed + ffn_sum + b_down.astype(F32), gains[1], shifts[1]
    )
    result_low = result.astype(BF)
    embed = dot(result_low, w_proj).astype(BF)

    other_embed = swap(embed, "c")
    row_embed = jnp.where(
        c == 0,
        jnp.concatenate([embed, other_embed], axis=0),
        jnp.concatenate([other_embed, embed], axis=0),
    )
    half_span = query_span // 2
    own_queries = rows_of(row_embed, c * half_span, half_span)
    chips = ("z", "x", "y")
    queries = lax.all_to_all(
        jnp.broadcast_to(own_queries[None], (chip_count,) + own_queries.shape), chips, 0, 0
    ).reshape(chip_count * half_span, -1)
    proj_width = w_proj.shape[1]
    cuts = (proj_width, 3 * proj_width // 4, proj_width // 2)
    sums = pool(cuts, query_span, queries, row_embed, seg_row)
    doc_sizes = jnp.tile(row_lengths.astype(F32), 3)[:, None]
    group = (
        jnp.arange(query_total * QLEN, dtype=jnp.int32)[:, None] // QLEN
        == jnp.arange(query_total, dtype=jnp.int32)[None, :]
    ).astype(F32)
    pooled = POOL_TEMP * jnp.log(sums / doc_sizes)
    logits = jnp.dot(pooled, group, precision=FULL_PRECISION) / LOSS_TEMP
    logits = logits.reshape(3, NDOC, query_total)
    doc_numbers = chip * NDOC + jnp.arange(NDOC, dtype=jnp.int32)
    picked = (doc_numbers[:, None] == pairs).astype(F32)
    own_high = jnp.max(logits, axis=1)
    own_lse = own_high + jnp.log(jnp.sum(jnp.exp(logits - own_high[:, None]), axis=1))
    own_target = jnp.sum(logits * picked, axis=1)
    notes = jnp.pad(jnp.concatenate([own_lse, own_target], axis=1), ((0, 5), (0, 0)))
    notes = lax.all_to_all(
        jnp.broadcast_to(notes[None], (chip_count,) + notes.shape), chips, 0, 0
    )
    chip_lse = notes[:, :3, :query_total]
    high = jnp.max(chip_lse, axis=0)
    all_lse = high + jnp.log(jnp.sum(jnp.exp(chip_lse - high), axis=0))
    target = jnp.sum(notes[:, :3, query_total:], axis=0)
    losses = jnp.sum(all_lse - target, axis=0).reshape(chip_count, half_queries)
    grad_logits = (jnp.exp(logits - all_lse[:, None]) - picked) / LOSS_TEMP
    coefficient = (
        lax.dot_general(
            grad_logits.reshape(3 * NDOC, query_total),
            group,
            (((1,), (1,)), ((), ())),
            precision=FULL_PRECISION,
        )
        / sums
    )
    losses = jnp.where(c == y, losses, swap(losses, "c"))
    loss_out = rows_of(losses, 4 * z + 2 * x + c, 1)
    query_grad, doc_grad = pool_back(cuts, query_span, queries, row_embed, seg_row, coefficient)
    grad_blocks = lax.all_to_all(
        query_grad.reshape(chip_count, half_span, proj_width), chips, 0, 0
    )
    own_query_grad = jnp.sum(grad_blocks.astype(F32), axis=0)
    row_grad = jnp.concatenate([jnp.zeros((query_span, proj_width), F32), doc_grad], axis=0)
    row_grad = lax.dynamic_update_slice_in_dim(row_grad, own_query_grad, c * half_span, 0)
    grad_embed = rows_of(row_grad, own_start, share) + swap(
        rows_of(row_grad, other_start, share), "c"
    )

    proj_low = w_proj
    grad_embed_low = grad_embed.astype(BF)
    grad_embed_rest = (grad_embed - grad_embed_low.astype(F32)).astype(BF)
    grad_result = own_cot.astype(F32) + (
        contract_cols(grad_embed_low, proj_low) + contract_cols(grad_embed_rest, proj_low)
    )
    proj_grad = contract_rows(result_low, grad_embed_low) + contract_rows(
        result_low, grad_embed_rest
    )
    gain_two = jnp.sum(grad_result * unit_two, axis=0)
    shift_two = jnp.sum(grad_result, axis=0)
    grad_second = norm_backward(grad_result, unit_two, rstd_two, gains[1])
    grad_ffn = grad_second.astype(BF)
    down_bias = jnp.sum(grad_ffn.astype(F32), axis=0)
    grad_ffn_all = jnp.concatenate([grad_ffn, swap(grad_ffn, "c")], axis=0)
    down_part = weight_sum(grad_ffn_all, activation, z, x, c, y)
    grad_up = (dot(grad_ffn_all, full_down) * slope.astype(F32)).astype(BF)
    up_bias = jnp.sum(grad_up.astype(F32), axis=0)
    up_part = weight_sum(normed_all, grad_up, z, x, c, y)
    full_up = full_mid[:, :up_wide]
    grad_normed = (
        row_sum(lambda which: grad_up[which * share : (which + 1) * share], full_up, True)
        + grad_second
    )
    gain_one = jnp.sum(grad_normed * unit_one, axis=0)
    shift_one = jnp.sum(grad_normed, axis=0)
    grad_first = norm_backward(grad_normed, unit_one, rstd_one, gains[0])
    grad_attn = grad_first.astype(BF)
    out_bias = jnp.sum(grad_attn.astype(F32), axis=0)
    other_attn = swap(grad_attn, "c")
    grad_attn_all = jnp.where(
        c == 0,
        jnp.concatenate([grad_attn, other_attn], axis=0),
        jnp.concatenate([other_attn, grad_attn], axis=0),
    )
    out_part = weight_sum(grad_attn_all, mixed, z, x, c, y)
    grad_mixed = dot(grad_attn_all, full_out).astype(BF)
    grads, grad_sums = attend_back(bounds, qkv, mixed, grad_mixed, lse, seg_col, seg_row)
    y_out = turn(tie(result_low, grads))
    qkv_part = weight_sum(row, grads, z, x, c, y)
    grad_input = turn(
        (
            row_sum(
                lambda which: rows_of(grads, other_start if which else own_start, share),
                full_qkv,
                True,
            )
            + grad_first
        ).astype(BF)
    )

    shared = jnp.stack([gain_one, gain_two, shift_one, shift_two, out_bias, down_bias])
    half_sums = jnp.concatenate(
        [grad_sums[:, 0].reshape(-1), grad_sums[:, 1].reshape(-1), up_bias]
    )
    small = jnp.concatenate([shared.reshape(-1), half_sums]).reshape(-1, 128)
    small = sum_chips(small, "xy01")
    other_small = swap(small, "c")
    shared_rows = 6 * width // 128
    shared = (small[:shared_rows] + other_small[:shared_rows]).reshape(6, width)
    half_sums = jnp.where(c == y, small[shared_rows:], other_small[shared_rows:]).reshape(-1)
    proj_half = rows_of(proj_grad, own_start, share) + swap(
        rows_of(proj_grad, other_start, share), "c"
    )
    for step in ("x", "y", "0", "1"):
        proj_half = proj_half + sum_other(proj_half.astype(BF), step).astype(F32)
    proj_sum = pair_up(proj_half, swap(proj_half, "c"), c, 0).reshape(width, -1)
    return (
        y_out,
        loss_out,
        grad_input,
        jnp.stack([qkv_part[:, k * half_width : (k + 1) * half_width] for k in range(3)]),
        half_sums[: 2 * half_width].reshape(2, half_width),
        out_part.T,
        shared[4],
        shared[0:2],
        shared[2:4],
        up_part,
        half_sums[2 * half_width :],
        down_part.T,
        shared[5],
        proj_sum,
    )


IN_SPECS = (
    P("dp", None),
    P(),
    P("dp", "tensor"),
    P(None, "dp", "tensor"),
    P(None, "tensor"),
    P("tensor", "dp"),
    P(),
    P(),
    P(),
    P("dp", "tensor"),
    P("tensor"),
    P("tensor", "dp"),
    P(),
    P(),
    P(("dp", "tensor"), None),
)
OUT_SPECS = (
    P(("dp", "tensor"), None),
    P("dp", "tensor"),
    P(("dp", "tensor"), None),
    P(None, "dp", "tensor"),
    P(None, "tensor"),
    P("tensor", "dp"),
    P(),
    P(),
    P(),
    P("dp", "tensor"),
    P("tensor"),
    P("tensor", "dp"),
    P(),
    P(),
)


def solution(mesh):
    if mesh.devices.shape != (16, 2):
        return jax.shard_map(
            local, mesh=mesh, in_specs=IN_SPECS, out_specs=OUT_SPECS, check_vma=False
        )
    names = {"dp": ("z", "x", "c"), "tensor": ("y",)}

    def respec(spec):
        parts = []
        for entry in spec:
            axes = () if entry is None else entry if isinstance(entry, tuple) else (entry,)
            parts.append(tuple(name for axis in axes for name in names[axis]) or None)
        return P(*parts)

    chips = Mesh(mesh.devices.reshape(4, 2, 2, 2), ("z", "x", "c", "y"))
    return jax.shard_map(
        local_chip,
        mesh=chips,
        in_specs=tuple(respec(spec) for spec in IN_SPECS),
        out_specs=tuple(respec(spec) for spec in OUT_SPECS),
        check_vma=False,
    )
```

```python
from functools import partial

import jax
import jax.numpy as jnp
from jax import lax
from jax.experimental import pallas as pl
from jax.experimental.pallas import tpu as pltpu
from jax.sharding import Mesh, PartitionSpec as P

HEAD_DIM = 64
QLEN = 32
NQ_ROW = 8
NDOC = 8


EPS_NORM = 1e-05
EPS_EMBED = 1e-06
POOL_TEMP = 0.1
LOSS_TEMP = 0.1
FULL_PRECISION = lax.Precision.HIGHEST
MASKED_SCORE = -1e30


def shortened(shard):

    def short(part):
        return part.astype(jnp.bfloat16) if part.dtype == jnp.float32 else part

    return jax.tree.map(short, shard)


def contract_rows(left, right, precision=None):
    return lax.dot_general(
        left,
        right,
        (((0,), (0,)), ((), ())),
        precision=precision,
        preferred_element_type=jnp.float32,
    )


def contract_cols(left, right, precision=None):
    return lax.dot_general(
        left,
        right,
        (((1,), (1,)), ((), ())),
        precision=precision,
        preferred_element_type=jnp.float32,
    )


def norm_forward(value, gain, shift):
    centred = value - jnp.mean(value, axis=1, keepdims=True)
    rstd = lax.rsqrt(jnp.mean(centred * centred, axis=1, keepdims=True) + EPS_NORM)
    unit = centred * rstd
    return (unit * gain + shift, unit, rstd)


def norm_backward(grad, unit, rstd, gain):
    scaled = grad * gain
    return rstd * (
        scaled
        - jnp.mean(scaled, axis=1, keepdims=True)
        - unit * jnp.mean(scaled * unit, axis=1, keepdims=True)
    )


def segments_of(row_lengths, token_count):
    position = jnp.arange(token_count, dtype=jnp.int32)
    query_span = NQ_ROW * QLEN
    ends = jnp.cumsum(row_lengths)
    passed = jnp.sum((position[:, None] - query_span >= ends[None, :]).astype(jnp.int32), axis=1)
    return jnp.where(position < query_span, position // QLEN, NQ_ROW + passed)


def normalize_cut(raw, width):
    part = raw[:, :width]
    scale = lax.rsqrt(jnp.sum(part * part, axis=1, keepdims=True) + EPS_EMBED)
    return (part * scale, part, scale)


def normalize_back(grad, part, scale, full_width):
    result = scale * grad - part * (scale * scale * scale) * jnp.sum(
        part * grad, axis=1, keepdims=True
    )
    return jnp.pad(result, ((0, 0), (0, full_width - grad.shape[1])))


def masked_scores(query_block, key_rows, block_segments, segments):
    scores = jnp.einsum(
        "qhd,khd->hqk", query_block, key_rows, preferred_element_type=jnp.float32
    ) * HEAD_DIM ** (-0.5)
    return jnp.where((block_segments[:, None] == segments[None, :])[None], scores, MASKED_SCORE)


def attend_forward(query_rows, key_rows, value_rows, segments, block_rows):
    token_count = query_rows.shape[0]

    def one_block(block_start):
        query_block = lax.dynamic_slice_in_dim(query_rows, block_start, block_rows, 0)
        block_segments = lax.dynamic_slice_in_dim(segments, block_start, block_rows, 0)
        scores = masked_scores(query_block, key_rows, block_segments, segments)
        highest = jnp.max(scores, axis=2, keepdims=True)
        expo = jnp.exp(scores - highest)
        totals = jnp.sum(expo, axis=2, keepdims=True)
        weights = (expo / totals).astype(jnp.bfloat16)
        mixed = jnp.einsum("hqk,khd->qhd", weights, value_rows, preferred_element_type=jnp.float32)
        return (mixed.astype(jnp.bfloat16), (highest + jnp.log(totals))[:, :, 0])

    starts = jnp.arange(token_count // block_rows, dtype=jnp.int32) * block_rows
    mixed, log_totals = lax.map(one_block, starts)
    return (mixed.reshape(token_count, -1), log_totals)


def attend_backward(query_rows, key_rows, value_rows, segments, log_totals, grad_mixed, block_rows):
    token_count, local_heads, head_size = query_rows.shape
    scale = HEAD_DIM ** (-0.5)
    grad_heads = grad_mixed.reshape(token_count, local_heads, head_size)

    def one_block(carried, inputs):
        grad_keys, grad_values = carried
        block_start, block_lse = inputs
        query_block = lax.dynamic_slice_in_dim(query_rows, block_start, block_rows, 0)
        grad_block = lax.dynamic_slice_in_dim(grad_heads, block_start, block_rows, 0)
        block_segments = lax.dynamic_slice_in_dim(segments, block_start, block_rows, 0)
        scores = masked_scores(query_block, key_rows, block_segments, segments)
        probs = jnp.exp(scores - block_lse[:, :, None])
        grad_probs = jnp.einsum(
            "qhd,khd->hqk", grad_block, value_rows, preferred_element_type=jnp.float32
        )
        inner = jnp.sum(probs * grad_probs, axis=2, keepdims=True)
        grad_scores = (probs * (grad_probs - inner)).astype(jnp.bfloat16)
        grad_query = (
            jnp.einsum("hqk,khd->qhd", grad_scores, key_rows, preferred_element_type=jnp.float32)
            * scale
        )
        grad_keys = (
            grad_keys
            + jnp.einsum(
                "hqk,qhd->khd", grad_scores, query_block, preferred_element_type=jnp.float32
            )
            * scale
        )
        grad_values = grad_values + jnp.einsum(
            "hqk,qhd->khd",
            probs.astype(jnp.bfloat16),
            grad_block,
            preferred_element_type=jnp.float32,
        )
        return ((grad_keys, grad_values), grad_query)

    starts = jnp.arange(token_count // block_rows, dtype=jnp.int32) * block_rows
    zero_rows = jnp.zeros(key_rows.shape, jnp.float32)
    (grad_keys, grad_values), grad_queries = lax.scan(
        one_block, (zero_rows, zero_rows), (starts, log_totals)
    )
    flat_width = local_heads * head_size
    return (
        grad_queries.reshape(token_count, flat_width),
        grad_keys.reshape(token_count, flat_width),
        grad_values.reshape(token_count, flat_width),
    )


def local(
    tokens,
    lengths,
    pairing,
    w_qkv,
    b_qv,
    w_out,
    b_out,
    ln_gain,
    ln_bias,
    w_up,
    b_up,
    w_down,
    b_down,
    w_proj,
    cot,
):
    tensor_count = lax.axis_size("tensor")
    tensor_index = lax.axis_index("tensor")
    data_index = lax.axis_index("dp")
    token_count = tokens.shape[0]
    share_rows = token_count // tensor_count
    block_rows = min(512, token_count)
    own_start = tensor_index * share_rows
    full_qkv, full_out, full_up, full_down = (
        lax.all_gather(w_qkv, "dp", axis=1, tiled=True),
        lax.all_gather(w_out, "dp", axis=1, tiled=True),
        lax.all_gather(w_up, "dp", axis=0, tiled=True),
        lax.all_gather(w_down, "dp", axis=1, tiled=True),
    )
    head_width = full_qkv.shape[2]
    local_heads = head_width // HEAD_DIM
    row_lengths = lax.dynamic_index_in_dim(lengths, data_index, 0, keepdims=False)
    segments = segments_of(row_lengths, token_count)
    projected = jnp.einsum("td,kdw->ktw", tokens, full_qkv, preferred_element_type=jnp.float32)
    qv_bias = b_qv.astype(jnp.float32)
    query_rows = (
        (projected[0] + qv_bias[0]).astype(jnp.bfloat16).reshape(token_count, local_heads, HEAD_DIM)
    )
    key_rows = projected[1].astype(jnp.bfloat16).reshape(token_count, local_heads, HEAD_DIM)
    value_rows = (
        (projected[2] + qv_bias[1]).astype(jnp.bfloat16).reshape(token_count, local_heads, HEAD_DIM)
    )
    mixed, log_totals = attend_forward(query_rows, key_rows, value_rows, segments, block_rows)
    attn_terms = jnp.dot(mixed, full_out, preferred_element_type=jnp.float32)
    attn_sum = lax.psum_scatter(
        attn_terms.astype(jnp.bfloat16), "tensor", scatter_dimension=0, tiled=True
    ).astype(jnp.float32)
    own_tokens = lax.dynamic_slice_in_dim(tokens, own_start, share_rows, 0).astype(jnp.float32)
    gains = ln_gain.astype(jnp.float32)
    shifts = ln_bias.astype(jnp.float32)
    normed, unit_one, rstd_one = norm_forward(
        own_tokens + attn_sum + b_out.astype(jnp.float32), gains[0], shifts[0]
    )
    normed_all = lax.all_gather(normed.astype(jnp.bfloat16), "tensor", axis=0, tiled=True)
    up_value = jnp.dot(normed_all, full_up, preferred_element_type=jnp.float32) + b_up.astype(
        jnp.float32
    )
    activation = jax.nn.gelu(up_value, approximate=False).astype(jnp.bfloat16)
    ffn_terms = jnp.dot(activation, full_down, preferred_element_type=jnp.float32)
    ffn_sum = lax.psum_scatter(
        ffn_terms.astype(jnp.bfloat16), "tensor", scatter_dimension=0, tiled=True
    ).astype(jnp.float32)
    result, unit_two, rstd_two = norm_forward(
        normed + ffn_sum + b_down.astype(jnp.float32), gains[1], shifts[1]
    )
    result_low = result.astype(jnp.bfloat16)
    embed = jnp.dot(result_low, w_proj, preferred_element_type=jnp.float32).astype(jnp.bfloat16)
    embed_all = lax.all_gather(embed, ("dp", "tensor"), axis=0, tiled=True)
    row_count = lengths.shape[0]
    proj_width = w_proj.shape[1]
    widths = (proj_width, 3 * proj_width // 4, proj_width // 2)
    per_device = pairing.shape[1]
    query_count = per_device * QLEN
    query_span = NQ_ROW * QLEN
    emb_rows = embed_all.reshape(row_count, token_count, proj_width)
    my_row = lax.dynamic_index_in_dim(emb_rows, data_index, 0, keepdims=False)
    query_raw = lax.dynamic_slice_in_dim(my_row, tensor_index * query_count, query_count, 0).astype(
        jnp.float32
    )
    query_levels = [normalize_cut(query_raw, width) for width in widths]
    query_units = [level_parts[0].astype(jnp.bfloat16) for level_parts in query_levels]
    doc_numbers = jnp.arange(NDOC, dtype=jnp.int32)

    def row_pool(carried, inputs):
        row_emb, lengths_row = inputs
        row_hot = (
            segments_of(lengths_row, token_count)[:, None] == NQ_ROW + doc_numbers[None, :]
        ).astype(jnp.float32)
        row_raw = row_emb.astype(jnp.float32)
        pooled_list = []
        sums_list = []
        for width, query_unit in zip(widths, query_units):
            doc_unit = normalize_cut(row_raw, width)[0].astype(jnp.bfloat16)
            expo = jnp.exp(contract_cols(query_unit, doc_unit) / POOL_TEMP)
            sums = jnp.dot(expo, row_hot, precision=FULL_PRECISION)
            pooled = POOL_TEMP * jnp.log(sums / lengths_row.astype(jnp.float32))
            pooled_list.append(jnp.sum(pooled.reshape(per_device, QLEN, NDOC), axis=1))
            sums_list.append(sums)
        return (carried, (jnp.stack(pooled_list), jnp.stack(sums_list)))

    _, (row_scores, row_sums) = lax.scan(row_pool, 0, (emb_rows, lengths))
    logits = (
        jnp.transpose(row_scores, (2, 1, 0, 3)).reshape(per_device, 3, row_count * NDOC) / LOSS_TEMP
    )
    own_pairs = pairing[0]
    target = jnp.take_along_axis(
        logits, jnp.broadcast_to(own_pairs[:, None, None], (per_device, 3, 1)), axis=2
    )[:, :, 0]
    loss_out = jnp.sum(jax.nn.logsumexp(logits, axis=2) - target, axis=1).reshape(1, per_device)
    picked = (
        jnp.arange(row_count * NDOC, dtype=jnp.int32)[None, None, :] == own_pairs[:, None, None]
    ).astype(jnp.float32)
    grad_logits = (jax.nn.softmax(logits, axis=2) - picked) / LOSS_TEMP
    grad_rows = jnp.transpose(grad_logits.reshape(per_device, 3, row_count, NDOC), (2, 1, 0, 3))
    coefficient = jnp.repeat(grad_rows, QLEN, axis=2) / row_sums

    def row_back(carried, inputs):
        row_emb, lengths_row, row_coef = inputs
        row_hot = (
            segments_of(lengths_row, token_count)[:, None] == NQ_ROW + doc_numbers[None, :]
        ).astype(jnp.float32)
        row_raw = row_emb.astype(jnp.float32)
        new_carried = []
        row_grad = jnp.zeros((token_count, proj_width), jnp.float32)
        for level_index in range(3):
            width = widths[level_index]
            doc_unit_f, doc_part, doc_scale = normalize_cut(row_raw, width)
            doc_unit = doc_unit_f.astype(jnp.bfloat16)
            expo = jnp.exp(contract_cols(query_units[level_index], doc_unit) / POOL_TEMP)
            spread = contract_cols(row_coef[level_index], row_hot, FULL_PRECISION)
            grad_sim = (expo * spread).astype(jnp.bfloat16)
            new_carried.append(
                carried[level_index]
                + jnp.dot(grad_sim, doc_unit, preferred_element_type=jnp.float32)
            )
        return (tuple(new_carried), row_grad)

    zero_query = tuple((jnp.zeros((query_count, width), jnp.float32) for width in widths))
    query_grads, doc_grads = lax.scan(row_back, zero_query, (emb_rows, lengths, coefficient))
    grad_query = jnp.zeros((query_count, proj_width), jnp.float32)
    for level_index in range(3):
        level_parts = query_levels[level_index]
        grad_query = grad_query + normalize_back(
            query_grads[level_index], level_parts[1], level_parts[2], proj_width
        )
    coef_mine = jnp.transpose(coefficient, (2, 1, 0, 3)).reshape(query_count, 3, row_count * NDOC)
    coef_all, grad_query_all = (
        lax.all_gather(shortened(coef_mine), ("dp", "tensor"), axis=0, tiled=True).astype(
            coef_mine.dtype
        ),
        lax.all_gather(
            grad_query.astype(jnp.bfloat16), ("dp", "tensor"), axis=0, tiled=True
        ).astype(grad_query.dtype),
    )
    own_raw = embed.astype(jnp.float32)
    own_segments = lax.dynamic_slice_in_dim(segments, own_start, share_rows, 0)
    own_docs = jnp.where(own_segments >= NQ_ROW, data_index * NDOC + own_segments - NQ_ROW, -1)
    own_hot = (own_docs[:, None] == jnp.arange(row_count * NDOC, dtype=jnp.int32)[None, :]).astype(
        jnp.float32
    )
    queries_all = (
        emb_rows[:, :query_span].reshape(row_count * query_span, proj_width).astype(jnp.float32)
    )
    grad_embed = jnp.zeros((share_rows, proj_width), jnp.float32)
    for level_index in range(3):
        width = widths[level_index]
        query_unit_all = normalize_cut(queries_all, width)[0].astype(jnp.bfloat16)
        doc_unit_f, doc_part, doc_scale = normalize_cut(own_raw, width)
        expo = jnp.exp(contract_cols(query_unit_all, doc_unit_f.astype(jnp.bfloat16)) / POOL_TEMP)
        spread = contract_cols(coef_all[:, level_index], own_hot, FULL_PRECISION)
        grad_sim = (expo * spread).astype(jnp.bfloat16)
        grad_doc = contract_rows(grad_sim, query_unit_all)
        grad_embed = grad_embed + normalize_back(grad_doc, doc_part, doc_scale, proj_width)
    row_query_grads = lax.dynamic_slice_in_dim(
        grad_query_all, data_index * query_span, query_span, 0
    )
    padded = jnp.pad(row_query_grads, ((0, token_count - query_span), (0, 0)))
    grad_embed = grad_embed + lax.dynamic_slice_in_dim(padded, own_start, share_rows, 0)
    proj_float = w_proj.astype(jnp.float32)
    grad_result = cot.astype(jnp.float32) + contract_cols(grad_embed, proj_float, FULL_PRECISION)
    proj_grad = contract_rows(result_low.astype(jnp.float32), grad_embed, FULL_PRECISION)
    gain_two = jnp.sum(grad_result * unit_two, axis=0)
    shift_two = jnp.sum(grad_result, axis=0)
    grad_second = norm_backward(grad_result, unit_two, rstd_two, gains[1])
    grad_ffn = grad_second.astype(jnp.bfloat16)
    down_bias = jnp.sum(grad_ffn.astype(jnp.float32), axis=0)
    grad_ffn_all = lax.all_gather(grad_ffn, "tensor", axis=0, tiled=True)
    grad_act = contract_cols(grad_ffn_all, full_down)
    down_grad = contract_rows(activation, grad_ffn_all)
    _, gelu_pull = jax.vjp(partial(jax.nn.gelu, approximate=False), up_value)
    grad_up = gelu_pull(grad_act)[0].astype(jnp.bfloat16)
    up_bias = jnp.sum(grad_up.astype(jnp.float32), axis=0)
    up_grad = contract_rows(normed_all, grad_up)
    normed_terms = contract_cols(grad_up, full_up)
    grad_normed = (
        lax.psum_scatter(
            normed_terms.astype(jnp.bfloat16), "tensor", scatter_dimension=0, tiled=True
        ).astype(jnp.float32)
        + grad_second
    )
    gain_one = jnp.sum(grad_normed * unit_one, axis=0)
    shift_one = jnp.sum(grad_normed, axis=0)
    grad_first = norm_backward(grad_normed, unit_one, rstd_one, gains[0])
    grad_attn = grad_first.astype(jnp.bfloat16)
    out_bias = jnp.sum(grad_attn.astype(jnp.float32), axis=0)
    grad_attn_all = lax.all_gather(grad_attn, "tensor", axis=0, tiled=True)
    out_grad = contract_rows(mixed, grad_attn_all)
    grad_mixed = contract_cols(grad_attn_all, full_out).astype(jnp.bfloat16)
    grad_q, grad_k, grad_v = attend_backward(
        query_rows, key_rows, value_rows, segments, log_totals, grad_mixed, block_rows
    )
    stacked_grads = jnp.stack(
        [grad_q.astype(jnp.bfloat16), grad_k.astype(jnp.bfloat16), grad_v.astype(jnp.bfloat16)]
    )
    qkv_grad = jnp.einsum("td,ktw->kdw", tokens, stacked_grads, preferred_element_type=jnp.float32)
    input_terms = jnp.einsum(
        "ktw,kdw->td", stacked_grads, full_qkv, preferred_element_type=jnp.float32
    )
    grad_input = (
        lax.psum_scatter(
            input_terms.astype(jnp.bfloat16), "tensor", scatter_dimension=0, tiled=True
        ).astype(jnp.float32)
        + grad_first
    )
    qv_grad = jnp.stack(
        [
            jnp.sum(stacked_grads[0].astype(jnp.float32), axis=0),
            jnp.sum(stacked_grads[2].astype(jnp.float32), axis=0),
        ]
    )
    qkv_part, out_part, up_part, down_part = (
        lax.psum_scatter(
            qkv_grad.astype(jnp.bfloat16), "dp", scatter_dimension=1, tiled=True
        ).astype(jnp.float32),
        lax.psum_scatter(
            out_grad.astype(jnp.bfloat16), "dp", scatter_dimension=1, tiled=True
        ).astype(jnp.float32),
        lax.psum_scatter(
            up_grad.astype(jnp.bfloat16), "dp", scatter_dimension=0, tiled=True
        ).astype(jnp.float32),
        lax.psum_scatter(
            down_grad.astype(jnp.bfloat16), "dp", scatter_dimension=1, tiled=True
        ).astype(jnp.float32),
    )
    gain_sum, shift_sum, out_bias_sum, down_bias_sum, proj_sum = lax.psum(
        (
            jnp.stack([gain_one, gain_two]),
            jnp.stack([shift_one, shift_two]),
            out_bias,
            down_bias,
            proj_grad,
        ),
        ("dp", "tensor"),
    )
    qv_sum, up_bias_sum = lax.psum((qv_grad, up_bias), "dp")
    return (
        result_low,
        loss_out,
        grad_input.astype(jnp.bfloat16),
        qkv_part,
        qv_sum,
        out_part,
        out_bias_sum,
        gain_sum,
        shift_sum,
        up_part,
        up_bias_sum,
        down_part,
        down_bias_sum,
        proj_sum,
    )


SWAP = [(0, 1), (1, 0)]
TURN = [(0, 0), (1, 2), (2, 1), (3, 3)]
FAR = [(0, 3), (3, 0), (1, 2), (2, 1)]
NEAR = [(0, 1), (1, 0), (2, 3), (3, 2)]
BF = jnp.bfloat16
F32 = jnp.float32


def dot(left, right):
    return jnp.dot(left, right, preferred_element_type=F32)


INTO_CORE = [(2, 0), (1, 3), (0, 1), (3, 2)]
OUT_OF_CORE = [(0, 2), (3, 1), (1, 0), (2, 3)]
CROSS = [(2, 1), (1, 2)]
CORES = ("c", "y")


def tie(value, *others):
    return lax.optimization_barrier((value,) + others)[0]


def exchange(*moves):
    return lax.optimization_barrier(
        tuple(lax.ppermute(value, axis, steps) for value, axis, steps in moves)
    )


def turn(value):
    return lax.ppermute(value, CORES, TURN)


def swap(value, axis):
    return lax.ppermute(value, axis, SWAP)


def pair_up(first, second, own_index, axis):
    return jnp.where(
        own_index == 0, jnp.stack([first, second], axis), jnp.stack([second, first], axis)
    )


def pair_core(value, got, cross, c, y, axis):
    first = jnp.where(c == y, value, got)
    second = jnp.where(c == y, got, cross)
    return pair_up(first, second, c, axis)


def far_pair(value, far, z):
    return jnp.where(z < 2, jnp.stack([value, far]), jnp.stack([far, value]))


def whole_line(pair, other, z):
    return jnp.where(
        (z == 0) | (z == 3),
        jnp.stack([pair[0], other[0], other[1], pair[1]]),
        jnp.stack([other[0], pair[0], pair[1], other[1]]),
    )


def first_moves(line):
    half = line.shape[1] // 2
    low, high = line[:, :half], line[:, half:]
    return ((low, "x", SWAP), (high, CORES, INTO_CORE), (high, CORES, CROSS))


def first_parts(line, moved, x, c, y):
    half = line.shape[1] // 2
    return (
        pair_up(line[:, :half], moved[0], x, 1),
        pair_core(line[:, half:], moved[1], moved[2], c, y, 1),
    )


def last_moves(parts):
    return ((parts[1], "x", SWAP), (parts[0], CORES, INTO_CORE), (parts[0], CORES, CROSS))


def full_rows(parts, moved, x, c, y):
    low = pair_core(parts[0], moved[1], moved[2], c, y, 2)
    high = pair_up(parts[1], moved[0], x, 1)
    return jnp.concatenate([low, high], axis=3).reshape(-1, low.shape[-1])


def at(blocks, index, axis):
    return lax.dynamic_index_in_dim(blocks, index, axis, keepdims=False)


def core_moves(blocks, c, y):
    axis = blocks.ndim - 3
    mine, other = at(blocks, c, axis), at(blocks, 1 - c, axis)
    given = jnp.where(c == y, other, mine).astype(BF)
    return ((given, CORES, OUT_OF_CORE), (other.astype(BF), CORES, CROSS))


def core_sum(blocks, got, cross, c, y):
    mine = at(blocks, c, blocks.ndim - 3)
    return got.astype(F32) + jnp.where(c == y, mine.astype(F32), cross.astype(F32))


def x_move(blocks, x):
    return (at(blocks, 1 - x, 1).astype(BF), "x", SWAP)


def x_sum(blocks, got, x):
    return at(blocks, x, 1).astype(F32) + got.astype(F32)


def near_move(line, z):
    ends = (z == 0) | (z == 3)
    outer, inner = jnp.stack([line[0], line[3]]), line[1:3]
    return (jnp.where(ends, inner, outer).astype(BF), "z", NEAR)


def near_sum(line, got, z):
    ends = (z == 0) | (z == 3)
    return jnp.where(ends, jnp.stack([line[0], line[3]]), line[1:3]) + got.astype(F32)


def far_move(pair, z):
    return (jnp.where(z < 2, pair[1], pair[0]).astype(BF), "z", FAR)


def far_sum(pair, got, z):
    return jnp.where(z < 2, pair[0], pair[1]) + got.astype(F32)


def blocks_of(left, right):
    return contract_rows(left, right).astype(BF).reshape(4, 2, 2, 64, right.shape[1])


def sum_moves(blocks, x, c, y):
    return (x_move(blocks[..., :32, :], x),) + core_moves(blocks[..., 32:, :], c, y)


def sum_parts(blocks, moved, x, c, y):
    return (
        x_sum(blocks[..., :32, :], moved[0], x),
        core_sum(blocks[..., 32:, :], moved[1], moved[2], c, y),
    )


def line_moves(parts, x, c, y):
    return (x_move(parts[1], x),) + core_moves(parts[0], c, y)


def line_of(parts, moved, x, c, y):
    return jnp.concatenate(
        [core_sum(parts[0], moved[1], moved[2], c, y), x_sum(parts[1], moved[0], x)], axis=1
    )


def tile_bounds(row_lengths, token_count):
    ends = jnp.cumsum(row_lengths)
    span = NQ_ROW * QLEN
    first = jnp.arange(token_count // TILE, dtype=jnp.int32) * TILE - span
    last = first + TILE - 1
    begin = jnp.max(jnp.where(ends[None, :] <= first[:, None], ends[None, :], 0), axis=1)
    end = jnp.min(jnp.where(ends[None, :] > last[:, None], ends[None, :], token_count), axis=1)
    low = jnp.where(first < 0, 0, (begin + span) // TILE)
    high = jnp.where(first < 0, 1, (end + span + TILE - 1) // TILE)
    return jnp.stack([low, high]).astype(jnp.int32)


def rows_of(value, start, count):
    return lax.dynamic_slice_in_dim(value, start, count, 0)


TILE = 256
NEG = -1e30


def exact(left, right, dims):
    return lax.dot_general(left, right, (dims, ((), ())), preferred_element_type=F32)


def head_masks(value):
    lane = lax.broadcasted_iota(jnp.int32, value.shape, 1)
    zero = jnp.zeros_like(value)
    return (jnp.where(lane < HEAD_DIM, value, zero), jnp.where(lane < HEAD_DIM, zero, value))


def fill_bias(seg_col, seg_row, bias):
    for start in range(0, bias.shape[0], TILE):
        rows = slice(start, start + TILE)
        bias[rows, :] = jnp.where(seg_col[rows, :] == seg_row[...], 0.0, NEG)


def attend_kernel(bounds, q_ref, k_ref, v_ref, seg_col, seg_row, out_ref, lse_ref, bias, held):
    @pl.when(pl.program_id(0) == 0)
    def _():
        fill_bias(seg_col, seg_row, bias)

    for block in range(q_ref.shape[0] // TILE):
        own = slice(block * TILE, (block + 1) * TILE)
        queries = head_masks(q_ref[own, :] * HEAD_DIM**-0.5)

        def score(step, highest):
            rows = pl.ds(pl.multiple_of(step * TILE, TILE), TILE)
            keys, shift = k_ref[rows, :], bias[rows, own]
            fresh = []
            for head in range(2):
                scores = exact(keys, queries[head], ((1,), (1,))) + shift
                held[head, rows, :] = scores
                fresh.append(jnp.maximum(highest[head], jnp.max(scores, axis=0, keepdims=True)))
            return tuple(fresh)

        low = jnp.full((1, TILE), NEG, F32)
        highest = lax.fori_loop(bounds[0, block], bounds[1, block], score, (low, low))

        def mix(step, carried):
            rows = pl.ds(pl.multiple_of(step * TILE, TILE), TILE)
            values = v_ref[rows, :]
            fresh = []
            for head in range(2):
                total, mixed = carried[head]
                expo = jnp.exp(held[head, rows, :] - highest[head])
                fresh.append(
                    (
                        total + jnp.sum(expo, axis=0, keepdims=True),
                        mixed + exact(values, expo.astype(BF), ((0,), (0,))),
                    )
                )
            return tuple(fresh)

        start = (jnp.zeros((1, TILE), F32), jnp.zeros((2 * HEAD_DIM, TILE), F32))
        parts = lax.fori_loop(bounds[0, block], bounds[1, block], mix, (start, start))
        mixed = jnp.concatenate(
            [parts[0][1][:HEAD_DIM] / parts[0][0], parts[1][1][HEAD_DIM:] / parts[1][0]], axis=0
        )
        out_ref[own, :] = jnp.transpose(mixed).astype(BF)
        for head in range(2):
            lse_ref[0, head : head + 1, own] = highest[head] + jnp.log(parts[head][0])


def attend(bounds, qkv, seg_col, seg_row):
    count, wide = qkv.shape
    pairs = wide // 3 // 128
    group = pairs // 2
    column = lambda part: pl.BlockSpec(
        (count, 128), lambda i: (0, (i // group) * 3 * group + part * group + i % group)
    )
    mixed_column = pl.BlockSpec((count, 128), lambda i: (0, i))
    whole = lambda shape: pl.BlockSpec(shape, lambda i: (0, 0))
    return pl.pallas_call(
        attend_kernel,
        grid=(pairs,),
        in_specs=[
            pl.BlockSpec(memory_space=pltpu.SMEM),
            column(0),
            column(1),
            column(2),
            whole((count, 1)),
            whole((1, count)),
        ],
        out_specs=[mixed_column, pl.BlockSpec((1, 8, count), lambda i: (i, 0, 0))],
        out_shape=[
            jax.ShapeDtypeStruct((count, wide // 3), BF),
            jax.ShapeDtypeStruct((pairs, 8, count), F32),
        ],
        scratch_shapes=[pltpu.VMEM((count, count), F32), pltpu.VMEM((2, count, TILE), F32)],
        compiler_params=pltpu.CompilerParams(vmem_limit_bytes=40 << 20),
        cost_estimate=pl.CostEstimate(
            flops=4 * pairs * count * count * 128,
            transcendentals=pairs * count * count,
            bytes_accessed=4 * count * wide * 2,
        ),
    )(bounds, qkv, qkv, qkv, seg_col, seg_row)


def attend_back_kernel(
    bounds, q_ref, k_ref, v_ref, out_ref, grad_ref, lse_ref, seg_col, seg_row,
    grads_ref, sums_ref, bias, key_sum, value_sum,
):
    pair = pl.program_id(0)

    @pl.when(pair == 0)
    def _():
        fill_bias(seg_col, seg_row, bias)

    key_sum[...] = jnp.zeros_like(key_sum)
    value_sum[...] = jnp.zeros_like(value_sum)
    columns = [
        pl.ds(pl.multiple_of(part * (grads_ref.shape[1] // 3) + pair * 128, 128), 128) for part in range(3)
    ]
    query_total = jnp.zeros((1, 128), F32)
    picks = head_masks(jnp.ones((8, 128), BF))
    for block in range(q_ref.shape[0] // TILE):
        own = slice(block * TILE, (block + 1) * TILE)
        queries = head_masks(q_ref[own, :] * HEAD_DIM**-0.5)
        grads = head_masks(grad_ref[own, :])
        product = grad_ref[own, :].astype(F32) * out_ref[own, :].astype(F32)
        product_high = product.astype(BF)
        product_low = (product - product_high.astype(F32)).astype(BF)
        inner = [
            (
                exact(picks[head], product_high, ((1,), (1,)))
                + exact(picks[head], product_low, ((1,), (1,)))
            )[0:1]
            for head in range(2)
        ]
        lse = [lse_ref[0, head : head + 1, own] for head in range(2)]

        def step_of(step, carried):
            rows = pl.ds(pl.multiple_of(step * TILE, TILE), TILE)
            keys, values, shift = k_ref[rows, :], v_ref[rows, :], bias[rows, own]
            fresh = []
            key_add = jnp.zeros((TILE, 128), F32)
            value_add = jnp.zeros((TILE, 128), F32)
            for head in range(2):
                scores = exact(keys, queries[head], ((1,), (1,))) + shift
                probs = jnp.exp(scores - lse[head])
                grad_probs = exact(values, grads[head], ((1,), (1,)))
                grad_scores = (probs * (grad_probs - inner[head])).astype(BF)
                value_add = value_add + exact(probs.astype(BF), grads[head], ((1,), (0,)))
                key_add = key_add + exact(grad_scores, queries[head], ((1,), (0,)))
                fresh.append(carried[head] + exact(keys, grad_scores, ((0,), (0,))))
            key_sum[rows, :] += key_add
            value_sum[rows, :] += value_add
            return tuple(fresh)

        start = jnp.zeros((2 * HEAD_DIM, TILE), F32)
        parts = lax.fori_loop(bounds[0, block], bounds[1, block], step_of, (start, start))
        grad_query = jnp.concatenate([parts[0][:HEAD_DIM], parts[1][HEAD_DIM:]], axis=0)
        grad_query = jnp.transpose(grad_query * HEAD_DIM**-0.5).astype(BF)
        grads_ref[own, columns[0]] = grad_query
        query_total = query_total + jnp.sum(grad_query.astype(F32), axis=0, keepdims=True)
    grad_value = value_sum[...].astype(BF)
    grads_ref[:, columns[1]] = key_sum[...].astype(BF)
    grads_ref[:, columns[2]] = grad_value
    sums_ref[0, 0:1, :] = query_total
    sums_ref[0, 1:2, :] = jnp.sum(grad_value.astype(F32), axis=0, keepdims=True)


def attend_back(bounds, group, qkv, mixed, grad_mixed, lse, seg_col, seg_row):
    count = qkv.shape[0]
    wide = qkv.shape[1] // 2
    pairs = wide // 3 // 128
    column = lambda shift: pl.BlockSpec((count, 128), lambda i: (0, shift + i))
    whole = lambda shape: pl.BlockSpec(shape, lambda i: (0, 0))
    first = group * pairs
    return pl.pallas_call(
        attend_back_kernel,
        grid=(pairs,),
        in_specs=[
            pl.BlockSpec(memory_space=pltpu.SMEM),
            column(3 * first),
            column(3 * first + pairs),
            column(3 * first + 2 * pairs),
            column(first),
            column(first),
            pl.BlockSpec((1, 8, count), lambda i: (first + i, 0, 0)),
            whole((count, 1)),
            whole((1, count)),
        ],
        out_specs=[whole((count, wide)), pl.BlockSpec((1, 8, 128), lambda i: (i, 0, 0))],
        out_shape=[
            jax.ShapeDtypeStruct((count, wide), BF),
            jax.ShapeDtypeStruct((pairs, 8, 128), F32),
        ],
        scratch_shapes=[
            pltpu.VMEM((count, count), F32),
            pltpu.VMEM((count, 128), F32),
            pltpu.VMEM((count, 128), F32),
        ],
        compiler_params=pltpu.CompilerParams(vmem_limit_bytes=40 << 20),
        cost_estimate=pl.CostEstimate(
            flops=10 * pairs * count * count * 128,
            transcendentals=pairs * count * count,
            bytes_accessed=8 * count * wide * 2,
        ),
    )(bounds, qkv, qkv, qkv, mixed, grad_mixed, lse, seg_col, seg_row)


ERFC = (
    -1.26551223, 1.00002368, 0.37409196, 0.09678418, -0.18628806,
    0.27886807, -1.13520398, 1.48851587, -0.82215223, 0.17087277,
)


def gelu_pair(value):
    size = jnp.abs(value) * 0.5**0.5
    ratio = 1.0 / (1.0 + 0.5 * size)
    series = jnp.full_like(value, ERFC[-1])
    for factor in ERFC[-2::-1]:
        series = series * ratio + factor
    bell = jnp.exp(-size * size)
    tail = 0.5 * ratio * bell * jnp.exp(series)
    phi = jnp.where(value < 0.0, tail, 1.0 - tail)
    return (value * phi, phi + value * bell * 0.3989422804014327)


def expand_kernel(x_ref, w_ref, b_ref, act_ref, slope_ref):
    rows = 256
    for start in range(0, x_ref.shape[0], rows):
        part = slice(start, start + rows)
        value = exact(x_ref[part, :], w_ref[...], ((1,), (0,))) + b_ref[...]
        active, slope = gelu_pair(value)
        act_ref[part, :] = active.astype(BF)
        slope_ref[part, :] = slope.astype(BF)


def expand(value, weight, shift):
    count, depth = value.shape
    width = shift.shape[1]
    tile = 256
    return pl.pallas_call(
        expand_kernel,
        grid=(width // tile,),
        in_specs=[
            pl.BlockSpec((count, depth), lambda i: (0, 0)),
            pl.BlockSpec((depth, tile), lambda i: (0, i)),
            pl.BlockSpec((1, tile), lambda i: (0, i)),
        ],
        out_specs=[pl.BlockSpec((count, tile), lambda i: (0, i))] * 2,
        out_shape=[jax.ShapeDtypeStruct((count, width), BF)] * 2,
        compiler_params=pltpu.CompilerParams(vmem_limit_bytes=32 << 20),
        cost_estimate=pl.CostEstimate(
            flops=2 * count * depth * width,
            transcendentals=3 * count * width,
            bytes_accessed=2 * (count * depth + depth * width + 2 * count * width),
        ),
    )(value, weight, shift)


def cut_levels(raw, cuts):
    lane = lax.broadcasted_iota(jnp.int32, raw.shape, 1)
    levels = []
    for cut in cuts:
        part = jnp.where(lane < cut, raw, 0.0)
        scale = lax.rsqrt(jnp.sum(part * part, axis=1, keepdims=True) + EPS_EMBED)
        levels.append(((part * scale).astype(BF), part, scale))
    return levels


def pool_kernel(cuts, span, q_ref, d_ref, seg_ref, out_ref, units, hot):
    @pl.when(pl.program_id(0) == 0)
    def _():
        raw = d_ref[span:, :].astype(F32)
        for level, parts in enumerate(cut_levels(raw, cuts)):
            units[level] = parts[0]
        doc = lax.broadcasted_iota(jnp.int32, hot.shape, 0)
        hot[...] = (seg_ref[:, span:] == NQ_ROW + doc).astype(F32).astype(BF)

    levels = cut_levels(q_ref[...].astype(F32), cuts)
    for level in range(len(cuts)):
        similar = exact(units[level], levels[level][0], ((1,), (1,)))
        expo = jnp.exp(similar * (1.0 / POOL_TEMP))
        high = expo.astype(BF)
        rest = (expo - high.astype(F32)).astype(BF)
        out_ref[level * NDOC : (level + 1) * NDOC, :] = exact(
            hot[...], high, ((1,), (0,))
        ) + exact(hot[...], rest, ((1,), (0,)))


def pool(cuts, span, queries, row_embed, seg_row):
    count, width = queries.shape
    tokens = row_embed.shape[0]
    whole = lambda shape: pl.BlockSpec(shape, lambda i: (0, 0))
    return pl.pallas_call(
        partial(pool_kernel, cuts, span),
        grid=(count // TILE,),
        in_specs=[
            pl.BlockSpec((TILE, width), lambda i: (i, 0)),
            whole((tokens, width)),
            whole((1, tokens)),
        ],
        out_specs=pl.BlockSpec((len(cuts) * NDOC, TILE), lambda i: (0, i)),
        out_shape=jax.ShapeDtypeStruct((len(cuts) * NDOC, count), F32),
        scratch_shapes=[
            pltpu.VMEM((len(cuts), tokens - span, width), BF),
            pltpu.VMEM((NDOC, tokens - span), BF),
        ],
        compiler_params=pltpu.CompilerParams(vmem_limit_bytes=32 << 20),
        cost_estimate=pl.CostEstimate(
            flops=2 * len(cuts) * count * tokens * 256,
            transcendentals=len(cuts) * count * tokens,
            bytes_accessed=2 * (count + tokens) * width,
        ),
    )(queries, row_embed, seg_row)


def level_back(grad, part, scale):
    return scale * grad - part * (scale * scale * scale) * jnp.sum(
        part * grad, axis=1, keepdims=True
    )


def pool_back_kernel(
    cuts, span, q_ref, d_ref, seg_ref, coef_ref, q_out, d_out, units, units_t, hot, sums
):
    step = pl.program_id(0)

    @pl.when(step == 0)
    def _():
        raw = d_ref[span:, :].astype(F32)
        for level, parts in enumerate(cut_levels(raw, cuts)):
            units[level] = parts[0]
            units_t[level] = jnp.transpose(parts[0])
        doc = lax.broadcasted_iota(jnp.int32, hot.shape, 0)
        wanted = NQ_ROW + jnp.where(doc < NDOC, doc, doc - NDOC)
        hot[...] = (seg_ref[:, span:] == wanted).astype(F32).astype(BF)
        sums[...] = jnp.zeros_like(sums)

    levels = cut_levels(q_ref[...].astype(F32), cuts)
    total = jnp.zeros(q_ref.shape, F32)
    for level in range(len(cuts)):
        unit, part, scale = levels[level]
        similar = exact(units[level], unit, ((1,), (1,)))
        coef = coef_ref[level * NDOC : (level + 1) * NDOC, :]
        high = coef.astype(BF).astype(F32)
        both = jnp.concatenate([high, coef - high], axis=0).astype(BF)
        spread = exact(hot[...], both, ((0,), (0,)))
        grad = (jnp.exp(similar * (1.0 / POOL_TEMP)) * spread).astype(BF)
        sums[level] += exact(grad, unit, ((1,), (0,)))
        grad_unit = jnp.transpose(exact(units_t[level], grad, ((1,), (0,))))
        total = total + level_back(grad_unit, part, scale)
    q_out[...] = total.astype(BF)

    @pl.when(step == pl.num_programs(0) - 1)
    def _():
        raw = d_ref[span:, :].astype(F32)
        result = jnp.zeros(raw.shape, F32)
        for level, parts in enumerate(cut_levels(raw, cuts)):
            lane = lax.broadcasted_iota(jnp.int32, raw.shape, 1)
            grad = jnp.where(lane < cuts[level], sums[level], 0.0)
            result = result + level_back(grad, parts[1], parts[2])
        d_out[...] = result


def pool_back(cuts, span, queries, row_embed, seg_row, coef):
    count, width = queries.shape
    tokens = row_embed.shape[0]
    docs = tokens - span
    whole = lambda shape: pl.BlockSpec(shape, lambda i: (0, 0))
    return pl.pallas_call(
        partial(pool_back_kernel, cuts, span),
        grid=(count // TILE,),
        in_specs=[
            pl.BlockSpec((TILE, width), lambda i: (i, 0)),
            whole((tokens, width)),
            whole((1, tokens)),
            pl.BlockSpec((len(cuts) * NDOC, TILE), lambda i: (0, i)),
        ],
        out_specs=[pl.BlockSpec((TILE, width), lambda i: (i, 0)), whole((docs, width))],
        out_shape=[
            jax.ShapeDtypeStruct((count, width), BF),
            jax.ShapeDtypeStruct((docs, width), F32),
        ],
        scratch_shapes=[
            pltpu.VMEM((len(cuts), docs, width), BF),
            pltpu.VMEM((len(cuts), width, docs), BF),
            pltpu.VMEM((2 * NDOC, docs), BF),
            pltpu.VMEM((len(cuts), docs, width), F32),
        ],
        compiler_params=pltpu.CompilerParams(vmem_limit_bytes=32 << 20),
        cost_estimate=pl.CostEstimate(
            flops=2 * len(cuts) * count * docs * 512,
            transcendentals=len(cuts) * count * docs,
            bytes_accessed=4 * (count + tokens) * width,
        ),
    )(queries, row_embed, seg_row, coef)


def local_chip(
    tokens,
    lengths,
    pairing,
    w_qkv,
    b_qv,
    w_out,
    b_out,
    ln_gain,
    ln_bias,
    w_up,
    b_up,
    w_down,
    b_down,
    w_proj,
    cot,
):
    z, x, c, y = (lax.axis_index(name) for name in ("z", "x", "c", "y"))
    chip = 4 * z + 2 * x + y
    token_count, width = tokens.shape
    share = token_count // 2
    own_start, other_start = c * share, (1 - c) * share
    gains, shifts = ln_gain.astype(F32), ln_bias.astype(F32)

    half_width = w_qkv.shape[2]
    up_wide = w_up.shape[1]
    chip_count = lengths.shape[0]
    half_queries = NQ_ROW // 2
    query_total = chip_count * half_queries
    quarter = half_width // 2
    qkv_rows = jnp.concatenate(
        [w_qkv[k][:, g * quarter : (g + 1) * quarter] for g in range(2) for k in range(3)], axis=1
    )
    pair_rows = jnp.pad(pairing.astype(BF), ((0, 63), (0, 128 - half_queries)))
    mid_rows = jnp.concatenate([w_up, w_out.T, pair_rows], axis=1)
    bias = jnp.concatenate([b_qv.reshape(-1), b_up])[None].astype(F32)
    down_rows = turn(w_down.T)
    got = exchange((qkv_rows, "z", FAR), (tokens, "c", SWAP), (bias, "y", SWAP))
    qkv_pair = far_pair(qkv_rows, got[0], z)
    row = jnp.where(c == y, tokens, got[1])
    bias = jnp.where(c == y, bias, got[2])
    got = exchange((qkv_pair, "z", NEAR), (tie(mid_rows, qkv_pair), "z", FAR))
    qkv_line = whole_line(qkv_pair, got[0], z)
    mid_pair = far_pair(mid_rows, got[1], z)
    full_down = lax.all_gather(tie(down_rows, qkv_line), ("z", "x", "y"), axis=0, tiled=True)
    got = exchange(*first_moves(qkv_line), (mid_pair, "z", NEAR))
    qkv_parts = first_parts(qkv_line, got, x, c, y)
    mid_line = whole_line(mid_pair, got[3], z)
    got = exchange(*last_moves(qkv_parts))
    full_qkv = full_rows(qkv_parts, got, x, c, y)
    got = exchange(*first_moves(tie(mid_line, full_qkv)))
    mid_parts = first_parts(mid_line, got, x, c, y)
    got = exchange(*last_moves(mid_parts))
    full_mid = full_rows(mid_parts, got, x, c, y)
    full_out = full_mid[:, up_wide : up_wide + half_width]
    pairs = full_mid[:, up_wide + half_width :].reshape(chip_count, 64, 128)
    pairs = pairs[:, 0, :half_queries].astype(jnp.int32).reshape(1, query_total)
    row_lengths = lax.dynamic_index_in_dim(lengths, chip, 0, keepdims=False)
    segments = segments_of(row_lengths, token_count)
    seg_col, seg_row = segments[:, None], segments[None, :]
    query_span = NQ_ROW * QLEN
    bounds = tile_bounds(row_lengths, token_count)
    no_bias = jnp.zeros((1, quarter), F32)
    qkv_bias = jnp.concatenate(
        [
            part
            for g in range(2)
            for part in (
                bias[:, g * quarter : (g + 1) * quarter],
                no_bias,
                bias[:, half_width + g * quarter : half_width + (g + 1) * quarter],
            )
        ],
        axis=1,
    )
    qkv = (dot(row, full_qkv) + qkv_bias).astype(BF)
    mixed, lse = attend(bounds, qkv, seg_col, seg_row)
    own_cot = turn(tie(cot, qkv))

    def row_sum(left, weight_t, transposed):
        times = contract_cols if transposed else dot
        theirs = swap(times(left(1), weight_t).astype(BF), "c")
        return times(left(0), weight_t) + theirs.astype(F32)

    def mixed_half(which):
        return rows_of(mixed, other_start if which else own_start, share)

    attn_sum = row_sum(mixed_half, full_out, True)
    own_tokens = rows_of(row, own_start, share).astype(F32)
    normed, unit_one, rstd_one = norm_forward(
        own_tokens + attn_sum + b_out.astype(F32), gains[0], shifts[0]
    )
    normed_low = normed.astype(BF)
    normed_all = jnp.concatenate([normed_low, swap(normed_low, "c")], axis=0)
    activation, slope = expand(normed_all, full_mid, bias[:, 2 * half_width :])
    ffn_sum = row_sum(
        lambda which: activation[which * share : (which + 1) * share], full_down, True
    )
    result, unit_two, rstd_two = norm_forward(
        normed + ffn_sum + b_down.astype(F32), gains[1], shifts[1]
    )
    result_low = result.astype(BF)
    embed = dot(result_low, w_proj).astype(BF)

    other_embed = swap(embed, "c")
    row_embed = jnp.where(
        c == 0,
        jnp.concatenate([embed, other_embed], axis=0),
        jnp.concatenate([other_embed, embed], axis=0),
    )
    half_span = query_span // 2
    own_queries = rows_of(row_embed, c * half_span, half_span)
    chips = ("z", "x", "y")
    queries = lax.all_to_all(
        jnp.broadcast_to(own_queries[None], (chip_count,) + own_queries.shape), chips, 0, 0
    ).reshape(chip_count * half_span, -1)
    proj_width = w_proj.shape[1]
    cuts = (proj_width, 3 * proj_width // 4, proj_width // 2)
    sums = pool(cuts, query_span, queries, row_embed, seg_row)
    doc_sizes = jnp.tile(row_lengths.astype(F32), 3)[:, None]
    group = (
        jnp.arange(query_total * QLEN, dtype=jnp.int32)[:, None] // QLEN
        == jnp.arange(query_total, dtype=jnp.int32)[None, :]
    ).astype(F32)
    pooled = POOL_TEMP * jnp.log(sums / doc_sizes)
    logits = jnp.dot(pooled, group, precision=FULL_PRECISION) / LOSS_TEMP
    logits = logits.reshape(3, NDOC, query_total)
    doc_numbers = chip * NDOC + jnp.arange(NDOC, dtype=jnp.int32)
    picked = (doc_numbers[:, None] == pairs).astype(F32)
    own_high = jnp.max(logits, axis=1)
    own_lse = own_high + jnp.log(jnp.sum(jnp.exp(logits - own_high[:, None]), axis=1))
    own_target = jnp.sum(logits * picked, axis=1)
    notes = jnp.pad(jnp.concatenate([own_lse, own_target], axis=1), ((0, 5), (0, 0)))
    notes = lax.all_to_all(
        jnp.broadcast_to(notes[None], (chip_count,) + notes.shape), chips, 0, 0
    )
    chip_lse = notes[:, :3, :query_total]
    high = jnp.max(chip_lse, axis=0)
    all_lse = high + jnp.log(jnp.sum(jnp.exp(chip_lse - high), axis=0))
    target = jnp.sum(notes[:, :3, query_total:], axis=0)
    losses = jnp.sum(all_lse - target, axis=0).reshape(chip_count, half_queries)
    grad_logits = (jnp.exp(logits - all_lse[:, None]) - picked) / LOSS_TEMP
    coefficient = (
        lax.dot_general(
            grad_logits.reshape(3 * NDOC, query_total),
            group,
            (((1,), (1,)), ((), ())),
            precision=FULL_PRECISION,
        )
        / sums
    )
    losses = jnp.where(c == y, losses, swap(losses, "c"))
    loss_out = rows_of(losses, 4 * z + 2 * x + c, 1)
    query_grad, doc_grad = pool_back(cuts, query_span, queries, row_embed, seg_row, coefficient)
    grad_blocks = lax.all_to_all(
        query_grad.reshape(chip_count, half_span, proj_width), chips, 0, 0
    )
    own_query_grad = jnp.sum(grad_blocks.astype(F32), axis=0)
    row_grad = jnp.concatenate([jnp.zeros((query_span, proj_width), F32), doc_grad], axis=0)
    row_grad = lax.dynamic_update_slice_in_dim(row_grad, own_query_grad, c * half_span, 0)
    grad_embed = rows_of(row_grad, own_start, share) + swap(
        rows_of(row_grad, other_start, share), "c"
    )

    proj_low = w_proj
    grad_embed_low = grad_embed.astype(BF)
    grad_embed_rest = (grad_embed - grad_embed_low.astype(F32)).astype(BF)
    grad_result = own_cot.astype(F32) + (
        contract_cols(grad_embed_low, proj_low) + contract_cols(grad_embed_rest, proj_low)
    )
    proj_grad = contract_rows(result_low, grad_embed_low) + contract_rows(
        result_low, grad_embed_rest
    )
    gain_two = jnp.sum(grad_result * unit_two, axis=0)
    shift_two = jnp.sum(grad_result, axis=0)
    grad_second = norm_backward(grad_result, unit_two, rstd_two, gains[1])
    grad_ffn = grad_second.astype(BF)
    down_bias = jnp.sum(grad_ffn.astype(F32), axis=0)
    grad_ffn_all = jnp.concatenate([grad_ffn, swap(grad_ffn, "c")], axis=0)
    down_blocks = contract_rows(grad_ffn_all, activation).astype(BF)
    down_part = turn(
        lax.psum_scatter(down_blocks, ("z", "x", "y"), scatter_dimension=0, tiled=True)
    ).astype(F32)
    grad_up = (dot(grad_ffn_all, full_down) * slope.astype(F32)).astype(BF)
    up_bias = jnp.sum(grad_up.astype(F32), axis=0)
    up_blocks = blocks_of(normed_all, grad_up)
    up_moved = exchange(*sum_moves(up_blocks, x, c, y))
    up_parts = sum_parts(up_blocks, up_moved, x, c, y)
    full_up = full_mid[:, :up_wide]
    grad_normed = (
        row_sum(lambda which: grad_up[which * share : (which + 1) * share], full_up, True)
        + grad_second
    )
    gain_one = jnp.sum(grad_normed * unit_one, axis=0)
    shift_one = jnp.sum(grad_normed, axis=0)
    grad_first = norm_backward(grad_normed, unit_one, rstd_one, gains[0])
    grad_attn = grad_first.astype(BF)
    out_bias = jnp.sum(grad_attn.astype(F32), axis=0)
    other_attn = swap(grad_attn, "c")
    grad_attn_all = jnp.where(
        c == 0,
        jnp.concatenate([grad_attn, other_attn], axis=0),
        jnp.concatenate([other_attn, grad_attn], axis=0),
    )
    grad_mixed = dot(grad_attn_all, full_out).astype(BF)
    out_blocks = blocks_of(grad_attn_all, mixed)
    grad_mixed, *up_parts = lax.optimization_barrier((grad_mixed,) + tuple(up_parts))
    up_moved = exchange(*line_moves(up_parts, x, c, y), x_move(out_blocks, x))
    up_line = line_of(up_parts, up_moved, x, c, y)
    out_line = x_sum(out_blocks, up_moved[3], x)
    grads_one, sums_one = attend_back(bounds, 0, qkv, mixed, grad_mixed, lse, seg_col, seg_row)
    grad_mixed, up_line, out_line = lax.optimization_barrier((grad_mixed, up_line, out_line))
    up_moved = exchange(near_move(up_line, z), *core_moves(out_line, c, y))
    up_pair = near_sum(up_line, up_moved[0], z)
    out_line = core_sum(out_line, up_moved[1], up_moved[2], c, y)
    grads_two, sums_two = attend_back(
        bounds, 1, qkv, mixed, tie(grad_mixed, grads_one), lse, seg_col, seg_row
    )
    grads_one = tie(grads_one, grads_two)
    proj_half = rows_of(proj_grad, own_start, share) + swap(
        rows_of(proj_grad, other_start, share), "c"
    )
    shared = jnp.stack([gain_one, gain_two, shift_one, shift_two, out_bias, down_bias])
    half_sums = jnp.concatenate(
        [
            sums_one[:, 0].reshape(-1),
            sums_two[:, 0].reshape(-1),
            sums_one[:, 1].reshape(-1),
            sums_two[:, 1].reshape(-1),
            up_bias,
        ]
    )
    small = jnp.concatenate([shared.reshape(-1, 128), half_sums.reshape(-1, 128), proj_half])

    qkv_blocks = jnp.concatenate(
        [blocks_of(row, grads_one), blocks_of(row, grads_two)], axis=4
    )
    qkv_blocks, up_pair, out_line = lax.optimization_barrier((qkv_blocks, up_pair, out_line))
    moved = exchange(
        *sum_moves(qkv_blocks, x, c, y), far_move(up_pair, z), near_move(out_line, z)
    )
    qkv_parts = sum_parts(qkv_blocks, moved, x, c, y)
    up_part = far_sum(up_pair, moved[3], z)
    out_pair = near_sum(out_line, moved[4], z)

    def input_terms(start):
        return contract_cols(
            rows_of(grads_one, start, share), full_qkv[:, : 3 * quarter]
        ) + contract_cols(rows_of(grads_two, start, share), full_qkv[:, 3 * quarter :])

    other_terms = swap(input_terms(other_start).astype(BF), "c")
    grad_input = (input_terms(own_start) + other_terms.astype(F32) + grad_first).astype(BF)
    moved = exchange(*line_moves(qkv_parts, x, c, y), far_move(out_pair, z), (small, "y", SWAP))
    qkv_line = line_of(qkv_parts, moved, x, c, y)
    out_part = far_sum(out_pair, moved[3], z)
    small = small + moved[4]
    moved = exchange(near_move(qkv_line, z), (small, "x", SWAP))
    qkv_pair = near_sum(qkv_line, moved[0], z)
    small = small + moved[1]
    y_out = turn(tie(result_low, grad_input, qkv_line))
    grad_input = turn(tie(grad_input, qkv_line))
    moved = exchange(far_move(qkv_pair, z), (small, "z", FAR))
    qkv_part = far_sum(qkv_pair, moved[0], z)
    small = small + moved[1]
    small = small + lax.ppermute(small, "z", NEAR)
    other_small = swap(small, "c")
    shared_rows = 6 * width // 128
    small_rows = small.shape[0] - share
    shared = (small[:shared_rows] + other_small[:shared_rows]).reshape(6, width)
    half_sums = jnp.where(
        c == y, small[shared_rows:small_rows], other_small[shared_rows:small_rows]
    ).reshape(-1)
    proj_sum = pair_up(small[small_rows:], other_small[small_rows:], c, 0).reshape(width, -1)
    qkv_part = qkv_part.reshape(64, 2, 3, quarter).transpose(2, 0, 1, 3).reshape(3, 64, half_width)
    return (
        y_out,
        loss_out,
        grad_input,
        qkv_part,
        half_sums[: 2 * half_width].reshape(2, half_width),
        out_part.T,
        shared[4],
        shared[0:2],
        shared[2:4],
        up_part,
        half_sums[2 * half_width :],
        down_part.T,
        shared[5],
        proj_sum,
    )


IN_SPECS = (
    P("dp", None),
    P(),
    P("dp", "tensor"),
    P(None, "dp", "tensor"),
    P(None, "tensor"),
    P("tensor", "dp"),
    P(),
    P(),
    P(),
    P("dp", "tensor"),
    P("tensor"),
    P("tensor", "dp"),
    P(),
    P(),
    P(("dp", "tensor"), None),
)
OUT_SPECS = (
    P(("dp", "tensor"), None),
    P("dp", "tensor"),
    P(("dp", "tensor"), None),
    P(None, "dp", "tensor"),
    P(None, "tensor"),
    P("tensor", "dp"),
    P(),
    P(),
    P(),
    P("dp", "tensor"),
    P("tensor"),
    P("tensor", "dp"),
    P(),
    P(),
)


def solution(mesh):
    if mesh.devices.shape != (16, 2):
        return jax.shard_map(
            local, mesh=mesh, in_specs=IN_SPECS, out_specs=OUT_SPECS, check_vma=False
        )
    names = {"dp": ("z", "x", "c"), "tensor": ("y",)}

    def respec(spec):
        parts = []
        for entry in spec:
            axes = () if entry is None else entry if isinstance(entry, tuple) else (entry,)
            parts.append(tuple(name for axis in axes for name in names[axis]) or None)
        return P(*parts)

    chips = Mesh(mesh.devices.reshape(4, 2, 2, 2), ("z", "x", "c", "y"))
    return jax.shard_map(
        local_chip,
        mesh=chips,
        in_specs=tuple(respec(spec) for spec in IN_SPECS),
        out_specs=tuple(respec(spec) for spec in OUT_SPECS),
        check_vma=False,
    )
```

```python
from functools import partial

import jax
import jax.numpy as jnp
from jax import lax
from jax.experimental import pallas as pl
from jax.experimental.pallas import tpu as pltpu
from jax.sharding import Mesh, PartitionSpec as P

HEAD_DIM = 64
QLEN = 32
NQ_ROW = 8
NDOC = 8


EPS_NORM = 1e-05
EPS_EMBED = 1e-06
POOL_TEMP = 0.1
LOSS_TEMP = 0.1
FULL_PRECISION = lax.Precision.HIGHEST
MASKED_SCORE = -1e30


def shortened(shard):

    def short(part):
        return part.astype(jnp.bfloat16) if part.dtype == jnp.float32 else part

    return jax.tree.map(short, shard)


def contract_rows(left, right, precision=None):
    return lax.dot_general(
        left,
        right,
        (((0,), (0,)), ((), ())),
        precision=precision,
        preferred_element_type=jnp.float32,
    )


def contract_cols(left, right, precision=None):
    return lax.dot_general(
        left,
        right,
        (((1,), (1,)), ((), ())),
        precision=precision,
        preferred_element_type=jnp.float32,
    )


def norm_forward(value, gain, shift):
    centred = value - jnp.mean(value, axis=1, keepdims=True)
    rstd = lax.rsqrt(jnp.mean(centred * centred, axis=1, keepdims=True) + EPS_NORM)
    unit = centred * rstd
    return (unit * gain + shift, unit, rstd)


def norm_backward(grad, unit, rstd, gain):
    scaled = grad * gain
    return rstd * (
        scaled
        - jnp.mean(scaled, axis=1, keepdims=True)
        - unit * jnp.mean(scaled * unit, axis=1, keepdims=True)
    )


def segments_of(row_lengths, token_count):
    position = jnp.arange(token_count, dtype=jnp.int32)
    query_span = NQ_ROW * QLEN
    ends = jnp.cumsum(row_lengths)
    passed = jnp.sum((position[:, None] - query_span >= ends[None, :]).astype(jnp.int32), axis=1)
    return jnp.where(position < query_span, position // QLEN, NQ_ROW + passed)


def normalize_cut(raw, width):
    part = raw[:, :width]
    scale = lax.rsqrt(jnp.sum(part * part, axis=1, keepdims=True) + EPS_EMBED)
    return (part * scale, part, scale)


def normalize_back(grad, part, scale, full_width):
    result = scale * grad - part * (scale * scale * scale) * jnp.sum(
        part * grad, axis=1, keepdims=True
    )
    return jnp.pad(result, ((0, 0), (0, full_width - grad.shape[1])))


def masked_scores(query_block, key_rows, block_segments, segments):
    scores = jnp.einsum(
        "qhd,khd->hqk", query_block, key_rows, preferred_element_type=jnp.float32
    ) * HEAD_DIM ** (-0.5)
    return jnp.where((block_segments[:, None] == segments[None, :])[None], scores, MASKED_SCORE)


def attend_forward(query_rows, key_rows, value_rows, segments, block_rows):
    token_count = query_rows.shape[0]

    def one_block(block_start):
        query_block = lax.dynamic_slice_in_dim(query_rows, block_start, block_rows, 0)
        block_segments = lax.dynamic_slice_in_dim(segments, block_start, block_rows, 0)
        scores = masked_scores(query_block, key_rows, block_segments, segments)
        highest = jnp.max(scores, axis=2, keepdims=True)
        expo = jnp.exp(scores - highest)
        totals = jnp.sum(expo, axis=2, keepdims=True)
        weights = (expo / totals).astype(jnp.bfloat16)
        mixed = jnp.einsum("hqk,khd->qhd", weights, value_rows, preferred_element_type=jnp.float32)
        return (mixed.astype(jnp.bfloat16), (highest + jnp.log(totals))[:, :, 0])

    starts = jnp.arange(token_count // block_rows, dtype=jnp.int32) * block_rows
    mixed, log_totals = lax.map(one_block, starts)
    return (mixed.reshape(token_count, -1), log_totals)


def attend_backward(query_rows, key_rows, value_rows, segments, log_totals, grad_mixed, block_rows):
    token_count, local_heads, head_size = query_rows.shape
    scale = HEAD_DIM ** (-0.5)
    grad_heads = grad_mixed.reshape(token_count, local_heads, head_size)

    def one_block(carried, inputs):
        grad_keys, grad_values = carried
        block_start, block_lse = inputs
        query_block = lax.dynamic_slice_in_dim(query_rows, block_start, block_rows, 0)
        grad_block = lax.dynamic_slice_in_dim(grad_heads, block_start, block_rows, 0)
        block_segments = lax.dynamic_slice_in_dim(segments, block_start, block_rows, 0)
        scores = masked_scores(query_block, key_rows, block_segments, segments)
        probs = jnp.exp(scores - block_lse[:, :, None])
        grad_probs = jnp.einsum(
            "qhd,khd->hqk", grad_block, value_rows, preferred_element_type=jnp.float32
        )
        inner = jnp.sum(probs * grad_probs, axis=2, keepdims=True)
        grad_scores = (probs * (grad_probs - inner)).astype(jnp.bfloat16)
        grad_query = (
            jnp.einsum("hqk,khd->qhd", grad_scores, key_rows, preferred_element_type=jnp.float32)
            * scale
        )
        grad_keys = (
            grad_keys
            + jnp.einsum(
                "hqk,qhd->khd", grad_scores, query_block, preferred_element_type=jnp.float32
            )
            * scale
        )
        grad_values = grad_values + jnp.einsum(
            "hqk,qhd->khd",
            probs.astype(jnp.bfloat16),
            grad_block,
            preferred_element_type=jnp.float32,
        )
        return ((grad_keys, grad_values), grad_query)

    starts = jnp.arange(token_count // block_rows, dtype=jnp.int32) * block_rows
    zero_rows = jnp.zeros(key_rows.shape, jnp.float32)
    (grad_keys, grad_values), grad_queries = lax.scan(
        one_block, (zero_rows, zero_rows), (starts, log_totals)
    )
    flat_width = local_heads * head_size
    return (
        grad_queries.reshape(token_count, flat_width),
        grad_keys.reshape(token_count, flat_width),
        grad_values.reshape(token_count, flat_width),
    )


def local(
    tokens,
    lengths,
    pairing,
    w_qkv,
    b_qv,
    w_out,
    b_out,
    ln_gain,
    ln_bias,
    w_up,
    b_up,
    w_down,
    b_down,
    w_proj,
    cot,
):
    tensor_count = lax.axis_size("tensor")
    tensor_index = lax.axis_index("tensor")
    data_index = lax.axis_index("dp")
    token_count = tokens.shape[0]
    share_rows = token_count // tensor_count
    block_rows = min(512, token_count)
    own_start = tensor_index * share_rows
    full_qkv, full_out, full_up, full_down = (
        lax.all_gather(w_qkv, "dp", axis=1, tiled=True),
        lax.all_gather(w_out, "dp", axis=1, tiled=True),
        lax.all_gather(w_up, "dp", axis=0, tiled=True),
        lax.all_gather(w_down, "dp", axis=1, tiled=True),
    )
    head_width = full_qkv.shape[2]
    local_heads = head_width // HEAD_DIM
    row_lengths = lax.dynamic_index_in_dim(lengths, data_index, 0, keepdims=False)
    segments = segments_of(row_lengths, token_count)
    projected = jnp.einsum("td,kdw->ktw", tokens, full_qkv, preferred_element_type=jnp.float32)
    qv_bias = b_qv.astype(jnp.float32)
    query_rows = (
        (projected[0] + qv_bias[0]).astype(jnp.bfloat16).reshape(token_count, local_heads, HEAD_DIM)
    )
    key_rows = projected[1].astype(jnp.bfloat16).reshape(token_count, local_heads, HEAD_DIM)
    value_rows = (
        (projected[2] + qv_bias[1]).astype(jnp.bfloat16).reshape(token_count, local_heads, HEAD_DIM)
    )
    mixed, log_totals = attend_forward(query_rows, key_rows, value_rows, segments, block_rows)
    attn_terms = jnp.dot(mixed, full_out, preferred_element_type=jnp.float32)
    attn_sum = lax.psum_scatter(
        attn_terms.astype(jnp.bfloat16), "tensor", scatter_dimension=0, tiled=True
    ).astype(jnp.float32)
    own_tokens = lax.dynamic_slice_in_dim(tokens, own_start, share_rows, 0).astype(jnp.float32)
    gains = ln_gain.astype(jnp.float32)
    shifts = ln_bias.astype(jnp.float32)
    normed, unit_one, rstd_one = norm_forward(
        own_tokens + attn_sum + b_out.astype(jnp.float32), gains[0], shifts[0]
    )
    normed_all = lax.all_gather(normed.astype(jnp.bfloat16), "tensor", axis=0, tiled=True)
    up_value = jnp.dot(normed_all, full_up, preferred_element_type=jnp.float32) + b_up.astype(
        jnp.float32
    )
    activation = jax.nn.gelu(up_value, approximate=False).astype(jnp.bfloat16)
    ffn_terms = jnp.dot(activation, full_down, preferred_element_type=jnp.float32)
    ffn_sum = lax.psum_scatter(
        ffn_terms.astype(jnp.bfloat16), "tensor", scatter_dimension=0, tiled=True
    ).astype(jnp.float32)
    result, unit_two, rstd_two = norm_forward(
        normed + ffn_sum + b_down.astype(jnp.float32), gains[1], shifts[1]
    )
    result_low = result.astype(jnp.bfloat16)
    embed = jnp.dot(result_low, w_proj, preferred_element_type=jnp.float32).astype(jnp.bfloat16)
    embed_all = lax.all_gather(embed, ("dp", "tensor"), axis=0, tiled=True)
    row_count = lengths.shape[0]
    proj_width = w_proj.shape[1]
    widths = (proj_width, 3 * proj_width // 4, proj_width // 2)
    per_device = pairing.shape[1]
    query_count = per_device * QLEN
    query_span = NQ_ROW * QLEN
    emb_rows = embed_all.reshape(row_count, token_count, proj_width)
    my_row = lax.dynamic_index_in_dim(emb_rows, data_index, 0, keepdims=False)
    query_raw = lax.dynamic_slice_in_dim(my_row, tensor_index * query_count, query_count, 0).astype(
        jnp.float32
    )
    query_levels = [normalize_cut(query_raw, width) for width in widths]
    query_units = [level_parts[0].astype(jnp.bfloat16) for level_parts in query_levels]
    doc_numbers = jnp.arange(NDOC, dtype=jnp.int32)

    def row_pool(carried, inputs):
        row_emb, lengths_row = inputs
        row_hot = (
            segments_of(lengths_row, token_count)[:, None] == NQ_ROW + doc_numbers[None, :]
        ).astype(jnp.float32)
        row_raw = row_emb.astype(jnp.float32)
        pooled_list = []
        sums_list = []
        for width, query_unit in zip(widths, query_units):
            doc_unit = normalize_cut(row_raw, width)[0].astype(jnp.bfloat16)
            expo = jnp.exp(contract_cols(query_unit, doc_unit) / POOL_TEMP)
            sums = jnp.dot(expo, row_hot, precision=FULL_PRECISION)
            pooled = POOL_TEMP * jnp.log(sums / lengths_row.astype(jnp.float32))
            pooled_list.append(jnp.sum(pooled.reshape(per_device, QLEN, NDOC), axis=1))
            sums_list.append(sums)
        return (carried, (jnp.stack(pooled_list), jnp.stack(sums_list)))

    _, (row_scores, row_sums) = lax.scan(row_pool, 0, (emb_rows, lengths))
    logits = (
        jnp.transpose(row_scores, (2, 1, 0, 3)).reshape(per_device, 3, row_count * NDOC) / LOSS_TEMP
    )
    own_pairs = pairing[0]
    target = jnp.take_along_axis(
        logits, jnp.broadcast_to(own_pairs[:, None, None], (per_device, 3, 1)), axis=2
    )[:, :, 0]
    loss_out = jnp.sum(jax.nn.logsumexp(logits, axis=2) - target, axis=1).reshape(1, per_device)
    picked = (
        jnp.arange(row_count * NDOC, dtype=jnp.int32)[None, None, :] == own_pairs[:, None, None]
    ).astype(jnp.float32)
    grad_logits = (jax.nn.softmax(logits, axis=2) - picked) / LOSS_TEMP
    grad_rows = jnp.transpose(grad_logits.reshape(per_device, 3, row_count, NDOC), (2, 1, 0, 3))
    coefficient = jnp.repeat(grad_rows, QLEN, axis=2) / row_sums

    def row_back(carried, inputs):
        row_emb, lengths_row, row_coef = inputs
        row_hot = (
            segments_of(lengths_row, token_count)[:, None] == NQ_ROW + doc_numbers[None, :]
        ).astype(jnp.float32)
        row_raw = row_emb.astype(jnp.float32)
        new_carried = []
        row_grad = jnp.zeros((token_count, proj_width), jnp.float32)
        for level_index in range(3):
            width = widths[level_index]
            doc_unit_f, doc_part, doc_scale = normalize_cut(row_raw, width)
            doc_unit = doc_unit_f.astype(jnp.bfloat16)
            expo = jnp.exp(contract_cols(query_units[level_index], doc_unit) / POOL_TEMP)
            spread = contract_cols(row_coef[level_index], row_hot, FULL_PRECISION)
            grad_sim = (expo * spread).astype(jnp.bfloat16)
            new_carried.append(
                carried[level_index]
                + jnp.dot(grad_sim, doc_unit, preferred_element_type=jnp.float32)
            )
        return (tuple(new_carried), row_grad)

    zero_query = tuple((jnp.zeros((query_count, width), jnp.float32) for width in widths))
    query_grads, doc_grads = lax.scan(row_back, zero_query, (emb_rows, lengths, coefficient))
    grad_query = jnp.zeros((query_count, proj_width), jnp.float32)
    for level_index in range(3):
        level_parts = query_levels[level_index]
        grad_query = grad_query + normalize_back(
            query_grads[level_index], level_parts[1], level_parts[2], proj_width
        )
    coef_mine = jnp.transpose(coefficient, (2, 1, 0, 3)).reshape(query_count, 3, row_count * NDOC)
    coef_all, grad_query_all = (
        lax.all_gather(shortened(coef_mine), ("dp", "tensor"), axis=0, tiled=True).astype(
            coef_mine.dtype
        ),
        lax.all_gather(
            grad_query.astype(jnp.bfloat16), ("dp", "tensor"), axis=0, tiled=True
        ).astype(grad_query.dtype),
    )
    own_raw = embed.astype(jnp.float32)
    own_segments = lax.dynamic_slice_in_dim(segments, own_start, share_rows, 0)
    own_docs = jnp.where(own_segments >= NQ_ROW, data_index * NDOC + own_segments - NQ_ROW, -1)
    own_hot = (own_docs[:, None] == jnp.arange(row_count * NDOC, dtype=jnp.int32)[None, :]).astype(
        jnp.float32
    )
    queries_all = (
        emb_rows[:, :query_span].reshape(row_count * query_span, proj_width).astype(jnp.float32)
    )
    grad_embed = jnp.zeros((share_rows, proj_width), jnp.float32)
    for level_index in range(3):
        width = widths[level_index]
        query_unit_all = normalize_cut(queries_all, width)[0].astype(jnp.bfloat16)
        doc_unit_f, doc_part, doc_scale = normalize_cut(own_raw, width)
        expo = jnp.exp(contract_cols(query_unit_all, doc_unit_f.astype(jnp.bfloat16)) / POOL_TEMP)
        spread = contract_cols(coef_all[:, level_index], own_hot, FULL_PRECISION)
        grad_sim = (expo * spread).astype(jnp.bfloat16)
        grad_doc = contract_rows(grad_sim, query_unit_all)
        grad_embed = grad_embed + normalize_back(grad_doc, doc_part, doc_scale, proj_width)
    row_query_grads = lax.dynamic_slice_in_dim(
        grad_query_all, data_index * query_span, query_span, 0
    )
    padded = jnp.pad(row_query_grads, ((0, token_count - query_span), (0, 0)))
    grad_embed = grad_embed + lax.dynamic_slice_in_dim(padded, own_start, share_rows, 0)
    proj_float = w_proj.astype(jnp.float32)
    grad_result = cot.astype(jnp.float32) + contract_cols(grad_embed, proj_float, FULL_PRECISION)
    proj_grad = contract_rows(result_low.astype(jnp.float32), grad_embed, FULL_PRECISION)
    gain_two = jnp.sum(grad_result * unit_two, axis=0)
    shift_two = jnp.sum(grad_result, axis=0)
    grad_second = norm_backward(grad_result, unit_two, rstd_two, gains[1])
    grad_ffn = grad_second.astype(jnp.bfloat16)
    down_bias = jnp.sum(grad_ffn.astype(jnp.float32), axis=0)
    grad_ffn_all = lax.all_gather(grad_ffn, "tensor", axis=0, tiled=True)
    grad_act = contract_cols(grad_ffn_all, full_down)
    down_grad = contract_rows(activation, grad_ffn_all)
    _, gelu_pull = jax.vjp(partial(jax.nn.gelu, approximate=False), up_value)
    grad_up = gelu_pull(grad_act)[0].astype(jnp.bfloat16)
    up_bias = jnp.sum(grad_up.astype(jnp.float32), axis=0)
    up_grad = contract_rows(normed_all, grad_up)
    normed_terms = contract_cols(grad_up, full_up)
    grad_normed = (
        lax.psum_scatter(
            normed_terms.astype(jnp.bfloat16), "tensor", scatter_dimension=0, tiled=True
        ).astype(jnp.float32)
        + grad_second
    )
    gain_one = jnp.sum(grad_normed * unit_one, axis=0)
    shift_one = jnp.sum(grad_normed, axis=0)
    grad_first = norm_backward(grad_normed, unit_one, rstd_one, gains[0])
    grad_attn = grad_first.astype(jnp.bfloat16)
    out_bias = jnp.sum(grad_attn.astype(jnp.float32), axis=0)
    grad_attn_all = lax.all_gather(grad_attn, "tensor", axis=0, tiled=True)
    out_grad = contract_rows(mixed, grad_attn_all)
    grad_mixed = contract_cols(grad_attn_all, full_out).astype(jnp.bfloat16)
    grad_q, grad_k, grad_v = attend_backward(
        query_rows, key_rows, value_rows, segments, log_totals, grad_mixed, block_rows
    )
    stacked_grads = jnp.stack(
        [grad_q.astype(jnp.bfloat16), grad_k.astype(jnp.bfloat16), grad_v.astype(jnp.bfloat16)]
    )
    qkv_grad = jnp.einsum("td,ktw->kdw", tokens, stacked_grads, preferred_element_type=jnp.float32)
    input_terms = jnp.einsum(
        "ktw,kdw->td", stacked_grads, full_qkv, preferred_element_type=jnp.float32
    )
    grad_input = (
        lax.psum_scatter(
            input_terms.astype(jnp.bfloat16), "tensor", scatter_dimension=0, tiled=True
        ).astype(jnp.float32)
        + grad_first
    )
    qv_grad = jnp.stack(
        [
            jnp.sum(stacked_grads[0].astype(jnp.float32), axis=0),
            jnp.sum(stacked_grads[2].astype(jnp.float32), axis=0),
        ]
    )
    qkv_part, out_part, up_part, down_part = (
        lax.psum_scatter(
            qkv_grad.astype(jnp.bfloat16), "dp", scatter_dimension=1, tiled=True
        ).astype(jnp.float32),
        lax.psum_scatter(
            out_grad.astype(jnp.bfloat16), "dp", scatter_dimension=1, tiled=True
        ).astype(jnp.float32),
        lax.psum_scatter(
            up_grad.astype(jnp.bfloat16), "dp", scatter_dimension=0, tiled=True
        ).astype(jnp.float32),
        lax.psum_scatter(
            down_grad.astype(jnp.bfloat16), "dp", scatter_dimension=1, tiled=True
        ).astype(jnp.float32),
    )
    gain_sum, shift_sum, out_bias_sum, down_bias_sum, proj_sum = lax.psum(
        (
            jnp.stack([gain_one, gain_two]),
            jnp.stack([shift_one, shift_two]),
            out_bias,
            down_bias,
            proj_grad,
        ),
        ("dp", "tensor"),
    )
    qv_sum, up_bias_sum = lax.psum((qv_grad, up_bias), "dp")
    return (
        result_low,
        loss_out,
        grad_input.astype(jnp.bfloat16),
        qkv_part,
        qv_sum,
        out_part,
        out_bias_sum,
        gain_sum,
        shift_sum,
        up_part,
        up_bias_sum,
        down_part,
        down_bias_sum,
        proj_sum,
    )


SWAP = [(0, 1), (1, 0)]
TURN = [(0, 0), (1, 2), (2, 1), (3, 3)]
FAR = [(0, 3), (3, 0), (1, 2), (2, 1)]
NEAR = [(0, 1), (1, 0), (2, 3), (3, 2)]
BF = jnp.bfloat16
F32 = jnp.float32


def dot(left, right):
    return jnp.dot(left, right, preferred_element_type=F32)


CORES = ("c", "y")


def tie(value, *others):
    return lax.optimization_barrier((value,) + others)[0]


def exchange(*moves):
    return lax.optimization_barrier(
        tuple(lax.ppermute(value, axis, steps) for value, axis, steps in moves)
    )


def swap(value, axis):
    return lax.ppermute(value, axis, SWAP)


def pair_up(first, second, own_index, axis):
    return jnp.where(
        own_index == 0, jnp.stack([first, second], axis), jnp.stack([second, first], axis)
    )


def far_pair(value, far, z):
    return jnp.where(z < 2, jnp.stack([value, far]), jnp.stack([far, value]))


def whole_line(pair, other, z):
    return jnp.where(
        (z == 0) | (z == 3),
        jnp.stack([pair[0], other[0], other[1], pair[1]]),
        jnp.stack([other[0], pair[0], pair[1], other[1]]),
    )


def first_moves(line):
    half = line.shape[1] // 2
    return ((line[:, :half], "x", SWAP), (line[:, half:], "y", SWAP))


def first_parts(line, moved, x, y):
    half = line.shape[1] // 2
    return (pair_up(line[:, :half], moved[0], x, 1), pair_up(line[:, half:], moved[1], y, 1))


def last_moves(parts):
    return ((parts[0], "y", SWAP), (parts[1], "x", SWAP))


def full_rows(parts, moved, x, y):
    low = pair_up(parts[0], moved[0], y, 2)
    high = pair_up(parts[1], moved[1], x, 1)
    return jnp.concatenate([low, high], axis=3).reshape(-1, low.shape[-1])


def at(blocks, index, axis):
    return lax.dynamic_index_in_dim(blocks, index, axis, keepdims=False)


def side_move(blocks, axis_name, own_index, axis):
    return (at(blocks, 1 - own_index, axis).astype(BF), axis_name, SWAP)


def side_sum(blocks, got, own_index, axis):
    return at(blocks, own_index, axis).astype(F32) + got.astype(F32)


def near_move(line, z):
    ends = (z == 0) | (z == 3)
    outer, inner = jnp.stack([line[0], line[3]]), line[1:3]
    return (jnp.where(ends, inner, outer).astype(BF), "z", NEAR)


def near_sum(line, got, z):
    ends = (z == 0) | (z == 3)
    return jnp.where(ends, jnp.stack([line[0], line[3]]), line[1:3]) + got.astype(F32)


def far_move(pair, z):
    return (jnp.where(z < 2, pair[1], pair[0]).astype(BF), "z", FAR)


def far_sum(pair, got, z):
    return jnp.where(z < 2, pair[0], pair[1]) + got.astype(F32)


def blocks_of(left, right):
    return contract_rows(left, right).astype(BF).reshape(4, 2, 2, 64, right.shape[1])


def sum_moves(blocks, x, y):
    half = blocks.shape[3] // 2
    return (
        side_move(blocks[..., :half, :], "x", x, 1),
        side_move(blocks[..., half:, :], "y", y, 2),
    )


def sum_parts(blocks, moved, x, y):
    half = blocks.shape[3] // 2
    return (
        side_sum(blocks[..., :half, :], moved[0], x, 1),
        side_sum(blocks[..., half:, :], moved[1], y, 2),
    )


def line_moves(parts, x, y):
    return (side_move(parts[0], "y", y, 1), side_move(parts[1], "x", x, 1))


def line_of(parts, moved, x, y):
    return jnp.concatenate(
        [side_sum(parts[0], moved[0], y, 1), side_sum(parts[1], moved[1], x, 1)], axis=1
    )


def tile_bounds(row_lengths, token_count):
    ends = jnp.cumsum(row_lengths)
    span = NQ_ROW * QLEN
    first = jnp.arange(token_count // TILE, dtype=jnp.int32) * TILE - span
    last = first + TILE - 1
    begin = jnp.max(jnp.where(ends[None, :] <= first[:, None], ends[None, :], 0), axis=1)
    end = jnp.min(jnp.where(ends[None, :] > last[:, None], ends[None, :], token_count), axis=1)
    low = jnp.where(first < 0, 0, (begin + span) // TILE)
    high = jnp.where(first < 0, 1, (end + span + TILE - 1) // TILE)
    return jnp.stack([low, high]).astype(jnp.int32)


def rows_of(value, start, count):
    return lax.dynamic_slice_in_dim(value, start, count, 0)


TILE = 256
NEG = -1e30


def exact(left, right, dims):
    return lax.dot_general(left, right, (dims, ((), ())), preferred_element_type=F32)


def head_masks(value):
    lane = lax.broadcasted_iota(jnp.int32, value.shape, 1)
    zero = jnp.zeros_like(value)
    return (jnp.where(lane < HEAD_DIM, value, zero), jnp.where(lane < HEAD_DIM, zero, value))


def fill_bias(seg_col, seg_row, bias):
    for start in range(0, bias.shape[0], TILE):
        rows = slice(start, start + TILE)
        bias[rows, :] = jnp.where(seg_col[rows, :] == seg_row[...], 0.0, NEG)


def attend_kernel(bounds, q_ref, k_ref, v_ref, seg_col, seg_row, out_ref, lse_ref, bias, held):
    @pl.when(pl.program_id(0) == 0)
    def _():
        fill_bias(seg_col, seg_row, bias)

    for block in range(q_ref.shape[0] // TILE):
        own = slice(block * TILE, (block + 1) * TILE)
        queries = head_masks(q_ref[own, :] * HEAD_DIM**-0.5)

        def score(step, highest):
            rows = pl.ds(pl.multiple_of(step * TILE, TILE), TILE)
            keys, shift = k_ref[rows, :], bias[rows, own]
            fresh = []
            for head in range(2):
                scores = exact(keys, queries[head], ((1,), (1,))) + shift
                held[head, rows, :] = scores
                fresh.append(jnp.maximum(highest[head], jnp.max(scores, axis=0, keepdims=True)))
            return tuple(fresh)

        low = jnp.full((1, TILE), NEG, F32)
        highest = lax.fori_loop(bounds[0, block], bounds[1, block], score, (low, low))

        def mix(step, carried):
            rows = pl.ds(pl.multiple_of(step * TILE, TILE), TILE)
            values = v_ref[rows, :]
            fresh = []
            for head in range(2):
                total, mixed = carried[head]
                expo = jnp.exp(held[head, rows, :] - highest[head])
                fresh.append(
                    (
                        total + jnp.sum(expo, axis=0, keepdims=True),
                        mixed + exact(values, expo.astype(BF), ((0,), (0,))),
                    )
                )
            return tuple(fresh)

        start = (jnp.zeros((1, TILE), F32), jnp.zeros((2 * HEAD_DIM, TILE), F32))
        parts = lax.fori_loop(bounds[0, block], bounds[1, block], mix, (start, start))
        mixed = jnp.concatenate(
            [parts[0][1][:HEAD_DIM] / parts[0][0], parts[1][1][HEAD_DIM:] / parts[1][0]], axis=0
        )
        out_ref[own, :] = jnp.transpose(mixed).astype(BF)
        for head in range(2):
            lse_ref[0, head : head + 1, own] = highest[head] + jnp.log(parts[head][0])


def attend(bounds, qkv, seg_col, seg_row):
    count, wide = qkv.shape
    pairs = wide // 3 // 128
    group = pairs // 2
    column = lambda part: pl.BlockSpec(
        (count, 128), lambda i: (0, (i // group) * 3 * group + part * group + i % group)
    )
    mixed_column = pl.BlockSpec((count, 128), lambda i: (0, i))
    whole = lambda shape: pl.BlockSpec(shape, lambda i: (0, 0))
    return pl.pallas_call(
        attend_kernel,
        grid=(pairs,),
        in_specs=[
            pl.BlockSpec(memory_space=pltpu.SMEM),
            column(0),
            column(1),
            column(2),
            whole((count, 1)),
            whole((1, count)),
        ],
        out_specs=[mixed_column, pl.BlockSpec((1, 8, count), lambda i: (i, 0, 0))],
        out_shape=[
            jax.ShapeDtypeStruct((count, wide // 3), BF),
            jax.ShapeDtypeStruct((pairs, 8, count), F32),
        ],
        scratch_shapes=[pltpu.VMEM((count, count), F32), pltpu.VMEM((2, count, TILE), F32)],
        compiler_params=pltpu.CompilerParams(vmem_limit_bytes=40 << 20),
        cost_estimate=pl.CostEstimate(
            flops=4 * pairs * count * count * 128,
            transcendentals=pairs * count * count,
            bytes_accessed=4 * count * wide * 2,
        ),
    )(bounds, qkv, qkv, qkv, seg_col, seg_row)


def attend_back_kernel(
    bounds, q_ref, k_ref, v_ref, out_ref, grad_ref, lse_ref, seg_col, seg_row,
    grads_ref, sums_ref, bias, key_sum, value_sum,
):
    pair = pl.program_id(0)

    @pl.when(pair == 0)
    def _():
        fill_bias(seg_col, seg_row, bias)

    key_sum[...] = jnp.zeros_like(key_sum)
    value_sum[...] = jnp.zeros_like(value_sum)
    columns = [
        pl.ds(pl.multiple_of(part * (grads_ref.shape[1] // 3) + pair * 128, 128), 128) for part in range(3)
    ]
    query_total = jnp.zeros((1, 128), F32)
    picks = head_masks(jnp.ones((8, 128), BF))
    for block in range(q_ref.shape[0] // TILE):
        own = slice(block * TILE, (block + 1) * TILE)
        queries = head_masks(q_ref[own, :] * HEAD_DIM**-0.5)
        grads = head_masks(grad_ref[own, :])
        product = grad_ref[own, :].astype(F32) * out_ref[own, :].astype(F32)
        product_high = product.astype(BF)
        product_low = (product - product_high.astype(F32)).astype(BF)
        inner = [
            (
                exact(picks[head], product_high, ((1,), (1,)))
                + exact(picks[head], product_low, ((1,), (1,)))
            )[0:1]
            for head in range(2)
        ]
        lse = [lse_ref[0, head : head + 1, own] for head in range(2)]

        def step_of(step, carried):
            rows = pl.ds(pl.multiple_of(step * TILE, TILE), TILE)
            keys, values, shift = k_ref[rows, :], v_ref[rows, :], bias[rows, own]
            fresh = []
            key_add = jnp.zeros((TILE, 128), F32)
            value_add = jnp.zeros((TILE, 128), F32)
            for head in range(2):
                scores = exact(keys, queries[head], ((1,), (1,))) + shift
                probs = jnp.exp(scores - lse[head])
                grad_probs = exact(values, grads[head], ((1,), (1,)))
                grad_scores = (probs * (grad_probs - inner[head])).astype(BF)
                value_add = value_add + exact(probs.astype(BF), grads[head], ((1,), (0,)))
                key_add = key_add + exact(grad_scores, queries[head], ((1,), (0,)))
                fresh.append(carried[head] + exact(keys, grad_scores, ((0,), (0,))))
            key_sum[rows, :] += key_add
            value_sum[rows, :] += value_add
            return tuple(fresh)

        start = jnp.zeros((2 * HEAD_DIM, TILE), F32)
        parts = lax.fori_loop(bounds[0, block], bounds[1, block], step_of, (start, start))
        grad_query = jnp.concatenate([parts[0][:HEAD_DIM], parts[1][HEAD_DIM:]], axis=0)
        grad_query = jnp.transpose(grad_query * HEAD_DIM**-0.5).astype(BF)
        grads_ref[own, columns[0]] = grad_query
        query_total = query_total + jnp.sum(grad_query.astype(F32), axis=0, keepdims=True)
    grad_value = value_sum[...].astype(BF)
    grads_ref[:, columns[1]] = key_sum[...].astype(BF)
    grads_ref[:, columns[2]] = grad_value
    sums_ref[0, 0:1, :] = query_total
    sums_ref[0, 1:2, :] = jnp.sum(grad_value.astype(F32), axis=0, keepdims=True)


def attend_back(bounds, group, qkv, mixed, grad_mixed, lse, seg_col, seg_row):
    count = qkv.shape[0]
    wide = qkv.shape[1] // 2
    pairs = wide // 3 // 128
    column = lambda shift: pl.BlockSpec((count, 128), lambda i: (0, shift + i))
    whole = lambda shape: pl.BlockSpec(shape, lambda i: (0, 0))
    first = group * pairs
    return pl.pallas_call(
        attend_back_kernel,
        grid=(pairs,),
        in_specs=[
            pl.BlockSpec(memory_space=pltpu.SMEM),
            column(3 * first),
            column(3 * first + pairs),
            column(3 * first + 2 * pairs),
            column(first),
            column(first),
            pl.BlockSpec((1, 8, count), lambda i: (first + i, 0, 0)),
            whole((count, 1)),
            whole((1, count)),
        ],
        out_specs=[whole((count, wide)), pl.BlockSpec((1, 8, 128), lambda i: (i, 0, 0))],
        out_shape=[
            jax.ShapeDtypeStruct((count, wide), BF),
            jax.ShapeDtypeStruct((pairs, 8, 128), F32),
        ],
        scratch_shapes=[
            pltpu.VMEM((count, count), F32),
            pltpu.VMEM((count, 128), F32),
            pltpu.VMEM((count, 128), F32),
        ],
        compiler_params=pltpu.CompilerParams(vmem_limit_bytes=40 << 20),
        cost_estimate=pl.CostEstimate(
            flops=10 * pairs * count * count * 128,
            transcendentals=pairs * count * count,
            bytes_accessed=8 * count * wide * 2,
        ),
    )(bounds, qkv, qkv, qkv, mixed, grad_mixed, lse, seg_col, seg_row)


ERFC = (
    -1.26551223, 1.00002368, 0.37409196, 0.09678418, -0.18628806,
    0.27886807, -1.13520398, 1.48851587, -0.82215223, 0.17087277,
)


def gelu_pair(value):
    size = jnp.abs(value) * 0.5**0.5
    ratio = 1.0 / (1.0 + 0.5 * size)
    series = jnp.full_like(value, ERFC[-1])
    for factor in ERFC[-2::-1]:
        series = series * ratio + factor
    bell = jnp.exp(-size * size)
    tail = 0.5 * ratio * bell * jnp.exp(series)
    phi = jnp.where(value < 0.0, tail, 1.0 - tail)
    return (value * phi, phi + value * bell * 0.3989422804014327)


def expand_kernel(x_ref, w_ref, b_ref, act_ref, slope_ref):
    rows = 256
    for start in range(0, x_ref.shape[0], rows):
        part = slice(start, start + rows)
        value = exact(x_ref[part, :], w_ref[...], ((1,), (0,))) + b_ref[...]
        active, slope = gelu_pair(value)
        act_ref[part, :] = active.astype(BF)
        slope_ref[part, :] = slope.astype(BF)


def expand(value, weight, shift):
    count, depth = value.shape
    width = shift.shape[1]
    tile = 256
    return pl.pallas_call(
        expand_kernel,
        grid=(width // tile,),
        in_specs=[
            pl.BlockSpec((count, depth), lambda i: (0, 0)),
            pl.BlockSpec((depth, tile), lambda i: (0, i)),
            pl.BlockSpec((1, tile), lambda i: (0, i)),
        ],
        out_specs=[pl.BlockSpec((count, tile), lambda i: (0, i))] * 2,
        out_shape=[jax.ShapeDtypeStruct((count, width), BF)] * 2,
        compiler_params=pltpu.CompilerParams(vmem_limit_bytes=32 << 20),
        cost_estimate=pl.CostEstimate(
            flops=2 * count * depth * width,
            transcendentals=3 * count * width,
            bytes_accessed=2 * (count * depth + depth * width + 2 * count * width),
        ),
    )(value, weight, shift)


def cut_levels(raw, cuts):
    lane = lax.broadcasted_iota(jnp.int32, raw.shape, 1)
    levels = []
    for cut in cuts:
        part = jnp.where(lane < cut, raw, 0.0)
        scale = lax.rsqrt(jnp.sum(part * part, axis=1, keepdims=True) + EPS_EMBED)
        levels.append(((part * scale).astype(BF), part, scale))
    return levels


def pool_kernel(cuts, span, q_ref, d_ref, seg_ref, out_ref, units, hot):
    @pl.when(pl.program_id(0) == 0)
    def _():
        raw = d_ref[span:, :].astype(F32)
        for level, parts in enumerate(cut_levels(raw, cuts)):
            units[level] = parts[0]
        doc = lax.broadcasted_iota(jnp.int32, hot.shape, 0)
        hot[...] = (seg_ref[:, span:] == NQ_ROW + doc).astype(F32).astype(BF)

    levels = cut_levels(q_ref[...].astype(F32), cuts)
    for level in range(len(cuts)):
        similar = exact(units[level], levels[level][0], ((1,), (1,)))
        expo = jnp.exp(similar * (1.0 / POOL_TEMP))
        high = expo.astype(BF)
        rest = (expo - high.astype(F32)).astype(BF)
        out_ref[level * NDOC : (level + 1) * NDOC, :] = exact(
            hot[...], high, ((1,), (0,))
        ) + exact(hot[...], rest, ((1,), (0,)))


def pool(cuts, span, queries, row_embed, seg_row):
    count, width = queries.shape
    tokens = row_embed.shape[0]
    whole = lambda shape: pl.BlockSpec(shape, lambda i: (0, 0))
    return pl.pallas_call(
        partial(pool_kernel, cuts, span),
        grid=(count // TILE,),
        in_specs=[
            pl.BlockSpec((TILE, width), lambda i: (i, 0)),
            whole((tokens, width)),
            whole((1, tokens)),
        ],
        out_specs=pl.BlockSpec((len(cuts) * NDOC, TILE), lambda i: (0, i)),
        out_shape=jax.ShapeDtypeStruct((len(cuts) * NDOC, count), F32),
        scratch_shapes=[
            pltpu.VMEM((len(cuts), tokens - span, width), BF),
            pltpu.VMEM((NDOC, tokens - span), BF),
        ],
        compiler_params=pltpu.CompilerParams(vmem_limit_bytes=32 << 20),
        cost_estimate=pl.CostEstimate(
            flops=2 * len(cuts) * count * tokens * 256,
            transcendentals=len(cuts) * count * tokens,
            bytes_accessed=2 * (count + tokens) * width,
        ),
    )(queries, row_embed, seg_row)


def level_back(grad, part, scale):
    return scale * grad - part * (scale * scale * scale) * jnp.sum(
        part * grad, axis=1, keepdims=True
    )


def pool_back_kernel(
    cuts, span, q_ref, d_ref, seg_ref, coef_ref, q_out, d_out, units, units_t, hot, sums
):
    step = pl.program_id(0)

    @pl.when(step == 0)
    def _():
        raw = d_ref[span:, :].astype(F32)
        for level, parts in enumerate(cut_levels(raw, cuts)):
            units[level] = parts[0]
            units_t[level] = jnp.transpose(parts[0])
        doc = lax.broadcasted_iota(jnp.int32, hot.shape, 0)
        wanted = NQ_ROW + jnp.where(doc < NDOC, doc, doc - NDOC)
        hot[...] = (seg_ref[:, span:] == wanted).astype(F32).astype(BF)
        sums[...] = jnp.zeros_like(sums)

    levels = cut_levels(q_ref[...].astype(F32), cuts)
    total = jnp.zeros(q_ref.shape, F32)
    for level in range(len(cuts)):
        unit, part, scale = levels[level]
        similar = exact(units[level], unit, ((1,), (1,)))
        coef = coef_ref[level * NDOC : (level + 1) * NDOC, :]
        high = coef.astype(BF).astype(F32)
        both = jnp.concatenate([high, coef - high], axis=0).astype(BF)
        spread = exact(hot[...], both, ((0,), (0,)))
        grad = (jnp.exp(similar * (1.0 / POOL_TEMP)) * spread).astype(BF)
        sums[level] += exact(grad, unit, ((1,), (0,)))
        grad_unit = jnp.transpose(exact(units_t[level], grad, ((1,), (0,))))
        total = total + level_back(grad_unit, part, scale)
    q_out[...] = total.astype(BF)

    @pl.when(step == pl.num_programs(0) - 1)
    def _():
        raw = d_ref[span:, :].astype(F32)
        result = jnp.zeros(raw.shape, F32)
        for level, parts in enumerate(cut_levels(raw, cuts)):
            lane = lax.broadcasted_iota(jnp.int32, raw.shape, 1)
            grad = jnp.where(lane < cuts[level], sums[level], 0.0)
            result = result + level_back(grad, parts[1], parts[2])
        d_out[...] = result


def pool_back(cuts, span, queries, row_embed, seg_row, coef):
    count, width = queries.shape
    tokens = row_embed.shape[0]
    docs = tokens - span
    whole = lambda shape: pl.BlockSpec(shape, lambda i: (0, 0))
    return pl.pallas_call(
        partial(pool_back_kernel, cuts, span),
        grid=(count // TILE,),
        in_specs=[
            pl.BlockSpec((TILE, width), lambda i: (i, 0)),
            whole((tokens, width)),
            whole((1, tokens)),
            pl.BlockSpec((len(cuts) * NDOC, TILE), lambda i: (0, i)),
        ],
        out_specs=[pl.BlockSpec((TILE, width), lambda i: (i, 0)), whole((docs, width))],
        out_shape=[
            jax.ShapeDtypeStruct((count, width), BF),
            jax.ShapeDtypeStruct((docs, width), F32),
        ],
        scratch_shapes=[
            pltpu.VMEM((len(cuts), docs, width), BF),
            pltpu.VMEM((len(cuts), width, docs), BF),
            pltpu.VMEM((2 * NDOC, docs), BF),
            pltpu.VMEM((len(cuts), docs, width), F32),
        ],
        compiler_params=pltpu.CompilerParams(vmem_limit_bytes=32 << 20),
        cost_estimate=pl.CostEstimate(
            flops=2 * len(cuts) * count * docs * 512,
            transcendentals=len(cuts) * count * docs,
            bytes_accessed=4 * (count + tokens) * width,
        ),
    )(queries, row_embed, seg_row, coef)


def local_chip(
    tokens,
    lengths,
    pairing,
    w_qkv,
    b_qv,
    w_out,
    b_out,
    ln_gain,
    ln_bias,
    w_up,
    b_up,
    w_down,
    b_down,
    w_proj,
    cot,
):
    z, x, c, y = (lax.axis_index(name) for name in ("z", "x", "c", "y"))
    chip = 4 * z + 2 * x + y
    token_count, width = tokens.shape
    share = token_count // 2
    own_start, other_start = c * share, (1 - c) * share
    gains, shifts = ln_gain.astype(F32), ln_bias.astype(F32)

    half_width = w_qkv.shape[2]
    up_wide = w_up.shape[1]
    chip_count = lengths.shape[0]
    half_queries = NQ_ROW // 2
    query_total = chip_count * half_queries
    quarter = half_width // 2
    qkv_rows = jnp.concatenate(
        [w_qkv[k][:, g * quarter : (g + 1) * quarter] for g in range(2) for k in range(3)], axis=1
    )
    pair_rows = jnp.pad(pairing.astype(BF), ((0, 63), (0, 128 - half_queries)))
    mid_rows = jnp.concatenate([w_up, w_out.T, pair_rows], axis=1)
    bias = jnp.concatenate([b_qv.reshape(-1), b_up])[None].astype(F32)
    got = exchange(
        (qkv_rows, CORES, TURN), (tokens, "c", SWAP), (bias, "y", SWAP)
    )
    qkv_rows = got[0]
    row = jnp.where(c == y, tokens, got[1])
    bias = jnp.where(c == y, bias, got[2])
    (rest_rows,) = exchange(
        (tie(jnp.concatenate([mid_rows, w_down.T], axis=1), row), CORES, TURN)
    )
    (far,) = exchange((qkv_rows, "z", FAR))
    qkv_pair = far_pair(qkv_rows, far, z)
    mid_wide = mid_rows.shape[1]
    rest_rows = tie(rest_rows, qkv_pair)
    mid_rows, down_rows = rest_rows[:, :mid_wide], rest_rows[:, mid_wide:]
    got = exchange((qkv_pair, "z", NEAR), (mid_rows, "z", FAR))
    qkv_line = whole_line(qkv_pair, got[0], z)
    mid_pair = far_pair(mid_rows, got[1], z)
    got = exchange(*first_moves(qkv_line), (mid_pair, "z", NEAR))
    qkv_parts = first_parts(qkv_line, got, x, y)
    mid_line = whole_line(mid_pair, got[2], z)
    last = last_moves(qkv_parts)
    got = exchange(*last, (tie(down_rows, mid_line), "z", FAR), *first_moves(mid_line))
    full_qkv = full_rows(qkv_parts, got, x, y)
    down_pair = far_pair(down_rows, got[2], z)
    mid_parts = first_parts(mid_line, got[3:], x, y)
    (near,) = exchange((down_pair, "z", NEAR))
    down_line = whole_line(down_pair, near, z)
    got = exchange(*last_moves(mid_parts), *first_moves(down_line))
    full_mid = full_rows(mid_parts, got, x, y)
    down_parts = first_parts(down_line, got[2:], x, y)
    got = exchange(*last_moves(down_parts))
    full_down = full_rows(down_parts, got, x, y)
    full_out = full_mid[:, up_wide : up_wide + half_width]
    pairs = full_mid[:, up_wide + half_width :].reshape(chip_count, 64, 128)
    pairs = pairs[:, 0, :half_queries].astype(jnp.int32).reshape(1, query_total)
    row_lengths = lax.dynamic_index_in_dim(lengths, chip, 0, keepdims=False)
    segments = segments_of(row_lengths, token_count)
    seg_col, seg_row = segments[:, None], segments[None, :]
    query_span = NQ_ROW * QLEN
    bounds = tile_bounds(row_lengths, token_count)
    no_bias = jnp.zeros((1, quarter), F32)
    qkv_bias = jnp.concatenate(
        [
            part
            for g in range(2)
            for part in (
                bias[:, g * quarter : (g + 1) * quarter],
                no_bias,
                bias[:, half_width + g * quarter : half_width + (g + 1) * quarter],
            )
        ],
        axis=1,
    )
    qkv = (dot(row, full_qkv) + qkv_bias).astype(BF)
    mixed, lse = attend(bounds, qkv, seg_col, seg_row)

    def row_sum(left, weight_t, transposed):
        times = contract_cols if transposed else dot
        theirs = swap(times(left(1), weight_t).astype(BF), "c")
        return times(left(0), weight_t) + theirs.astype(F32)

    def mixed_half(which):
        return rows_of(mixed, other_start if which else own_start, share)

    attn_sum = row_sum(mixed_half, full_out, True)
    own_tokens = rows_of(row, own_start, share).astype(F32)
    normed, unit_one, rstd_one = norm_forward(
        own_tokens + attn_sum + b_out.astype(F32), gains[0], shifts[0]
    )
    normed_low = normed.astype(BF)
    normed_all = jnp.concatenate([normed_low, swap(normed_low, "c")], axis=0)
    activation, slope = expand(normed_all, full_mid, bias[:, 2 * half_width :])
    ffn_sum = row_sum(
        lambda which: activation[which * share : (which + 1) * share], full_down, True
    )
    result, unit_two, rstd_two = norm_forward(
        normed + ffn_sum + b_down.astype(F32), gains[1], shifts[1]
    )
    result_low = result.astype(BF)
    embed = dot(result_low, w_proj).astype(BF)

    other_embed = swap(embed, "c")
    row_embed = jnp.where(
        c == 0,
        jnp.concatenate([embed, other_embed], axis=0),
        jnp.concatenate([other_embed, embed], axis=0),
    )
    half_span = query_span // 2
    own_queries = rows_of(row_embed, c * half_span, half_span)
    chips = ("z", "x", "y")
    queries = lax.all_to_all(
        jnp.broadcast_to(own_queries[None], (chip_count,) + own_queries.shape), chips, 0, 0
    ).reshape(chip_count * half_span, -1)
    proj_width = w_proj.shape[1]
    cuts = (proj_width, 3 * proj_width // 4, proj_width // 2)
    sums = pool(cuts, query_span, queries, row_embed, seg_row)
    doc_sizes = jnp.tile(row_lengths.astype(F32), 3)[:, None]
    group = (
        jnp.arange(query_total * QLEN, dtype=jnp.int32)[:, None] // QLEN
        == jnp.arange(query_total, dtype=jnp.int32)[None, :]
    ).astype(F32)
    pooled = POOL_TEMP * jnp.log(sums / doc_sizes)
    logits = jnp.dot(pooled, group, precision=FULL_PRECISION) / LOSS_TEMP
    logits = logits.reshape(3, NDOC, query_total)
    doc_numbers = chip * NDOC + jnp.arange(NDOC, dtype=jnp.int32)
    picked = (doc_numbers[:, None] == pairs).astype(F32)
    own_high = jnp.max(logits, axis=1)
    own_lse = own_high + jnp.log(jnp.sum(jnp.exp(logits - own_high[:, None]), axis=1))
    own_target = jnp.sum(logits * picked, axis=1)
    notes = jnp.pad(jnp.concatenate([own_lse, own_target], axis=1), ((0, 5), (0, 0)))
    notes = lax.all_to_all(
        jnp.broadcast_to(notes[None], (chip_count,) + notes.shape), chips, 0, 0
    )
    chip_lse = notes[:, :3, :query_total]
    high = jnp.max(chip_lse, axis=0)
    all_lse = high + jnp.log(jnp.sum(jnp.exp(chip_lse - high), axis=0))
    target = jnp.sum(notes[:, :3, query_total:], axis=0)
    losses = jnp.sum(all_lse - target, axis=0).reshape(chip_count, half_queries)
    grad_logits = (jnp.exp(logits - all_lse[:, None]) - picked) / LOSS_TEMP
    coefficient = (
        lax.dot_general(
            grad_logits.reshape(3 * NDOC, query_total),
            group,
            (((1,), (1,)), ((), ())),
            precision=FULL_PRECISION,
        )
        / sums
    )
    losses = jnp.where(c == y, losses, swap(losses, "c"))
    loss_out = rows_of(losses, 4 * z + 2 * x + c, 1)
    y_out, own_cot = exchange((result_low, CORES, TURN), (tie(cot, queries), CORES, TURN))
    query_grad, doc_grad = pool_back(cuts, query_span, tie(queries, y_out, own_cot), row_embed, seg_row, coefficient)
    grad_blocks = lax.all_to_all(
        query_grad.reshape(chip_count, half_span, proj_width), chips, 0, 0
    )
    own_query_grad = jnp.sum(grad_blocks.astype(F32), axis=0)
    row_grad = jnp.concatenate([jnp.zeros((query_span, proj_width), F32), doc_grad], axis=0)
    row_grad = lax.dynamic_update_slice_in_dim(row_grad, own_query_grad, c * half_span, 0)
    grad_embed = rows_of(row_grad, own_start, share) + swap(
        rows_of(row_grad, other_start, share), "c"
    )

    proj_low = w_proj
    grad_embed_low = grad_embed.astype(BF)
    grad_embed_rest = (grad_embed - grad_embed_low.astype(F32)).astype(BF)
    grad_result = own_cot.astype(F32) + (
        contract_cols(grad_embed_low, proj_low) + contract_cols(grad_embed_rest, proj_low)
    )
    proj_grad = contract_rows(result_low, grad_embed_low) + contract_rows(
        result_low, grad_embed_rest
    )
    gain_two = jnp.sum(grad_result * unit_two, axis=0)
    shift_two = jnp.sum(grad_result, axis=0)
    grad_second = norm_backward(grad_result, unit_two, rstd_two, gains[1])
    grad_ffn = grad_second.astype(BF)
    down_bias = jnp.sum(grad_ffn.astype(F32), axis=0)
    grad_ffn_all = jnp.concatenate([grad_ffn, swap(grad_ffn, "c")], axis=0)
    down_blocks = blocks_of(grad_ffn_all, activation)
    grad_ffn_all = tie(grad_ffn_all, down_blocks)
    down_moved = exchange(*sum_moves(down_blocks, x, y))
    grad_up = (dot(grad_ffn_all, full_down) * slope.astype(F32)).astype(BF)
    up_bias = jnp.sum(grad_up.astype(F32), axis=0)
    up_blocks = blocks_of(normed_all, tie(grad_up, *down_moved))
    down_parts = sum_parts(down_blocks, down_moved, x, y)
    moved = exchange(*line_moves(down_parts, x, y), *sum_moves(up_blocks, x, y))
    down_line = line_of(down_parts, moved, x, y)
    up_parts = sum_parts(up_blocks, moved[2:], x, y)
    full_up = full_mid[:, :up_wide]
    grad_normed = (
        row_sum(lambda which: grad_up[which * share : (which + 1) * share], full_up, True)
        + grad_second
    )
    gain_one = jnp.sum(grad_normed * unit_one, axis=0)
    shift_one = jnp.sum(grad_normed, axis=0)
    grad_first = norm_backward(grad_normed, unit_one, rstd_one, gains[0])
    grad_attn = grad_first.astype(BF)
    out_bias = jnp.sum(grad_attn.astype(F32), axis=0)
    other_attn = swap(grad_attn, "c")
    grad_attn_all = jnp.where(
        c == 0,
        jnp.concatenate([grad_attn, other_attn], axis=0),
        jnp.concatenate([other_attn, grad_attn], axis=0),
    )
    grad_mixed = dot(grad_attn_all, full_out).astype(BF)
    out_blocks = blocks_of(grad_attn_all, mixed)
    grad_mixed, out_blocks, down_line, *up_parts = lax.optimization_barrier(
        (grad_mixed, out_blocks, down_line) + tuple(up_parts)
    )
    moved = exchange(
        near_move(down_line, z), *line_moves(up_parts, x, y), *sum_moves(out_blocks, x, y)
    )
    grads_one, sums_one = attend_back(bounds, 0, qkv, mixed, grad_mixed, lse, seg_col, seg_row)
    down_pair = near_sum(down_line, moved[0], z)
    up_line = line_of(up_parts, moved[1:], x, y)
    out_parts = sum_parts(out_blocks, moved[3:], x, y)
    grad_mixed, down_pair, up_line, *out_parts = lax.optimization_barrier(
        (grad_mixed, down_pair, up_line) + tuple(out_parts)
    )
    moved = exchange(
        far_move(down_pair, z), near_move(up_line, z), *line_moves(out_parts, x, y)
    )
    grads_two, sums_two = attend_back(
        bounds, 1, qkv, mixed, tie(grad_mixed, grads_one), lse, seg_col, seg_row
    )
    down_part = far_sum(down_pair, moved[0], z)
    up_pair = near_sum(up_line, moved[1], z)
    out_line = line_of(out_parts, moved[2:], x, y)
    grads_one, grads_two, down_part, up_pair, out_line = lax.optimization_barrier(
        (grads_one, grads_two, down_part, up_pair, out_line)
    )
    proj_half = rows_of(proj_grad, own_start, share) + swap(
        rows_of(proj_grad, other_start, share), "c"
    )
    shared = jnp.stack([gain_one, gain_two, shift_one, shift_two, out_bias, down_bias])
    half_sums = jnp.concatenate(
        [
            sums_one[:, 0].reshape(-1),
            sums_two[:, 0].reshape(-1),
            sums_one[:, 1].reshape(-1),
            sums_two[:, 1].reshape(-1),
            up_bias,
        ]
    )
    small = jnp.concatenate([shared.reshape(-1, 128), half_sums.reshape(-1, 128), proj_half])

    qkv_blocks = jnp.concatenate(
        [blocks_of(row, grads_one), blocks_of(row, grads_two)], axis=4
    )
    moved = exchange(
        *sum_moves(qkv_blocks, x, y), far_move(up_pair, z), near_move(out_line, z)
    )
    qkv_parts = sum_parts(qkv_blocks, moved, x, y)
    up_part = far_sum(up_pair, moved[2], z)
    out_pair = near_sum(out_line, moved[3], z)

    def input_terms(start):
        return contract_cols(
            rows_of(grads_one, start, share), full_qkv[:, : 3 * quarter]
        ) + contract_cols(rows_of(grads_two, start, share), full_qkv[:, 3 * quarter :])

    other_terms = swap(input_terms(other_start).astype(BF), "c")
    grad_input = (input_terms(own_start) + other_terms.astype(F32) + grad_first).astype(BF)
    moved = exchange(*line_moves(qkv_parts, x, y), far_move(out_pair, z), (small, "y", SWAP))
    qkv_line = line_of(qkv_parts, moved, x, y)
    out_part = far_sum(out_pair, moved[2], z)
    small = small + moved[3]
    rest_part = jnp.concatenate([down_part, up_part, out_part], axis=1).astype(BF)
    moved = exchange(
        near_move(qkv_line, z), (small, "x", SWAP), (rest_part, CORES, TURN),
        (tie(grad_input, qkv_line), CORES, TURN),
    )
    qkv_pair = near_sum(qkv_line, moved[0], z)
    small = small + moved[1]
    rest_part = moved[2].astype(F32)
    grad_input = moved[3]
    down_part, up_part, out_part = (
        rest_part[:, :up_wide],
        rest_part[:, up_wide : 2 * up_wide],
        rest_part[:, 2 * up_wide :],
    )
    moved = exchange(far_move(qkv_pair, z), (small, "z", FAR))
    qkv_part = far_sum(qkv_pair, moved[0], z).astype(BF)
    small = small + moved[1]
    moved = exchange((qkv_part, CORES, TURN), (small, "z", NEAR))
    qkv_part = moved[0].astype(F32)
    small = small + moved[1]
    other_small = swap(small, "c")
    shared_rows = 6 * width // 128
    small_rows = small.shape[0] - share
    shared = (small[:shared_rows] + other_small[:shared_rows]).reshape(6, width)
    half_sums = jnp.where(
        c == y, small[shared_rows:small_rows], other_small[shared_rows:small_rows]
    ).reshape(-1)
    proj_sum = pair_up(small[small_rows:], other_small[small_rows:], c, 0).reshape(width, -1)
    qkv_part = qkv_part.reshape(64, 2, 3, quarter).transpose(2, 0, 1, 3).reshape(3, 64, half_width)
    return (
        y_out,
        loss_out,
        grad_input,
        qkv_part,
        half_sums[: 2 * half_width].reshape(2, half_width),
        out_part.T,
        shared[4],
        shared[0:2],
        shared[2:4],
        up_part,
        half_sums[2 * half_width :],
        down_part.T,
        shared[5],
        proj_sum,
    )


IN_SPECS = (
    P("dp", None),
    P(),
    P("dp", "tensor"),
    P(None, "dp", "tensor"),
    P(None, "tensor"),
    P("tensor", "dp"),
    P(),
    P(),
    P(),
    P("dp", "tensor"),
    P("tensor"),
    P("tensor", "dp"),
    P(),
    P(),
    P(("dp", "tensor"), None),
)
OUT_SPECS = (
    P(("dp", "tensor"), None),
    P("dp", "tensor"),
    P(("dp", "tensor"), None),
    P(None, "dp", "tensor"),
    P(None, "tensor"),
    P("tensor", "dp"),
    P(),
    P(),
    P(),
    P("dp", "tensor"),
    P("tensor"),
    P("tensor", "dp"),
    P(),
    P(),
)


def solution(mesh):
    if mesh.devices.shape != (16, 2):
        return jax.shard_map(
            local, mesh=mesh, in_specs=IN_SPECS, out_specs=OUT_SPECS, check_vma=False
        )
    names = {"dp": ("z", "x", "c"), "tensor": ("y",)}

    def respec(spec):
        parts = []
        for entry in spec:
            axes = () if entry is None else entry if isinstance(entry, tuple) else (entry,)
            parts.append(tuple(name for axis in axes for name in names[axis]) or None)
        return P(*parts)

    chips = Mesh(mesh.devices.reshape(4, 2, 2, 2), ("z", "x", "c", "y"))
    return jax.shard_map(
        local_chip,
        mesh=chips,
        in_specs=tuple(respec(spec) for spec in IN_SPECS),
        out_specs=tuple(respec(spec) for spec in OUT_SPECS),
        check_vma=False,
    )
```

```python
from functools import partial

import jax
import jax.numpy as jnp
from jax import lax
from jax.experimental import pallas as pl
from jax.experimental.pallas import tpu as pltpu
from jax.sharding import Mesh, PartitionSpec as P

HEAD_DIM = 64
QLEN = 32
NQ_ROW = 8
NDOC = 8


EPS_NORM = 1e-05
EPS_EMBED = 1e-06
POOL_TEMP = 0.1
LOSS_TEMP = 0.1
FULL_PRECISION = lax.Precision.HIGHEST
MASKED_SCORE = -1e30


def shortened(shard):

    def short(part):
        return part.astype(jnp.bfloat16) if part.dtype == jnp.float32 else part

    return jax.tree.map(short, shard)


def contract_rows(left, right, precision=None):
    return lax.dot_general(
        left,
        right,
        (((0,), (0,)), ((), ())),
        precision=precision,
        preferred_element_type=jnp.float32,
    )


def contract_cols(left, right, precision=None):
    return lax.dot_general(
        left,
        right,
        (((1,), (1,)), ((), ())),
        precision=precision,
        preferred_element_type=jnp.float32,
    )


def norm_forward(value, gain, shift):
    centred = value - jnp.mean(value, axis=1, keepdims=True)
    rstd = lax.rsqrt(jnp.mean(centred * centred, axis=1, keepdims=True) + EPS_NORM)
    unit = centred * rstd
    return (unit * gain + shift, unit, rstd)


def norm_backward(grad, unit, rstd, gain):
    scaled = grad * gain
    return rstd * (
        scaled
        - jnp.mean(scaled, axis=1, keepdims=True)
        - unit * jnp.mean(scaled * unit, axis=1, keepdims=True)
    )


def segments_of(row_lengths, token_count):
    position = jnp.arange(token_count, dtype=jnp.int32)
    query_span = NQ_ROW * QLEN
    ends = jnp.cumsum(row_lengths)
    passed = jnp.sum((position[:, None] - query_span >= ends[None, :]).astype(jnp.int32), axis=1)
    return jnp.where(position < query_span, position // QLEN, NQ_ROW + passed)


def normalize_cut(raw, width):
    part = raw[:, :width]
    scale = lax.rsqrt(jnp.sum(part * part, axis=1, keepdims=True) + EPS_EMBED)
    return (part * scale, part, scale)


def normalize_back(grad, part, scale, full_width):
    result = scale * grad - part * (scale * scale * scale) * jnp.sum(
        part * grad, axis=1, keepdims=True
    )
    return jnp.pad(result, ((0, 0), (0, full_width - grad.shape[1])))


def masked_scores(query_block, key_rows, block_segments, segments):
    scores = jnp.einsum(
        "qhd,khd->hqk", query_block, key_rows, preferred_element_type=jnp.float32
    ) * HEAD_DIM ** (-0.5)
    return jnp.where((block_segments[:, None] == segments[None, :])[None], scores, MASKED_SCORE)


def attend_forward(query_rows, key_rows, value_rows, segments, block_rows):
    token_count = query_rows.shape[0]

    def one_block(block_start):
        query_block = lax.dynamic_slice_in_dim(query_rows, block_start, block_rows, 0)
        block_segments = lax.dynamic_slice_in_dim(segments, block_start, block_rows, 0)
        scores = masked_scores(query_block, key_rows, block_segments, segments)
        highest = jnp.max(scores, axis=2, keepdims=True)
        expo = jnp.exp(scores - highest)
        totals = jnp.sum(expo, axis=2, keepdims=True)
        weights = (expo / totals).astype(jnp.bfloat16)
        mixed = jnp.einsum("hqk,khd->qhd", weights, value_rows, preferred_element_type=jnp.float32)
        return (mixed.astype(jnp.bfloat16), (highest + jnp.log(totals))[:, :, 0])

    starts = jnp.arange(token_count // block_rows, dtype=jnp.int32) * block_rows
    mixed, log_totals = lax.map(one_block, starts)
    return (mixed.reshape(token_count, -1), log_totals)


def attend_backward(query_rows, key_rows, value_rows, segments, log_totals, grad_mixed, block_rows):
    token_count, local_heads, head_size = query_rows.shape
    scale = HEAD_DIM ** (-0.5)
    grad_heads = grad_mixed.reshape(token_count, local_heads, head_size)

    def one_block(carried, inputs):
        grad_keys, grad_values = carried
        block_start, block_lse = inputs
        query_block = lax.dynamic_slice_in_dim(query_rows, block_start, block_rows, 0)
        grad_block = lax.dynamic_slice_in_dim(grad_heads, block_start, block_rows, 0)
        block_segments = lax.dynamic_slice_in_dim(segments, block_start, block_rows, 0)
        scores = masked_scores(query_block, key_rows, block_segments, segments)
        probs = jnp.exp(scores - block_lse[:, :, None])
        grad_probs = jnp.einsum(
            "qhd,khd->hqk", grad_block, value_rows, preferred_element_type=jnp.float32
        )
        inner = jnp.sum(probs * grad_probs, axis=2, keepdims=True)
        grad_scores = (probs * (grad_probs - inner)).astype(jnp.bfloat16)
        grad_query = (
            jnp.einsum("hqk,khd->qhd", grad_scores, key_rows, preferred_element_type=jnp.float32)
            * scale
        )
        grad_keys = (
            grad_keys
            + jnp.einsum(
                "hqk,qhd->khd", grad_scores, query_block, preferred_element_type=jnp.float32
            )
            * scale
        )
        grad_values = grad_values + jnp.einsum(
            "hqk,qhd->khd",
            probs.astype(jnp.bfloat16),
            grad_block,
            preferred_element_type=jnp.float32,
        )
        return ((grad_keys, grad_values), grad_query)

    starts = jnp.arange(token_count // block_rows, dtype=jnp.int32) * block_rows
    zero_rows = jnp.zeros(key_rows.shape, jnp.float32)
    (grad_keys, grad_values), grad_queries = lax.scan(
        one_block, (zero_rows, zero_rows), (starts, log_totals)
    )
    flat_width = local_heads * head_size
    return (
        grad_queries.reshape(token_count, flat_width),
        grad_keys.reshape(token_count, flat_width),
        grad_values.reshape(token_count, flat_width),
    )


def local(
    tokens,
    lengths,
    pairing,
    w_qkv,
    b_qv,
    w_out,
    b_out,
    ln_gain,
    ln_bias,
    w_up,
    b_up,
    w_down,
    b_down,
    w_proj,
    cot,
):
    tensor_count = lax.axis_size("tensor")
    tensor_index = lax.axis_index("tensor")
    data_index = lax.axis_index("dp")
    token_count = tokens.shape[0]
    share_rows = token_count // tensor_count
    block_rows = min(512, token_count)
    own_start = tensor_index * share_rows
    full_qkv, full_out, full_up, full_down = (
        lax.all_gather(w_qkv, "dp", axis=1, tiled=True),
        lax.all_gather(w_out, "dp", axis=1, tiled=True),
        lax.all_gather(w_up, "dp", axis=0, tiled=True),
        lax.all_gather(w_down, "dp", axis=1, tiled=True),
    )
    head_width = full_qkv.shape[2]
    local_heads = head_width // HEAD_DIM
    row_lengths = lax.dynamic_index_in_dim(lengths, data_index, 0, keepdims=False)
    segments = segments_of(row_lengths, token_count)
    projected = jnp.einsum("td,kdw->ktw", tokens, full_qkv, preferred_element_type=jnp.float32)
    qv_bias = b_qv.astype(jnp.float32)
    query_rows = (
        (projected[0] + qv_bias[0]).astype(jnp.bfloat16).reshape(token_count, local_heads, HEAD_DIM)
    )
    key_rows = projected[1].astype(jnp.bfloat16).reshape(token_count, local_heads, HEAD_DIM)
    value_rows = (
        (projected[2] + qv_bias[1]).astype(jnp.bfloat16).reshape(token_count, local_heads, HEAD_DIM)
    )
    mixed, log_totals = attend_forward(query_rows, key_rows, value_rows, segments, block_rows)
    attn_terms = jnp.dot(mixed, full_out, preferred_element_type=jnp.float32)
    attn_sum = lax.psum_scatter(
        attn_terms.astype(jnp.bfloat16), "tensor", scatter_dimension=0, tiled=True
    ).astype(jnp.float32)
    own_tokens = lax.dynamic_slice_in_dim(tokens, own_start, share_rows, 0).astype(jnp.float32)
    gains = ln_gain.astype(jnp.float32)
    shifts = ln_bias.astype(jnp.float32)
    normed, unit_one, rstd_one = norm_forward(
        own_tokens + attn_sum + b_out.astype(jnp.float32), gains[0], shifts[0]
    )
    normed_all = lax.all_gather(normed.astype(jnp.bfloat16), "tensor", axis=0, tiled=True)
    up_value = jnp.dot(normed_all, full_up, preferred_element_type=jnp.float32) + b_up.astype(
        jnp.float32
    )
    activation = jax.nn.gelu(up_value, approximate=False).astype(jnp.bfloat16)
    ffn_terms = jnp.dot(activation, full_down, preferred_element_type=jnp.float32)
    ffn_sum = lax.psum_scatter(
        ffn_terms.astype(jnp.bfloat16), "tensor", scatter_dimension=0, tiled=True
    ).astype(jnp.float32)
    result, unit_two, rstd_two = norm_forward(
        normed + ffn_sum + b_down.astype(jnp.float32), gains[1], shifts[1]
    )
    result_low = result.astype(jnp.bfloat16)
    embed = jnp.dot(result_low, w_proj, preferred_element_type=jnp.float32).astype(jnp.bfloat16)
    embed_all = lax.all_gather(embed, ("dp", "tensor"), axis=0, tiled=True)
    row_count = lengths.shape[0]
    proj_width = w_proj.shape[1]
    widths = (proj_width, 3 * proj_width // 4, proj_width // 2)
    per_device = pairing.shape[1]
    query_count = per_device * QLEN
    query_span = NQ_ROW * QLEN
    emb_rows = embed_all.reshape(row_count, token_count, proj_width)
    my_row = lax.dynamic_index_in_dim(emb_rows, data_index, 0, keepdims=False)
    query_raw = lax.dynamic_slice_in_dim(my_row, tensor_index * query_count, query_count, 0).astype(
        jnp.float32
    )
    query_levels = [normalize_cut(query_raw, width) for width in widths]
    query_units = [level_parts[0].astype(jnp.bfloat16) for level_parts in query_levels]
    doc_numbers = jnp.arange(NDOC, dtype=jnp.int32)

    def row_pool(carried, inputs):
        row_emb, lengths_row = inputs
        row_hot = (
            segments_of(lengths_row, token_count)[:, None] == NQ_ROW + doc_numbers[None, :]
        ).astype(jnp.float32)
        row_raw = row_emb.astype(jnp.float32)
        pooled_list = []
        sums_list = []
        for width, query_unit in zip(widths, query_units):
            doc_unit = normalize_cut(row_raw, width)[0].astype(jnp.bfloat16)
            expo = jnp.exp(contract_cols(query_unit, doc_unit) / POOL_TEMP)
            sums = jnp.dot(expo, row_hot, precision=FULL_PRECISION)
            pooled = POOL_TEMP * jnp.log(sums / lengths_row.astype(jnp.float32))
            pooled_list.append(jnp.sum(pooled.reshape(per_device, QLEN, NDOC), axis=1))
            sums_list.append(sums)
        return (carried, (jnp.stack(pooled_list), jnp.stack(sums_list)))

    _, (row_scores, row_sums) = lax.scan(row_pool, 0, (emb_rows, lengths))
    logits = (
        jnp.transpose(row_scores, (2, 1, 0, 3)).reshape(per_device, 3, row_count * NDOC) / LOSS_TEMP
    )
    own_pairs = pairing[0]
    target = jnp.take_along_axis(
        logits, jnp.broadcast_to(own_pairs[:, None, None], (per_device, 3, 1)), axis=2
    )[:, :, 0]
    loss_out = jnp.sum(jax.nn.logsumexp(logits, axis=2) - target, axis=1).reshape(1, per_device)
    picked = (
        jnp.arange(row_count * NDOC, dtype=jnp.int32)[None, None, :] == own_pairs[:, None, None]
    ).astype(jnp.float32)
    grad_logits = (jax.nn.softmax(logits, axis=2) - picked) / LOSS_TEMP
    grad_rows = jnp.transpose(grad_logits.reshape(per_device, 3, row_count, NDOC), (2, 1, 0, 3))
    coefficient = jnp.repeat(grad_rows, QLEN, axis=2) / row_sums

    def row_back(carried, inputs):
        row_emb, lengths_row, row_coef = inputs
        row_hot = (
            segments_of(lengths_row, token_count)[:, None] == NQ_ROW + doc_numbers[None, :]
        ).astype(jnp.float32)
        row_raw = row_emb.astype(jnp.float32)
        new_carried = []
        row_grad = jnp.zeros((token_count, proj_width), jnp.float32)
        for level_index in range(3):
            width = widths[level_index]
            doc_unit_f, doc_part, doc_scale = normalize_cut(row_raw, width)
            doc_unit = doc_unit_f.astype(jnp.bfloat16)
            expo = jnp.exp(contract_cols(query_units[level_index], doc_unit) / POOL_TEMP)
            spread = contract_cols(row_coef[level_index], row_hot, FULL_PRECISION)
            grad_sim = (expo * spread).astype(jnp.bfloat16)
            new_carried.append(
                carried[level_index]
                + jnp.dot(grad_sim, doc_unit, preferred_element_type=jnp.float32)
            )
        return (tuple(new_carried), row_grad)

    zero_query = tuple((jnp.zeros((query_count, width), jnp.float32) for width in widths))
    query_grads, doc_grads = lax.scan(row_back, zero_query, (emb_rows, lengths, coefficient))
    grad_query = jnp.zeros((query_count, proj_width), jnp.float32)
    for level_index in range(3):
        level_parts = query_levels[level_index]
        grad_query = grad_query + normalize_back(
            query_grads[level_index], level_parts[1], level_parts[2], proj_width
        )
    coef_mine = jnp.transpose(coefficient, (2, 1, 0, 3)).reshape(query_count, 3, row_count * NDOC)
    coef_all, grad_query_all = (
        lax.all_gather(shortened(coef_mine), ("dp", "tensor"), axis=0, tiled=True).astype(
            coef_mine.dtype
        ),
        lax.all_gather(
            grad_query.astype(jnp.bfloat16), ("dp", "tensor"), axis=0, tiled=True
        ).astype(grad_query.dtype),
    )
    own_raw = embed.astype(jnp.float32)
    own_segments = lax.dynamic_slice_in_dim(segments, own_start, share_rows, 0)
    own_docs = jnp.where(own_segments >= NQ_ROW, data_index * NDOC + own_segments - NQ_ROW, -1)
    own_hot = (own_docs[:, None] == jnp.arange(row_count * NDOC, dtype=jnp.int32)[None, :]).astype(
        jnp.float32
    )
    queries_all = (
        emb_rows[:, :query_span].reshape(row_count * query_span, proj_width).astype(jnp.float32)
    )
    grad_embed = jnp.zeros((share_rows, proj_width), jnp.float32)
    for level_index in range(3):
        width = widths[level_index]
        query_unit_all = normalize_cut(queries_all, width)[0].astype(jnp.bfloat16)
        doc_unit_f, doc_part, doc_scale = normalize_cut(own_raw, width)
        expo = jnp.exp(contract_cols(query_unit_all, doc_unit_f.astype(jnp.bfloat16)) / POOL_TEMP)
        spread = contract_cols(coef_all[:, level_index], own_hot, FULL_PRECISION)
        grad_sim = (expo * spread).astype(jnp.bfloat16)
        grad_doc = contract_rows(grad_sim, query_unit_all)
        grad_embed = grad_embed + normalize_back(grad_doc, doc_part, doc_scale, proj_width)
    row_query_grads = lax.dynamic_slice_in_dim(
        grad_query_all, data_index * query_span, query_span, 0
    )
    padded = jnp.pad(row_query_grads, ((0, token_count - query_span), (0, 0)))
    grad_embed = grad_embed + lax.dynamic_slice_in_dim(padded, own_start, share_rows, 0)
    proj_float = w_proj.astype(jnp.float32)
    grad_result = cot.astype(jnp.float32) + contract_cols(grad_embed, proj_float, FULL_PRECISION)
    proj_grad = contract_rows(result_low.astype(jnp.float32), grad_embed, FULL_PRECISION)
    gain_two = jnp.sum(grad_result * unit_two, axis=0)
    shift_two = jnp.sum(grad_result, axis=0)
    grad_second = norm_backward(grad_result, unit_two, rstd_two, gains[1])
    grad_ffn = grad_second.astype(jnp.bfloat16)
    down_bias = jnp.sum(grad_ffn.astype(jnp.float32), axis=0)
    grad_ffn_all = lax.all_gather(grad_ffn, "tensor", axis=0, tiled=True)
    grad_act = contract_cols(grad_ffn_all, full_down)
    down_grad = contract_rows(activation, grad_ffn_all)
    _, gelu_pull = jax.vjp(partial(jax.nn.gelu, approximate=False), up_value)
    grad_up = gelu_pull(grad_act)[0].astype(jnp.bfloat16)
    up_bias = jnp.sum(grad_up.astype(jnp.float32), axis=0)
    up_grad = contract_rows(normed_all, grad_up)
    normed_terms = contract_cols(grad_up, full_up)
    grad_normed = (
        lax.psum_scatter(
            normed_terms.astype(jnp.bfloat16), "tensor", scatter_dimension=0, tiled=True
        ).astype(jnp.float32)
        + grad_second
    )
    gain_one = jnp.sum(grad_normed * unit_one, axis=0)
    shift_one = jnp.sum(grad_normed, axis=0)
    grad_first = norm_backward(grad_normed, unit_one, rstd_one, gains[0])
    grad_attn = grad_first.astype(jnp.bfloat16)
    out_bias = jnp.sum(grad_attn.astype(jnp.float32), axis=0)
    grad_attn_all = lax.all_gather(grad_attn, "tensor", axis=0, tiled=True)
    out_grad = contract_rows(mixed, grad_attn_all)
    grad_mixed = contract_cols(grad_attn_all, full_out).astype(jnp.bfloat16)
    grad_q, grad_k, grad_v = attend_backward(
        query_rows, key_rows, value_rows, segments, log_totals, grad_mixed, block_rows
    )
    stacked_grads = jnp.stack(
        [grad_q.astype(jnp.bfloat16), grad_k.astype(jnp.bfloat16), grad_v.astype(jnp.bfloat16)]
    )
    qkv_grad = jnp.einsum("td,ktw->kdw", tokens, stacked_grads, preferred_element_type=jnp.float32)
    input_terms = jnp.einsum(
        "ktw,kdw->td", stacked_grads, full_qkv, preferred_element_type=jnp.float32
    )
    grad_input = (
        lax.psum_scatter(
            input_terms.astype(jnp.bfloat16), "tensor", scatter_dimension=0, tiled=True
        ).astype(jnp.float32)
        + grad_first
    )
    qv_grad = jnp.stack(
        [
            jnp.sum(stacked_grads[0].astype(jnp.float32), axis=0),
            jnp.sum(stacked_grads[2].astype(jnp.float32), axis=0),
        ]
    )
    qkv_part, out_part, up_part, down_part = (
        lax.psum_scatter(
            qkv_grad.astype(jnp.bfloat16), "dp", scatter_dimension=1, tiled=True
        ).astype(jnp.float32),
        lax.psum_scatter(
            out_grad.astype(jnp.bfloat16), "dp", scatter_dimension=1, tiled=True
        ).astype(jnp.float32),
        lax.psum_scatter(
            up_grad.astype(jnp.bfloat16), "dp", scatter_dimension=0, tiled=True
        ).astype(jnp.float32),
        lax.psum_scatter(
            down_grad.astype(jnp.bfloat16), "dp", scatter_dimension=1, tiled=True
        ).astype(jnp.float32),
    )
    gain_sum, shift_sum, out_bias_sum, down_bias_sum, proj_sum = lax.psum(
        (
            jnp.stack([gain_one, gain_two]),
            jnp.stack([shift_one, shift_two]),
            out_bias,
            down_bias,
            proj_grad,
        ),
        ("dp", "tensor"),
    )
    qv_sum, up_bias_sum = lax.psum((qv_grad, up_bias), "dp")
    return (
        result_low,
        loss_out,
        grad_input.astype(jnp.bfloat16),
        qkv_part,
        qv_sum,
        out_part,
        out_bias_sum,
        gain_sum,
        shift_sum,
        up_part,
        up_bias_sum,
        down_part,
        down_bias_sum,
        proj_sum,
    )


SWAP = [(0, 1), (1, 0)]
TURN = [(0, 0), (1, 2), (2, 1), (3, 3)]
FAR = [(0, 3), (3, 0), (1, 2), (2, 1)]
NEAR = [(0, 1), (1, 0), (2, 3), (3, 2)]
BF = jnp.bfloat16
F32 = jnp.float32


def dot(left, right):
    return jnp.dot(left, right, preferred_element_type=F32)


CORES = ("c", "y")


def tie(value, *others):
    return lax.optimization_barrier((value,) + others)[0]


def tie_all(values, *others):
    return lax.optimization_barrier(tuple(values) + others)[: len(values)]


def exchange(*moves):
    return lax.optimization_barrier(
        tuple(lax.ppermute(value, axis, steps) for value, axis, steps in moves)
    )


def swap(value, axis):
    return lax.ppermute(value, axis, SWAP)


def pair_up(first, second, own_index, axis):
    return jnp.where(
        own_index == 0, jnp.stack([first, second], axis), jnp.stack([second, first], axis)
    )


def far_pair(value, far, z):
    return jnp.where(z < 2, jnp.stack([value, far]), jnp.stack([far, value]))


def whole_line(pair, other, z):
    return jnp.where(
        (z == 0) | (z == 3),
        jnp.stack([pair[0], other[0], other[1], pair[1]]),
        jnp.stack([other[0], pair[0], pair[1], other[1]]),
    )


def first_moves(line):
    half = line.shape[1] // 2
    return ((line[:, :half], "x", SWAP), (line[:, half:], "y", SWAP))


def first_parts(line, moved, x, y):
    half = line.shape[1] // 2
    return (pair_up(line[:, :half], moved[0], x, 1), pair_up(line[:, half:], moved[1], y, 1))


def last_moves(parts):
    return ((parts[0], "y", SWAP), (parts[1], "x", SWAP))


def full_rows(parts, moved, x, y):
    low = pair_up(parts[0], moved[0], y, 2)
    high = pair_up(parts[1], moved[1], x, 1)
    return jnp.concatenate([low, high], axis=3).reshape(-1, low.shape[-1])


def at(blocks, index, axis):
    return lax.dynamic_index_in_dim(blocks, index, axis, keepdims=False)


def side_move(blocks, axis_name, own_index, axis):
    return (at(blocks, 1 - own_index, axis).astype(BF), axis_name, SWAP)


def side_sum(blocks, got, own_index, axis):
    return at(blocks, own_index, axis).astype(F32) + got.astype(F32)


def near_move(line, z):
    ends = (z == 0) | (z == 3)
    outer, inner = jnp.stack([line[0], line[3]]), line[1:3]
    return (jnp.where(ends, inner, outer).astype(BF), "z", NEAR)


def near_sum(line, got, z):
    ends = (z == 0) | (z == 3)
    return jnp.where(ends, jnp.stack([line[0], line[3]]), line[1:3]) + got.astype(F32)


def far_move(pair, z):
    return (jnp.where(z < 2, pair[1], pair[0]).astype(BF), "z", FAR)


def far_sum(pair, got, z):
    return jnp.where(z < 2, pair[0], pair[1]) + got.astype(F32)


def blocks_of(left, right):
    return contract_rows(left, right).astype(BF).reshape(4, 2, 2, 64, right.shape[1])


def sum_moves(blocks, x, y):
    half = blocks.shape[3] // 2
    return (
        side_move(blocks[..., :half, :], "x", x, 1),
        side_move(blocks[..., half:, :], "y", y, 2),
    )


def sum_parts(blocks, moved, x, y):
    half = blocks.shape[3] // 2
    return (
        side_sum(blocks[..., :half, :], moved[0], x, 1),
        side_sum(blocks[..., half:, :], moved[1], y, 2),
    )


def line_moves(parts, x, y):
    return (side_move(parts[0], "y", y, 1), side_move(parts[1], "x", x, 1))


def line_of(parts, moved, x, y):
    return jnp.concatenate(
        [side_sum(parts[0], moved[0], y, 1), side_sum(parts[1], moved[1], x, 1)], axis=1
    )


def tile_bounds(row_lengths, token_count):
    ends = jnp.cumsum(row_lengths)
    span = NQ_ROW * QLEN
    first = jnp.arange(token_count // TILE, dtype=jnp.int32) * TILE - span
    last = first + TILE - 1
    begin = jnp.max(jnp.where(ends[None, :] <= first[:, None], ends[None, :], 0), axis=1)
    end = jnp.min(jnp.where(ends[None, :] > last[:, None], ends[None, :], token_count), axis=1)
    low = jnp.where(first < 0, 0, (begin + span) // TILE)
    high = jnp.where(first < 0, 1, (end + span + TILE - 1) // TILE)
    return jnp.stack([low, high]).astype(jnp.int32)


def token_spans(row_lengths, token_count):
    ends = jnp.cumsum(row_lengths)[:, None]
    span = NQ_ROW * QLEN
    place = jnp.arange(token_count, dtype=jnp.int32)[None, :]
    doc = place - span
    begin = jnp.max(jnp.where(ends <= doc, ends, 0), axis=0) + span
    end = jnp.min(jnp.where(ends > doc, ends, token_count), axis=0) + span
    query = place[0] // QLEN * QLEN
    return jnp.stack(
        [jnp.where(doc[0] < 0, query, begin), jnp.where(doc[0] < 0, query + QLEN, end)]
    ).astype(jnp.int32)


def rows_of(value, start, count):
    return lax.dynamic_slice_in_dim(value, start, count, 0)


TILE = 256
KEYS = 256
NEG = -1e30


def exact(left, right, dims):
    return lax.dot_general(left, right, (dims, ((), ())), preferred_element_type=F32)


def head_masks(value):
    lane = lax.broadcasted_iota(jnp.int32, value.shape, 1)
    zero = jnp.zeros_like(value)
    return (jnp.where(lane < HEAD_DIM, value, zero), jnp.where(lane < HEAD_DIM, zero, value))


def key_shift(step, spans):
    place = step * KEYS + lax.broadcasted_iota(jnp.int32, (KEYS, TILE), 0)
    inside = (place >= spans[0:1, :]) & (place < spans[1:2, :])
    return jnp.where(inside, 0.0, NEG)


def attend_kernel(bounds, own_ref, qkv_ref, spans, out_ref, lse_ref, held):
    block = pl.program_id(0)
    groups = 2
    pairs = out_ref.shape[1] // 128
    per_group = pairs // groups

    def column(pair, part):
        start = ((pair // per_group) * 3 + part) * per_group + pair % per_group
        return slice(start * 128, (start + 1) * 128)

    queries = [head_masks(own_ref[:, column(pair, 0)] * HEAD_DIM**-0.5) for pair in range(pairs)]
    heads = [(pair, head) for pair in range(pairs) for head in range(2)]

    def score(step, highest):
        rows = pl.ds(pl.multiple_of(step * KEYS, KEYS), KEYS)
        shift = key_shift(step, spans)
        fresh = []
        for index, (pair, head) in enumerate(heads):
            keys = qkv_ref[rows, column(pair, 1)]
            scores = exact(keys, queries[pair][head], ((1,), (1,))) + shift
            held[index, rows, :] = scores
            fresh.append(jnp.maximum(highest[index], jnp.max(scores, axis=0, keepdims=True)))
        return tuple(fresh)

    low = jnp.full((1, TILE), NEG, F32)
    highest = lax.fori_loop(bounds[0, block], bounds[1, block], score, (low,) * len(heads))

    def mix(step, carried):
        rows = pl.ds(pl.multiple_of(step * KEYS, KEYS), KEYS)
        fresh = []
        for index, (pair, head) in enumerate(heads):
            values = qkv_ref[rows, column(pair, 2)]
            total, mixed = carried[index]
            expo = jnp.exp(held[index, rows, :] - highest[index])
            product = exact(values, expo.astype(BF), ((0,), (0,)))
            fresh.append(
                (
                    total + jnp.sum(expo, axis=0, keepdims=True),
                    mixed + product[head * HEAD_DIM : (head + 1) * HEAD_DIM],
                )
            )
        return tuple(fresh)

    start = (jnp.zeros((1, TILE), F32), jnp.zeros((HEAD_DIM, TILE), F32))
    parts = lax.fori_loop(bounds[0, block], bounds[1, block], mix, (start,) * len(heads))
    for pair in range(pairs):
        both = [parts[2 * pair + head][1] / parts[2 * pair + head][0] for head in range(2)]
        mixed = jnp.transpose(jnp.concatenate(both, axis=0))
        out_ref[:, pair * 128 : (pair + 1) * 128] = mixed.astype(BF)
    for index in range(len(heads)):
        lse_ref[index : index + 1, :] = highest[index] + jnp.log(parts[index][0])


def attend(bounds, qkv, spans):
    count, wide = qkv.shape
    heads = wide // 3 // HEAD_DIM
    whole = lambda shape: pl.BlockSpec(shape, lambda i: (0, 0))
    return pl.pallas_call(
        attend_kernel,
        grid=(count // TILE,),
        in_specs=[
            pl.BlockSpec(memory_space=pltpu.SMEM),
            pl.BlockSpec((TILE, wide), lambda i: (i, 0)),
            whole((count, wide)),
            pl.BlockSpec((2, TILE), lambda i: (0, i)),
        ],
        out_specs=[
            pl.BlockSpec((TILE, wide // 3), lambda i: (i, 0)),
            pl.BlockSpec((heads, TILE), lambda i: (0, i)),
        ],
        out_shape=[
            jax.ShapeDtypeStruct((count, wide // 3), BF),
            jax.ShapeDtypeStruct((heads, count), F32),
        ],
        scratch_shapes=[pltpu.VMEM((heads, count, TILE), F32)],
        compiler_params=pltpu.CompilerParams(vmem_limit_bytes=40 << 20),
        cost_estimate=pl.CostEstimate(
            flops=4 * heads * count * count * 64,
            transcendentals=heads * count * count // 2,
            bytes_accessed=4 * count * wide * 2,
        ),
    )(bounds, qkv, qkv, spans)


def attend_back_kernel(
    first, bounds, own_ref, qkv_ref, out_ref, grad_ref, lse_ref, spans,
    grads_ref, sums_ref, key_sum, value_sum,
):
    block = pl.program_id(0)
    pairs = out_ref.shape[1] // 128
    heads = [(pair, head) for pair in range(pairs) for head in range(2)]
    cut = lambda index: slice(index * 128, (index + 1) * 128)

    @pl.when(block == 0)
    def _():
        key_sum[...] = jnp.zeros_like(key_sum)
        value_sum[...] = jnp.zeros_like(value_sum)
        sums_ref[...] = jnp.zeros_like(sums_ref)

    queries = [head_masks(own_ref[:, cut(pair)] * HEAD_DIM**-0.5) for pair in range(pairs)]
    grads = [head_masks(grad_ref[:, cut(pair)]) for pair in range(pairs)]
    picks = head_masks(jnp.ones((8, 128), BF))
    inner = []
    for pair, head in heads:
        product = grad_ref[:, cut(pair)].astype(F32) * out_ref[:, cut(pair)].astype(F32)
        high = product.astype(BF)
        rest = (product - high.astype(F32)).astype(BF)
        inner.append(
            (
                exact(picks[head], high, ((1,), (1,))) + exact(picks[head], rest, ((1,), (1,)))
            )[0:1]
        )
    lse = [lse_ref[first + index : first + index + 1, :] for index in range(len(heads))]

    def step_of(step, carried):
        rows = pl.ds(pl.multiple_of(step * KEYS, KEYS), KEYS)
        shift = key_shift(step, spans)
        fresh = []
        for pair in range(pairs):
            keys = qkv_ref[rows, cut(pairs + pair)]
            values = qkv_ref[rows, cut(2 * pairs + pair)]
            key_add = jnp.zeros((KEYS, 128), F32)
            value_add = jnp.zeros((KEYS, 128), F32)
            for head in range(2):
                index = 2 * pair + head
                scores = exact(keys, queries[pair][head], ((1,), (1,))) + shift
                probs = jnp.exp(scores - lse[index])
                grad_probs = exact(values, grads[pair][head], ((1,), (1,)))
                grad_scores = (probs * (grad_probs - inner[index])).astype(BF)
                value_add = value_add + exact(probs.astype(BF), grads[pair][head], ((1,), (0,)))
                key_add = key_add + exact(grad_scores, queries[pair][head], ((1,), (0,)))
                product = exact(keys, grad_scores, ((0,), (0,)))
                fresh.append(carried[index] + product[head * HEAD_DIM : (head + 1) * HEAD_DIM])
            key_sum[rows, cut(pair)] += key_add
            value_sum[rows, cut(pair)] += value_add
        return tuple(fresh)

    start = jnp.zeros((HEAD_DIM, TILE), F32)
    parts = lax.fori_loop(bounds[0, block], bounds[1, block], step_of, (start,) * len(heads))
    own = pl.ds(pl.multiple_of(block * TILE, TILE), TILE)
    for pair in range(pairs):
        grad_query = jnp.concatenate([parts[2 * pair], parts[2 * pair + 1]], axis=0)
        grad_query = jnp.transpose(grad_query * HEAD_DIM**-0.5).astype(BF)
        grads_ref[own, cut(pair)] = grad_query
        sums_ref[0:1, cut(pair)] += jnp.sum(grad_query.astype(F32), axis=0, keepdims=True)

    @pl.when(block == pl.num_programs(0) - 1)
    def _():
        wide = pairs * 128
        grad_value = value_sum[...].astype(BF)
        grads_ref[:, wide : 2 * wide] = key_sum[...].astype(BF)
        grads_ref[:, 2 * wide :] = grad_value
        sums_ref[1:2, :] = jnp.sum(grad_value.astype(F32), axis=0, keepdims=True)


def attend_back(bounds, group, qkv, mixed, grad_mixed, lse, spans):
    count = qkv.shape[0]
    wide = qkv.shape[1] // 2
    heads = wide // 3 // HEAD_DIM
    whole = lambda shape: pl.BlockSpec(shape, lambda i: (0, 0))
    return pl.pallas_call(
        partial(attend_back_kernel, group * heads),
        grid=(count // TILE,),
        in_specs=[
            pl.BlockSpec(memory_space=pltpu.SMEM),
            pl.BlockSpec((TILE, wide), lambda i: (i, group)),
            pl.BlockSpec((count, wide), lambda i: (0, group)),
            pl.BlockSpec((TILE, wide // 3), lambda i: (i, group)),
            pl.BlockSpec((TILE, wide // 3), lambda i: (i, group)),
            pl.BlockSpec((2 * heads, TILE), lambda i: (0, i)),
            pl.BlockSpec((2, TILE), lambda i: (0, i)),
        ],
        out_specs=[whole((count, wide)), whole((8, wide // 3))],
        out_shape=[
            jax.ShapeDtypeStruct((count, wide), BF),
            jax.ShapeDtypeStruct((8, wide // 3), F32),
        ],
        scratch_shapes=[
            pltpu.VMEM((count, wide // 3), F32),
            pltpu.VMEM((count, wide // 3), F32),
        ],
        compiler_params=pltpu.CompilerParams(vmem_limit_bytes=40 << 20),
        cost_estimate=pl.CostEstimate(
            flops=10 * heads * count * count * 64,
            transcendentals=heads * count * count // 2,
            bytes_accessed=8 * count * wide * 2,
        ),
    )(
        bounds, qkv, qkv, mixed, grad_mixed,
        lse, spans,
    )


ERFC = (
    -1.26551223, 1.00002368, 0.37409196, 0.09678418, -0.18628806,
    0.27886807, -1.13520398, 1.48851587, -0.82215223, 0.17087277,
)


def gelu_pair(value):
    size = jnp.abs(value) * 0.5**0.5
    ratio = 1.0 / (1.0 + 0.5 * size)
    series = jnp.full_like(value, ERFC[-1])
    for factor in ERFC[-2::-1]:
        series = series * ratio + factor
    bell = jnp.exp(-size * size)
    tail = 0.5 * ratio * bell * jnp.exp(series)
    phi = jnp.where(value < 0.0, tail, 1.0 - tail)
    return (value * phi, phi + value * bell * 0.3989422804014327)


def expand_kernel(x_ref, w_ref, b_ref, act_ref, slope_ref):
    rows = 256
    for start in range(0, x_ref.shape[0], rows):
        part = slice(start, start + rows)
        value = exact(x_ref[part, :], w_ref[...], ((1,), (0,))) + b_ref[...]
        active, slope = gelu_pair(value)
        act_ref[part, :] = active.astype(BF)
        slope_ref[part, :] = slope.astype(BF)


def expand(value, weight, shift):
    count, depth = value.shape
    width = shift.shape[1]
    tile = 256
    return pl.pallas_call(
        expand_kernel,
        grid=(width // tile,),
        in_specs=[
            pl.BlockSpec((count, depth), lambda i: (0, 0)),
            pl.BlockSpec((depth, tile), lambda i: (0, i)),
            pl.BlockSpec((1, tile), lambda i: (0, i)),
        ],
        out_specs=[pl.BlockSpec((count, tile), lambda i: (0, i))] * 2,
        out_shape=[jax.ShapeDtypeStruct((count, width), BF)] * 2,
        compiler_params=pltpu.CompilerParams(vmem_limit_bytes=32 << 20),
        cost_estimate=pl.CostEstimate(
            flops=10 * count * depth * width,
            transcendentals=3 * count * width,
            bytes_accessed=2 * (count * depth + depth * width + 2 * count * width),
        ),
    )(value, weight, shift)


def cut_levels(raw, cuts):
    lane = lax.broadcasted_iota(jnp.int32, raw.shape, 1)
    levels = []
    for cut in cuts:
        part = jnp.where(lane < cut, raw, 0.0)
        scale = lax.rsqrt(jnp.sum(part * part, axis=1, keepdims=True) + EPS_EMBED)
        levels.append(((part * scale).astype(BF), part, scale))
    return levels


def pool_kernel(cuts, span, q_ref, d_ref, seg_ref, out_ref, units, hot):
    @pl.when(pl.program_id(0) == 0)
    def _():
        raw = d_ref[span:, :].astype(F32)
        for level, parts in enumerate(cut_levels(raw, cuts)):
            units[level] = parts[0]
        doc = lax.broadcasted_iota(jnp.int32, hot.shape, 0)
        hot[...] = (seg_ref[:, span:] == NQ_ROW + doc).astype(F32).astype(BF)

    levels = cut_levels(q_ref[...].astype(F32), cuts)
    for level in range(len(cuts)):
        similar = exact(units[level], levels[level][0], ((1,), (1,)))
        expo = jnp.exp(similar * (1.0 / POOL_TEMP))
        high = expo.astype(BF)
        rest = (expo - high.astype(F32)).astype(BF)
        out_ref[level * NDOC : (level + 1) * NDOC, :] = exact(
            hot[...], high, ((1,), (0,))
        ) + exact(hot[...], rest, ((1,), (0,)))


def pool(cuts, span, queries, row_embed, seg_row):
    count, width = queries.shape
    tokens = row_embed.shape[0]
    whole = lambda shape: pl.BlockSpec(shape, lambda i: (0, 0))
    return pl.pallas_call(
        partial(pool_kernel, cuts, span),
        grid=(count // TILE,),
        in_specs=[
            pl.BlockSpec((TILE, width), lambda i: (i, 0)),
            whole((tokens, width)),
            whole((1, tokens)),
        ],
        out_specs=pl.BlockSpec((len(cuts) * NDOC, TILE), lambda i: (0, i)),
        out_shape=jax.ShapeDtypeStruct((len(cuts) * NDOC, count), F32),
        scratch_shapes=[
            pltpu.VMEM((len(cuts), tokens - span, width), BF),
            pltpu.VMEM((NDOC, tokens - span), BF),
        ],
        compiler_params=pltpu.CompilerParams(vmem_limit_bytes=32 << 20),
        cost_estimate=pl.CostEstimate(
            flops=2 * len(cuts) * count * tokens * 256,
            transcendentals=len(cuts) * count * tokens,
            bytes_accessed=2 * (count + tokens) * width,
        ),
    )(queries, row_embed, seg_row)


def level_back(grad, part, scale):
    return scale * grad - part * (scale * scale * scale) * jnp.sum(
        part * grad, axis=1, keepdims=True
    )


def pool_back_kernel(
    cuts, span, q_ref, d_ref, seg_ref, coef_ref, q_out, d_out, units, units_t, hot, sums
):
    step = pl.program_id(0)

    @pl.when(step == 0)
    def _():
        raw = d_ref[span:, :].astype(F32)
        for level, parts in enumerate(cut_levels(raw, cuts)):
            units[level] = parts[0]
            units_t[level] = jnp.transpose(parts[0])
        doc = lax.broadcasted_iota(jnp.int32, hot.shape, 0)
        wanted = NQ_ROW + jnp.where(doc < NDOC, doc, doc - NDOC)
        hot[...] = (seg_ref[:, span:] == wanted).astype(F32).astype(BF)
        sums[...] = jnp.zeros_like(sums)

    levels = cut_levels(q_ref[...].astype(F32), cuts)
    total = jnp.zeros(q_ref.shape, F32)
    for level in range(len(cuts)):
        unit, part, scale = levels[level]
        similar = exact(units[level], unit, ((1,), (1,)))
        coef = coef_ref[level * NDOC : (level + 1) * NDOC, :]
        high = coef.astype(BF).astype(F32)
        both = jnp.concatenate([high, coef - high], axis=0).astype(BF)
        spread = exact(hot[...], both, ((0,), (0,)))
        grad = (jnp.exp(similar * (1.0 / POOL_TEMP)) * spread).astype(BF)
        sums[level] += exact(grad, unit, ((1,), (0,)))
        grad_unit = jnp.transpose(exact(units_t[level], grad, ((1,), (0,))))
        total = total + level_back(grad_unit, part, scale)
    q_out[...] = total.astype(BF)

    @pl.when(step == pl.num_programs(0) - 1)
    def _():
        raw = d_ref[span:, :].astype(F32)
        result = jnp.zeros(raw.shape, F32)
        for level, parts in enumerate(cut_levels(raw, cuts)):
            lane = lax.broadcasted_iota(jnp.int32, raw.shape, 1)
            grad = jnp.where(lane < cuts[level], sums[level], 0.0)
            result = result + level_back(grad, parts[1], parts[2])
        d_out[...] = result


def pool_back(cuts, span, queries, row_embed, seg_row, coef):
    count, width = queries.shape
    tokens = row_embed.shape[0]
    docs = tokens - span
    whole = lambda shape: pl.BlockSpec(shape, lambda i: (0, 0))
    return pl.pallas_call(
        partial(pool_back_kernel, cuts, span),
        grid=(count // TILE,),
        in_specs=[
            pl.BlockSpec((TILE, width), lambda i: (i, 0)),
            whole((tokens, width)),
            whole((1, tokens)),
            pl.BlockSpec((len(cuts) * NDOC, TILE), lambda i: (0, i)),
        ],
        out_specs=[pl.BlockSpec((TILE, width), lambda i: (i, 0)), whole((docs, width))],
        out_shape=[
            jax.ShapeDtypeStruct((count, width), BF),
            jax.ShapeDtypeStruct((docs, width), F32),
        ],
        scratch_shapes=[
            pltpu.VMEM((len(cuts), docs, width), BF),
            pltpu.VMEM((len(cuts), width, docs), BF),
            pltpu.VMEM((2 * NDOC, docs), BF),
            pltpu.VMEM((len(cuts), docs, width), F32),
        ],
        compiler_params=pltpu.CompilerParams(vmem_limit_bytes=32 << 20),
        cost_estimate=pl.CostEstimate(
            flops=2 * len(cuts) * count * docs * 512,
            transcendentals=len(cuts) * count * docs,
            bytes_accessed=4 * (count + tokens) * width,
        ),
    )(queries, row_embed, seg_row, coef)


def local_chip(
    tokens,
    lengths,
    pairing,
    w_qkv,
    b_qv,
    w_out,
    b_out,
    ln_gain,
    ln_bias,
    w_up,
    b_up,
    w_down,
    b_down,
    w_proj,
    cot,
):
    z, x, c, y = (lax.axis_index(name) for name in ("z", "x", "c", "y"))
    chip = 4 * z + 2 * x + y
    token_count, width = tokens.shape
    share = token_count // 2
    own_start, other_start = c * share, (1 - c) * share
    gains, shifts = ln_gain.astype(F32), ln_bias.astype(F32)

    half_width = w_qkv.shape[2]
    up_wide = w_up.shape[1]
    chip_count = lengths.shape[0]
    half_queries = NQ_ROW // 2
    query_total = chip_count * half_queries
    quarter = half_width // 2
    qkv_rows = jnp.concatenate(
        [w_qkv[k][:, g * quarter : (g + 1) * quarter] for g in range(2) for k in range(3)], axis=1
    )
    pair_rows = jnp.pad(pairing.astype(BF), ((0, 63), (0, 128 - half_queries)))
    mid_rows = jnp.concatenate([w_up, w_out.T, pair_rows], axis=1)
    bias = jnp.concatenate([b_qv.reshape(-1), b_up])[None].astype(F32)
    got = exchange(
        (qkv_rows, CORES, TURN), (tokens, "c", SWAP), (bias, "y", SWAP)
    )
    qkv_rows = got[0]
    row = jnp.where(c == y, tokens, got[1])
    bias = jnp.where(c == y, bias, got[2])
    (rest_rows,) = exchange(
        (tie(jnp.concatenate([mid_rows, w_down.T], axis=1), row), CORES, TURN)
    )
    (far,) = exchange((qkv_rows, "z", FAR))
    qkv_pair = far_pair(qkv_rows, far, z)
    mid_wide = mid_rows.shape[1]
    rest_rows = tie(rest_rows, qkv_pair)
    mid_rows, down_rows = rest_rows[:, :mid_wide], rest_rows[:, mid_wide:]
    got = exchange((qkv_pair, "z", NEAR), (mid_rows, "z", FAR), (tie(cot, qkv_pair), CORES, TURN))
    own_cot = got[2]
    qkv_line = whole_line(qkv_pair, got[0], z)
    mid_pair = far_pair(mid_rows, got[1], z)
    got = exchange(*first_moves(qkv_line), (mid_pair, "z", NEAR))
    qkv_parts = first_parts(qkv_line, got, x, y)
    mid_line = whole_line(mid_pair, got[2], z)
    last = last_moves(qkv_parts)
    got = exchange(*last, (tie(down_rows, mid_line), "z", FAR), *first_moves(mid_line))
    full_qkv = full_rows(qkv_parts, got, x, y)
    down_pair = far_pair(down_rows, got[2], z)
    mid_parts = first_parts(mid_line, got[3:], x, y)
    (near,) = exchange((down_pair, "z", NEAR))
    down_line = whole_line(down_pair, near, z)
    got = exchange(*last_moves(mid_parts), *first_moves(down_line))
    full_mid = full_rows(mid_parts, got, x, y)
    down_parts = first_parts(down_line, got[2:], x, y)
    down_got = exchange(*last_moves(down_parts))
    full_out = full_mid[:, up_wide : up_wide + half_width]
    pairs = full_mid[:, up_wide + half_width :].reshape(chip_count, 64, 128)
    pairs = pairs[:, 0, :half_queries].astype(jnp.int32).reshape(1, query_total)
    row_lengths = lax.dynamic_index_in_dim(lengths, chip, 0, keepdims=False)
    segments = segments_of(row_lengths, token_count)
    seg_row, spans = segments[None, :], token_spans(row_lengths, token_count)
    query_span = NQ_ROW * QLEN
    bounds = tile_bounds(row_lengths, token_count)
    no_bias = jnp.zeros((1, quarter), F32)
    qkv_bias = jnp.concatenate(
        [
            part
            for g in range(2)
            for part in (
                bias[:, g * quarter : (g + 1) * quarter],
                no_bias,
                bias[:, half_width + g * quarter : half_width + (g + 1) * quarter],
            )
        ],
        axis=1,
    )
    qkv = (dot(row, full_qkv) + qkv_bias).astype(BF)
    mixed, lse = attend(bounds, tie(qkv, down_line), spans)

    def row_sum(left, weight_t, transposed):
        times = contract_cols if transposed else dot
        theirs = swap(times(left(1), weight_t).astype(BF), "c")
        return times(left(0), weight_t) + theirs.astype(F32)

    def mixed_half(which):
        return rows_of(mixed, other_start if which else own_start, share)

    attn_sum = row_sum(mixed_half, full_out, True)
    own_tokens = rows_of(row, own_start, share).astype(F32)
    normed, unit_one, rstd_one = norm_forward(
        own_tokens + attn_sum + b_out.astype(F32), gains[0], shifts[0]
    )
    normed_low = normed.astype(BF)
    normed_all = jnp.concatenate([normed_low, swap(normed_low, "c")], axis=0)
    activation, slope = expand(normed_all, full_mid, bias[:, 2 * half_width :])
    down_got = tie_all(down_got, activation)
    full_down = full_rows(down_parts, down_got, x, y)
    ffn_sum = row_sum(
        lambda which: activation[which * share : (which + 1) * share], full_down, True
    )
    result, unit_two, rstd_two = norm_forward(
        normed + ffn_sum + b_down.astype(F32), gains[1], shifts[1]
    )
    result_low = result.astype(BF)
    embed = dot(result_low, w_proj).astype(BF)

    other_embed = swap(embed, "c")
    row_embed = jnp.where(
        c == 0,
        jnp.concatenate([embed, other_embed], axis=0),
        jnp.concatenate([other_embed, embed], axis=0),
    )
    half_span = query_span // 2
    own_queries = rows_of(row_embed, c * half_span, half_span)
    chips = ("z", "x", "y")
    queries = lax.all_to_all(
        jnp.broadcast_to(own_queries[None], (chip_count,) + own_queries.shape), chips, 0, 0
    ).reshape(chip_count * half_span, -1)
    proj_width = w_proj.shape[1]
    cuts = (proj_width, 3 * proj_width // 4, proj_width // 2)
    sums = pool(cuts, query_span, queries, row_embed, seg_row)
    doc_sizes = jnp.tile(row_lengths.astype(F32), 3)[:, None]
    group = (
        jnp.arange(query_total * QLEN, dtype=jnp.int32)[:, None] // QLEN
        == jnp.arange(query_total, dtype=jnp.int32)[None, :]
    ).astype(F32)
    pooled = POOL_TEMP * jnp.log(sums / doc_sizes)
    logits = jnp.dot(pooled, group, precision=FULL_PRECISION) / LOSS_TEMP
    logits = logits.reshape(3, NDOC, query_total)
    doc_numbers = chip * NDOC + jnp.arange(NDOC, dtype=jnp.int32)
    picked = (doc_numbers[:, None] == pairs).astype(F32)
    own_high = jnp.max(logits, axis=1)
    own_lse = own_high + jnp.log(jnp.sum(jnp.exp(logits - own_high[:, None]), axis=1))
    own_target = jnp.sum(logits * picked, axis=1)
    notes = jnp.pad(jnp.concatenate([own_lse, own_target], axis=1), ((0, 5), (0, 0)))
    notes = lax.all_to_all(
        jnp.broadcast_to(notes[None], (chip_count,) + notes.shape), chips, 0, 0
    )
    chip_lse = notes[:, :3, :query_total]
    high = jnp.max(chip_lse, axis=0)
    all_lse = high + jnp.log(jnp.sum(jnp.exp(chip_lse - high), axis=0))
    target = jnp.sum(notes[:, :3, query_total:], axis=0)
    losses = jnp.sum(all_lse - target, axis=0).reshape(chip_count, half_queries)
    grad_logits = (jnp.exp(logits - all_lse[:, None]) - picked) / LOSS_TEMP
    coefficient = (
        lax.dot_general(
            grad_logits.reshape(3 * NDOC, query_total),
            group,
            (((1,), (1,)), ((), ())),
            precision=FULL_PRECISION,
        )
        / sums
    )
    query_grad, doc_grad = pool_back(cuts, query_span, queries, row_embed, seg_row, coefficient)
    grad_blocks = lax.all_to_all(
        query_grad.reshape(chip_count, half_span, proj_width), chips, 0, 0
    )
    own_query_grad = jnp.sum(grad_blocks.astype(F32), axis=0)
    row_grad = jnp.concatenate([jnp.zeros((query_span, proj_width), F32), doc_grad], axis=0)
    row_grad = lax.dynamic_update_slice_in_dim(row_grad, own_query_grad, c * half_span, 0)
    grad_embed = rows_of(row_grad, own_start, share) + swap(
        rows_of(row_grad, other_start, share), "c"
    )

    proj_low = w_proj
    grad_embed_low = grad_embed.astype(BF)
    grad_embed_rest = (grad_embed - grad_embed_low.astype(F32)).astype(BF)
    grad_result = own_cot.astype(F32) + (
        contract_cols(grad_embed_low, proj_low) + contract_cols(grad_embed_rest, proj_low)
    )
    proj_grad = contract_rows(result_low, grad_embed_low) + contract_rows(
        result_low, grad_embed_rest
    )
    gain_two = jnp.sum(grad_result * unit_two, axis=0)
    shift_two = jnp.sum(grad_result, axis=0)
    grad_second = norm_backward(grad_result, unit_two, rstd_two, gains[1])
    grad_ffn = grad_second.astype(BF)
    down_bias = jnp.sum(grad_ffn.astype(F32), axis=0)
    other_ffn, other_losses = exchange((grad_ffn, "c", SWAP), (losses, "c", SWAP))
    losses = jnp.where(c == y, losses, other_losses)
    loss_out = rows_of(losses, 4 * z + 2 * x + c, 1)
    grad_ffn_all = jnp.concatenate([grad_ffn, other_ffn], axis=0)
    down_blocks = blocks_of(grad_ffn_all, activation)
    down_moved = exchange(*sum_moves(down_blocks, x, y))
    grad_up = (dot(grad_ffn_all, full_down) * slope.astype(F32)).astype(BF)
    up_bias = jnp.sum(grad_up.astype(F32), axis=0)
    up_blocks = blocks_of(normed_all, grad_up)
    down_parts = sum_parts(down_blocks, down_moved, x, y)
    moved = exchange(*line_moves(down_parts, x, y))
    down_line = line_of(down_parts, moved, x, y)
    full_up = full_mid[:, :up_wide]
    grad_normed = (
        row_sum(lambda which: grad_up[which * share : (which + 1) * share], full_up, True)
        + grad_second
    )
    gain_one = jnp.sum(grad_normed * unit_one, axis=0)
    shift_one = jnp.sum(grad_normed, axis=0)
    grad_first = norm_backward(grad_normed, unit_one, rstd_one, gains[0])
    grad_attn = grad_first.astype(BF)
    out_bias = jnp.sum(grad_attn.astype(F32), axis=0)
    other_attn = swap(grad_attn, "c")
    grad_attn_all = jnp.where(
        c == 0,
        jnp.concatenate([grad_attn, other_attn], axis=0),
        jnp.concatenate([other_attn, grad_attn], axis=0),
    )
    grad_mixed = dot(grad_attn_all, full_out).astype(BF)
    out_blocks = blocks_of(grad_attn_all, mixed)
    grad_mixed, out_blocks, down_line, up_blocks = lax.optimization_barrier(
        (grad_mixed, out_blocks, down_line, up_blocks)
    )
    moved = exchange(near_move(down_line, z), *sum_moves(up_blocks, x, y))
    grads_one, sums_one = attend_back(bounds, 0, qkv, mixed, grad_mixed, lse, spans)
    down_pair = near_sum(down_line, moved[0], z)
    up_parts = sum_parts(up_blocks, moved[1:], x, y)
    grad_mixed, down_pair, out_blocks, *up_parts = lax.optimization_barrier(
        (grad_mixed, down_pair, out_blocks) + tuple(up_parts)
    )
    moves = line_moves(up_parts, x, y) + sum_moves(out_blocks, x, y)
    grad_mixed, *given = lax.optimization_barrier(
        (grad_mixed,) + tuple(value for value, _, _ in moves)
    )
    moved = exchange(*((value,) + move[1:] for value, move in zip(given, moves)))
    grads_two, sums_two = attend_back(
        bounds, 1, qkv, mixed, tie(grad_mixed, grads_one), lse, spans
    )
    up_line = line_of(up_parts, moved, x, y)
    out_parts = sum_parts(out_blocks, moved[2:], x, y)
    grads_one, grads_two, down_pair, up_line, *out_parts = lax.optimization_barrier(
        (grads_one, grads_two, down_pair, up_line) + tuple(out_parts)
    )
    moved = exchange(
        near_move(up_line, z),
        *line_moves(out_parts, x, y),
        (tie(result_low, up_line), CORES, TURN),
        far_move(down_pair, z),
    )
    down_part = far_sum(down_pair, moved[4], z)
    up_pair = near_sum(up_line, moved[0], z)
    out_line = line_of(out_parts, moved[1:3], x, y)
    y_out = moved[3]
    proj_half = rows_of(proj_grad, own_start, share) + swap(
        rows_of(proj_grad, other_start, share), "c"
    )
    shared = jnp.stack([gain_one, gain_two, shift_one, shift_two, out_bias, down_bias])
    half_sums = jnp.concatenate(
        [
            sums_one[0],
            sums_two[0],
            sums_one[1],
            sums_two[1],
            up_bias,
        ]
    )
    small = jnp.concatenate([shared.reshape(-1, 128), half_sums.reshape(-1, 128), proj_half])

    qkv_blocks = jnp.concatenate(
        [blocks_of(row, grads_one), blocks_of(row, grads_two)], axis=4
    )
    qkv_blocks, up_pair, out_line, down_part, small = lax.optimization_barrier(
        (qkv_blocks, up_pair, out_line, down_part, small)
    )
    moved = exchange(
        *sum_moves(qkv_blocks, x, y),
        far_move(up_pair, z),
        near_move(out_line, z),
        (small, "y", SWAP),
    )
    qkv_parts = sum_parts(qkv_blocks, moved, x, y)
    up_part = far_sum(up_pair, moved[2], z)
    out_pair = near_sum(out_line, moved[3], z)
    small = small + moved[4]

    def input_terms(start):
        return contract_cols(
            rows_of(grads_one, start, share), full_qkv[:, : 3 * quarter]
        ) + contract_cols(rows_of(grads_two, start, share), full_qkv[:, 3 * quarter :])

    other_terms = swap(input_terms(other_start).astype(BF), "c")
    grad_input = (input_terms(own_start) + other_terms.astype(F32) + grad_first).astype(BF)
    moved = exchange(*line_moves(qkv_parts, x, y), far_move(out_pair, z), (small, "x", SWAP))
    qkv_line = line_of(qkv_parts, moved, x, y)
    out_part = far_sum(out_pair, moved[2], z)
    small = small + moved[3]
    moved = exchange(
        near_move(qkv_line, z),
        (small, "z", FAR),
        (tie(grad_input, qkv_line), CORES, TURN),
    )
    qkv_pair = near_sum(qkv_line, moved[0], z)
    small = small + moved[1]
    grad_input = moved[2]
    ffn_part = jnp.concatenate([down_part, up_part], axis=1).astype(BF)
    moved = exchange(
        far_move(qkv_pair, z), (small, "z", NEAR), (tie(ffn_part, qkv_pair), CORES, TURN)
    )
    attn_part = jnp.concatenate([far_sum(qkv_pair, moved[0], z), out_part], axis=1).astype(BF)
    small = small + moved[1]
    ffn_part = moved[2].astype(F32)
    down_part, up_part = ffn_part[:, :up_wide], ffn_part[:, up_wide:]
    attn_part, other_small = exchange((attn_part, CORES, TURN), (small, "c", SWAP))
    attn_part = attn_part.astype(F32)
    qkv_part, out_part = attn_part[:, : 3 * half_width], attn_part[:, 3 * half_width :]
    shared_rows = 6 * width // 128
    small_rows = small.shape[0] - share
    shared = (small[:shared_rows] + other_small[:shared_rows]).reshape(6, width)
    half_sums = jnp.where(
        c == y, small[shared_rows:small_rows], other_small[shared_rows:small_rows]
    ).reshape(-1)
    proj_sum = pair_up(small[small_rows:], other_small[small_rows:], c, 0).reshape(width, -1)
    qkv_part = qkv_part.reshape(64, 2, 3, quarter).transpose(2, 0, 1, 3).reshape(3, 64, half_width)
    return (
        y_out,
        loss_out,
        grad_input,
        qkv_part,
        half_sums[: 2 * half_width].reshape(2, half_width),
        out_part.T,
        shared[4],
        shared[0:2],
        shared[2:4],
        up_part,
        half_sums[2 * half_width :],
        down_part.T,
        shared[5],
        proj_sum,
    )


IN_SPECS = (
    P("dp", None),
    P(),
    P("dp", "tensor"),
    P(None, "dp", "tensor"),
    P(None, "tensor"),
    P("tensor", "dp"),
    P(),
    P(),
    P(),
    P("dp", "tensor"),
    P("tensor"),
    P("tensor", "dp"),
    P(),
    P(),
    P(("dp", "tensor"), None),
)
OUT_SPECS = (
    P(("dp", "tensor"), None),
    P("dp", "tensor"),
    P(("dp", "tensor"), None),
    P(None, "dp", "tensor"),
    P(None, "tensor"),
    P("tensor", "dp"),
    P(),
    P(),
    P(),
    P("dp", "tensor"),
    P("tensor"),
    P("tensor", "dp"),
    P(),
    P(),
)


def solution(mesh):
    if mesh.devices.shape != (16, 2):
        return jax.shard_map(
            local, mesh=mesh, in_specs=IN_SPECS, out_specs=OUT_SPECS, check_vma=False
        )
    names = {"dp": ("z", "x", "c"), "tensor": ("y",)}

    def respec(spec):
        parts = []
        for entry in spec:
            axes = () if entry is None else entry if isinstance(entry, tuple) else (entry,)
            parts.append(tuple(name for axis in axes for name in names[axis]) or None)
        return P(*parts)

    chips = Mesh(mesh.devices.reshape(4, 2, 2, 2), ("z", "x", "c", "y"))
    return jax.shard_map(
        local_chip,
        mesh=chips,
        in_specs=tuple(respec(spec) for spec in IN_SPECS),
        out_specs=tuple(respec(spec) for spec in OUT_SPECS),
        check_vma=False,
    )
```

```python
from functools import partial

import jax
import jax.numpy as jnp
from jax import lax
from jax.experimental import pallas as pl
from jax.experimental.pallas import tpu as pltpu
from jax.sharding import Mesh, PartitionSpec as P

HEAD_DIM = 64
QLEN = 32
NQ_ROW = 8
NDOC = 8


EPS_NORM = 1e-05
EPS_EMBED = 1e-06
POOL_TEMP = 0.1
LOSS_TEMP = 0.1
FULL_PRECISION = lax.Precision.HIGHEST
MASKED_SCORE = -1e30


def shortened(shard):

    def short(part):
        return part.astype(jnp.bfloat16) if part.dtype == jnp.float32 else part

    return jax.tree.map(short, shard)


def contract_rows(left, right, precision=None):
    return lax.dot_general(
        left,
        right,
        (((0,), (0,)), ((), ())),
        precision=precision,
        preferred_element_type=jnp.float32,
    )


def contract_cols(left, right, precision=None):
    return lax.dot_general(
        left,
        right,
        (((1,), (1,)), ((), ())),
        precision=precision,
        preferred_element_type=jnp.float32,
    )


def norm_forward(value, gain, shift):
    centred = value - jnp.mean(value, axis=1, keepdims=True)
    rstd = lax.rsqrt(jnp.mean(centred * centred, axis=1, keepdims=True) + EPS_NORM)
    unit = centred * rstd
    return (unit * gain + shift, unit, rstd)


def norm_backward(grad, unit, rstd, gain):
    scaled = grad * gain
    return rstd * (
        scaled
        - jnp.mean(scaled, axis=1, keepdims=True)
        - unit * jnp.mean(scaled * unit, axis=1, keepdims=True)
    )


def segments_of(row_lengths, token_count):
    position = jnp.arange(token_count, dtype=jnp.int32)
    query_span = NQ_ROW * QLEN
    ends = jnp.cumsum(row_lengths)
    passed = jnp.sum((position[:, None] - query_span >= ends[None, :]).astype(jnp.int32), axis=1)
    return jnp.where(position < query_span, position // QLEN, NQ_ROW + passed)


def normalize_cut(raw, width):
    part = raw[:, :width]
    scale = lax.rsqrt(jnp.sum(part * part, axis=1, keepdims=True) + EPS_EMBED)
    return (part * scale, part, scale)


def normalize_back(grad, part, scale, full_width):
    result = scale * grad - part * (scale * scale * scale) * jnp.sum(
        part * grad, axis=1, keepdims=True
    )
    return jnp.pad(result, ((0, 0), (0, full_width - grad.shape[1])))


def masked_scores(query_block, key_rows, block_segments, segments):
    scores = jnp.einsum(
        "qhd,khd->hqk", query_block, key_rows, preferred_element_type=jnp.float32
    ) * HEAD_DIM ** (-0.5)
    return jnp.where((block_segments[:, None] == segments[None, :])[None], scores, MASKED_SCORE)


def attend_forward(query_rows, key_rows, value_rows, segments, block_rows):
    token_count = query_rows.shape[0]

    def one_block(block_start):
        query_block = lax.dynamic_slice_in_dim(query_rows, block_start, block_rows, 0)
        block_segments = lax.dynamic_slice_in_dim(segments, block_start, block_rows, 0)
        scores = masked_scores(query_block, key_rows, block_segments, segments)
        highest = jnp.max(scores, axis=2, keepdims=True)
        expo = jnp.exp(scores - highest)
        totals = jnp.sum(expo, axis=2, keepdims=True)
        weights = (expo / totals).astype(jnp.bfloat16)
        mixed = jnp.einsum("hqk,khd->qhd", weights, value_rows, preferred_element_type=jnp.float32)
        return (mixed.astype(jnp.bfloat16), (highest + jnp.log(totals))[:, :, 0])

    starts = jnp.arange(token_count // block_rows, dtype=jnp.int32) * block_rows
    mixed, log_totals = lax.map(one_block, starts)
    return (mixed.reshape(token_count, -1), log_totals)


def attend_backward(query_rows, key_rows, value_rows, segments, log_totals, grad_mixed, block_rows):
    token_count, local_heads, head_size = query_rows.shape
    scale = HEAD_DIM ** (-0.5)
    grad_heads = grad_mixed.reshape(token_count, local_heads, head_size)

    def one_block(carried, inputs):
        grad_keys, grad_values = carried
        block_start, block_lse = inputs
        query_block = lax.dynamic_slice_in_dim(query_rows, block_start, block_rows, 0)
        grad_block = lax.dynamic_slice_in_dim(grad_heads, block_start, block_rows, 0)
        block_segments = lax.dynamic_slice_in_dim(segments, block_start, block_rows, 0)
        scores = masked_scores(query_block, key_rows, block_segments, segments)
        probs = jnp.exp(scores - block_lse[:, :, None])
        grad_probs = jnp.einsum(
            "qhd,khd->hqk", grad_block, value_rows, preferred_element_type=jnp.float32
        )
        inner = jnp.sum(probs * grad_probs, axis=2, keepdims=True)
        grad_scores = (probs * (grad_probs - inner)).astype(jnp.bfloat16)
        grad_query = (
            jnp.einsum("hqk,khd->qhd", grad_scores, key_rows, preferred_element_type=jnp.float32)
            * scale
        )
        grad_keys = (
            grad_keys
            + jnp.einsum(
                "hqk,qhd->khd", grad_scores, query_block, preferred_element_type=jnp.float32
            )
            * scale
        )
        grad_values = grad_values + jnp.einsum(
            "hqk,qhd->khd",
            probs.astype(jnp.bfloat16),
            grad_block,
            preferred_element_type=jnp.float32,
        )
        return ((grad_keys, grad_values), grad_query)

    starts = jnp.arange(token_count // block_rows, dtype=jnp.int32) * block_rows
    zero_rows = jnp.zeros(key_rows.shape, jnp.float32)
    (grad_keys, grad_values), grad_queries = lax.scan(
        one_block, (zero_rows, zero_rows), (starts, log_totals)
    )
    flat_width = local_heads * head_size
    return (
        grad_queries.reshape(token_count, flat_width),
        grad_keys.reshape(token_count, flat_width),
        grad_values.reshape(token_count, flat_width),
    )


def local(
    tokens,
    lengths,
    pairing,
    w_qkv,
    b_qv,
    w_out,
    b_out,
    ln_gain,
    ln_bias,
    w_up,
    b_up,
    w_down,
    b_down,
    w_proj,
    cot,
):
    tensor_count = lax.axis_size("tensor")
    tensor_index = lax.axis_index("tensor")
    data_index = lax.axis_index("dp")
    token_count = tokens.shape[0]
    share_rows = token_count // tensor_count
    block_rows = min(512, token_count)
    own_start = tensor_index * share_rows
    full_qkv, full_out, full_up, full_down = (
        lax.all_gather(w_qkv, "dp", axis=1, tiled=True),
        lax.all_gather(w_out, "dp", axis=1, tiled=True),
        lax.all_gather(w_up, "dp", axis=0, tiled=True),
        lax.all_gather(w_down, "dp", axis=1, tiled=True),
    )
    head_width = full_qkv.shape[2]
    local_heads = head_width // HEAD_DIM
    row_lengths = lax.dynamic_index_in_dim(lengths, data_index, 0, keepdims=False)
    segments = segments_of(row_lengths, token_count)
    projected = jnp.einsum("td,kdw->ktw", tokens, full_qkv, preferred_element_type=jnp.float32)
    qv_bias = b_qv.astype(jnp.float32)
    query_rows = (
        (projected[0] + qv_bias[0]).astype(jnp.bfloat16).reshape(token_count, local_heads, HEAD_DIM)
    )
    key_rows = projected[1].astype(jnp.bfloat16).reshape(token_count, local_heads, HEAD_DIM)
    value_rows = (
        (projected[2] + qv_bias[1]).astype(jnp.bfloat16).reshape(token_count, local_heads, HEAD_DIM)
    )
    mixed, log_totals = attend_forward(query_rows, key_rows, value_rows, segments, block_rows)
    attn_terms = jnp.dot(mixed, full_out, preferred_element_type=jnp.float32)
    attn_sum = lax.psum_scatter(
        attn_terms.astype(jnp.bfloat16), "tensor", scatter_dimension=0, tiled=True
    ).astype(jnp.float32)
    own_tokens = lax.dynamic_slice_in_dim(tokens, own_start, share_rows, 0).astype(jnp.float32)
    gains = ln_gain.astype(jnp.float32)
    shifts = ln_bias.astype(jnp.float32)
    normed, unit_one, rstd_one = norm_forward(
        own_tokens + attn_sum + b_out.astype(jnp.float32), gains[0], shifts[0]
    )
    normed_all = lax.all_gather(normed.astype(jnp.bfloat16), "tensor", axis=0, tiled=True)
    up_value = jnp.dot(normed_all, full_up, preferred_element_type=jnp.float32) + b_up.astype(
        jnp.float32
    )
    activation = jax.nn.gelu(up_value, approximate=False).astype(jnp.bfloat16)
    ffn_terms = jnp.dot(activation, full_down, preferred_element_type=jnp.float32)
    ffn_sum = lax.psum_scatter(
        ffn_terms.astype(jnp.bfloat16), "tensor", scatter_dimension=0, tiled=True
    ).astype(jnp.float32)
    result, unit_two, rstd_two = norm_forward(
        normed + ffn_sum + b_down.astype(jnp.float32), gains[1], shifts[1]
    )
    result_low = result.astype(jnp.bfloat16)
    embed = jnp.dot(result_low, w_proj, preferred_element_type=jnp.float32).astype(jnp.bfloat16)
    embed_all = lax.all_gather(embed, ("dp", "tensor"), axis=0, tiled=True)
    row_count = lengths.shape[0]
    proj_width = w_proj.shape[1]
    widths = (proj_width, 3 * proj_width // 4, proj_width // 2)
    per_device = pairing.shape[1]
    query_count = per_device * QLEN
    query_span = NQ_ROW * QLEN
    emb_rows = embed_all.reshape(row_count, token_count, proj_width)
    my_row = lax.dynamic_index_in_dim(emb_rows, data_index, 0, keepdims=False)
    query_raw = lax.dynamic_slice_in_dim(my_row, tensor_index * query_count, query_count, 0).astype(
        jnp.float32
    )
    query_levels = [normalize_cut(query_raw, width) for width in widths]
    query_units = [level_parts[0].astype(jnp.bfloat16) for level_parts in query_levels]
    doc_numbers = jnp.arange(NDOC, dtype=jnp.int32)

    def row_pool(carried, inputs):
        row_emb, lengths_row = inputs
        row_hot = (
            segments_of(lengths_row, token_count)[:, None] == NQ_ROW + doc_numbers[None, :]
        ).astype(jnp.float32)
        row_raw = row_emb.astype(jnp.float32)
        pooled_list = []
        sums_list = []
        for width, query_unit in zip(widths, query_units):
            doc_unit = normalize_cut(row_raw, width)[0].astype(jnp.bfloat16)
            expo = jnp.exp(contract_cols(query_unit, doc_unit) / POOL_TEMP)
            sums = jnp.dot(expo, row_hot, precision=FULL_PRECISION)
            pooled = POOL_TEMP * jnp.log(sums / lengths_row.astype(jnp.float32))
            pooled_list.append(jnp.sum(pooled.reshape(per_device, QLEN, NDOC), axis=1))
            sums_list.append(sums)
        return (carried, (jnp.stack(pooled_list), jnp.stack(sums_list)))

    _, (row_scores, row_sums) = lax.scan(row_pool, 0, (emb_rows, lengths))
    logits = (
        jnp.transpose(row_scores, (2, 1, 0, 3)).reshape(per_device, 3, row_count * NDOC) / LOSS_TEMP
    )
    own_pairs = pairing[0]
    target = jnp.take_along_axis(
        logits, jnp.broadcast_to(own_pairs[:, None, None], (per_device, 3, 1)), axis=2
    )[:, :, 0]
    loss_out = jnp.sum(jax.nn.logsumexp(logits, axis=2) - target, axis=1).reshape(1, per_device)
    picked = (
        jnp.arange(row_count * NDOC, dtype=jnp.int32)[None, None, :] == own_pairs[:, None, None]
    ).astype(jnp.float32)
    grad_logits = (jax.nn.softmax(logits, axis=2) - picked) / LOSS_TEMP
    grad_rows = jnp.transpose(grad_logits.reshape(per_device, 3, row_count, NDOC), (2, 1, 0, 3))
    coefficient = jnp.repeat(grad_rows, QLEN, axis=2) / row_sums

    def row_back(carried, inputs):
        row_emb, lengths_row, row_coef = inputs
        row_hot = (
            segments_of(lengths_row, token_count)[:, None] == NQ_ROW + doc_numbers[None, :]
        ).astype(jnp.float32)
        row_raw = row_emb.astype(jnp.float32)
        new_carried = []
        row_grad = jnp.zeros((token_count, proj_width), jnp.float32)
        for level_index in range(3):
            width = widths[level_index]
            doc_unit_f, doc_part, doc_scale = normalize_cut(row_raw, width)
            doc_unit = doc_unit_f.astype(jnp.bfloat16)
            expo = jnp.exp(contract_cols(query_units[level_index], doc_unit) / POOL_TEMP)
            spread = contract_cols(row_coef[level_index], row_hot, FULL_PRECISION)
            grad_sim = (expo * spread).astype(jnp.bfloat16)
            new_carried.append(
                carried[level_index]
                + jnp.dot(grad_sim, doc_unit, preferred_element_type=jnp.float32)
            )
        return (tuple(new_carried), row_grad)

    zero_query = tuple((jnp.zeros((query_count, width), jnp.float32) for width in widths))
    query_grads, doc_grads = lax.scan(row_back, zero_query, (emb_rows, lengths, coefficient))
    grad_query = jnp.zeros((query_count, proj_width), jnp.float32)
    for level_index in range(3):
        level_parts = query_levels[level_index]
        grad_query = grad_query + normalize_back(
            query_grads[level_index], level_parts[1], level_parts[2], proj_width
        )
    coef_mine = jnp.transpose(coefficient, (2, 1, 0, 3)).reshape(query_count, 3, row_count * NDOC)
    coef_all, grad_query_all = (
        lax.all_gather(shortened(coef_mine), ("dp", "tensor"), axis=0, tiled=True).astype(
            coef_mine.dtype
        ),
        lax.all_gather(
            grad_query.astype(jnp.bfloat16), ("dp", "tensor"), axis=0, tiled=True
        ).astype(grad_query.dtype),
    )
    own_raw = embed.astype(jnp.float32)
    own_segments = lax.dynamic_slice_in_dim(segments, own_start, share_rows, 0)
    own_docs = jnp.where(own_segments >= NQ_ROW, data_index * NDOC + own_segments - NQ_ROW, -1)
    own_hot = (own_docs[:, None] == jnp.arange(row_count * NDOC, dtype=jnp.int32)[None, :]).astype(
        jnp.float32
    )
    queries_all = (
        emb_rows[:, :query_span].reshape(row_count * query_span, proj_width).astype(jnp.float32)
    )
    grad_embed = jnp.zeros((share_rows, proj_width), jnp.float32)
    for level_index in range(3):
        width = widths[level_index]
        query_unit_all = normalize_cut(queries_all, width)[0].astype(jnp.bfloat16)
        doc_unit_f, doc_part, doc_scale = normalize_cut(own_raw, width)
        expo = jnp.exp(contract_cols(query_unit_all, doc_unit_f.astype(jnp.bfloat16)) / POOL_TEMP)
        spread = contract_cols(coef_all[:, level_index], own_hot, FULL_PRECISION)
        grad_sim = (expo * spread).astype(jnp.bfloat16)
        grad_doc = contract_rows(grad_sim, query_unit_all)
        grad_embed = grad_embed + normalize_back(grad_doc, doc_part, doc_scale, proj_width)
    row_query_grads = lax.dynamic_slice_in_dim(
        grad_query_all, data_index * query_span, query_span, 0
    )
    padded = jnp.pad(row_query_grads, ((0, token_count - query_span), (0, 0)))
    grad_embed = grad_embed + lax.dynamic_slice_in_dim(padded, own_start, share_rows, 0)
    proj_float = w_proj.astype(jnp.float32)
    grad_result = cot.astype(jnp.float32) + contract_cols(grad_embed, proj_float, FULL_PRECISION)
    proj_grad = contract_rows(result_low.astype(jnp.float32), grad_embed, FULL_PRECISION)
    gain_two = jnp.sum(grad_result * unit_two, axis=0)
    shift_two = jnp.sum(grad_result, axis=0)
    grad_second = norm_backward(grad_result, unit_two, rstd_two, gains[1])
    grad_ffn = grad_second.astype(jnp.bfloat16)
    down_bias = jnp.sum(grad_ffn.astype(jnp.float32), axis=0)
    grad_ffn_all = lax.all_gather(grad_ffn, "tensor", axis=0, tiled=True)
    grad_act = contract_cols(grad_ffn_all, full_down)
    down_grad = contract_rows(activation, grad_ffn_all)
    _, gelu_pull = jax.vjp(partial(jax.nn.gelu, approximate=False), up_value)
    grad_up = gelu_pull(grad_act)[0].astype(jnp.bfloat16)
    up_bias = jnp.sum(grad_up.astype(jnp.float32), axis=0)
    up_grad = contract_rows(normed_all, grad_up)
    normed_terms = contract_cols(grad_up, full_up)
    grad_normed = (
        lax.psum_scatter(
            normed_terms.astype(jnp.bfloat16), "tensor", scatter_dimension=0, tiled=True
        ).astype(jnp.float32)
        + grad_second
    )
    gain_one = jnp.sum(grad_normed * unit_one, axis=0)
    shift_one = jnp.sum(grad_normed, axis=0)
    grad_first = norm_backward(grad_normed, unit_one, rstd_one, gains[0])
    grad_attn = grad_first.astype(jnp.bfloat16)
    out_bias = jnp.sum(grad_attn.astype(jnp.float32), axis=0)
    grad_attn_all = lax.all_gather(grad_attn, "tensor", axis=0, tiled=True)
    out_grad = contract_rows(mixed, grad_attn_all)
    grad_mixed = contract_cols(grad_attn_all, full_out).astype(jnp.bfloat16)
    grad_q, grad_k, grad_v = attend_backward(
        query_rows, key_rows, value_rows, segments, log_totals, grad_mixed, block_rows
    )
    stacked_grads = jnp.stack(
        [grad_q.astype(jnp.bfloat16), grad_k.astype(jnp.bfloat16), grad_v.astype(jnp.bfloat16)]
    )
    qkv_grad = jnp.einsum("td,ktw->kdw", tokens, stacked_grads, preferred_element_type=jnp.float32)
    input_terms = jnp.einsum(
        "ktw,kdw->td", stacked_grads, full_qkv, preferred_element_type=jnp.float32
    )
    grad_input = (
        lax.psum_scatter(
            input_terms.astype(jnp.bfloat16), "tensor", scatter_dimension=0, tiled=True
        ).astype(jnp.float32)
        + grad_first
    )
    qv_grad = jnp.stack(
        [
            jnp.sum(stacked_grads[0].astype(jnp.float32), axis=0),
            jnp.sum(stacked_grads[2].astype(jnp.float32), axis=0),
        ]
    )
    qkv_part, out_part, up_part, down_part = (
        lax.psum_scatter(
            qkv_grad.astype(jnp.bfloat16), "dp", scatter_dimension=1, tiled=True
        ).astype(jnp.float32),
        lax.psum_scatter(
            out_grad.astype(jnp.bfloat16), "dp", scatter_dimension=1, tiled=True
        ).astype(jnp.float32),
        lax.psum_scatter(
            up_grad.astype(jnp.bfloat16), "dp", scatter_dimension=0, tiled=True
        ).astype(jnp.float32),
        lax.psum_scatter(
            down_grad.astype(jnp.bfloat16), "dp", scatter_dimension=1, tiled=True
        ).astype(jnp.float32),
    )
    gain_sum, shift_sum, out_bias_sum, down_bias_sum, proj_sum = lax.psum(
        (
            jnp.stack([gain_one, gain_two]),
            jnp.stack([shift_one, shift_two]),
            out_bias,
            down_bias,
            proj_grad,
        ),
        ("dp", "tensor"),
    )
    qv_sum, up_bias_sum = lax.psum((qv_grad, up_bias), "dp")
    return (
        result_low,
        loss_out,
        grad_input.astype(jnp.bfloat16),
        qkv_part,
        qv_sum,
        out_part,
        out_bias_sum,
        gain_sum,
        shift_sum,
        up_part,
        up_bias_sum,
        down_part,
        down_bias_sum,
        proj_sum,
    )


SWAP = [(0, 1), (1, 0)]
TURN = [(0, 0), (1, 2), (2, 1), (3, 3)]
FAR = [(0, 3), (3, 0), (1, 2), (2, 1)]
NEAR = [(0, 1), (1, 0), (2, 3), (3, 2)]
BF = jnp.bfloat16
F32 = jnp.float32


def dot(left, right):
    return jnp.dot(left, right, preferred_element_type=F32)


CORES = ("c", "y")


def tie(value, *others):
    return lax.optimization_barrier((value,) + others)[0]


def tie_all(values, *others):
    return lax.optimization_barrier(tuple(values) + others)[: len(values)]


def exchange(*moves):
    return lax.optimization_barrier(
        tuple(lax.ppermute(value, axis, steps) for value, axis, steps in moves)
    )


def swap(value, axis):
    return lax.ppermute(value, axis, SWAP)


def pair_up(first, second, own_index, axis):
    return jnp.where(
        own_index == 0, jnp.stack([first, second], axis), jnp.stack([second, first], axis)
    )


def far_pair(value, far, z):
    return jnp.where(z < 2, jnp.stack([value, far]), jnp.stack([far, value]))


def whole_line(pair, other, z):
    return jnp.where(
        (z == 0) | (z == 3),
        jnp.stack([pair[0], other[0], other[1], pair[1]]),
        jnp.stack([other[0], pair[0], pair[1], other[1]]),
    )


def first_moves(line):
    half = line.shape[1] // 2
    return ((line[:, :half], "x", SWAP), (line[:, half:], "y", SWAP))


def first_parts(line, moved, x, y):
    half = line.shape[1] // 2
    return (pair_up(line[:, :half], moved[0], x, 1), pair_up(line[:, half:], moved[1], y, 1))


def last_moves(parts):
    return ((parts[0], "y", SWAP), (parts[1], "x", SWAP))


def full_rows(parts, moved, x, y):
    low = pair_up(parts[0], moved[0], y, 2)
    high = pair_up(parts[1], moved[1], x, 1)
    return jnp.concatenate([low, high], axis=3).reshape(-1, low.shape[-1])


def at(blocks, index, axis):
    return lax.dynamic_index_in_dim(blocks, index, axis, keepdims=False)


def side_move(blocks, axis_name, own_index, axis):
    return (at(blocks, 1 - own_index, axis).astype(BF), axis_name, SWAP)


def side_sum(blocks, got, own_index, axis):
    return at(blocks, own_index, axis).astype(F32) + got.astype(F32)


def near_move(line, z):
    ends = (z == 0) | (z == 3)
    outer, inner = jnp.stack([line[0], line[3]]), line[1:3]
    return (jnp.where(ends, inner, outer).astype(BF), "z", NEAR)


def near_sum(line, got, z):
    ends = (z == 0) | (z == 3)
    return jnp.where(ends, jnp.stack([line[0], line[3]]), line[1:3]) + got.astype(F32)


def far_move(pair, z):
    return (jnp.where(z < 2, pair[1], pair[0]).astype(BF), "z", FAR)


def far_sum(pair, got, z):
    return jnp.where(z < 2, pair[0], pair[1]) + got.astype(F32)


def blocks_of(left, right):
    return contract_rows(left, right).astype(BF).reshape(4, 2, 2, 64, right.shape[1])


def sum_moves(blocks, x, y):
    half = blocks.shape[3] // 2
    return (
        side_move(blocks[..., :half, :], "x", x, 1),
        side_move(blocks[..., half:, :], "y", y, 2),
    )


def sum_parts(blocks, moved, x, y):
    half = blocks.shape[3] // 2
    return (
        side_sum(blocks[..., :half, :], moved[0], x, 1),
        side_sum(blocks[..., half:, :], moved[1], y, 2),
    )


def line_moves(parts, x, y):
    return (side_move(parts[0], "y", y, 1), side_move(parts[1], "x", x, 1))


def line_of(parts, moved, x, y):
    return jnp.concatenate(
        [side_sum(parts[0], moved[0], y, 1), side_sum(parts[1], moved[1], x, 1)], axis=1
    )


def tile_bounds(row_lengths, token_count):
    ends = jnp.cumsum(row_lengths)
    span = NQ_ROW * QLEN
    first = jnp.arange(token_count // TILE, dtype=jnp.int32) * TILE - span
    last = first + TILE - 1
    begin = jnp.max(jnp.where(ends[None, :] <= first[:, None], ends[None, :], 0), axis=1)
    end = jnp.min(jnp.where(ends[None, :] > last[:, None], ends[None, :], token_count), axis=1)
    low = jnp.where(first < 0, 0, (begin + span) // TILE)
    high = jnp.where(first < 0, 1, (end + span + TILE - 1) // TILE)
    return jnp.stack([low, high]).astype(jnp.int32)


def token_spans(row_lengths, token_count):
    ends = jnp.cumsum(row_lengths)[:, None]
    span = NQ_ROW * QLEN
    place = jnp.arange(token_count, dtype=jnp.int32)[None, :]
    doc = place - span
    begin = jnp.max(jnp.where(ends <= doc, ends, 0), axis=0) + span
    end = jnp.min(jnp.where(ends > doc, ends, token_count), axis=0) + span
    query = place[0] // QLEN * QLEN
    return jnp.stack(
        [jnp.where(doc[0] < 0, query, begin), jnp.where(doc[0] < 0, query + QLEN, end)]
    ).astype(jnp.int32)


def rows_of(value, start, count):
    return lax.dynamic_slice_in_dim(value, start, count, 0)


TILE = 256
KEYS = 256
NEG = -1e30


def exact(left, right, dims):
    return lax.dot_general(left, right, (dims, ((), ())), preferred_element_type=F32)


def head_masks(value):
    lane = lax.broadcasted_iota(jnp.int32, value.shape, 1)
    zero = jnp.zeros_like(value)
    return (jnp.where(lane < HEAD_DIM, value, zero), jnp.where(lane < HEAD_DIM, zero, value))


def key_shift(step, spans):
    place = step * KEYS + lax.broadcasted_iota(jnp.int32, (KEYS, TILE), 0)
    inside = (place >= spans[0:1, :]) & (place < spans[1:2, :])
    return jnp.where(inside, 0.0, NEG)


def attend_kernel(bounds, own_ref, qkv_ref, spans, out_ref, lse_ref, held):
    block = pl.program_id(0)
    groups = 2
    pairs = out_ref.shape[1] // 128
    per_group = pairs // groups

    def column(pair, part):
        start = ((pair // per_group) * 3 + part) * per_group + pair % per_group
        return slice(start * 128, (start + 1) * 128)

    queries = [head_masks(own_ref[:, column(pair, 0)] * HEAD_DIM**-0.5) for pair in range(pairs)]
    heads = [(pair, head) for pair in range(pairs) for head in range(2)]

    def score(step, highest):
        rows = pl.ds(pl.multiple_of(step * KEYS, KEYS), KEYS)
        shift = key_shift(step, spans)
        fresh = []
        for index, (pair, head) in enumerate(heads):
            keys = qkv_ref[rows, column(pair, 1)]
            scores = exact(keys, queries[pair][head], ((1,), (1,))) + shift
            held[index, rows, :] = scores
            fresh.append(jnp.maximum(highest[index], jnp.max(scores, axis=0, keepdims=True)))
        return tuple(fresh)

    low = jnp.full((1, TILE), NEG, F32)
    highest = lax.fori_loop(bounds[0, block], bounds[1, block], score, (low,) * len(heads))

    def mix(step, carried):
        rows = pl.ds(pl.multiple_of(step * KEYS, KEYS), KEYS)
        fresh = []
        for index, (pair, head) in enumerate(heads):
            values = qkv_ref[rows, column(pair, 2)]
            total, mixed = carried[index]
            expo = jnp.exp(held[index, rows, :] - highest[index])
            product = exact(values, expo.astype(BF), ((0,), (0,)))
            fresh.append(
                (
                    total + jnp.sum(expo, axis=0, keepdims=True),
                    mixed + product[head * HEAD_DIM : (head + 1) * HEAD_DIM],
                )
            )
        return tuple(fresh)

    start = (jnp.zeros((1, TILE), F32), jnp.zeros((HEAD_DIM, TILE), F32))
    parts = lax.fori_loop(bounds[0, block], bounds[1, block], mix, (start,) * len(heads))
    for pair in range(pairs):
        both = [parts[2 * pair + head][1] / parts[2 * pair + head][0] for head in range(2)]
        mixed = jnp.transpose(jnp.concatenate(both, axis=0))
        out_ref[:, pair * 128 : (pair + 1) * 128] = mixed.astype(BF)
    for index in range(len(heads)):
        lse_ref[index : index + 1, :] = highest[index] + jnp.log(parts[index][0])


def attend(bounds, qkv, spans):
    count, wide = qkv.shape
    heads = wide // 3 // HEAD_DIM
    whole = lambda shape: pl.BlockSpec(shape, lambda i: (0, 0))
    return pl.pallas_call(
        attend_kernel,
        grid=(count // TILE,),
        in_specs=[
            pl.BlockSpec(memory_space=pltpu.SMEM),
            pl.BlockSpec((TILE, wide), lambda i: (i, 0)),
            whole((count, wide)),
            pl.BlockSpec((2, TILE), lambda i: (0, i)),
        ],
        out_specs=[
            pl.BlockSpec((TILE, wide // 3), lambda i: (i, 0)),
            pl.BlockSpec((heads, TILE), lambda i: (0, i)),
        ],
        out_shape=[
            jax.ShapeDtypeStruct((count, wide // 3), BF),
            jax.ShapeDtypeStruct((heads, count), F32),
        ],
        scratch_shapes=[pltpu.VMEM((heads, count, TILE), F32)],
        compiler_params=pltpu.CompilerParams(vmem_limit_bytes=40 << 20),
        cost_estimate=pl.CostEstimate(
            flops=4 * heads * count * count * 64,
            transcendentals=heads * count * count // 2,
            bytes_accessed=4 * count * wide * 2,
        ),
    )(bounds, qkv, qkv, spans)


def attend_back_kernel(
    first, bounds, own_ref, qkv_ref, out_ref, grad_ref, lse_ref, spans,
    grads_ref, sums_ref, key_sum, value_sum,
):
    block = pl.program_id(0)
    pairs = out_ref.shape[1] // 128
    heads = [(pair, head) for pair in range(pairs) for head in range(2)]
    cut = lambda index: slice(index * 128, (index + 1) * 128)

    @pl.when(block == 0)
    def _():
        key_sum[...] = jnp.zeros_like(key_sum)
        value_sum[...] = jnp.zeros_like(value_sum)
        sums_ref[...] = jnp.zeros_like(sums_ref)

    queries = [head_masks(own_ref[:, cut(pair)] * HEAD_DIM**-0.5) for pair in range(pairs)]
    grads = [head_masks(grad_ref[:, cut(pair)]) for pair in range(pairs)]
    picks = head_masks(jnp.ones((8, 128), BF))
    inner = []
    for pair, head in heads:
        product = grad_ref[:, cut(pair)].astype(F32) * out_ref[:, cut(pair)].astype(F32)
        high = product.astype(BF)
        rest = (product - high.astype(F32)).astype(BF)
        inner.append(
            (
                exact(picks[head], high, ((1,), (1,))) + exact(picks[head], rest, ((1,), (1,)))
            )[0:1]
        )
    lse = [lse_ref[first + index : first + index + 1, :] for index in range(len(heads))]

    def step_of(step, carried):
        rows = pl.ds(pl.multiple_of(step * KEYS, KEYS), KEYS)
        shift = key_shift(step, spans)
        fresh = []
        for pair in range(pairs):
            keys = qkv_ref[rows, cut(pairs + pair)]
            values = qkv_ref[rows, cut(2 * pairs + pair)]
            key_add = jnp.zeros((KEYS, 128), F32)
            value_add = jnp.zeros((KEYS, 128), F32)
            for head in range(2):
                index = 2 * pair + head
                scores = exact(keys, queries[pair][head], ((1,), (1,))) + shift
                probs = jnp.exp(scores - lse[index])
                grad_probs = exact(values, grads[pair][head], ((1,), (1,)))
                grad_scores = (probs * (grad_probs - inner[index])).astype(BF)
                value_add = value_add + exact(probs.astype(BF), grads[pair][head], ((1,), (0,)))
                key_add = key_add + exact(grad_scores, queries[pair][head], ((1,), (0,)))
                product = exact(keys, grad_scores, ((0,), (0,)))
                fresh.append(carried[index] + product[head * HEAD_DIM : (head + 1) * HEAD_DIM])
            key_sum[rows, cut(pair)] += key_add
            value_sum[rows, cut(pair)] += value_add
        return tuple(fresh)

    start = jnp.zeros((HEAD_DIM, TILE), F32)
    parts = lax.fori_loop(bounds[0, block], bounds[1, block], step_of, (start,) * len(heads))
    own = pl.ds(pl.multiple_of(block * TILE, TILE), TILE)
    for pair in range(pairs):
        grad_query = jnp.concatenate([parts[2 * pair], parts[2 * pair + 1]], axis=0)
        grad_query = jnp.transpose(grad_query * HEAD_DIM**-0.5).astype(BF)
        grads_ref[own, cut(pair)] = grad_query
        sums_ref[0:1, cut(pair)] += jnp.sum(grad_query.astype(F32), axis=0, keepdims=True)

    @pl.when(block == pl.num_programs(0) - 1)
    def _():
        wide = pairs * 128
        grad_value = value_sum[...].astype(BF)
        grads_ref[:, wide : 2 * wide] = key_sum[...].astype(BF)
        grads_ref[:, 2 * wide :] = grad_value
        sums_ref[1:2, :] = jnp.sum(grad_value.astype(F32), axis=0, keepdims=True)


def attend_back(bounds, group, qkv, mixed, grad_mixed, lse, spans):
    count = qkv.shape[0]
    wide = qkv.shape[1] // 2
    heads = wide // 3 // HEAD_DIM
    whole = lambda shape: pl.BlockSpec(shape, lambda i: (0, 0))
    return pl.pallas_call(
        partial(attend_back_kernel, group * heads),
        grid=(count // TILE,),
        in_specs=[
            pl.BlockSpec(memory_space=pltpu.SMEM),
            pl.BlockSpec((TILE, wide), lambda i: (i, group)),
            pl.BlockSpec((count, wide), lambda i: (0, group)),
            pl.BlockSpec((TILE, wide // 3), lambda i: (i, group)),
            pl.BlockSpec((TILE, wide // 3), lambda i: (i, group)),
            pl.BlockSpec((2 * heads, TILE), lambda i: (0, i)),
            pl.BlockSpec((2, TILE), lambda i: (0, i)),
        ],
        out_specs=[whole((count, wide)), whole((8, wide // 3))],
        out_shape=[
            jax.ShapeDtypeStruct((count, wide), BF),
            jax.ShapeDtypeStruct((8, wide // 3), F32),
        ],
        scratch_shapes=[
            pltpu.VMEM((count, wide // 3), F32),
            pltpu.VMEM((count, wide // 3), F32),
        ],
        compiler_params=pltpu.CompilerParams(vmem_limit_bytes=40 << 20),
        cost_estimate=pl.CostEstimate(
            flops=10 * heads * count * count * 64,
            transcendentals=heads * count * count // 2,
            bytes_accessed=8 * count * wide * 2,
        ),
    )(
        bounds, qkv, qkv, mixed, grad_mixed,
        lse, spans,
    )


ERFC = (
    -1.26551223, 1.00002368, 0.37409196, 0.09678418, -0.18628806,
    0.27886807, -1.13520398, 1.48851587, -0.82215223, 0.17087277,
)


def gelu_pair(value):
    size = jnp.abs(value) * 0.5**0.5
    ratio = 1.0 / (1.0 + 0.5 * size)
    series = jnp.full_like(value, ERFC[-1])
    for factor in ERFC[-2::-1]:
        series = series * ratio + factor
    bell = jnp.exp(-size * size)
    tail = 0.5 * ratio * bell * jnp.exp(series)
    phi = jnp.where(value < 0.0, tail, 1.0 - tail)
    return (value * phi, phi + value * bell * 0.3989422804014327)


def expand_kernel(x_ref, w_ref, b_ref, *refs):
    act_ref, slope_ref = refs[-2:]
    rows = 256
    for start in range(0, x_ref.shape[0], rows):
        part = slice(start, start + rows)
        value = exact(x_ref[part, :], w_ref[...], ((1,), (0,))) + b_ref[...]
        active, slope = gelu_pair(value)
        act_ref[part, :] = active.astype(BF)
        slope_ref[part, :] = slope.astype(BF)


def expand(value, weight, shift, first, tiles, filled=()):
    count, depth = value.shape
    width = shift.shape[1]
    tile = 256
    column = lambda rows: pl.BlockSpec((rows, tile), lambda i: (0, first + i))
    return pl.pallas_call(
        expand_kernel,
        grid=(tiles,),
        in_specs=[
            pl.BlockSpec((count, depth), lambda i: (0, 0)),
            column(depth),
            column(1),
        ]
        + [pl.BlockSpec(memory_space=pl.ANY)] * len(filled),
        out_specs=[column(count)] * 2,
        out_shape=[jax.ShapeDtypeStruct((count, width), BF)] * 2,
        input_output_aliases={3: 0, 4: 1} if filled else {},
        compiler_params=pltpu.CompilerParams(vmem_limit_bytes=32 << 20),
        cost_estimate=pl.CostEstimate(
            flops=2 * count * depth * tile * tiles,
            transcendentals=3 * count * tile * tiles,
            bytes_accessed=2 * (count * depth + depth * tile * tiles + 2 * count * tile * tiles),
        ),
    )(value, weight, shift, *filled)


def cut_levels(raw, cuts):
    lane = lax.broadcasted_iota(jnp.int32, raw.shape, 1)
    levels = []
    for cut in cuts:
        part = jnp.where(lane < cut, raw, 0.0)
        scale = lax.rsqrt(jnp.sum(part * part, axis=1, keepdims=True) + EPS_EMBED)
        levels.append(((part * scale).astype(BF), part, scale))
    return levels


def pool_kernel(cuts, span, q_ref, d_ref, seg_ref, out_ref, units, hot):
    @pl.when(pl.program_id(0) == 0)
    def _():
        raw = d_ref[span:, :].astype(F32)
        for level, parts in enumerate(cut_levels(raw, cuts)):
            units[level] = parts[0]
        doc = lax.broadcasted_iota(jnp.int32, hot.shape, 0)
        hot[...] = (seg_ref[:, span:] == NQ_ROW + doc).astype(F32).astype(BF)

    levels = cut_levels(q_ref[...].astype(F32), cuts)
    for level in range(len(cuts)):
        similar = exact(units[level], levels[level][0], ((1,), (1,)))
        expo = jnp.exp(similar * (1.0 / POOL_TEMP))
        high = expo.astype(BF)
        rest = (expo - high.astype(F32)).astype(BF)
        out_ref[level * NDOC : (level + 1) * NDOC, :] = exact(
            hot[...], high, ((1,), (0,))
        ) + exact(hot[...], rest, ((1,), (0,)))


def pool(cuts, span, queries, row_embed, seg_row):
    count, width = queries.shape
    tokens = row_embed.shape[0]
    whole = lambda shape: pl.BlockSpec(shape, lambda i: (0, 0))
    return pl.pallas_call(
        partial(pool_kernel, cuts, span),
        grid=(count // TILE,),
        in_specs=[
            pl.BlockSpec((TILE, width), lambda i: (i, 0)),
            whole((tokens, width)),
            whole((1, tokens)),
        ],
        out_specs=pl.BlockSpec((len(cuts) * NDOC, TILE), lambda i: (0, i)),
        out_shape=jax.ShapeDtypeStruct((len(cuts) * NDOC, count), F32),
        scratch_shapes=[
            pltpu.VMEM((len(cuts), tokens - span, width), BF),
            pltpu.VMEM((NDOC, tokens - span), BF),
        ],
        compiler_params=pltpu.CompilerParams(vmem_limit_bytes=32 << 20),
        cost_estimate=pl.CostEstimate(
            flops=2 * len(cuts) * count * tokens * 256,
            transcendentals=len(cuts) * count * tokens,
            bytes_accessed=2 * (count + tokens) * width,
        ),
    )(queries, row_embed, seg_row)


def level_back(grad, part, scale):
    return scale * grad - part * (scale * scale * scale) * jnp.sum(
        part * grad, axis=1, keepdims=True
    )


def pool_back_kernel(
    cuts, span, q_ref, d_ref, seg_ref, coef_ref, q_out, d_out, units, units_t, hot, sums
):
    step = pl.program_id(0)

    @pl.when(step == 0)
    def _():
        raw = d_ref[span:, :].astype(F32)
        for level, parts in enumerate(cut_levels(raw, cuts)):
            units[level] = parts[0]
            units_t[level] = jnp.transpose(parts[0])
        doc = lax.broadcasted_iota(jnp.int32, hot.shape, 0)
        wanted = NQ_ROW + jnp.where(doc < NDOC, doc, doc - NDOC)
        hot[...] = (seg_ref[:, span:] == wanted).astype(F32).astype(BF)
        sums[...] = jnp.zeros_like(sums)

    levels = cut_levels(q_ref[...].astype(F32), cuts)
    total = jnp.zeros(q_ref.shape, F32)
    for level in range(len(cuts)):
        unit, part, scale = levels[level]
        similar = exact(units[level], unit, ((1,), (1,)))
        coef = coef_ref[level * NDOC : (level + 1) * NDOC, :]
        high = coef.astype(BF).astype(F32)
        both = jnp.concatenate([high, coef - high], axis=0).astype(BF)
        spread = exact(hot[...], both, ((0,), (0,)))
        grad = (jnp.exp(similar * (1.0 / POOL_TEMP)) * spread).astype(BF)
        sums[level] += exact(grad, unit, ((1,), (0,)))
        grad_unit = jnp.transpose(exact(units_t[level], grad, ((1,), (0,))))
        total = total + level_back(grad_unit, part, scale)
    q_out[...] = total.astype(BF)

    @pl.when(step == pl.num_programs(0) - 1)
    def _():
        raw = d_ref[span:, :].astype(F32)
        result = jnp.zeros(raw.shape, F32)
        for level, parts in enumerate(cut_levels(raw, cuts)):
            lane = lax.broadcasted_iota(jnp.int32, raw.shape, 1)
            grad = jnp.where(lane < cuts[level], sums[level], 0.0)
            result = result + level_back(grad, parts[1], parts[2])
        d_out[...] = result


def pool_back(cuts, span, queries, row_embed, seg_row, coef):
    count, width = queries.shape
    tokens = row_embed.shape[0]
    docs = tokens - span
    whole = lambda shape: pl.BlockSpec(shape, lambda i: (0, 0))
    return pl.pallas_call(
        partial(pool_back_kernel, cuts, span),
        grid=(count // TILE,),
        in_specs=[
            pl.BlockSpec((TILE, width), lambda i: (i, 0)),
            whole((tokens, width)),
            whole((1, tokens)),
            pl.BlockSpec((len(cuts) * NDOC, TILE), lambda i: (0, i)),
        ],
        out_specs=[pl.BlockSpec((TILE, width), lambda i: (i, 0)), whole((docs, width))],
        out_shape=[
            jax.ShapeDtypeStruct((count, width), BF),
            jax.ShapeDtypeStruct((docs, width), F32),
        ],
        scratch_shapes=[
            pltpu.VMEM((len(cuts), docs, width), BF),
            pltpu.VMEM((len(cuts), width, docs), BF),
            pltpu.VMEM((2 * NDOC, docs), BF),
            pltpu.VMEM((len(cuts), docs, width), F32),
        ],
        compiler_params=pltpu.CompilerParams(vmem_limit_bytes=32 << 20),
        cost_estimate=pl.CostEstimate(
            flops=2 * len(cuts) * count * docs * 512,
            transcendentals=len(cuts) * count * docs,
            bytes_accessed=4 * (count + tokens) * width,
        ),
    )(queries, row_embed, seg_row, coef)


def local_chip(
    tokens,
    lengths,
    pairing,
    w_qkv,
    b_qv,
    w_out,
    b_out,
    ln_gain,
    ln_bias,
    w_up,
    b_up,
    w_down,
    b_down,
    w_proj,
    cot,
):
    z, x, c, y = (lax.axis_index(name) for name in ("z", "x", "c", "y"))
    chip = 4 * z + 2 * x + y
    token_count, width = tokens.shape
    share = token_count // 2
    own_start, other_start = c * share, (1 - c) * share
    gains, shifts = ln_gain.astype(F32), ln_bias.astype(F32)

    half_width = w_qkv.shape[2]
    up_wide = w_up.shape[1]
    chip_count = lengths.shape[0]
    half_queries = NQ_ROW // 2
    query_total = chip_count * half_queries
    quarter = half_width // 2
    qkv_rows = jnp.concatenate(
        [w_qkv[k][:, g * quarter : (g + 1) * quarter] for g in range(2) for k in range(3)], axis=1
    )
    pair_rows = jnp.pad(pairing.astype(BF), ((0, 63), (0, 128 - half_queries)))
    mid_rows = jnp.concatenate([w_up, w_out.T, pair_rows], axis=1)
    bias = jnp.concatenate([b_qv.reshape(-1), b_up])[None].astype(F32)
    got = exchange(
        (qkv_rows, CORES, TURN), (tokens, "c", SWAP), (bias, "y", SWAP)
    )
    qkv_rows = got[0]
    row = jnp.where(c == y, tokens, got[1])
    bias = jnp.where(c == y, bias, got[2])
    (rest_rows,) = exchange(
        (tie(jnp.concatenate([mid_rows, w_down.T], axis=1), row), CORES, TURN)
    )
    (far,) = exchange((qkv_rows, "z", FAR))
    qkv_pair = far_pair(qkv_rows, far, z)
    mid_wide = mid_rows.shape[1]
    rest_rows = tie(rest_rows, qkv_pair)
    mid_rows, down_rows = rest_rows[:, :mid_wide], rest_rows[:, mid_wide:]
    got = exchange((qkv_pair, "z", NEAR), (mid_rows, "z", FAR), (cot[16:], CORES, TURN))
    own_cot = got[2]
    qkv_line = whole_line(qkv_pair, got[0], z)
    mid_pair = far_pair(mid_rows, got[1], z)
    got = exchange(*first_moves(qkv_line), (mid_pair, "z", NEAR))
    qkv_parts = first_parts(qkv_line, got, x, y)
    mid_line = whole_line(mid_pair, got[2], z)
    last = last_moves(qkv_parts)
    got = exchange(*last, (tie(down_rows, mid_line), "z", FAR), *first_moves(mid_line))
    full_qkv = full_rows(qkv_parts, got, x, y)
    down_pair = far_pair(down_rows, got[2], z)
    mid_parts = first_parts(mid_line, got[3:], x, y)
    (near,) = exchange((down_pair, "z", NEAR))
    down_line = whole_line(down_pair, near, z)
    got = exchange(*last_moves(mid_parts), *first_moves(down_line))
    full_mid = full_rows(mid_parts, got, x, y)
    down_parts = first_parts(down_line, got[2:], x, y)
    full_out = full_mid[:, up_wide : up_wide + half_width]
    pairs = full_mid[:, up_wide + half_width :].reshape(chip_count, 64, 128)
    pairs = pairs[:, 0, :half_queries].astype(jnp.int32).reshape(1, query_total)
    row_lengths = lax.dynamic_index_in_dim(lengths, chip, 0, keepdims=False)
    segments = segments_of(row_lengths, token_count)
    seg_row, spans = segments[None, :], token_spans(row_lengths, token_count)
    query_span = NQ_ROW * QLEN
    bounds = tile_bounds(row_lengths, token_count)
    no_bias = jnp.zeros((1, quarter), F32)
    qkv_bias = jnp.concatenate(
        [
            part
            for g in range(2)
            for part in (
                bias[:, g * quarter : (g + 1) * quarter],
                no_bias,
                bias[:, half_width + g * quarter : half_width + (g + 1) * quarter],
            )
        ],
        axis=1,
    )
    qkv = (dot(row, full_qkv) + qkv_bias).astype(BF)
    mixed, lse = attend(bounds, tie(qkv, down_line), spans)

    def row_sum(left, weight_t, transposed):
        times = contract_cols if transposed else dot
        theirs = swap(times(left(1), weight_t).astype(BF), "c")
        return times(left(0), weight_t) + theirs.astype(F32)

    def mixed_half(which):
        return rows_of(mixed, other_start if which else own_start, share)

    other_attn = swap(contract_cols(mixed_half(1), full_out).astype(BF), "c")
    other_attn, cot_head = lax.optimization_barrier((other_attn, cot[:16]))
    cot_head = lax.ppermute(cot_head, CORES, TURN)
    cot_head, *down_parts = lax.optimization_barrier((cot_head,) + tuple(down_parts))
    own_cot = jnp.concatenate([cot_head, own_cot], axis=0)
    down_got = exchange(*last_moves(down_parts))
    attn_sum = contract_cols(mixed_half(0), full_out) + other_attn.astype(F32)
    own_tokens = rows_of(row, own_start, share).astype(F32)
    normed, unit_one, rstd_one = norm_forward(
        own_tokens + attn_sum + b_out.astype(F32), gains[0], shifts[0]
    )
    normed_low = normed.astype(BF)
    normed_all = jnp.concatenate([normed_low, swap(normed_low, "c")], axis=0)
    activation, slope = expand(
        normed_all, full_mid, bias[:, 2 * half_width :], 0, up_wide // 256
    )
    full_down = full_rows(down_parts, down_got, x, y)
    ffn_sum = row_sum(
        lambda which: activation[which * share : (which + 1) * share], full_down, True
    )
    result, unit_two, rstd_two = norm_forward(
        normed + ffn_sum + b_down.astype(F32), gains[1], shifts[1]
    )
    result_low = result.astype(BF)
    embed = dot(result_low, w_proj).astype(BF)

    other_embed = swap(embed, "c")
    row_embed = jnp.where(
        c == 0,
        jnp.concatenate([embed, other_embed], axis=0),
        jnp.concatenate([other_embed, embed], axis=0),
    )
    half_span = query_span // 2
    own_queries = rows_of(row_embed, c * half_span, half_span)
    chips = ("z", "x", "y")
    queries = lax.all_to_all(
        jnp.broadcast_to(own_queries[None], (chip_count,) + own_queries.shape), chips, 0, 0
    ).reshape(chip_count * half_span, -1)
    proj_width = w_proj.shape[1]
    cuts = (proj_width, 3 * proj_width // 4, proj_width // 2)
    sums = pool(cuts, query_span, queries, row_embed, seg_row)
    doc_sizes = jnp.tile(row_lengths.astype(F32), 3)[:, None]
    group = (
        jnp.arange(query_total * QLEN, dtype=jnp.int32)[:, None] // QLEN
        == jnp.arange(query_total, dtype=jnp.int32)[None, :]
    ).astype(F32)
    pooled = POOL_TEMP * jnp.log(sums / doc_sizes)
    logits = jnp.dot(pooled, group, precision=FULL_PRECISION) / LOSS_TEMP
    logits = logits.reshape(3, NDOC, query_total)
    doc_numbers = chip * NDOC + jnp.arange(NDOC, dtype=jnp.int32)
    picked = (doc_numbers[:, None] == pairs).astype(F32)
    own_high = jnp.max(logits, axis=1)
    own_lse = own_high + jnp.log(jnp.sum(jnp.exp(logits - own_high[:, None]), axis=1))
    own_target = jnp.sum(logits * picked, axis=1)
    notes = jnp.pad(jnp.concatenate([own_lse, own_target], axis=1), ((0, 5), (0, 0)))
    notes = lax.all_to_all(
        jnp.broadcast_to(notes[None], (chip_count,) + notes.shape), chips, 0, 0
    )
    chip_lse = notes[:, :3, :query_total]
    high = jnp.max(chip_lse, axis=0)
    all_lse = high + jnp.log(jnp.sum(jnp.exp(chip_lse - high), axis=0))
    target = jnp.sum(notes[:, :3, query_total:], axis=0)
    losses = jnp.sum(all_lse - target, axis=0).reshape(chip_count, half_queries)
    grad_logits = (jnp.exp(logits - all_lse[:, None]) - picked) / LOSS_TEMP
    coefficient = (
        lax.dot_general(
            grad_logits.reshape(3 * NDOC, query_total),
            group,
            (((1,), (1,)), ((), ())),
            precision=FULL_PRECISION,
        )
        / sums
    )
    query_grad, doc_grad = pool_back(cuts, query_span, queries, row_embed, seg_row, coefficient)
    grad_blocks = lax.all_to_all(
        query_grad.reshape(chip_count, half_span, proj_width), chips, 0, 0
    )
    own_query_grad = jnp.sum(grad_blocks.astype(F32), axis=0)
    row_grad = jnp.concatenate([jnp.zeros((query_span, proj_width), F32), doc_grad], axis=0)
    row_grad = lax.dynamic_update_slice_in_dim(row_grad, own_query_grad, c * half_span, 0)
    grad_embed = rows_of(row_grad, own_start, share) + swap(
        rows_of(row_grad, other_start, share), "c"
    )

    proj_low = w_proj
    grad_embed_low = grad_embed.astype(BF)
    grad_embed_rest = (grad_embed - grad_embed_low.astype(F32)).astype(BF)
    grad_result = own_cot.astype(F32) + (
        contract_cols(grad_embed_low, proj_low) + contract_cols(grad_embed_rest, proj_low)
    )
    proj_grad = contract_rows(result_low, grad_embed_low) + contract_rows(
        result_low, grad_embed_rest
    )
    gain_two = jnp.sum(grad_result * unit_two, axis=0)
    shift_two = jnp.sum(grad_result, axis=0)
    grad_second = norm_backward(grad_result, unit_two, rstd_two, gains[1])
    grad_ffn = grad_second.astype(BF)
    down_bias = jnp.sum(grad_ffn.astype(F32), axis=0)
    other_ffn, other_losses = exchange((grad_ffn, "c", SWAP), (losses, "c", SWAP))
    losses = jnp.where(c == y, losses, other_losses)
    loss_out = rows_of(losses, 4 * z + 2 * x + c, 1)
    grad_ffn_all = jnp.concatenate([grad_ffn, other_ffn], axis=0)
    down_blocks = blocks_of(grad_ffn_all, activation)
    (y_out,) = exchange((result_low, CORES, TURN))
    down_blocks = tie(down_blocks, y_out)
    down_moved = exchange(*sum_moves(down_blocks, x, y))
    grad_up = (dot(grad_ffn_all, full_down) * slope.astype(F32)).astype(BF)
    up_bias = jnp.sum(grad_up.astype(F32), axis=0)
    up_blocks = blocks_of(normed_all, tie(grad_up, *down_moved))
    full_up = full_mid[:, :up_wide]
    grad_normed = (
        row_sum(lambda which: grad_up[which * share : (which + 1) * share], full_up, True)
        + grad_second
    )
    gain_one = jnp.sum(grad_normed * unit_one, axis=0)
    shift_one = jnp.sum(grad_normed, axis=0)
    grad_first = norm_backward(grad_normed, unit_one, rstd_one, gains[0])
    grad_attn = grad_first.astype(BF)
    out_bias = jnp.sum(grad_attn.astype(F32), axis=0)
    other_attn = swap(grad_attn, "c")
    grad_attn_all = jnp.where(
        c == 0,
        jnp.concatenate([grad_attn, other_attn], axis=0),
        jnp.concatenate([other_attn, grad_attn], axis=0),
    )
    grad_mixed = dot(grad_attn_all, full_out).astype(BF)
    out_blocks = blocks_of(grad_attn_all, mixed)
    down_parts = sum_parts(down_blocks, down_moved, x, y)
    moved = exchange(*line_moves(down_parts, x, y), *sum_moves(up_blocks, x, y))
    down_line = line_of(down_parts, moved, x, y)
    up_parts = sum_parts(up_blocks, moved[2:], x, y)
    grad_mixed, out_blocks, down_line, *up_parts = lax.optimization_barrier(
        (grad_mixed, out_blocks, down_line) + tuple(up_parts)
    )
    moved = exchange(
        near_move(down_line, z), *line_moves(up_parts, x, y), *sum_moves(out_blocks, x, y)
    )
    grads_one, sums_one = attend_back(bounds, 0, qkv, mixed, grad_mixed, lse, spans)
    down_pair = near_sum(down_line, moved[0], z)
    up_line = line_of(up_parts, moved[1:], x, y)
    out_parts = sum_parts(out_blocks, moved[3:], x, y)
    grad_mixed, down_pair, up_line, *out_parts = lax.optimization_barrier(
        (grad_mixed, down_pair, up_line) + tuple(out_parts)
    )
    moved = exchange(
        far_move(down_pair, z), near_move(up_line, z), *line_moves(out_parts, x, y)
    )
    grads_two, sums_two = attend_back(
        bounds, 1, qkv, mixed, tie(grad_mixed, grads_one), lse, spans
    )
    down_part = far_sum(down_pair, moved[0], z)
    up_pair = near_sum(up_line, moved[1], z)
    out_line = line_of(out_parts, moved[2:], x, y)
    grads_one, grads_two, down_part, up_pair, out_line = lax.optimization_barrier(
        (grads_one, grads_two, down_part, up_pair, out_line)
    )
    proj_half = rows_of(proj_grad, own_start, share) + swap(
        rows_of(proj_grad, other_start, share), "c"
    )
    shared = jnp.stack([gain_one, gain_two, shift_one, shift_two, out_bias, down_bias])
    half_sums = jnp.concatenate(
        [
            sums_one[0],
            sums_two[0],
            sums_one[1],
            sums_two[1],
            up_bias,
        ]
    )
    small = jnp.concatenate([shared.reshape(-1, 128), half_sums.reshape(-1, 128), proj_half])

    qkv_blocks = jnp.concatenate(
        [blocks_of(row, grads_one), blocks_of(row, grads_two)], axis=4
    )
    qkv_blocks, up_pair, out_line, down_part, small = lax.optimization_barrier(
        (qkv_blocks, up_pair, out_line, down_part, small)
    )
    moved = exchange(
        *sum_moves(qkv_blocks, x, y),
        far_move(up_pair, z),
        near_move(out_line, z),
        (small.astype(BF), "y", SWAP),
    )
    qkv_parts = sum_parts(qkv_blocks, moved, x, y)
    up_part = far_sum(up_pair, moved[2], z)
    out_pair = near_sum(out_line, moved[3], z)
    small = small + moved[4].astype(F32)

    def input_terms(start):
        return contract_cols(
            rows_of(grads_one, start, share), full_qkv[:, : 3 * quarter]
        ) + contract_cols(rows_of(grads_two, start, share), full_qkv[:, 3 * quarter :])

    other_terms = swap(input_terms(other_start).astype(BF), "c")
    grad_input = (input_terms(own_start) + other_terms.astype(F32) + grad_first).astype(BF)
    moved = exchange(*line_moves(qkv_parts, x, y), far_move(out_pair, z), (small.astype(BF), "x", SWAP))
    qkv_line = line_of(qkv_parts, moved, x, y)
    out_part = far_sum(out_pair, moved[2], z)
    small = small + moved[3].astype(F32)
    moved = exchange(
        near_move(qkv_line, z),
        (small.astype(BF), "z", FAR),
        (tie(grad_input, qkv_line), CORES, TURN),
    )
    qkv_pair = near_sum(qkv_line, moved[0], z)
    small = small + moved[1].astype(F32)
    grad_input = moved[2]
    ffn_part = jnp.concatenate([down_part, up_part], axis=1).astype(BF)
    moved = exchange(
        far_move(qkv_pair, z), (small.astype(BF), "z", NEAR), (tie(ffn_part, qkv_pair), CORES, TURN)
    )
    attn_part = jnp.concatenate([far_sum(qkv_pair, moved[0], z), out_part], axis=1).astype(BF)
    small = small + moved[1].astype(F32)
    ffn_part = moved[2].astype(F32)
    down_part, up_part = ffn_part[:, :up_wide], ffn_part[:, up_wide:]
    attn_part, other_small = exchange((attn_part, CORES, TURN), (small.astype(BF), "c", SWAP))
    attn_part = attn_part.astype(F32)
    other_small = other_small.astype(F32)
    qkv_part, out_part = attn_part[:, : 3 * half_width], attn_part[:, 3 * half_width :]
    shared_rows = 6 * width // 128
    small_rows = small.shape[0] - share
    shared = (small[:shared_rows] + other_small[:shared_rows]).reshape(6, width)
    half_sums = jnp.where(
        c == y, small[shared_rows:small_rows], other_small[shared_rows:small_rows]
    ).reshape(-1)
    proj_sum = pair_up(small[small_rows:], other_small[small_rows:], c, 0).reshape(width, -1)
    qkv_part = qkv_part.reshape(64, 2, 3, quarter).transpose(2, 0, 1, 3).reshape(3, 64, half_width)
    return (
        y_out,
        loss_out,
        grad_input,
        qkv_part,
        half_sums[: 2 * half_width].reshape(2, half_width),
        out_part.T,
        shared[4],
        shared[0:2],
        shared[2:4],
        up_part,
        half_sums[2 * half_width :],
        down_part.T,
        shared[5],
        proj_sum,
    )


IN_SPECS = (
    P("dp", None),
    P(),
    P("dp", "tensor"),
    P(None, "dp", "tensor"),
    P(None, "tensor"),
    P("tensor", "dp"),
    P(),
    P(),
    P(),
    P("dp", "tensor"),
    P("tensor"),
    P("tensor", "dp"),
    P(),
    P(),
    P(("dp", "tensor"), None),
)
OUT_SPECS = (
    P(("dp", "tensor"), None),
    P("dp", "tensor"),
    P(("dp", "tensor"), None),
    P(None, "dp", "tensor"),
    P(None, "tensor"),
    P("tensor", "dp"),
    P(),
    P(),
    P(),
    P("dp", "tensor"),
    P("tensor"),
    P("tensor", "dp"),
    P(),
    P(),
)


def solution(mesh):
    if mesh.devices.shape != (16, 2):
        return jax.shard_map(
            local, mesh=mesh, in_specs=IN_SPECS, out_specs=OUT_SPECS, check_vma=False
        )
    names = {"dp": ("z", "x", "c"), "tensor": ("y",)}

    def respec(spec):
        parts = []
        for entry in spec:
            axes = () if entry is None else entry if isinstance(entry, tuple) else (entry,)
            parts.append(tuple(name for axis in axes for name in names[axis]) or None)
        return P(*parts)

    chips = Mesh(mesh.devices.reshape(4, 2, 2, 2), ("z", "x", "c", "y"))
    return jax.shard_map(
        local_chip,
        mesh=chips,
        in_specs=tuple(respec(spec) for spec in IN_SPECS),
        out_specs=tuple(respec(spec) for spec in OUT_SPECS),
        check_vma=False,
    )
```

```python
from functools import partial

import jax
import jax.numpy as jnp
from jax import lax
from jax.experimental import pallas as pl
from jax.experimental.pallas import tpu as pltpu
from jax.sharding import Mesh, PartitionSpec as P

HEAD_DIM = 64
QLEN = 32
NQ_ROW = 8
NDOC = 8


EPS_NORM = 1e-05
EPS_EMBED = 1e-06
POOL_TEMP = 0.1
LOSS_TEMP = 0.1
FULL_PRECISION = lax.Precision.HIGHEST
MASKED_SCORE = -1e30


def shortened(shard):

    def short(part):
        return part.astype(jnp.bfloat16) if part.dtype == jnp.float32 else part

    return jax.tree.map(short, shard)


def contract_rows(left, right, precision=None):
    return lax.dot_general(
        left,
        right,
        (((0,), (0,)), ((), ())),
        precision=precision,
        preferred_element_type=jnp.float32,
    )


def contract_cols(left, right, precision=None):
    return lax.dot_general(
        left,
        right,
        (((1,), (1,)), ((), ())),
        precision=precision,
        preferred_element_type=jnp.float32,
    )


def norm_forward(value, gain, shift):
    centred = value - jnp.mean(value, axis=1, keepdims=True)
    rstd = lax.rsqrt(jnp.mean(centred * centred, axis=1, keepdims=True) + EPS_NORM)
    unit = centred * rstd
    return (unit * gain + shift, unit, rstd)


def norm_backward(grad, unit, rstd, gain):
    scaled = grad * gain
    return rstd * (
        scaled
        - jnp.mean(scaled, axis=1, keepdims=True)
        - unit * jnp.mean(scaled * unit, axis=1, keepdims=True)
    )


def segments_of(row_lengths, token_count):
    position = jnp.arange(token_count, dtype=jnp.int32)
    query_span = NQ_ROW * QLEN
    ends = jnp.cumsum(row_lengths)
    passed = jnp.sum((position[:, None] - query_span >= ends[None, :]).astype(jnp.int32), axis=1)
    return jnp.where(position < query_span, position // QLEN, NQ_ROW + passed)


def normalize_cut(raw, width):
    part = raw[:, :width]
    scale = lax.rsqrt(jnp.sum(part * part, axis=1, keepdims=True) + EPS_EMBED)
    return (part * scale, part, scale)


def normalize_back(grad, part, scale, full_width):
    result = scale * grad - part * (scale * scale * scale) * jnp.sum(
        part * grad, axis=1, keepdims=True
    )
    return jnp.pad(result, ((0, 0), (0, full_width - grad.shape[1])))


def masked_scores(query_block, key_rows, block_segments, segments):
    scores = jnp.einsum(
        "qhd,khd->hqk", query_block, key_rows, preferred_element_type=jnp.float32
    ) * HEAD_DIM ** (-0.5)
    return jnp.where((block_segments[:, None] == segments[None, :])[None], scores, MASKED_SCORE)


def attend_forward(query_rows, key_rows, value_rows, segments, block_rows):
    token_count = query_rows.shape[0]

    def one_block(block_start):
        query_block = lax.dynamic_slice_in_dim(query_rows, block_start, block_rows, 0)
        block_segments = lax.dynamic_slice_in_dim(segments, block_start, block_rows, 0)
        scores = masked_scores(query_block, key_rows, block_segments, segments)
        highest = jnp.max(scores, axis=2, keepdims=True)
        expo = jnp.exp(scores - highest)
        totals = jnp.sum(expo, axis=2, keepdims=True)
        weights = (expo / totals).astype(jnp.bfloat16)
        mixed = jnp.einsum("hqk,khd->qhd", weights, value_rows, preferred_element_type=jnp.float32)
        return (mixed.astype(jnp.bfloat16), (highest + jnp.log(totals))[:, :, 0])

    starts = jnp.arange(token_count // block_rows, dtype=jnp.int32) * block_rows
    mixed, log_totals = lax.map(one_block, starts)
    return (mixed.reshape(token_count, -1), log_totals)


def attend_backward(query_rows, key_rows, value_rows, segments, log_totals, grad_mixed, block_rows):
    token_count, local_heads, head_size = query_rows.shape
    scale = HEAD_DIM ** (-0.5)
    grad_heads = grad_mixed.reshape(token_count, local_heads, head_size)

    def one_block(carried, inputs):
        grad_keys, grad_values = carried
        block_start, block_lse = inputs
        query_block = lax.dynamic_slice_in_dim(query_rows, block_start, block_rows, 0)
        grad_block = lax.dynamic_slice_in_dim(grad_heads, block_start, block_rows, 0)
        block_segments = lax.dynamic_slice_in_dim(segments, block_start, block_rows, 0)
        scores = masked_scores(query_block, key_rows, block_segments, segments)
        probs = jnp.exp(scores - block_lse[:, :, None])
        grad_probs = jnp.einsum(
            "qhd,khd->hqk", grad_block, value_rows, preferred_element_type=jnp.float32
        )
        inner = jnp.sum(probs * grad_probs, axis=2, keepdims=True)
        grad_scores = (probs * (grad_probs - inner)).astype(jnp.bfloat16)
        grad_query = (
            jnp.einsum("hqk,khd->qhd", grad_scores, key_rows, preferred_element_type=jnp.float32)
            * scale
        )
        grad_keys = (
            grad_keys
            + jnp.einsum(
                "hqk,qhd->khd", grad_scores, query_block, preferred_element_type=jnp.float32
            )
            * scale
        )
        grad_values = grad_values + jnp.einsum(
            "hqk,qhd->khd",
            probs.astype(jnp.bfloat16),
            grad_block,
            preferred_element_type=jnp.float32,
        )
        return ((grad_keys, grad_values), grad_query)

    starts = jnp.arange(token_count // block_rows, dtype=jnp.int32) * block_rows
    zero_rows = jnp.zeros(key_rows.shape, jnp.float32)
    (grad_keys, grad_values), grad_queries = lax.scan(
        one_block, (zero_rows, zero_rows), (starts, log_totals)
    )
    flat_width = local_heads * head_size
    return (
        grad_queries.reshape(token_count, flat_width),
        grad_keys.reshape(token_count, flat_width),
        grad_values.reshape(token_count, flat_width),
    )


def local(
    tokens,
    lengths,
    pairing,
    w_qkv,
    b_qv,
    w_out,
    b_out,
    ln_gain,
    ln_bias,
    w_up,
    b_up,
    w_down,
    b_down,
    w_proj,
    cot,
):
    tensor_count = lax.axis_size("tensor")
    tensor_index = lax.axis_index("tensor")
    data_index = lax.axis_index("dp")
    token_count = tokens.shape[0]
    share_rows = token_count // tensor_count
    block_rows = min(512, token_count)
    own_start = tensor_index * share_rows
    full_qkv, full_out, full_up, full_down = (
        lax.all_gather(w_qkv, "dp", axis=1, tiled=True),
        lax.all_gather(w_out, "dp", axis=1, tiled=True),
        lax.all_gather(w_up, "dp", axis=0, tiled=True),
        lax.all_gather(w_down, "dp", axis=1, tiled=True),
    )
    head_width = full_qkv.shape[2]
    local_heads = head_width // HEAD_DIM
    row_lengths = lax.dynamic_index_in_dim(lengths, data_index, 0, keepdims=False)
    segments = segments_of(row_lengths, token_count)
    projected = jnp.einsum("td,kdw->ktw", tokens, full_qkv, preferred_element_type=jnp.float32)
    qv_bias = b_qv.astype(jnp.float32)
    query_rows = (
        (projected[0] + qv_bias[0]).astype(jnp.bfloat16).reshape(token_count, local_heads, HEAD_DIM)
    )
    key_rows = projected[1].astype(jnp.bfloat16).reshape(token_count, local_heads, HEAD_DIM)
    value_rows = (
        (projected[2] + qv_bias[1]).astype(jnp.bfloat16).reshape(token_count, local_heads, HEAD_DIM)
    )
    mixed, log_totals = attend_forward(query_rows, key_rows, value_rows, segments, block_rows)
    attn_terms = jnp.dot(mixed, full_out, preferred_element_type=jnp.float32)
    attn_sum = lax.psum_scatter(
        attn_terms.astype(jnp.bfloat16), "tensor", scatter_dimension=0, tiled=True
    ).astype(jnp.float32)
    own_tokens = lax.dynamic_slice_in_dim(tokens, own_start, share_rows, 0).astype(jnp.float32)
    gains = ln_gain.astype(jnp.float32)
    shifts = ln_bias.astype(jnp.float32)
    normed, unit_one, rstd_one = norm_forward(
        own_tokens + attn_sum + b_out.astype(jnp.float32), gains[0], shifts[0]
    )
    normed_all = lax.all_gather(normed.astype(jnp.bfloat16), "tensor", axis=0, tiled=True)
    up_value = jnp.dot(normed_all, full_up, preferred_element_type=jnp.float32) + b_up.astype(
        jnp.float32
    )
    activation = jax.nn.gelu(up_value, approximate=False).astype(jnp.bfloat16)
    ffn_terms = jnp.dot(activation, full_down, preferred_element_type=jnp.float32)
    ffn_sum = lax.psum_scatter(
        ffn_terms.astype(jnp.bfloat16), "tensor", scatter_dimension=0, tiled=True
    ).astype(jnp.float32)
    result, unit_two, rstd_two = norm_forward(
        normed + ffn_sum + b_down.astype(jnp.float32), gains[1], shifts[1]
    )
    result_low = result.astype(jnp.bfloat16)
    embed = jnp.dot(result_low, w_proj, preferred_element_type=jnp.float32).astype(jnp.bfloat16)
    embed_all = lax.all_gather(embed, ("dp", "tensor"), axis=0, tiled=True)
    row_count = lengths.shape[0]
    proj_width = w_proj.shape[1]
    widths = (proj_width, 3 * proj_width // 4, proj_width // 2)
    per_device = pairing.shape[1]
    query_count = per_device * QLEN
    query_span = NQ_ROW * QLEN
    emb_rows = embed_all.reshape(row_count, token_count, proj_width)
    my_row = lax.dynamic_index_in_dim(emb_rows, data_index, 0, keepdims=False)
    query_raw = lax.dynamic_slice_in_dim(my_row, tensor_index * query_count, query_count, 0).astype(
        jnp.float32
    )
    query_levels = [normalize_cut(query_raw, width) for width in widths]
    query_units = [level_parts[0].astype(jnp.bfloat16) for level_parts in query_levels]
    doc_numbers = jnp.arange(NDOC, dtype=jnp.int32)

    def row_pool(carried, inputs):
        row_emb, lengths_row = inputs
        row_hot = (
            segments_of(lengths_row, token_count)[:, None] == NQ_ROW + doc_numbers[None, :]
        ).astype(jnp.float32)
        row_raw = row_emb.astype(jnp.float32)
        pooled_list = []
        sums_list = []
        for width, query_unit in zip(widths, query_units):
            doc_unit = normalize_cut(row_raw, width)[0].astype(jnp.bfloat16)
            expo = jnp.exp(contract_cols(query_unit, doc_unit) / POOL_TEMP)
            sums = jnp.dot(expo, row_hot, precision=FULL_PRECISION)
            pooled = POOL_TEMP * jnp.log(sums / lengths_row.astype(jnp.float32))
            pooled_list.append(jnp.sum(pooled.reshape(per_device, QLEN, NDOC), axis=1))
            sums_list.append(sums)
        return (carried, (jnp.stack(pooled_list), jnp.stack(sums_list)))

    _, (row_scores, row_sums) = lax.scan(row_pool, 0, (emb_rows, lengths))
    logits = (
        jnp.transpose(row_scores, (2, 1, 0, 3)).reshape(per_device, 3, row_count * NDOC) / LOSS_TEMP
    )
    own_pairs = pairing[0]
    target = jnp.take_along_axis(
        logits, jnp.broadcast_to(own_pairs[:, None, None], (per_device, 3, 1)), axis=2
    )[:, :, 0]
    loss_out = jnp.sum(jax.nn.logsumexp(logits, axis=2) - target, axis=1).reshape(1, per_device)
    picked = (
        jnp.arange(row_count * NDOC, dtype=jnp.int32)[None, None, :] == own_pairs[:, None, None]
    ).astype(jnp.float32)
    grad_logits = (jax.nn.softmax(logits, axis=2) - picked) / LOSS_TEMP
    grad_rows = jnp.transpose(grad_logits.reshape(per_device, 3, row_count, NDOC), (2, 1, 0, 3))
    coefficient = jnp.repeat(grad_rows, QLEN, axis=2) / row_sums

    def row_back(carried, inputs):
        row_emb, lengths_row, row_coef = inputs
        row_hot = (
            segments_of(lengths_row, token_count)[:, None] == NQ_ROW + doc_numbers[None, :]
        ).astype(jnp.float32)
        row_raw = row_emb.astype(jnp.float32)
        new_carried = []
        row_grad = jnp.zeros((token_count, proj_width), jnp.float32)
        for level_index in range(3):
            width = widths[level_index]
            doc_unit_f, doc_part, doc_scale = normalize_cut(row_raw, width)
            doc_unit = doc_unit_f.astype(jnp.bfloat16)
            expo = jnp.exp(contract_cols(query_units[level_index], doc_unit) / POOL_TEMP)
            spread = contract_cols(row_coef[level_index], row_hot, FULL_PRECISION)
            grad_sim = (expo * spread).astype(jnp.bfloat16)
            new_carried.append(
                carried[level_index]
                + jnp.dot(grad_sim, doc_unit, preferred_element_type=jnp.float32)
            )
        return (tuple(new_carried), row_grad)

    zero_query = tuple((jnp.zeros((query_count, width), jnp.float32) for width in widths))
    query_grads, doc_grads = lax.scan(row_back, zero_query, (emb_rows, lengths, coefficient))
    grad_query = jnp.zeros((query_count, proj_width), jnp.float32)
    for level_index in range(3):
        level_parts = query_levels[level_index]
        grad_query = grad_query + normalize_back(
            query_grads[level_index], level_parts[1], level_parts[2], proj_width
        )
    coef_mine = jnp.transpose(coefficient, (2, 1, 0, 3)).reshape(query_count, 3, row_count * NDOC)
    coef_all, grad_query_all = (
        lax.all_gather(shortened(coef_mine), ("dp", "tensor"), axis=0, tiled=True).astype(
            coef_mine.dtype
        ),
        lax.all_gather(
            grad_query.astype(jnp.bfloat16), ("dp", "tensor"), axis=0, tiled=True
        ).astype(grad_query.dtype),
    )
    own_raw = embed.astype(jnp.float32)
    own_segments = lax.dynamic_slice_in_dim(segments, own_start, share_rows, 0)
    own_docs = jnp.where(own_segments >= NQ_ROW, data_index * NDOC + own_segments - NQ_ROW, -1)
    own_hot = (own_docs[:, None] == jnp.arange(row_count * NDOC, dtype=jnp.int32)[None, :]).astype(
        jnp.float32
    )
    queries_all = (
        emb_rows[:, :query_span].reshape(row_count * query_span, proj_width).astype(jnp.float32)
    )
    grad_embed = jnp.zeros((share_rows, proj_width), jnp.float32)
    for level_index in range(3):
        width = widths[level_index]
        query_unit_all = normalize_cut(queries_all, width)[0].astype(jnp.bfloat16)
        doc_unit_f, doc_part, doc_scale = normalize_cut(own_raw, width)
        expo = jnp.exp(contract_cols(query_unit_all, doc_unit_f.astype(jnp.bfloat16)) / POOL_TEMP)
        spread = contract_cols(coef_all[:, level_index], own_hot, FULL_PRECISION)
        grad_sim = (expo * spread).astype(jnp.bfloat16)
        grad_doc = contract_rows(grad_sim, query_unit_all)
        grad_embed = grad_embed + normalize_back(grad_doc, doc_part, doc_scale, proj_width)
    row_query_grads = lax.dynamic_slice_in_dim(
        grad_query_all, data_index * query_span, query_span, 0
    )
    padded = jnp.pad(row_query_grads, ((0, token_count - query_span), (0, 0)))
    grad_embed = grad_embed + lax.dynamic_slice_in_dim(padded, own_start, share_rows, 0)
    proj_float = w_proj.astype(jnp.float32)
    grad_result = cot.astype(jnp.float32) + contract_cols(grad_embed, proj_float, FULL_PRECISION)
    proj_grad = contract_rows(result_low.astype(jnp.float32), grad_embed, FULL_PRECISION)
    gain_two = jnp.sum(grad_result * unit_two, axis=0)
    shift_two = jnp.sum(grad_result, axis=0)
    grad_second = norm_backward(grad_result, unit_two, rstd_two, gains[1])
    grad_ffn = grad_second.astype(jnp.bfloat16)
    down_bias = jnp.sum(grad_ffn.astype(jnp.float32), axis=0)
    grad_ffn_all = lax.all_gather(grad_ffn, "tensor", axis=0, tiled=True)
    grad_act = contract_cols(grad_ffn_all, full_down)
    down_grad = contract_rows(activation, grad_ffn_all)
    _, gelu_pull = jax.vjp(partial(jax.nn.gelu, approximate=False), up_value)
    grad_up = gelu_pull(grad_act)[0].astype(jnp.bfloat16)
    up_bias = jnp.sum(grad_up.astype(jnp.float32), axis=0)
    up_grad = contract_rows(normed_all, grad_up)
    normed_terms = contract_cols(grad_up, full_up)
    grad_normed = (
        lax.psum_scatter(
            normed_terms.astype(jnp.bfloat16), "tensor", scatter_dimension=0, tiled=True
        ).astype(jnp.float32)
        + grad_second
    )
    gain_one = jnp.sum(grad_normed * unit_one, axis=0)
    shift_one = jnp.sum(grad_normed, axis=0)
    grad_first = norm_backward(grad_normed, unit_one, rstd_one, gains[0])
    grad_attn = grad_first.astype(jnp.bfloat16)
    out_bias = jnp.sum(grad_attn.astype(jnp.float32), axis=0)
    grad_attn_all = lax.all_gather(grad_attn, "tensor", axis=0, tiled=True)
    out_grad = contract_rows(mixed, grad_attn_all)
    grad_mixed = contract_cols(grad_attn_all, full_out).astype(jnp.bfloat16)
    grad_q, grad_k, grad_v = attend_backward(
        query_rows, key_rows, value_rows, segments, log_totals, grad_mixed, block_rows
    )
    stacked_grads = jnp.stack(
        [grad_q.astype(jnp.bfloat16), grad_k.astype(jnp.bfloat16), grad_v.astype(jnp.bfloat16)]
    )
    qkv_grad = jnp.einsum("td,ktw->kdw", tokens, stacked_grads, preferred_element_type=jnp.float32)
    input_terms = jnp.einsum(
        "ktw,kdw->td", stacked_grads, full_qkv, preferred_element_type=jnp.float32
    )
    grad_input = (
        lax.psum_scatter(
            input_terms.astype(jnp.bfloat16), "tensor", scatter_dimension=0, tiled=True
        ).astype(jnp.float32)
        + grad_first
    )
    qv_grad = jnp.stack(
        [
            jnp.sum(stacked_grads[0].astype(jnp.float32), axis=0),
            jnp.sum(stacked_grads[2].astype(jnp.float32), axis=0),
        ]
    )
    qkv_part, out_part, up_part, down_part = (
        lax.psum_scatter(
            qkv_grad.astype(jnp.bfloat16), "dp", scatter_dimension=1, tiled=True
        ).astype(jnp.float32),
        lax.psum_scatter(
            out_grad.astype(jnp.bfloat16), "dp", scatter_dimension=1, tiled=True
        ).astype(jnp.float32),
        lax.psum_scatter(
            up_grad.astype(jnp.bfloat16), "dp", scatter_dimension=0, tiled=True
        ).astype(jnp.float32),
        lax.psum_scatter(
            down_grad.astype(jnp.bfloat16), "dp", scatter_dimension=1, tiled=True
        ).astype(jnp.float32),
    )
    gain_sum, shift_sum, out_bias_sum, down_bias_sum, proj_sum = lax.psum(
        (
            jnp.stack([gain_one, gain_two]),
            jnp.stack([shift_one, shift_two]),
            out_bias,
            down_bias,
            proj_grad,
        ),
        ("dp", "tensor"),
    )
    qv_sum, up_bias_sum = lax.psum((qv_grad, up_bias), "dp")
    return (
        result_low,
        loss_out,
        grad_input.astype(jnp.bfloat16),
        qkv_part,
        qv_sum,
        out_part,
        out_bias_sum,
        gain_sum,
        shift_sum,
        up_part,
        up_bias_sum,
        down_part,
        down_bias_sum,
        proj_sum,
    )


SWAP = [(0, 1), (1, 0)]
TURN = [(0, 0), (1, 2), (2, 1), (3, 3)]
FAR = [(0, 3), (3, 0), (1, 2), (2, 1)]
NEAR = [(0, 1), (1, 0), (2, 3), (3, 2)]
BF = jnp.bfloat16
F32 = jnp.float32


def dot(left, right):
    return jnp.dot(left, right, preferred_element_type=F32)


CORES = ("c", "y")


def tie(value, *others):
    return lax.optimization_barrier((value,) + others)[0]


def tie_all(values, *others):
    return lax.optimization_barrier(tuple(values) + others)[: len(values)]


def exchange(*moves):
    return lax.optimization_barrier(
        tuple(lax.ppermute(value, axis, steps) for value, axis, steps in moves)
    )


def swap(value, axis):
    return lax.ppermute(value, axis, SWAP)


def pair_up(first, second, own_index, axis):
    return jnp.where(
        own_index == 0, jnp.stack([first, second], axis), jnp.stack([second, first], axis)
    )


def far_pair(value, far, z):
    return jnp.where(z < 2, jnp.stack([value, far]), jnp.stack([far, value]))


def whole_line(pair, other, z):
    return jnp.where(
        (z == 0) | (z == 3),
        jnp.stack([pair[0], other[0], other[1], pair[1]]),
        jnp.stack([other[0], pair[0], pair[1], other[1]]),
    )


def first_moves(line):
    half = line.shape[1] // 2
    return ((line[:, :half], "x", SWAP), (line[:, half:], "y", SWAP))


def first_parts(line, moved, x, y):
    half = line.shape[1] // 2
    return (pair_up(line[:, :half], moved[0], x, 1), pair_up(line[:, half:], moved[1], y, 1))


def last_moves(parts):
    return ((parts[0], "y", SWAP), (parts[1], "x", SWAP))


def full_rows(parts, moved, x, y):
    low = pair_up(parts[0], moved[0], y, 2)
    high = pair_up(parts[1], moved[1], x, 1)
    return jnp.concatenate([low, high], axis=3).reshape(-1, low.shape[-1])


def at(blocks, index, axis):
    return lax.dynamic_index_in_dim(blocks, index, axis, keepdims=False)


def side_move(blocks, axis_name, own_index, axis):
    return (at(blocks, 1 - own_index, axis).astype(BF), axis_name, SWAP)


def side_sum(blocks, got, own_index, axis):
    return at(blocks, own_index, axis).astype(F32) + got.astype(F32)


def near_move(line, z):
    ends = (z == 0) | (z == 3)
    outer, inner = jnp.stack([line[0], line[3]]), line[1:3]
    return (jnp.where(ends, inner, outer).astype(BF), "z", NEAR)


def near_sum(line, got, z):
    ends = (z == 0) | (z == 3)
    return jnp.where(ends, jnp.stack([line[0], line[3]]), line[1:3]) + got.astype(F32)


def far_move(pair, z):
    return (jnp.where(z < 2, pair[1], pair[0]).astype(BF), "z", FAR)


def far_sum(pair, got, z):
    return jnp.where(z < 2, pair[0], pair[1]) + got.astype(F32)


def blocks_of(left, right):
    return contract_rows(left, right).astype(BF).reshape(4, 2, 2, 64, right.shape[1])


def sum_moves(blocks, x, y):
    half = blocks.shape[3] // 2
    return (
        side_move(blocks[..., :half, :], "x", x, 1),
        side_move(blocks[..., half:, :], "y", y, 2),
    )


def sum_parts(blocks, moved, x, y):
    half = blocks.shape[3] // 2
    return (
        side_sum(blocks[..., :half, :], moved[0], x, 1),
        side_sum(blocks[..., half:, :], moved[1], y, 2),
    )


def line_moves(parts, x, y):
    return (side_move(parts[0], "y", y, 1), side_move(parts[1], "x", x, 1))


def line_of(parts, moved, x, y):
    return jnp.concatenate(
        [side_sum(parts[0], moved[0], y, 1), side_sum(parts[1], moved[1], x, 1)], axis=1
    )


def tile_bounds(row_lengths, token_count):
    ends = jnp.cumsum(row_lengths)
    span = NQ_ROW * QLEN
    first = jnp.arange(token_count // TILE, dtype=jnp.int32) * TILE - span
    last = first + TILE - 1
    begin = jnp.max(jnp.where(ends[None, :] <= first[:, None], ends[None, :], 0), axis=1)
    end = jnp.min(jnp.where(ends[None, :] > last[:, None], ends[None, :], token_count), axis=1)
    low = jnp.where(first < 0, 0, (begin + span) // TILE)
    high = jnp.where(first < 0, 1, (end + span + TILE - 1) // TILE)
    return jnp.stack([low, high]).astype(jnp.int32)


def token_spans(row_lengths, token_count):
    ends = jnp.cumsum(row_lengths)[:, None]
    span = NQ_ROW * QLEN
    place = jnp.arange(token_count, dtype=jnp.int32)[None, :]
    doc = place - span
    begin = jnp.max(jnp.where(ends <= doc, ends, 0), axis=0) + span
    end = jnp.min(jnp.where(ends > doc, ends, token_count), axis=0) + span
    query = place[0] // QLEN * QLEN
    return jnp.stack(
        [jnp.where(doc[0] < 0, query, begin), jnp.where(doc[0] < 0, query + QLEN, end)]
    ).astype(jnp.int32)


def rows_of(value, start, count):
    return lax.dynamic_slice_in_dim(value, start, count, 0)


TILE = 256
KEYS = 256
NEG = -1e30


def exact(left, right, dims):
    return lax.dot_general(left, right, (dims, ((), ())), preferred_element_type=F32)


def head_masks(value):
    lane = lax.broadcasted_iota(jnp.int32, value.shape, 1)
    zero = jnp.zeros_like(value)
    return (jnp.where(lane < HEAD_DIM, value, zero), jnp.where(lane < HEAD_DIM, zero, value))


def key_shift(step, spans):
    place = step * KEYS + lax.broadcasted_iota(jnp.int32, (KEYS, TILE), 0)
    inside = (place >= spans[0:1, :]) & (place < spans[1:2, :])
    return jnp.where(inside, 0.0, NEG)


def attend_kernel(bounds, own_ref, qkv_ref, spans, out_ref, lse_ref, held):
    block = pl.program_id(0)
    groups = 2
    pairs = out_ref.shape[1] // 128
    per_group = pairs // groups

    def column(pair, part):
        start = ((pair // per_group) * 3 + part) * per_group + pair % per_group
        return slice(start * 128, (start + 1) * 128)

    queries = [head_masks(own_ref[:, column(pair, 0)] * HEAD_DIM**-0.5) for pair in range(pairs)]
    heads = [(pair, head) for pair in range(pairs) for head in range(2)]

    def score(step, highest):
        rows = pl.ds(pl.multiple_of(step * KEYS, KEYS), KEYS)
        shift = key_shift(step, spans)
        fresh = []
        for index, (pair, head) in enumerate(heads):
            keys = qkv_ref[rows, column(pair, 1)]
            scores = exact(keys, queries[pair][head], ((1,), (1,))) + shift
            held[index, rows, :] = scores
            fresh.append(jnp.maximum(highest[index], jnp.max(scores, axis=0, keepdims=True)))
        return tuple(fresh)

    low = jnp.full((1, TILE), NEG, F32)
    highest = lax.fori_loop(bounds[0, block], bounds[1, block], score, (low,) * len(heads))

    def mix(step, carried):
        rows = pl.ds(pl.multiple_of(step * KEYS, KEYS), KEYS)
        fresh = []
        for index, (pair, head) in enumerate(heads):
            values = qkv_ref[rows, column(pair, 2)]
            total, mixed = carried[index]
            expo = jnp.exp(held[index, rows, :] - highest[index])
            product = exact(values, expo.astype(BF), ((0,), (0,)))
            fresh.append(
                (
                    total + jnp.sum(expo, axis=0, keepdims=True),
                    mixed + product[head * HEAD_DIM : (head + 1) * HEAD_DIM],
                )
            )
        return tuple(fresh)

    start = (jnp.zeros((1, TILE), F32), jnp.zeros((HEAD_DIM, TILE), F32))
    parts = lax.fori_loop(bounds[0, block], bounds[1, block], mix, (start,) * len(heads))
    for pair in range(pairs):
        both = [parts[2 * pair + head][1] / parts[2 * pair + head][0] for head in range(2)]
        mixed = jnp.transpose(jnp.concatenate(both, axis=0))
        out_ref[:, pair * 128 : (pair + 1) * 128] = mixed.astype(BF)
    for index in range(len(heads)):
        lse_ref[index : index + 1, :] = highest[index] + jnp.log(parts[index][0])


def attend(bounds, qkv, spans):
    count, wide = qkv.shape
    heads = wide // 3 // HEAD_DIM
    whole = lambda shape: pl.BlockSpec(shape, lambda i: (0, 0))
    return pl.pallas_call(
        attend_kernel,
        grid=(count // TILE,),
        in_specs=[
            pl.BlockSpec(memory_space=pltpu.SMEM),
            pl.BlockSpec((TILE, wide), lambda i: (i, 0)),
            whole((count, wide)),
            pl.BlockSpec((2, TILE), lambda i: (0, i)),
        ],
        out_specs=[
            pl.BlockSpec((TILE, wide // 3), lambda i: (i, 0)),
            pl.BlockSpec((heads, TILE), lambda i: (0, i)),
        ],
        out_shape=[
            jax.ShapeDtypeStruct((count, wide // 3), BF),
            jax.ShapeDtypeStruct((heads, count), F32),
        ],
        scratch_shapes=[pltpu.VMEM((heads, count, TILE), F32)],
        compiler_params=pltpu.CompilerParams(vmem_limit_bytes=40 << 20),
        cost_estimate=pl.CostEstimate(
            flops=4 * heads * count * count * 64,
            transcendentals=heads * count * count // 2,
            bytes_accessed=4 * count * wide * 2,
        ),
    )(bounds, qkv, qkv, spans)


def attend_back_kernel(
    first, bounds, own_ref, qkv_ref, out_ref, grad_ref, lse_ref, spans,
    grads_ref, sums_ref, key_sum, value_sum,
):
    block = pl.program_id(0)
    pairs = out_ref.shape[1] // 128
    heads = [(pair, head) for pair in range(pairs) for head in range(2)]
    cut = lambda index: slice(index * 128, (index + 1) * 128)

    @pl.when(block == 0)
    def _():
        key_sum[...] = jnp.zeros_like(key_sum)
        value_sum[...] = jnp.zeros_like(value_sum)
        sums_ref[...] = jnp.zeros_like(sums_ref)

    queries = [head_masks(own_ref[:, cut(pair)] * HEAD_DIM**-0.5) for pair in range(pairs)]
    grads = [head_masks(grad_ref[:, cut(pair)]) for pair in range(pairs)]
    picks = head_masks(jnp.ones((8, 128), BF))
    inner = []
    for pair, head in heads:
        product = grad_ref[:, cut(pair)].astype(F32) * out_ref[:, cut(pair)].astype(F32)
        high = product.astype(BF)
        rest = (product - high.astype(F32)).astype(BF)
        inner.append(
            (
                exact(picks[head], high, ((1,), (1,))) + exact(picks[head], rest, ((1,), (1,)))
            )[0:1]
        )
    lse = [lse_ref[first + index : first + index + 1, :] for index in range(len(heads))]

    def step_of(step, carried):
        rows = pl.ds(pl.multiple_of(step * KEYS, KEYS), KEYS)
        shift = key_shift(step, spans)
        fresh = []
        for pair in range(pairs):
            keys = qkv_ref[rows, cut(pairs + pair)]
            values = qkv_ref[rows, cut(2 * pairs + pair)]
            key_add = jnp.zeros((KEYS, 128), F32)
            value_add = jnp.zeros((KEYS, 128), F32)
            for head in range(2):
                index = 2 * pair + head
                scores = exact(keys, queries[pair][head], ((1,), (1,))) + shift
                probs = jnp.exp(scores - lse[index])
                grad_probs = exact(values, grads[pair][head], ((1,), (1,)))
                grad_scores = (probs * (grad_probs - inner[index])).astype(BF)
                value_add = value_add + exact(probs.astype(BF), grads[pair][head], ((1,), (0,)))
                key_add = key_add + exact(grad_scores, queries[pair][head], ((1,), (0,)))
                product = exact(keys, grad_scores, ((0,), (0,)))
                fresh.append(carried[index] + product[head * HEAD_DIM : (head + 1) * HEAD_DIM])
            key_sum[rows, cut(pair)] += key_add
            value_sum[rows, cut(pair)] += value_add
        return tuple(fresh)

    start = jnp.zeros((HEAD_DIM, TILE), F32)
    parts = lax.fori_loop(bounds[0, block], bounds[1, block], step_of, (start,) * len(heads))
    own = pl.ds(pl.multiple_of(block * TILE, TILE), TILE)
    for pair in range(pairs):
        grad_query = jnp.concatenate([parts[2 * pair], parts[2 * pair + 1]], axis=0)
        grad_query = jnp.transpose(grad_query * HEAD_DIM**-0.5).astype(BF)
        grads_ref[own, cut(pair)] = grad_query
        sums_ref[0:1, cut(pair)] += jnp.sum(grad_query.astype(F32), axis=0, keepdims=True)

    @pl.when(block == pl.num_programs(0) - 1)
    def _():
        wide = pairs * 128
        grad_value = value_sum[...].astype(BF)
        grads_ref[:, wide : 2 * wide] = key_sum[...].astype(BF)
        grads_ref[:, 2 * wide :] = grad_value
        sums_ref[1:2, :] = jnp.sum(grad_value.astype(F32), axis=0, keepdims=True)


def attend_back(bounds, group, qkv, mixed, grad_mixed, lse, spans):
    count = qkv.shape[0]
    wide = qkv.shape[1] // 2
    heads = wide // 3 // HEAD_DIM
    whole = lambda shape: pl.BlockSpec(shape, lambda i: (0, 0))
    return pl.pallas_call(
        partial(attend_back_kernel, group * heads),
        grid=(count // TILE,),
        in_specs=[
            pl.BlockSpec(memory_space=pltpu.SMEM),
            pl.BlockSpec((TILE, wide), lambda i: (i, group)),
            pl.BlockSpec((count, wide), lambda i: (0, group)),
            pl.BlockSpec((TILE, wide // 3), lambda i: (i, group)),
            pl.BlockSpec((TILE, wide // 3), lambda i: (i, group)),
            pl.BlockSpec((2 * heads, TILE), lambda i: (0, i)),
            pl.BlockSpec((2, TILE), lambda i: (0, i)),
        ],
        out_specs=[whole((count, wide)), whole((8, wide // 3))],
        out_shape=[
            jax.ShapeDtypeStruct((count, wide), BF),
            jax.ShapeDtypeStruct((8, wide // 3), F32),
        ],
        scratch_shapes=[
            pltpu.VMEM((count, wide // 3), F32),
            pltpu.VMEM((count, wide // 3), F32),
        ],
        compiler_params=pltpu.CompilerParams(vmem_limit_bytes=40 << 20),
        cost_estimate=pl.CostEstimate(
            flops=10 * heads * count * count * 64,
            transcendentals=heads * count * count // 2,
            bytes_accessed=8 * count * wide * 2,
        ),
    )(
        bounds, qkv, qkv, mixed, grad_mixed,
        lse, spans,
    )


ERFC = (
    -1.26551223, 1.00002368, 0.37409196, 0.09678418, -0.18628806,
    0.27886807, -1.13520398, 1.48851587, -0.82215223, 0.17087277,
)


def gelu_pair(value):
    size = jnp.abs(value) * 0.5**0.5
    ratio = 1.0 / (1.0 + 0.5 * size)
    series = jnp.full_like(value, ERFC[-1])
    for factor in ERFC[-2::-1]:
        series = series * ratio + factor
    bell = jnp.exp(-size * size)
    tail = 0.5 * ratio * bell * jnp.exp(series)
    phi = jnp.where(value < 0.0, tail, 1.0 - tail)
    return (value * phi, phi + value * bell * 0.3989422804014327)


def expand_kernel(x_ref, w_ref, b_ref, *refs):
    act_ref, slope_ref = refs[-2:]
    rows = 256
    for start in range(0, x_ref.shape[0], rows):
        part = slice(start, start + rows)
        value = exact(x_ref[part, :], w_ref[...], ((1,), (0,))) + b_ref[...]
        active, slope = gelu_pair(value)
        act_ref[part, :] = active.astype(BF)
        slope_ref[part, :] = slope.astype(BF)


def expand(value, weight, shift, first, tiles, filled=()):
    count, depth = value.shape
    width = shift.shape[1]
    tile = 256
    column = lambda rows: pl.BlockSpec((rows, tile), lambda i: (0, first + i))
    return pl.pallas_call(
        expand_kernel,
        grid=(tiles,),
        in_specs=[
            pl.BlockSpec((count, depth), lambda i: (0, 0)),
            column(depth),
            column(1),
        ]
        + [pl.BlockSpec(memory_space=pl.ANY)] * len(filled),
        out_specs=[column(count)] * 2,
        out_shape=[jax.ShapeDtypeStruct((count, width), BF)] * 2,
        input_output_aliases={3: 0, 4: 1} if filled else {},
        compiler_params=pltpu.CompilerParams(vmem_limit_bytes=32 << 20),
        cost_estimate=pl.CostEstimate(
            flops=2 * count * depth * tile * tiles,
            transcendentals=3 * count * tile * tiles,
            bytes_accessed=2 * (count * depth + depth * tile * tiles + 2 * count * tile * tiles),
        ),
    )(value, weight, shift, *filled)


def cut_levels(raw, cuts):
    lane = lax.broadcasted_iota(jnp.int32, raw.shape, 1)
    levels = []
    for cut in cuts:
        part = jnp.where(lane < cut, raw, 0.0)
        scale = lax.rsqrt(jnp.sum(part * part, axis=1, keepdims=True) + EPS_EMBED)
        levels.append(((part * scale).astype(BF), part, scale))
    return levels


def pool_kernel(cuts, span, q_ref, d_ref, seg_ref, out_ref, units, hot):
    @pl.when(pl.program_id(0) == 0)
    def _():
        raw = d_ref[span:, :].astype(F32)
        for level, parts in enumerate(cut_levels(raw, cuts)):
            units[level] = parts[0]
        doc = lax.broadcasted_iota(jnp.int32, hot.shape, 0)
        hot[...] = (seg_ref[:, span:] == NQ_ROW + doc).astype(F32).astype(BF)

    levels = cut_levels(q_ref[...].astype(F32), cuts)
    for level in range(len(cuts)):
        similar = exact(units[level], levels[level][0], ((1,), (1,)))
        expo = jnp.exp(similar * (1.0 / POOL_TEMP))
        high = expo.astype(BF)
        rest = (expo - high.astype(F32)).astype(BF)
        out_ref[level * NDOC : (level + 1) * NDOC, :] = exact(
            hot[...], high, ((1,), (0,))
        ) + exact(hot[...], rest, ((1,), (0,)))


def pool(cuts, span, queries, row_embed, seg_row):
    count, width = queries.shape
    tokens = row_embed.shape[0]
    whole = lambda shape: pl.BlockSpec(shape, lambda i: (0, 0))
    return pl.pallas_call(
        partial(pool_kernel, cuts, span),
        grid=(count // TILE,),
        in_specs=[
            pl.BlockSpec((TILE, width), lambda i: (i, 0)),
            whole((tokens, width)),
            whole((1, tokens)),
        ],
        out_specs=pl.BlockSpec((len(cuts) * NDOC, TILE), lambda i: (0, i)),
        out_shape=jax.ShapeDtypeStruct((len(cuts) * NDOC, count), F32),
        scratch_shapes=[
            pltpu.VMEM((len(cuts), tokens - span, width), BF),
            pltpu.VMEM((NDOC, tokens - span), BF),
        ],
        compiler_params=pltpu.CompilerParams(vmem_limit_bytes=32 << 20),
        cost_estimate=pl.CostEstimate(
            flops=2 * len(cuts) * count * tokens * 256,
            transcendentals=len(cuts) * count * tokens,
            bytes_accessed=2 * (count + tokens) * width,
        ),
    )(queries, row_embed, seg_row)


def level_back(grad, part, scale):
    return scale * grad - part * (scale * scale * scale) * jnp.sum(
        part * grad, axis=1, keepdims=True
    )


def pool_back_kernel(
    cuts, span, q_ref, d_ref, seg_ref, coef_ref, q_out, d_out, units, units_t, hot, sums
):
    step = pl.program_id(0)

    @pl.when(step == 0)
    def _():
        raw = d_ref[span:, :].astype(F32)
        for level, parts in enumerate(cut_levels(raw, cuts)):
            units[level] = parts[0]
            units_t[level] = jnp.transpose(parts[0])
        doc = lax.broadcasted_iota(jnp.int32, hot.shape, 0)
        wanted = NQ_ROW + jnp.where(doc < NDOC, doc, doc - NDOC)
        hot[...] = (seg_ref[:, span:] == wanted).astype(F32).astype(BF)
        sums[...] = jnp.zeros_like(sums)

    levels = cut_levels(q_ref[...].astype(F32), cuts)
    total = jnp.zeros(q_ref.shape, F32)
    for level in range(len(cuts)):
        unit, part, scale = levels[level]
        similar = exact(units[level], unit, ((1,), (1,)))
        coef = coef_ref[level * NDOC : (level + 1) * NDOC, :]
        high = coef.astype(BF).astype(F32)
        both = jnp.concatenate([high, coef - high], axis=0).astype(BF)
        spread = exact(hot[...], both, ((0,), (0,)))
        grad = (jnp.exp(similar * (1.0 / POOL_TEMP)) * spread).astype(BF)
        sums[level] += exact(grad, unit, ((1,), (0,)))
        grad_unit = jnp.transpose(exact(units_t[level], grad, ((1,), (0,))))
        total = total + level_back(grad_unit, part, scale)
    q_out[...] = total.astype(BF)

    @pl.when(step == pl.num_programs(0) - 1)
    def _():
        raw = d_ref[span:, :].astype(F32)
        result = jnp.zeros(raw.shape, F32)
        for level, parts in enumerate(cut_levels(raw, cuts)):
            lane = lax.broadcasted_iota(jnp.int32, raw.shape, 1)
            grad = jnp.where(lane < cuts[level], sums[level], 0.0)
            result = result + level_back(grad, parts[1], parts[2])
        d_out[...] = result


def pool_back(cuts, span, queries, row_embed, seg_row, coef):
    count, width = queries.shape
    tokens = row_embed.shape[0]
    docs = tokens - span
    whole = lambda shape: pl.BlockSpec(shape, lambda i: (0, 0))
    return pl.pallas_call(
        partial(pool_back_kernel, cuts, span),
        grid=(count // TILE,),
        in_specs=[
            pl.BlockSpec((TILE, width), lambda i: (i, 0)),
            whole((tokens, width)),
            whole((1, tokens)),
            pl.BlockSpec((len(cuts) * NDOC, TILE), lambda i: (0, i)),
        ],
        out_specs=[pl.BlockSpec((TILE, width), lambda i: (i, 0)), whole((docs, width))],
        out_shape=[
            jax.ShapeDtypeStruct((count, width), BF),
            jax.ShapeDtypeStruct((docs, width), F32),
        ],
        scratch_shapes=[
            pltpu.VMEM((len(cuts), docs, width), BF),
            pltpu.VMEM((len(cuts), width, docs), BF),
            pltpu.VMEM((2 * NDOC, docs), BF),
            pltpu.VMEM((len(cuts), docs, width), F32),
        ],
        compiler_params=pltpu.CompilerParams(vmem_limit_bytes=32 << 20),
        cost_estimate=pl.CostEstimate(
            flops=2 * len(cuts) * count * docs * 512,
            transcendentals=len(cuts) * count * docs,
            bytes_accessed=4 * (count + tokens) * width,
        ),
    )(queries, row_embed, seg_row, coef)


def local_chip(
    tokens,
    lengths,
    pairing,
    w_qkv,
    b_qv,
    w_out,
    b_out,
    ln_gain,
    ln_bias,
    w_up,
    b_up,
    w_down,
    b_down,
    w_proj,
    cot,
):
    z, x, c, y = (lax.axis_index(name) for name in ("z", "x", "c", "y"))
    chip = 4 * z + 2 * x + y
    token_count, width = tokens.shape
    share = token_count // 2
    own_start, other_start = c * share, (1 - c) * share
    gains, shifts = ln_gain.astype(F32), ln_bias.astype(F32)

    half_width = w_qkv.shape[2]
    up_wide = w_up.shape[1]
    chip_count = lengths.shape[0]
    half_queries = NQ_ROW // 2
    query_total = chip_count * half_queries
    quarter = half_width // 2
    qkv_rows = jnp.concatenate(
        [w_qkv[k][:, g * quarter : (g + 1) * quarter] for g in range(2) for k in range(3)], axis=1
    )
    pair_rows = jnp.pad(pairing.astype(BF), ((0, 63), (0, 128 - half_queries)))
    mid_rows = jnp.concatenate([w_up, w_out.T, pair_rows], axis=1)
    bias = jnp.concatenate([b_qv.reshape(-1), b_up])[None].astype(F32)
    got = exchange(
        (qkv_rows, CORES, TURN), (tokens, "c", SWAP), (bias, "y", SWAP)
    )
    qkv_rows = got[0]
    row = jnp.where(c == y, tokens, got[1])
    bias = jnp.where(c == y, bias, got[2])
    (rest_rows,) = exchange(
        (tie(jnp.concatenate([mid_rows, w_down.T], axis=1), row), CORES, TURN)
    )
    (far,) = exchange((qkv_rows, "z", FAR))
    qkv_pair = far_pair(qkv_rows, far, z)
    mid_wide = mid_rows.shape[1]
    rest_rows = tie(rest_rows, qkv_pair)
    mid_rows, down_rows = rest_rows[:, :mid_wide], rest_rows[:, mid_wide:]
    qkv_pair, mid_rows, cot_rest = lax.optimization_barrier((qkv_pair, mid_rows, cot[16:]))
    got = exchange((qkv_pair, "z", NEAR), (mid_rows, "z", FAR), (cot_rest, CORES, TURN))
    own_cot = got[2]
    qkv_line = whole_line(qkv_pair, got[0], z)
    mid_pair = far_pair(mid_rows, got[1], z)
    got = exchange(*first_moves(qkv_line), (mid_pair, "z", NEAR))
    qkv_parts = first_parts(qkv_line, got, x, y)
    mid_line = whole_line(mid_pair, got[2], z)
    last = last_moves(qkv_parts)
    got = exchange(*last, (tie(down_rows, mid_line), "z", FAR), *first_moves(mid_line))
    full_qkv = full_rows(qkv_parts, got, x, y)
    down_pair = far_pair(down_rows, got[2], z)
    mid_parts = first_parts(mid_line, got[3:], x, y)
    (near,) = exchange((down_pair, "z", NEAR))
    down_line = whole_line(down_pair, near, z)
    got = exchange(*last_moves(mid_parts), *first_moves(down_line))
    full_mid = full_rows(mid_parts, got, x, y)
    down_parts = first_parts(down_line, got[2:], x, y)
    full_out = full_mid[:, up_wide : up_wide + half_width]
    pairs = full_mid[:, up_wide + half_width :].reshape(chip_count, 64, 128)
    pairs = pairs[:, 0, :half_queries].astype(jnp.int32).reshape(1, query_total)
    row_lengths = lax.dynamic_index_in_dim(lengths, chip, 0, keepdims=False)
    segments = segments_of(row_lengths, token_count)
    seg_row, spans = segments[None, :], token_spans(row_lengths, token_count)
    query_span = NQ_ROW * QLEN
    bounds = tile_bounds(row_lengths, token_count)
    no_bias = jnp.zeros((1, quarter), F32)
    qkv_bias = jnp.concatenate(
        [
            part
            for g in range(2)
            for part in (
                bias[:, g * quarter : (g + 1) * quarter],
                no_bias,
                bias[:, half_width + g * quarter : half_width + (g + 1) * quarter],
            )
        ],
        axis=1,
    )
    qkv = (dot(row, full_qkv) + qkv_bias).astype(BF)
    mixed, lse = attend(bounds, tie(qkv, down_line), spans)

    def row_sum(left, weight_t, transposed):
        times = contract_cols if transposed else dot
        theirs = swap(times(left(1), weight_t).astype(BF), "c")
        return times(left(0), weight_t) + theirs.astype(F32)

    def mixed_half(which):
        return rows_of(mixed, other_start if which else own_start, share)

    other_attn = swap(contract_cols(mixed_half(1), full_out).astype(BF), "c")
    other_attn, cot_head = lax.optimization_barrier((other_attn, cot[:16]))
    cot_head = lax.ppermute(cot_head, CORES, TURN)
    cot_head, *down_parts = lax.optimization_barrier((cot_head,) + tuple(down_parts))
    own_cot = jnp.concatenate([cot_head, own_cot], axis=0)
    down_got = exchange(*last_moves(down_parts))
    attn_sum = contract_cols(mixed_half(0), full_out) + other_attn.astype(F32)
    own_tokens = rows_of(row, own_start, share).astype(F32)
    normed, unit_one, rstd_one = norm_forward(
        own_tokens + attn_sum + b_out.astype(F32), gains[0], shifts[0]
    )
    normed_low = normed.astype(BF)
    normed_all = jnp.concatenate([normed_low, swap(normed_low, "c")], axis=0)
    activation, slope = expand(
        normed_all, full_mid, bias[:, 2 * half_width :], 0, up_wide // 256
    )
    full_down = full_rows(down_parts, down_got, x, y)
    ffn_sum = row_sum(
        lambda which: activation[which * share : (which + 1) * share], full_down, True
    )
    result, unit_two, rstd_two = norm_forward(
        normed + ffn_sum + b_down.astype(F32), gains[1], shifts[1]
    )
    result_low = result.astype(BF)
    embed = dot(result_low, w_proj).astype(BF)

    other_embed = swap(embed, "c")
    row_embed = jnp.where(
        c == 0,
        jnp.concatenate([embed, other_embed], axis=0),
        jnp.concatenate([other_embed, embed], axis=0),
    )
    half_span = query_span // 2
    own_queries = rows_of(row_embed, c * half_span, half_span)
    chips = ("z", "x", "y")
    queries = lax.all_to_all(
        jnp.broadcast_to(own_queries[None], (chip_count,) + own_queries.shape), chips, 0, 0
    ).reshape(chip_count * half_span, -1)
    proj_width = w_proj.shape[1]
    cuts = (proj_width, 3 * proj_width // 4, proj_width // 2)
    sums = pool(cuts, query_span, queries, row_embed, seg_row)
    doc_sizes = jnp.tile(row_lengths.astype(F32), 3)[:, None]
    group = (
        jnp.arange(query_total * QLEN, dtype=jnp.int32)[:, None] // QLEN
        == jnp.arange(query_total, dtype=jnp.int32)[None, :]
    ).astype(F32)
    pooled = POOL_TEMP * jnp.log(sums / doc_sizes)
    logits = jnp.dot(pooled, group, precision=FULL_PRECISION) / LOSS_TEMP
    logits = logits.reshape(3, NDOC, query_total)
    doc_numbers = chip * NDOC + jnp.arange(NDOC, dtype=jnp.int32)
    picked = (doc_numbers[:, None] == pairs).astype(F32)
    own_high = jnp.max(logits, axis=1)
    own_lse = own_high + jnp.log(jnp.sum(jnp.exp(logits - own_high[:, None]), axis=1))
    own_target = jnp.sum(logits * picked, axis=1)
    notes = jnp.pad(jnp.concatenate([own_lse, own_target], axis=1), ((0, 5), (0, 0)))
    notes = lax.all_to_all(
        jnp.broadcast_to(notes[None], (chip_count,) + notes.shape), chips, 0, 0
    )
    chip_lse = notes[:, :3, :query_total]
    high = jnp.max(chip_lse, axis=0)
    all_lse = high + jnp.log(jnp.sum(jnp.exp(chip_lse - high), axis=0))
    target = jnp.sum(notes[:, :3, query_total:], axis=0)
    losses = jnp.sum(all_lse - target, axis=0).reshape(chip_count, half_queries)
    grad_logits = (jnp.exp(logits - all_lse[:, None]) - picked) / LOSS_TEMP
    coefficient = (
        lax.dot_general(
            grad_logits.reshape(3 * NDOC, query_total),
            group,
            (((1,), (1,)), ((), ())),
            precision=FULL_PRECISION,
        )
        / sums
    )
    query_grad, doc_grad = pool_back(cuts, query_span, queries, row_embed, seg_row, coefficient)
    grad_blocks = lax.all_to_all(
        query_grad.reshape(chip_count, half_span, proj_width), chips, 0, 0
    )
    own_query_grad = jnp.sum(grad_blocks.astype(F32), axis=0)
    row_grad = jnp.concatenate([jnp.zeros((query_span, proj_width), F32), doc_grad], axis=0)
    row_grad = lax.dynamic_update_slice_in_dim(row_grad, own_query_grad, c * half_span, 0)
    grad_embed = rows_of(row_grad, own_start, share) + swap(
        rows_of(row_grad, other_start, share), "c"
    )

    proj_low = w_proj
    grad_embed_low = grad_embed.astype(BF)
    grad_embed_rest = (grad_embed - grad_embed_low.astype(F32)).astype(BF)
    grad_result = own_cot.astype(F32) + (
        contract_cols(grad_embed_low, proj_low) + contract_cols(grad_embed_rest, proj_low)
    )
    proj_grad = contract_rows(result_low, grad_embed_low) + contract_rows(
        result_low, grad_embed_rest
    )
    gain_two = jnp.sum(grad_result * unit_two, axis=0)
    shift_two = jnp.sum(grad_result, axis=0)
    grad_second = norm_backward(grad_result, unit_two, rstd_two, gains[1])
    grad_ffn = grad_second.astype(BF)
    down_bias = jnp.sum(grad_ffn.astype(F32), axis=0)
    other_ffn = swap(grad_ffn, "c")
    grad_ffn_all = jnp.concatenate([grad_ffn, other_ffn], axis=0)
    down_blocks = blocks_of(grad_ffn_all, activation)
    down_moved = exchange(*sum_moves(down_blocks, x, y))
    grad_up = (dot(grad_ffn_all, full_down) * slope.astype(F32)).astype(BF)
    up_bias = jnp.sum(grad_up.astype(F32), axis=0)
    up_blocks = blocks_of(normed_all, tie(grad_up, *down_moved))
    full_up = full_mid[:, :up_wide]
    grad_normed = (
        row_sum(lambda which: grad_up[which * share : (which + 1) * share], full_up, True)
        + grad_second
    )
    gain_one = jnp.sum(grad_normed * unit_one, axis=0)
    shift_one = jnp.sum(grad_normed, axis=0)
    grad_first = norm_backward(grad_normed, unit_one, rstd_one, gains[0])
    grad_attn = grad_first.astype(BF)
    out_bias = jnp.sum(grad_attn.astype(F32), axis=0)
    other_attn = swap(grad_attn, "c")
    grad_attn_all = jnp.where(
        c == 0,
        jnp.concatenate([grad_attn, other_attn], axis=0),
        jnp.concatenate([other_attn, grad_attn], axis=0),
    )
    grad_mixed = dot(grad_attn_all, full_out).astype(BF)
    out_blocks = blocks_of(grad_attn_all, mixed)
    down_parts = sum_parts(down_blocks, down_moved, x, y)
    moved = exchange(*line_moves(down_parts, x, y), *sum_moves(up_blocks, x, y))
    down_line = line_of(down_parts, moved, x, y)
    up_parts = sum_parts(up_blocks, moved[2:], x, y)
    grad_mixed, out_blocks, down_line, *up_parts = lax.optimization_barrier(
        (grad_mixed, out_blocks, down_line) + tuple(up_parts)
    )
    moved = exchange(
        near_move(down_line, z), *line_moves(up_parts, x, y), *sum_moves(out_blocks, x, y)
    )
    grads_one, sums_one = attend_back(bounds, 0, qkv, mixed, grad_mixed, lse, spans)
    down_pair = near_sum(down_line, moved[0], z)
    up_line = line_of(up_parts, moved[1:], x, y)
    out_parts = sum_parts(out_blocks, moved[3:], x, y)
    grad_mixed, down_pair, up_line, *out_parts = lax.optimization_barrier(
        (grad_mixed, down_pair, up_line) + tuple(out_parts)
    )
    up_line, y_given, losses = lax.optimization_barrier((up_line, result_low, losses))
    moved = exchange(
        far_move(down_pair, z),
        near_move(up_line, z),
        *line_moves(out_parts, x, y),
        (y_given, CORES, TURN),
    )
    other_losses = swap(losses, "c")
    proj_given, other_losses, grad_mixed = lax.optimization_barrier(
        (rows_of(proj_grad, other_start, share), other_losses, grad_mixed)
    )
    proj_half = rows_of(proj_grad, own_start, share)
    other_proj = swap(proj_given, "c")
    grad_mixed, other_proj = lax.optimization_barrier((grad_mixed, other_proj))
    proj_half = proj_half + other_proj
    losses = jnp.where(c == y, losses, other_losses)
    loss_out = rows_of(losses, 4 * z + 2 * x + c, 1)
    grads_two, sums_two = attend_back(bounds, 1, qkv, mixed, grad_mixed, lse, spans)
    y_out = moved[4]
    down_part = far_sum(down_pair, moved[0], z)
    up_pair = near_sum(up_line, moved[1], z)
    out_line = line_of(out_parts, moved[2:], x, y)
    grads_one, grads_two, down_part, up_pair, out_line = lax.optimization_barrier(
        (grads_one, grads_two, down_part, up_pair, out_line)
    )
    shared = jnp.stack([gain_one, gain_two, shift_one, shift_two, out_bias, down_bias])
    half_sums = jnp.concatenate(
        [
            sums_one[0],
            sums_two[0],
            sums_one[1],
            sums_two[1],
            up_bias,
        ]
    )
    small = jnp.concatenate([shared.reshape(-1, 128), half_sums.reshape(-1, 128), proj_half])

    qkv_blocks = jnp.concatenate(
        [blocks_of(row, grads_one), blocks_of(row, grads_two)], axis=4
    )
    qkv_blocks, up_pair, out_line, down_part, small = lax.optimization_barrier(
        (qkv_blocks, up_pair, out_line, down_part, small)
    )
    moved = exchange(
        *sum_moves(qkv_blocks, x, y),
        far_move(up_pair, z),
        near_move(out_line, z),
        (small.astype(BF), "y", SWAP),
    )
    qkv_parts = sum_parts(qkv_blocks, moved, x, y)
    up_part = far_sum(up_pair, moved[2], z)
    out_pair = near_sum(out_line, moved[3], z)
    small = small + moved[4].astype(F32)

    def input_terms(start):
        return contract_cols(
            rows_of(grads_one, start, share), full_qkv[:, : 3 * quarter]
        ) + contract_cols(rows_of(grads_two, start, share), full_qkv[:, 3 * quarter :])

    other_terms = swap(input_terms(other_start).astype(BF), "c")
    grad_input = (input_terms(own_start) + other_terms.astype(F32) + grad_first).astype(BF)
    moved = exchange(*line_moves(qkv_parts, x, y), far_move(out_pair, z), (small.astype(BF), "x", SWAP))
    qkv_line = line_of(qkv_parts, moved, x, y)
    out_part = far_sum(out_pair, moved[2], z)
    small = small + moved[3].astype(F32)
    moved = exchange(
        near_move(qkv_line, z),
        (small.astype(BF), "z", FAR),
        (tie(grad_input, qkv_line), CORES, TURN),
    )
    qkv_pair = near_sum(qkv_line, moved[0], z)
    small = small + moved[1].astype(F32)
    grad_input = moved[2]
    ffn_part = jnp.concatenate([down_part, up_part], axis=1).astype(BF)
    moved = exchange(
        far_move(qkv_pair, z), (small.astype(BF), "z", NEAR), (tie(ffn_part, qkv_pair), CORES, TURN)
    )
    attn_part = jnp.concatenate([far_sum(qkv_pair, moved[0], z), out_part], axis=1).astype(BF)
    small = small + moved[1].astype(F32)
    ffn_part = moved[2].astype(F32)
    down_part, up_part = ffn_part[:, :up_wide], ffn_part[:, up_wide:]
    attn_part, other_small = exchange((attn_part, CORES, TURN), (small.astype(BF), "c", SWAP))
    attn_part = attn_part.astype(F32)
    other_small = other_small.astype(F32)
    qkv_part, out_part = attn_part[:, : 3 * half_width], attn_part[:, 3 * half_width :]
    shared_rows = 6 * width // 128
    small_rows = small.shape[0] - share
    shared = (small[:shared_rows] + other_small[:shared_rows]).reshape(6, width)
    half_sums = jnp.where(
        c == y, small[shared_rows:small_rows], other_small[shared_rows:small_rows]
    ).reshape(-1)
    proj_sum = pair_up(small[small_rows:], other_small[small_rows:], c, 0).reshape(width, -1)
    qkv_part = qkv_part.reshape(64, 2, 3, quarter).transpose(2, 0, 1, 3).reshape(3, 64, half_width)
    return (
        y_out,
        loss_out,
        grad_input,
        qkv_part,
        half_sums[: 2 * half_width].reshape(2, half_width),
        out_part.T,
        shared[4],
        shared[0:2],
        shared[2:4],
        up_part,
        half_sums[2 * half_width :],
        down_part.T,
        shared[5],
        proj_sum,
    )


IN_SPECS = (
    P("dp", None),
    P(),
    P("dp", "tensor"),
    P(None, "dp", "tensor"),
    P(None, "tensor"),
    P("tensor", "dp"),
    P(),
    P(),
    P(),
    P("dp", "tensor"),
    P("tensor"),
    P("tensor", "dp"),
    P(),
    P(),
    P(("dp", "tensor"), None),
)
OUT_SPECS = (
    P(("dp", "tensor"), None),
    P("dp", "tensor"),
    P(("dp", "tensor"), None),
    P(None, "dp", "tensor"),
    P(None, "tensor"),
    P("tensor", "dp"),
    P(),
    P(),
    P(),
    P("dp", "tensor"),
    P("tensor"),
    P("tensor", "dp"),
    P(),
    P(),
)


def solution(mesh):
    if mesh.devices.shape != (16, 2):
        return jax.shard_map(
            local, mesh=mesh, in_specs=IN_SPECS, out_specs=OUT_SPECS, check_vma=False
        )
    names = {"dp": ("z", "x", "c"), "tensor": ("y",)}

    def respec(spec):
        parts = []
        for entry in spec:
            axes = () if entry is None else entry if isinstance(entry, tuple) else (entry,)
            parts.append(tuple(name for axis in axes for name in names[axis]) or None)
        return P(*parts)

    chips = Mesh(mesh.devices.reshape(4, 2, 2, 2), ("z", "x", "c", "y"))
    return jax.shard_map(
        local_chip,
        mesh=chips,
        in_specs=tuple(respec(spec) for spec in IN_SPECS),
        out_specs=tuple(respec(spec) for spec in OUT_SPECS),
        check_vma=False,
    )
```

```python
from functools import partial

import jax
import jax.numpy as jnp
from jax import lax
from jax.experimental import pallas as pl
from jax.experimental.pallas import tpu as pltpu
from jax.sharding import Mesh, PartitionSpec as P

HEAD_DIM = 64
QLEN = 32
NQ_ROW = 8
NDOC = 8


EPS_NORM = 1e-05
EPS_EMBED = 1e-06
POOL_TEMP = 0.1
LOSS_TEMP = 0.1
FULL_PRECISION = lax.Precision.HIGHEST
MASKED_SCORE = -1e30


def shortened(shard):

    def short(part):
        return part.astype(jnp.bfloat16) if part.dtype == jnp.float32 else part

    return jax.tree.map(short, shard)


def contract_rows(left, right, precision=None):
    return lax.dot_general(
        left,
        right,
        (((0,), (0,)), ((), ())),
        precision=precision,
        preferred_element_type=jnp.float32,
    )


def contract_cols(left, right, precision=None):
    return lax.dot_general(
        left,
        right,
        (((1,), (1,)), ((), ())),
        precision=precision,
        preferred_element_type=jnp.float32,
    )


def norm_forward(value, gain, shift):
    centred = value - jnp.mean(value, axis=1, keepdims=True)
    rstd = lax.rsqrt(jnp.mean(centred * centred, axis=1, keepdims=True) + EPS_NORM)
    unit = centred * rstd
    return (unit * gain + shift, unit, rstd)


def norm_backward(grad, unit, rstd, gain):
    scaled = grad * gain
    return rstd * (
        scaled
        - jnp.mean(scaled, axis=1, keepdims=True)
        - unit * jnp.mean(scaled * unit, axis=1, keepdims=True)
    )


def segments_of(row_lengths, token_count):
    position = jnp.arange(token_count, dtype=jnp.int32)
    query_span = NQ_ROW * QLEN
    ends = jnp.cumsum(row_lengths)
    passed = jnp.sum((position[:, None] - query_span >= ends[None, :]).astype(jnp.int32), axis=1)
    return jnp.where(position < query_span, position // QLEN, NQ_ROW + passed)


def normalize_cut(raw, width):
    part = raw[:, :width]
    scale = lax.rsqrt(jnp.sum(part * part, axis=1, keepdims=True) + EPS_EMBED)
    return (part * scale, part, scale)


def normalize_back(grad, part, scale, full_width):
    result = scale * grad - part * (scale * scale * scale) * jnp.sum(
        part * grad, axis=1, keepdims=True
    )
    return jnp.pad(result, ((0, 0), (0, full_width - grad.shape[1])))


def masked_scores(query_block, key_rows, block_segments, segments):
    scores = jnp.einsum(
        "qhd,khd->hqk", query_block, key_rows, preferred_element_type=jnp.float32
    ) * HEAD_DIM ** (-0.5)
    return jnp.where((block_segments[:, None] == segments[None, :])[None], scores, MASKED_SCORE)


def attend_forward(query_rows, key_rows, value_rows, segments, block_rows):
    token_count = query_rows.shape[0]

    def one_block(block_start):
        query_block = lax.dynamic_slice_in_dim(query_rows, block_start, block_rows, 0)
        block_segments = lax.dynamic_slice_in_dim(segments, block_start, block_rows, 0)
        scores = masked_scores(query_block, key_rows, block_segments, segments)
        highest = jnp.max(scores, axis=2, keepdims=True)
        expo = jnp.exp(scores - highest)
        totals = jnp.sum(expo, axis=2, keepdims=True)
        weights = (expo / totals).astype(jnp.bfloat16)
        mixed = jnp.einsum("hqk,khd->qhd", weights, value_rows, preferred_element_type=jnp.float32)
        return (mixed.astype(jnp.bfloat16), (highest + jnp.log(totals))[:, :, 0])

    starts = jnp.arange(token_count // block_rows, dtype=jnp.int32) * block_rows
    mixed, log_totals = lax.map(one_block, starts)
    return (mixed.reshape(token_count, -1), log_totals)


def attend_backward(query_rows, key_rows, value_rows, segments, log_totals, grad_mixed, block_rows):
    token_count, local_heads, head_size = query_rows.shape
    scale = HEAD_DIM ** (-0.5)
    grad_heads = grad_mixed.reshape(token_count, local_heads, head_size)

    def one_block(carried, inputs):
        grad_keys, grad_values = carried
        block_start, block_lse = inputs
        query_block = lax.dynamic_slice_in_dim(query_rows, block_start, block_rows, 0)
        grad_block = lax.dynamic_slice_in_dim(grad_heads, block_start, block_rows, 0)
        block_segments = lax.dynamic_slice_in_dim(segments, block_start, block_rows, 0)
        scores = masked_scores(query_block, key_rows, block_segments, segments)
        probs = jnp.exp(scores - block_lse[:, :, None])
        grad_probs = jnp.einsum(
            "qhd,khd->hqk", grad_block, value_rows, preferred_element_type=jnp.float32
        )
        inner = jnp.sum(probs * grad_probs, axis=2, keepdims=True)
        grad_scores = (probs * (grad_probs - inner)).astype(jnp.bfloat16)
        grad_query = (
            jnp.einsum("hqk,khd->qhd", grad_scores, key_rows, preferred_element_type=jnp.float32)
            * scale
        )
        grad_keys = (
            grad_keys
            + jnp.einsum(
                "hqk,qhd->khd", grad_scores, query_block, preferred_element_type=jnp.float32
            )
            * scale
        )
        grad_values = grad_values + jnp.einsum(
            "hqk,qhd->khd",
            probs.astype(jnp.bfloat16),
            grad_block,
            preferred_element_type=jnp.float32,
        )
        return ((grad_keys, grad_values), grad_query)

    starts = jnp.arange(token_count // block_rows, dtype=jnp.int32) * block_rows
    zero_rows = jnp.zeros(key_rows.shape, jnp.float32)
    (grad_keys, grad_values), grad_queries = lax.scan(
        one_block, (zero_rows, zero_rows), (starts, log_totals)
    )
    flat_width = local_heads * head_size
    return (
        grad_queries.reshape(token_count, flat_width),
        grad_keys.reshape(token_count, flat_width),
        grad_values.reshape(token_count, flat_width),
    )


def local(
    tokens,
    lengths,
    pairing,
    w_qkv,
    b_qv,
    w_out,
    b_out,
    ln_gain,
    ln_bias,
    w_up,
    b_up,
    w_down,
    b_down,
    w_proj,
    cot,
):
    tensor_count = lax.axis_size("tensor")
    tensor_index = lax.axis_index("tensor")
    data_index = lax.axis_index("dp")
    token_count = tokens.shape[0]
    share_rows = token_count // tensor_count
    block_rows = min(512, token_count)
    own_start = tensor_index * share_rows
    full_qkv, full_out, full_up, full_down = (
        lax.all_gather(w_qkv, "dp", axis=1, tiled=True),
        lax.all_gather(w_out, "dp", axis=1, tiled=True),
        lax.all_gather(w_up, "dp", axis=0, tiled=True),
        lax.all_gather(w_down, "dp", axis=1, tiled=True),
    )
    head_width = full_qkv.shape[2]
    local_heads = head_width // HEAD_DIM
    row_lengths = lax.dynamic_index_in_dim(lengths, data_index, 0, keepdims=False)
    segments = segments_of(row_lengths, token_count)
    projected = jnp.einsum("td,kdw->ktw", tokens, full_qkv, preferred_element_type=jnp.float32)
    qv_bias = b_qv.astype(jnp.float32)
    query_rows = (
        (projected[0] + qv_bias[0]).astype(jnp.bfloat16).reshape(token_count, local_heads, HEAD_DIM)
    )
    key_rows = projected[1].astype(jnp.bfloat16).reshape(token_count, local_heads, HEAD_DIM)
    value_rows = (
        (projected[2] + qv_bias[1]).astype(jnp.bfloat16).reshape(token_count, local_heads, HEAD_DIM)
    )
    mixed, log_totals = attend_forward(query_rows, key_rows, value_rows, segments, block_rows)
    attn_terms = jnp.dot(mixed, full_out, preferred_element_type=jnp.float32)
    attn_sum = lax.psum_scatter(
        attn_terms.astype(jnp.bfloat16), "tensor", scatter_dimension=0, tiled=True
    ).astype(jnp.float32)
    own_tokens = lax.dynamic_slice_in_dim(tokens, own_start, share_rows, 0).astype(jnp.float32)
    gains = ln_gain.astype(jnp.float32)
    shifts = ln_bias.astype(jnp.float32)
    normed, unit_one, rstd_one = norm_forward(
        own_tokens + attn_sum + b_out.astype(jnp.float32), gains[0], shifts[0]
    )
    normed_all = lax.all_gather(normed.astype(jnp.bfloat16), "tensor", axis=0, tiled=True)
    up_value = jnp.dot(normed_all, full_up, preferred_element_type=jnp.float32) + b_up.astype(
        jnp.float32
    )
    activation = jax.nn.gelu(up_value, approximate=False).astype(jnp.bfloat16)
    ffn_terms = jnp.dot(activation, full_down, preferred_element_type=jnp.float32)
    ffn_sum = lax.psum_scatter(
        ffn_terms.astype(jnp.bfloat16), "tensor", scatter_dimension=0, tiled=True
    ).astype(jnp.float32)
    result, unit_two, rstd_two = norm_forward(
        normed + ffn_sum + b_down.astype(jnp.float32), gains[1], shifts[1]
    )
    result_low = result.astype(jnp.bfloat16)
    embed = jnp.dot(result_low, w_proj, preferred_element_type=jnp.float32).astype(jnp.bfloat16)
    embed_all = lax.all_gather(embed, ("dp", "tensor"), axis=0, tiled=True)
    row_count = lengths.shape[0]
    proj_width = w_proj.shape[1]
    widths = (proj_width, 3 * proj_width // 4, proj_width // 2)
    per_device = pairing.shape[1]
    query_count = per_device * QLEN
    query_span = NQ_ROW * QLEN
    emb_rows = embed_all.reshape(row_count, token_count, proj_width)
    my_row = lax.dynamic_index_in_dim(emb_rows, data_index, 0, keepdims=False)
    query_raw = lax.dynamic_slice_in_dim(my_row, tensor_index * query_count, query_count, 0).astype(
        jnp.float32
    )
    query_levels = [normalize_cut(query_raw, width) for width in widths]
    query_units = [level_parts[0].astype(jnp.bfloat16) for level_parts in query_levels]
    doc_numbers = jnp.arange(NDOC, dtype=jnp.int32)

    def row_pool(carried, inputs):
        row_emb, lengths_row = inputs
        row_hot = (
            segments_of(lengths_row, token_count)[:, None] == NQ_ROW + doc_numbers[None, :]
        ).astype(jnp.float32)
        row_raw = row_emb.astype(jnp.float32)
        pooled_list = []
        sums_list = []
        for width, query_unit in zip(widths, query_units):
            doc_unit = normalize_cut(row_raw, width)[0].astype(jnp.bfloat16)
            expo = jnp.exp(contract_cols(query_unit, doc_unit) / POOL_TEMP)
            sums = jnp.dot(expo, row_hot, precision=FULL_PRECISION)
            pooled = POOL_TEMP * jnp.log(sums / lengths_row.astype(jnp.float32))
            pooled_list.append(jnp.sum(pooled.reshape(per_device, QLEN, NDOC), axis=1))
            sums_list.append(sums)
        return (carried, (jnp.stack(pooled_list), jnp.stack(sums_list)))

    _, (row_scores, row_sums) = lax.scan(row_pool, 0, (emb_rows, lengths))
    logits = (
        jnp.transpose(row_scores, (2, 1, 0, 3)).reshape(per_device, 3, row_count * NDOC) / LOSS_TEMP
    )
    own_pairs = pairing[0]
    target = jnp.take_along_axis(
        logits, jnp.broadcast_to(own_pairs[:, None, None], (per_device, 3, 1)), axis=2
    )[:, :, 0]
    loss_out = jnp.sum(jax.nn.logsumexp(logits, axis=2) - target, axis=1).reshape(1, per_device)
    picked = (
        jnp.arange(row_count * NDOC, dtype=jnp.int32)[None, None, :] == own_pairs[:, None, None]
    ).astype(jnp.float32)
    grad_logits = (jax.nn.softmax(logits, axis=2) - picked) / LOSS_TEMP
    grad_rows = jnp.transpose(grad_logits.reshape(per_device, 3, row_count, NDOC), (2, 1, 0, 3))
    coefficient = jnp.repeat(grad_rows, QLEN, axis=2) / row_sums

    def row_back(carried, inputs):
        row_emb, lengths_row, row_coef = inputs
        row_hot = (
            segments_of(lengths_row, token_count)[:, None] == NQ_ROW + doc_numbers[None, :]
        ).astype(jnp.float32)
        row_raw = row_emb.astype(jnp.float32)
        new_carried = []
        row_grad = jnp.zeros((token_count, proj_width), jnp.float32)
        for level_index in range(3):
            width = widths[level_index]
            doc_unit_f, doc_part, doc_scale = normalize_cut(row_raw, width)
            doc_unit = doc_unit_f.astype(jnp.bfloat16)
            expo = jnp.exp(contract_cols(query_units[level_index], doc_unit) / POOL_TEMP)
            spread = contract_cols(row_coef[level_index], row_hot, FULL_PRECISION)
            grad_sim = (expo * spread).astype(jnp.bfloat16)
            new_carried.append(
                carried[level_index]
                + jnp.dot(grad_sim, doc_unit, preferred_element_type=jnp.float32)
            )
        return (tuple(new_carried), row_grad)

    zero_query = tuple((jnp.zeros((query_count, width), jnp.float32) for width in widths))
    query_grads, doc_grads = lax.scan(row_back, zero_query, (emb_rows, lengths, coefficient))
    grad_query = jnp.zeros((query_count, proj_width), jnp.float32)
    for level_index in range(3):
        level_parts = query_levels[level_index]
        grad_query = grad_query + normalize_back(
            query_grads[level_index], level_parts[1], level_parts[2], proj_width
        )
    coef_mine = jnp.transpose(coefficient, (2, 1, 0, 3)).reshape(query_count, 3, row_count * NDOC)
    coef_all, grad_query_all = (
        lax.all_gather(shortened(coef_mine), ("dp", "tensor"), axis=0, tiled=True).astype(
            coef_mine.dtype
        ),
        lax.all_gather(
            grad_query.astype(jnp.bfloat16), ("dp", "tensor"), axis=0, tiled=True
        ).astype(grad_query.dtype),
    )
    own_raw = embed.astype(jnp.float32)
    own_segments = lax.dynamic_slice_in_dim(segments, own_start, share_rows, 0)
    own_docs = jnp.where(own_segments >= NQ_ROW, data_index * NDOC + own_segments - NQ_ROW, -1)
    own_hot = (own_docs[:, None] == jnp.arange(row_count * NDOC, dtype=jnp.int32)[None, :]).astype(
        jnp.float32
    )
    queries_all = (
        emb_rows[:, :query_span].reshape(row_count * query_span, proj_width).astype(jnp.float32)
    )
    grad_embed = jnp.zeros((share_rows, proj_width), jnp.float32)
    for level_index in range(3):
        width = widths[level_index]
        query_unit_all = normalize_cut(queries_all, width)[0].astype(jnp.bfloat16)
        doc_unit_f, doc_part, doc_scale = normalize_cut(own_raw, width)
        expo = jnp.exp(contract_cols(query_unit_all, doc_unit_f.astype(jnp.bfloat16)) / POOL_TEMP)
        spread = contract_cols(coef_all[:, level_index], own_hot, FULL_PRECISION)
        grad_sim = (expo * spread).astype(jnp.bfloat16)
        grad_doc = contract_rows(grad_sim, query_unit_all)
        grad_embed = grad_embed + normalize_back(grad_doc, doc_part, doc_scale, proj_width)
    row_query_grads = lax.dynamic_slice_in_dim(
        grad_query_all, data_index * query_span, query_span, 0
    )
    padded = jnp.pad(row_query_grads, ((0, token_count - query_span), (0, 0)))
    grad_embed = grad_embed + lax.dynamic_slice_in_dim(padded, own_start, share_rows, 0)
    proj_float = w_proj.astype(jnp.float32)
    grad_result = cot.astype(jnp.float32) + contract_cols(grad_embed, proj_float, FULL_PRECISION)
    proj_grad = contract_rows(result_low.astype(jnp.float32), grad_embed, FULL_PRECISION)
    gain_two = jnp.sum(grad_result * unit_two, axis=0)
    shift_two = jnp.sum(grad_result, axis=0)
    grad_second = norm_backward(grad_result, unit_two, rstd_two, gains[1])
    grad_ffn = grad_second.astype(jnp.bfloat16)
    down_bias = jnp.sum(grad_ffn.astype(jnp.float32), axis=0)
    grad_ffn_all = lax.all_gather(grad_ffn, "tensor", axis=0, tiled=True)
    grad_act = contract_cols(grad_ffn_all, full_down)
    down_grad = contract_rows(activation, grad_ffn_all)
    _, gelu_pull = jax.vjp(partial(jax.nn.gelu, approximate=False), up_value)
    grad_up = gelu_pull(grad_act)[0].astype(jnp.bfloat16)
    up_bias = jnp.sum(grad_up.astype(jnp.float32), axis=0)
    up_grad = contract_rows(normed_all, grad_up)
    normed_terms = contract_cols(grad_up, full_up)
    grad_normed = (
        lax.psum_scatter(
            normed_terms.astype(jnp.bfloat16), "tensor", scatter_dimension=0, tiled=True
        ).astype(jnp.float32)
        + grad_second
    )
    gain_one = jnp.sum(grad_normed * unit_one, axis=0)
    shift_one = jnp.sum(grad_normed, axis=0)
    grad_first = norm_backward(grad_normed, unit_one, rstd_one, gains[0])
    grad_attn = grad_first.astype(jnp.bfloat16)
    out_bias = jnp.sum(grad_attn.astype(jnp.float32), axis=0)
    grad_attn_all = lax.all_gather(grad_attn, "tensor", axis=0, tiled=True)
    out_grad = contract_rows(mixed, grad_attn_all)
    grad_mixed = contract_cols(grad_attn_all, full_out).astype(jnp.bfloat16)
    grad_q, grad_k, grad_v = attend_backward(
        query_rows, key_rows, value_rows, segments, log_totals, grad_mixed, block_rows
    )
    stacked_grads = jnp.stack(
        [grad_q.astype(jnp.bfloat16), grad_k.astype(jnp.bfloat16), grad_v.astype(jnp.bfloat16)]
    )
    qkv_grad = jnp.einsum("td,ktw->kdw", tokens, stacked_grads, preferred_element_type=jnp.float32)
    input_terms = jnp.einsum(
        "ktw,kdw->td", stacked_grads, full_qkv, preferred_element_type=jnp.float32
    )
    grad_input = (
        lax.psum_scatter(
            input_terms.astype(jnp.bfloat16), "tensor", scatter_dimension=0, tiled=True
        ).astype(jnp.float32)
        + grad_first
    )
    qv_grad = jnp.stack(
        [
            jnp.sum(stacked_grads[0].astype(jnp.float32), axis=0),
            jnp.sum(stacked_grads[2].astype(jnp.float32), axis=0),
        ]
    )
    qkv_part, out_part, up_part, down_part = (
        lax.psum_scatter(
            qkv_grad.astype(jnp.bfloat16), "dp", scatter_dimension=1, tiled=True
        ).astype(jnp.float32),
        lax.psum_scatter(
            out_grad.astype(jnp.bfloat16), "dp", scatter_dimension=1, tiled=True
        ).astype(jnp.float32),
        lax.psum_scatter(
            up_grad.astype(jnp.bfloat16), "dp", scatter_dimension=0, tiled=True
        ).astype(jnp.float32),
        lax.psum_scatter(
            down_grad.astype(jnp.bfloat16), "dp", scatter_dimension=1, tiled=True
        ).astype(jnp.float32),
    )
    gain_sum, shift_sum, out_bias_sum, down_bias_sum, proj_sum = lax.psum(
        (
            jnp.stack([gain_one, gain_two]),
            jnp.stack([shift_one, shift_two]),
            out_bias,
            down_bias,
            proj_grad,
        ),
        ("dp", "tensor"),
    )
    qv_sum, up_bias_sum = lax.psum((qv_grad, up_bias), "dp")
    return (
        result_low,
        loss_out,
        grad_input.astype(jnp.bfloat16),
        qkv_part,
        qv_sum,
        out_part,
        out_bias_sum,
        gain_sum,
        shift_sum,
        up_part,
        up_bias_sum,
        down_part,
        down_bias_sum,
        proj_sum,
    )


SWAP = [(0, 1), (1, 0)]
TURN = [(0, 0), (1, 2), (2, 1), (3, 3)]
FAR = [(0, 3), (3, 0), (1, 2), (2, 1)]
NEAR = [(0, 1), (1, 0), (2, 3), (3, 2)]
BF = jnp.bfloat16
F32 = jnp.float32


def dot(left, right):
    return jnp.dot(left, right, preferred_element_type=F32)


CORES = ("c", "y")


def tie(value, *others):
    return lax.optimization_barrier((value,) + others)[0]


def tie_all(values, *others):
    return lax.optimization_barrier(tuple(values) + others)[: len(values)]


def exchange(*moves):
    return lax.optimization_barrier(
        tuple(lax.ppermute(value, axis, steps) for value, axis, steps in moves)
    )


def swap(value, axis):
    return lax.ppermute(value, axis, SWAP)


def pair_up(first, second, own_index, axis):
    return jnp.where(
        own_index == 0, jnp.stack([first, second], axis), jnp.stack([second, first], axis)
    )


def far_pair(value, far, z):
    return jnp.where(z < 2, jnp.stack([value, far]), jnp.stack([far, value]))


def whole_line(pair, other, z):
    return jnp.where(
        (z == 0) | (z == 3),
        jnp.stack([pair[0], other[0], other[1], pair[1]]),
        jnp.stack([other[0], pair[0], pair[1], other[1]]),
    )


def first_moves(line):
    half = line.shape[1] // 2
    return ((line[:, :half], "x", SWAP), (line[:, half:], "y", SWAP))


def first_parts(line, moved, x, y):
    half = line.shape[1] // 2
    return (pair_up(line[:, :half], moved[0], x, 1), pair_up(line[:, half:], moved[1], y, 1))


def last_moves(parts):
    return ((parts[0], "y", SWAP), (parts[1], "x", SWAP))


def full_rows(parts, moved, x, y):
    low = pair_up(parts[0], moved[0], y, 2)
    high = pair_up(parts[1], moved[1], x, 1)
    return jnp.concatenate([low, high], axis=3).reshape(-1, low.shape[-1])


def at(blocks, index, axis):
    return lax.dynamic_index_in_dim(blocks, index, axis, keepdims=False)


def side_move(blocks, axis_name, own_index, axis):
    return (at(blocks, 1 - own_index, axis).astype(BF), axis_name, SWAP)


def side_sum(blocks, got, own_index, axis):
    return at(blocks, own_index, axis).astype(F32) + got.astype(F32)


def near_move(line, z):
    ends = (z == 0) | (z == 3)
    outer, inner = jnp.stack([line[0], line[3]]), line[1:3]
    return (jnp.where(ends, inner, outer).astype(BF), "z", NEAR)


def near_sum(line, got, z):
    ends = (z == 0) | (z == 3)
    return jnp.where(ends, jnp.stack([line[0], line[3]]), line[1:3]) + got.astype(F32)


def far_move(pair, z):
    return (jnp.where(z < 2, pair[1], pair[0]).astype(BF), "z", FAR)


def far_sum(pair, got, z):
    return jnp.where(z < 2, pair[0], pair[1]) + got.astype(F32)


def blocks_of(left, right):
    return contract_rows(left, right).astype(BF).reshape(4, 2, 2, 64, right.shape[1])


def sum_moves(blocks, x, y):
    half = blocks.shape[3] // 2
    return (
        side_move(blocks[..., :half, :], "x", x, 1),
        side_move(blocks[..., half:, :], "y", y, 2),
    )


def sum_parts(blocks, moved, x, y):
    half = blocks.shape[3] // 2
    return (
        side_sum(blocks[..., :half, :], moved[0], x, 1),
        side_sum(blocks[..., half:, :], moved[1], y, 2),
    )


def line_moves(parts, x, y):
    return (side_move(parts[0], "y", y, 1), side_move(parts[1], "x", x, 1))


def line_of(parts, moved, x, y):
    return jnp.concatenate(
        [side_sum(parts[0], moved[0], y, 1), side_sum(parts[1], moved[1], x, 1)], axis=1
    )


def tile_bounds(row_lengths, token_count):
    ends = jnp.cumsum(row_lengths)
    span = NQ_ROW * QLEN
    first = jnp.arange(token_count // TILE, dtype=jnp.int32) * TILE - span
    last = first + TILE - 1
    begin = jnp.max(jnp.where(ends[None, :] <= first[:, None], ends[None, :], 0), axis=1)
    end = jnp.min(jnp.where(ends[None, :] > last[:, None], ends[None, :], token_count), axis=1)
    low = jnp.where(first < 0, 0, (begin + span) // TILE)
    high = jnp.where(first < 0, 1, (end + span + TILE - 1) // TILE)
    return jnp.stack([low, high]).astype(jnp.int32)


def token_spans(row_lengths, token_count):
    ends = jnp.cumsum(row_lengths)[:, None]
    span = NQ_ROW * QLEN
    place = jnp.arange(token_count, dtype=jnp.int32)[None, :]
    doc = place - span
    begin = jnp.max(jnp.where(ends <= doc, ends, 0), axis=0) + span
    end = jnp.min(jnp.where(ends > doc, ends, token_count), axis=0) + span
    query = place[0] // QLEN * QLEN
    return jnp.stack(
        [jnp.where(doc[0] < 0, query, begin), jnp.where(doc[0] < 0, query + QLEN, end)]
    ).astype(jnp.int32)


def rows_of(value, start, count):
    return lax.dynamic_slice_in_dim(value, start, count, 0)


TILE = 256
KEYS = 256
NEG = -1e30


def exact(left, right, dims):
    return lax.dot_general(left, right, (dims, ((), ())), preferred_element_type=F32)


def head_masks(value):
    lane = lax.broadcasted_iota(jnp.int32, value.shape, 1)
    zero = jnp.zeros_like(value)
    return (jnp.where(lane < HEAD_DIM, value, zero), jnp.where(lane < HEAD_DIM, zero, value))


def key_shift(step, spans):
    place = step * KEYS + lax.broadcasted_iota(jnp.int32, (KEYS, TILE), 0)
    inside = (place >= spans[0:1, :]) & (place < spans[1:2, :])
    return jnp.where(inside, 0.0, NEG)


def attend_kernel(bounds, own_ref, qkv_ref, spans, out_ref, lse_ref, held):
    block = pl.program_id(0)
    groups = 2
    pairs = out_ref.shape[1] // 128
    per_group = pairs // groups

    def column(pair, part):
        start = ((pair // per_group) * 3 + part) * per_group + pair % per_group
        return slice(start * 128, (start + 1) * 128)

    queries = [head_masks(own_ref[:, column(pair, 0)] * HEAD_DIM**-0.5) for pair in range(pairs)]
    heads = [(pair, head) for pair in range(pairs) for head in range(2)]

    def score(step, highest):
        rows = pl.ds(pl.multiple_of(step * KEYS, KEYS), KEYS)
        shift = key_shift(step, spans)
        fresh = []
        for index, (pair, head) in enumerate(heads):
            keys = qkv_ref[rows, column(pair, 1)]
            scores = exact(keys, queries[pair][head], ((1,), (1,))) + shift
            held[index, rows, :] = scores
            fresh.append(jnp.maximum(highest[index], jnp.max(scores, axis=0, keepdims=True)))
        return tuple(fresh)

    low = jnp.full((1, TILE), NEG, F32)
    highest = lax.fori_loop(bounds[0, block], bounds[1, block], score, (low,) * len(heads))

    def mix(step, carried):
        rows = pl.ds(pl.multiple_of(step * KEYS, KEYS), KEYS)
        fresh = []
        for index, (pair, head) in enumerate(heads):
            values = qkv_ref[rows, column(pair, 2)]
            total, mixed = carried[index]
            expo = jnp.exp(held[index, rows, :] - highest[index])
            product = exact(values, expo.astype(BF), ((0,), (0,)))
            fresh.append(
                (
                    total + jnp.sum(expo, axis=0, keepdims=True),
                    mixed + product[head * HEAD_DIM : (head + 1) * HEAD_DIM],
                )
            )
        return tuple(fresh)

    start = (jnp.zeros((1, TILE), F32), jnp.zeros((HEAD_DIM, TILE), F32))
    parts = lax.fori_loop(bounds[0, block], bounds[1, block], mix, (start,) * len(heads))
    for pair in range(pairs):
        both = [parts[2 * pair + head][1] / parts[2 * pair + head][0] for head in range(2)]
        mixed = jnp.transpose(jnp.concatenate(both, axis=0))
        out_ref[:, pair * 128 : (pair + 1) * 128] = mixed.astype(BF)
    for index in range(len(heads)):
        lse_ref[index : index + 1, :] = highest[index] + jnp.log(parts[index][0])


def attend(bounds, qkv, spans):
    count, wide = qkv.shape
    heads = wide // 3 // HEAD_DIM
    whole = lambda shape: pl.BlockSpec(shape, lambda i: (0, 0))
    return pl.pallas_call(
        attend_kernel,
        grid=(count // TILE,),
        in_specs=[
            pl.BlockSpec(memory_space=pltpu.SMEM),
            pl.BlockSpec((TILE, wide), lambda i: (i, 0)),
            whole((count, wide)),
            pl.BlockSpec((2, TILE), lambda i: (0, i)),
        ],
        out_specs=[
            pl.BlockSpec((TILE, wide // 3), lambda i: (i, 0)),
            pl.BlockSpec((heads, TILE), lambda i: (0, i)),
        ],
        out_shape=[
            jax.ShapeDtypeStruct((count, wide // 3), BF),
            jax.ShapeDtypeStruct((heads, count), F32),
        ],
        scratch_shapes=[pltpu.VMEM((heads, count, TILE), F32)],
        compiler_params=pltpu.CompilerParams(vmem_limit_bytes=40 << 20),
        cost_estimate=pl.CostEstimate(
            flops=4 * heads * count * count * 64,
            transcendentals=heads * count * count // 2,
            bytes_accessed=4 * count * wide * 2,
        ),
    )(bounds, qkv, qkv, spans)


def attend_back_kernel(
    first, bounds, own_ref, qkv_ref, out_ref, grad_ref, lse_ref, spans,
    grads_ref, sums_ref, key_sum, value_sum,
):
    block = pl.program_id(0)
    pairs = out_ref.shape[1] // 128
    heads = [(pair, head) for pair in range(pairs) for head in range(2)]
    cut = lambda index: slice(index * 128, (index + 1) * 128)

    @pl.when(block == 0)
    def _():
        key_sum[...] = jnp.zeros_like(key_sum)
        value_sum[...] = jnp.zeros_like(value_sum)
        sums_ref[...] = jnp.zeros_like(sums_ref)

    queries = [head_masks(own_ref[:, cut(pair)] * HEAD_DIM**-0.5) for pair in range(pairs)]
    grads = [head_masks(grad_ref[:, cut(pair)]) for pair in range(pairs)]
    picks = head_masks(jnp.ones((8, 128), BF))
    inner = []
    for pair, head in heads:
        product = grad_ref[:, cut(pair)].astype(F32) * out_ref[:, cut(pair)].astype(F32)
        high = product.astype(BF)
        rest = (product - high.astype(F32)).astype(BF)
        inner.append(
            (
                exact(picks[head], high, ((1,), (1,))) + exact(picks[head], rest, ((1,), (1,)))
            )[0:1]
        )
    lse = [lse_ref[first + index : first + index + 1, :] for index in range(len(heads))]

    def step_of(step, carried):
        rows = pl.ds(pl.multiple_of(step * KEYS, KEYS), KEYS)
        shift = key_shift(step, spans)
        fresh = []
        for pair in range(pairs):
            keys = qkv_ref[rows, cut(pairs + pair)]
            values = qkv_ref[rows, cut(2 * pairs + pair)]
            key_add = jnp.zeros((KEYS, 128), F32)
            value_add = jnp.zeros((KEYS, 128), F32)
            for head in range(2):
                index = 2 * pair + head
                scores = exact(keys, queries[pair][head], ((1,), (1,))) + shift
                probs = jnp.exp(scores - lse[index])
                grad_probs = exact(values, grads[pair][head], ((1,), (1,)))
                grad_scores = (probs * (grad_probs - inner[index])).astype(BF)
                value_add = value_add + exact(probs.astype(BF), grads[pair][head], ((1,), (0,)))
                key_add = key_add + exact(grad_scores, queries[pair][head], ((1,), (0,)))
                product = exact(keys, grad_scores, ((0,), (0,)))
                fresh.append(carried[index] + product[head * HEAD_DIM : (head + 1) * HEAD_DIM])
            key_sum[rows, cut(pair)] += key_add
            value_sum[rows, cut(pair)] += value_add
        return tuple(fresh)

    start = jnp.zeros((HEAD_DIM, TILE), F32)
    parts = lax.fori_loop(bounds[0, block], bounds[1, block], step_of, (start,) * len(heads))
    own = pl.ds(pl.multiple_of(block * TILE, TILE), TILE)
    for pair in range(pairs):
        grad_query = jnp.concatenate([parts[2 * pair], parts[2 * pair + 1]], axis=0)
        grad_query = jnp.transpose(grad_query * HEAD_DIM**-0.5).astype(BF)
        grads_ref[own, cut(pair)] = grad_query
        sums_ref[0:1, cut(pair)] += jnp.sum(grad_query.astype(F32), axis=0, keepdims=True)

    @pl.when(block == pl.num_programs(0) - 1)
    def _():
        wide = pairs * 128
        grad_value = value_sum[...].astype(BF)
        grads_ref[:, wide : 2 * wide] = key_sum[...].astype(BF)
        grads_ref[:, 2 * wide :] = grad_value
        sums_ref[1:2, :] = jnp.sum(grad_value.astype(F32), axis=0, keepdims=True)


def attend_back(bounds, group, qkv, mixed, grad_mixed, lse, spans):
    count = qkv.shape[0]
    wide = qkv.shape[1] // 2
    heads = wide // 3 // HEAD_DIM
    whole = lambda shape: pl.BlockSpec(shape, lambda i: (0, 0))
    return pl.pallas_call(
        partial(attend_back_kernel, group * heads),
        grid=(count // TILE,),
        in_specs=[
            pl.BlockSpec(memory_space=pltpu.SMEM),
            pl.BlockSpec((TILE, wide), lambda i: (i, group)),
            pl.BlockSpec((count, wide), lambda i: (0, group)),
            pl.BlockSpec((TILE, wide // 3), lambda i: (i, group)),
            pl.BlockSpec((TILE, wide // 3), lambda i: (i, group)),
            pl.BlockSpec((2 * heads, TILE), lambda i: (0, i)),
            pl.BlockSpec((2, TILE), lambda i: (0, i)),
        ],
        out_specs=[whole((count, wide)), whole((8, wide // 3))],
        out_shape=[
            jax.ShapeDtypeStruct((count, wide), BF),
            jax.ShapeDtypeStruct((8, wide // 3), F32),
        ],
        scratch_shapes=[
            pltpu.VMEM((count, wide // 3), F32),
            pltpu.VMEM((count, wide // 3), F32),
        ],
        compiler_params=pltpu.CompilerParams(vmem_limit_bytes=40 << 20),
        cost_estimate=pl.CostEstimate(
            flops=10 * heads * count * count * 64,
            transcendentals=heads * count * count // 2,
            bytes_accessed=8 * count * wide * 2,
        ),
    )(
        bounds, qkv, qkv, mixed, grad_mixed,
        lse, spans,
    )


ERFC = (
    -1.26551223, 1.00002368, 0.37409196, 0.09678418, -0.18628806,
    0.27886807, -1.13520398, 1.48851587, -0.82215223, 0.17087277,
)


def gelu_pair(value):
    size = jnp.abs(value) * 0.5**0.5
    ratio = 1.0 / (1.0 + 0.5 * size)
    series = jnp.full_like(value, ERFC[-1])
    for factor in ERFC[-2::-1]:
        series = series * ratio + factor
    bell = jnp.exp(-size * size)
    tail = 0.5 * ratio * bell * jnp.exp(series)
    phi = jnp.where(value < 0.0, tail, 1.0 - tail)
    return (value * phi, phi + value * bell * 0.3989422804014327)


def expand_kernel(x_ref, w_ref, b_ref, *refs):
    act_ref, slope_ref = refs[-2:]
    rows = 256
    for start in range(0, x_ref.shape[0], rows):
        part = slice(start, start + rows)
        value = exact(x_ref[part, :], w_ref[...], ((1,), (0,))) + b_ref[...]
        active, slope = gelu_pair(value)
        act_ref[part, :] = active.astype(BF)
        slope_ref[part, :] = slope.astype(BF)


def expand(value, weight, shift, first, tiles, filled=()):
    count, depth = value.shape
    width = shift.shape[1]
    tile = 256
    column = lambda rows: pl.BlockSpec((rows, tile), lambda i: (0, first + i))
    return pl.pallas_call(
        expand_kernel,
        grid=(tiles,),
        in_specs=[
            pl.BlockSpec((count, depth), lambda i: (0, 0)),
            column(depth),
            column(1),
        ]
        + [pl.BlockSpec(memory_space=pl.ANY)] * len(filled),
        out_specs=[column(count)] * 2,
        out_shape=[jax.ShapeDtypeStruct((count, width), BF)] * 2,
        input_output_aliases={3: 0, 4: 1} if filled else {},
        compiler_params=pltpu.CompilerParams(vmem_limit_bytes=32 << 20),
        cost_estimate=pl.CostEstimate(
            flops=2 * count * depth * tile * tiles,
            transcendentals=3 * count * tile * tiles,
            bytes_accessed=2 * (count * depth + depth * tile * tiles + 2 * count * tile * tiles),
        ),
    )(value, weight, shift, *filled)


def cut_levels(raw, cuts):
    lane = lax.broadcasted_iota(jnp.int32, raw.shape, 1)
    levels = []
    for cut in cuts:
        part = jnp.where(lane < cut, raw, 0.0)
        scale = lax.rsqrt(jnp.sum(part * part, axis=1, keepdims=True) + EPS_EMBED)
        levels.append(((part * scale).astype(BF), part, scale))
    return levels


def pool_kernel(cuts, span, q_ref, d_ref, seg_ref, out_ref, units, hot):
    @pl.when(pl.program_id(0) == 0)
    def _():
        raw = d_ref[span:, :].astype(F32)
        for level, parts in enumerate(cut_levels(raw, cuts)):
            units[level] = parts[0]
        doc = lax.broadcasted_iota(jnp.int32, hot.shape, 0)
        hot[...] = (seg_ref[:, span:] == NQ_ROW + doc).astype(F32).astype(BF)

    levels = cut_levels(q_ref[...].astype(F32), cuts)
    for level in range(len(cuts)):
        similar = exact(units[level], levels[level][0], ((1,), (1,)))
        expo = jnp.exp(similar * (1.0 / POOL_TEMP))
        high = expo.astype(BF)
        rest = (expo - high.astype(F32)).astype(BF)
        out_ref[level * NDOC : (level + 1) * NDOC, :] = exact(
            hot[...], high, ((1,), (0,))
        ) + exact(hot[...], rest, ((1,), (0,)))


def pool(cuts, span, queries, row_embed, seg_row):
    count, width = queries.shape
    tokens = row_embed.shape[0]
    whole = lambda shape: pl.BlockSpec(shape, lambda i: (0, 0))
    return pl.pallas_call(
        partial(pool_kernel, cuts, span),
        grid=(count // TILE,),
        in_specs=[
            pl.BlockSpec((TILE, width), lambda i: (i, 0)),
            whole((tokens, width)),
            whole((1, tokens)),
        ],
        out_specs=pl.BlockSpec((len(cuts) * NDOC, TILE), lambda i: (0, i)),
        out_shape=jax.ShapeDtypeStruct((len(cuts) * NDOC, count), F32),
        scratch_shapes=[
            pltpu.VMEM((len(cuts), tokens - span, width), BF),
            pltpu.VMEM((NDOC, tokens - span), BF),
        ],
        compiler_params=pltpu.CompilerParams(vmem_limit_bytes=32 << 20),
        cost_estimate=pl.CostEstimate(
            flops=2 * len(cuts) * count * tokens * 256,
            transcendentals=len(cuts) * count * tokens,
            bytes_accessed=2 * (count + tokens) * width,
        ),
    )(queries, row_embed, seg_row)


def level_back(grad, part, scale):
    return scale * grad - part * (scale * scale * scale) * jnp.sum(
        part * grad, axis=1, keepdims=True
    )


def pool_back_kernel(
    cuts, span, q_ref, d_ref, seg_ref, coef_ref, q_out, d_out, units, units_t, hot, sums
):
    step = pl.program_id(0)

    @pl.when(step == 0)
    def _():
        raw = d_ref[span:, :].astype(F32)
        for level, parts in enumerate(cut_levels(raw, cuts)):
            units[level] = parts[0]
            units_t[level] = jnp.transpose(parts[0])
        doc = lax.broadcasted_iota(jnp.int32, hot.shape, 0)
        wanted = NQ_ROW + jnp.where(doc < NDOC, doc, doc - NDOC)
        hot[...] = (seg_ref[:, span:] == wanted).astype(F32).astype(BF)
        sums[...] = jnp.zeros_like(sums)

    levels = cut_levels(q_ref[...].astype(F32), cuts)
    total = jnp.zeros(q_ref.shape, F32)
    for level in range(len(cuts)):
        unit, part, scale = levels[level]
        similar = exact(units[level], unit, ((1,), (1,)))
        coef = coef_ref[level * NDOC : (level + 1) * NDOC, :]
        high = coef.astype(BF).astype(F32)
        both = jnp.concatenate([high, coef - high], axis=0).astype(BF)
        spread = exact(hot[...], both, ((0,), (0,)))
        grad = (jnp.exp(similar * (1.0 / POOL_TEMP)) * spread).astype(BF)
        sums[level] += exact(grad, unit, ((1,), (0,)))
        grad_unit = jnp.transpose(exact(units_t[level], grad, ((1,), (0,))))
        total = total + level_back(grad_unit, part, scale)
    q_out[...] = total.astype(BF)

    @pl.when(step == pl.num_programs(0) - 1)
    def _():
        raw = d_ref[span:, :].astype(F32)
        result = jnp.zeros(raw.shape, F32)
        for level, parts in enumerate(cut_levels(raw, cuts)):
            lane = lax.broadcasted_iota(jnp.int32, raw.shape, 1)
            grad = jnp.where(lane < cuts[level], sums[level], 0.0)
            result = result + level_back(grad, parts[1], parts[2])
        d_out[...] = result


def pool_back(cuts, span, queries, row_embed, seg_row, coef):
    count, width = queries.shape
    tokens = row_embed.shape[0]
    docs = tokens - span
    whole = lambda shape: pl.BlockSpec(shape, lambda i: (0, 0))
    return pl.pallas_call(
        partial(pool_back_kernel, cuts, span),
        grid=(count // TILE,),
        in_specs=[
            pl.BlockSpec((TILE, width), lambda i: (i, 0)),
            whole((tokens, width)),
            whole((1, tokens)),
            pl.BlockSpec((len(cuts) * NDOC, TILE), lambda i: (0, i)),
        ],
        out_specs=[pl.BlockSpec((TILE, width), lambda i: (i, 0)), whole((docs, width))],
        out_shape=[
            jax.ShapeDtypeStruct((count, width), BF),
            jax.ShapeDtypeStruct((docs, width), F32),
        ],
        scratch_shapes=[
            pltpu.VMEM((len(cuts), docs, width), BF),
            pltpu.VMEM((len(cuts), width, docs), BF),
            pltpu.VMEM((2 * NDOC, docs), BF),
            pltpu.VMEM((len(cuts), docs, width), F32),
        ],
        compiler_params=pltpu.CompilerParams(vmem_limit_bytes=32 << 20),
        cost_estimate=pl.CostEstimate(
            flops=2 * len(cuts) * count * docs * 512,
            transcendentals=len(cuts) * count * docs,
            bytes_accessed=4 * (count + tokens) * width,
        ),
    )(queries, row_embed, seg_row, coef)


def local_chip(
    tokens,
    lengths,
    pairing,
    w_qkv,
    b_qv,
    w_out,
    b_out,
    ln_gain,
    ln_bias,
    w_up,
    b_up,
    w_down,
    b_down,
    w_proj,
    cot,
):
    z, x, c, y = (lax.axis_index(name) for name in ("z", "x", "c", "y"))
    chip = 4 * z + 2 * x + y
    token_count, width = tokens.shape
    share = token_count // 2
    own_start, other_start = c * share, (1 - c) * share
    gains, shifts = ln_gain.astype(F32), ln_bias.astype(F32)

    half_width = w_qkv.shape[2]
    up_wide = w_up.shape[1]
    chip_count = lengths.shape[0]
    half_queries = NQ_ROW // 2
    query_total = chip_count * half_queries
    quarter = half_width // 2
    qkv_rows = jnp.concatenate(
        [w_qkv[k][:, g * quarter : (g + 1) * quarter] for g in range(2) for k in range(3)], axis=1
    )
    pair_rows = jnp.pad(pairing.astype(BF), ((0, 63), (0, 128 - half_queries)))
    mid_rows = jnp.concatenate([w_up, w_out.T, pair_rows], axis=1)
    bias = jnp.concatenate([b_qv.reshape(-1), b_up])[None].astype(F32)
    got = exchange(
        (qkv_rows, CORES, TURN), (tokens, "c", SWAP), (bias, "y", SWAP)
    )
    qkv_rows = got[0]
    row = jnp.where(c == y, tokens, got[1])
    bias = jnp.where(c == y, bias, got[2])
    (rest_rows,) = exchange(
        (tie(jnp.concatenate([mid_rows, w_down.T], axis=1), row), CORES, TURN)
    )
    (far,) = exchange((qkv_rows, "z", FAR))
    qkv_pair = far_pair(qkv_rows, far, z)
    mid_wide = mid_rows.shape[1]
    rest_rows = tie(rest_rows, qkv_pair)
    mid_rows, down_rows = rest_rows[:, :mid_wide], rest_rows[:, mid_wide:]
    got = exchange((qkv_pair, "z", NEAR), (mid_rows, "z", FAR))
    qkv_line = whole_line(qkv_pair, got[0], z)
    mid_pair = far_pair(mid_rows, got[1], z)
    got = exchange(*first_moves(qkv_line), (mid_pair, "z", NEAR))
    qkv_parts = first_parts(qkv_line, got, x, y)
    mid_line = whole_line(mid_pair, got[2], z)
    last = last_moves(qkv_parts)
    got = exchange(*last, (tie(down_rows, mid_line), "z", FAR), *first_moves(mid_line))
    full_qkv = full_rows(qkv_parts, got, x, y)
    down_pair = far_pair(down_rows, got[2], z)
    mid_parts = first_parts(mid_line, got[3:], x, y)
    (near,) = exchange((down_pair, "z", NEAR))
    down_line = whole_line(down_pair, near, z)
    got = exchange(*last_moves(mid_parts), *first_moves(down_line))
    full_mid = full_rows(mid_parts, got, x, y)
    down_parts = first_parts(down_line, got[2:], x, y)
    full_out = full_mid[:, up_wide : up_wide + half_width]
    pairs = full_mid[:, up_wide + half_width :].reshape(chip_count, 64, 128)
    pairs = pairs[:, 0, :half_queries].astype(jnp.int32).reshape(1, query_total)
    row_lengths = lax.dynamic_index_in_dim(lengths, chip, 0, keepdims=False)
    segments = segments_of(row_lengths, token_count)
    seg_row, spans = segments[None, :], token_spans(row_lengths, token_count)
    query_span = NQ_ROW * QLEN
    bounds = tile_bounds(row_lengths, token_count)
    no_bias = jnp.zeros((1, quarter), F32)
    qkv_bias = jnp.concatenate(
        [
            part
            for g in range(2)
            for part in (
                bias[:, g * quarter : (g + 1) * quarter],
                no_bias,
                bias[:, half_width + g * quarter : half_width + (g + 1) * quarter],
            )
        ],
        axis=1,
    )
    qkv = (dot(row, full_qkv) + qkv_bias).astype(BF)
    mixed, lse = attend(bounds, tie(qkv, down_line), spans)

    def row_sum(left, weight_t, transposed):
        times = contract_cols if transposed else dot
        theirs = swap(times(left(1), weight_t).astype(BF), "c")
        return times(left(0), weight_t) + theirs.astype(F32)

    def mixed_half(which):
        return rows_of(mixed, other_start if which else own_start, share)

    other_attn = swap(contract_cols(mixed_half(1), full_out).astype(BF), "c")
    other_attn, second_norm = lax.optimization_barrier(
        (other_attn, jnp.stack([gains[1], shifts[1]]))
    )
    second_norm = swap(second_norm, "c")
    second_norm, cot_given, *down_parts = lax.optimization_barrier(
        (second_norm, cot) + tuple(down_parts)
    )
    down_got = exchange(*last_moves(down_parts), (cot_given, CORES, TURN))
    own_cot = down_got[2]
    attn_sum = contract_cols(mixed_half(0), full_out) + other_attn.astype(F32)
    own_tokens = rows_of(row, own_start, share).astype(F32)
    normed, unit_one, rstd_one = norm_forward(
        own_tokens + attn_sum + b_out.astype(F32), gains[0], shifts[0]
    )
    normed_low = normed.astype(BF)
    normed_all = jnp.concatenate([normed_low, swap(normed_low, "c")], axis=0)
    activation, slope = expand(
        normed_all, full_mid, bias[:, 2 * half_width :], 0, up_wide // 256
    )
    full_down = full_rows(down_parts, down_got, x, y)
    ffn_sum = row_sum(
        lambda which: activation[which * share : (which + 1) * share], full_down, True
    )
    result, unit_two, rstd_two = norm_forward(
        normed + ffn_sum + b_down.astype(F32), second_norm[0], second_norm[1]
    )
    result_low = result.astype(BF)
    embed = dot(result_low, w_proj).astype(BF)

    other_embed = swap(embed, "c")
    row_embed = jnp.where(
        c == 0,
        jnp.concatenate([embed, other_embed], axis=0),
        jnp.concatenate([other_embed, embed], axis=0),
    )
    half_span = query_span // 2
    own_queries = rows_of(row_embed, c * half_span, half_span)
    chips = ("z", "x", "y")
    queries = lax.all_to_all(
        jnp.broadcast_to(own_queries[None], (chip_count,) + own_queries.shape), chips, 0, 0
    ).reshape(chip_count * half_span, -1)
    proj_width = w_proj.shape[1]
    cuts = (proj_width, 3 * proj_width // 4, proj_width // 2)
    sums = pool(cuts, query_span, queries, row_embed, seg_row)
    doc_sizes = jnp.tile(row_lengths.astype(F32), 3)[:, None]
    group = (
        jnp.arange(query_total * QLEN, dtype=jnp.int32)[:, None] // QLEN
        == jnp.arange(query_total, dtype=jnp.int32)[None, :]
    ).astype(F32)
    pooled = POOL_TEMP * jnp.log(sums / doc_sizes)
    logits = jnp.dot(pooled, group, precision=FULL_PRECISION) / LOSS_TEMP
    logits = logits.reshape(3, NDOC, query_total)
    doc_numbers = chip * NDOC + jnp.arange(NDOC, dtype=jnp.int32)
    picked = (doc_numbers[:, None] == pairs).astype(F32)
    own_high = jnp.max(logits, axis=1)
    own_lse = own_high + jnp.log(jnp.sum(jnp.exp(logits - own_high[:, None]), axis=1))
    own_target = jnp.sum(logits * picked, axis=1)
    notes = jnp.pad(jnp.concatenate([own_lse, own_target], axis=1), ((0, 5), (0, 0)))
    notes = lax.all_to_all(
        jnp.broadcast_to(notes[None], (chip_count,) + notes.shape), chips, 0, 0
    )
    chip_lse = notes[:, :3, :query_total]
    high = jnp.max(chip_lse, axis=0)
    all_lse = high + jnp.log(jnp.sum(jnp.exp(chip_lse - high), axis=0))
    target = jnp.sum(notes[:, :3, query_total:], axis=0)
    losses = jnp.sum(all_lse - target, axis=0).reshape(chip_count, half_queries)
    grad_logits = (jnp.exp(logits - all_lse[:, None]) - picked) / LOSS_TEMP
    coefficient = (
        lax.dot_general(
            grad_logits.reshape(3 * NDOC, query_total),
            group,
            (((1,), (1,)), ((), ())),
            precision=FULL_PRECISION,
        )
        / sums
    )
    query_grad, doc_grad = pool_back(cuts, query_span, queries, row_embed, seg_row, coefficient)
    grad_blocks = lax.all_to_all(
        query_grad.reshape(chip_count, half_span, proj_width), chips, 0, 0
    )
    own_query_grad = jnp.sum(grad_blocks.astype(F32), axis=0)
    row_grad = jnp.concatenate([jnp.zeros((query_span, proj_width), F32), doc_grad], axis=0)
    row_grad = lax.dynamic_update_slice_in_dim(row_grad, own_query_grad, c * half_span, 0)
    grad_embed = rows_of(row_grad, own_start, share) + swap(
        rows_of(row_grad, other_start, share), "c"
    )

    proj_low = w_proj
    grad_embed_low = grad_embed.astype(BF)
    grad_embed_rest = (grad_embed - grad_embed_low.astype(F32)).astype(BF)
    grad_result = own_cot.astype(F32) + (
        contract_cols(grad_embed_low, proj_low) + contract_cols(grad_embed_rest, proj_low)
    )
    proj_grad = contract_rows(result_low, grad_embed_low) + contract_rows(
        result_low, grad_embed_rest
    )
    gain_two = jnp.sum(grad_result * unit_two, axis=0)
    shift_two = jnp.sum(grad_result, axis=0)
    grad_second = norm_backward(grad_result, unit_two, rstd_two, second_norm[0])
    grad_ffn = grad_second.astype(BF)
    down_bias = jnp.sum(grad_ffn.astype(F32), axis=0)
    other_ffn = swap(grad_ffn, "c")
    grad_ffn_all = jnp.concatenate([grad_ffn, other_ffn], axis=0)
    down_blocks = blocks_of(grad_ffn_all, activation)
    down_moved = exchange(*sum_moves(down_blocks, x, y))
    grad_up = (dot(grad_ffn_all, full_down) * slope.astype(F32)).astype(BF)
    up_bias = jnp.sum(grad_up.astype(F32), axis=0)
    up_blocks = blocks_of(normed_all, tie(grad_up, *down_moved))
    full_up = full_mid[:, :up_wide]
    grad_normed = (
        row_sum(lambda which: grad_up[which * share : (which + 1) * share], full_up, True)
        + grad_second
    )
    gain_one = jnp.sum(grad_normed * unit_one, axis=0)
    shift_one = jnp.sum(grad_normed, axis=0)
    grad_first = norm_backward(grad_normed, unit_one, rstd_one, gains[0])
    grad_attn = grad_first.astype(BF)
    out_bias = jnp.sum(grad_attn.astype(F32), axis=0)
    other_attn = swap(grad_attn, "c")
    grad_attn_all = jnp.where(
        c == 0,
        jnp.concatenate([grad_attn, other_attn], axis=0),
        jnp.concatenate([other_attn, grad_attn], axis=0),
    )
    grad_mixed = dot(grad_attn_all, full_out).astype(BF)
    out_blocks = blocks_of(grad_attn_all, mixed)
    down_parts = sum_parts(down_blocks, down_moved, x, y)
    moved = exchange(*line_moves(down_parts, x, y), *sum_moves(up_blocks, x, y))
    down_line = line_of(down_parts, moved, x, y)
    up_parts = sum_parts(up_blocks, moved[2:], x, y)
    grad_mixed, out_blocks, down_line, *up_parts = lax.optimization_barrier(
        (grad_mixed, out_blocks, down_line) + tuple(up_parts)
    )
    moved = exchange(
        near_move(down_line, z), *line_moves(up_parts, x, y), *sum_moves(out_blocks, x, y)
    )
    grads_one, sums_one = attend_back(bounds, 0, qkv, mixed, grad_mixed, lse, spans)
    down_pair = near_sum(down_line, moved[0], z)
    up_line = line_of(up_parts, moved[1:], x, y)
    out_parts = sum_parts(out_blocks, moved[3:], x, y)
    grad_mixed, down_pair, up_line, *out_parts = lax.optimization_barrier(
        (grad_mixed, down_pair, up_line) + tuple(out_parts)
    )
    up_line, y_given, losses = lax.optimization_barrier((up_line, result_low, losses))
    moved = exchange(
        far_move(down_pair, z),
        near_move(up_line, z),
        *line_moves(out_parts, x, y),
        (y_given, CORES, TURN),
    )
    other_losses = swap(losses, "c")
    proj_given, other_losses, grad_mixed = lax.optimization_barrier(
        (rows_of(proj_grad, other_start, share), other_losses, grad_mixed)
    )
    proj_half = rows_of(proj_grad, own_start, share)
    other_proj = swap(proj_given, "c")
    grad_mixed, other_proj = lax.optimization_barrier((grad_mixed, other_proj))
    proj_half = proj_half + other_proj
    losses = jnp.where(c == y, losses, other_losses)
    loss_out = rows_of(losses, 4 * z + 2 * x + c, 1)
    grads_two, sums_two = attend_back(bounds, 1, qkv, mixed, grad_mixed, lse, spans)
    y_out = moved[4]
    down_part = far_sum(down_pair, moved[0], z)
    up_pair = near_sum(up_line, moved[1], z)
    out_line = line_of(out_parts, moved[2:], x, y)
    grads_one, grads_two, down_part, up_pair, out_line = lax.optimization_barrier(
        (grads_one, grads_two, down_part, up_pair, out_line)
    )
    shared = jnp.stack([gain_one, gain_two, shift_one, shift_two, out_bias, down_bias])
    half_sums = jnp.concatenate(
        [
            sums_one[0],
            sums_two[0],
            sums_one[1],
            sums_two[1],
            up_bias,
        ]
    )
    small = jnp.concatenate([shared.reshape(-1, 128), half_sums.reshape(-1, 128), proj_half])

    qkv_blocks = jnp.concatenate(
        [blocks_of(row, grads_one), blocks_of(row, grads_two)], axis=4
    )
    qkv_blocks, up_pair, out_line, down_part, small = lax.optimization_barrier(
        (qkv_blocks, up_pair, out_line, down_part, small)
    )
    moved = exchange(
        *sum_moves(qkv_blocks, x, y),
        far_move(up_pair, z),
        near_move(out_line, z),
        (small.astype(BF), "y", SWAP),
    )
    qkv_parts = sum_parts(qkv_blocks, moved, x, y)
    up_part = far_sum(up_pair, moved[2], z)
    out_pair = near_sum(out_line, moved[3], z)
    small = small + moved[4].astype(F32)

    def input_terms(start):
        return contract_cols(
            rows_of(grads_one, start, share), full_qkv[:, : 3 * quarter]
        ) + contract_cols(rows_of(grads_two, start, share), full_qkv[:, 3 * quarter :])

    other_terms = swap(input_terms(other_start).astype(BF), "c")
    grad_input = (input_terms(own_start) + other_terms.astype(F32) + grad_first).astype(BF)
    moved = exchange(*line_moves(qkv_parts, x, y), far_move(out_pair, z), (small.astype(BF), "x", SWAP))
    qkv_line = line_of(qkv_parts, moved, x, y)
    out_part = far_sum(out_pair, moved[2], z)
    small = small + moved[3].astype(F32)
    moved = exchange(
        near_move(qkv_line, z),
        (small.astype(BF), "z", FAR),
        (tie(grad_input, qkv_line), CORES, TURN),
    )
    qkv_pair = near_sum(qkv_line, moved[0], z)
    small = small + moved[1].astype(F32)
    grad_input = moved[2]
    ffn_part = jnp.concatenate([down_part, up_part], axis=1).astype(BF)
    moved = exchange(
        far_move(qkv_pair, z), (small.astype(BF), "z", NEAR), (tie(ffn_part, qkv_pair), CORES, TURN)
    )
    attn_part = jnp.concatenate([far_sum(qkv_pair, moved[0], z), out_part], axis=1).astype(BF)
    small = small + moved[1].astype(F32)
    ffn_part = moved[2].astype(F32)
    down_part, up_part = ffn_part[:, :up_wide], ffn_part[:, up_wide:]
    attn_part, other_small = exchange((attn_part, CORES, TURN), (small.astype(BF), "c", SWAP))
    attn_part = attn_part.astype(F32)
    other_small = other_small.astype(F32)
    qkv_part, out_part = attn_part[:, : 3 * half_width], attn_part[:, 3 * half_width :]
    shared_rows = 6 * width // 128
    small_rows = small.shape[0] - share
    shared = (small[:shared_rows] + other_small[:shared_rows]).reshape(6, width)
    half_sums = jnp.where(
        c == y, small[shared_rows:small_rows], other_small[shared_rows:small_rows]
    ).reshape(-1)
    proj_sum = pair_up(small[small_rows:], other_small[small_rows:], c, 0).reshape(width, -1)
    qkv_part = qkv_part.reshape(64, 2, 3, quarter).transpose(2, 0, 1, 3).reshape(3, 64, half_width)
    return (
        y_out,
        loss_out,
        grad_input,
        qkv_part,
        half_sums[: 2 * half_width].reshape(2, half_width),
        out_part.T,
        shared[4],
        shared[0:2],
        shared[2:4],
        up_part,
        half_sums[2 * half_width :],
        down_part.T,
        shared[5],
        proj_sum,
    )


IN_SPECS = (
    P("dp", None),
    P(),
    P("dp", "tensor"),
    P(None, "dp", "tensor"),
    P(None, "tensor"),
    P("tensor", "dp"),
    P(),
    P(),
    P(),
    P("dp", "tensor"),
    P("tensor"),
    P("tensor", "dp"),
    P(),
    P(),
    P(("dp", "tensor"), None),
)
OUT_SPECS = (
    P(("dp", "tensor"), None),
    P("dp", "tensor"),
    P(("dp", "tensor"), None),
    P(None, "dp", "tensor"),
    P(None, "tensor"),
    P("tensor", "dp"),
    P(),
    P(),
    P(),
    P("dp", "tensor"),
    P("tensor"),
    P("tensor", "dp"),
    P(),
    P(),
)


def solution(mesh):
    if mesh.devices.shape != (16, 2):
        return jax.shard_map(
            local, mesh=mesh, in_specs=IN_SPECS, out_specs=OUT_SPECS, check_vma=False
        )
    names = {"dp": ("z", "x", "c"), "tensor": ("y",)}

    def respec(spec):
        parts = []
        for entry in spec:
            axes = () if entry is None else entry if isinstance(entry, tuple) else (entry,)
            parts.append(tuple(name for axis in axes for name in names[axis]) or None)
        return P(*parts)

    chips = Mesh(mesh.devices.reshape(4, 2, 2, 2), ("z", "x", "c", "y"))
    return jax.shard_map(
        local_chip,
        mesh=chips,
        in_specs=tuple(respec(spec) for spec in IN_SPECS),
        out_specs=tuple(respec(spec) for spec in OUT_SPECS),
        check_vma=False,
    )
```

```python
from functools import partial

import jax
import jax.numpy as jnp
from jax import lax
from jax.experimental import pallas as pl
from jax.experimental.pallas import tpu as pltpu
from jax.sharding import Mesh, PartitionSpec as P

HEAD_DIM = 64
QLEN = 32
NQ_ROW = 8
NDOC = 8


EPS_NORM = 1e-05
EPS_EMBED = 1e-06
POOL_TEMP = 0.1
LOSS_TEMP = 0.1
FULL_PRECISION = lax.Precision.HIGHEST
MASKED_SCORE = -1e30


def shortened(shard):

    def short(part):
        return part.astype(jnp.bfloat16) if part.dtype == jnp.float32 else part

    return jax.tree.map(short, shard)


def contract_rows(left, right, precision=None):
    return lax.dot_general(
        left,
        right,
        (((0,), (0,)), ((), ())),
        precision=precision,
        preferred_element_type=jnp.float32,
    )


def contract_cols(left, right, precision=None):
    return lax.dot_general(
        left,
        right,
        (((1,), (1,)), ((), ())),
        precision=precision,
        preferred_element_type=jnp.float32,
    )


def norm_forward(value, gain, shift):
    centred = value - jnp.mean(value, axis=1, keepdims=True)
    rstd = lax.rsqrt(jnp.mean(centred * centred, axis=1, keepdims=True) + EPS_NORM)
    unit = centred * rstd
    return (unit * gain + shift, unit, rstd)


def norm_backward(grad, unit, rstd, gain):
    scaled = grad * gain
    return rstd * (
        scaled
        - jnp.mean(scaled, axis=1, keepdims=True)
        - unit * jnp.mean(scaled * unit, axis=1, keepdims=True)
    )


def segments_of(row_lengths, token_count):
    position = jnp.arange(token_count, dtype=jnp.int32)
    query_span = NQ_ROW * QLEN
    ends = jnp.cumsum(row_lengths)
    passed = jnp.sum((position[:, None] - query_span >= ends[None, :]).astype(jnp.int32), axis=1)
    return jnp.where(position < query_span, position // QLEN, NQ_ROW + passed)


def normalize_cut(raw, width):
    part = raw[:, :width]
    scale = lax.rsqrt(jnp.sum(part * part, axis=1, keepdims=True) + EPS_EMBED)
    return (part * scale, part, scale)


def normalize_back(grad, part, scale, full_width):
    result = scale * grad - part * (scale * scale * scale) * jnp.sum(
        part * grad, axis=1, keepdims=True
    )
    return jnp.pad(result, ((0, 0), (0, full_width - grad.shape[1])))


def masked_scores(query_block, key_rows, block_segments, segments):
    scores = jnp.einsum(
        "qhd,khd->hqk", query_block, key_rows, preferred_element_type=jnp.float32
    ) * HEAD_DIM ** (-0.5)
    return jnp.where((block_segments[:, None] == segments[None, :])[None], scores, MASKED_SCORE)


def attend_forward(query_rows, key_rows, value_rows, segments, block_rows):
    token_count = query_rows.shape[0]

    def one_block(block_start):
        query_block = lax.dynamic_slice_in_dim(query_rows, block_start, block_rows, 0)
        block_segments = lax.dynamic_slice_in_dim(segments, block_start, block_rows, 0)
        scores = masked_scores(query_block, key_rows, block_segments, segments)
        highest = jnp.max(scores, axis=2, keepdims=True)
        expo = jnp.exp(scores - highest)
        totals = jnp.sum(expo, axis=2, keepdims=True)
        weights = (expo / totals).astype(jnp.bfloat16)
        mixed = jnp.einsum("hqk,khd->qhd", weights, value_rows, preferred_element_type=jnp.float32)
        return (mixed.astype(jnp.bfloat16), (highest + jnp.log(totals))[:, :, 0])

    starts = jnp.arange(token_count // block_rows, dtype=jnp.int32) * block_rows
    mixed, log_totals = lax.map(one_block, starts)
    return (mixed.reshape(token_count, -1), log_totals)


def attend_backward(query_rows, key_rows, value_rows, segments, log_totals, grad_mixed, block_rows):
    token_count, local_heads, head_size = query_rows.shape
    scale = HEAD_DIM ** (-0.5)
    grad_heads = grad_mixed.reshape(token_count, local_heads, head_size)

    def one_block(carried, inputs):
        grad_keys, grad_values = carried
        block_start, block_lse = inputs
        query_block = lax.dynamic_slice_in_dim(query_rows, block_start, block_rows, 0)
        grad_block = lax.dynamic_slice_in_dim(grad_heads, block_start, block_rows, 0)
        block_segments = lax.dynamic_slice_in_dim(segments, block_start, block_rows, 0)
        scores = masked_scores(query_block, key_rows, block_segments, segments)
        probs = jnp.exp(scores - block_lse[:, :, None])
        grad_probs = jnp.einsum(
            "qhd,khd->hqk", grad_block, value_rows, preferred_element_type=jnp.float32
        )
        inner = jnp.sum(probs * grad_probs, axis=2, keepdims=True)
        grad_scores = (probs * (grad_probs - inner)).astype(jnp.bfloat16)
        grad_query = (
            jnp.einsum("hqk,khd->qhd", grad_scores, key_rows, preferred_element_type=jnp.float32)
            * scale
        )
        grad_keys = (
            grad_keys
            + jnp.einsum(
                "hqk,qhd->khd", grad_scores, query_block, preferred_element_type=jnp.float32
            )
            * scale
        )
        grad_values = grad_values + jnp.einsum(
            "hqk,qhd->khd",
            probs.astype(jnp.bfloat16),
            grad_block,
            preferred_element_type=jnp.float32,
        )
        return ((grad_keys, grad_values), grad_query)

    starts = jnp.arange(token_count // block_rows, dtype=jnp.int32) * block_rows
    zero_rows = jnp.zeros(key_rows.shape, jnp.float32)
    (grad_keys, grad_values), grad_queries = lax.scan(
        one_block, (zero_rows, zero_rows), (starts, log_totals)
    )
    flat_width = local_heads * head_size
    return (
        grad_queries.reshape(token_count, flat_width),
        grad_keys.reshape(token_count, flat_width),
        grad_values.reshape(token_count, flat_width),
    )


def local(
    tokens,
    lengths,
    pairing,
    w_qkv,
    b_qv,
    w_out,
    b_out,
    ln_gain,
    ln_bias,
    w_up,
    b_up,
    w_down,
    b_down,
    w_proj,
    cot,
):
    tensor_count = lax.axis_size("tensor")
    tensor_index = lax.axis_index("tensor")
    data_index = lax.axis_index("dp")
    token_count = tokens.shape[0]
    share_rows = token_count // tensor_count
    block_rows = min(512, token_count)
    own_start = tensor_index * share_rows
    full_qkv, full_out, full_up, full_down = (
        lax.all_gather(w_qkv, "dp", axis=1, tiled=True),
        lax.all_gather(w_out, "dp", axis=1, tiled=True),
        lax.all_gather(w_up, "dp", axis=0, tiled=True),
        lax.all_gather(w_down, "dp", axis=1, tiled=True),
    )
    head_width = full_qkv.shape[2]
    local_heads = head_width // HEAD_DIM
    row_lengths = lax.dynamic_index_in_dim(lengths, data_index, 0, keepdims=False)
    segments = segments_of(row_lengths, token_count)
    projected = jnp.einsum("td,kdw->ktw", tokens, full_qkv, preferred_element_type=jnp.float32)
    qv_bias = b_qv.astype(jnp.float32)
    query_rows = (
        (projected[0] + qv_bias[0]).astype(jnp.bfloat16).reshape(token_count, local_heads, HEAD_DIM)
    )
    key_rows = projected[1].astype(jnp.bfloat16).reshape(token_count, local_heads, HEAD_DIM)
    value_rows = (
        (projected[2] + qv_bias[1]).astype(jnp.bfloat16).reshape(token_count, local_heads, HEAD_DIM)
    )
    mixed, log_totals = attend_forward(query_rows, key_rows, value_rows, segments, block_rows)
    attn_terms = jnp.dot(mixed, full_out, preferred_element_type=jnp.float32)
    attn_sum = lax.psum_scatter(
        attn_terms.astype(jnp.bfloat16), "tensor", scatter_dimension=0, tiled=True
    ).astype(jnp.float32)
    own_tokens = lax.dynamic_slice_in_dim(tokens, own_start, share_rows, 0).astype(jnp.float32)
    gains = ln_gain.astype(jnp.float32)
    shifts = ln_bias.astype(jnp.float32)
    normed, unit_one, rstd_one = norm_forward(
        own_tokens + attn_sum + b_out.astype(jnp.float32), gains[0], shifts[0]
    )
    normed_all = lax.all_gather(normed.astype(jnp.bfloat16), "tensor", axis=0, tiled=True)
    up_value = jnp.dot(normed_all, full_up, preferred_element_type=jnp.float32) + b_up.astype(
        jnp.float32
    )
    activation = jax.nn.gelu(up_value, approximate=False).astype(jnp.bfloat16)
    ffn_terms = jnp.dot(activation, full_down, preferred_element_type=jnp.float32)
    ffn_sum = lax.psum_scatter(
        ffn_terms.astype(jnp.bfloat16), "tensor", scatter_dimension=0, tiled=True
    ).astype(jnp.float32)
    result, unit_two, rstd_two = norm_forward(
        normed + ffn_sum + b_down.astype(jnp.float32), gains[1], shifts[1]
    )
    result_low = result.astype(jnp.bfloat16)
    embed = jnp.dot(result_low, w_proj, preferred_element_type=jnp.float32).astype(jnp.bfloat16)
    embed_all = lax.all_gather(embed, ("dp", "tensor"), axis=0, tiled=True)
    row_count = lengths.shape[0]
    proj_width = w_proj.shape[1]
    widths = (proj_width, 3 * proj_width // 4, proj_width // 2)
    per_device = pairing.shape[1]
    query_count = per_device * QLEN
    query_span = NQ_ROW * QLEN
    emb_rows = embed_all.reshape(row_count, token_count, proj_width)
    my_row = lax.dynamic_index_in_dim(emb_rows, data_index, 0, keepdims=False)
    query_raw = lax.dynamic_slice_in_dim(my_row, tensor_index * query_count, query_count, 0).astype(
        jnp.float32
    )
    query_levels = [normalize_cut(query_raw, width) for width in widths]
    query_units = [level_parts[0].astype(jnp.bfloat16) for level_parts in query_levels]
    doc_numbers = jnp.arange(NDOC, dtype=jnp.int32)

    def row_pool(carried, inputs):
        row_emb, lengths_row = inputs
        row_hot = (
            segments_of(lengths_row, token_count)[:, None] == NQ_ROW + doc_numbers[None, :]
        ).astype(jnp.float32)
        row_raw = row_emb.astype(jnp.float32)
        pooled_list = []
        sums_list = []
        for width, query_unit in zip(widths, query_units):
            doc_unit = normalize_cut(row_raw, width)[0].astype(jnp.bfloat16)
            expo = jnp.exp(contract_cols(query_unit, doc_unit) / POOL_TEMP)
            sums = jnp.dot(expo, row_hot, precision=FULL_PRECISION)
            pooled = POOL_TEMP * jnp.log(sums / lengths_row.astype(jnp.float32))
            pooled_list.append(jnp.sum(pooled.reshape(per_device, QLEN, NDOC), axis=1))
            sums_list.append(sums)
        return (carried, (jnp.stack(pooled_list), jnp.stack(sums_list)))

    _, (row_scores, row_sums) = lax.scan(row_pool, 0, (emb_rows, lengths))
    logits = (
        jnp.transpose(row_scores, (2, 1, 0, 3)).reshape(per_device, 3, row_count * NDOC) / LOSS_TEMP
    )
    own_pairs = pairing[0]
    target = jnp.take_along_axis(
        logits, jnp.broadcast_to(own_pairs[:, None, None], (per_device, 3, 1)), axis=2
    )[:, :, 0]
    loss_out = jnp.sum(jax.nn.logsumexp(logits, axis=2) - target, axis=1).reshape(1, per_device)
    picked = (
        jnp.arange(row_count * NDOC, dtype=jnp.int32)[None, None, :] == own_pairs[:, None, None]
    ).astype(jnp.float32)
    grad_logits = (jax.nn.softmax(logits, axis=2) - picked) / LOSS_TEMP
    grad_rows = jnp.transpose(grad_logits.reshape(per_device, 3, row_count, NDOC), (2, 1, 0, 3))
    coefficient = jnp.repeat(grad_rows, QLEN, axis=2) / row_sums

    def row_back(carried, inputs):
        row_emb, lengths_row, row_coef = inputs
        row_hot = (
            segments_of(lengths_row, token_count)[:, None] == NQ_ROW + doc_numbers[None, :]
        ).astype(jnp.float32)
        row_raw = row_emb.astype(jnp.float32)
        new_carried = []
        row_grad = jnp.zeros((token_count, proj_width), jnp.float32)
        for level_index in range(3):
            width = widths[level_index]
            doc_unit_f, doc_part, doc_scale = normalize_cut(row_raw, width)
            doc_unit = doc_unit_f.astype(jnp.bfloat16)
            expo = jnp.exp(contract_cols(query_units[level_index], doc_unit) / POOL_TEMP)
            spread = contract_cols(row_coef[level_index], row_hot, FULL_PRECISION)
            grad_sim = (expo * spread).astype(jnp.bfloat16)
            new_carried.append(
                carried[level_index]
                + jnp.dot(grad_sim, doc_unit, preferred_element_type=jnp.float32)
            )
        return (tuple(new_carried), row_grad)

    zero_query = tuple((jnp.zeros((query_count, width), jnp.float32) for width in widths))
    query_grads, doc_grads = lax.scan(row_back, zero_query, (emb_rows, lengths, coefficient))
    grad_query = jnp.zeros((query_count, proj_width), jnp.float32)
    for level_index in range(3):
        level_parts = query_levels[level_index]
        grad_query = grad_query + normalize_back(
            query_grads[level_index], level_parts[1], level_parts[2], proj_width
        )
    coef_mine = jnp.transpose(coefficient, (2, 1, 0, 3)).reshape(query_count, 3, row_count * NDOC)
    coef_all, grad_query_all = (
        lax.all_gather(shortened(coef_mine), ("dp", "tensor"), axis=0, tiled=True).astype(
            coef_mine.dtype
        ),
        lax.all_gather(
            grad_query.astype(jnp.bfloat16), ("dp", "tensor"), axis=0, tiled=True
        ).astype(grad_query.dtype),
    )
    own_raw = embed.astype(jnp.float32)
    own_segments = lax.dynamic_slice_in_dim(segments, own_start, share_rows, 0)
    own_docs = jnp.where(own_segments >= NQ_ROW, data_index * NDOC + own_segments - NQ_ROW, -1)
    own_hot = (own_docs[:, None] == jnp.arange(row_count * NDOC, dtype=jnp.int32)[None, :]).astype(
        jnp.float32
    )
    queries_all = (
        emb_rows[:, :query_span].reshape(row_count * query_span, proj_width).astype(jnp.float32)
    )
    grad_embed = jnp.zeros((share_rows, proj_width), jnp.float32)
    for level_index in range(3):
        width = widths[level_index]
        query_unit_all = normalize_cut(queries_all, width)[0].astype(jnp.bfloat16)
        doc_unit_f, doc_part, doc_scale = normalize_cut(own_raw, width)
        expo = jnp.exp(contract_cols(query_unit_all, doc_unit_f.astype(jnp.bfloat16)) / POOL_TEMP)
        spread = contract_cols(coef_all[:, level_index], own_hot, FULL_PRECISION)
        grad_sim = (expo * spread).astype(jnp.bfloat16)
        grad_doc = contract_rows(grad_sim, query_unit_all)
        grad_embed = grad_embed + normalize_back(grad_doc, doc_part, doc_scale, proj_width)
    row_query_grads = lax.dynamic_slice_in_dim(
        grad_query_all, data_index * query_span, query_span, 0
    )
    padded = jnp.pad(row_query_grads, ((0, token_count - query_span), (0, 0)))
    grad_embed = grad_embed + lax.dynamic_slice_in_dim(padded, own_start, share_rows, 0)
    proj_float = w_proj.astype(jnp.float32)
    grad_result = cot.astype(jnp.float32) + contract_cols(grad_embed, proj_float, FULL_PRECISION)
    proj_grad = contract_rows(result_low.astype(jnp.float32), grad_embed, FULL_PRECISION)
    gain_two = jnp.sum(grad_result * unit_two, axis=0)
    shift_two = jnp.sum(grad_result, axis=0)
    grad_second = norm_backward(grad_result, unit_two, rstd_two, gains[1])
    grad_ffn = grad_second.astype(jnp.bfloat16)
    down_bias = jnp.sum(grad_ffn.astype(jnp.float32), axis=0)
    grad_ffn_all = lax.all_gather(grad_ffn, "tensor", axis=0, tiled=True)
    grad_act = contract_cols(grad_ffn_all, full_down)
    down_grad = contract_rows(activation, grad_ffn_all)
    _, gelu_pull = jax.vjp(partial(jax.nn.gelu, approximate=False), up_value)
    grad_up = gelu_pull(grad_act)[0].astype(jnp.bfloat16)
    up_bias = jnp.sum(grad_up.astype(jnp.float32), axis=0)
    up_grad = contract_rows(normed_all, grad_up)
    normed_terms = contract_cols(grad_up, full_up)
    grad_normed = (
        lax.psum_scatter(
            normed_terms.astype(jnp.bfloat16), "tensor", scatter_dimension=0, tiled=True
        ).astype(jnp.float32)
        + grad_second
    )
    gain_one = jnp.sum(grad_normed * unit_one, axis=0)
    shift_one = jnp.sum(grad_normed, axis=0)
    grad_first = norm_backward(grad_normed, unit_one, rstd_one, gains[0])
    grad_attn = grad_first.astype(jnp.bfloat16)
    out_bias = jnp.sum(grad_attn.astype(jnp.float32), axis=0)
    grad_attn_all = lax.all_gather(grad_attn, "tensor", axis=0, tiled=True)
    out_grad = contract_rows(mixed, grad_attn_all)
    grad_mixed = contract_cols(grad_attn_all, full_out).astype(jnp.bfloat16)
    grad_q, grad_k, grad_v = attend_backward(
        query_rows, key_rows, value_rows, segments, log_totals, grad_mixed, block_rows
    )
    stacked_grads = jnp.stack(
        [grad_q.astype(jnp.bfloat16), grad_k.astype(jnp.bfloat16), grad_v.astype(jnp.bfloat16)]
    )
    qkv_grad = jnp.einsum("td,ktw->kdw", tokens, stacked_grads, preferred_element_type=jnp.float32)
    input_terms = jnp.einsum(
        "ktw,kdw->td", stacked_grads, full_qkv, preferred_element_type=jnp.float32
    )
    grad_input = (
        lax.psum_scatter(
            input_terms.astype(jnp.bfloat16), "tensor", scatter_dimension=0, tiled=True
        ).astype(jnp.float32)
        + grad_first
    )
    qv_grad = jnp.stack(
        [
            jnp.sum(stacked_grads[0].astype(jnp.float32), axis=0),
            jnp.sum(stacked_grads[2].astype(jnp.float32), axis=0),
        ]
    )
    qkv_part, out_part, up_part, down_part = (
        lax.psum_scatter(
            qkv_grad.astype(jnp.bfloat16), "dp", scatter_dimension=1, tiled=True
        ).astype(jnp.float32),
        lax.psum_scatter(
            out_grad.astype(jnp.bfloat16), "dp", scatter_dimension=1, tiled=True
        ).astype(jnp.float32),
        lax.psum_scatter(
            up_grad.astype(jnp.bfloat16), "dp", scatter_dimension=0, tiled=True
        ).astype(jnp.float32),
        lax.psum_scatter(
            down_grad.astype(jnp.bfloat16), "dp", scatter_dimension=1, tiled=True
        ).astype(jnp.float32),
    )
    gain_sum, shift_sum, out_bias_sum, down_bias_sum, proj_sum = lax.psum(
        (
            jnp.stack([gain_one, gain_two]),
            jnp.stack([shift_one, shift_two]),
            out_bias,
            down_bias,
            proj_grad,
        ),
        ("dp", "tensor"),
    )
    qv_sum, up_bias_sum = lax.psum((qv_grad, up_bias), "dp")
    return (
        result_low,
        loss_out,
        grad_input.astype(jnp.bfloat16),
        qkv_part,
        qv_sum,
        out_part,
        out_bias_sum,
        gain_sum,
        shift_sum,
        up_part,
        up_bias_sum,
        down_part,
        down_bias_sum,
        proj_sum,
    )


SWAP = [(0, 1), (1, 0)]
TURN = [(0, 0), (1, 2), (2, 1), (3, 3)]
FAR = [(0, 3), (3, 0), (1, 2), (2, 1)]
NEAR = [(0, 1), (1, 0), (2, 3), (3, 2)]
BF = jnp.bfloat16
F32 = jnp.float32


def dot(left, right):
    return jnp.dot(left, right, preferred_element_type=F32)


CORES = ("c", "y")


def tie(value, *others):
    return lax.optimization_barrier((value,) + others)[0]


def tie_all(values, *others):
    return lax.optimization_barrier(tuple(values) + others)[: len(values)]


def exchange(*moves):
    return lax.optimization_barrier(
        tuple(lax.ppermute(value, axis, steps) for value, axis, steps in moves)
    )


def swap(value, axis):
    return lax.ppermute(value, axis, SWAP)


def pair_up(first, second, own_index, axis):
    return jnp.where(
        own_index == 0, jnp.stack([first, second], axis), jnp.stack([second, first], axis)
    )


def far_pair(value, far, z):
    return jnp.where(z < 2, jnp.stack([value, far]), jnp.stack([far, value]))


def whole_line(pair, other, z):
    return jnp.where(
        (z == 0) | (z == 3),
        jnp.stack([pair[0], other[0], other[1], pair[1]]),
        jnp.stack([other[0], pair[0], pair[1], other[1]]),
    )


def first_moves(line):
    half = line.shape[1] // 2
    return ((line[:, :half], "x", SWAP), (line[:, half:], "y", SWAP))


def first_parts(line, moved, x, y):
    half = line.shape[1] // 2
    return (pair_up(line[:, :half], moved[0], x, 1), pair_up(line[:, half:], moved[1], y, 1))


def last_moves(parts):
    return ((parts[0], "y", SWAP), (parts[1], "x", SWAP))


def full_rows(parts, moved, x, y):
    low = pair_up(parts[0], moved[0], y, 2)
    high = pair_up(parts[1], moved[1], x, 1)
    return jnp.concatenate([low, high], axis=3).reshape(-1, low.shape[-1])


def at(blocks, index, axis):
    return lax.dynamic_index_in_dim(blocks, index, axis, keepdims=False)


def side_move(blocks, axis_name, own_index, axis):
    return (at(blocks, 1 - own_index, axis).astype(BF), axis_name, SWAP)


def side_sum(blocks, got, own_index, axis):
    return at(blocks, own_index, axis).astype(F32) + got.astype(F32)


def near_move(line, z):
    ends = (z == 0) | (z == 3)
    outer, inner = jnp.stack([line[0], line[3]]), line[1:3]
    return (jnp.where(ends, inner, outer).astype(BF), "z", NEAR)


def near_sum(line, got, z):
    ends = (z == 0) | (z == 3)
    return jnp.where(ends, jnp.stack([line[0], line[3]]), line[1:3]) + got.astype(F32)


def far_move(pair, z):
    return (jnp.where(z < 2, pair[1], pair[0]).astype(BF), "z", FAR)


def far_sum(pair, got, z):
    return jnp.where(z < 2, pair[0], pair[1]) + got.astype(F32)


def blocks_of(left, right):
    return contract_rows(left, right).astype(BF).reshape(4, 2, 2, 64, right.shape[1])


def sum_moves(blocks, x, y):
    half = blocks.shape[3] // 2
    return (
        side_move(blocks[..., :half, :], "x", x, 1),
        side_move(blocks[..., half:, :], "y", y, 2),
    )


def sum_parts(blocks, moved, x, y):
    half = blocks.shape[3] // 2
    return (
        side_sum(blocks[..., :half, :], moved[0], x, 1),
        side_sum(blocks[..., half:, :], moved[1], y, 2),
    )


def line_moves(parts, x, y):
    return (side_move(parts[0], "y", y, 1), side_move(parts[1], "x", x, 1))


def line_of(parts, moved, x, y):
    return jnp.concatenate(
        [side_sum(parts[0], moved[0], y, 1), side_sum(parts[1], moved[1], x, 1)], axis=1
    )


def tile_bounds(row_lengths, token_count):
    ends = jnp.cumsum(row_lengths)
    span = NQ_ROW * QLEN
    first = jnp.arange(token_count // TILE, dtype=jnp.int32) * TILE - span
    last = first + TILE - 1
    begin = jnp.max(jnp.where(ends[None, :] <= first[:, None], ends[None, :], 0), axis=1)
    end = jnp.min(jnp.where(ends[None, :] > last[:, None], ends[None, :], token_count), axis=1)
    low = jnp.where(first < 0, 0, (begin + span) // TILE)
    high = jnp.where(first < 0, 1, (end + span + TILE - 1) // TILE)
    return jnp.stack([low, high]).astype(jnp.int32)


def token_spans(row_lengths, token_count):
    ends = jnp.cumsum(row_lengths)[:, None]
    span = NQ_ROW * QLEN
    place = jnp.arange(token_count, dtype=jnp.int32)[None, :]
    doc = place - span
    begin = jnp.max(jnp.where(ends <= doc, ends, 0), axis=0) + span
    end = jnp.min(jnp.where(ends > doc, ends, token_count), axis=0) + span
    query = place[0] // QLEN * QLEN
    return jnp.stack(
        [jnp.where(doc[0] < 0, query, begin), jnp.where(doc[0] < 0, query + QLEN, end)]
    ).astype(jnp.int32)


def rows_of(value, start, count):
    return lax.dynamic_slice_in_dim(value, start, count, 0)


TILE = 256
KEYS = 256
NEG = -1e30


def exact(left, right, dims):
    return lax.dot_general(left, right, (dims, ((), ())), preferred_element_type=F32)


def head_masks(value):
    lane = lax.broadcasted_iota(jnp.int32, value.shape, 1)
    zero = jnp.zeros_like(value)
    return (jnp.where(lane < HEAD_DIM, value, zero), jnp.where(lane < HEAD_DIM, zero, value))


def key_shift(step, spans):
    place = step * KEYS + lax.broadcasted_iota(jnp.int32, (KEYS, TILE), 0)
    inside = (place >= spans[0:1, :]) & (place < spans[1:2, :])
    return jnp.where(inside, 0.0, NEG)


def attend_kernel(bounds, own_ref, qkv_ref, spans, out_ref, lse_ref, held):
    block = pl.program_id(0)
    groups = 2
    pairs = out_ref.shape[1] // 128
    per_group = pairs // groups

    def column(pair, part):
        start = ((pair // per_group) * 3 + part) * per_group + pair % per_group
        return slice(start * 128, (start + 1) * 128)

    queries = [head_masks(own_ref[:, column(pair, 0)] * HEAD_DIM**-0.5) for pair in range(pairs)]
    heads = [(pair, head) for pair in range(pairs) for head in range(2)]

    def score(step, highest):
        rows = pl.ds(pl.multiple_of(step * KEYS, KEYS), KEYS)
        shift = key_shift(step, spans)
        fresh = []
        for index, (pair, head) in enumerate(heads):
            keys = qkv_ref[rows, column(pair, 1)]
            scores = exact(keys, queries[pair][head], ((1,), (1,))) + shift
            held[index, rows, :] = scores
            fresh.append(jnp.maximum(highest[index], jnp.max(scores, axis=0, keepdims=True)))
        return tuple(fresh)

    low = jnp.full((1, TILE), NEG, F32)
    highest = lax.fori_loop(bounds[0, block], bounds[1, block], score, (low,) * len(heads))

    def mix(step, carried):
        rows = pl.ds(pl.multiple_of(step * KEYS, KEYS), KEYS)
        fresh = []
        for index, (pair, head) in enumerate(heads):
            values = qkv_ref[rows, column(pair, 2)]
            total, mixed = carried[index]
            expo = jnp.exp(held[index, rows, :] - highest[index])
            product = exact(values, expo.astype(BF), ((0,), (0,)))
            fresh.append(
                (
                    total + jnp.sum(expo, axis=0, keepdims=True),
                    mixed + product[head * HEAD_DIM : (head + 1) * HEAD_DIM],
                )
            )
        return tuple(fresh)

    start = (jnp.zeros((1, TILE), F32), jnp.zeros((HEAD_DIM, TILE), F32))
    parts = lax.fori_loop(bounds[0, block], bounds[1, block], mix, (start,) * len(heads))
    for pair in range(pairs):
        both = [parts[2 * pair + head][1] / parts[2 * pair + head][0] for head in range(2)]
        mixed = jnp.transpose(jnp.concatenate(both, axis=0))
        out_ref[:, pair * 128 : (pair + 1) * 128] = mixed.astype(BF)
    for index in range(len(heads)):
        lse_ref[index : index + 1, :] = highest[index] + jnp.log(parts[index][0])


def attend(bounds, qkv, spans):
    count, wide = qkv.shape
    heads = wide // 3 // HEAD_DIM
    whole = lambda shape: pl.BlockSpec(shape, lambda i: (0, 0))
    return pl.pallas_call(
        attend_kernel,
        grid=(count // TILE,),
        in_specs=[
            pl.BlockSpec(memory_space=pltpu.SMEM),
            pl.BlockSpec((TILE, wide), lambda i: (i, 0)),
            whole((count, wide)),
            pl.BlockSpec((2, TILE), lambda i: (0, i)),
        ],
        out_specs=[
            pl.BlockSpec((TILE, wide // 3), lambda i: (i, 0)),
            pl.BlockSpec((heads, TILE), lambda i: (0, i)),
        ],
        out_shape=[
            jax.ShapeDtypeStruct((count, wide // 3), BF),
            jax.ShapeDtypeStruct((heads, count), F32),
        ],
        scratch_shapes=[pltpu.VMEM((heads, count, TILE), F32)],
        compiler_params=pltpu.CompilerParams(vmem_limit_bytes=40 << 20),
        cost_estimate=pl.CostEstimate(
            flops=4 * heads * count * count * 64,
            transcendentals=heads * count * count // 2,
            bytes_accessed=4 * count * wide * 2,
        ),
    )(bounds, qkv, qkv, spans)


def attend_back_kernel(
    first, bounds, own_ref, qkv_ref, out_ref, grad_ref, lse_ref, spans,
    grads_ref, sums_ref, key_sum, value_sum,
):
    block = pl.program_id(0)
    pairs = out_ref.shape[1] // 128
    heads = [(pair, head) for pair in range(pairs) for head in range(2)]
    cut = lambda index: slice(index * 128, (index + 1) * 128)

    @pl.when(block == 0)
    def _():
        key_sum[...] = jnp.zeros_like(key_sum)
        value_sum[...] = jnp.zeros_like(value_sum)
        sums_ref[...] = jnp.zeros_like(sums_ref)

    queries = [head_masks(own_ref[:, cut(pair)] * HEAD_DIM**-0.5) for pair in range(pairs)]
    grads = [head_masks(grad_ref[:, cut(pair)]) for pair in range(pairs)]
    picks = head_masks(jnp.ones((8, 128), BF))
    inner = []
    for pair, head in heads:
        product = grad_ref[:, cut(pair)].astype(F32) * out_ref[:, cut(pair)].astype(F32)
        high = product.astype(BF)
        rest = (product - high.astype(F32)).astype(BF)
        inner.append(
            (
                exact(picks[head], high, ((1,), (1,))) + exact(picks[head], rest, ((1,), (1,)))
            )[0:1]
        )
    lse = [lse_ref[first + index : first + index + 1, :] for index in range(len(heads))]

    def step_of(step, carried):
        rows = pl.ds(pl.multiple_of(step * KEYS, KEYS), KEYS)
        shift = key_shift(step, spans)
        fresh = []
        for pair in range(pairs):
            keys = qkv_ref[rows, cut(pairs + pair)]
            values = qkv_ref[rows, cut(2 * pairs + pair)]
            key_add = jnp.zeros((KEYS, 128), F32)
            value_add = jnp.zeros((KEYS, 128), F32)
            for head in range(2):
                index = 2 * pair + head
                scores = exact(keys, queries[pair][head], ((1,), (1,))) + shift
                probs = jnp.exp(scores - lse[index])
                grad_probs = exact(values, grads[pair][head], ((1,), (1,)))
                grad_scores = (probs * (grad_probs - inner[index])).astype(BF)
                value_add = value_add + exact(probs.astype(BF), grads[pair][head], ((1,), (0,)))
                key_add = key_add + exact(grad_scores, queries[pair][head], ((1,), (0,)))
                product = exact(keys, grad_scores, ((0,), (0,)))
                fresh.append(carried[index] + product[head * HEAD_DIM : (head + 1) * HEAD_DIM])
            key_sum[rows, cut(pair)] += key_add
            value_sum[rows, cut(pair)] += value_add
        return tuple(fresh)

    start = jnp.zeros((HEAD_DIM, TILE), F32)
    parts = lax.fori_loop(bounds[0, block], bounds[1, block], step_of, (start,) * len(heads))
    own = pl.ds(pl.multiple_of(block * TILE, TILE), TILE)
    for pair in range(pairs):
        grad_query = jnp.concatenate([parts[2 * pair], parts[2 * pair + 1]], axis=0)
        grad_query = jnp.transpose(grad_query * HEAD_DIM**-0.5).astype(BF)
        grads_ref[own, cut(pair)] = grad_query
        sums_ref[0:1, cut(pair)] += jnp.sum(grad_query.astype(F32), axis=0, keepdims=True)

    @pl.when(block == pl.num_programs(0) - 1)
    def _():
        wide = pairs * 128
        grad_value = value_sum[...].astype(BF)
        grads_ref[:, wide : 2 * wide] = key_sum[...].astype(BF)
        grads_ref[:, 2 * wide :] = grad_value
        sums_ref[1:2, :] = jnp.sum(grad_value.astype(F32), axis=0, keepdims=True)


def attend_back(bounds, group, qkv, mixed, grad_mixed, lse, spans):
    count = qkv.shape[0]
    wide = qkv.shape[1] // 2
    heads = wide // 3 // HEAD_DIM
    whole = lambda shape: pl.BlockSpec(shape, lambda i: (0, 0))
    return pl.pallas_call(
        partial(attend_back_kernel, group * heads),
        grid=(count // TILE,),
        in_specs=[
            pl.BlockSpec(memory_space=pltpu.SMEM),
            pl.BlockSpec((TILE, wide), lambda i: (i, group)),
            pl.BlockSpec((count, wide), lambda i: (0, group)),
            pl.BlockSpec((TILE, wide // 3), lambda i: (i, group)),
            pl.BlockSpec((TILE, wide // 3), lambda i: (i, group)),
            pl.BlockSpec((2 * heads, TILE), lambda i: (0, i)),
            pl.BlockSpec((2, TILE), lambda i: (0, i)),
        ],
        out_specs=[whole((count, wide)), whole((8, wide // 3))],
        out_shape=[
            jax.ShapeDtypeStruct((count, wide), BF),
            jax.ShapeDtypeStruct((8, wide // 3), F32),
        ],
        scratch_shapes=[
            pltpu.VMEM((count, wide // 3), F32),
            pltpu.VMEM((count, wide // 3), F32),
        ],
        compiler_params=pltpu.CompilerParams(vmem_limit_bytes=40 << 20),
        cost_estimate=pl.CostEstimate(
            flops=10 * heads * count * count * 64,
            transcendentals=heads * count * count // 2,
            bytes_accessed=8 * count * wide * 2,
        ),
    )(
        bounds, qkv, qkv, mixed, grad_mixed,
        lse, spans,
    )


ERFC = (
    -1.26551223, 1.00002368, 0.37409196, 0.09678418, -0.18628806,
    0.27886807, -1.13520398, 1.48851587, -0.82215223, 0.17087277,
)


def gelu_pair(value):
    size = jnp.abs(value) * 0.5**0.5
    ratio = 1.0 / (1.0 + 0.5 * size)
    series = jnp.full_like(value, ERFC[-1])
    for factor in ERFC[-2::-1]:
        series = series * ratio + factor
    bell = jnp.exp(-size * size)
    tail = 0.5 * ratio * bell * jnp.exp(series)
    phi = jnp.where(value < 0.0, tail, 1.0 - tail)
    return (value * phi, phi + value * bell * 0.3989422804014327)


def expand_kernel(x_ref, w_ref, b_ref, *refs):
    act_ref, slope_ref = refs[-2:]
    rows = 256
    for start in range(0, x_ref.shape[0], rows):
        part = slice(start, start + rows)
        value = exact(x_ref[part, :], w_ref[...], ((1,), (0,))) + b_ref[...]
        active, slope = gelu_pair(value)
        act_ref[part, :] = active.astype(BF)
        slope_ref[part, :] = slope.astype(BF)


def expand(value, weight, shift, first, tiles, filled=()):
    count, depth = value.shape
    width = shift.shape[1]
    tile = 256
    column = lambda rows: pl.BlockSpec((rows, tile), lambda i: (0, first + i))
    return pl.pallas_call(
        expand_kernel,
        grid=(tiles,),
        in_specs=[
            pl.BlockSpec((count, depth), lambda i: (0, 0)),
            column(depth),
            column(1),
        ]
        + [pl.BlockSpec(memory_space=pl.ANY)] * len(filled),
        out_specs=[column(count)] * 2,
        out_shape=[jax.ShapeDtypeStruct((count, width), BF)] * 2,
        input_output_aliases={3: 0, 4: 1} if filled else {},
        compiler_params=pltpu.CompilerParams(vmem_limit_bytes=32 << 20),
        cost_estimate=pl.CostEstimate(
            flops=2 * count * depth * tile * tiles,
            transcendentals=3 * count * tile * tiles,
            bytes_accessed=2 * (count * depth + depth * tile * tiles + 2 * count * tile * tiles),
        ),
    )(value, weight, shift, *filled)


def cut_levels(raw, cuts):
    lane = lax.broadcasted_iota(jnp.int32, raw.shape, 1)
    levels = []
    for cut in cuts:
        part = jnp.where(lane < cut, raw, 0.0)
        scale = lax.rsqrt(jnp.sum(part * part, axis=1, keepdims=True) + EPS_EMBED)
        levels.append(((part * scale).astype(BF), part, scale))
    return levels


def pool_kernel(cuts, span, q_ref, d_ref, seg_ref, out_ref, units, hot):
    @pl.when(pl.program_id(0) == 0)
    def _():
        raw = d_ref[span:, :].astype(F32)
        for level, parts in enumerate(cut_levels(raw, cuts)):
            units[level] = parts[0]
        doc = lax.broadcasted_iota(jnp.int32, hot.shape, 0)
        hot[...] = (seg_ref[:, span:] == NQ_ROW + doc).astype(F32).astype(BF)

    levels = cut_levels(q_ref[...].astype(F32), cuts)
    for level in range(len(cuts)):
        similar = exact(units[level], levels[level][0], ((1,), (1,)))
        expo = jnp.exp(similar * (1.0 / POOL_TEMP))
        high = expo.astype(BF)
        rest = (expo - high.astype(F32)).astype(BF)
        out_ref[level * NDOC : (level + 1) * NDOC, :] = exact(
            hot[...], high, ((1,), (0,))
        ) + exact(hot[...], rest, ((1,), (0,)))


def pool(cuts, span, queries, row_embed, seg_row):
    count, width = queries.shape
    tokens = row_embed.shape[0]
    whole = lambda shape: pl.BlockSpec(shape, lambda i: (0, 0))
    return pl.pallas_call(
        partial(pool_kernel, cuts, span),
        grid=(count // TILE,),
        in_specs=[
            pl.BlockSpec((TILE, width), lambda i: (i, 0)),
            whole((tokens, width)),
            whole((1, tokens)),
        ],
        out_specs=pl.BlockSpec((len(cuts) * NDOC, TILE), lambda i: (0, i)),
        out_shape=jax.ShapeDtypeStruct((len(cuts) * NDOC, count), F32),
        scratch_shapes=[
            pltpu.VMEM((len(cuts), tokens - span, width), BF),
            pltpu.VMEM((NDOC, tokens - span), BF),
        ],
        compiler_params=pltpu.CompilerParams(vmem_limit_bytes=32 << 20),
        cost_estimate=pl.CostEstimate(
            flops=2 * len(cuts) * count * tokens * 256,
            transcendentals=len(cuts) * count * tokens,
            bytes_accessed=2 * (count + tokens) * width,
        ),
    )(queries, row_embed, seg_row)


def level_back(grad, part, scale):
    return scale * grad - part * (scale * scale * scale) * jnp.sum(
        part * grad, axis=1, keepdims=True
    )


def pool_back_kernel(
    cuts, span, q_ref, d_ref, seg_ref, coef_ref, q_out, d_out, units, units_t, hot, sums
):
    step = pl.program_id(0)

    @pl.when(step == 0)
    def _():
        raw = d_ref[span:, :].astype(F32)
        for level, parts in enumerate(cut_levels(raw, cuts)):
            units[level] = parts[0]
            units_t[level] = jnp.transpose(parts[0])
        doc = lax.broadcasted_iota(jnp.int32, hot.shape, 0)
        wanted = NQ_ROW + jnp.where(doc < NDOC, doc, doc - NDOC)
        hot[...] = (seg_ref[:, span:] == wanted).astype(F32).astype(BF)
        sums[...] = jnp.zeros_like(sums)

    levels = cut_levels(q_ref[...].astype(F32), cuts)
    total = jnp.zeros(q_ref.shape, F32)
    for level in range(len(cuts)):
        unit, part, scale = levels[level]
        similar = exact(units[level], unit, ((1,), (1,)))
        coef = coef_ref[level * NDOC : (level + 1) * NDOC, :]
        high = coef.astype(BF).astype(F32)
        both = jnp.concatenate([high, coef - high], axis=0).astype(BF)
        spread = exact(hot[...], both, ((0,), (0,)))
        grad = (jnp.exp(similar * (1.0 / POOL_TEMP)) * spread).astype(BF)
        sums[level] += exact(grad, unit, ((1,), (0,)))
        grad_unit = jnp.transpose(exact(units_t[level], grad, ((1,), (0,))))
        total = total + level_back(grad_unit, part, scale)
    q_out[...] = total.astype(BF)

    @pl.when(step == pl.num_programs(0) - 1)
    def _():
        raw = d_ref[span:, :].astype(F32)
        result = jnp.zeros(raw.shape, F32)
        for level, parts in enumerate(cut_levels(raw, cuts)):
            lane = lax.broadcasted_iota(jnp.int32, raw.shape, 1)
            grad = jnp.where(lane < cuts[level], sums[level], 0.0)
            result = result + level_back(grad, parts[1], parts[2])
        d_out[...] = result


def pool_back(cuts, span, queries, row_embed, seg_row, coef):
    count, width = queries.shape
    tokens = row_embed.shape[0]
    docs = tokens - span
    whole = lambda shape: pl.BlockSpec(shape, lambda i: (0, 0))
    return pl.pallas_call(
        partial(pool_back_kernel, cuts, span),
        grid=(count // TILE,),
        in_specs=[
            pl.BlockSpec((TILE, width), lambda i: (i, 0)),
            whole((tokens, width)),
            whole((1, tokens)),
            pl.BlockSpec((len(cuts) * NDOC, TILE), lambda i: (0, i)),
        ],
        out_specs=[pl.BlockSpec((TILE, width), lambda i: (i, 0)), whole((docs, width))],
        out_shape=[
            jax.ShapeDtypeStruct((count, width), BF),
            jax.ShapeDtypeStruct((docs, width), F32),
        ],
        scratch_shapes=[
            pltpu.VMEM((len(cuts), docs, width), BF),
            pltpu.VMEM((len(cuts), width, docs), BF),
            pltpu.VMEM((2 * NDOC, docs), BF),
            pltpu.VMEM((len(cuts), docs, width), F32),
        ],
        compiler_params=pltpu.CompilerParams(vmem_limit_bytes=32 << 20),
        cost_estimate=pl.CostEstimate(
            flops=2 * len(cuts) * count * docs * 512,
            transcendentals=len(cuts) * count * docs,
            bytes_accessed=4 * (count + tokens) * width,
        ),
    )(queries, row_embed, seg_row, coef)


def local_chip(
    tokens,
    lengths,
    pairing,
    w_qkv,
    b_qv,
    w_out,
    b_out,
    ln_gain,
    ln_bias,
    w_up,
    b_up,
    w_down,
    b_down,
    w_proj,
    cot,
):
    z, x, c, y = (lax.axis_index(name) for name in ("z", "x", "c", "y"))
    chip = 4 * z + 2 * x + y
    token_count, width = tokens.shape
    share = token_count // 2
    own_start, other_start = c * share, (1 - c) * share
    gains, shifts = ln_gain.astype(F32), ln_bias.astype(F32)

    half_width = w_qkv.shape[2]
    up_wide = w_up.shape[1]
    chip_count = lengths.shape[0]
    half_queries = NQ_ROW // 2
    query_total = chip_count * half_queries
    quarter = half_width // 2
    qkv_rows = jnp.concatenate(
        [w_qkv[k][:, g * quarter : (g + 1) * quarter] for g in range(2) for k in range(3)], axis=1
    )
    pair_rows = jnp.pad(pairing.astype(BF), ((0, 63), (0, 128 - half_queries)))
    mid_rows = jnp.concatenate([w_up, w_out.T, pair_rows], axis=1)
    bias = jnp.concatenate([b_qv.reshape(-1), b_up])[None].astype(F32)
    got = exchange(
        (qkv_rows, CORES, TURN), (tokens, "c", SWAP), (bias, "y", SWAP)
    )
    qkv_rows = got[0]
    row = jnp.where(c == y, tokens, got[1])
    bias = jnp.where(c == y, bias, got[2])
    (rest_rows,) = exchange(
        (tie(jnp.concatenate([mid_rows, w_down.T], axis=1), row), CORES, TURN)
    )
    (far,) = exchange((qkv_rows, "z", FAR))
    qkv_pair = far_pair(qkv_rows, far, z)
    mid_wide = mid_rows.shape[1]
    rest_rows = tie(rest_rows, qkv_pair)
    mid_rows, down_rows = rest_rows[:, :mid_wide], rest_rows[:, mid_wide:]
    got = exchange((qkv_pair, "z", NEAR), (mid_rows, "z", FAR))
    qkv_line = whole_line(qkv_pair, got[0], z)
    mid_pair = far_pair(mid_rows, got[1], z)
    got = exchange(*first_moves(qkv_line), (mid_pair, "z", NEAR))
    qkv_parts = first_parts(qkv_line, got, x, y)
    mid_line = whole_line(mid_pair, got[2], z)
    last = last_moves(qkv_parts)
    got = exchange(*last, (tie(down_rows, mid_line), "z", FAR), *first_moves(mid_line))
    full_qkv = full_rows(qkv_parts, got, x, y)
    down_pair = far_pair(down_rows, got[2], z)
    mid_parts = first_parts(mid_line, got[3:], x, y)
    (near,) = exchange((down_pair, "z", NEAR))
    down_line = whole_line(down_pair, near, z)
    got = exchange(*last_moves(mid_parts), *first_moves(down_line))
    full_mid = full_rows(mid_parts, got, x, y)
    down_parts = first_parts(down_line, got[2:], x, y)
    full_out = full_mid[:, up_wide : up_wide + half_width]
    pairs = full_mid[:, up_wide + half_width :].reshape(chip_count, 64, 128)
    pairs = pairs[:, 0, :half_queries].astype(jnp.int32).reshape(1, query_total)
    row_lengths = lax.dynamic_index_in_dim(lengths, chip, 0, keepdims=False)
    segments = segments_of(row_lengths, token_count)
    seg_row, spans = segments[None, :], token_spans(row_lengths, token_count)
    query_span = NQ_ROW * QLEN
    bounds = tile_bounds(row_lengths, token_count)
    no_bias = jnp.zeros((1, quarter), F32)
    qkv_bias = jnp.concatenate(
        [
            part
            for g in range(2)
            for part in (
                bias[:, g * quarter : (g + 1) * quarter],
                no_bias,
                bias[:, half_width + g * quarter : half_width + (g + 1) * quarter],
            )
        ],
        axis=1,
    )
    qkv = (dot(row, full_qkv) + qkv_bias).astype(BF)
    mixed, lse = attend(bounds, tie(qkv, down_line), spans)

    def row_sum(left, weight_t, transposed):
        times = contract_cols if transposed else dot
        theirs = swap(times(left(1), weight_t).astype(BF), "c")
        return times(left(0), weight_t) + theirs.astype(F32)

    def mixed_half(which):
        return rows_of(mixed, other_start if which else own_start, share)

    other_attn = swap(contract_cols(mixed_half(1), full_out).astype(BF), "c")
    other_attn, second_norm = lax.optimization_barrier(
        (other_attn, jnp.stack([gains[1], shifts[1]]))
    )
    second_norm = swap(second_norm, "c")
    second_norm, *down_parts = lax.optimization_barrier((second_norm,) + tuple(down_parts))
    down_got = exchange(*last_moves(down_parts))
    attn_sum = contract_cols(mixed_half(0), full_out) + other_attn.astype(F32)
    own_tokens = rows_of(row, own_start, share).astype(F32)
    normed, unit_one, rstd_one = norm_forward(
        own_tokens + attn_sum + b_out.astype(F32), gains[0], shifts[0]
    )
    normed_low = normed.astype(BF)
    normed_all = jnp.concatenate([normed_low, swap(normed_low, "c")], axis=0)
    activation, slope = expand(
        normed_all, full_mid, bias[:, 2 * half_width :], 0, up_wide // 256
    )
    full_down = full_rows(down_parts, down_got, x, y)
    ffn_sum = row_sum(
        lambda which: activation[which * share : (which + 1) * share], full_down, True
    )
    result, unit_two, rstd_two = norm_forward(
        normed + ffn_sum + b_down.astype(F32), second_norm[0], second_norm[1]
    )
    result_low = result.astype(BF)
    embed = dot(result_low, w_proj).astype(BF)

    other_embed = swap(embed, "c")
    row_embed = jnp.where(
        c == 0,
        jnp.concatenate([embed, other_embed], axis=0),
        jnp.concatenate([other_embed, embed], axis=0),
    )
    half_span = query_span // 2
    own_queries = rows_of(row_embed, c * half_span, half_span)
    chips = ("z", "x", "y")
    queries = lax.all_to_all(
        jnp.broadcast_to(own_queries[None], (chip_count,) + own_queries.shape), chips, 0, 0
    ).reshape(chip_count * half_span, -1)
    queries, own_cot = lax.optimization_barrier((queries, lax.ppermute(cot, CORES, TURN)))
    proj_width = w_proj.shape[1]
    cuts = (proj_width, 3 * proj_width // 4, proj_width // 2)
    sums = pool(cuts, query_span, queries, row_embed, seg_row)
    doc_sizes = jnp.tile(row_lengths.astype(F32), 3)[:, None]
    group = (
        jnp.arange(query_total * QLEN, dtype=jnp.int32)[:, None] // QLEN
        == jnp.arange(query_total, dtype=jnp.int32)[None, :]
    ).astype(F32)
    pooled = POOL_TEMP * jnp.log(sums / doc_sizes)
    logits = jnp.dot(pooled, group, precision=FULL_PRECISION) / LOSS_TEMP
    logits = logits.reshape(3, NDOC, query_total)
    doc_numbers = chip * NDOC + jnp.arange(NDOC, dtype=jnp.int32)
    picked = (doc_numbers[:, None] == pairs).astype(F32)
    own_high = jnp.max(logits, axis=1)
    own_lse = own_high + jnp.log(jnp.sum(jnp.exp(logits - own_high[:, None]), axis=1))
    own_target = jnp.sum(logits * picked, axis=1)
    notes = jnp.pad(jnp.concatenate([own_lse, own_target], axis=1), ((0, 5), (0, 0)))
    notes = lax.all_to_all(
        jnp.broadcast_to(notes[None], (chip_count,) + notes.shape), chips, 0, 0
    )
    chip_lse = notes[:, :3, :query_total]
    high = jnp.max(chip_lse, axis=0)
    all_lse = high + jnp.log(jnp.sum(jnp.exp(chip_lse - high), axis=0))
    target = jnp.sum(notes[:, :3, query_total:], axis=0)
    losses = jnp.sum(all_lse - target, axis=0).reshape(chip_count, half_queries)
    grad_logits = (jnp.exp(logits - all_lse[:, None]) - picked) / LOSS_TEMP
    coefficient = (
        lax.dot_general(
            grad_logits.reshape(3 * NDOC, query_total),
            group,
            (((1,), (1,)), ((), ())),
            precision=FULL_PRECISION,
        )
        / sums
    )
    query_grad, doc_grad = pool_back(cuts, query_span, queries, row_embed, seg_row, coefficient)
    query_grad, y_out = lax.optimization_barrier(
        (query_grad, lax.ppermute(result_low, CORES, TURN))
    )
    grad_blocks = lax.all_to_all(
        query_grad.reshape(chip_count, half_span, proj_width), chips, 0, 0
    )
    own_query_grad = jnp.sum(grad_blocks.astype(F32), axis=0)
    row_grad = jnp.concatenate([jnp.zeros((query_span, proj_width), F32), doc_grad], axis=0)
    row_grad = lax.dynamic_update_slice_in_dim(row_grad, own_query_grad, c * half_span, 0)
    grad_embed = rows_of(row_grad, own_start, share) + swap(
        rows_of(row_grad, other_start, share), "c"
    )

    proj_low = w_proj
    grad_embed_low = grad_embed.astype(BF)
    grad_embed_rest = (grad_embed - grad_embed_low.astype(F32)).astype(BF)
    grad_result = own_cot.astype(F32) + (
        contract_cols(grad_embed_low, proj_low) + contract_cols(grad_embed_rest, proj_low)
    )
    proj_grad = contract_rows(result_low, grad_embed_low) + contract_rows(
        result_low, grad_embed_rest
    )
    gain_two = jnp.sum(grad_result * unit_two, axis=0)
    shift_two = jnp.sum(grad_result, axis=0)
    grad_second = norm_backward(grad_result, unit_two, rstd_two, second_norm[0])
    grad_ffn = grad_second.astype(BF)
    down_bias = jnp.sum(grad_ffn.astype(F32), axis=0)
    other_ffn = swap(grad_ffn, "c")
    grad_ffn_all = jnp.concatenate([grad_ffn, other_ffn], axis=0)
    down_blocks = blocks_of(grad_ffn_all, activation)
    down_moved = exchange(*sum_moves(down_blocks, x, y))
    grad_up = (dot(grad_ffn_all, full_down) * slope.astype(F32)).astype(BF)
    up_bias = jnp.sum(grad_up.astype(F32), axis=0)
    up_blocks = blocks_of(normed_all, tie(grad_up, *down_moved))
    full_up = full_mid[:, :up_wide]
    grad_normed = (
        row_sum(lambda which: grad_up[which * share : (which + 1) * share], full_up, True)
        + grad_second
    )
    gain_one = jnp.sum(grad_normed * unit_one, axis=0)
    shift_one = jnp.sum(grad_normed, axis=0)
    grad_first = norm_backward(grad_normed, unit_one, rstd_one, gains[0])
    grad_attn = grad_first.astype(BF)
    out_bias = jnp.sum(grad_attn.astype(F32), axis=0)
    other_attn = swap(grad_attn, "c")
    grad_attn_all = jnp.where(
        c == 0,
        jnp.concatenate([grad_attn, other_attn], axis=0),
        jnp.concatenate([other_attn, grad_attn], axis=0),
    )
    grad_mixed = dot(grad_attn_all, full_out).astype(BF)
    out_blocks = blocks_of(grad_attn_all, mixed)
    down_parts = sum_parts(down_blocks, down_moved, x, y)
    moved = exchange(*line_moves(down_parts, x, y), *sum_moves(up_blocks, x, y))
    down_line = line_of(down_parts, moved, x, y)
    up_parts = sum_parts(up_blocks, moved[2:], x, y)
    grad_mixed, out_blocks, down_line, *up_parts = lax.optimization_barrier(
        (grad_mixed, out_blocks, down_line) + tuple(up_parts)
    )
    moved = exchange(
        near_move(down_line, z), *line_moves(up_parts, x, y), *sum_moves(out_blocks, x, y)
    )
    grads_one, sums_one = attend_back(bounds, 0, qkv, mixed, grad_mixed, lse, spans)
    down_pair = near_sum(down_line, moved[0], z)
    up_line = line_of(up_parts, moved[1:], x, y)
    out_parts = sum_parts(out_blocks, moved[3:], x, y)
    grad_mixed, down_pair, up_line, *out_parts = lax.optimization_barrier(
        (grad_mixed, down_pair, up_line) + tuple(out_parts)
    )
    up_line, losses = lax.optimization_barrier((up_line, losses))
    moved = exchange(
        far_move(down_pair, z), near_move(up_line, z), *line_moves(out_parts, x, y)
    )
    other_losses = swap(losses, "c")
    proj_given, other_losses, grad_mixed = lax.optimization_barrier(
        (rows_of(proj_grad, other_start, share), other_losses, grad_mixed)
    )
    proj_half = rows_of(proj_grad, own_start, share)
    other_proj = swap(proj_given, "c")
    grad_mixed, other_proj = lax.optimization_barrier((grad_mixed, other_proj))
    proj_half = proj_half + other_proj
    losses = jnp.where(c == y, losses, other_losses)
    loss_out = rows_of(losses, 4 * z + 2 * x + c, 1)
    grads_two, sums_two = attend_back(bounds, 1, qkv, mixed, grad_mixed, lse, spans)
    down_part = far_sum(down_pair, moved[0], z)
    up_pair = near_sum(up_line, moved[1], z)
    out_line = line_of(out_parts, moved[2:], x, y)
    grads_one, grads_two, down_part, up_pair, out_line = lax.optimization_barrier(
        (grads_one, grads_two, down_part, up_pair, out_line)
    )
    shared = jnp.stack([gain_one, gain_two, shift_one, shift_two, out_bias, down_bias])
    half_sums = jnp.concatenate(
        [
            sums_one[0],
            sums_two[0],
            sums_one[1],
            sums_two[1],
            up_bias,
        ]
    )
    small = jnp.concatenate([shared.reshape(-1, 128), half_sums.reshape(-1, 128), proj_half])

    qkv_blocks = jnp.concatenate(
        [blocks_of(row, grads_one), blocks_of(row, grads_two)], axis=4
    )
    qkv_blocks, up_pair, out_line, down_part, small = lax.optimization_barrier(
        (qkv_blocks, up_pair, out_line, down_part, small)
    )
    moved = exchange(
        *sum_moves(qkv_blocks, x, y),
        far_move(up_pair, z),
        near_move(out_line, z),
        (small.astype(BF), "y", SWAP),
    )
    qkv_parts = sum_parts(qkv_blocks, moved, x, y)
    up_part = far_sum(up_pair, moved[2], z)
    out_pair = near_sum(out_line, moved[3], z)
    small = small + moved[4].astype(F32)

    def input_terms(start):
        return contract_cols(
            rows_of(grads_one, start, share), full_qkv[:, : 3 * quarter]
        ) + contract_cols(rows_of(grads_two, start, share), full_qkv[:, 3 * quarter :])

    other_terms = swap(input_terms(other_start).astype(BF), "c")
    grad_input = (input_terms(own_start) + other_terms.astype(F32) + grad_first).astype(BF)
    moved = exchange(*line_moves(qkv_parts, x, y), far_move(out_pair, z), (small.astype(BF), "x", SWAP))
    qkv_line = line_of(qkv_parts, moved, x, y)
    out_part = far_sum(out_pair, moved[2], z)
    small = small + moved[3].astype(F32)
    moved = exchange(
        near_move(qkv_line, z),
        (small.astype(BF), "z", FAR),
        (tie(grad_input, qkv_line), CORES, TURN),
    )
    qkv_pair = near_sum(qkv_line, moved[0], z)
    small = small + moved[1].astype(F32)
    grad_input = moved[2]
    ffn_part = jnp.concatenate([down_part, up_part], axis=1).astype(BF)
    moved = exchange(
        far_move(qkv_pair, z), (small.astype(BF), "z", NEAR), (tie(ffn_part, qkv_pair), CORES, TURN)
    )
    attn_part = jnp.concatenate([far_sum(qkv_pair, moved[0], z), out_part], axis=1).astype(BF)
    small = small + moved[1].astype(F32)
    ffn_part = moved[2].astype(F32)
    down_part, up_part = ffn_part[:, :up_wide], ffn_part[:, up_wide:]
    attn_part, other_small = exchange((attn_part, CORES, TURN), (small.astype(BF), "c", SWAP))
    attn_part = attn_part.astype(F32)
    other_small = other_small.astype(F32)
    qkv_part, out_part = attn_part[:, : 3 * half_width], attn_part[:, 3 * half_width :]
    shared_rows = 6 * width // 128
    small_rows = small.shape[0] - share
    shared = (small[:shared_rows] + other_small[:shared_rows]).reshape(6, width)
    half_sums = jnp.where(
        c == y, small[shared_rows:small_rows], other_small[shared_rows:small_rows]
    ).reshape(-1)
    proj_sum = pair_up(small[small_rows:], other_small[small_rows:], c, 0).reshape(width, -1)
    qkv_part = qkv_part.reshape(64, 2, 3, quarter).transpose(2, 0, 1, 3).reshape(3, 64, half_width)
    return (
        y_out,
        loss_out,
        grad_input,
        qkv_part,
        half_sums[: 2 * half_width].reshape(2, half_width),
        out_part.T,
        shared[4],
        shared[0:2],
        shared[2:4],
        up_part,
        half_sums[2 * half_width :],
        down_part.T,
        shared[5],
        proj_sum,
    )


IN_SPECS = (
    P("dp", None),
    P(),
    P("dp", "tensor"),
    P(None, "dp", "tensor"),
    P(None, "tensor"),
    P("tensor", "dp"),
    P(),
    P(),
    P(),
    P("dp", "tensor"),
    P("tensor"),
    P("tensor", "dp"),
    P(),
    P(),
    P(("dp", "tensor"), None),
)
OUT_SPECS = (
    P(("dp", "tensor"), None),
    P("dp", "tensor"),
    P(("dp", "tensor"), None),
    P(None, "dp", "tensor"),
    P(None, "tensor"),
    P("tensor", "dp"),
    P(),
    P(),
    P(),
    P("dp", "tensor"),
    P("tensor"),
    P("tensor", "dp"),
    P(),
    P(),
)


def solution(mesh):
    if mesh.devices.shape != (16, 2):
        return jax.shard_map(
            local, mesh=mesh, in_specs=IN_SPECS, out_specs=OUT_SPECS, check_vma=False
        )
    names = {"dp": ("z", "x", "c"), "tensor": ("y",)}

    def respec(spec):
        parts = []
        for entry in spec:
            axes = () if entry is None else entry if isinstance(entry, tuple) else (entry,)
            parts.append(tuple(name for axis in axes for name in names[axis]) or None)
        return P(*parts)

    chips = Mesh(mesh.devices.reshape(4, 2, 2, 2), ("z", "x", "c", "y"))
    return jax.shard_map(
        local_chip,
        mesh=chips,
        in_specs=tuple(respec(spec) for spec in IN_SPECS),
        out_specs=tuple(respec(spec) for spec in OUT_SPECS),
        check_vma=False,
    )
```

```python
from functools import partial

import jax
import jax.numpy as jnp
from jax import lax
from jax.experimental import pallas as pl
from jax.experimental.pallas import tpu as pltpu
from jax.sharding import Mesh, PartitionSpec as P

HEAD_DIM = 64
QLEN = 32
NQ_ROW = 8
NDOC = 8


EPS_NORM = 1e-05
EPS_EMBED = 1e-06
POOL_TEMP = 0.1
LOSS_TEMP = 0.1
FULL_PRECISION = lax.Precision.HIGHEST
MASKED_SCORE = -1e30


def shortened(shard):

    def short(part):
        return part.astype(jnp.bfloat16) if part.dtype == jnp.float32 else part

    return jax.tree.map(short, shard)


def contract_rows(left, right, precision=None):
    return lax.dot_general(
        left,
        right,
        (((0,), (0,)), ((), ())),
        precision=precision,
        preferred_element_type=jnp.float32,
    )


def contract_cols(left, right, precision=None):
    return lax.dot_general(
        left,
        right,
        (((1,), (1,)), ((), ())),
        precision=precision,
        preferred_element_type=jnp.float32,
    )


def norm_forward(value, gain, shift):
    centred = value - jnp.mean(value, axis=1, keepdims=True)
    rstd = lax.rsqrt(jnp.mean(centred * centred, axis=1, keepdims=True) + EPS_NORM)
    unit = centred * rstd
    return (unit * gain + shift, unit, rstd)


def norm_backward(grad, unit, rstd, gain):
    scaled = grad * gain
    return rstd * (
        scaled
        - jnp.mean(scaled, axis=1, keepdims=True)
        - unit * jnp.mean(scaled * unit, axis=1, keepdims=True)
    )


def segments_of(row_lengths, token_count):
    position = jnp.arange(token_count, dtype=jnp.int32)
    query_span = NQ_ROW * QLEN
    ends = jnp.cumsum(row_lengths)
    passed = jnp.sum((position[:, None] - query_span >= ends[None, :]).astype(jnp.int32), axis=1)
    return jnp.where(position < query_span, position // QLEN, NQ_ROW + passed)


def normalize_cut(raw, width):
    part = raw[:, :width]
    scale = lax.rsqrt(jnp.sum(part * part, axis=1, keepdims=True) + EPS_EMBED)
    return (part * scale, part, scale)


def normalize_back(grad, part, scale, full_width):
    result = scale * grad - part * (scale * scale * scale) * jnp.sum(
        part * grad, axis=1, keepdims=True
    )
    return jnp.pad(result, ((0, 0), (0, full_width - grad.shape[1])))


def masked_scores(query_block, key_rows, block_segments, segments):
    scores = jnp.einsum(
        "qhd,khd->hqk", query_block, key_rows, preferred_element_type=jnp.float32
    ) * HEAD_DIM ** (-0.5)
    return jnp.where((block_segments[:, None] == segments[None, :])[None], scores, MASKED_SCORE)


def attend_forward(query_rows, key_rows, value_rows, segments, block_rows):
    token_count = query_rows.shape[0]

    def one_block(block_start):
        query_block = lax.dynamic_slice_in_dim(query_rows, block_start, block_rows, 0)
        block_segments = lax.dynamic_slice_in_dim(segments, block_start, block_rows, 0)
        scores = masked_scores(query_block, key_rows, block_segments, segments)
        highest = jnp.max(scores, axis=2, keepdims=True)
        expo = jnp.exp(scores - highest)
        totals = jnp.sum(expo, axis=2, keepdims=True)
        weights = (expo / totals).astype(jnp.bfloat16)
        mixed = jnp.einsum("hqk,khd->qhd", weights, value_rows, preferred_element_type=jnp.float32)
        return (mixed.astype(jnp.bfloat16), (highest + jnp.log(totals))[:, :, 0])

    starts = jnp.arange(token_count // block_rows, dtype=jnp.int32) * block_rows
    mixed, log_totals = lax.map(one_block, starts)
    return (mixed.reshape(token_count, -1), log_totals)


def attend_backward(query_rows, key_rows, value_rows, segments, log_totals, grad_mixed, block_rows):
    token_count, local_heads, head_size = query_rows.shape
    scale = HEAD_DIM ** (-0.5)
    grad_heads = grad_mixed.reshape(token_count, local_heads, head_size)

    def one_block(carried, inputs):
        grad_keys, grad_values = carried
        block_start, block_lse = inputs
        query_block = lax.dynamic_slice_in_dim(query_rows, block_start, block_rows, 0)
        grad_block = lax.dynamic_slice_in_dim(grad_heads, block_start, block_rows, 0)
        block_segments = lax.dynamic_slice_in_dim(segments, block_start, block_rows, 0)
        scores = masked_scores(query_block, key_rows, block_segments, segments)
        probs = jnp.exp(scores - block_lse[:, :, None])
        grad_probs = jnp.einsum(
            "qhd,khd->hqk", grad_block, value_rows, preferred_element_type=jnp.float32
        )
        inner = jnp.sum(probs * grad_probs, axis=2, keepdims=True)
        grad_scores = (probs * (grad_probs - inner)).astype(jnp.bfloat16)
        grad_query = (
            jnp.einsum("hqk,khd->qhd", grad_scores, key_rows, preferred_element_type=jnp.float32)
            * scale
        )
        grad_keys = (
            grad_keys
            + jnp.einsum(
                "hqk,qhd->khd", grad_scores, query_block, preferred_element_type=jnp.float32
            )
            * scale
        )
        grad_values = grad_values + jnp.einsum(
            "hqk,qhd->khd",
            probs.astype(jnp.bfloat16),
            grad_block,
            preferred_element_type=jnp.float32,
        )
        return ((grad_keys, grad_values), grad_query)

    starts = jnp.arange(token_count // block_rows, dtype=jnp.int32) * block_rows
    zero_rows = jnp.zeros(key_rows.shape, jnp.float32)
    (grad_keys, grad_values), grad_queries = lax.scan(
        one_block, (zero_rows, zero_rows), (starts, log_totals)
    )
    flat_width = local_heads * head_size
    return (
        grad_queries.reshape(token_count, flat_width),
        grad_keys.reshape(token_count, flat_width),
        grad_values.reshape(token_count, flat_width),
    )


def local(
    tokens,
    lengths,
    pairing,
    w_qkv,
    b_qv,
    w_out,
    b_out,
    ln_gain,
    ln_bias,
    w_up,
    b_up,
    w_down,
    b_down,
    w_proj,
    cot,
):
    tensor_count = lax.axis_size("tensor")
    tensor_index = lax.axis_index("tensor")
    data_index = lax.axis_index("dp")
    token_count = tokens.shape[0]
    share_rows = token_count // tensor_count
    block_rows = min(512, token_count)
    own_start = tensor_index * share_rows
    full_qkv, full_out, full_up, full_down = (
        lax.all_gather(w_qkv, "dp", axis=1, tiled=True),
        lax.all_gather(w_out, "dp", axis=1, tiled=True),
        lax.all_gather(w_up, "dp", axis=0, tiled=True),
        lax.all_gather(w_down, "dp", axis=1, tiled=True),
    )
    head_width = full_qkv.shape[2]
    local_heads = head_width // HEAD_DIM
    row_lengths = lax.dynamic_index_in_dim(lengths, data_index, 0, keepdims=False)
    segments = segments_of(row_lengths, token_count)
    projected = jnp.einsum("td,kdw->ktw", tokens, full_qkv, preferred_element_type=jnp.float32)
    qv_bias = b_qv.astype(jnp.float32)
    query_rows = (
        (projected[0] + qv_bias[0]).astype(jnp.bfloat16).reshape(token_count, local_heads, HEAD_DIM)
    )
    key_rows = projected[1].astype(jnp.bfloat16).reshape(token_count, local_heads, HEAD_DIM)
    value_rows = (
        (projected[2] + qv_bias[1]).astype(jnp.bfloat16).reshape(token_count, local_heads, HEAD_DIM)
    )
    mixed, log_totals = attend_forward(query_rows, key_rows, value_rows, segments, block_rows)
    attn_terms = jnp.dot(mixed, full_out, preferred_element_type=jnp.float32)
    attn_sum = lax.psum_scatter(
        attn_terms.astype(jnp.bfloat16), "tensor", scatter_dimension=0, tiled=True
    ).astype(jnp.float32)
    own_tokens = lax.dynamic_slice_in_dim(tokens, own_start, share_rows, 0).astype(jnp.float32)
    gains = ln_gain.astype(jnp.float32)
    shifts = ln_bias.astype(jnp.float32)
    normed, unit_one, rstd_one = norm_forward(
        own_tokens + attn_sum + b_out.astype(jnp.float32), gains[0], shifts[0]
    )
    normed_all = lax.all_gather(normed.astype(jnp.bfloat16), "tensor", axis=0, tiled=True)
    up_value = jnp.dot(normed_all, full_up, preferred_element_type=jnp.float32) + b_up.astype(
        jnp.float32
    )
    activation = jax.nn.gelu(up_value, approximate=False).astype(jnp.bfloat16)
    ffn_terms = jnp.dot(activation, full_down, preferred_element_type=jnp.float32)
    ffn_sum = lax.psum_scatter(
        ffn_terms.astype(jnp.bfloat16), "tensor", scatter_dimension=0, tiled=True
    ).astype(jnp.float32)
    result, unit_two, rstd_two = norm_forward(
        normed + ffn_sum + b_down.astype(jnp.float32), gains[1], shifts[1]
    )
    result_low = result.astype(jnp.bfloat16)
    embed = jnp.dot(result_low, w_proj, preferred_element_type=jnp.float32).astype(jnp.bfloat16)
    embed_all = lax.all_gather(embed, ("dp", "tensor"), axis=0, tiled=True)
    row_count = lengths.shape[0]
    proj_width = w_proj.shape[1]
    widths = (proj_width, 3 * proj_width // 4, proj_width // 2)
    per_device = pairing.shape[1]
    query_count = per_device * QLEN
    query_span = NQ_ROW * QLEN
    emb_rows = embed_all.reshape(row_count, token_count, proj_width)
    my_row = lax.dynamic_index_in_dim(emb_rows, data_index, 0, keepdims=False)
    query_raw = lax.dynamic_slice_in_dim(my_row, tensor_index * query_count, query_count, 0).astype(
        jnp.float32
    )
    query_levels = [normalize_cut(query_raw, width) for width in widths]
    query_units = [level_parts[0].astype(jnp.bfloat16) for level_parts in query_levels]
    doc_numbers = jnp.arange(NDOC, dtype=jnp.int32)

    def row_pool(carried, inputs):
        row_emb, lengths_row = inputs
        row_hot = (
            segments_of(lengths_row, token_count)[:, None] == NQ_ROW + doc_numbers[None, :]
        ).astype(jnp.float32)
        row_raw = row_emb.astype(jnp.float32)
        pooled_list = []
        sums_list = []
        for width, query_unit in zip(widths, query_units):
            doc_unit = normalize_cut(row_raw, width)[0].astype(jnp.bfloat16)
            expo = jnp.exp(contract_cols(query_unit, doc_unit) / POOL_TEMP)
            sums = jnp.dot(expo, row_hot, precision=FULL_PRECISION)
            pooled = POOL_TEMP * jnp.log(sums / lengths_row.astype(jnp.float32))
            pooled_list.append(jnp.sum(pooled.reshape(per_device, QLEN, NDOC), axis=1))
            sums_list.append(sums)
        return (carried, (jnp.stack(pooled_list), jnp.stack(sums_list)))

    _, (row_scores, row_sums) = lax.scan(row_pool, 0, (emb_rows, lengths))
    logits = (
        jnp.transpose(row_scores, (2, 1, 0, 3)).reshape(per_device, 3, row_count * NDOC) / LOSS_TEMP
    )
    own_pairs = pairing[0]
    target = jnp.take_along_axis(
        logits, jnp.broadcast_to(own_pairs[:, None, None], (per_device, 3, 1)), axis=2
    )[:, :, 0]
    loss_out = jnp.sum(jax.nn.logsumexp(logits, axis=2) - target, axis=1).reshape(1, per_device)
    picked = (
        jnp.arange(row_count * NDOC, dtype=jnp.int32)[None, None, :] == own_pairs[:, None, None]
    ).astype(jnp.float32)
    grad_logits = (jax.nn.softmax(logits, axis=2) - picked) / LOSS_TEMP
    grad_rows = jnp.transpose(grad_logits.reshape(per_device, 3, row_count, NDOC), (2, 1, 0, 3))
    coefficient = jnp.repeat(grad_rows, QLEN, axis=2) / row_sums

    def row_back(carried, inputs):
        row_emb, lengths_row, row_coef = inputs
        row_hot = (
            segments_of(lengths_row, token_count)[:, None] == NQ_ROW + doc_numbers[None, :]
        ).astype(jnp.float32)
        row_raw = row_emb.astype(jnp.float32)
        new_carried = []
        row_grad = jnp.zeros((token_count, proj_width), jnp.float32)
        for level_index in range(3):
            width = widths[level_index]
            doc_unit_f, doc_part, doc_scale = normalize_cut(row_raw, width)
            doc_unit = doc_unit_f.astype(jnp.bfloat16)
            expo = jnp.exp(contract_cols(query_units[level_index], doc_unit) / POOL_TEMP)
            spread = contract_cols(row_coef[level_index], row_hot, FULL_PRECISION)
            grad_sim = (expo * spread).astype(jnp.bfloat16)
            new_carried.append(
                carried[level_index]
                + jnp.dot(grad_sim, doc_unit, preferred_element_type=jnp.float32)
            )
        return (tuple(new_carried), row_grad)

    zero_query = tuple((jnp.zeros((query_count, width), jnp.float32) for width in widths))
    query_grads, doc_grads = lax.scan(row_back, zero_query, (emb_rows, lengths, coefficient))
    grad_query = jnp.zeros((query_count, proj_width), jnp.float32)
    for level_index in range(3):
        level_parts = query_levels[level_index]
        grad_query = grad_query + normalize_back(
            query_grads[level_index], level_parts[1], level_parts[2], proj_width
        )
    coef_mine = jnp.transpose(coefficient, (2, 1, 0, 3)).reshape(query_count, 3, row_count * NDOC)
    coef_all, grad_query_all = (
        lax.all_gather(shortened(coef_mine), ("dp", "tensor"), axis=0, tiled=True).astype(
            coef_mine.dtype
        ),
        lax.all_gather(
            grad_query.astype(jnp.bfloat16), ("dp", "tensor"), axis=0, tiled=True
        ).astype(grad_query.dtype),
    )
    own_raw = embed.astype(jnp.float32)
    own_segments = lax.dynamic_slice_in_dim(segments, own_start, share_rows, 0)
    own_docs = jnp.where(own_segments >= NQ_ROW, data_index * NDOC + own_segments - NQ_ROW, -1)
    own_hot = (own_docs[:, None] == jnp.arange(row_count * NDOC, dtype=jnp.int32)[None, :]).astype(
        jnp.float32
    )
    queries_all = (
        emb_rows[:, :query_span].reshape(row_count * query_span, proj_width).astype(jnp.float32)
    )
    grad_embed = jnp.zeros((share_rows, proj_width), jnp.float32)
    for level_index in range(3):
        width = widths[level_index]
        query_unit_all = normalize_cut(queries_all, width)[0].astype(jnp.bfloat16)
        doc_unit_f, doc_part, doc_scale = normalize_cut(own_raw, width)
        expo = jnp.exp(contract_cols(query_unit_all, doc_unit_f.astype(jnp.bfloat16)) / POOL_TEMP)
        spread = contract_cols(coef_all[:, level_index], own_hot, FULL_PRECISION)
        grad_sim = (expo * spread).astype(jnp.bfloat16)
        grad_doc = contract_rows(grad_sim, query_unit_all)
        grad_embed = grad_embed + normalize_back(grad_doc, doc_part, doc_scale, proj_width)
    row_query_grads = lax.dynamic_slice_in_dim(
        grad_query_all, data_index * query_span, query_span, 0
    )
    padded = jnp.pad(row_query_grads, ((0, token_count - query_span), (0, 0)))
    grad_embed = grad_embed + lax.dynamic_slice_in_dim(padded, own_start, share_rows, 0)
    proj_float = w_proj.astype(jnp.float32)
    grad_result = cot.astype(jnp.float32) + contract_cols(grad_embed, proj_float, FULL_PRECISION)
    proj_grad = contract_rows(result_low.astype(jnp.float32), grad_embed, FULL_PRECISION)
    gain_two = jnp.sum(grad_result * unit_two, axis=0)
    shift_two = jnp.sum(grad_result, axis=0)
    grad_second = norm_backward(grad_result, unit_two, rstd_two, gains[1])
    grad_ffn = grad_second.astype(jnp.bfloat16)
    down_bias = jnp.sum(grad_ffn.astype(jnp.float32), axis=0)
    grad_ffn_all = lax.all_gather(grad_ffn, "tensor", axis=0, tiled=True)
    grad_act = contract_cols(grad_ffn_all, full_down)
    down_grad = contract_rows(activation, grad_ffn_all)
    _, gelu_pull = jax.vjp(partial(jax.nn.gelu, approximate=False), up_value)
    grad_up = gelu_pull(grad_act)[0].astype(jnp.bfloat16)
    up_bias = jnp.sum(grad_up.astype(jnp.float32), axis=0)
    up_grad = contract_rows(normed_all, grad_up)
    normed_terms = contract_cols(grad_up, full_up)
    grad_normed = (
        lax.psum_scatter(
            normed_terms.astype(jnp.bfloat16), "tensor", scatter_dimension=0, tiled=True
        ).astype(jnp.float32)
        + grad_second
    )
    gain_one = jnp.sum(grad_normed * unit_one, axis=0)
    shift_one = jnp.sum(grad_normed, axis=0)
    grad_first = norm_backward(grad_normed, unit_one, rstd_one, gains[0])
    grad_attn = grad_first.astype(jnp.bfloat16)
    out_bias = jnp.sum(grad_attn.astype(jnp.float32), axis=0)
    grad_attn_all = lax.all_gather(grad_attn, "tensor", axis=0, tiled=True)
    out_grad = contract_rows(mixed, grad_attn_all)
    grad_mixed = contract_cols(grad_attn_all, full_out).astype(jnp.bfloat16)
    grad_q, grad_k, grad_v = attend_backward(
        query_rows, key_rows, value_rows, segments, log_totals, grad_mixed, block_rows
    )
    stacked_grads = jnp.stack(
        [grad_q.astype(jnp.bfloat16), grad_k.astype(jnp.bfloat16), grad_v.astype(jnp.bfloat16)]
    )
    qkv_grad = jnp.einsum("td,ktw->kdw", tokens, stacked_grads, preferred_element_type=jnp.float32)
    input_terms = jnp.einsum(
        "ktw,kdw->td", stacked_grads, full_qkv, preferred_element_type=jnp.float32
    )
    grad_input = (
        lax.psum_scatter(
            input_terms.astype(jnp.bfloat16), "tensor", scatter_dimension=0, tiled=True
        ).astype(jnp.float32)
        + grad_first
    )
    qv_grad = jnp.stack(
        [
            jnp.sum(stacked_grads[0].astype(jnp.float32), axis=0),
            jnp.sum(stacked_grads[2].astype(jnp.float32), axis=0),
        ]
    )
    qkv_part, out_part, up_part, down_part = (
        lax.psum_scatter(
            qkv_grad.astype(jnp.bfloat16), "dp", scatter_dimension=1, tiled=True
        ).astype(jnp.float32),
        lax.psum_scatter(
            out_grad.astype(jnp.bfloat16), "dp", scatter_dimension=1, tiled=True
        ).astype(jnp.float32),
        lax.psum_scatter(
            up_grad.astype(jnp.bfloat16), "dp", scatter_dimension=0, tiled=True
        ).astype(jnp.float32),
        lax.psum_scatter(
            down_grad.astype(jnp.bfloat16), "dp", scatter_dimension=1, tiled=True
        ).astype(jnp.float32),
    )
    gain_sum, shift_sum, out_bias_sum, down_bias_sum, proj_sum = lax.psum(
        (
            jnp.stack([gain_one, gain_two]),
            jnp.stack([shift_one, shift_two]),
            out_bias,
            down_bias,
            proj_grad,
        ),
        ("dp", "tensor"),
    )
    qv_sum, up_bias_sum = lax.psum((qv_grad, up_bias), "dp")
    return (
        result_low,
        loss_out,
        grad_input.astype(jnp.bfloat16),
        qkv_part,
        qv_sum,
        out_part,
        out_bias_sum,
        gain_sum,
        shift_sum,
        up_part,
        up_bias_sum,
        down_part,
        down_bias_sum,
        proj_sum,
    )


SWAP = [(0, 1), (1, 0)]
TURN = [(0, 0), (1, 2), (2, 1), (3, 3)]
FAR = [(0, 3), (3, 0), (1, 2), (2, 1)]
NEAR = [(0, 1), (1, 0), (2, 3), (3, 2)]
BF = jnp.bfloat16
F32 = jnp.float32


def dot(left, right):
    return jnp.dot(left, right, preferred_element_type=F32)


CORES = ("c", "y")


def tie(value, *others):
    return lax.optimization_barrier((value,) + others)[0]


def tie_all(values, *others):
    return lax.optimization_barrier(tuple(values) + others)[: len(values)]


def exchange(*moves):
    return lax.optimization_barrier(
        tuple(lax.ppermute(value, axis, steps) for value, axis, steps in moves)
    )


def swap(value, axis):
    return lax.ppermute(value, axis, SWAP)


def pair_up(first, second, own_index, axis):
    return jnp.where(
        own_index == 0, jnp.stack([first, second], axis), jnp.stack([second, first], axis)
    )


def far_pair(value, far, z):
    return jnp.where(z < 2, jnp.stack([value, far]), jnp.stack([far, value]))


def whole_line(pair, other, z):
    return jnp.where(
        (z == 0) | (z == 3),
        jnp.stack([pair[0], other[0], other[1], pair[1]]),
        jnp.stack([other[0], pair[0], pair[1], other[1]]),
    )


def first_moves(line):
    half = line.shape[1] // 2
    return ((line[:, :half], "x", SWAP), (line[:, half:], "y", SWAP))


def first_parts(line, moved, x, y):
    half = line.shape[1] // 2
    return (pair_up(line[:, :half], moved[0], x, 1), pair_up(line[:, half:], moved[1], y, 1))


def last_moves(parts):
    return ((parts[0], "y", SWAP), (parts[1], "x", SWAP))


def full_rows(parts, moved, x, y):
    low = pair_up(parts[0], moved[0], y, 2)
    high = pair_up(parts[1], moved[1], x, 1)
    return jnp.concatenate([low, high], axis=3).reshape(-1, low.shape[-1])


def at(blocks, index, axis):
    return lax.dynamic_index_in_dim(blocks, index, axis, keepdims=False)


def side_move(blocks, axis_name, own_index, axis):
    return (at(blocks, 1 - own_index, axis).astype(BF), axis_name, SWAP)


def side_sum(blocks, got, own_index, axis):
    return at(blocks, own_index, axis).astype(F32) + got.astype(F32)


def near_move(line, z):
    ends = (z == 0) | (z == 3)
    outer, inner = jnp.stack([line[0], line[3]]), line[1:3]
    return (jnp.where(ends, inner, outer).astype(BF), "z", NEAR)


def near_sum(line, got, z):
    ends = (z == 0) | (z == 3)
    return jnp.where(ends, jnp.stack([line[0], line[3]]), line[1:3]) + got.astype(F32)


def far_move(pair, z):
    return (jnp.where(z < 2, pair[1], pair[0]).astype(BF), "z", FAR)


def far_sum(pair, got, z):
    return jnp.where(z < 2, pair[0], pair[1]) + got.astype(F32)


def blocks_of(left, right):
    return contract_rows(left, right).astype(BF).reshape(4, 2, 2, 64, right.shape[1])


def sum_moves(blocks, x, y):
    half = blocks.shape[3] // 2
    return (
        side_move(blocks[..., :half, :], "x", x, 1),
        side_move(blocks[..., half:, :], "y", y, 2),
    )


def sum_parts(blocks, moved, x, y):
    half = blocks.shape[3] // 2
    return (
        side_sum(blocks[..., :half, :], moved[0], x, 1),
        side_sum(blocks[..., half:, :], moved[1], y, 2),
    )


def line_moves(parts, x, y):
    return (side_move(parts[0], "y", y, 1), side_move(parts[1], "x", x, 1))


def line_of(parts, moved, x, y):
    return jnp.concatenate(
        [side_sum(parts[0], moved[0], y, 1), side_sum(parts[1], moved[1], x, 1)], axis=1
    )


def tile_bounds(row_lengths, token_count):
    ends = jnp.cumsum(row_lengths)
    span = NQ_ROW * QLEN
    first = jnp.arange(token_count // TILE, dtype=jnp.int32) * TILE - span
    last = first + TILE - 1
    begin = jnp.max(jnp.where(ends[None, :] <= first[:, None], ends[None, :], 0), axis=1)
    end = jnp.min(jnp.where(ends[None, :] > last[:, None], ends[None, :], token_count), axis=1)
    low = jnp.where(first < 0, 0, (begin + span) // TILE)
    high = jnp.where(first < 0, 1, (end + span + TILE - 1) // TILE)
    return jnp.stack([low, high]).astype(jnp.int32)


def token_spans(row_lengths, token_count):
    ends = jnp.cumsum(row_lengths)[:, None]
    span = NQ_ROW * QLEN
    place = jnp.arange(token_count, dtype=jnp.int32)[None, :]
    doc = place - span
    begin = jnp.max(jnp.where(ends <= doc, ends, 0), axis=0) + span
    end = jnp.min(jnp.where(ends > doc, ends, token_count), axis=0) + span
    query = place[0] // QLEN * QLEN
    return jnp.stack(
        [jnp.where(doc[0] < 0, query, begin), jnp.where(doc[0] < 0, query + QLEN, end)]
    ).astype(jnp.int32)


def rows_of(value, start, count):
    return lax.dynamic_slice_in_dim(value, start, count, 0)


TILE = 256
KEYS = 256
LOSS_TILE = 512
NEG = -1e30


def exact(left, right, dims):
    return lax.dot_general(left, right, (dims, ((), ())), preferred_element_type=F32)


def head_masks(value):
    lane = lax.broadcasted_iota(jnp.int32, value.shape, 1)
    zero = jnp.zeros_like(value)
    return (jnp.where(lane < HEAD_DIM, value, zero), jnp.where(lane < HEAD_DIM, zero, value))


def key_shift(step, spans):
    place = step * KEYS + lax.broadcasted_iota(jnp.int32, (KEYS, TILE), 0)
    inside = (place >= spans[0:1, :]) & (place < spans[1:2, :])
    return jnp.where(inside, 0.0, NEG)


def attend_kernel(bounds, own_ref, qkv_ref, spans, out_ref, lse_ref, held):
    block = pl.program_id(0)
    groups = 2
    pairs = out_ref.shape[1] // 128
    per_group = pairs // groups

    def column(pair, part):
        start = ((pair // per_group) * 3 + part) * per_group + pair % per_group
        return slice(start * 128, (start + 1) * 128)

    queries = [head_masks(own_ref[:, column(pair, 0)] * HEAD_DIM**-0.5) for pair in range(pairs)]
    heads = [(pair, head) for pair in range(pairs) for head in range(2)]

    def score(step, highest):
        rows = pl.ds(pl.multiple_of(step * KEYS, KEYS), KEYS)
        shift = key_shift(step, spans)
        fresh = []
        for index, (pair, head) in enumerate(heads):
            keys = qkv_ref[rows, column(pair, 1)]
            scores = exact(keys, queries[pair][head], ((1,), (1,))) + shift
            held[index, rows, :] = scores
            fresh.append(jnp.maximum(highest[index], jnp.max(scores, axis=0, keepdims=True)))
        return tuple(fresh)

    low = jnp.full((1, TILE), NEG, F32)
    highest = lax.fori_loop(bounds[0, block], bounds[1, block], score, (low,) * len(heads))

    def mix(step, carried):
        rows = pl.ds(pl.multiple_of(step * KEYS, KEYS), KEYS)
        fresh = []
        for index, (pair, head) in enumerate(heads):
            values = qkv_ref[rows, column(pair, 2)]
            total, mixed = carried[index]
            expo = jnp.exp(held[index, rows, :] - highest[index])
            product = exact(values, expo.astype(BF), ((0,), (0,)))
            fresh.append(
                (
                    total + jnp.sum(expo, axis=0, keepdims=True),
                    mixed + product[head * HEAD_DIM : (head + 1) * HEAD_DIM],
                )
            )
        return tuple(fresh)

    start = (jnp.zeros((1, TILE), F32), jnp.zeros((HEAD_DIM, TILE), F32))
    parts = lax.fori_loop(bounds[0, block], bounds[1, block], mix, (start,) * len(heads))
    for pair in range(pairs):
        both = [parts[2 * pair + head][1] / parts[2 * pair + head][0] for head in range(2)]
        mixed = jnp.transpose(jnp.concatenate(both, axis=0))
        out_ref[:, pair * 128 : (pair + 1) * 128] = mixed.astype(BF)
    for index in range(len(heads)):
        lse_ref[index : index + 1, :] = highest[index] + jnp.log(parts[index][0])


def attend(bounds, qkv, spans):
    count, wide = qkv.shape
    heads = wide // 3 // HEAD_DIM
    whole = lambda shape: pl.BlockSpec(shape, lambda i: (0, 0))
    return pl.pallas_call(
        attend_kernel,
        grid=(count // TILE,),
        in_specs=[
            pl.BlockSpec(memory_space=pltpu.SMEM),
            pl.BlockSpec((TILE, wide), lambda i: (i, 0)),
            whole((count, wide)),
            pl.BlockSpec((2, TILE), lambda i: (0, i)),
        ],
        out_specs=[
            pl.BlockSpec((TILE, wide // 3), lambda i: (i, 0)),
            pl.BlockSpec((heads, TILE), lambda i: (0, i)),
        ],
        out_shape=[
            jax.ShapeDtypeStruct((count, wide // 3), BF),
            jax.ShapeDtypeStruct((heads, count), F32),
        ],
        scratch_shapes=[pltpu.VMEM((heads, count, TILE), F32)],
        compiler_params=pltpu.CompilerParams(vmem_limit_bytes=40 << 20),
        cost_estimate=pl.CostEstimate(
            flops=4 * heads * count * count * 64,
            transcendentals=heads * count * count // 2,
            bytes_accessed=4 * count * wide * 2,
        ),
    )(bounds, qkv, qkv, spans)


def attend_back_kernel(
    first, bounds, own_ref, qkv_ref, out_ref, grad_ref, lse_ref, spans,
    grads_ref, sums_ref, key_sum, value_sum,
):
    block = pl.program_id(0)
    pairs = out_ref.shape[1] // 128
    heads = [(pair, head) for pair in range(pairs) for head in range(2)]
    cut = lambda index: slice(index * 128, (index + 1) * 128)

    @pl.when(block == 0)
    def _():
        key_sum[...] = jnp.zeros_like(key_sum)
        value_sum[...] = jnp.zeros_like(value_sum)
        sums_ref[...] = jnp.zeros_like(sums_ref)

    queries = [head_masks(own_ref[:, cut(pair)] * HEAD_DIM**-0.5) for pair in range(pairs)]
    grads = [head_masks(grad_ref[:, cut(pair)]) for pair in range(pairs)]
    picks = head_masks(jnp.ones((8, 128), BF))
    inner = []
    for pair, head in heads:
        product = grad_ref[:, cut(pair)].astype(F32) * out_ref[:, cut(pair)].astype(F32)
        high = product.astype(BF)
        rest = (product - high.astype(F32)).astype(BF)
        inner.append(
            (
                exact(picks[head], high, ((1,), (1,))) + exact(picks[head], rest, ((1,), (1,)))
            )[0:1]
        )
    lse = [lse_ref[first + index : first + index + 1, :] for index in range(len(heads))]

    def step_of(step, carried):
        rows = pl.ds(pl.multiple_of(step * KEYS, KEYS), KEYS)
        shift = key_shift(step, spans)
        fresh = []
        for pair in range(pairs):
            keys = qkv_ref[rows, cut(pairs + pair)]
            values = qkv_ref[rows, cut(2 * pairs + pair)]
            key_add = jnp.zeros((KEYS, 128), F32)
            value_add = jnp.zeros((KEYS, 128), F32)
            for head in range(2):
                index = 2 * pair + head
                scores = exact(keys, queries[pair][head], ((1,), (1,))) + shift
                probs = jnp.exp(scores - lse[index])
                grad_probs = exact(values, grads[pair][head], ((1,), (1,)))
                grad_scores = (probs * (grad_probs - inner[index])).astype(BF)
                value_add = value_add + exact(probs.astype(BF), grads[pair][head], ((1,), (0,)))
                key_add = key_add + exact(grad_scores, queries[pair][head], ((1,), (0,)))
                product = exact(keys, grad_scores, ((0,), (0,)))
                fresh.append(carried[index] + product[head * HEAD_DIM : (head + 1) * HEAD_DIM])
            key_sum[rows, cut(pair)] += key_add
            value_sum[rows, cut(pair)] += value_add
        return tuple(fresh)

    start = jnp.zeros((HEAD_DIM, TILE), F32)
    parts = lax.fori_loop(bounds[0, block], bounds[1, block], step_of, (start,) * len(heads))
    own = pl.ds(pl.multiple_of(block * TILE, TILE), TILE)
    for pair in range(pairs):
        grad_query = jnp.concatenate([parts[2 * pair], parts[2 * pair + 1]], axis=0)
        grad_query = jnp.transpose(grad_query * HEAD_DIM**-0.5).astype(BF)
        grads_ref[own, cut(pair)] = grad_query
        sums_ref[0:1, cut(pair)] += jnp.sum(grad_query.astype(F32), axis=0, keepdims=True)

    @pl.when(block == pl.num_programs(0) - 1)
    def _():
        wide = pairs * 128
        grad_value = value_sum[...].astype(BF)
        grads_ref[:, wide : 2 * wide] = key_sum[...].astype(BF)
        grads_ref[:, 2 * wide :] = grad_value
        sums_ref[1:2, :] = jnp.sum(grad_value.astype(F32), axis=0, keepdims=True)


def attend_back(bounds, group, qkv, mixed, grad_mixed, lse, spans):
    count = qkv.shape[0]
    wide = qkv.shape[1] // 2
    heads = wide // 3 // HEAD_DIM
    whole = lambda shape: pl.BlockSpec(shape, lambda i: (0, 0))
    return pl.pallas_call(
        partial(attend_back_kernel, group * heads),
        grid=(count // TILE,),
        in_specs=[
            pl.BlockSpec(memory_space=pltpu.SMEM),
            pl.BlockSpec((TILE, wide), lambda i: (i, group)),
            pl.BlockSpec((count, wide), lambda i: (0, group)),
            pl.BlockSpec((TILE, wide // 3), lambda i: (i, group)),
            pl.BlockSpec((TILE, wide // 3), lambda i: (i, group)),
            pl.BlockSpec((2 * heads, TILE), lambda i: (0, i)),
            pl.BlockSpec((2, TILE), lambda i: (0, i)),
        ],
        out_specs=[whole((count, wide)), whole((8, wide // 3))],
        out_shape=[
            jax.ShapeDtypeStruct((count, wide), BF),
            jax.ShapeDtypeStruct((8, wide // 3), F32),
        ],
        scratch_shapes=[
            pltpu.VMEM((count, wide // 3), F32),
            pltpu.VMEM((count, wide // 3), F32),
        ],
        compiler_params=pltpu.CompilerParams(vmem_limit_bytes=40 << 20),
        cost_estimate=pl.CostEstimate(
            flops=10 * heads * count * count * 64,
            transcendentals=heads * count * count // 2,
            bytes_accessed=8 * count * wide * 2,
        ),
    )(
        bounds, qkv, qkv, mixed, grad_mixed,
        lse, spans,
    )


ERFC = (
    -1.26551223, 1.00002368, 0.37409196, 0.09678418, -0.18628806,
    0.27886807, -1.13520398, 1.48851587, -0.82215223, 0.17087277,
)


def gelu_pair(value):
    size = jnp.abs(value) * 0.5**0.5
    ratio = 1.0 / (1.0 + 0.5 * size)
    series = jnp.full_like(value, ERFC[-1])
    for factor in ERFC[-2::-1]:
        series = series * ratio + factor
    bell = jnp.exp(-size * size)
    tail = 0.5 * ratio * bell * jnp.exp(series)
    phi = jnp.where(value < 0.0, tail, 1.0 - tail)
    return (value * phi, phi + value * bell * 0.3989422804014327)


def expand_kernel(x_ref, w_ref, b_ref, *refs):
    act_ref, slope_ref = refs[-2:]
    rows = 128
    for start in range(0, x_ref.shape[0], rows):
        part = slice(start, start + rows)
        value = exact(x_ref[part, :], w_ref[...], ((1,), (0,))) + b_ref[...]
        active, slope = gelu_pair(value)
        act_ref[part, :] = active.astype(BF)
        slope_ref[part, :] = slope.astype(BF)


def expand(value, weight, shift, first, tiles, filled=()):
    count, depth = value.shape
    width = shift.shape[1]
    tile = 256
    column = lambda rows: pl.BlockSpec((rows, tile), lambda i: (0, first + i))
    return pl.pallas_call(
        expand_kernel,
        grid=(tiles,),
        in_specs=[
            pl.BlockSpec((count, depth), lambda i: (0, 0)),
            column(depth),
            column(1),
        ]
        + [pl.BlockSpec(memory_space=pl.ANY)] * len(filled),
        out_specs=[column(count)] * 2,
        out_shape=[jax.ShapeDtypeStruct((count, width), BF)] * 2,
        input_output_aliases={3: 0, 4: 1} if filled else {},
        compiler_params=pltpu.CompilerParams(vmem_limit_bytes=32 << 20),
        cost_estimate=pl.CostEstimate(
            flops=2 * count * depth * tile * tiles,
            transcendentals=3 * count * tile * tiles,
            bytes_accessed=2 * (count * depth + depth * tile * tiles + 2 * count * tile * tiles),
        ),
    )(value, weight, shift, *filled)


def cut_levels(raw, cuts):
    lane = lax.broadcasted_iota(jnp.int32, raw.shape, 1)
    levels = []
    for cut in cuts:
        part = jnp.where(lane < cut, raw, 0.0)
        scale = lax.rsqrt(jnp.sum(part * part, axis=1, keepdims=True) + EPS_EMBED)
        levels.append(((part * scale).astype(BF), part, scale))
    return levels


def pool_kernel(cuts, span, q_ref, d_ref, seg_ref, out_ref, units, hot):
    @pl.when(pl.program_id(0) == 0)
    def _():
        raw = d_ref[span:, :].astype(F32)
        for level, parts in enumerate(cut_levels(raw, cuts)):
            units[level] = parts[0]
        doc = lax.broadcasted_iota(jnp.int32, hot.shape, 0)
        hot[...] = (seg_ref[:, span:] == NQ_ROW + doc).astype(F32).astype(BF)

    levels = cut_levels(q_ref[...].astype(F32), cuts)
    for level in range(len(cuts)):
        similar = exact(units[level], levels[level][0], ((1,), (1,)))
        expo = jnp.exp(similar * (1.0 / POOL_TEMP))
        high = expo.astype(BF)
        rest = (expo - high.astype(F32)).astype(BF)
        out_ref[level * NDOC : (level + 1) * NDOC, :] = exact(
            hot[...], high, ((1,), (0,))
        ) + exact(hot[...], rest, ((1,), (0,)))


def pool(cuts, span, queries, row_embed, seg_row):
    count, width = queries.shape
    tokens = row_embed.shape[0]
    whole = lambda shape: pl.BlockSpec(shape, lambda i: (0, 0))
    return pl.pallas_call(
        partial(pool_kernel, cuts, span),
        grid=(count // LOSS_TILE,),
        in_specs=[
            pl.BlockSpec((LOSS_TILE, width), lambda i: (i, 0)),
            whole((tokens, width)),
            whole((1, tokens)),
        ],
        out_specs=pl.BlockSpec((len(cuts) * NDOC, LOSS_TILE), lambda i: (0, i)),
        out_shape=jax.ShapeDtypeStruct((len(cuts) * NDOC, count), F32),
        scratch_shapes=[
            pltpu.VMEM((len(cuts), tokens - span, width), BF),
            pltpu.VMEM((NDOC, tokens - span), BF),
        ],
        compiler_params=pltpu.CompilerParams(vmem_limit_bytes=32 << 20),
        cost_estimate=pl.CostEstimate(
            flops=2 * len(cuts) * count * tokens * 256,
            transcendentals=len(cuts) * count * tokens,
            bytes_accessed=2 * (count + tokens) * width,
        ),
    )(queries, row_embed, seg_row)


def level_back(grad, part, scale):
    return scale * grad - part * (scale * scale * scale) * jnp.sum(
        part * grad, axis=1, keepdims=True
    )


def pool_back_kernel(
    cuts, span, q_ref, d_ref, seg_ref, coef_ref, q_out, d_out, units, units_t, hot, sums
):
    step = pl.program_id(0)

    @pl.when(step == 0)
    def _():
        raw = d_ref[span:, :].astype(F32)
        for level, parts in enumerate(cut_levels(raw, cuts)):
            units[level] = parts[0]
            units_t[level] = jnp.transpose(parts[0])
        doc = lax.broadcasted_iota(jnp.int32, hot.shape, 0)
        wanted = NQ_ROW + jnp.where(doc < NDOC, doc, doc - NDOC)
        hot[...] = (seg_ref[:, span:] == wanted).astype(F32).astype(BF)
        sums[...] = jnp.zeros_like(sums)

    levels = cut_levels(q_ref[...].astype(F32), cuts)
    total = jnp.zeros(q_ref.shape, F32)
    for level in range(len(cuts)):
        unit, part, scale = levels[level]
        similar = exact(units[level], unit, ((1,), (1,)))
        coef = coef_ref[level * NDOC : (level + 1) * NDOC, :]
        high = coef.astype(BF).astype(F32)
        both = jnp.concatenate([high, coef - high], axis=0).astype(BF)
        spread = exact(hot[...], both, ((0,), (0,)))
        grad = (jnp.exp(similar * (1.0 / POOL_TEMP)) * spread).astype(BF)
        sums[level] += exact(grad, unit, ((1,), (0,)))
        grad_unit = jnp.transpose(exact(units_t[level], grad, ((1,), (0,))))
        total = total + level_back(grad_unit, part, scale)
    q_out[...] = total.astype(BF)

    @pl.when(step == pl.num_programs(0) - 1)
    def _():
        raw = d_ref[span:, :].astype(F32)
        result = jnp.zeros(raw.shape, F32)
        for level, parts in enumerate(cut_levels(raw, cuts)):
            lane = lax.broadcasted_iota(jnp.int32, raw.shape, 1)
            grad = jnp.where(lane < cuts[level], sums[level], 0.0)
            result = result + level_back(grad, parts[1], parts[2])
        d_out[...] = result


def pool_back(cuts, span, queries, row_embed, seg_row, coef):
    count, width = queries.shape
    tokens = row_embed.shape[0]
    docs = tokens - span
    whole = lambda shape: pl.BlockSpec(shape, lambda i: (0, 0))
    return pl.pallas_call(
        partial(pool_back_kernel, cuts, span),
        grid=(count // LOSS_TILE,),
        in_specs=[
            pl.BlockSpec((LOSS_TILE, width), lambda i: (i, 0)),
            whole((tokens, width)),
            whole((1, tokens)),
            pl.BlockSpec((len(cuts) * NDOC, LOSS_TILE), lambda i: (0, i)),
        ],
        out_specs=[pl.BlockSpec((LOSS_TILE, width), lambda i: (i, 0)), whole((docs, width))],
        out_shape=[
            jax.ShapeDtypeStruct((count, width), BF),
            jax.ShapeDtypeStruct((docs, width), F32),
        ],
        scratch_shapes=[
            pltpu.VMEM((len(cuts), docs, width), BF),
            pltpu.VMEM((len(cuts), width, docs), BF),
            pltpu.VMEM((2 * NDOC, docs), BF),
            pltpu.VMEM((len(cuts), docs, width), F32),
        ],
        compiler_params=pltpu.CompilerParams(vmem_limit_bytes=32 << 20),
        cost_estimate=pl.CostEstimate(
            flops=2 * len(cuts) * count * docs * 512,
            transcendentals=len(cuts) * count * docs,
            bytes_accessed=4 * (count + tokens) * width,
        ),
    )(queries, row_embed, seg_row, coef)


def local_chip(
    tokens,
    lengths,
    pairing,
    w_qkv,
    b_qv,
    w_out,
    b_out,
    ln_gain,
    ln_bias,
    w_up,
    b_up,
    w_down,
    b_down,
    w_proj,
    cot,
):
    z, x, c, y = (lax.axis_index(name) for name in ("z", "x", "c", "y"))
    chip = 4 * z + 2 * x + y
    token_count, width = tokens.shape
    share = token_count // 2
    own_start, other_start = c * share, (1 - c) * share
    gains, shifts = ln_gain.astype(F32), ln_bias.astype(F32)

    half_width = w_qkv.shape[2]
    up_wide = w_up.shape[1]
    chip_count = lengths.shape[0]
    half_queries = NQ_ROW // 2
    query_total = chip_count * half_queries
    quarter = half_width // 2
    qkv_rows = jnp.concatenate(
        [w_qkv[k][:, g * quarter : (g + 1) * quarter] for g in range(2) for k in range(3)], axis=1
    )
    pair_rows = jnp.pad(pairing.astype(BF), ((0, 63), (0, 128 - half_queries)))
    qkv_rows = jnp.concatenate([qkv_rows, w_out.T], axis=1)
    mid_rows = jnp.concatenate([w_up, pair_rows], axis=1)
    bias = jnp.concatenate([b_qv.reshape(-1), b_up])[None].astype(F32)
    got = exchange(
        (qkv_rows, CORES, TURN), (tokens, "c", SWAP), (bias, "y", SWAP)
    )
    qkv_rows = got[0]
    row = jnp.where(c == y, tokens, got[1])
    bias = jnp.where(c == y, bias, got[2])
    (rest_rows,) = exchange(
        (tie(jnp.concatenate([mid_rows, w_down.T], axis=1), row), CORES, TURN)
    )
    (far,) = exchange((qkv_rows, "z", FAR))
    qkv_pair = far_pair(qkv_rows, far, z)
    mid_wide = mid_rows.shape[1]
    rest_rows = tie(rest_rows, qkv_pair)
    mid_rows, down_rows = rest_rows[:, :mid_wide], rest_rows[:, mid_wide:]
    got = exchange((qkv_pair, "z", NEAR), (mid_rows, "z", FAR))
    qkv_line = whole_line(qkv_pair, got[0], z)
    mid_pair = far_pair(mid_rows, got[1], z)
    got = exchange(*first_moves(qkv_line), (mid_pair, "z", NEAR))
    qkv_parts = first_parts(qkv_line, got, x, y)
    mid_line = whole_line(mid_pair, got[2], z)
    last = last_moves(qkv_parts)
    got = exchange(*last, (tie(down_rows, mid_line), "z", FAR), *first_moves(mid_line))
    full_qkv = full_rows(qkv_parts, got, x, y)
    down_pair = far_pair(down_rows, got[2], z)
    mid_parts = first_parts(mid_line, got[3:], x, y)
    (near,) = exchange((down_pair, "z", NEAR))
    down_line = whole_line(down_pair, near, z)
    full_qkv, full_out = full_qkv[:, : 3 * half_width], full_qkv[:, 3 * half_width :]
    row_lengths = lax.dynamic_index_in_dim(lengths, chip, 0, keepdims=False)
    segments = segments_of(row_lengths, token_count)
    seg_row, spans = segments[None, :], token_spans(row_lengths, token_count)
    query_span = NQ_ROW * QLEN
    bounds = tile_bounds(row_lengths, token_count)
    no_bias = jnp.zeros((1, quarter), F32)
    qkv_bias = jnp.concatenate(
        [
            part
            for g in range(2)
            for part in (
                bias[:, g * quarter : (g + 1) * quarter],
                no_bias,
                bias[:, half_width + g * quarter : half_width + (g + 1) * quarter],
            )
        ],
        axis=1,
    )
    qkv = (dot(row, full_qkv) + qkv_bias).astype(BF)
    down_line, qkv, first_norm = lax.optimization_barrier(
        (down_line, qkv, jnp.stack([gains[0], shifts[0]]))
    )
    first_norm = swap(first_norm, "c")
    first_norm, qkv = lax.optimization_barrier((first_norm, qkv))
    full_mid = full_rows(mid_parts, exchange(*last_moves(mid_parts)), x, y)
    down_parts = first_parts(down_line, exchange(*first_moves(down_line)), x, y)
    pairs = full_mid[:, up_wide:].reshape(chip_count, 64, 128)
    pairs = pairs[:, 0, :half_queries].astype(jnp.int32).reshape(1, query_total)
    mixed, lse = attend(bounds, qkv, spans)

    def row_sum(left, weight_t, transposed):
        times = contract_cols if transposed else dot
        theirs = swap(times(left(1), weight_t).astype(BF), "c")
        return times(left(0), weight_t) + theirs.astype(F32)

    def mixed_half(which):
        return rows_of(mixed, other_start if which else own_start, share)

    other_attn = swap(contract_cols(mixed_half(1), full_out).astype(BF), "c")
    attn_sum = contract_cols(mixed_half(0), full_out) + other_attn.astype(F32)
    own_tokens = rows_of(row, own_start, share).astype(F32)
    normed, unit_one, rstd_one = norm_forward(
        own_tokens + attn_sum + b_out.astype(F32), first_norm[0], first_norm[1]
    )
    normed_low = normed.astype(BF)
    other_normed = swap(normed_low, "c")
    other_normed, second_norm = lax.optimization_barrier(
        (other_normed, jnp.stack([gains[1], shifts[1]]))
    )
    second_norm = swap(second_norm, "c")
    second_norm, *down_parts = lax.optimization_barrier((second_norm,) + tuple(down_parts))
    down_got = exchange(*last_moves(down_parts))
    normed_all = jnp.concatenate([normed_low, other_normed], axis=0)
    activation, slope = expand(
        normed_all, full_mid, bias[:, 2 * half_width :], 0, up_wide // 256
    )
    full_down = full_rows(down_parts, down_got, x, y)
    ffn_sum = row_sum(
        lambda which: activation[which * share : (which + 1) * share], full_down, True
    )
    result, unit_two, rstd_two = norm_forward(
        normed + ffn_sum + b_down.astype(F32), second_norm[0], second_norm[1]
    )
    result_low = result.astype(BF)
    embed = dot(result_low, w_proj).astype(BF)

    other_embed = swap(embed, "c")
    row_embed = jnp.where(
        c == 0,
        jnp.concatenate([embed, other_embed], axis=0),
        jnp.concatenate([other_embed, embed], axis=0),
    )
    half_span = query_span // 2
    own_queries = rows_of(row_embed, c * half_span, half_span)
    chips = ("z", "x", "y")
    queries = lax.all_to_all(
        jnp.broadcast_to(own_queries[None], (chip_count,) + own_queries.shape), chips, 0, 0
    ).reshape(chip_count * half_span, -1)
    queries, own_cot = lax.optimization_barrier((queries, lax.ppermute(cot, CORES, TURN)))
    proj_width = w_proj.shape[1]
    cuts = (proj_width, 3 * proj_width // 4, proj_width // 2)
    sums = pool(cuts, query_span, queries, row_embed, seg_row)
    doc_sizes = jnp.tile(row_lengths.astype(F32), 3)[:, None]
    group = (
        jnp.arange(query_total * QLEN, dtype=jnp.int32)[:, None] // QLEN
        == jnp.arange(query_total, dtype=jnp.int32)[None, :]
    ).astype(F32)
    pooled = POOL_TEMP * jnp.log(sums / doc_sizes)
    logits = jnp.dot(pooled, group, precision=FULL_PRECISION) / LOSS_TEMP
    logits = logits.reshape(3, NDOC, query_total)
    doc_numbers = chip * NDOC + jnp.arange(NDOC, dtype=jnp.int32)
    picked = (doc_numbers[:, None] == pairs).astype(F32)
    own_high = jnp.max(logits, axis=1)
    own_lse = own_high + jnp.log(jnp.sum(jnp.exp(logits - own_high[:, None]), axis=1))
    own_target = jnp.sum(logits * picked, axis=1)
    notes = jnp.pad(jnp.concatenate([own_lse, own_target], axis=1), ((0, 5), (0, 0)))
    notes = lax.all_to_all(
        jnp.broadcast_to(notes[None], (chip_count,) + notes.shape), chips, 0, 0
    )
    chip_lse = notes[:, :3, :query_total]
    high = jnp.max(chip_lse, axis=0)
    all_lse = high + jnp.log(jnp.sum(jnp.exp(chip_lse - high), axis=0))
    target = jnp.sum(notes[:, :3, query_total:], axis=0)
    losses = jnp.sum(all_lse - target, axis=0).reshape(chip_count, half_queries)
    grad_logits = (jnp.exp(logits - all_lse[:, None]) - picked) / LOSS_TEMP
    coefficient = (
        lax.dot_general(
            grad_logits.reshape(3 * NDOC, query_total),
            group,
            (((1,), (1,)), ((), ())),
            precision=FULL_PRECISION,
        )
        / sums
    )
    query_grad, doc_grad = pool_back(cuts, query_span, queries, row_embed, seg_row, coefficient)
    query_grad, y_out = lax.optimization_barrier(
        (query_grad, lax.ppermute(result_low, CORES, TURN))
    )
    grad_blocks = lax.all_to_all(
        query_grad.reshape(chip_count, half_span, proj_width), chips, 0, 0
    )
    own_query_grad = jnp.sum(grad_blocks.astype(F32), axis=0)
    row_grad = jnp.concatenate([jnp.zeros((query_span, proj_width), F32), doc_grad], axis=0)
    row_grad = lax.dynamic_update_slice_in_dim(row_grad, own_query_grad, c * half_span, 0)
    grad_embed = rows_of(row_grad, own_start, share) + swap(
        rows_of(row_grad, other_start, share), "c"
    )

    proj_low = w_proj
    grad_embed_low = grad_embed.astype(BF)
    grad_embed_rest = (grad_embed - grad_embed_low.astype(F32)).astype(BF)
    grad_result = own_cot.astype(F32) + (
        contract_cols(grad_embed_low, proj_low) + contract_cols(grad_embed_rest, proj_low)
    )
    proj_grad = contract_rows(result_low, grad_embed_low) + contract_rows(
        result_low, grad_embed_rest
    )
    gain_two = jnp.sum(grad_result * unit_two, axis=0)
    shift_two = jnp.sum(grad_result, axis=0)
    grad_second = norm_backward(grad_result, unit_two, rstd_two, second_norm[0])
    grad_ffn = grad_second.astype(BF)
    down_bias = jnp.sum(grad_ffn.astype(F32), axis=0)
    other_ffn = swap(grad_ffn, "c")
    grad_ffn_all = jnp.concatenate([grad_ffn, other_ffn], axis=0)
    down_blocks = blocks_of(grad_ffn_all, activation)
    down_moved = exchange(*sum_moves(down_blocks, x, y))
    grad_up = (dot(grad_ffn_all, full_down) * slope.astype(F32)).astype(BF)
    up_bias = jnp.sum(grad_up.astype(F32), axis=0)
    up_blocks = blocks_of(normed_all, tie(grad_up, *down_moved))
    full_up = full_mid[:, :up_wide]
    grad_normed = (
        row_sum(lambda which: grad_up[which * share : (which + 1) * share], full_up, True)
        + grad_second
    )
    gain_one = jnp.sum(grad_normed * unit_one, axis=0)
    shift_one = jnp.sum(grad_normed, axis=0)
    grad_first = norm_backward(grad_normed, unit_one, rstd_one, first_norm[0])
    grad_attn = grad_first.astype(BF)
    out_bias = jnp.sum(grad_attn.astype(F32), axis=0)
    other_attn = swap(grad_attn, "c")
    grad_attn_all = jnp.where(
        c == 0,
        jnp.concatenate([grad_attn, other_attn], axis=0),
        jnp.concatenate([other_attn, grad_attn], axis=0),
    )
    grad_mixed = dot(grad_attn_all, full_out).astype(BF)
    out_blocks = blocks_of(grad_attn_all, mixed)
    down_parts = sum_parts(down_blocks, down_moved, x, y)
    moved = exchange(*line_moves(down_parts, x, y), *sum_moves(up_blocks, x, y))
    down_line = line_of(down_parts, moved, x, y)
    up_parts = sum_parts(up_blocks, moved[2:], x, y)
    grad_mixed, out_blocks, down_line, *up_parts = lax.optimization_barrier(
        (grad_mixed, out_blocks, down_line) + tuple(up_parts)
    )
    moved = exchange(
        near_move(down_line, z), *line_moves(up_parts, x, y), *sum_moves(out_blocks, x, y)
    )
    grads_one, sums_one = attend_back(bounds, 0, qkv, mixed, grad_mixed, lse, spans)
    down_pair = near_sum(down_line, moved[0], z)
    up_line = line_of(up_parts, moved[1:], x, y)
    out_parts = sum_parts(out_blocks, moved[3:], x, y)
    grad_mixed, down_pair, up_line, *out_parts = lax.optimization_barrier(
        (grad_mixed, down_pair, up_line) + tuple(out_parts)
    )
    up_line, losses = lax.optimization_barrier((up_line, losses))
    moved = exchange(
        far_move(down_pair, z), near_move(up_line, z), *line_moves(out_parts, x, y)
    )
    other_losses = swap(losses, "c")
    proj_given, other_losses, grad_mixed = lax.optimization_barrier(
        (rows_of(proj_grad, other_start, share), other_losses, grad_mixed)
    )
    proj_half = rows_of(proj_grad, own_start, share)
    other_proj = swap(proj_given, "c")
    grad_mixed, other_proj = lax.optimization_barrier((grad_mixed, other_proj))
    proj_half = proj_half + other_proj
    losses = jnp.where(c == y, losses, other_losses)
    loss_out = rows_of(losses, 4 * z + 2 * x + c, 1)
    grads_two, sums_two = attend_back(bounds, 1, qkv, mixed, grad_mixed, lse, spans)
    down_part = far_sum(down_pair, moved[0], z)
    up_pair = near_sum(up_line, moved[1], z)
    out_line = line_of(out_parts, moved[2:], x, y)
    grads_one, grads_two, down_part, up_pair, out_line = lax.optimization_barrier(
        (grads_one, grads_two, down_part, up_pair, out_line)
    )
    shared = jnp.stack([gain_one, gain_two, shift_one, shift_two, out_bias, down_bias])
    half_sums = jnp.concatenate(
        [
            sums_one[0],
            sums_two[0],
            sums_one[1],
            sums_two[1],
            up_bias,
        ]
    )
    small = jnp.concatenate([shared.reshape(-1, 128), half_sums.reshape(-1, 128), proj_half])

    qkv_blocks = jnp.concatenate(
        [blocks_of(row, grads_one), blocks_of(row, grads_two)], axis=4
    )
    qkv_blocks, up_pair, out_line, down_part, small = lax.optimization_barrier(
        (qkv_blocks, up_pair, out_line, down_part, small)
    )
    moved = exchange(
        *sum_moves(qkv_blocks, x, y),
        far_move(up_pair, z),
        near_move(out_line, z),
        (small.astype(BF), "y", SWAP),
    )
    qkv_parts = sum_parts(qkv_blocks, moved, x, y)
    up_part = far_sum(up_pair, moved[2], z)
    out_pair = near_sum(out_line, moved[3], z)
    small = small + moved[4].astype(F32)

    def input_terms(start):
        return contract_cols(
            rows_of(grads_one, start, share), full_qkv[:, : 3 * quarter]
        ) + contract_cols(rows_of(grads_two, start, share), full_qkv[:, 3 * quarter :])

    other_terms = swap(input_terms(other_start).astype(BF), "c")
    grad_input = (input_terms(own_start) + other_terms.astype(F32) + grad_first).astype(BF)
    moved = exchange(*line_moves(qkv_parts, x, y), far_move(out_pair, z), (small.astype(BF), "x", SWAP))
    qkv_line = line_of(qkv_parts, moved, x, y)
    out_part = far_sum(out_pair, moved[2], z)
    small = small + moved[3].astype(F32)
    moved = exchange(
        near_move(qkv_line, z),
        (small.astype(BF), "z", FAR),
        (tie(grad_input, qkv_line), CORES, TURN),
    )
    qkv_pair = near_sum(qkv_line, moved[0], z)
    small = small + moved[1].astype(F32)
    grad_input = moved[2]
    ffn_part = jnp.concatenate([down_part, up_part], axis=1).astype(BF)
    moved = exchange(
        far_move(qkv_pair, z), (small.astype(BF), "z", NEAR), (tie(ffn_part, qkv_pair), CORES, TURN)
    )
    attn_part = jnp.concatenate([far_sum(qkv_pair, moved[0], z), out_part], axis=1).astype(BF)
    small = small + moved[1].astype(F32)
    ffn_part = moved[2].astype(F32)
    down_part, up_part = ffn_part[:, :up_wide], ffn_part[:, up_wide:]
    attn_part, other_small = exchange((attn_part, CORES, TURN), (small.astype(BF), "c", SWAP))
    attn_part = attn_part.astype(F32)
    other_small = other_small.astype(F32)
    qkv_part, out_part = attn_part[:, : 3 * half_width], attn_part[:, 3 * half_width :]
    shared_rows = 6 * width // 128
    small_rows = small.shape[0] - share
    shared = (small[:shared_rows] + other_small[:shared_rows]).reshape(6, width)
    half_sums = jnp.where(
        c == y, small[shared_rows:small_rows], other_small[shared_rows:small_rows]
    ).reshape(-1)
    proj_sum = pair_up(small[small_rows:], other_small[small_rows:], c, 0).reshape(width, -1)
    qkv_part = qkv_part.reshape(64, 2, 3, quarter).transpose(2, 0, 1, 3).reshape(3, 64, half_width)
    return (
        y_out,
        loss_out,
        grad_input,
        qkv_part,
        half_sums[: 2 * half_width].reshape(2, half_width),
        out_part.T,
        shared[4],
        shared[0:2],
        shared[2:4],
        up_part,
        half_sums[2 * half_width :],
        down_part.T,
        shared[5],
        proj_sum,
    )


IN_SPECS = (
    P("dp", None),
    P(),
    P("dp", "tensor"),
    P(None, "dp", "tensor"),
    P(None, "tensor"),
    P("tensor", "dp"),
    P(),
    P(),
    P(),
    P("dp", "tensor"),
    P("tensor"),
    P("tensor", "dp"),
    P(),
    P(),
    P(("dp", "tensor"), None),
)
OUT_SPECS = (
    P(("dp", "tensor"), None),
    P("dp", "tensor"),
    P(("dp", "tensor"), None),
    P(None, "dp", "tensor"),
    P(None, "tensor"),
    P("tensor", "dp"),
    P(),
    P(),
    P(),
    P("dp", "tensor"),
    P("tensor"),
    P("tensor", "dp"),
    P(),
    P(),
)


def solution(mesh):
    if mesh.devices.shape != (16, 2):
        return jax.shard_map(
            local, mesh=mesh, in_specs=IN_SPECS, out_specs=OUT_SPECS, check_vma=False
        )
    names = {"dp": ("z", "x", "c"), "tensor": ("y",)}

    def respec(spec):
        parts = []
        for entry in spec:
            axes = () if entry is None else entry if isinstance(entry, tuple) else (entry,)
            parts.append(tuple(name for axis in axes for name in names[axis]) or None)
        return P(*parts)

    chips = Mesh(mesh.devices.reshape(4, 2, 2, 2), ("z", "x", "c", "y"))
    return jax.shard_map(
        local_chip,
        mesh=chips,
        in_specs=tuple(respec(spec) for spec in IN_SPECS),
        out_specs=tuple(respec(spec) for spec in OUT_SPECS),
        check_vma=False,
    )
```

```python
from functools import partial

import jax
import jax.numpy as jnp
from jax import lax
from jax.experimental import pallas as pl
from jax.experimental.pallas import tpu as pltpu
from jax.sharding import Mesh, PartitionSpec as P

HEAD_DIM = 64
QLEN = 32
NQ_ROW = 8
NDOC = 8


EPS_NORM = 1e-05
EPS_EMBED = 1e-06
POOL_TEMP = 0.1
LOSS_TEMP = 0.1
FULL_PRECISION = lax.Precision.HIGHEST
MASKED_SCORE = -1e30


def shortened(shard):

    def short(part):
        return part.astype(jnp.bfloat16) if part.dtype == jnp.float32 else part

    return jax.tree.map(short, shard)


def contract_rows(left, right, precision=None):
    return lax.dot_general(
        left,
        right,
        (((0,), (0,)), ((), ())),
        precision=precision,
        preferred_element_type=jnp.float32,
    )


def contract_cols(left, right, precision=None):
    return lax.dot_general(
        left,
        right,
        (((1,), (1,)), ((), ())),
        precision=precision,
        preferred_element_type=jnp.float32,
    )


def norm_forward(value, gain, shift):
    centred = value - jnp.mean(value, axis=1, keepdims=True)
    rstd = lax.rsqrt(jnp.mean(centred * centred, axis=1, keepdims=True) + EPS_NORM)
    unit = centred * rstd
    return (unit * gain + shift, unit, rstd)


def norm_backward(grad, unit, rstd, gain):
    scaled = grad * gain
    return rstd * (
        scaled
        - jnp.mean(scaled, axis=1, keepdims=True)
        - unit * jnp.mean(scaled * unit, axis=1, keepdims=True)
    )


def segments_of(row_lengths, token_count):
    position = jnp.arange(token_count, dtype=jnp.int32)
    query_span = NQ_ROW * QLEN
    ends = jnp.cumsum(row_lengths)
    passed = jnp.sum((position[:, None] - query_span >= ends[None, :]).astype(jnp.int32), axis=1)
    return jnp.where(position < query_span, position // QLEN, NQ_ROW + passed)


def normalize_cut(raw, width):
    part = raw[:, :width]
    scale = lax.rsqrt(jnp.sum(part * part, axis=1, keepdims=True) + EPS_EMBED)
    return (part * scale, part, scale)


def normalize_back(grad, part, scale, full_width):
    result = scale * grad - part * (scale * scale * scale) * jnp.sum(
        part * grad, axis=1, keepdims=True
    )
    return jnp.pad(result, ((0, 0), (0, full_width - grad.shape[1])))


def masked_scores(query_block, key_rows, block_segments, segments):
    scores = jnp.einsum(
        "qhd,khd->hqk", query_block, key_rows, preferred_element_type=jnp.float32
    ) * HEAD_DIM ** (-0.5)
    return jnp.where((block_segments[:, None] == segments[None, :])[None], scores, MASKED_SCORE)


def attend_forward(query_rows, key_rows, value_rows, segments, block_rows):
    token_count = query_rows.shape[0]

    def one_block(block_start):
        query_block = lax.dynamic_slice_in_dim(query_rows, block_start, block_rows, 0)
        block_segments = lax.dynamic_slice_in_dim(segments, block_start, block_rows, 0)
        scores = masked_scores(query_block, key_rows, block_segments, segments)
        highest = jnp.max(scores, axis=2, keepdims=True)
        expo = jnp.exp(scores - highest)
        totals = jnp.sum(expo, axis=2, keepdims=True)
        weights = (expo / totals).astype(jnp.bfloat16)
        mixed = jnp.einsum("hqk,khd->qhd", weights, value_rows, preferred_element_type=jnp.float32)
        return (mixed.astype(jnp.bfloat16), (highest + jnp.log(totals))[:, :, 0])

    starts = jnp.arange(token_count // block_rows, dtype=jnp.int32) * block_rows
    mixed, log_totals = lax.map(one_block, starts)
    return (mixed.reshape(token_count, -1), log_totals)


def attend_backward(query_rows, key_rows, value_rows, segments, log_totals, grad_mixed, block_rows):
    token_count, local_heads, head_size = query_rows.shape
    scale = HEAD_DIM ** (-0.5)
    grad_heads = grad_mixed.reshape(token_count, local_heads, head_size)

    def one_block(carried, inputs):
        grad_keys, grad_values = carried
        block_start, block_lse = inputs
        query_block = lax.dynamic_slice_in_dim(query_rows, block_start, block_rows, 0)
        grad_block = lax.dynamic_slice_in_dim(grad_heads, block_start, block_rows, 0)
        block_segments = lax.dynamic_slice_in_dim(segments, block_start, block_rows, 0)
        scores = masked_scores(query_block, key_rows, block_segments, segments)
        probs = jnp.exp(scores - block_lse[:, :, None])
        grad_probs = jnp.einsum(
            "qhd,khd->hqk", grad_block, value_rows, preferred_element_type=jnp.float32
        )
        inner = jnp.sum(probs * grad_probs, axis=2, keepdims=True)
        grad_scores = (probs * (grad_probs - inner)).astype(jnp.bfloat16)
        grad_query = (
            jnp.einsum("hqk,khd->qhd", grad_scores, key_rows, preferred_element_type=jnp.float32)
            * scale
        )
        grad_keys = (
            grad_keys
            + jnp.einsum(
                "hqk,qhd->khd", grad_scores, query_block, preferred_element_type=jnp.float32
            )
            * scale
        )
        grad_values = grad_values + jnp.einsum(
            "hqk,qhd->khd",
            probs.astype(jnp.bfloat16),
            grad_block,
            preferred_element_type=jnp.float32,
        )
        return ((grad_keys, grad_values), grad_query)

    starts = jnp.arange(token_count // block_rows, dtype=jnp.int32) * block_rows
    zero_rows = jnp.zeros(key_rows.shape, jnp.float32)
    (grad_keys, grad_values), grad_queries = lax.scan(
        one_block, (zero_rows, zero_rows), (starts, log_totals)
    )
    flat_width = local_heads * head_size
    return (
        grad_queries.reshape(token_count, flat_width),
        grad_keys.reshape(token_count, flat_width),
        grad_values.reshape(token_count, flat_width),
    )


def local(
    tokens,
    lengths,
    pairing,
    w_qkv,
    b_qv,
    w_out,
    b_out,
    ln_gain,
    ln_bias,
    w_up,
    b_up,
    w_down,
    b_down,
    w_proj,
    cot,
):
    tensor_count = lax.axis_size("tensor")
    tensor_index = lax.axis_index("tensor")
    data_index = lax.axis_index("dp")
    token_count = tokens.shape[0]
    share_rows = token_count // tensor_count
    block_rows = min(512, token_count)
    own_start = tensor_index * share_rows
    full_qkv, full_out, full_up, full_down = (
        lax.all_gather(w_qkv, "dp", axis=1, tiled=True),
        lax.all_gather(w_out, "dp", axis=1, tiled=True),
        lax.all_gather(w_up, "dp", axis=0, tiled=True),
        lax.all_gather(w_down, "dp", axis=1, tiled=True),
    )
    head_width = full_qkv.shape[2]
    local_heads = head_width // HEAD_DIM
    row_lengths = lax.dynamic_index_in_dim(lengths, data_index, 0, keepdims=False)
    segments = segments_of(row_lengths, token_count)
    projected = jnp.einsum("td,kdw->ktw", tokens, full_qkv, preferred_element_type=jnp.float32)
    qv_bias = b_qv.astype(jnp.float32)
    query_rows = (
        (projected[0] + qv_bias[0]).astype(jnp.bfloat16).reshape(token_count, local_heads, HEAD_DIM)
    )
    key_rows = projected[1].astype(jnp.bfloat16).reshape(token_count, local_heads, HEAD_DIM)
    value_rows = (
        (projected[2] + qv_bias[1]).astype(jnp.bfloat16).reshape(token_count, local_heads, HEAD_DIM)
    )
    mixed, log_totals = attend_forward(query_rows, key_rows, value_rows, segments, block_rows)
    attn_terms = jnp.dot(mixed, full_out, preferred_element_type=jnp.float32)
    attn_sum = lax.psum_scatter(
        attn_terms.astype(jnp.bfloat16), "tensor", scatter_dimension=0, tiled=True
    ).astype(jnp.float32)
    own_tokens = lax.dynamic_slice_in_dim(tokens, own_start, share_rows, 0).astype(jnp.float32)
    gains = ln_gain.astype(jnp.float32)
    shifts = ln_bias.astype(jnp.float32)
    normed, unit_one, rstd_one = norm_forward(
        own_tokens + attn_sum + b_out.astype(jnp.float32), gains[0], shifts[0]
    )
    normed_all = lax.all_gather(normed.astype(jnp.bfloat16), "tensor", axis=0, tiled=True)
    up_value = jnp.dot(normed_all, full_up, preferred_element_type=jnp.float32) + b_up.astype(
        jnp.float32
    )
    activation = jax.nn.gelu(up_value, approximate=False).astype(jnp.bfloat16)
    ffn_terms = jnp.dot(activation, full_down, preferred_element_type=jnp.float32)
    ffn_sum = lax.psum_scatter(
        ffn_terms.astype(jnp.bfloat16), "tensor", scatter_dimension=0, tiled=True
    ).astype(jnp.float32)
    result, unit_two, rstd_two = norm_forward(
        normed + ffn_sum + b_down.astype(jnp.float32), gains[1], shifts[1]
    )
    result_low = result.astype(jnp.bfloat16)
    embed = jnp.dot(result_low, w_proj, preferred_element_type=jnp.float32).astype(jnp.bfloat16)
    embed_all = lax.all_gather(embed, ("dp", "tensor"), axis=0, tiled=True)
    row_count = lengths.shape[0]
    proj_width = w_proj.shape[1]
    widths = (proj_width, 3 * proj_width // 4, proj_width // 2)
    per_device = pairing.shape[1]
    query_count = per_device * QLEN
    query_span = NQ_ROW * QLEN
    emb_rows = embed_all.reshape(row_count, token_count, proj_width)
    my_row = lax.dynamic_index_in_dim(emb_rows, data_index, 0, keepdims=False)
    query_raw = lax.dynamic_slice_in_dim(my_row, tensor_index * query_count, query_count, 0).astype(
        jnp.float32
    )
    query_levels = [normalize_cut(query_raw, width) for width in widths]
    query_units = [level_parts[0].astype(jnp.bfloat16) for level_parts in query_levels]
    doc_numbers = jnp.arange(NDOC, dtype=jnp.int32)

    def row_pool(carried, inputs):
        row_emb, lengths_row = inputs
        row_hot = (
            segments_of(lengths_row, token_count)[:, None] == NQ_ROW + doc_numbers[None, :]
        ).astype(jnp.float32)
        row_raw = row_emb.astype(jnp.float32)
        pooled_list = []
        sums_list = []
        for width, query_unit in zip(widths, query_units):
            doc_unit = normalize_cut(row_raw, width)[0].astype(jnp.bfloat16)
            expo = jnp.exp(contract_cols(query_unit, doc_unit) / POOL_TEMP)
            sums = jnp.dot(expo, row_hot, precision=FULL_PRECISION)
            pooled = POOL_TEMP * jnp.log(sums / lengths_row.astype(jnp.float32))
            pooled_list.append(jnp.sum(pooled.reshape(per_device, QLEN, NDOC), axis=1))
            sums_list.append(sums)
        return (carried, (jnp.stack(pooled_list), jnp.stack(sums_list)))

    _, (row_scores, row_sums) = lax.scan(row_pool, 0, (emb_rows, lengths))
    logits = (
        jnp.transpose(row_scores, (2, 1, 0, 3)).reshape(per_device, 3, row_count * NDOC) / LOSS_TEMP
    )
    own_pairs = pairing[0]
    target = jnp.take_along_axis(
        logits, jnp.broadcast_to(own_pairs[:, None, None], (per_device, 3, 1)), axis=2
    )[:, :, 0]
    loss_out = jnp.sum(jax.nn.logsumexp(logits, axis=2) - target, axis=1).reshape(1, per_device)
    picked = (
        jnp.arange(row_count * NDOC, dtype=jnp.int32)[None, None, :] == own_pairs[:, None, None]
    ).astype(jnp.float32)
    grad_logits = (jax.nn.softmax(logits, axis=2) - picked) / LOSS_TEMP
    grad_rows = jnp.transpose(grad_logits.reshape(per_device, 3, row_count, NDOC), (2, 1, 0, 3))
    coefficient = jnp.repeat(grad_rows, QLEN, axis=2) / row_sums

    def row_back(carried, inputs):
        row_emb, lengths_row, row_coef = inputs
        row_hot = (
            segments_of(lengths_row, token_count)[:, None] == NQ_ROW + doc_numbers[None, :]
        ).astype(jnp.float32)
        row_raw = row_emb.astype(jnp.float32)
        new_carried = []
        row_grad = jnp.zeros((token_count, proj_width), jnp.float32)
        for level_index in range(3):
            width = widths[level_index]
            doc_unit_f, doc_part, doc_scale = normalize_cut(row_raw, width)
            doc_unit = doc_unit_f.astype(jnp.bfloat16)
            expo = jnp.exp(contract_cols(query_units[level_index], doc_unit) / POOL_TEMP)
            spread = contract_cols(row_coef[level_index], row_hot, FULL_PRECISION)
            grad_sim = (expo * spread).astype(jnp.bfloat16)
            new_carried.append(
                carried[level_index]
                + jnp.dot(grad_sim, doc_unit, preferred_element_type=jnp.float32)
            )
        return (tuple(new_carried), row_grad)

    zero_query = tuple((jnp.zeros((query_count, width), jnp.float32) for width in widths))
    query_grads, doc_grads = lax.scan(row_back, zero_query, (emb_rows, lengths, coefficient))
    grad_query = jnp.zeros((query_count, proj_width), jnp.float32)
    for level_index in range(3):
        level_parts = query_levels[level_index]
        grad_query = grad_query + normalize_back(
            query_grads[level_index], level_parts[1], level_parts[2], proj_width
        )
    coef_mine = jnp.transpose(coefficient, (2, 1, 0, 3)).reshape(query_count, 3, row_count * NDOC)
    coef_all, grad_query_all = (
        lax.all_gather(shortened(coef_mine), ("dp", "tensor"), axis=0, tiled=True).astype(
            coef_mine.dtype
        ),
        lax.all_gather(
            grad_query.astype(jnp.bfloat16), ("dp", "tensor"), axis=0, tiled=True
        ).astype(grad_query.dtype),
    )
    own_raw = embed.astype(jnp.float32)
    own_segments = lax.dynamic_slice_in_dim(segments, own_start, share_rows, 0)
    own_docs = jnp.where(own_segments >= NQ_ROW, data_index * NDOC + own_segments - NQ_ROW, -1)
    own_hot = (own_docs[:, None] == jnp.arange(row_count * NDOC, dtype=jnp.int32)[None, :]).astype(
        jnp.float32
    )
    queries_all = (
        emb_rows[:, :query_span].reshape(row_count * query_span, proj_width).astype(jnp.float32)
    )
    grad_embed = jnp.zeros((share_rows, proj_width), jnp.float32)
    for level_index in range(3):
        width = widths[level_index]
        query_unit_all = normalize_cut(queries_all, width)[0].astype(jnp.bfloat16)
        doc_unit_f, doc_part, doc_scale = normalize_cut(own_raw, width)
        expo = jnp.exp(contract_cols(query_unit_all, doc_unit_f.astype(jnp.bfloat16)) / POOL_TEMP)
        spread = contract_cols(coef_all[:, level_index], own_hot, FULL_PRECISION)
        grad_sim = (expo * spread).astype(jnp.bfloat16)
        grad_doc = contract_rows(grad_sim, query_unit_all)
        grad_embed = grad_embed + normalize_back(grad_doc, doc_part, doc_scale, proj_width)
    row_query_grads = lax.dynamic_slice_in_dim(
        grad_query_all, data_index * query_span, query_span, 0
    )
    padded = jnp.pad(row_query_grads, ((0, token_count - query_span), (0, 0)))
    grad_embed = grad_embed + lax.dynamic_slice_in_dim(padded, own_start, share_rows, 0)
    proj_float = w_proj.astype(jnp.float32)
    grad_result = cot.astype(jnp.float32) + contract_cols(grad_embed, proj_float, FULL_PRECISION)
    proj_grad = contract_rows(result_low.astype(jnp.float32), grad_embed, FULL_PRECISION)
    gain_two = jnp.sum(grad_result * unit_two, axis=0)
    shift_two = jnp.sum(grad_result, axis=0)
    grad_second = norm_backward(grad_result, unit_two, rstd_two, gains[1])
    grad_ffn = grad_second.astype(jnp.bfloat16)
    down_bias = jnp.sum(grad_ffn.astype(jnp.float32), axis=0)
    grad_ffn_all = lax.all_gather(grad_ffn, "tensor", axis=0, tiled=True)
    grad_act = contract_cols(grad_ffn_all, full_down)
    down_grad = contract_rows(activation, grad_ffn_all)
    _, gelu_pull = jax.vjp(partial(jax.nn.gelu, approximate=False), up_value)
    grad_up = gelu_pull(grad_act)[0].astype(jnp.bfloat16)
    up_bias = jnp.sum(grad_up.astype(jnp.float32), axis=0)
    up_grad = contract_rows(normed_all, grad_up)
    normed_terms = contract_cols(grad_up, full_up)
    grad_normed = (
        lax.psum_scatter(
            normed_terms.astype(jnp.bfloat16), "tensor", scatter_dimension=0, tiled=True
        ).astype(jnp.float32)
        + grad_second
    )
    gain_one = jnp.sum(grad_normed * unit_one, axis=0)
    shift_one = jnp.sum(grad_normed, axis=0)
    grad_first = norm_backward(grad_normed, unit_one, rstd_one, gains[0])
    grad_attn = grad_first.astype(jnp.bfloat16)
    out_bias = jnp.sum(grad_attn.astype(jnp.float32), axis=0)
    grad_attn_all = lax.all_gather(grad_attn, "tensor", axis=0, tiled=True)
    out_grad = contract_rows(mixed, grad_attn_all)
    grad_mixed = contract_cols(grad_attn_all, full_out).astype(jnp.bfloat16)
    grad_q, grad_k, grad_v = attend_backward(
        query_rows, key_rows, value_rows, segments, log_totals, grad_mixed, block_rows
    )
    stacked_grads = jnp.stack(
        [grad_q.astype(jnp.bfloat16), grad_k.astype(jnp.bfloat16), grad_v.astype(jnp.bfloat16)]
    )
    qkv_grad = jnp.einsum("td,ktw->kdw", tokens, stacked_grads, preferred_element_type=jnp.float32)
    input_terms = jnp.einsum(
        "ktw,kdw->td", stacked_grads, full_qkv, preferred_element_type=jnp.float32
    )
    grad_input = (
        lax.psum_scatter(
            input_terms.astype(jnp.bfloat16), "tensor", scatter_dimension=0, tiled=True
        ).astype(jnp.float32)
        + grad_first
    )
    qv_grad = jnp.stack(
        [
            jnp.sum(stacked_grads[0].astype(jnp.float32), axis=0),
            jnp.sum(stacked_grads[2].astype(jnp.float32), axis=0),
        ]
    )
    qkv_part, out_part, up_part, down_part = (
        lax.psum_scatter(
            qkv_grad.astype(jnp.bfloat16), "dp", scatter_dimension=1, tiled=True
        ).astype(jnp.float32),
        lax.psum_scatter(
            out_grad.astype(jnp.bfloat16), "dp", scatter_dimension=1, tiled=True
        ).astype(jnp.float32),
        lax.psum_scatter(
            up_grad.astype(jnp.bfloat16), "dp", scatter_dimension=0, tiled=True
        ).astype(jnp.float32),
        lax.psum_scatter(
            down_grad.astype(jnp.bfloat16), "dp", scatter_dimension=1, tiled=True
        ).astype(jnp.float32),
    )
    gain_sum, shift_sum, out_bias_sum, down_bias_sum, proj_sum = lax.psum(
        (
            jnp.stack([gain_one, gain_two]),
            jnp.stack([shift_one, shift_two]),
            out_bias,
            down_bias,
            proj_grad,
        ),
        ("dp", "tensor"),
    )
    qv_sum, up_bias_sum = lax.psum((qv_grad, up_bias), "dp")
    return (
        result_low,
        loss_out,
        grad_input.astype(jnp.bfloat16),
        qkv_part,
        qv_sum,
        out_part,
        out_bias_sum,
        gain_sum,
        shift_sum,
        up_part,
        up_bias_sum,
        down_part,
        down_bias_sum,
        proj_sum,
    )


SWAP = [(0, 1), (1, 0)]
TURN = [(0, 0), (1, 2), (2, 1), (3, 3)]
FAR = [(0, 3), (3, 0), (1, 2), (2, 1)]
NEAR = [(0, 1), (1, 0), (2, 3), (3, 2)]
BF = jnp.bfloat16
F32 = jnp.float32


def dot(left, right):
    return jnp.dot(left, right, preferred_element_type=F32)


CORES = ("c", "y")


def tie(value, *others):
    return lax.optimization_barrier((value,) + others)[0]


def tie_all(values, *others):
    return lax.optimization_barrier(tuple(values) + others)[: len(values)]


def exchange(*moves):
    return lax.optimization_barrier(
        tuple(lax.ppermute(value, axis, steps) for value, axis, steps in moves)
    )


def swap(value, axis):
    return lax.ppermute(value, axis, SWAP)


def pair_up(first, second, own_index, axis):
    return jnp.where(
        own_index == 0, jnp.stack([first, second], axis), jnp.stack([second, first], axis)
    )


def far_pair(value, far, z):
    return jnp.where(z < 2, jnp.stack([value, far]), jnp.stack([far, value]))


def whole_line(pair, other, z):
    return jnp.where(
        (z == 0) | (z == 3),
        jnp.stack([pair[0], other[0], other[1], pair[1]]),
        jnp.stack([other[0], pair[0], pair[1], other[1]]),
    )


def first_moves(line):
    half = line.shape[1] // 2
    return ((line[:, :half], "x", SWAP), (line[:, half:], "y", SWAP))


def first_parts(line, moved, x, y):
    half = line.shape[1] // 2
    return (pair_up(line[:, :half], moved[0], x, 1), pair_up(line[:, half:], moved[1], y, 1))


def last_moves(parts):
    return ((parts[0], "y", SWAP), (parts[1], "x", SWAP))


def full_rows(parts, moved, x, y):
    low = pair_up(parts[0], moved[0], y, 2)
    high = pair_up(parts[1], moved[1], x, 1)
    return jnp.concatenate([low, high], axis=3).reshape(-1, low.shape[-1])


def at(blocks, index, axis):
    return lax.dynamic_index_in_dim(blocks, index, axis, keepdims=False)


def side_move(blocks, axis_name, own_index, axis):
    return (at(blocks, 1 - own_index, axis).astype(BF), axis_name, SWAP)


def side_sum(blocks, got, own_index, axis):
    return at(blocks, own_index, axis).astype(F32) + got.astype(F32)


def near_move(line, z):
    ends = (z == 0) | (z == 3)
    outer, inner = jnp.stack([line[0], line[3]]), line[1:3]
    return (jnp.where(ends, inner, outer).astype(BF), "z", NEAR)


def near_sum(line, got, z):
    ends = (z == 0) | (z == 3)
    return jnp.where(ends, jnp.stack([line[0], line[3]]), line[1:3]) + got.astype(F32)


def far_move(pair, z):
    return (jnp.where(z < 2, pair[1], pair[0]).astype(BF), "z", FAR)


def far_sum(pair, got, z):
    return jnp.where(z < 2, pair[0], pair[1]) + got.astype(F32)


def blocks_of(left, right):
    return contract_rows(left, right).astype(BF).reshape(4, 2, 2, 64, right.shape[1])


def sum_moves(blocks, x, y):
    half = blocks.shape[3] // 2
    return (
        side_move(blocks[..., :half, :], "x", x, 1),
        side_move(blocks[..., half:, :], "y", y, 2),
    )


def sum_parts(blocks, moved, x, y):
    half = blocks.shape[3] // 2
    return (
        side_sum(blocks[..., :half, :], moved[0], x, 1),
        side_sum(blocks[..., half:, :], moved[1], y, 2),
    )


def line_moves(parts, x, y):
    return (side_move(parts[0], "y", y, 1), side_move(parts[1], "x", x, 1))


def line_of(parts, moved, x, y):
    return jnp.concatenate(
        [side_sum(parts[0], moved[0], y, 1), side_sum(parts[1], moved[1], x, 1)], axis=1
    )


def tile_bounds(row_lengths, token_count):
    ends = jnp.cumsum(row_lengths)
    span = NQ_ROW * QLEN
    first = jnp.arange(token_count // TILE, dtype=jnp.int32) * TILE - span
    last = first + TILE - 1
    begin = jnp.max(jnp.where(ends[None, :] <= first[:, None], ends[None, :], 0), axis=1)
    end = jnp.min(jnp.where(ends[None, :] > last[:, None], ends[None, :], token_count), axis=1)
    low = jnp.where(first < 0, 0, (begin + span) // TILE)
    high = jnp.where(first < 0, 1, (end + span + TILE - 1) // TILE)
    return jnp.stack([low, high]).astype(jnp.int32)


def token_spans(row_lengths, token_count):
    ends = jnp.cumsum(row_lengths)[:, None]
    span = NQ_ROW * QLEN
    place = jnp.arange(token_count, dtype=jnp.int32)[None, :]
    doc = place - span
    begin = jnp.max(jnp.where(ends <= doc, ends, 0), axis=0) + span
    end = jnp.min(jnp.where(ends > doc, ends, token_count), axis=0) + span
    query = place[0] // QLEN * QLEN
    return jnp.stack(
        [jnp.where(doc[0] < 0, query, begin), jnp.where(doc[0] < 0, query + QLEN, end)]
    ).astype(jnp.int32)


def rows_of(value, start, count):
    return lax.dynamic_slice_in_dim(value, start, count, 0)


TILE = 256
KEYS = 256
LOSS_TILE = 1024
NEG = -1e30


def exact(left, right, dims):
    return lax.dot_general(left, right, (dims, ((), ())), preferred_element_type=F32)


def head_masks(value):
    lane = lax.broadcasted_iota(jnp.int32, value.shape, 1)
    zero = jnp.zeros_like(value)
    return (jnp.where(lane < HEAD_DIM, value, zero), jnp.where(lane < HEAD_DIM, zero, value))


def key_shift(step, spans):
    place = step * KEYS + lax.broadcasted_iota(jnp.int32, (KEYS, TILE), 0)
    inside = (place >= spans[0:1, :]) & (place < spans[1:2, :])
    return jnp.where(inside, 0.0, NEG)


def attend_kernel(bounds, own_ref, qkv_ref, spans, out_ref, lse_ref, held):
    block = pl.program_id(0)
    groups = 2
    pairs = out_ref.shape[1] // 128
    per_group = pairs // groups

    def column(pair, part):
        start = ((pair // per_group) * 3 + part) * per_group + pair % per_group
        return slice(start * 128, (start + 1) * 128)

    queries = [head_masks(own_ref[:, column(pair, 0)] * HEAD_DIM**-0.5) for pair in range(pairs)]
    heads = [(pair, head) for pair in range(pairs) for head in range(2)]

    def score(step, highest):
        rows = pl.ds(pl.multiple_of(step * KEYS, KEYS), KEYS)
        shift = key_shift(step, spans)
        fresh = []
        for index, (pair, head) in enumerate(heads):
            keys = qkv_ref[rows, column(pair, 1)]
            scores = exact(keys, queries[pair][head], ((1,), (1,))) + shift
            held[index, rows, :] = scores
            fresh.append(jnp.maximum(highest[index], jnp.max(scores, axis=0, keepdims=True)))
        return tuple(fresh)

    low = jnp.full((1, TILE), NEG, F32)
    highest = lax.fori_loop(bounds[0, block], bounds[1, block], score, (low,) * len(heads))

    def mix(step, carried):
        rows = pl.ds(pl.multiple_of(step * KEYS, KEYS), KEYS)
        fresh = []
        for index, (pair, head) in enumerate(heads):
            values = qkv_ref[rows, column(pair, 2)]
            total, mixed = carried[index]
            expo = jnp.exp(held[index, rows, :] - highest[index])
            product = exact(values, expo.astype(BF), ((0,), (0,)))
            fresh.append(
                (
                    total + jnp.sum(expo, axis=0, keepdims=True),
                    mixed + product[head * HEAD_DIM : (head + 1) * HEAD_DIM],
                )
            )
        return tuple(fresh)

    start = (jnp.zeros((1, TILE), F32), jnp.zeros((HEAD_DIM, TILE), F32))
    parts = lax.fori_loop(bounds[0, block], bounds[1, block], mix, (start,) * len(heads))
    for pair in range(pairs):
        both = [parts[2 * pair + head][1] / parts[2 * pair + head][0] for head in range(2)]
        mixed = jnp.transpose(jnp.concatenate(both, axis=0))
        out_ref[:, pair * 128 : (pair + 1) * 128] = mixed.astype(BF)
    for index in range(len(heads)):
        lse_ref[index : index + 1, :] = highest[index] + jnp.log(parts[index][0])


def attend(bounds, qkv, spans):
    count, wide = qkv.shape
    heads = wide // 3 // HEAD_DIM
    whole = lambda shape: pl.BlockSpec(shape, lambda i: (0, 0))
    return pl.pallas_call(
        attend_kernel,
        grid=(count // TILE,),
        in_specs=[
            pl.BlockSpec(memory_space=pltpu.SMEM),
            pl.BlockSpec((TILE, wide), lambda i: (i, 0)),
            whole((count, wide)),
            pl.BlockSpec((2, TILE), lambda i: (0, i)),
        ],
        out_specs=[
            pl.BlockSpec((TILE, wide // 3), lambda i: (i, 0)),
            pl.BlockSpec((heads, TILE), lambda i: (0, i)),
        ],
        out_shape=[
            jax.ShapeDtypeStruct((count, wide // 3), BF),
            jax.ShapeDtypeStruct((heads, count), F32),
        ],
        scratch_shapes=[pltpu.VMEM((heads, count, TILE), F32)],
        compiler_params=pltpu.CompilerParams(vmem_limit_bytes=40 << 20),
        cost_estimate=pl.CostEstimate(
            flops=4 * heads * count * count * 64,
            transcendentals=heads * count * count // 2,
            bytes_accessed=4 * count * wide * 2,
        ),
    )(bounds, qkv, qkv, spans)


def attend_back_kernel(
    first, bounds, own_ref, qkv_ref, out_ref, grad_ref, lse_ref, spans,
    grads_ref, sums_ref, key_sum, value_sum,
):
    block = pl.program_id(0)
    pairs = out_ref.shape[1] // 128
    heads = [(pair, head) for pair in range(pairs) for head in range(2)]
    cut = lambda index: slice(index * 128, (index + 1) * 128)

    @pl.when(block == 0)
    def _():
        key_sum[...] = jnp.zeros_like(key_sum)
        value_sum[...] = jnp.zeros_like(value_sum)
        sums_ref[...] = jnp.zeros_like(sums_ref)

    queries = [head_masks(own_ref[:, cut(pair)] * HEAD_DIM**-0.5) for pair in range(pairs)]
    grads = [head_masks(grad_ref[:, cut(pair)]) for pair in range(pairs)]
    picks = head_masks(jnp.ones((8, 128), BF))
    inner = []
    for pair, head in heads:
        product = grad_ref[:, cut(pair)].astype(F32) * out_ref[:, cut(pair)].astype(F32)
        high = product.astype(BF)
        rest = (product - high.astype(F32)).astype(BF)
        inner.append(
            (
                exact(picks[head], high, ((1,), (1,))) + exact(picks[head], rest, ((1,), (1,)))
            )[0:1]
        )
    lse = [lse_ref[first + index : first + index + 1, :] for index in range(len(heads))]

    def step_of(step, carried):
        rows = pl.ds(pl.multiple_of(step * KEYS, KEYS), KEYS)
        shift = key_shift(step, spans)
        fresh = []
        for pair in range(pairs):
            keys = qkv_ref[rows, cut(pairs + pair)]
            values = qkv_ref[rows, cut(2 * pairs + pair)]
            key_add = jnp.zeros((KEYS, 128), F32)
            value_add = jnp.zeros((KEYS, 128), F32)
            for head in range(2):
                index = 2 * pair + head
                scores = exact(keys, queries[pair][head], ((1,), (1,))) + shift
                probs = jnp.exp(scores - lse[index])
                grad_probs = exact(values, grads[pair][head], ((1,), (1,)))
                grad_scores = (probs * (grad_probs - inner[index])).astype(BF)
                value_add = value_add + exact(probs.astype(BF), grads[pair][head], ((1,), (0,)))
                key_add = key_add + exact(grad_scores, queries[pair][head], ((1,), (0,)))
                product = exact(keys, grad_scores, ((0,), (0,)))
                fresh.append(carried[index] + product[head * HEAD_DIM : (head + 1) * HEAD_DIM])
            key_sum[rows, cut(pair)] += key_add
            value_sum[rows, cut(pair)] += value_add
        return tuple(fresh)

    start = jnp.zeros((HEAD_DIM, TILE), F32)
    parts = lax.fori_loop(bounds[0, block], bounds[1, block], step_of, (start,) * len(heads))
    own = pl.ds(pl.multiple_of(block * TILE, TILE), TILE)
    for pair in range(pairs):
        grad_query = jnp.concatenate([parts[2 * pair], parts[2 * pair + 1]], axis=0)
        grad_query = jnp.transpose(grad_query * HEAD_DIM**-0.5).astype(BF)
        grads_ref[own, cut(pair)] = grad_query
        sums_ref[0:1, cut(pair)] += jnp.sum(grad_query.astype(F32), axis=0, keepdims=True)

    @pl.when(block == pl.num_programs(0) - 1)
    def _():
        wide = pairs * 128
        grad_value = value_sum[...].astype(BF)
        grads_ref[:, wide : 2 * wide] = key_sum[...].astype(BF)
        grads_ref[:, 2 * wide :] = grad_value
        sums_ref[1:2, :] = jnp.sum(grad_value.astype(F32), axis=0, keepdims=True)


def attend_back(bounds, group, qkv, mixed, grad_mixed, lse, spans):
    count = qkv.shape[0]
    wide = qkv.shape[1] // 2
    heads = wide // 3 // HEAD_DIM
    whole = lambda shape: pl.BlockSpec(shape, lambda i: (0, 0))
    return pl.pallas_call(
        partial(attend_back_kernel, group * heads),
        grid=(count // TILE,),
        in_specs=[
            pl.BlockSpec(memory_space=pltpu.SMEM),
            pl.BlockSpec((TILE, wide), lambda i: (i, group)),
            pl.BlockSpec((count, wide), lambda i: (0, group)),
            pl.BlockSpec((TILE, wide // 3), lambda i: (i, group)),
            pl.BlockSpec((TILE, wide // 3), lambda i: (i, group)),
            pl.BlockSpec((2 * heads, TILE), lambda i: (0, i)),
            pl.BlockSpec((2, TILE), lambda i: (0, i)),
        ],
        out_specs=[whole((count, wide)), whole((8, wide // 3))],
        out_shape=[
            jax.ShapeDtypeStruct((count, wide), BF),
            jax.ShapeDtypeStruct((8, wide // 3), F32),
        ],
        scratch_shapes=[
            pltpu.VMEM((count, wide // 3), F32),
            pltpu.VMEM((count, wide // 3), F32),
        ],
        compiler_params=pltpu.CompilerParams(vmem_limit_bytes=40 << 20),
        cost_estimate=pl.CostEstimate(
            flops=10 * heads * count * count * 64,
            transcendentals=heads * count * count // 2,
            bytes_accessed=8 * count * wide * 2,
        ),
    )(
        bounds, qkv, qkv, mixed, grad_mixed,
        lse, spans,
    )


ERFC = (
    -1.26551223, 1.00002368, 0.37409196, 0.09678418, -0.18628806,
    0.27886807, -1.13520398, 1.48851587, -0.82215223, 0.17087277,
)


def gelu_pair(value):
    size = jnp.abs(value) * 0.5**0.5
    ratio = 1.0 / (1.0 + 0.5 * size)
    series = jnp.full_like(value, ERFC[-1])
    for factor in ERFC[-2::-1]:
        series = series * ratio + factor
    bell = jnp.exp(-size * size)
    tail = 0.5 * ratio * bell * jnp.exp(series)
    phi = jnp.where(value < 0.0, tail, 1.0 - tail)
    return (value * phi, phi + value * bell * 0.3989422804014327)


def expand_kernel(x_ref, w_ref, b_ref, *refs):
    act_ref, slope_ref = refs[-2:]
    rows = 128
    for start in range(0, x_ref.shape[0], rows):
        part = slice(start, start + rows)
        value = exact(x_ref[part, :], w_ref[...], ((1,), (0,))) + b_ref[...]
        active, slope = gelu_pair(value)
        act_ref[part, :] = active.astype(BF)
        slope_ref[part, :] = slope.astype(BF)


def expand(value, weight, shift, first, tiles, filled=()):
    count, depth = value.shape
    width = shift.shape[1]
    tile = 256
    column = lambda rows: pl.BlockSpec((rows, tile), lambda i: (0, first + i))
    return pl.pallas_call(
        expand_kernel,
        grid=(tiles,),
        in_specs=[
            pl.BlockSpec((count, depth), lambda i: (0, 0)),
            column(depth),
            column(1),
        ]
        + [pl.BlockSpec(memory_space=pl.ANY)] * len(filled),
        out_specs=[column(count)] * 2,
        out_shape=[jax.ShapeDtypeStruct((count, width), BF)] * 2,
        input_output_aliases={3: 0, 4: 1} if filled else {},
        compiler_params=pltpu.CompilerParams(vmem_limit_bytes=32 << 20),
        cost_estimate=pl.CostEstimate(
            flops=2 * count * depth * tile * tiles,
            transcendentals=3 * count * tile * tiles,
            bytes_accessed=2 * (count * depth + depth * tile * tiles + 2 * count * tile * tiles),
        ),
    )(value, weight, shift, *filled)


def cut_levels(raw, cuts):
    lane = lax.broadcasted_iota(jnp.int32, raw.shape, 1)
    levels = []
    for cut in cuts:
        part = jnp.where(lane < cut, raw, 0.0)
        scale = lax.rsqrt(jnp.sum(part * part, axis=1, keepdims=True) + EPS_EMBED)
        levels.append(((part * scale).astype(BF), part, scale))
    return levels


def pool_kernel(cuts, span, q_ref, d_ref, seg_ref, out_ref, units, hot):
    @pl.when(pl.program_id(0) == 0)
    def _():
        raw = d_ref[span:, :].astype(F32)
        for level, parts in enumerate(cut_levels(raw, cuts)):
            units[level] = parts[0]
        doc = lax.broadcasted_iota(jnp.int32, hot.shape, 0)
        hot[...] = (seg_ref[:, span:] == NQ_ROW + doc).astype(F32).astype(BF)

    levels = cut_levels(q_ref[...].astype(F32), cuts)
    for level in range(len(cuts)):
        similar = exact(units[level], levels[level][0], ((1,), (1,)))
        expo = jnp.exp(similar * (1.0 / POOL_TEMP))
        high = expo.astype(BF)
        rest = (expo - high.astype(F32)).astype(BF)
        out_ref[level * NDOC : (level + 1) * NDOC, :] = exact(
            hot[...], high, ((1,), (0,))
        ) + exact(hot[...], rest, ((1,), (0,)))


def pool(cuts, span, queries, row_embed, seg_row):
    count, width = queries.shape
    tokens = row_embed.shape[0]
    whole = lambda shape: pl.BlockSpec(shape, lambda i: (0, 0))
    return pl.pallas_call(
        partial(pool_kernel, cuts, span),
        grid=(count // LOSS_TILE,),
        in_specs=[
            pl.BlockSpec((LOSS_TILE, width), lambda i: (i, 0)),
            whole((tokens, width)),
            whole((1, tokens)),
        ],
        out_specs=pl.BlockSpec((len(cuts) * NDOC, LOSS_TILE), lambda i: (0, i)),
        out_shape=jax.ShapeDtypeStruct((len(cuts) * NDOC, count), F32),
        scratch_shapes=[
            pltpu.VMEM((len(cuts), tokens - span, width), BF),
            pltpu.VMEM((NDOC, tokens - span), BF),
        ],
        compiler_params=pltpu.CompilerParams(vmem_limit_bytes=32 << 20),
        cost_estimate=pl.CostEstimate(
            flops=2 * len(cuts) * count * tokens * 256,
            transcendentals=len(cuts) * count * tokens,
            bytes_accessed=2 * (count + tokens) * width,
        ),
    )(queries, row_embed, seg_row)


def level_back(grad, part, scale):
    return scale * grad - part * (scale * scale * scale) * jnp.sum(
        part * grad, axis=1, keepdims=True
    )


def pool_back_kernel(
    cuts, span, q_ref, d_ref, seg_ref, coef_ref, q_out, d_out, units, units_t, hot, sums
):
    step = pl.program_id(0)

    @pl.when(step == 0)
    def _():
        raw = d_ref[span:, :].astype(F32)
        for level, parts in enumerate(cut_levels(raw, cuts)):
            units[level] = parts[0]
            units_t[level] = jnp.transpose(parts[0])
        doc = lax.broadcasted_iota(jnp.int32, hot.shape, 0)
        wanted = NQ_ROW + jnp.where(doc < NDOC, doc, doc - NDOC)
        hot[...] = (seg_ref[:, span:] == wanted).astype(F32).astype(BF)
        sums[...] = jnp.zeros_like(sums)

    levels = cut_levels(q_ref[...].astype(F32), cuts)
    total = jnp.zeros(q_ref.shape, F32)
    for level in range(len(cuts)):
        unit, part, scale = levels[level]
        similar = exact(units[level], unit, ((1,), (1,)))
        coef = coef_ref[level * NDOC : (level + 1) * NDOC, :]
        high = coef.astype(BF).astype(F32)
        both = jnp.concatenate([high, coef - high], axis=0).astype(BF)
        spread = exact(hot[...], both, ((0,), (0,)))
        grad = (jnp.exp(similar * (1.0 / POOL_TEMP)) * spread).astype(BF)
        sums[level] += exact(grad, unit, ((1,), (0,)))
        grad_unit = jnp.transpose(exact(units_t[level], grad, ((1,), (0,))))
        total = total + level_back(grad_unit, part, scale)
    q_out[...] = total.astype(BF)

    @pl.when(step == pl.num_programs(0) - 1)
    def _():
        raw = d_ref[span:, :].astype(F32)
        result = jnp.zeros(raw.shape, F32)
        for level, parts in enumerate(cut_levels(raw, cuts)):
            lane = lax.broadcasted_iota(jnp.int32, raw.shape, 1)
            grad = jnp.where(lane < cuts[level], sums[level], 0.0)
            result = result + level_back(grad, parts[1], parts[2])
        d_out[...] = result


def pool_back(cuts, span, queries, row_embed, seg_row, coef):
    count, width = queries.shape
    tokens = row_embed.shape[0]
    docs = tokens - span
    whole = lambda shape: pl.BlockSpec(shape, lambda i: (0, 0))
    return pl.pallas_call(
        partial(pool_back_kernel, cuts, span),
        grid=(count // LOSS_TILE,),
        in_specs=[
            pl.BlockSpec((LOSS_TILE, width), lambda i: (i, 0)),
            whole((tokens, width)),
            whole((1, tokens)),
            pl.BlockSpec((len(cuts) * NDOC, LOSS_TILE), lambda i: (0, i)),
        ],
        out_specs=[pl.BlockSpec((LOSS_TILE, width), lambda i: (i, 0)), whole((docs, width))],
        out_shape=[
            jax.ShapeDtypeStruct((count, width), BF),
            jax.ShapeDtypeStruct((docs, width), F32),
        ],
        scratch_shapes=[
            pltpu.VMEM((len(cuts), docs, width), BF),
            pltpu.VMEM((len(cuts), width, docs), BF),
            pltpu.VMEM((2 * NDOC, docs), BF),
            pltpu.VMEM((len(cuts), docs, width), F32),
        ],
        compiler_params=pltpu.CompilerParams(vmem_limit_bytes=32 << 20),
        cost_estimate=pl.CostEstimate(
            flops=2 * len(cuts) * count * docs * 512,
            transcendentals=len(cuts) * count * docs,
            bytes_accessed=4 * (count + tokens) * width,
        ),
    )(queries, row_embed, seg_row, coef)


def local_chip(
    tokens,
    lengths,
    pairing,
    w_qkv,
    b_qv,
    w_out,
    b_out,
    ln_gain,
    ln_bias,
    w_up,
    b_up,
    w_down,
    b_down,
    w_proj,
    cot,
):
    z, x, c, y = (lax.axis_index(name) for name in ("z", "x", "c", "y"))
    chip = 4 * z + 2 * x + y
    token_count, width = tokens.shape
    share = token_count // 2
    own_start, other_start = c * share, (1 - c) * share
    gains, shifts = ln_gain.astype(F32), ln_bias.astype(F32)

    half_width = w_qkv.shape[2]
    up_wide = w_up.shape[1]
    chip_count = lengths.shape[0]
    half_queries = NQ_ROW // 2
    query_total = chip_count * half_queries
    quarter = half_width // 2
    qkv_rows = jnp.concatenate(
        [w_qkv[k][:, g * quarter : (g + 1) * quarter] for g in range(2) for k in range(3)], axis=1
    )
    pair_rows = jnp.pad(pairing.astype(BF), ((0, 63), (0, 128 - half_queries)))
    mid_rows = jnp.concatenate([w_up, w_out.T, pair_rows], axis=1)
    bias = jnp.concatenate([b_qv.reshape(-1), b_up])[None].astype(F32)
    got = exchange(
        (qkv_rows, CORES, TURN), (tokens, "c", SWAP), (bias, "y", SWAP)
    )
    qkv_rows = got[0]
    row = jnp.where(c == y, tokens, got[1])
    bias = jnp.where(c == y, bias, got[2])
    (rest_rows,) = exchange(
        (tie(jnp.concatenate([mid_rows, w_down.T], axis=1), row), CORES, TURN)
    )
    (far,) = exchange((qkv_rows, "z", FAR))
    qkv_pair = far_pair(qkv_rows, far, z)
    mid_wide = mid_rows.shape[1]
    rest_rows = tie(rest_rows, qkv_pair)
    mid_rows, down_rows = rest_rows[:, :mid_wide], rest_rows[:, mid_wide:]
    got = exchange((qkv_pair, "z", NEAR), (mid_rows, "z", FAR))
    qkv_line = whole_line(qkv_pair, got[0], z)
    mid_pair = far_pair(mid_rows, got[1], z)
    got = exchange(*first_moves(qkv_line), (mid_pair, "z", NEAR))
    qkv_parts = first_parts(qkv_line, got, x, y)
    mid_line = whole_line(mid_pair, got[2], z)
    last = last_moves(qkv_parts)
    got = exchange(*last, (tie(down_rows, mid_line), "z", FAR), *first_moves(mid_line))
    full_qkv = full_rows(qkv_parts, got, x, y)
    down_pair = far_pair(down_rows, got[2], z)
    mid_parts = first_parts(mid_line, got[3:], x, y)
    (near,) = exchange((down_pair, "z", NEAR))
    down_line = whole_line(down_pair, near, z)
    got = exchange(*last_moves(mid_parts), *first_moves(down_line))
    full_mid = full_rows(mid_parts, got, x, y)
    down_parts = first_parts(down_line, got[2:], x, y)
    full_out = full_mid[:, up_wide : up_wide + half_width]
    pairs = full_mid[:, up_wide + half_width :].reshape(chip_count, 64, 128)
    pairs = pairs[:, 0, :half_queries].astype(jnp.int32).reshape(1, query_total)
    row_lengths = lax.dynamic_index_in_dim(lengths, chip, 0, keepdims=False)
    segments = segments_of(row_lengths, token_count)
    seg_row, spans = segments[None, :], token_spans(row_lengths, token_count)
    query_span = NQ_ROW * QLEN
    bounds = tile_bounds(row_lengths, token_count)
    no_bias = jnp.zeros((1, quarter), F32)
    qkv_bias = jnp.concatenate(
        [
            part
            for g in range(2)
            for part in (
                bias[:, g * quarter : (g + 1) * quarter],
                no_bias,
                bias[:, half_width + g * quarter : half_width + (g + 1) * quarter],
            )
        ],
        axis=1,
    )
    qkv = (dot(row, full_qkv) + qkv_bias).astype(BF)
    mixed, lse = attend(bounds, tie(qkv, down_line), spans)

    def row_sum(left, weight_t, transposed):
        times = contract_cols if transposed else dot
        theirs = swap(times(left(1), weight_t).astype(BF), "c")
        return times(left(0), weight_t) + theirs.astype(F32)

    def mixed_half(which):
        return rows_of(mixed, other_start if which else own_start, share)

    other_attn = swap(contract_cols(mixed_half(1), full_out).astype(BF), "c")
    other_attn, second_norm = lax.optimization_barrier(
        (other_attn, jnp.stack([gains[1], shifts[1]]))
    )
    second_norm = swap(second_norm, "c")
    second_norm, *down_parts = lax.optimization_barrier((second_norm,) + tuple(down_parts))
    down_got = exchange(*last_moves(down_parts))
    attn_sum = contract_cols(mixed_half(0), full_out) + other_attn.astype(F32)
    own_tokens = rows_of(row, own_start, share).astype(F32)
    normed, unit_one, rstd_one = norm_forward(
        own_tokens + attn_sum + b_out.astype(F32), gains[0], shifts[0]
    )
    normed_low = normed.astype(BF)
    normed_all = jnp.concatenate([normed_low, swap(normed_low, "c")], axis=0)
    activation, slope = expand(
        normed_all, full_mid, bias[:, 2 * half_width :], 0, up_wide // 256
    )
    full_down = full_rows(down_parts, down_got, x, y)
    ffn_sum = row_sum(
        lambda which: activation[which * share : (which + 1) * share], full_down, True
    )
    result, unit_two, rstd_two = norm_forward(
        normed + ffn_sum + b_down.astype(F32), second_norm[0], second_norm[1]
    )
    result_low = result.astype(BF)
    embed = dot(result_low, w_proj).astype(BF)

    other_embed = swap(embed, "c")
    row_embed = jnp.where(
        c == 0,
        jnp.concatenate([embed, other_embed], axis=0),
        jnp.concatenate([other_embed, embed], axis=0),
    )
    half_span = query_span // 2
    own_queries = rows_of(row_embed, c * half_span, half_span)
    chips = ("z", "x", "y")
    queries = lax.all_to_all(
        jnp.broadcast_to(own_queries[None], (chip_count,) + own_queries.shape), chips, 0, 0
    ).reshape(chip_count * half_span, -1)
    queries, own_cot = lax.optimization_barrier((queries, lax.ppermute(cot, CORES, TURN)))
    proj_width = w_proj.shape[1]
    cuts = (proj_width, 3 * proj_width // 4, proj_width // 2)
    sums = pool(cuts, query_span, queries, row_embed, seg_row)
    doc_sizes = jnp.tile(row_lengths.astype(F32), 3)[:, None]
    group = (
        jnp.arange(query_total * QLEN, dtype=jnp.int32)[:, None] // QLEN
        == jnp.arange(query_total, dtype=jnp.int32)[None, :]
    ).astype(F32)
    pooled = POOL_TEMP * jnp.log(sums / doc_sizes)
    logits = jnp.dot(pooled, group, precision=FULL_PRECISION) / LOSS_TEMP
    logits = logits.reshape(3, NDOC, query_total)
    doc_numbers = chip * NDOC + jnp.arange(NDOC, dtype=jnp.int32)
    picked = (doc_numbers[:, None] == pairs).astype(F32)
    own_high = jnp.max(logits, axis=1)
    own_lse = own_high + jnp.log(jnp.sum(jnp.exp(logits - own_high[:, None]), axis=1))
    own_target = jnp.sum(logits * picked, axis=1)
    notes = jnp.pad(jnp.concatenate([own_lse, own_target], axis=1), ((0, 5), (0, 0)))
    notes = lax.all_to_all(
        jnp.broadcast_to(notes[None], (chip_count,) + notes.shape), chips, 0, 0
    )
    chip_lse = notes[:, :3, :query_total]
    high = jnp.max(chip_lse, axis=0)
    all_lse = high + jnp.log(jnp.sum(jnp.exp(chip_lse - high), axis=0))
    target = jnp.sum(notes[:, :3, query_total:], axis=0)
    losses = jnp.sum(all_lse - target, axis=0).reshape(chip_count, half_queries)
    grad_logits = (jnp.exp(logits - all_lse[:, None]) - picked) / LOSS_TEMP
    coefficient = (
        lax.dot_general(
            grad_logits.reshape(3 * NDOC, query_total),
            group,
            (((1,), (1,)), ((), ())),
            precision=FULL_PRECISION,
        )
        / sums
    )
    query_grad, doc_grad = pool_back(cuts, query_span, queries, row_embed, seg_row, coefficient)
    query_grad, y_out = lax.optimization_barrier(
        (query_grad, lax.ppermute(result_low, CORES, TURN))
    )
    grad_blocks = lax.all_to_all(
        query_grad.reshape(chip_count, half_span, proj_width), chips, 0, 0
    )
    own_query_grad = jnp.sum(grad_blocks.astype(F32), axis=0)
    row_grad = jnp.concatenate([jnp.zeros((query_span, proj_width), F32), doc_grad], axis=0)
    row_grad = lax.dynamic_update_slice_in_dim(row_grad, own_query_grad, c * half_span, 0)
    grad_embed = rows_of(row_grad, own_start, share) + swap(
        rows_of(row_grad, other_start, share), "c"
    )

    proj_low = w_proj
    grad_embed_low = grad_embed.astype(BF)
    grad_embed_rest = (grad_embed - grad_embed_low.astype(F32)).astype(BF)
    grad_result = own_cot.astype(F32) + (
        contract_cols(grad_embed_low, proj_low) + contract_cols(grad_embed_rest, proj_low)
    )
    proj_grad = contract_rows(result_low, grad_embed_low) + contract_rows(
        result_low, grad_embed_rest
    )
    gain_two = jnp.sum(grad_result * unit_two, axis=0)
    shift_two = jnp.sum(grad_result, axis=0)
    grad_second = norm_backward(grad_result, unit_two, rstd_two, second_norm[0])
    grad_ffn = grad_second.astype(BF)
    down_bias = jnp.sum(grad_ffn.astype(F32), axis=0)
    other_ffn = swap(grad_ffn, "c")
    grad_ffn_all = jnp.concatenate([grad_ffn, other_ffn], axis=0)
    down_blocks = blocks_of(grad_ffn_all, activation)
    down_moved = exchange(*sum_moves(down_blocks, x, y))
    grad_up = (dot(grad_ffn_all, full_down) * slope.astype(F32)).astype(BF)
    up_bias = jnp.sum(grad_up.astype(F32), axis=0)
    up_blocks = blocks_of(normed_all, tie(grad_up, *down_moved))
    full_up = full_mid[:, :up_wide]
    grad_normed = (
        row_sum(lambda which: grad_up[which * share : (which + 1) * share], full_up, True)
        + grad_second
    )
    gain_one = jnp.sum(grad_normed * unit_one, axis=0)
    shift_one = jnp.sum(grad_normed, axis=0)
    grad_first = norm_backward(grad_normed, unit_one, rstd_one, gains[0])
    grad_attn = grad_first.astype(BF)
    out_bias = jnp.sum(grad_attn.astype(F32), axis=0)
    other_attn = swap(grad_attn, "c")
    grad_attn_all = jnp.where(
        c == 0,
        jnp.concatenate([grad_attn, other_attn], axis=0),
        jnp.concatenate([other_attn, grad_attn], axis=0),
    )
    grad_mixed = dot(grad_attn_all, full_out).astype(BF)
    out_blocks = blocks_of(grad_attn_all, mixed)
    down_parts = sum_parts(down_blocks, down_moved, x, y)
    moved = exchange(*line_moves(down_parts, x, y), *sum_moves(up_blocks, x, y))
    down_line = line_of(down_parts, moved, x, y)
    up_parts = sum_parts(up_blocks, moved[2:], x, y)
    grad_mixed, out_blocks, down_line, *up_parts = lax.optimization_barrier(
        (grad_mixed, out_blocks, down_line) + tuple(up_parts)
    )
    moved = exchange(
        near_move(down_line, z), *line_moves(up_parts, x, y), *sum_moves(out_blocks, x, y)
    )
    grads_one, sums_one = attend_back(bounds, 0, qkv, mixed, grad_mixed, lse, spans)
    down_pair = near_sum(down_line, moved[0], z)
    up_line = line_of(up_parts, moved[1:], x, y)
    out_parts = sum_parts(out_blocks, moved[3:], x, y)
    grad_mixed, down_pair, up_line, *out_parts = lax.optimization_barrier(
        (grad_mixed, down_pair, up_line) + tuple(out_parts)
    )
    up_line, losses = lax.optimization_barrier((up_line, losses))
    moved = exchange(
        far_move(down_pair, z), near_move(up_line, z), *line_moves(out_parts, x, y)
    )
    other_losses = swap(losses, "c")
    proj_given, other_losses, grad_mixed = lax.optimization_barrier(
        (rows_of(proj_grad, other_start, share), other_losses, grad_mixed)
    )
    proj_half = rows_of(proj_grad, own_start, share)
    other_proj = swap(proj_given, "c")
    grad_mixed, other_proj = lax.optimization_barrier((grad_mixed, other_proj))
    proj_half = proj_half + other_proj
    losses = jnp.where(c == y, losses, other_losses)
    loss_out = rows_of(losses, 4 * z + 2 * x + c, 1)
    grads_two, sums_two = attend_back(bounds, 1, qkv, mixed, grad_mixed, lse, spans)
    down_part = far_sum(down_pair, moved[0], z)
    up_pair = near_sum(up_line, moved[1], z)
    out_line = line_of(out_parts, moved[2:], x, y)
    grads_one, grads_two, down_part, up_pair, out_line = lax.optimization_barrier(
        (grads_one, grads_two, down_part, up_pair, out_line)
    )
    shared = jnp.stack([gain_one, gain_two, shift_one, shift_two, out_bias, down_bias])
    half_sums = jnp.concatenate(
        [
            sums_one[0],
            sums_two[0],
            sums_one[1],
            sums_two[1],
            up_bias,
        ]
    )
    small = jnp.concatenate([shared.reshape(-1, 128), half_sums.reshape(-1, 128), proj_half])

    qkv_blocks = jnp.concatenate(
        [blocks_of(row, grads_one), blocks_of(row, grads_two)], axis=4
    )
    qkv_blocks, up_pair, out_line, down_part, small = lax.optimization_barrier(
        (qkv_blocks, up_pair, out_line, down_part, small)
    )
    moved = exchange(
        *sum_moves(qkv_blocks, x, y),
        far_move(up_pair, z),
        near_move(out_line, z),
        (small.astype(BF), "y", SWAP),
    )
    qkv_parts = sum_parts(qkv_blocks, moved, x, y)
    up_part = far_sum(up_pair, moved[2], z)
    out_pair = near_sum(out_line, moved[3], z)
    small = small + moved[4].astype(F32)

    def input_terms(start):
        return contract_cols(
            rows_of(grads_one, start, share), full_qkv[:, : 3 * quarter]
        ) + contract_cols(rows_of(grads_two, start, share), full_qkv[:, 3 * quarter :])

    other_terms = swap(input_terms(other_start).astype(BF), "c")
    grad_input = (input_terms(own_start) + other_terms.astype(F32) + grad_first).astype(BF)
    moved = exchange(*line_moves(qkv_parts, x, y), far_move(out_pair, z), (small.astype(BF), "x", SWAP))
    qkv_line = line_of(qkv_parts, moved, x, y)
    out_part = far_sum(out_pair, moved[2], z)
    small = small + moved[3].astype(F32)
    moved = exchange(
        near_move(qkv_line, z),
        (small.astype(BF), "z", FAR),
        (tie(grad_input, qkv_line), CORES, TURN),
    )
    qkv_pair = near_sum(qkv_line, moved[0], z)
    small = small + moved[1].astype(F32)
    grad_input = moved[2]
    ffn_part = jnp.concatenate([down_part, up_part], axis=1).astype(BF)
    moved = exchange(
        far_move(qkv_pair, z), (small.astype(BF), "z", NEAR), (tie(ffn_part, qkv_pair), CORES, TURN)
    )
    attn_part = jnp.concatenate([far_sum(qkv_pair, moved[0], z), out_part], axis=1).astype(BF)
    small = small + moved[1].astype(F32)
    ffn_part = moved[2].astype(F32)
    down_part, up_part = ffn_part[:, :up_wide], ffn_part[:, up_wide:]
    attn_part, other_small = exchange((attn_part, CORES, TURN), (small.astype(BF), "c", SWAP))
    attn_part = attn_part.astype(F32)
    other_small = other_small.astype(F32)
    qkv_part, out_part = attn_part[:, : 3 * half_width], attn_part[:, 3 * half_width :]
    shared_rows = 6 * width // 128
    small_rows = small.shape[0] - share
    shared = (small[:shared_rows] + other_small[:shared_rows]).reshape(6, width)
    half_sums = jnp.where(
        c == y, small[shared_rows:small_rows], other_small[shared_rows:small_rows]
    ).reshape(-1)
    proj_sum = pair_up(small[small_rows:], other_small[small_rows:], c, 0).reshape(width, -1)
    qkv_part = qkv_part.reshape(64, 2, 3, quarter).transpose(2, 0, 1, 3).reshape(3, 64, half_width)
    return (
        y_out,
        loss_out,
        grad_input,
        qkv_part,
        half_sums[: 2 * half_width].reshape(2, half_width),
        out_part.T,
        shared[4],
        shared[0:2],
        shared[2:4],
        up_part,
        half_sums[2 * half_width :],
        down_part.T,
        shared[5],
        proj_sum,
    )


IN_SPECS = (
    P("dp", None),
    P(),
    P("dp", "tensor"),
    P(None, "dp", "tensor"),
    P(None, "tensor"),
    P("tensor", "dp"),
    P(),
    P(),
    P(),
    P("dp", "tensor"),
    P("tensor"),
    P("tensor", "dp"),
    P(),
    P(),
    P(("dp", "tensor"), None),
)
OUT_SPECS = (
    P(("dp", "tensor"), None),
    P("dp", "tensor"),
    P(("dp", "tensor"), None),
    P(None, "dp", "tensor"),
    P(None, "tensor"),
    P("tensor", "dp"),
    P(),
    P(),
    P(),
    P("dp", "tensor"),
    P("tensor"),
    P("tensor", "dp"),
    P(),
    P(),
)


def solution(mesh):
    if mesh.devices.shape != (16, 2):
        return jax.shard_map(
            local, mesh=mesh, in_specs=IN_SPECS, out_specs=OUT_SPECS, check_vma=False
        )
    names = {"dp": ("z", "x", "c"), "tensor": ("y",)}

    def respec(spec):
        parts = []
        for entry in spec:
            axes = () if entry is None else entry if isinstance(entry, tuple) else (entry,)
            parts.append(tuple(name for axis in axes for name in names[axis]) or None)
        return P(*parts)

    chips = Mesh(mesh.devices.reshape(4, 2, 2, 2), ("z", "x", "c", "y"))
    return jax.shard_map(
        local_chip,
        mesh=chips,
        in_specs=tuple(respec(spec) for spec in IN_SPECS),
        out_specs=tuple(respec(spec) for spec in OUT_SPECS),
        check_vma=False,
    )
```

```python
from functools import partial

import jax
import jax.numpy as jnp
from jax import lax
from jax.experimental import pallas as pl
from jax.experimental.pallas import tpu as pltpu
from jax.sharding import Mesh, PartitionSpec as P

HEAD_DIM = 64
QLEN = 32
NQ_ROW = 8
NDOC = 8


EPS_NORM = 1e-05
EPS_EMBED = 1e-06
POOL_TEMP = 0.1
LOSS_TEMP = 0.1
FULL_PRECISION = lax.Precision.HIGHEST
MASKED_SCORE = -1e30


def shortened(shard):

    def short(part):
        return part.astype(jnp.bfloat16) if part.dtype == jnp.float32 else part

    return jax.tree.map(short, shard)


def contract_rows(left, right, precision=None):
    return lax.dot_general(
        left,
        right,
        (((0,), (0,)), ((), ())),
        precision=precision,
        preferred_element_type=jnp.float32,
    )


def contract_cols(left, right, precision=None):
    return lax.dot_general(
        left,
        right,
        (((1,), (1,)), ((), ())),
        precision=precision,
        preferred_element_type=jnp.float32,
    )


def norm_forward(value, gain, shift):
    centred = value - jnp.mean(value, axis=1, keepdims=True)
    rstd = lax.rsqrt(jnp.mean(centred * centred, axis=1, keepdims=True) + EPS_NORM)
    unit = centred * rstd
    return (unit * gain + shift, unit, rstd)


def norm_backward(grad, unit, rstd, gain):
    scaled = grad * gain
    return rstd * (
        scaled
        - jnp.mean(scaled, axis=1, keepdims=True)
        - unit * jnp.mean(scaled * unit, axis=1, keepdims=True)
    )


def segments_of(row_lengths, token_count):
    position = jnp.arange(token_count, dtype=jnp.int32)
    query_span = NQ_ROW * QLEN
    ends = jnp.cumsum(row_lengths)
    passed = jnp.sum((position[:, None] - query_span >= ends[None, :]).astype(jnp.int32), axis=1)
    return jnp.where(position < query_span, position // QLEN, NQ_ROW + passed)


def normalize_cut(raw, width):
    part = raw[:, :width]
    scale = lax.rsqrt(jnp.sum(part * part, axis=1, keepdims=True) + EPS_EMBED)
    return (part * scale, part, scale)


def normalize_back(grad, part, scale, full_width):
    result = scale * grad - part * (scale * scale * scale) * jnp.sum(
        part * grad, axis=1, keepdims=True
    )
    return jnp.pad(result, ((0, 0), (0, full_width - grad.shape[1])))


def masked_scores(query_block, key_rows, block_segments, segments):
    scores = jnp.einsum(
        "qhd,khd->hqk", query_block, key_rows, preferred_element_type=jnp.float32
    ) * HEAD_DIM ** (-0.5)
    return jnp.where((block_segments[:, None] == segments[None, :])[None], scores, MASKED_SCORE)


def attend_forward(query_rows, key_rows, value_rows, segments, block_rows):
    token_count = query_rows.shape[0]

    def one_block(block_start):
        query_block = lax.dynamic_slice_in_dim(query_rows, block_start, block_rows, 0)
        block_segments = lax.dynamic_slice_in_dim(segments, block_start, block_rows, 0)
        scores = masked_scores(query_block, key_rows, block_segments, segments)
        highest = jnp.max(scores, axis=2, keepdims=True)
        expo = jnp.exp(scores - highest)
        totals = jnp.sum(expo, axis=2, keepdims=True)
        weights = (expo / totals).astype(jnp.bfloat16)
        mixed = jnp.einsum("hqk,khd->qhd", weights, value_rows, preferred_element_type=jnp.float32)
        return (mixed.astype(jnp.bfloat16), (highest + jnp.log(totals))[:, :, 0])

    starts = jnp.arange(token_count // block_rows, dtype=jnp.int32) * block_rows
    mixed, log_totals = lax.map(one_block, starts)
    return (mixed.reshape(token_count, -1), log_totals)


def attend_backward(query_rows, key_rows, value_rows, segments, log_totals, grad_mixed, block_rows):
    token_count, local_heads, head_size = query_rows.shape
    scale = HEAD_DIM ** (-0.5)
    grad_heads = grad_mixed.reshape(token_count, local_heads, head_size)

    def one_block(carried, inputs):
        grad_keys, grad_values = carried
        block_start, block_lse = inputs
        query_block = lax.dynamic_slice_in_dim(query_rows, block_start, block_rows, 0)
        grad_block = lax.dynamic_slice_in_dim(grad_heads, block_start, block_rows, 0)
        block_segments = lax.dynamic_slice_in_dim(segments, block_start, block_rows, 0)
        scores = masked_scores(query_block, key_rows, block_segments, segments)
        probs = jnp.exp(scores - block_lse[:, :, None])
        grad_probs = jnp.einsum(
            "qhd,khd->hqk", grad_block, value_rows, preferred_element_type=jnp.float32
        )
        inner = jnp.sum(probs * grad_probs, axis=2, keepdims=True)
        grad_scores = (probs * (grad_probs - inner)).astype(jnp.bfloat16)
        grad_query = (
            jnp.einsum("hqk,khd->qhd", grad_scores, key_rows, preferred_element_type=jnp.float32)
            * scale
        )
        grad_keys = (
            grad_keys
            + jnp.einsum(
                "hqk,qhd->khd", grad_scores, query_block, preferred_element_type=jnp.float32
            )
            * scale
        )
        grad_values = grad_values + jnp.einsum(
            "hqk,qhd->khd",
            probs.astype(jnp.bfloat16),
            grad_block,
            preferred_element_type=jnp.float32,
        )
        return ((grad_keys, grad_values), grad_query)

    starts = jnp.arange(token_count // block_rows, dtype=jnp.int32) * block_rows
    zero_rows = jnp.zeros(key_rows.shape, jnp.float32)
    (grad_keys, grad_values), grad_queries = lax.scan(
        one_block, (zero_rows, zero_rows), (starts, log_totals)
    )
    flat_width = local_heads * head_size
    return (
        grad_queries.reshape(token_count, flat_width),
        grad_keys.reshape(token_count, flat_width),
        grad_values.reshape(token_count, flat_width),
    )


def local(
    tokens,
    lengths,
    pairing,
    w_qkv,
    b_qv,
    w_out,
    b_out,
    ln_gain,
    ln_bias,
    w_up,
    b_up,
    w_down,
    b_down,
    w_proj,
    cot,
):
    tensor_count = lax.axis_size("tensor")
    tensor_index = lax.axis_index("tensor")
    data_index = lax.axis_index("dp")
    token_count = tokens.shape[0]
    share_rows = token_count // tensor_count
    block_rows = min(512, token_count)
    own_start = tensor_index * share_rows
    full_qkv, full_out, full_up, full_down = (
        lax.all_gather(w_qkv, "dp", axis=1, tiled=True),
        lax.all_gather(w_out, "dp", axis=1, tiled=True),
        lax.all_gather(w_up, "dp", axis=0, tiled=True),
        lax.all_gather(w_down, "dp", axis=1, tiled=True),
    )
    head_width = full_qkv.shape[2]
    local_heads = head_width // HEAD_DIM
    row_lengths = lax.dynamic_index_in_dim(lengths, data_index, 0, keepdims=False)
    segments = segments_of(row_lengths, token_count)
    projected = jnp.einsum("td,kdw->ktw", tokens, full_qkv, preferred_element_type=jnp.float32)
    qv_bias = b_qv.astype(jnp.float32)
    query_rows = (
        (projected[0] + qv_bias[0]).astype(jnp.bfloat16).reshape(token_count, local_heads, HEAD_DIM)
    )
    key_rows = projected[1].astype(jnp.bfloat16).reshape(token_count, local_heads, HEAD_DIM)
    value_rows = (
        (projected[2] + qv_bias[1]).astype(jnp.bfloat16).reshape(token_count, local_heads, HEAD_DIM)
    )
    mixed, log_totals = attend_forward(query_rows, key_rows, value_rows, segments, block_rows)
    attn_terms = jnp.dot(mixed, full_out, preferred_element_type=jnp.float32)
    attn_sum = lax.psum_scatter(
        attn_terms.astype(jnp.bfloat16), "tensor", scatter_dimension=0, tiled=True
    ).astype(jnp.float32)
    own_tokens = lax.dynamic_slice_in_dim(tokens, own_start, share_rows, 0).astype(jnp.float32)
    gains = ln_gain.astype(jnp.float32)
    shifts = ln_bias.astype(jnp.float32)
    normed, unit_one, rstd_one = norm_forward(
        own_tokens + attn_sum + b_out.astype(jnp.float32), gains[0], shifts[0]
    )
    normed_all = lax.all_gather(normed.astype(jnp.bfloat16), "tensor", axis=0, tiled=True)
    up_value = jnp.dot(normed_all, full_up, preferred_element_type=jnp.float32) + b_up.astype(
        jnp.float32
    )
    activation = jax.nn.gelu(up_value, approximate=False).astype(jnp.bfloat16)
    ffn_terms = jnp.dot(activation, full_down, preferred_element_type=jnp.float32)
    ffn_sum = lax.psum_scatter(
        ffn_terms.astype(jnp.bfloat16), "tensor", scatter_dimension=0, tiled=True
    ).astype(jnp.float32)
    result, unit_two, rstd_two = norm_forward(
        normed + ffn_sum + b_down.astype(jnp.float32), gains[1], shifts[1]
    )
    result_low = result.astype(jnp.bfloat16)
    embed = jnp.dot(result_low, w_proj, preferred_element_type=jnp.float32).astype(jnp.bfloat16)
    embed_all = lax.all_gather(embed, ("dp", "tensor"), axis=0, tiled=True)
    row_count = lengths.shape[0]
    proj_width = w_proj.shape[1]
    widths = (proj_width, 3 * proj_width // 4, proj_width // 2)
    per_device = pairing.shape[1]
    query_count = per_device * QLEN
    query_span = NQ_ROW * QLEN
    emb_rows = embed_all.reshape(row_count, token_count, proj_width)
    my_row = lax.dynamic_index_in_dim(emb_rows, data_index, 0, keepdims=False)
    query_raw = lax.dynamic_slice_in_dim(my_row, tensor_index * query_count, query_count, 0).astype(
        jnp.float32
    )
    query_levels = [normalize_cut(query_raw, width) for width in widths]
    query_units = [level_parts[0].astype(jnp.bfloat16) for level_parts in query_levels]
    doc_numbers = jnp.arange(NDOC, dtype=jnp.int32)

    def row_pool(carried, inputs):
        row_emb, lengths_row = inputs
        row_hot = (
            segments_of(lengths_row, token_count)[:, None] == NQ_ROW + doc_numbers[None, :]
        ).astype(jnp.float32)
        row_raw = row_emb.astype(jnp.float32)
        pooled_list = []
        sums_list = []
        for width, query_unit in zip(widths, query_units):
            doc_unit = normalize_cut(row_raw, width)[0].astype(jnp.bfloat16)
            expo = jnp.exp(contract_cols(query_unit, doc_unit) / POOL_TEMP)
            sums = jnp.dot(expo, row_hot, precision=FULL_PRECISION)
            pooled = POOL_TEMP * jnp.log(sums / lengths_row.astype(jnp.float32))
            pooled_list.append(jnp.sum(pooled.reshape(per_device, QLEN, NDOC), axis=1))
            sums_list.append(sums)
        return (carried, (jnp.stack(pooled_list), jnp.stack(sums_list)))

    _, (row_scores, row_sums) = lax.scan(row_pool, 0, (emb_rows, lengths))
    logits = (
        jnp.transpose(row_scores, (2, 1, 0, 3)).reshape(per_device, 3, row_count * NDOC) / LOSS_TEMP
    )
    own_pairs = pairing[0]
    target = jnp.take_along_axis(
        logits, jnp.broadcast_to(own_pairs[:, None, None], (per_device, 3, 1)), axis=2
    )[:, :, 0]
    loss_out = jnp.sum(jax.nn.logsumexp(logits, axis=2) - target, axis=1).reshape(1, per_device)
    picked = (
        jnp.arange(row_count * NDOC, dtype=jnp.int32)[None, None, :] == own_pairs[:, None, None]
    ).astype(jnp.float32)
    grad_logits = (jax.nn.softmax(logits, axis=2) - picked) / LOSS_TEMP
    grad_rows = jnp.transpose(grad_logits.reshape(per_device, 3, row_count, NDOC), (2, 1, 0, 3))
    coefficient = jnp.repeat(grad_rows, QLEN, axis=2) / row_sums

    def row_back(carried, inputs):
        row_emb, lengths_row, row_coef = inputs
        row_hot = (
            segments_of(lengths_row, token_count)[:, None] == NQ_ROW + doc_numbers[None, :]
        ).astype(jnp.float32)
        row_raw = row_emb.astype(jnp.float32)
        new_carried = []
        row_grad = jnp.zeros((token_count, proj_width), jnp.float32)
        for level_index in range(3):
            width = widths[level_index]
            doc_unit_f, doc_part, doc_scale = normalize_cut(row_raw, width)
            doc_unit = doc_unit_f.astype(jnp.bfloat16)
            expo = jnp.exp(contract_cols(query_units[level_index], doc_unit) / POOL_TEMP)
            spread = contract_cols(row_coef[level_index], row_hot, FULL_PRECISION)
            grad_sim = (expo * spread).astype(jnp.bfloat16)
            new_carried.append(
                carried[level_index]
                + jnp.dot(grad_sim, doc_unit, preferred_element_type=jnp.float32)
            )
        return (tuple(new_carried), row_grad)

    zero_query = tuple((jnp.zeros((query_count, width), jnp.float32) for width in widths))
    query_grads, doc_grads = lax.scan(row_back, zero_query, (emb_rows, lengths, coefficient))
    grad_query = jnp.zeros((query_count, proj_width), jnp.float32)
    for level_index in range(3):
        level_parts = query_levels[level_index]
        grad_query = grad_query + normalize_back(
            query_grads[level_index], level_parts[1], level_parts[2], proj_width
        )
    coef_mine = jnp.transpose(coefficient, (2, 1, 0, 3)).reshape(query_count, 3, row_count * NDOC)
    coef_all, grad_query_all = (
        lax.all_gather(shortened(coef_mine), ("dp", "tensor"), axis=0, tiled=True).astype(
            coef_mine.dtype
        ),
        lax.all_gather(
            grad_query.astype(jnp.bfloat16), ("dp", "tensor"), axis=0, tiled=True
        ).astype(grad_query.dtype),
    )
    own_raw = embed.astype(jnp.float32)
    own_segments = lax.dynamic_slice_in_dim(segments, own_start, share_rows, 0)
    own_docs = jnp.where(own_segments >= NQ_ROW, data_index * NDOC + own_segments - NQ_ROW, -1)
    own_hot = (own_docs[:, None] == jnp.arange(row_count * NDOC, dtype=jnp.int32)[None, :]).astype(
        jnp.float32
    )
    queries_all = (
        emb_rows[:, :query_span].reshape(row_count * query_span, proj_width).astype(jnp.float32)
    )
    grad_embed = jnp.zeros((share_rows, proj_width), jnp.float32)
    for level_index in range(3):
        width = widths[level_index]
        query_unit_all = normalize_cut(queries_all, width)[0].astype(jnp.bfloat16)
        doc_unit_f, doc_part, doc_scale = normalize_cut(own_raw, width)
        expo = jnp.exp(contract_cols(query_unit_all, doc_unit_f.astype(jnp.bfloat16)) / POOL_TEMP)
        spread = contract_cols(coef_all[:, level_index], own_hot, FULL_PRECISION)
        grad_sim = (expo * spread).astype(jnp.bfloat16)
        grad_doc = contract_rows(grad_sim, query_unit_all)
        grad_embed = grad_embed + normalize_back(grad_doc, doc_part, doc_scale, proj_width)
    row_query_grads = lax.dynamic_slice_in_dim(
        grad_query_all, data_index * query_span, query_span, 0
    )
    padded = jnp.pad(row_query_grads, ((0, token_count - query_span), (0, 0)))
    grad_embed = grad_embed + lax.dynamic_slice_in_dim(padded, own_start, share_rows, 0)
    proj_float = w_proj.astype(jnp.float32)
    grad_result = cot.astype(jnp.float32) + contract_cols(grad_embed, proj_float, FULL_PRECISION)
    proj_grad = contract_rows(result_low.astype(jnp.float32), grad_embed, FULL_PRECISION)
    gain_two = jnp.sum(grad_result * unit_two, axis=0)
    shift_two = jnp.sum(grad_result, axis=0)
    grad_second = norm_backward(grad_result, unit_two, rstd_two, gains[1])
    grad_ffn = grad_second.astype(jnp.bfloat16)
    down_bias = jnp.sum(grad_ffn.astype(jnp.float32), axis=0)
    grad_ffn_all = lax.all_gather(grad_ffn, "tensor", axis=0, tiled=True)
    grad_act = contract_cols(grad_ffn_all, full_down)
    down_grad = contract_rows(activation, grad_ffn_all)
    _, gelu_pull = jax.vjp(partial(jax.nn.gelu, approximate=False), up_value)
    grad_up = gelu_pull(grad_act)[0].astype(jnp.bfloat16)
    up_bias = jnp.sum(grad_up.astype(jnp.float32), axis=0)
    up_grad = contract_rows(normed_all, grad_up)
    normed_terms = contract_cols(grad_up, full_up)
    grad_normed = (
        lax.psum_scatter(
            normed_terms.astype(jnp.bfloat16), "tensor", scatter_dimension=0, tiled=True
        ).astype(jnp.float32)
        + grad_second
    )
    gain_one = jnp.sum(grad_normed * unit_one, axis=0)
    shift_one = jnp.sum(grad_normed, axis=0)
    grad_first = norm_backward(grad_normed, unit_one, rstd_one, gains[0])
    grad_attn = grad_first.astype(jnp.bfloat16)
    out_bias = jnp.sum(grad_attn.astype(jnp.float32), axis=0)
    grad_attn_all = lax.all_gather(grad_attn, "tensor", axis=0, tiled=True)
    out_grad = contract_rows(mixed, grad_attn_all)
    grad_mixed = contract_cols(grad_attn_all, full_out).astype(jnp.bfloat16)
    grad_q, grad_k, grad_v = attend_backward(
        query_rows, key_rows, value_rows, segments, log_totals, grad_mixed, block_rows
    )
    stacked_grads = jnp.stack(
        [grad_q.astype(jnp.bfloat16), grad_k.astype(jnp.bfloat16), grad_v.astype(jnp.bfloat16)]
    )
    qkv_grad = jnp.einsum("td,ktw->kdw", tokens, stacked_grads, preferred_element_type=jnp.float32)
    input_terms = jnp.einsum(
        "ktw,kdw->td", stacked_grads, full_qkv, preferred_element_type=jnp.float32
    )
    grad_input = (
        lax.psum_scatter(
            input_terms.astype(jnp.bfloat16), "tensor", scatter_dimension=0, tiled=True
        ).astype(jnp.float32)
        + grad_first
    )
    qv_grad = jnp.stack(
        [
            jnp.sum(stacked_grads[0].astype(jnp.float32), axis=0),
            jnp.sum(stacked_grads[2].astype(jnp.float32), axis=0),
        ]
    )
    qkv_part, out_part, up_part, down_part = (
        lax.psum_scatter(
            qkv_grad.astype(jnp.bfloat16), "dp", scatter_dimension=1, tiled=True
        ).astype(jnp.float32),
        lax.psum_scatter(
            out_grad.astype(jnp.bfloat16), "dp", scatter_dimension=1, tiled=True
        ).astype(jnp.float32),
        lax.psum_scatter(
            up_grad.astype(jnp.bfloat16), "dp", scatter_dimension=0, tiled=True
        ).astype(jnp.float32),
        lax.psum_scatter(
            down_grad.astype(jnp.bfloat16), "dp", scatter_dimension=1, tiled=True
        ).astype(jnp.float32),
    )
    gain_sum, shift_sum, out_bias_sum, down_bias_sum, proj_sum = lax.psum(
        (
            jnp.stack([gain_one, gain_two]),
            jnp.stack([shift_one, shift_two]),
            out_bias,
            down_bias,
            proj_grad,
        ),
        ("dp", "tensor"),
    )
    qv_sum, up_bias_sum = lax.psum((qv_grad, up_bias), "dp")
    return (
        result_low,
        loss_out,
        grad_input.astype(jnp.bfloat16),
        qkv_part,
        qv_sum,
        out_part,
        out_bias_sum,
        gain_sum,
        shift_sum,
        up_part,
        up_bias_sum,
        down_part,
        down_bias_sum,
        proj_sum,
    )


SWAP = [(0, 1), (1, 0)]
TURN = [(0, 0), (1, 2), (2, 1), (3, 3)]
FAR = [(0, 3), (3, 0), (1, 2), (2, 1)]
NEAR = [(0, 1), (1, 0), (2, 3), (3, 2)]
BF = jnp.bfloat16
F32 = jnp.float32


def dot(left, right):
    return jnp.dot(left, right, preferred_element_type=F32)


CORES = ("c", "y")


def tie(value, *others):
    return lax.optimization_barrier((value,) + others)[0]


def tie_all(values, *others):
    return lax.optimization_barrier(tuple(values) + others)[: len(values)]


def exchange(*moves):
    return lax.optimization_barrier(
        tuple(lax.ppermute(value, axis, steps) for value, axis, steps in moves)
    )


def swap(value, axis):
    return lax.ppermute(value, axis, SWAP)


def pair_up(first, second, own_index, axis):
    return jnp.where(
        own_index == 0, jnp.stack([first, second], axis), jnp.stack([second, first], axis)
    )


def far_pair(value, far, z):
    return jnp.where(z < 2, jnp.stack([value, far]), jnp.stack([far, value]))


def whole_line(pair, other, z):
    return jnp.where(
        (z == 0) | (z == 3),
        jnp.stack([pair[0], other[0], other[1], pair[1]]),
        jnp.stack([other[0], pair[0], pair[1], other[1]]),
    )


def first_moves(line):
    half = line.shape[1] // 2
    return ((line[:, :half], "x", SWAP), (line[:, half:], "y", SWAP))


def first_parts(line, moved, x, y):
    half = line.shape[1] // 2
    return (pair_up(line[:, :half], moved[0], x, 1), pair_up(line[:, half:], moved[1], y, 1))


def last_moves(parts):
    return ((parts[0], "y", SWAP), (parts[1], "x", SWAP))


def full_rows(parts, moved, x, y):
    low = pair_up(parts[0], moved[0], y, 2)
    high = pair_up(parts[1], moved[1], x, 1)
    return jnp.concatenate([low, high], axis=3).reshape(-1, low.shape[-1])


def at(blocks, index, axis):
    return lax.dynamic_index_in_dim(blocks, index, axis, keepdims=False)


def side_move(blocks, axis_name, own_index, axis):
    return (at(blocks, 1 - own_index, axis).astype(BF), axis_name, SWAP)


def side_sum(blocks, got, own_index, axis):
    return at(blocks, own_index, axis).astype(F32) + got.astype(F32)


def near_move(line, z):
    ends = (z == 0) | (z == 3)
    outer, inner = jnp.stack([line[0], line[3]]), line[1:3]
    return (jnp.where(ends, inner, outer).astype(BF), "z", NEAR)


def near_sum(line, got, z):
    ends = (z == 0) | (z == 3)
    return jnp.where(ends, jnp.stack([line[0], line[3]]), line[1:3]) + got.astype(F32)


def far_move(pair, z):
    return (jnp.where(z < 2, pair[1], pair[0]).astype(BF), "z", FAR)


def far_sum(pair, got, z):
    return jnp.where(z < 2, pair[0], pair[1]) + got.astype(F32)


def blocks_of(left, right):
    return contract_rows(left, right).astype(BF).reshape(4, 2, 2, 64, right.shape[1])


def sum_moves(blocks, x, y):
    half = blocks.shape[3] // 2
    return (
        side_move(blocks[..., :half, :], "x", x, 1),
        side_move(blocks[..., half:, :], "y", y, 2),
    )


def sum_parts(blocks, moved, x, y):
    half = blocks.shape[3] // 2
    return (
        side_sum(blocks[..., :half, :], moved[0], x, 1),
        side_sum(blocks[..., half:, :], moved[1], y, 2),
    )


def line_moves(parts, x, y):
    return (side_move(parts[0], "y", y, 1), side_move(parts[1], "x", x, 1))


def line_of(parts, moved, x, y):
    return jnp.concatenate(
        [side_sum(parts[0], moved[0], y, 1), side_sum(parts[1], moved[1], x, 1)], axis=1
    )


def tile_bounds(row_lengths, token_count):
    ends = jnp.cumsum(row_lengths)
    span = NQ_ROW * QLEN
    first = jnp.arange(token_count // TILE, dtype=jnp.int32) * TILE - span
    last = first + TILE - 1
    begin = jnp.max(jnp.where(ends[None, :] <= first[:, None], ends[None, :], 0), axis=1)
    end = jnp.min(jnp.where(ends[None, :] > last[:, None], ends[None, :], token_count), axis=1)
    low = jnp.where(first < 0, 0, (begin + span) // TILE)
    high = jnp.where(first < 0, 1, (end + span + TILE - 1) // TILE)
    return jnp.stack([low, high]).astype(jnp.int32)


def token_spans(row_lengths, token_count):
    ends = jnp.cumsum(row_lengths)[:, None]
    span = NQ_ROW * QLEN
    place = jnp.arange(token_count, dtype=jnp.int32)[None, :]
    doc = place - span
    begin = jnp.max(jnp.where(ends <= doc, ends, 0), axis=0) + span
    end = jnp.min(jnp.where(ends > doc, ends, token_count), axis=0) + span
    query = place[0] // QLEN * QLEN
    return jnp.stack(
        [jnp.where(doc[0] < 0, query, begin), jnp.where(doc[0] < 0, query + QLEN, end)]
    ).astype(jnp.int32)


def rows_of(value, start, count):
    return lax.dynamic_slice_in_dim(value, start, count, 0)


TILE = 256
KEYS = 256
LOSS_TILE = 1024
NEG = -1e30


def exact(left, right, dims):
    return lax.dot_general(left, right, (dims, ((), ())), preferred_element_type=F32)


def head_masks(value):
    lane = lax.broadcasted_iota(jnp.int32, value.shape, 1)
    zero = jnp.zeros_like(value)
    return (jnp.where(lane < HEAD_DIM, value, zero), jnp.where(lane < HEAD_DIM, zero, value))


def key_shift(step, spans):
    place = step * KEYS + lax.broadcasted_iota(jnp.int32, (KEYS, TILE), 0)
    inside = (place >= spans[0:1, :]) & (place < spans[1:2, :])
    return jnp.where(inside, 0.0, NEG)


def attend_kernel(bounds, own_ref, qkv_ref, spans, out_ref, lse_ref, held):
    block = pl.program_id(0)
    groups = 2
    pairs = out_ref.shape[1] // 128
    per_group = pairs // groups

    def column(pair, part):
        start = ((pair // per_group) * 3 + part) * per_group + pair % per_group
        return slice(start * 128, (start + 1) * 128)

    queries = [head_masks(own_ref[:, column(pair, 0)] * HEAD_DIM**-0.5) for pair in range(pairs)]
    heads = [(pair, head) for pair in range(pairs) for head in range(2)]

    def score(step, highest):
        rows = pl.ds(pl.multiple_of(step * KEYS, KEYS), KEYS)
        shift = key_shift(step, spans)
        fresh = []
        for index, (pair, head) in enumerate(heads):
            keys = qkv_ref[rows, column(pair, 1)]
            scores = exact(keys, queries[pair][head], ((1,), (1,))) + shift
            held[index, rows, :] = scores
            fresh.append(jnp.maximum(highest[index], jnp.max(scores, axis=0, keepdims=True)))
        return tuple(fresh)

    low = jnp.full((1, TILE), NEG, F32)
    highest = lax.fori_loop(bounds[0, block], bounds[1, block], score, (low,) * len(heads))

    def mix(step, carried):
        rows = pl.ds(pl.multiple_of(step * KEYS, KEYS), KEYS)
        fresh = []
        for index, (pair, head) in enumerate(heads):
            values = qkv_ref[rows, column(pair, 2)]
            total, mixed = carried[index]
            expo = jnp.exp(held[index, rows, :] - highest[index])
            product = exact(values, expo.astype(BF), ((0,), (0,)))
            fresh.append(
                (
                    total + jnp.sum(expo, axis=0, keepdims=True),
                    mixed + product[head * HEAD_DIM : (head + 1) * HEAD_DIM],
                )
            )
        return tuple(fresh)

    start = (jnp.zeros((1, TILE), F32), jnp.zeros((HEAD_DIM, TILE), F32))
    parts = lax.fori_loop(bounds[0, block], bounds[1, block], mix, (start,) * len(heads))
    for pair in range(pairs):
        both = [parts[2 * pair + head][1] / parts[2 * pair + head][0] for head in range(2)]
        mixed = jnp.transpose(jnp.concatenate(both, axis=0))
        out_ref[:, pair * 128 : (pair + 1) * 128] = mixed.astype(BF)
    for index in range(len(heads)):
        lse_ref[index : index + 1, :] = highest[index] + jnp.log(parts[index][0])


def attend(bounds, qkv, spans):
    count, wide = qkv.shape
    heads = wide // 3 // HEAD_DIM
    whole = lambda shape: pl.BlockSpec(shape, lambda i: (0, 0))
    return pl.pallas_call(
        attend_kernel,
        grid=(count // TILE,),
        in_specs=[
            pl.BlockSpec(memory_space=pltpu.SMEM),
            pl.BlockSpec((TILE, wide), lambda i: (i, 0)),
            whole((count, wide)),
            pl.BlockSpec((2, TILE), lambda i: (0, i)),
        ],
        out_specs=[
            pl.BlockSpec((TILE, wide // 3), lambda i: (i, 0)),
            pl.BlockSpec((heads, TILE), lambda i: (0, i)),
        ],
        out_shape=[
            jax.ShapeDtypeStruct((count, wide // 3), BF),
            jax.ShapeDtypeStruct((heads, count), F32),
        ],
        scratch_shapes=[pltpu.VMEM((heads, count, TILE), F32)],
        compiler_params=pltpu.CompilerParams(vmem_limit_bytes=40 << 20),
        cost_estimate=pl.CostEstimate(
            flops=4 * heads * count * count * 64,
            transcendentals=heads * count * count // 2,
            bytes_accessed=4 * count * wide * 2,
        ),
    )(bounds, qkv, qkv, spans)


def attend_back_kernel(
    first, bounds, own_ref, qkv_ref, out_ref, grad_ref, lse_ref, spans,
    grads_ref, sums_ref, key_sum, value_sum,
):
    block = pl.program_id(0)
    pairs = out_ref.shape[1] // 128
    heads = [(pair, head) for pair in range(pairs) for head in range(2)]
    cut = lambda index: slice(index * 128, (index + 1) * 128)

    @pl.when(block == 0)
    def _():
        key_sum[...] = jnp.zeros_like(key_sum)
        value_sum[...] = jnp.zeros_like(value_sum)
        sums_ref[...] = jnp.zeros_like(sums_ref)

    queries = [head_masks(own_ref[:, cut(pair)] * HEAD_DIM**-0.5) for pair in range(pairs)]
    grads = [head_masks(grad_ref[:, cut(pair)]) for pair in range(pairs)]
    picks = head_masks(jnp.ones((8, 128), BF))
    inner = []
    for pair, head in heads:
        product = grad_ref[:, cut(pair)].astype(F32) * out_ref[:, cut(pair)].astype(F32)
        high = product.astype(BF)
        rest = (product - high.astype(F32)).astype(BF)
        inner.append(
            (
                exact(picks[head], high, ((1,), (1,))) + exact(picks[head], rest, ((1,), (1,)))
            )[0:1]
        )
    lse = [lse_ref[first + index : first + index + 1, :] for index in range(len(heads))]

    def step_of(step, carried):
        rows = pl.ds(pl.multiple_of(step * KEYS, KEYS), KEYS)
        shift = key_shift(step, spans)
        fresh = []
        for pair in range(pairs):
            keys = qkv_ref[rows, cut(pairs + pair)]
            values = qkv_ref[rows, cut(2 * pairs + pair)]
            key_add = jnp.zeros((KEYS, 128), F32)
            value_add = jnp.zeros((KEYS, 128), F32)
            for head in range(2):
                index = 2 * pair + head
                scores = exact(keys, queries[pair][head], ((1,), (1,))) + shift
                probs = jnp.exp(scores - lse[index])
                grad_probs = exact(values, grads[pair][head], ((1,), (1,)))
                grad_scores = (probs * (grad_probs - inner[index])).astype(BF)
                value_add = value_add + exact(probs.astype(BF), grads[pair][head], ((1,), (0,)))
                key_add = key_add + exact(grad_scores, queries[pair][head], ((1,), (0,)))
                product = exact(keys, grad_scores, ((0,), (0,)))
                fresh.append(carried[index] + product[head * HEAD_DIM : (head + 1) * HEAD_DIM])
            key_sum[rows, cut(pair)] += key_add
            value_sum[rows, cut(pair)] += value_add
        return tuple(fresh)

    start = jnp.zeros((HEAD_DIM, TILE), F32)
    parts = lax.fori_loop(bounds[0, block], bounds[1, block], step_of, (start,) * len(heads))
    own = pl.ds(pl.multiple_of(block * TILE, TILE), TILE)
    for pair in range(pairs):
        grad_query = jnp.concatenate([parts[2 * pair], parts[2 * pair + 1]], axis=0)
        grad_query = jnp.transpose(grad_query * HEAD_DIM**-0.5).astype(BF)
        grads_ref[own, cut(pair)] = grad_query
        sums_ref[0:1, cut(pair)] += jnp.sum(grad_query.astype(F32), axis=0, keepdims=True)

    @pl.when(block == pl.num_programs(0) - 1)
    def _():
        wide = pairs * 128
        grad_value = value_sum[...].astype(BF)
        grads_ref[:, wide : 2 * wide] = key_sum[...].astype(BF)
        grads_ref[:, 2 * wide :] = grad_value
        sums_ref[1:2, :] = jnp.sum(grad_value.astype(F32), axis=0, keepdims=True)


def attend_back(bounds, group, qkv, mixed, grad_mixed, lse, spans):
    count = qkv.shape[0]
    wide = qkv.shape[1] // 2
    heads = wide // 3 // HEAD_DIM
    whole = lambda shape: pl.BlockSpec(shape, lambda i: (0, 0))
    return pl.pallas_call(
        partial(attend_back_kernel, group * heads),
        grid=(count // TILE,),
        in_specs=[
            pl.BlockSpec(memory_space=pltpu.SMEM),
            pl.BlockSpec((TILE, wide), lambda i: (i, group)),
            pl.BlockSpec((count, wide), lambda i: (0, group)),
            pl.BlockSpec((TILE, wide // 3), lambda i: (i, group)),
            pl.BlockSpec((TILE, wide // 3), lambda i: (i, group)),
            pl.BlockSpec((2 * heads, TILE), lambda i: (0, i)),
            pl.BlockSpec((2, TILE), lambda i: (0, i)),
        ],
        out_specs=[whole((count, wide)), whole((8, wide // 3))],
        out_shape=[
            jax.ShapeDtypeStruct((count, wide), BF),
            jax.ShapeDtypeStruct((8, wide // 3), F32),
        ],
        scratch_shapes=[
            pltpu.VMEM((count, wide // 3), F32),
            pltpu.VMEM((count, wide // 3), F32),
        ],
        compiler_params=pltpu.CompilerParams(vmem_limit_bytes=40 << 20),
        cost_estimate=pl.CostEstimate(
            flops=10 * heads * count * count * 64,
            transcendentals=heads * count * count // 2,
            bytes_accessed=8 * count * wide * 2,
        ),
    )(
        bounds, qkv, qkv, mixed, grad_mixed,
        lse, spans,
    )


ERFC = (
    -1.26551223, 1.00002368, 0.37409196, 0.09678418, -0.18628806,
    0.27886807, -1.13520398, 1.48851587, -0.82215223, 0.17087277,
)


def gelu_pair(value):
    size = jnp.abs(value) * 0.5**0.5
    ratio = 1.0 / (1.0 + 0.5 * size)
    series = jnp.full_like(value, ERFC[-1])
    for factor in ERFC[-2::-1]:
        series = series * ratio + factor
    bell = jnp.exp(-size * size)
    tail = 0.5 * ratio * bell * jnp.exp(series)
    phi = jnp.where(value < 0.0, tail, 1.0 - tail)
    return (value * phi, phi + value * bell * 0.3989422804014327)


def expand_kernel(x_ref, w_ref, b_ref, *refs):
    act_ref, slope_ref = refs[-2:]
    rows = 128
    for start in range(0, x_ref.shape[0], rows):
        part = slice(start, start + rows)
        value = exact(x_ref[part, :], w_ref[...], ((1,), (0,))) + b_ref[...]
        active, slope = gelu_pair(value)
        act_ref[part, :] = active.astype(BF)
        slope_ref[part, :] = slope.astype(BF)


def expand(value, weight, shift, first, tiles, filled=()):
    count, depth = value.shape
    width = shift.shape[1]
    tile = 256
    column = lambda rows: pl.BlockSpec((rows, tile), lambda i: (0, first + i))
    return pl.pallas_call(
        expand_kernel,
        grid=(tiles,),
        in_specs=[
            pl.BlockSpec((count, depth), lambda i: (0, 0)),
            column(depth),
            column(1),
        ]
        + [pl.BlockSpec(memory_space=pl.ANY)] * len(filled),
        out_specs=[column(count)] * 2,
        out_shape=[jax.ShapeDtypeStruct((count, width), BF)] * 2,
        input_output_aliases={3: 0, 4: 1} if filled else {},
        compiler_params=pltpu.CompilerParams(vmem_limit_bytes=32 << 20),
        cost_estimate=pl.CostEstimate(
            flops=2 * count * depth * tile * tiles,
            transcendentals=3 * count * tile * tiles,
            bytes_accessed=2 * (count * depth + depth * tile * tiles + 2 * count * tile * tiles),
        ),
    )(value, weight, shift, *filled)


def cut_levels(raw, cuts):
    lane = lax.broadcasted_iota(jnp.int32, raw.shape, 1)
    levels = []
    for cut in cuts:
        part = jnp.where(lane < cut, raw, 0.0)
        scale = lax.rsqrt(jnp.sum(part * part, axis=1, keepdims=True) + EPS_EMBED)
        levels.append(((part * scale).astype(BF), part, scale))
    return levels


def pool_kernel(cuts, span, q_ref, d_ref, seg_ref, out_ref, units, hot):
    @pl.when(pl.program_id(0) == 0)
    def _():
        raw = d_ref[span:, :].astype(F32)
        for level, parts in enumerate(cut_levels(raw, cuts)):
            units[level] = parts[0]
        doc = lax.broadcasted_iota(jnp.int32, hot.shape, 0)
        hot[...] = (seg_ref[:, span:] == NQ_ROW + doc).astype(F32).astype(BF)

    levels = cut_levels(q_ref[...].astype(F32), cuts)
    for level in range(len(cuts)):
        similar = exact(units[level], levels[level][0], ((1,), (1,)))
        expo = jnp.exp(similar * (1.0 / POOL_TEMP))
        high = expo.astype(BF)
        rest = (expo - high.astype(F32)).astype(BF)
        out_ref[level * NDOC : (level + 1) * NDOC, :] = exact(
            hot[...], high, ((1,), (0,))
        ) + exact(hot[...], rest, ((1,), (0,)))


def pool(cuts, span, queries, row_embed, seg_row):
    count, width = queries.shape
    tokens = row_embed.shape[0]
    whole = lambda shape: pl.BlockSpec(shape, lambda i: (0, 0))
    return pl.pallas_call(
        partial(pool_kernel, cuts, span),
        grid=(count // LOSS_TILE,),
        in_specs=[
            pl.BlockSpec((LOSS_TILE, width), lambda i: (i, 0)),
            whole((tokens, width)),
            whole((1, tokens)),
        ],
        out_specs=pl.BlockSpec((len(cuts) * NDOC, LOSS_TILE), lambda i: (0, i)),
        out_shape=jax.ShapeDtypeStruct((len(cuts) * NDOC, count), F32),
        scratch_shapes=[
            pltpu.VMEM((len(cuts), tokens - span, width), BF),
            pltpu.VMEM((NDOC, tokens - span), BF),
        ],
        compiler_params=pltpu.CompilerParams(vmem_limit_bytes=32 << 20),
        cost_estimate=pl.CostEstimate(
            flops=2 * len(cuts) * count * tokens * 256,
            transcendentals=len(cuts) * count * tokens,
            bytes_accessed=2 * (count + tokens) * width,
        ),
    )(queries, row_embed, seg_row)


def level_back(grad, part, scale):
    return scale * grad - part * (scale * scale * scale) * jnp.sum(
        part * grad, axis=1, keepdims=True
    )


def pool_back_kernel(
    cuts, span, q_ref, d_ref, seg_ref, coef_ref, q_out, d_out, units, units_t, hot, sums
):
    step = pl.program_id(0)

    @pl.when(step == 0)
    def _():
        raw = d_ref[span:, :].astype(F32)
        for level, parts in enumerate(cut_levels(raw, cuts)):
            units[level] = parts[0]
            units_t[level] = jnp.transpose(parts[0])
        doc = lax.broadcasted_iota(jnp.int32, hot.shape, 0)
        wanted = NQ_ROW + jnp.where(doc < NDOC, doc, doc - NDOC)
        hot[...] = (seg_ref[:, span:] == wanted).astype(F32).astype(BF)
        sums[...] = jnp.zeros_like(sums)

    levels = cut_levels(q_ref[...].astype(F32), cuts)
    total = jnp.zeros(q_ref.shape, F32)
    for level in range(len(cuts)):
        unit, part, scale = levels[level]
        similar = exact(units[level], unit, ((1,), (1,)))
        coef = coef_ref[level * NDOC : (level + 1) * NDOC, :]
        high = coef.astype(BF).astype(F32)
        both = jnp.concatenate([high, coef - high], axis=0).astype(BF)
        spread = exact(hot[...], both, ((0,), (0,)))
        grad = (jnp.exp(similar * (1.0 / POOL_TEMP)) * spread).astype(BF)
        sums[level] += exact(grad, unit, ((1,), (0,)))
        grad_unit = jnp.transpose(exact(units_t[level], grad, ((1,), (0,))))
        total = total + level_back(grad_unit, part, scale)
    q_out[...] = total.astype(BF)

    @pl.when(step == pl.num_programs(0) - 1)
    def _():
        raw = d_ref[span:, :].astype(F32)
        result = jnp.zeros(raw.shape, F32)
        for level, parts in enumerate(cut_levels(raw, cuts)):
            lane = lax.broadcasted_iota(jnp.int32, raw.shape, 1)
            grad = jnp.where(lane < cuts[level], sums[level], 0.0)
            result = result + level_back(grad, parts[1], parts[2])
        d_out[...] = result


def pool_back(cuts, span, queries, row_embed, seg_row, coef):
    count, width = queries.shape
    tokens = row_embed.shape[0]
    docs = tokens - span
    whole = lambda shape: pl.BlockSpec(shape, lambda i: (0, 0))
    return pl.pallas_call(
        partial(pool_back_kernel, cuts, span),
        grid=(count // LOSS_TILE,),
        in_specs=[
            pl.BlockSpec((LOSS_TILE, width), lambda i: (i, 0)),
            whole((tokens, width)),
            whole((1, tokens)),
            pl.BlockSpec((len(cuts) * NDOC, LOSS_TILE), lambda i: (0, i)),
        ],
        out_specs=[pl.BlockSpec((LOSS_TILE, width), lambda i: (i, 0)), whole((docs, width))],
        out_shape=[
            jax.ShapeDtypeStruct((count, width), BF),
            jax.ShapeDtypeStruct((docs, width), F32),
        ],
        scratch_shapes=[
            pltpu.VMEM((len(cuts), docs, width), BF),
            pltpu.VMEM((len(cuts), width, docs), BF),
            pltpu.VMEM((2 * NDOC, docs), BF),
            pltpu.VMEM((len(cuts), docs, width), F32),
        ],
        compiler_params=pltpu.CompilerParams(vmem_limit_bytes=32 << 20),
        cost_estimate=pl.CostEstimate(
            flops=2 * len(cuts) * count * docs * 512,
            transcendentals=len(cuts) * count * docs,
            bytes_accessed=4 * (count + tokens) * width,
        ),
    )(queries, row_embed, seg_row, coef)


def local_chip(
    tokens,
    lengths,
    pairing,
    w_qkv,
    b_qv,
    w_out,
    b_out,
    ln_gain,
    ln_bias,
    w_up,
    b_up,
    w_down,
    b_down,
    w_proj,
    cot,
):
    z, x, c, y = (lax.axis_index(name) for name in ("z", "x", "c", "y"))
    chip = 4 * z + 2 * x + y
    token_count, width = tokens.shape
    share = token_count // 2
    own_start, other_start = c * share, (1 - c) * share
    gains, shifts = ln_gain.astype(F32), ln_bias.astype(F32)

    half_width = w_qkv.shape[2]
    up_wide = w_up.shape[1]
    chip_count = lengths.shape[0]
    half_queries = NQ_ROW // 2
    query_total = chip_count * half_queries
    quarter = half_width // 2
    qkv_rows = jnp.concatenate(
        [w_qkv[k][:, g * quarter : (g + 1) * quarter] for g in range(2) for k in range(3)], axis=1
    )
    pair_rows = jnp.pad(pairing.astype(BF), ((0, 63), (0, 128 - half_queries)))
    mid_rows = jnp.concatenate([w_up, w_out.T, pair_rows], axis=1)
    bias = jnp.concatenate([b_qv.reshape(-1), b_up])[None].astype(F32)
    got = exchange(
        (qkv_rows, CORES, TURN), (tokens, "c", SWAP), (bias, "y", SWAP)
    )
    qkv_rows = got[0]
    row = jnp.where(c == y, tokens, got[1])
    bias = jnp.where(c == y, bias, got[2])
    (rest_rows,) = exchange(
        (tie(jnp.concatenate([mid_rows, w_down.T], axis=1), row), CORES, TURN)
    )
    (far,) = exchange((qkv_rows, "z", FAR))
    qkv_pair = far_pair(qkv_rows, far, z)
    mid_wide = mid_rows.shape[1]
    rest_rows = tie(rest_rows, qkv_pair)
    mid_rows, down_rows = rest_rows[:, :mid_wide], rest_rows[:, mid_wide:]
    got = exchange((qkv_pair, "z", NEAR), (mid_rows, "z", FAR))
    qkv_line = whole_line(qkv_pair, got[0], z)
    mid_pair = far_pair(mid_rows, got[1], z)
    got = exchange(*first_moves(qkv_line), (mid_pair, "z", NEAR))
    qkv_parts = first_parts(qkv_line, got, x, y)
    mid_line = whole_line(mid_pair, got[2], z)
    last = last_moves(qkv_parts)
    got = exchange(*last, (tie(down_rows, mid_line), "z", FAR), *first_moves(mid_line))
    full_qkv = full_rows(qkv_parts, got, x, y)
    down_pair = far_pair(down_rows, got[2], z)
    mid_parts = first_parts(mid_line, got[3:], x, y)
    (near,) = exchange((down_pair, "z", NEAR))
    down_line = whole_line(down_pair, near, z)
    got = exchange(*last_moves(mid_parts), *first_moves(down_line))
    full_mid = full_rows(mid_parts, got, x, y)
    down_parts = first_parts(down_line, got[2:], x, y)
    full_out = full_mid[:, up_wide : up_wide + half_width]
    pairs = full_mid[:, up_wide + half_width :].reshape(chip_count, 64, 128)
    pairs = pairs[:, 0, :half_queries].astype(jnp.int32).reshape(1, query_total)
    row_lengths = lax.dynamic_index_in_dim(lengths, chip, 0, keepdims=False)
    segments = segments_of(row_lengths, token_count)
    seg_row, spans = segments[None, :], token_spans(row_lengths, token_count)
    query_span = NQ_ROW * QLEN
    bounds = tile_bounds(row_lengths, token_count)
    no_bias = jnp.zeros((1, quarter), F32)
    qkv_bias = jnp.concatenate(
        [
            part
            for g in range(2)
            for part in (
                bias[:, g * quarter : (g + 1) * quarter],
                no_bias,
                bias[:, half_width + g * quarter : half_width + (g + 1) * quarter],
            )
        ],
        axis=1,
    )
    qkv = (dot(row, full_qkv) + qkv_bias).astype(BF)
    mixed, lse = attend(bounds, tie(qkv, down_line), spans)

    def row_sum(left, weight_t, transposed):
        times = contract_cols if transposed else dot
        theirs = swap(times(left(1), weight_t).astype(BF), "c")
        return times(left(0), weight_t) + theirs.astype(F32)

    def mixed_half(which):
        return rows_of(mixed, other_start if which else own_start, share)

    other_attn = swap(contract_cols(mixed_half(1), full_out).astype(BF), "c")
    other_attn, second_norm = lax.optimization_barrier(
        (other_attn, jnp.stack([gains[1], shifts[1]]))
    )
    second_norm = swap(second_norm, "c")
    second_norm, *down_parts = lax.optimization_barrier((second_norm,) + tuple(down_parts))
    down_got = exchange(*last_moves(down_parts))
    attn_sum = contract_cols(mixed_half(0), full_out) + other_attn.astype(F32)
    own_tokens = rows_of(row, own_start, share).astype(F32)
    normed, unit_one, rstd_one = norm_forward(
        own_tokens + attn_sum + b_out.astype(F32), gains[0], shifts[0]
    )
    normed_low = normed.astype(BF)
    normed_all = jnp.concatenate([normed_low, swap(normed_low, "c")], axis=0)
    activation, slope = expand(
        normed_all, full_mid, bias[:, 2 * half_width :], 0, up_wide // 256
    )
    full_down = full_rows(down_parts, down_got, x, y)
    ffn_sum = row_sum(
        lambda which: activation[which * share : (which + 1) * share], full_down, True
    )
    result, unit_two, rstd_two = norm_forward(
        normed + ffn_sum + b_down.astype(F32), second_norm[0], second_norm[1]
    )
    result_low = result.astype(BF)
    embed = dot(result_low, w_proj).astype(BF)

    other_embed = swap(embed, "c")
    row_embed = jnp.where(
        c == 0,
        jnp.concatenate([embed, other_embed], axis=0),
        jnp.concatenate([other_embed, embed], axis=0),
    )
    half_span = query_span // 2
    own_queries = rows_of(row_embed, c * half_span, half_span)
    chips = ("z", "x", "y")
    queries = lax.all_to_all(
        jnp.broadcast_to(own_queries[None], (chip_count,) + own_queries.shape), chips, 0, 0
    ).reshape(chip_count * half_span, -1)
    queries, own_cot = lax.optimization_barrier((queries, lax.ppermute(cot, CORES, TURN)))
    proj_width = w_proj.shape[1]
    cuts = (proj_width, 3 * proj_width // 4, proj_width // 2)
    sums = pool(cuts, query_span, queries, row_embed, seg_row)
    doc_sizes = jnp.tile(row_lengths.astype(F32), 3)[:, None]
    group = (
        jnp.arange(query_total * QLEN, dtype=jnp.int32)[:, None] // QLEN
        == jnp.arange(query_total, dtype=jnp.int32)[None, :]
    ).astype(F32)
    pooled = POOL_TEMP * jnp.log(sums / doc_sizes)
    logits = jnp.dot(pooled, group, precision=FULL_PRECISION) / LOSS_TEMP
    logits = logits.reshape(3, NDOC, query_total)
    doc_numbers = chip * NDOC + jnp.arange(NDOC, dtype=jnp.int32)
    picked = (doc_numbers[:, None] == pairs).astype(F32)
    own_high = jnp.max(logits, axis=1)
    own_lse = own_high + jnp.log(jnp.sum(jnp.exp(logits - own_high[:, None]), axis=1))
    own_target = jnp.sum(logits * picked, axis=1)
    notes = jnp.pad(jnp.concatenate([own_lse, own_target], axis=1), ((0, 5), (0, 0)))
    notes = lax.all_to_all(
        jnp.broadcast_to(notes[None], (chip_count,) + notes.shape), chips, 0, 0
    )
    chip_lse = notes[:, :3, :query_total]
    high = jnp.max(chip_lse, axis=0)
    all_lse = high + jnp.log(jnp.sum(jnp.exp(chip_lse - high), axis=0))
    target = jnp.sum(notes[:, :3, query_total:], axis=0)
    losses = jnp.sum(all_lse - target, axis=0).reshape(chip_count, half_queries)
    grad_logits = (jnp.exp(logits - all_lse[:, None]) - picked) / LOSS_TEMP
    coefficient = (
        lax.dot_general(
            grad_logits.reshape(3 * NDOC, query_total),
            group,
            (((1,), (1,)), ((), ())),
            precision=FULL_PRECISION,
        )
        / sums
    )
    query_grad, doc_grad = pool_back(cuts, query_span, queries, row_embed, seg_row, coefficient)
    query_grad, y_out = lax.optimization_barrier(
        (query_grad, lax.ppermute(result_low, CORES, TURN))
    )
    grad_blocks = lax.all_to_all(
        query_grad.reshape(chip_count, half_span, proj_width), chips, 0, 0
    )
    own_query_grad = jnp.sum(grad_blocks.astype(F32), axis=0)
    row_grad = jnp.concatenate([jnp.zeros((query_span, proj_width), F32), doc_grad], axis=0)
    row_grad = lax.dynamic_update_slice_in_dim(row_grad, own_query_grad, c * half_span, 0)
    grad_embed = rows_of(row_grad, own_start, share) + swap(
        rows_of(row_grad, other_start, share), "c"
    )

    proj_low = w_proj
    grad_embed_low = grad_embed.astype(BF)
    grad_embed_rest = (grad_embed - grad_embed_low.astype(F32)).astype(BF)
    grad_result = own_cot.astype(F32) + (
        contract_cols(grad_embed_low, proj_low) + contract_cols(grad_embed_rest, proj_low)
    )
    proj_grad = contract_rows(result_low, grad_embed_low) + contract_rows(
        result_low, grad_embed_rest
    )
    gain_two = jnp.sum(grad_result * unit_two, axis=0)
    shift_two = jnp.sum(grad_result, axis=0)
    grad_second = norm_backward(grad_result, unit_two, rstd_two, second_norm[0])
    grad_ffn = grad_second.astype(BF)
    down_bias = jnp.sum(grad_ffn.astype(F32), axis=0)
    other_ffn = swap(grad_ffn, "c")
    grad_ffn_all = jnp.concatenate([grad_ffn, other_ffn], axis=0)
    down_blocks = blocks_of(grad_ffn_all, activation)
    down_moved = exchange(*sum_moves(down_blocks, x, y))
    grad_up = (dot(grad_ffn_all, full_down) * slope.astype(F32)).astype(BF)
    up_bias = jnp.sum(grad_up.astype(F32), axis=0)
    up_blocks = blocks_of(normed_all, tie(grad_up, *down_moved))
    full_up = full_mid[:, :up_wide]
    grad_normed = (
        row_sum(lambda which: grad_up[which * share : (which + 1) * share], full_up, True)
        + grad_second
    )
    gain_one = jnp.sum(grad_normed * unit_one, axis=0)
    shift_one = jnp.sum(grad_normed, axis=0)
    grad_first = norm_backward(grad_normed, unit_one, rstd_one, gains[0])
    grad_attn = grad_first.astype(BF)
    out_bias = jnp.sum(grad_attn.astype(F32), axis=0)
    other_attn = swap(grad_attn, "c")
    grad_attn_all = jnp.where(
        c == 0,
        jnp.concatenate([grad_attn, other_attn], axis=0),
        jnp.concatenate([other_attn, grad_attn], axis=0),
    )
    grad_mixed = dot(grad_attn_all, full_out).astype(BF)
    out_blocks = blocks_of(grad_attn_all, mixed)
    down_parts = sum_parts(down_blocks, down_moved, x, y)
    moved = exchange(*line_moves(down_parts, x, y), *sum_moves(up_blocks, x, y))
    down_line = line_of(down_parts, moved, x, y)
    up_parts = sum_parts(up_blocks, moved[2:], x, y)
    grad_mixed, out_blocks, down_line, *up_parts = lax.optimization_barrier(
        (grad_mixed, out_blocks, down_line) + tuple(up_parts)
    )
    moved = exchange(
        near_move(down_line, z), *line_moves(up_parts, x, y), *sum_moves(out_blocks, x, y)
    )
    grads_one, sums_one = attend_back(bounds, 0, qkv, mixed, grad_mixed, lse, spans)
    down_pair = near_sum(down_line, moved[0], z)
    up_line = line_of(up_parts, moved[1:], x, y)
    out_parts = sum_parts(out_blocks, moved[3:], x, y)
    grad_mixed, down_pair, up_line, *out_parts = lax.optimization_barrier(
        (grad_mixed, down_pair, up_line) + tuple(out_parts)
    )
    up_line, losses = lax.optimization_barrier((up_line, losses))
    moved = exchange(
        far_move(down_pair, z), near_move(up_line, z), *line_moves(out_parts, x, y)
    )
    other_losses = swap(losses, "c")
    proj_given, other_losses, grad_mixed = lax.optimization_barrier(
        (rows_of(proj_grad, other_start, share), other_losses, grad_mixed)
    )
    proj_half = rows_of(proj_grad, own_start, share)
    other_proj = swap(proj_given, "c")
    grad_mixed, other_proj = lax.optimization_barrier((grad_mixed, other_proj))
    proj_half = proj_half + other_proj
    losses = jnp.where(c == y, losses, other_losses)
    loss_out = rows_of(losses, 4 * z + 2 * x + c, 1)
    grads_two, sums_two = attend_back(bounds, 1, qkv, mixed, grad_mixed, lse, spans)
    down_part = far_sum(down_pair, moved[0], z)
    up_pair = near_sum(up_line, moved[1], z)
    out_line = line_of(out_parts, moved[2:], x, y)
    grads_one, grads_two, down_part, up_pair, out_line = lax.optimization_barrier(
        (grads_one, grads_two, down_part, up_pair, out_line)
    )
    shared = jnp.stack([gain_one, gain_two, shift_one, shift_two, out_bias, down_bias])
    half_sums = jnp.concatenate(
        [
            sums_one[0],
            sums_two[0],
            sums_one[1],
            sums_two[1],
            up_bias,
        ]
    )
    small = jnp.concatenate([shared.reshape(-1, 128), half_sums.reshape(-1, 128), proj_half])

    qkv_blocks = jnp.concatenate(
        [blocks_of(row, grads_one), blocks_of(row, grads_two)], axis=4
    )
    qkv_blocks, up_pair, out_line, down_part, small = lax.optimization_barrier(
        (qkv_blocks, up_pair, out_line, down_part, small)
    )
    moved = exchange(
        *sum_moves(qkv_blocks, x, y),
        far_move(up_pair, z),
        near_move(out_line, z),
        (small.astype(BF), "z", NEAR),
    )
    qkv_parts = sum_parts(qkv_blocks, moved, x, y)
    up_part = far_sum(up_pair, moved[2], z)
    out_pair = near_sum(out_line, moved[3], z)
    small = small + moved[4].astype(F32)

    def input_terms(start):
        return contract_cols(
            rows_of(grads_one, start, share), full_qkv[:, : 3 * quarter]
        ) + contract_cols(rows_of(grads_two, start, share), full_qkv[:, 3 * quarter :])

    other_terms = swap(input_terms(other_start).astype(BF), "c")
    grad_input = (input_terms(own_start) + other_terms.astype(F32) + grad_first).astype(BF)
    moved = exchange(*line_moves(qkv_parts, x, y), far_move(out_pair, z), (small.astype(BF), "z", FAR))
    qkv_line = line_of(qkv_parts, moved, x, y)
    out_part = far_sum(out_pair, moved[2], z)
    small = small + moved[3].astype(F32)
    moved = exchange(
        near_move(qkv_line, z),
        (small.astype(BF), "x", SWAP),
        (tie(grad_input, qkv_line), CORES, TURN),
    )
    qkv_pair = near_sum(qkv_line, moved[0], z)
    small = small + moved[1].astype(F32)
    grad_input = moved[2]
    ffn_part = jnp.concatenate([down_part, up_part], axis=1).astype(BF)
    moved = exchange(
        far_move(qkv_pair, z), (small.astype(BF), "y", SWAP), (tie(ffn_part, qkv_pair), CORES, TURN)
    )
    attn_part = jnp.concatenate([far_sum(qkv_pair, moved[0], z), out_part], axis=1).astype(BF)
    small = small + moved[1].astype(F32)
    ffn_part = moved[2].astype(F32)
    down_part, up_part = ffn_part[:, :up_wide], ffn_part[:, up_wide:]
    attn_part, other_small = exchange((attn_part, CORES, TURN), (small.astype(BF), "c", SWAP))
    attn_part = attn_part.astype(F32)
    other_small = other_small.astype(F32)
    qkv_part, out_part = attn_part[:, : 3 * half_width], attn_part[:, 3 * half_width :]
    shared_rows = 6 * width // 128
    small_rows = small.shape[0] - share
    shared = (small[:shared_rows] + other_small[:shared_rows]).reshape(6, width)
    half_sums = jnp.where(
        c == y, small[shared_rows:small_rows], other_small[shared_rows:small_rows]
    ).reshape(-1)
    proj_sum = pair_up(small[small_rows:], other_small[small_rows:], c, 0).reshape(width, -1)
    qkv_part = qkv_part.reshape(64, 2, 3, quarter).transpose(2, 0, 1, 3).reshape(3, 64, half_width)
    return (
        y_out,
        loss_out,
        grad_input,
        qkv_part,
        half_sums[: 2 * half_width].reshape(2, half_width),
        out_part.T,
        shared[4],
        shared[0:2],
        shared[2:4],
        up_part,
        half_sums[2 * half_width :],
        down_part.T,
        shared[5],
        proj_sum,
    )


IN_SPECS = (
    P("dp", None),
    P(),
    P("dp", "tensor"),
    P(None, "dp", "tensor"),
    P(None, "tensor"),
    P("tensor", "dp"),
    P(),
    P(),
    P(),
    P("dp", "tensor"),
    P("tensor"),
    P("tensor", "dp"),
    P(),
    P(),
    P(("dp", "tensor"), None),
)
OUT_SPECS = (
    P(("dp", "tensor"), None),
    P("dp", "tensor"),
    P(("dp", "tensor"), None),
    P(None, "dp", "tensor"),
    P(None, "tensor"),
    P("tensor", "dp"),
    P(),
    P(),
    P(),
    P("dp", "tensor"),
    P("tensor"),
    P("tensor", "dp"),
    P(),
    P(),
)


def solution(mesh):
    if mesh.devices.shape != (16, 2):
        return jax.shard_map(
            local, mesh=mesh, in_specs=IN_SPECS, out_specs=OUT_SPECS, check_vma=False
        )
    names = {"dp": ("z", "x", "c"), "tensor": ("y",)}

    def respec(spec):
        parts = []
        for entry in spec:
            axes = () if entry is None else entry if isinstance(entry, tuple) else (entry,)
            parts.append(tuple(name for axis in axes for name in names[axis]) or None)
        return P(*parts)

    chips = Mesh(mesh.devices.reshape(4, 2, 2, 2), ("z", "x", "c", "y"))
    return jax.shard_map(
        local_chip,
        mesh=chips,
        in_specs=tuple(respec(spec) for spec in IN_SPECS),
        out_specs=tuple(respec(spec) for spec in OUT_SPECS),
        check_vma=False,
    )
```

```python
from functools import partial

import jax
import jax.numpy as jnp
from jax import lax
from jax.experimental import pallas as pl
from jax.experimental.pallas import tpu as pltpu
from jax.sharding import Mesh, PartitionSpec as P

HEAD_DIM = 64
QLEN = 32
NQ_ROW = 8
NDOC = 8


EPS_NORM = 1e-05
EPS_EMBED = 1e-06
POOL_TEMP = 0.1
LOSS_TEMP = 0.1
FULL_PRECISION = lax.Precision.HIGHEST
MASKED_SCORE = -1e30


def shortened(shard):

    def short(part):
        return part.astype(jnp.bfloat16) if part.dtype == jnp.float32 else part

    return jax.tree.map(short, shard)


def contract_rows(left, right, precision=None):
    return lax.dot_general(
        left,
        right,
        (((0,), (0,)), ((), ())),
        precision=precision,
        preferred_element_type=jnp.float32,
    )


def contract_cols(left, right, precision=None):
    return lax.dot_general(
        left,
        right,
        (((1,), (1,)), ((), ())),
        precision=precision,
        preferred_element_type=jnp.float32,
    )


def norm_forward(value, gain, shift):
    centred = value - jnp.mean(value, axis=1, keepdims=True)
    rstd = lax.rsqrt(jnp.mean(centred * centred, axis=1, keepdims=True) + EPS_NORM)
    unit = centred * rstd
    return (unit * gain + shift, unit, rstd)


def norm_backward(grad, unit, rstd, gain):
    scaled = grad * gain
    return rstd * (
        scaled
        - jnp.mean(scaled, axis=1, keepdims=True)
        - unit * jnp.mean(scaled * unit, axis=1, keepdims=True)
    )


def segments_of(row_lengths, token_count):
    position = jnp.arange(token_count, dtype=jnp.int32)
    query_span = NQ_ROW * QLEN
    ends = jnp.cumsum(row_lengths)
    passed = jnp.sum((position[:, None] - query_span >= ends[None, :]).astype(jnp.int32), axis=1)
    return jnp.where(position < query_span, position // QLEN, NQ_ROW + passed)


def normalize_cut(raw, width):
    part = raw[:, :width]
    scale = lax.rsqrt(jnp.sum(part * part, axis=1, keepdims=True) + EPS_EMBED)
    return (part * scale, part, scale)


def normalize_back(grad, part, scale, full_width):
    result = scale * grad - part * (scale * scale * scale) * jnp.sum(
        part * grad, axis=1, keepdims=True
    )
    return jnp.pad(result, ((0, 0), (0, full_width - grad.shape[1])))


def masked_scores(query_block, key_rows, block_segments, segments):
    scores = jnp.einsum(
        "qhd,khd->hqk", query_block, key_rows, preferred_element_type=jnp.float32
    ) * HEAD_DIM ** (-0.5)
    return jnp.where((block_segments[:, None] == segments[None, :])[None], scores, MASKED_SCORE)


def attend_forward(query_rows, key_rows, value_rows, segments, block_rows):
    token_count = query_rows.shape[0]

    def one_block(block_start):
        query_block = lax.dynamic_slice_in_dim(query_rows, block_start, block_rows, 0)
        block_segments = lax.dynamic_slice_in_dim(segments, block_start, block_rows, 0)
        scores = masked_scores(query_block, key_rows, block_segments, segments)
        highest = jnp.max(scores, axis=2, keepdims=True)
        expo = jnp.exp(scores - highest)
        totals = jnp.sum(expo, axis=2, keepdims=True)
        weights = (expo / totals).astype(jnp.bfloat16)
        mixed = jnp.einsum("hqk,khd->qhd", weights, value_rows, preferred_element_type=jnp.float32)
        return (mixed.astype(jnp.bfloat16), (highest + jnp.log(totals))[:, :, 0])

    starts = jnp.arange(token_count // block_rows, dtype=jnp.int32) * block_rows
    mixed, log_totals = lax.map(one_block, starts)
    return (mixed.reshape(token_count, -1), log_totals)


def attend_backward(query_rows, key_rows, value_rows, segments, log_totals, grad_mixed, block_rows):
    token_count, local_heads, head_size = query_rows.shape
    scale = HEAD_DIM ** (-0.5)
    grad_heads = grad_mixed.reshape(token_count, local_heads, head_size)

    def one_block(carried, inputs):
        grad_keys, grad_values = carried
        block_start, block_lse = inputs
        query_block = lax.dynamic_slice_in_dim(query_rows, block_start, block_rows, 0)
        grad_block = lax.dynamic_slice_in_dim(grad_heads, block_start, block_rows, 0)
        block_segments = lax.dynamic_slice_in_dim(segments, block_start, block_rows, 0)
        scores = masked_scores(query_block, key_rows, block_segments, segments)
        probs = jnp.exp(scores - block_lse[:, :, None])
        grad_probs = jnp.einsum(
            "qhd,khd->hqk", grad_block, value_rows, preferred_element_type=jnp.float32
        )
        inner = jnp.sum(probs * grad_probs, axis=2, keepdims=True)
        grad_scores = (probs * (grad_probs - inner)).astype(jnp.bfloat16)
        grad_query = (
            jnp.einsum("hqk,khd->qhd", grad_scores, key_rows, preferred_element_type=jnp.float32)
            * scale
        )
        grad_keys = (
            grad_keys
            + jnp.einsum(
                "hqk,qhd->khd", grad_scores, query_block, preferred_element_type=jnp.float32
            )
            * scale
        )
        grad_values = grad_values + jnp.einsum(
            "hqk,qhd->khd",
            probs.astype(jnp.bfloat16),
            grad_block,
            preferred_element_type=jnp.float32,
        )
        return ((grad_keys, grad_values), grad_query)

    starts = jnp.arange(token_count // block_rows, dtype=jnp.int32) * block_rows
    zero_rows = jnp.zeros(key_rows.shape, jnp.float32)
    (grad_keys, grad_values), grad_queries = lax.scan(
        one_block, (zero_rows, zero_rows), (starts, log_totals)
    )
    flat_width = local_heads * head_size
    return (
        grad_queries.reshape(token_count, flat_width),
        grad_keys.reshape(token_count, flat_width),
        grad_values.reshape(token_count, flat_width),
    )


def local(
    tokens,
    lengths,
    pairing,
    w_qkv,
    b_qv,
    w_out,
    b_out,
    ln_gain,
    ln_bias,
    w_up,
    b_up,
    w_down,
    b_down,
    w_proj,
    cot,
):
    tensor_count = lax.axis_size("tensor")
    tensor_index = lax.axis_index("tensor")
    data_index = lax.axis_index("dp")
    token_count = tokens.shape[0]
    share_rows = token_count // tensor_count
    block_rows = min(512, token_count)
    own_start = tensor_index * share_rows
    full_qkv, full_out, full_up, full_down = (
        lax.all_gather(w_qkv, "dp", axis=1, tiled=True),
        lax.all_gather(w_out, "dp", axis=1, tiled=True),
        lax.all_gather(w_up, "dp", axis=0, tiled=True),
        lax.all_gather(w_down, "dp", axis=1, tiled=True),
    )
    head_width = full_qkv.shape[2]
    local_heads = head_width // HEAD_DIM
    row_lengths = lax.dynamic_index_in_dim(lengths, data_index, 0, keepdims=False)
    segments = segments_of(row_lengths, token_count)
    projected = jnp.einsum("td,kdw->ktw", tokens, full_qkv, preferred_element_type=jnp.float32)
    qv_bias = b_qv.astype(jnp.float32)
    query_rows = (
        (projected[0] + qv_bias[0]).astype(jnp.bfloat16).reshape(token_count, local_heads, HEAD_DIM)
    )
    key_rows = projected[1].astype(jnp.bfloat16).reshape(token_count, local_heads, HEAD_DIM)
    value_rows = (
        (projected[2] + qv_bias[1]).astype(jnp.bfloat16).reshape(token_count, local_heads, HEAD_DIM)
    )
    mixed, log_totals = attend_forward(query_rows, key_rows, value_rows, segments, block_rows)
    attn_terms = jnp.dot(mixed, full_out, preferred_element_type=jnp.float32)
    attn_sum = lax.psum_scatter(
        attn_terms.astype(jnp.bfloat16), "tensor", scatter_dimension=0, tiled=True
    ).astype(jnp.float32)
    own_tokens = lax.dynamic_slice_in_dim(tokens, own_start, share_rows, 0).astype(jnp.float32)
    gains = ln_gain.astype(jnp.float32)
    shifts = ln_bias.astype(jnp.float32)
    normed, unit_one, rstd_one = norm_forward(
        own_tokens + attn_sum + b_out.astype(jnp.float32), gains[0], shifts[0]
    )
    normed_all = lax.all_gather(normed.astype(jnp.bfloat16), "tensor", axis=0, tiled=True)
    up_value = jnp.dot(normed_all, full_up, preferred_element_type=jnp.float32) + b_up.astype(
        jnp.float32
    )
    activation = jax.nn.gelu(up_value, approximate=False).astype(jnp.bfloat16)
    ffn_terms = jnp.dot(activation, full_down, preferred_element_type=jnp.float32)
    ffn_sum = lax.psum_scatter(
        ffn_terms.astype(jnp.bfloat16), "tensor", scatter_dimension=0, tiled=True
    ).astype(jnp.float32)
    result, unit_two, rstd_two = norm_forward(
        normed + ffn_sum + b_down.astype(jnp.float32), gains[1], shifts[1]
    )
    result_low = result.astype(jnp.bfloat16)
    embed = jnp.dot(result_low, w_proj, preferred_element_type=jnp.float32).astype(jnp.bfloat16)
    embed_all = lax.all_gather(embed, ("dp", "tensor"), axis=0, tiled=True)
    row_count = lengths.shape[0]
    proj_width = w_proj.shape[1]
    widths = (proj_width, 3 * proj_width // 4, proj_width // 2)
    per_device = pairing.shape[1]
    query_count = per_device * QLEN
    query_span = NQ_ROW * QLEN
    emb_rows = embed_all.reshape(row_count, token_count, proj_width)
    my_row = lax.dynamic_index_in_dim(emb_rows, data_index, 0, keepdims=False)
    query_raw = lax.dynamic_slice_in_dim(my_row, tensor_index * query_count, query_count, 0).astype(
        jnp.float32
    )
    query_levels = [normalize_cut(query_raw, width) for width in widths]
    query_units = [level_parts[0].astype(jnp.bfloat16) for level_parts in query_levels]
    doc_numbers = jnp.arange(NDOC, dtype=jnp.int32)

    def row_pool(carried, inputs):
        row_emb, lengths_row = inputs
        row_hot = (
            segments_of(lengths_row, token_count)[:, None] == NQ_ROW + doc_numbers[None, :]
        ).astype(jnp.float32)
        row_raw = row_emb.astype(jnp.float32)
        pooled_list = []
        sums_list = []
        for width, query_unit in zip(widths, query_units):
            doc_unit = normalize_cut(row_raw, width)[0].astype(jnp.bfloat16)
            expo = jnp.exp(contract_cols(query_unit, doc_unit) / POOL_TEMP)
            sums = jnp.dot(expo, row_hot, precision=FULL_PRECISION)
            pooled = POOL_TEMP * jnp.log(sums / lengths_row.astype(jnp.float32))
            pooled_list.append(jnp.sum(pooled.reshape(per_device, QLEN, NDOC), axis=1))
            sums_list.append(sums)
        return (carried, (jnp.stack(pooled_list), jnp.stack(sums_list)))

    _, (row_scores, row_sums) = lax.scan(row_pool, 0, (emb_rows, lengths))
    logits = (
        jnp.transpose(row_scores, (2, 1, 0, 3)).reshape(per_device, 3, row_count * NDOC) / LOSS_TEMP
    )
    own_pairs = pairing[0]
    target = jnp.take_along_axis(
        logits, jnp.broadcast_to(own_pairs[:, None, None], (per_device, 3, 1)), axis=2
    )[:, :, 0]
    loss_out = jnp.sum(jax.nn.logsumexp(logits, axis=2) - target, axis=1).reshape(1, per_device)
    picked = (
        jnp.arange(row_count * NDOC, dtype=jnp.int32)[None, None, :] == own_pairs[:, None, None]
    ).astype(jnp.float32)
    grad_logits = (jax.nn.softmax(logits, axis=2) - picked) / LOSS_TEMP
    grad_rows = jnp.transpose(grad_logits.reshape(per_device, 3, row_count, NDOC), (2, 1, 0, 3))
    coefficient = jnp.repeat(grad_rows, QLEN, axis=2) / row_sums

    def row_back(carried, inputs):
        row_emb, lengths_row, row_coef = inputs
        row_hot = (
            segments_of(lengths_row, token_count)[:, None] == NQ_ROW + doc_numbers[None, :]
        ).astype(jnp.float32)
        row_raw = row_emb.astype(jnp.float32)
        new_carried = []
        row_grad = jnp.zeros((token_count, proj_width), jnp.float32)
        for level_index in range(3):
            width = widths[level_index]
            doc_unit_f, doc_part, doc_scale = normalize_cut(row_raw, width)
            doc_unit = doc_unit_f.astype(jnp.bfloat16)
            expo = jnp.exp(contract_cols(query_units[level_index], doc_unit) / POOL_TEMP)
            spread = contract_cols(row_coef[level_index], row_hot, FULL_PRECISION)
            grad_sim = (expo * spread).astype(jnp.bfloat16)
            new_carried.append(
                carried[level_index]
                + jnp.dot(grad_sim, doc_unit, preferred_element_type=jnp.float32)
            )
        return (tuple(new_carried), row_grad)

    zero_query = tuple((jnp.zeros((query_count, width), jnp.float32) for width in widths))
    query_grads, doc_grads = lax.scan(row_back, zero_query, (emb_rows, lengths, coefficient))
    grad_query = jnp.zeros((query_count, proj_width), jnp.float32)
    for level_index in range(3):
        level_parts = query_levels[level_index]
        grad_query = grad_query + normalize_back(
            query_grads[level_index], level_parts[1], level_parts[2], proj_width
        )
    coef_mine = jnp.transpose(coefficient, (2, 1, 0, 3)).reshape(query_count, 3, row_count * NDOC)
    coef_all, grad_query_all = (
        lax.all_gather(shortened(coef_mine), ("dp", "tensor"), axis=0, tiled=True).astype(
            coef_mine.dtype
        ),
        lax.all_gather(
            grad_query.astype(jnp.bfloat16), ("dp", "tensor"), axis=0, tiled=True
        ).astype(grad_query.dtype),
    )
    own_raw = embed.astype(jnp.float32)
    own_segments = lax.dynamic_slice_in_dim(segments, own_start, share_rows, 0)
    own_docs = jnp.where(own_segments >= NQ_ROW, data_index * NDOC + own_segments - NQ_ROW, -1)
    own_hot = (own_docs[:, None] == jnp.arange(row_count * NDOC, dtype=jnp.int32)[None, :]).astype(
        jnp.float32
    )
    queries_all = (
        emb_rows[:, :query_span].reshape(row_count * query_span, proj_width).astype(jnp.float32)
    )
    grad_embed = jnp.zeros((share_rows, proj_width), jnp.float32)
    for level_index in range(3):
        width = widths[level_index]
        query_unit_all = normalize_cut(queries_all, width)[0].astype(jnp.bfloat16)
        doc_unit_f, doc_part, doc_scale = normalize_cut(own_raw, width)
        expo = jnp.exp(contract_cols(query_unit_all, doc_unit_f.astype(jnp.bfloat16)) / POOL_TEMP)
        spread = contract_cols(coef_all[:, level_index], own_hot, FULL_PRECISION)
        grad_sim = (expo * spread).astype(jnp.bfloat16)
        grad_doc = contract_rows(grad_sim, query_unit_all)
        grad_embed = grad_embed + normalize_back(grad_doc, doc_part, doc_scale, proj_width)
    row_query_grads = lax.dynamic_slice_in_dim(
        grad_query_all, data_index * query_span, query_span, 0
    )
    padded = jnp.pad(row_query_grads, ((0, token_count - query_span), (0, 0)))
    grad_embed = grad_embed + lax.dynamic_slice_in_dim(padded, own_start, share_rows, 0)
    proj_float = w_proj.astype(jnp.float32)
    grad_result = cot.astype(jnp.float32) + contract_cols(grad_embed, proj_float, FULL_PRECISION)
    proj_grad = contract_rows(result_low.astype(jnp.float32), grad_embed, FULL_PRECISION)
    gain_two = jnp.sum(grad_result * unit_two, axis=0)
    shift_two = jnp.sum(grad_result, axis=0)
    grad_second = norm_backward(grad_result, unit_two, rstd_two, gains[1])
    grad_ffn = grad_second.astype(jnp.bfloat16)
    down_bias = jnp.sum(grad_ffn.astype(jnp.float32), axis=0)
    grad_ffn_all = lax.all_gather(grad_ffn, "tensor", axis=0, tiled=True)
    grad_act = contract_cols(grad_ffn_all, full_down)
    down_grad = contract_rows(activation, grad_ffn_all)
    _, gelu_pull = jax.vjp(partial(jax.nn.gelu, approximate=False), up_value)
    grad_up = gelu_pull(grad_act)[0].astype(jnp.bfloat16)
    up_bias = jnp.sum(grad_up.astype(jnp.float32), axis=0)
    up_grad = contract_rows(normed_all, grad_up)
    normed_terms = contract_cols(grad_up, full_up)
    grad_normed = (
        lax.psum_scatter(
            normed_terms.astype(jnp.bfloat16), "tensor", scatter_dimension=0, tiled=True
        ).astype(jnp.float32)
        + grad_second
    )
    gain_one = jnp.sum(grad_normed * unit_one, axis=0)
    shift_one = jnp.sum(grad_normed, axis=0)
    grad_first = norm_backward(grad_normed, unit_one, rstd_one, gains[0])
    grad_attn = grad_first.astype(jnp.bfloat16)
    out_bias = jnp.sum(grad_attn.astype(jnp.float32), axis=0)
    grad_attn_all = lax.all_gather(grad_attn, "tensor", axis=0, tiled=True)
    out_grad = contract_rows(mixed, grad_attn_all)
    grad_mixed = contract_cols(grad_attn_all, full_out).astype(jnp.bfloat16)
    grad_q, grad_k, grad_v = attend_backward(
        query_rows, key_rows, value_rows, segments, log_totals, grad_mixed, block_rows
    )
    stacked_grads = jnp.stack(
        [grad_q.astype(jnp.bfloat16), grad_k.astype(jnp.bfloat16), grad_v.astype(jnp.bfloat16)]
    )
    qkv_grad = jnp.einsum("td,ktw->kdw", tokens, stacked_grads, preferred_element_type=jnp.float32)
    input_terms = jnp.einsum(
        "ktw,kdw->td", stacked_grads, full_qkv, preferred_element_type=jnp.float32
    )
    grad_input = (
        lax.psum_scatter(
            input_terms.astype(jnp.bfloat16), "tensor", scatter_dimension=0, tiled=True
        ).astype(jnp.float32)
        + grad_first
    )
    qv_grad = jnp.stack(
        [
            jnp.sum(stacked_grads[0].astype(jnp.float32), axis=0),
            jnp.sum(stacked_grads[2].astype(jnp.float32), axis=0),
        ]
    )
    qkv_part, out_part, up_part, down_part = (
        lax.psum_scatter(
            qkv_grad.astype(jnp.bfloat16), "dp", scatter_dimension=1, tiled=True
        ).astype(jnp.float32),
        lax.psum_scatter(
            out_grad.astype(jnp.bfloat16), "dp", scatter_dimension=1, tiled=True
        ).astype(jnp.float32),
        lax.psum_scatter(
            up_grad.astype(jnp.bfloat16), "dp", scatter_dimension=0, tiled=True
        ).astype(jnp.float32),
        lax.psum_scatter(
            down_grad.astype(jnp.bfloat16), "dp", scatter_dimension=1, tiled=True
        ).astype(jnp.float32),
    )
    gain_sum, shift_sum, out_bias_sum, down_bias_sum, proj_sum = lax.psum(
        (
            jnp.stack([gain_one, gain_two]),
            jnp.stack([shift_one, shift_two]),
            out_bias,
            down_bias,
            proj_grad,
        ),
        ("dp", "tensor"),
    )
    qv_sum, up_bias_sum = lax.psum((qv_grad, up_bias), "dp")
    return (
        result_low,
        loss_out,
        grad_input.astype(jnp.bfloat16),
        qkv_part,
        qv_sum,
        out_part,
        out_bias_sum,
        gain_sum,
        shift_sum,
        up_part,
        up_bias_sum,
        down_part,
        down_bias_sum,
        proj_sum,
    )


SWAP = [(0, 1), (1, 0)]
TURN = [(0, 0), (1, 2), (2, 1), (3, 3)]
FAR = [(0, 3), (3, 0), (1, 2), (2, 1)]
NEAR = [(0, 1), (1, 0), (2, 3), (3, 2)]
BF = jnp.bfloat16
F32 = jnp.float32


def dot(left, right):
    return jnp.dot(left, right, preferred_element_type=F32)


CORES = ("c", "y")


def tie(value, *others):
    return lax.optimization_barrier((value,) + others)[0]


def tie_all(values, *others):
    return lax.optimization_barrier(tuple(values) + others)[: len(values)]


def exchange(*moves):
    return lax.optimization_barrier(
        tuple(lax.ppermute(value, axis, steps) for value, axis, steps in moves)
    )


def swap(value, axis):
    return lax.ppermute(value, axis, SWAP)


def pair_up(first, second, own_index, axis):
    return jnp.where(
        own_index == 0, jnp.stack([first, second], axis), jnp.stack([second, first], axis)
    )


def far_pair(value, far, z):
    return jnp.where(z < 2, jnp.stack([value, far]), jnp.stack([far, value]))


def whole_line(pair, other, z):
    return jnp.where(
        (z == 0) | (z == 3),
        jnp.stack([pair[0], other[0], other[1], pair[1]]),
        jnp.stack([other[0], pair[0], pair[1], other[1]]),
    )


def first_moves(line):
    half = line.shape[1] // 2
    return ((line[:, :half], "x", SWAP), (line[:, half:], "y", SWAP))


def first_parts(line, moved, x, y):
    half = line.shape[1] // 2
    return (pair_up(line[:, :half], moved[0], x, 1), pair_up(line[:, half:], moved[1], y, 1))


def last_moves(parts):
    return ((parts[0], "y", SWAP), (parts[1], "x", SWAP))


def full_rows(parts, moved, x, y):
    low = pair_up(parts[0], moved[0], y, 2)
    high = pair_up(parts[1], moved[1], x, 1)
    return jnp.concatenate([low, high], axis=3).reshape(-1, low.shape[-1])


def at(blocks, index, axis):
    return lax.dynamic_index_in_dim(blocks, index, axis, keepdims=False)


def side_move(blocks, axis_name, own_index, axis):
    return (at(blocks, 1 - own_index, axis).astype(BF), axis_name, SWAP)


def side_sum(blocks, got, own_index, axis):
    return at(blocks, own_index, axis).astype(F32) + got.astype(F32)


def near_move(line, z):
    ends = (z == 0) | (z == 3)
    outer, inner = jnp.stack([line[0], line[3]]), line[1:3]
    return (jnp.where(ends, inner, outer).astype(BF), "z", NEAR)


def near_sum(line, got, z):
    ends = (z == 0) | (z == 3)
    return jnp.where(ends, jnp.stack([line[0], line[3]]), line[1:3]) + got.astype(F32)


def far_move(pair, z):
    return (jnp.where(z < 2, pair[1], pair[0]).astype(BF), "z", FAR)


def far_sum(pair, got, z):
    return jnp.where(z < 2, pair[0], pair[1]) + got.astype(F32)


def blocks_of(left, right):
    return contract_rows(left, right).astype(BF).reshape(4, 2, 2, 64, right.shape[1])


def sum_moves(blocks, x, y):
    half = blocks.shape[3] // 2
    return (
        side_move(blocks[..., :half, :], "x", x, 1),
        side_move(blocks[..., half:, :], "y", y, 2),
    )


def sum_parts(blocks, moved, x, y):
    half = blocks.shape[3] // 2
    return (
        side_sum(blocks[..., :half, :], moved[0], x, 1),
        side_sum(blocks[..., half:, :], moved[1], y, 2),
    )


def line_moves(parts, x, y):
    return (side_move(parts[0], "y", y, 1), side_move(parts[1], "x", x, 1))


def line_of(parts, moved, x, y):
    return jnp.concatenate(
        [side_sum(parts[0], moved[0], y, 1), side_sum(parts[1], moved[1], x, 1)], axis=1
    )


def tile_bounds(row_lengths, token_count):
    ends = jnp.cumsum(row_lengths)
    span = NQ_ROW * QLEN
    first = jnp.arange(token_count // TILE, dtype=jnp.int32) * TILE - span
    last = first + TILE - 1
    begin = jnp.max(jnp.where(ends[None, :] <= first[:, None], ends[None, :], 0), axis=1)
    end = jnp.min(jnp.where(ends[None, :] > last[:, None], ends[None, :], token_count), axis=1)
    low = jnp.where(first < 0, 0, (begin + span) // TILE)
    high = jnp.where(first < 0, 1, (end + span + TILE - 1) // TILE)
    return jnp.stack([low, high]).astype(jnp.int32)


def token_spans(row_lengths, token_count):
    ends = jnp.cumsum(row_lengths)[:, None]
    span = NQ_ROW * QLEN
    place = jnp.arange(token_count, dtype=jnp.int32)[None, :]
    doc = place - span
    begin = jnp.max(jnp.where(ends <= doc, ends, 0), axis=0) + span
    end = jnp.min(jnp.where(ends > doc, ends, token_count), axis=0) + span
    query = place[0] // QLEN * QLEN
    return jnp.stack(
        [jnp.where(doc[0] < 0, query, begin), jnp.where(doc[0] < 0, query + QLEN, end)]
    ).astype(jnp.int32)


def rows_of(value, start, count):
    return lax.dynamic_slice_in_dim(value, start, count, 0)


TILE = 256
KEYS = 256
LOSS_TILE = 1024
NEG = -1e30


def exact(left, right, dims):
    return lax.dot_general(left, right, (dims, ((), ())), preferred_element_type=F32)


def head_masks(value):
    lane = lax.broadcasted_iota(jnp.int32, value.shape, 1)
    zero = jnp.zeros_like(value)
    return (jnp.where(lane < HEAD_DIM, value, zero), jnp.where(lane < HEAD_DIM, zero, value))


def key_shift(step, spans):
    place = step * KEYS + lax.broadcasted_iota(jnp.int32, (KEYS, TILE), 0)
    inside = (place >= spans[0:1, :]) & (place < spans[1:2, :])
    return jnp.where(inside, 0.0, NEG)


def attend_kernel(bounds, own_ref, qkv_ref, spans, out_ref, lse_ref, held):
    block = pl.program_id(0)
    groups = 2
    pairs = out_ref.shape[1] // 128
    per_group = pairs // groups

    def column(pair, part):
        start = ((pair // per_group) * 3 + part) * per_group + pair % per_group
        return slice(start * 128, (start + 1) * 128)

    queries = [head_masks(own_ref[:, column(pair, 0)] * HEAD_DIM**-0.5) for pair in range(pairs)]
    heads = [(pair, head) for pair in range(pairs) for head in range(2)]

    def score(step, highest):
        rows = pl.ds(pl.multiple_of(step * KEYS, KEYS), KEYS)
        shift = key_shift(step, spans)
        fresh = []
        for index, (pair, head) in enumerate(heads):
            keys = qkv_ref[rows, column(pair, 1)]
            scores = exact(keys, queries[pair][head], ((1,), (1,))) + shift
            held[index, rows, :] = scores
            fresh.append(jnp.maximum(highest[index], jnp.max(scores, axis=0, keepdims=True)))
        return tuple(fresh)

    low = jnp.full((1, TILE), NEG, F32)
    highest = lax.fori_loop(bounds[0, block], bounds[1, block], score, (low,) * len(heads))

    def mix(step, carried):
        rows = pl.ds(pl.multiple_of(step * KEYS, KEYS), KEYS)
        fresh = []
        for index, (pair, head) in enumerate(heads):
            values = qkv_ref[rows, column(pair, 2)]
            total, mixed = carried[index]
            expo = jnp.exp(held[index, rows, :] - highest[index])
            product = exact(values, expo.astype(BF), ((0,), (0,)))
            fresh.append(
                (
                    total + jnp.sum(expo, axis=0, keepdims=True),
                    mixed + product[head * HEAD_DIM : (head + 1) * HEAD_DIM],
                )
            )
        return tuple(fresh)

    start = (jnp.zeros((1, TILE), F32), jnp.zeros((HEAD_DIM, TILE), F32))
    parts = lax.fori_loop(bounds[0, block], bounds[1, block], mix, (start,) * len(heads))
    for pair in range(pairs):
        both = [parts[2 * pair + head][1] / parts[2 * pair + head][0] for head in range(2)]
        mixed = jnp.transpose(jnp.concatenate(both, axis=0))
        out_ref[:, pair * 128 : (pair + 1) * 128] = mixed.astype(BF)
    for index in range(len(heads)):
        lse_ref[index : index + 1, :] = highest[index] + jnp.log(parts[index][0])


def attend(bounds, qkv, spans):
    count, wide = qkv.shape
    heads = wide // 3 // HEAD_DIM
    whole = lambda shape: pl.BlockSpec(shape, lambda i: (0, 0))
    return pl.pallas_call(
        attend_kernel,
        grid=(count // TILE,),
        in_specs=[
            pl.BlockSpec(memory_space=pltpu.SMEM),
            pl.BlockSpec((TILE, wide), lambda i: (i, 0)),
            whole((count, wide)),
            pl.BlockSpec((2, TILE), lambda i: (0, i)),
        ],
        out_specs=[
            pl.BlockSpec((TILE, wide // 3), lambda i: (i, 0)),
            pl.BlockSpec((heads, TILE), lambda i: (0, i)),
        ],
        out_shape=[
            jax.ShapeDtypeStruct((count, wide // 3), BF),
            jax.ShapeDtypeStruct((heads, count), F32),
        ],
        scratch_shapes=[pltpu.VMEM((heads, count, TILE), F32)],
        compiler_params=pltpu.CompilerParams(vmem_limit_bytes=40 << 20),
        cost_estimate=pl.CostEstimate(
            flops=4 * heads * count * count * 64,
            transcendentals=heads * count * count // 2,
            bytes_accessed=4 * count * wide * 2,
        ),
    )(bounds, qkv, qkv, spans)


def attend_back_kernel(
    first, bounds, own_ref, qkv_ref, out_ref, grad_ref, lse_ref, spans,
    grads_ref, sums_ref, key_sum, value_sum,
):
    block = pl.program_id(0)
    pairs = out_ref.shape[1] // 128
    heads = [(pair, head) for pair in range(pairs) for head in range(2)]
    cut = lambda index: slice(index * 128, (index + 1) * 128)

    @pl.when(block == 0)
    def _():
        key_sum[...] = jnp.zeros_like(key_sum)
        value_sum[...] = jnp.zeros_like(value_sum)
        sums_ref[...] = jnp.zeros_like(sums_ref)

    queries = [head_masks(own_ref[:, cut(pair)] * HEAD_DIM**-0.5) for pair in range(pairs)]
    grads = [head_masks(grad_ref[:, cut(pair)]) for pair in range(pairs)]
    picks = head_masks(jnp.ones((8, 128), BF))
    inner = []
    for pair, head in heads:
        product = grad_ref[:, cut(pair)].astype(F32) * out_ref[:, cut(pair)].astype(F32)
        high = product.astype(BF)
        rest = (product - high.astype(F32)).astype(BF)
        inner.append(
            (
                exact(picks[head], high, ((1,), (1,))) + exact(picks[head], rest, ((1,), (1,)))
            )[0:1]
        )
    lse = [lse_ref[first + index : first + index + 1, :] for index in range(len(heads))]

    def step_of(step, carried):
        rows = pl.ds(pl.multiple_of(step * KEYS, KEYS), KEYS)
        shift = key_shift(step, spans)
        fresh = []
        for pair in range(pairs):
            keys = qkv_ref[rows, cut(pairs + pair)]
            values = qkv_ref[rows, cut(2 * pairs + pair)]
            key_add = jnp.zeros((KEYS, 128), F32)
            value_add = jnp.zeros((KEYS, 128), F32)
            for head in range(2):
                index = 2 * pair + head
                scores = exact(keys, queries[pair][head], ((1,), (1,))) + shift
                probs = jnp.exp(scores - lse[index])
                grad_probs = exact(values, grads[pair][head], ((1,), (1,)))
                grad_scores = (probs * (grad_probs - inner[index])).astype(BF)
                value_add = value_add + exact(probs.astype(BF), grads[pair][head], ((1,), (0,)))
                key_add = key_add + exact(grad_scores, queries[pair][head], ((1,), (0,)))
                product = exact(keys, grad_scores, ((0,), (0,)))
                fresh.append(carried[index] + product[head * HEAD_DIM : (head + 1) * HEAD_DIM])
            key_sum[rows, cut(pair)] += key_add
            value_sum[rows, cut(pair)] += value_add
        return tuple(fresh)

    start = jnp.zeros((HEAD_DIM, TILE), F32)
    parts = lax.fori_loop(bounds[0, block], bounds[1, block], step_of, (start,) * len(heads))
    own = pl.ds(pl.multiple_of(block * TILE, TILE), TILE)
    for pair in range(pairs):
        grad_query = jnp.concatenate([parts[2 * pair], parts[2 * pair + 1]], axis=0)
        grad_query = jnp.transpose(grad_query * HEAD_DIM**-0.5).astype(BF)
        grads_ref[own, cut(pair)] = grad_query
        sums_ref[0:1, cut(pair)] += jnp.sum(grad_query.astype(F32), axis=0, keepdims=True)

    @pl.when(block == pl.num_programs(0) - 1)
    def _():
        wide = pairs * 128
        grad_value = value_sum[...].astype(BF)
        grads_ref[:, wide : 2 * wide] = key_sum[...].astype(BF)
        grads_ref[:, 2 * wide :] = grad_value
        sums_ref[1:2, :] = jnp.sum(grad_value.astype(F32), axis=0, keepdims=True)


def attend_back(bounds, group, qkv, mixed, grad_mixed, lse, spans):
    count = qkv.shape[0]
    wide = qkv.shape[1] // 2
    heads = wide // 3 // HEAD_DIM
    whole = lambda shape: pl.BlockSpec(shape, lambda i: (0, 0))
    return pl.pallas_call(
        partial(attend_back_kernel, group * heads),
        grid=(count // TILE,),
        in_specs=[
            pl.BlockSpec(memory_space=pltpu.SMEM),
            pl.BlockSpec((TILE, wide), lambda i: (i, group)),
            pl.BlockSpec((count, wide), lambda i: (0, group)),
            pl.BlockSpec((TILE, wide // 3), lambda i: (i, group)),
            pl.BlockSpec((TILE, wide // 3), lambda i: (i, group)),
            pl.BlockSpec((2 * heads, TILE), lambda i: (0, i)),
            pl.BlockSpec((2, TILE), lambda i: (0, i)),
        ],
        out_specs=[whole((count, wide)), whole((8, wide // 3))],
        out_shape=[
            jax.ShapeDtypeStruct((count, wide), BF),
            jax.ShapeDtypeStruct((8, wide // 3), F32),
        ],
        scratch_shapes=[
            pltpu.VMEM((count, wide // 3), F32),
            pltpu.VMEM((count, wide // 3), F32),
        ],
        compiler_params=pltpu.CompilerParams(vmem_limit_bytes=40 << 20),
        cost_estimate=pl.CostEstimate(
            flops=10 * heads * count * count * 64,
            transcendentals=heads * count * count // 2,
            bytes_accessed=8 * count * wide * 2,
        ),
    )(
        bounds, qkv, qkv, mixed, grad_mixed,
        lse, spans,
    )


ERFC = (
    -1.26551223, 1.00002368, 0.37409196, 0.09678418, -0.18628806,
    0.27886807, -1.13520398, 1.48851587, -0.82215223, 0.17087277,
)


def gelu_pair(value):
    size = jnp.abs(value) * 0.5**0.5
    ratio = 1.0 / (1.0 + 0.5 * size)
    series = jnp.full_like(value, ERFC[-1])
    for factor in ERFC[-2::-1]:
        series = series * ratio + factor
    bell = jnp.exp(-size * size)
    tail = 0.5 * ratio * bell * jnp.exp(series)
    phi = jnp.where(value < 0.0, tail, 1.0 - tail)
    return (value * phi, phi + value * bell * 0.3989422804014327)


def expand_kernel(x_ref, w_ref, b_ref, *refs):
    act_ref, slope_ref = refs[-2:]
    rows = 128
    for start in range(0, x_ref.shape[0], rows):
        part = slice(start, start + rows)
        value = exact(x_ref[part, :], w_ref[...], ((1,), (0,))) + b_ref[...]
        active, slope = gelu_pair(value)
        act_ref[part, :] = active.astype(BF)
        slope_ref[part, :] = slope.astype(BF)


def expand(value, weight, shift, first, tiles, filled=()):
    count, depth = value.shape
    width = shift.shape[1]
    tile = 256
    column = lambda rows: pl.BlockSpec((rows, tile), lambda i: (0, first + i))
    return pl.pallas_call(
        expand_kernel,
        grid=(tiles,),
        in_specs=[
            pl.BlockSpec((count, depth), lambda i: (0, 0)),
            column(depth),
            column(1),
        ]
        + [pl.BlockSpec(memory_space=pl.ANY)] * len(filled),
        out_specs=[column(count)] * 2,
        out_shape=[jax.ShapeDtypeStruct((count, width), BF)] * 2,
        input_output_aliases={3: 0, 4: 1} if filled else {},
        compiler_params=pltpu.CompilerParams(vmem_limit_bytes=32 << 20),
        cost_estimate=pl.CostEstimate(
            flops=2 * count * depth * tile * tiles,
            transcendentals=3 * count * tile * tiles,
            bytes_accessed=2 * (count * depth + depth * tile * tiles + 2 * count * tile * tiles),
        ),
    )(value, weight, shift, *filled)


def cut_levels(raw, cuts):
    lane = lax.broadcasted_iota(jnp.int32, raw.shape, 1)
    levels = []
    for cut in cuts:
        part = jnp.where(lane < cut, raw, 0.0)
        scale = lax.rsqrt(jnp.sum(part * part, axis=1, keepdims=True) + EPS_EMBED)
        levels.append(((part * scale).astype(BF), part, scale))
    return levels


def pool_kernel(cuts, span, q_ref, d_ref, seg_ref, out_ref, units, hot):
    @pl.when(pl.program_id(0) == 0)
    def _():
        raw = d_ref[span:, :].astype(F32)
        for level, parts in enumerate(cut_levels(raw, cuts)):
            units[level] = parts[0]
        doc = lax.broadcasted_iota(jnp.int32, hot.shape, 0)
        hot[...] = (seg_ref[:, span:] == NQ_ROW + doc).astype(F32).astype(BF)

    levels = cut_levels(q_ref[...].astype(F32), cuts)
    for level in range(len(cuts)):
        similar = exact(units[level], levels[level][0], ((1,), (1,)))
        expo = jnp.exp(similar * (1.0 / POOL_TEMP))
        high = expo.astype(BF)
        rest = (expo - high.astype(F32)).astype(BF)
        out_ref[level * NDOC : (level + 1) * NDOC, :] = exact(
            hot[...], high, ((1,), (0,))
        ) + exact(hot[...], rest, ((1,), (0,)))


def pool(cuts, span, queries, row_embed, seg_row):
    count, width = queries.shape
    tokens = row_embed.shape[0]
    whole = lambda shape: pl.BlockSpec(shape, lambda i: (0, 0))
    return pl.pallas_call(
        partial(pool_kernel, cuts, span),
        grid=(count // LOSS_TILE,),
        in_specs=[
            pl.BlockSpec((LOSS_TILE, width), lambda i: (i, 0)),
            whole((tokens, width)),
            whole((1, tokens)),
        ],
        out_specs=pl.BlockSpec((len(cuts) * NDOC, LOSS_TILE), lambda i: (0, i)),
        out_shape=jax.ShapeDtypeStruct((len(cuts) * NDOC, count), F32),
        scratch_shapes=[
            pltpu.VMEM((len(cuts), tokens - span, width), BF),
            pltpu.VMEM((NDOC, tokens - span), BF),
        ],
        compiler_params=pltpu.CompilerParams(vmem_limit_bytes=32 << 20),
        cost_estimate=pl.CostEstimate(
            flops=2 * len(cuts) * count * tokens * 256,
            transcendentals=len(cuts) * count * tokens,
            bytes_accessed=2 * (count + tokens) * width,
        ),
    )(queries, row_embed, seg_row)


def level_back(grad, part, scale):
    return scale * grad - part * (scale * scale * scale) * jnp.sum(
        part * grad, axis=1, keepdims=True
    )


def pool_back_kernel(
    cuts, span, q_ref, d_ref, seg_ref, coef_ref, q_out, d_out, units, units_t, hot, sums
):
    step = pl.program_id(0)

    @pl.when(step == 0)
    def _():
        raw = d_ref[span:, :].astype(F32)
        for level, parts in enumerate(cut_levels(raw, cuts)):
            units[level] = parts[0]
            units_t[level] = jnp.transpose(parts[0])
        doc = lax.broadcasted_iota(jnp.int32, hot.shape, 0)
        wanted = NQ_ROW + jnp.where(doc < NDOC, doc, doc - NDOC)
        hot[...] = (seg_ref[:, span:] == wanted).astype(F32).astype(BF)
        sums[...] = jnp.zeros_like(sums)

    levels = cut_levels(q_ref[...].astype(F32), cuts)
    total = jnp.zeros(q_ref.shape, F32)
    for level in range(len(cuts)):
        unit, part, scale = levels[level]
        similar = exact(units[level], unit, ((1,), (1,)))
        coef = coef_ref[level * NDOC : (level + 1) * NDOC, :]
        high = coef.astype(BF).astype(F32)
        both = jnp.concatenate([high, coef - high], axis=0).astype(BF)
        spread = exact(hot[...], both, ((0,), (0,)))
        grad = (jnp.exp(similar * (1.0 / POOL_TEMP)) * spread).astype(BF)
        sums[level] += exact(grad, unit, ((1,), (0,)))
        grad_unit = jnp.transpose(exact(units_t[level], grad, ((1,), (0,))))
        total = total + level_back(grad_unit, part, scale)
    q_out[...] = total.astype(BF)

    @pl.when(step == pl.num_programs(0) - 1)
    def _():
        raw = d_ref[span:, :].astype(F32)
        result = jnp.zeros(raw.shape, F32)
        for level, parts in enumerate(cut_levels(raw, cuts)):
            lane = lax.broadcasted_iota(jnp.int32, raw.shape, 1)
            grad = jnp.where(lane < cuts[level], sums[level], 0.0)
            result = result + level_back(grad, parts[1], parts[2])
        d_out[...] = result


def pool_back(cuts, span, queries, row_embed, seg_row, coef):
    count, width = queries.shape
    tokens = row_embed.shape[0]
    docs = tokens - span
    whole = lambda shape: pl.BlockSpec(shape, lambda i: (0, 0))
    return pl.pallas_call(
        partial(pool_back_kernel, cuts, span),
        grid=(count // LOSS_TILE,),
        in_specs=[
            pl.BlockSpec((LOSS_TILE, width), lambda i: (i, 0)),
            whole((tokens, width)),
            whole((1, tokens)),
            pl.BlockSpec((len(cuts) * NDOC, LOSS_TILE), lambda i: (0, i)),
        ],
        out_specs=[pl.BlockSpec((LOSS_TILE, width), lambda i: (i, 0)), whole((docs, width))],
        out_shape=[
            jax.ShapeDtypeStruct((count, width), BF),
            jax.ShapeDtypeStruct((docs, width), F32),
        ],
        scratch_shapes=[
            pltpu.VMEM((len(cuts), docs, width), BF),
            pltpu.VMEM((len(cuts), width, docs), BF),
            pltpu.VMEM((2 * NDOC, docs), BF),
            pltpu.VMEM((len(cuts), docs, width), F32),
        ],
        compiler_params=pltpu.CompilerParams(vmem_limit_bytes=32 << 20),
        cost_estimate=pl.CostEstimate(
            flops=2 * len(cuts) * count * docs * 512,
            transcendentals=len(cuts) * count * docs,
            bytes_accessed=4 * (count + tokens) * width,
        ),
    )(queries, row_embed, seg_row, coef)


def local_chip(
    tokens,
    lengths,
    pairing,
    w_qkv,
    b_qv,
    w_out,
    b_out,
    ln_gain,
    ln_bias,
    w_up,
    b_up,
    w_down,
    b_down,
    w_proj,
    cot,
):
    z, x, c, y = (lax.axis_index(name) for name in ("z", "x", "c", "y"))
    chip = 4 * z + 2 * x + y
    token_count, width = tokens.shape
    share = token_count // 2
    own_start, other_start = c * share, (1 - c) * share
    gains, shifts = ln_gain.astype(F32), ln_bias.astype(F32)

    half_width = w_qkv.shape[2]
    up_wide = w_up.shape[1]
    chip_count = lengths.shape[0]
    half_queries = NQ_ROW // 2
    query_total = chip_count * half_queries
    quarter = half_width // 2
    qkv_rows = jnp.concatenate(
        [w_qkv[k][:, g * quarter : (g + 1) * quarter] for g in range(2) for k in range(3)], axis=1
    )
    pair_rows = jnp.pad(pairing.astype(BF), ((0, 63), (0, 128 - half_queries)))
    mid_rows = jnp.concatenate([w_up, w_out.T, pair_rows], axis=1)
    bias = jnp.concatenate([b_qv.reshape(-1), b_up])[None].astype(F32)
    got = exchange(
        (qkv_rows, CORES, TURN), (tokens, "c", SWAP), (bias, "y", SWAP)
    )
    qkv_rows = got[0]
    row = jnp.where(c == y, tokens, got[1])
    bias = jnp.where(c == y, bias, got[2])
    (rest_rows,) = exchange(
        (tie(jnp.concatenate([mid_rows, w_down.T], axis=1), row), CORES, TURN)
    )
    (far,) = exchange((qkv_rows, "z", FAR))
    qkv_pair = far_pair(qkv_rows, far, z)
    mid_wide = mid_rows.shape[1]
    rest_rows = tie(rest_rows, qkv_pair)
    mid_rows, down_rows = rest_rows[:, :mid_wide], rest_rows[:, mid_wide:]
    (near,) = exchange((qkv_pair, "z", NEAR))
    qkv_line = whole_line(qkv_pair, near, z)
    (far,) = exchange((mid_rows, "z", FAR))
    mid_pair = far_pair(mid_rows, far, z)
    qkv_parts = first_parts(qkv_line, exchange(*first_moves(qkv_line)), x, y)
    (near,) = exchange((mid_pair, "z", NEAR))
    mid_line = whole_line(mid_pair, near, z)
    full_qkv = full_rows(qkv_parts, exchange(*last_moves(qkv_parts)), x, y)
    down_rows, mid_line = lax.optimization_barrier((down_rows, mid_line))
    got = exchange((down_rows, "z", FAR), *first_moves(mid_line))
    down_pair = far_pair(down_rows, got[0], z)
    mid_parts = first_parts(mid_line, got[1:], x, y)
    (near,) = exchange((down_pair, "z", NEAR))
    down_line = whole_line(down_pair, near, z)
    got = exchange(*last_moves(mid_parts), *first_moves(down_line))
    full_mid = full_rows(mid_parts, got, x, y)
    down_parts = first_parts(down_line, got[2:], x, y)
    full_out = full_mid[:, up_wide : up_wide + half_width]
    pairs = full_mid[:, up_wide + half_width :].reshape(chip_count, 64, 128)
    pairs = pairs[:, 0, :half_queries].astype(jnp.int32).reshape(1, query_total)
    row_lengths = lax.dynamic_index_in_dim(lengths, chip, 0, keepdims=False)
    segments = segments_of(row_lengths, token_count)
    seg_row, spans = segments[None, :], token_spans(row_lengths, token_count)
    query_span = NQ_ROW * QLEN
    bounds = tile_bounds(row_lengths, token_count)
    no_bias = jnp.zeros((1, quarter), F32)
    qkv_bias = jnp.concatenate(
        [
            part
            for g in range(2)
            for part in (
                bias[:, g * quarter : (g + 1) * quarter],
                no_bias,
                bias[:, half_width + g * quarter : half_width + (g + 1) * quarter],
            )
        ],
        axis=1,
    )
    qkv = (dot(row, full_qkv) + qkv_bias).astype(BF)
    mixed, lse = attend(bounds, tie(qkv, down_line), spans)

    def row_sum(left, weight_t, transposed):
        times = contract_cols if transposed else dot
        theirs = swap(times(left(1), weight_t).astype(BF), "c")
        return times(left(0), weight_t) + theirs.astype(F32)

    def mixed_half(which):
        return rows_of(mixed, other_start if which else own_start, share)

    other_attn = swap(contract_cols(mixed_half(1), full_out).astype(BF), "c")
    other_attn, second_norm = lax.optimization_barrier(
        (other_attn, jnp.stack([gains[1], shifts[1]]))
    )
    second_norm = swap(second_norm, "c")
    second_norm, *down_parts = lax.optimization_barrier((second_norm,) + tuple(down_parts))
    down_got = exchange(*last_moves(down_parts))
    attn_sum = contract_cols(mixed_half(0), full_out) + other_attn.astype(F32)
    own_tokens = rows_of(row, own_start, share).astype(F32)
    normed, unit_one, rstd_one = norm_forward(
        own_tokens + attn_sum + b_out.astype(F32), gains[0], shifts[0]
    )
    normed_low = normed.astype(BF)
    normed_all = jnp.concatenate([normed_low, swap(normed_low, "c")], axis=0)
    activation, slope = expand(
        normed_all, full_mid, bias[:, 2 * half_width :], 0, up_wide // 256
    )
    full_down = full_rows(down_parts, down_got, x, y)
    ffn_sum = row_sum(
        lambda which: activation[which * share : (which + 1) * share], full_down, True
    )
    result, unit_two, rstd_two = norm_forward(
        normed + ffn_sum + b_down.astype(F32), second_norm[0], second_norm[1]
    )
    result_low = result.astype(BF)
    embed = dot(result_low, w_proj).astype(BF)

    other_embed = swap(embed, "c")
    row_embed = jnp.where(
        c == 0,
        jnp.concatenate([embed, other_embed], axis=0),
        jnp.concatenate([other_embed, embed], axis=0),
    )
    half_span = query_span // 2
    own_queries = rows_of(row_embed, c * half_span, half_span)
    chips = ("z", "x", "y")
    queries = lax.all_to_all(
        jnp.broadcast_to(own_queries[None], (chip_count,) + own_queries.shape), chips, 0, 0
    ).reshape(chip_count * half_span, -1)
    queries, own_cot = lax.optimization_barrier((queries, lax.ppermute(cot, CORES, TURN)))
    proj_width = w_proj.shape[1]
    cuts = (proj_width, 3 * proj_width // 4, proj_width // 2)
    sums = pool(cuts, query_span, queries, row_embed, seg_row)
    doc_sizes = jnp.tile(row_lengths.astype(F32), 3)[:, None]
    group = (
        jnp.arange(query_total * QLEN, dtype=jnp.int32)[:, None] // QLEN
        == jnp.arange(query_total, dtype=jnp.int32)[None, :]
    ).astype(F32)
    pooled = POOL_TEMP * jnp.log(sums / doc_sizes)
    logits = jnp.dot(pooled, group, precision=FULL_PRECISION) / LOSS_TEMP
    logits = logits.reshape(3, NDOC, query_total)
    doc_numbers = chip * NDOC + jnp.arange(NDOC, dtype=jnp.int32)
    picked = (doc_numbers[:, None] == pairs).astype(F32)
    own_high = jnp.max(logits, axis=1)
    own_lse = own_high + jnp.log(jnp.sum(jnp.exp(logits - own_high[:, None]), axis=1))
    own_target = jnp.sum(logits * picked, axis=1)
    notes = jnp.pad(jnp.concatenate([own_lse, own_target], axis=1), ((0, 5), (0, 0)))
    notes = lax.all_to_all(
        jnp.broadcast_to(notes[None], (chip_count,) + notes.shape), chips, 0, 0
    )
    chip_lse = notes[:, :3, :query_total]
    high = jnp.max(chip_lse, axis=0)
    all_lse = high + jnp.log(jnp.sum(jnp.exp(chip_lse - high), axis=0))
    target = jnp.sum(notes[:, :3, query_total:], axis=0)
    losses = jnp.sum(all_lse - target, axis=0).reshape(chip_count, half_queries)
    grad_logits = (jnp.exp(logits - all_lse[:, None]) - picked) / LOSS_TEMP
    coefficient = (
        lax.dot_general(
            grad_logits.reshape(3 * NDOC, query_total),
            group,
            (((1,), (1,)), ((), ())),
            precision=FULL_PRECISION,
        )
        / sums
    )
    query_grad, doc_grad = pool_back(cuts, query_span, queries, row_embed, seg_row, coefficient)
    query_grad, y_out = lax.optimization_barrier(
        (query_grad, lax.ppermute(result_low, CORES, TURN))
    )
    grad_blocks = lax.all_to_all(
        query_grad.reshape(chip_count, half_span, proj_width), chips, 0, 0
    )
    own_query_grad = jnp.sum(grad_blocks.astype(F32), axis=0)
    row_grad = jnp.concatenate([jnp.zeros((query_span, proj_width), F32), doc_grad], axis=0)
    row_grad = lax.dynamic_update_slice_in_dim(row_grad, own_query_grad, c * half_span, 0)
    grad_embed = rows_of(row_grad, own_start, share) + swap(
        rows_of(row_grad, other_start, share), "c"
    )

    proj_low = w_proj
    grad_embed_low = grad_embed.astype(BF)
    grad_embed_rest = (grad_embed - grad_embed_low.astype(F32)).astype(BF)
    grad_result = own_cot.astype(F32) + (
        contract_cols(grad_embed_low, proj_low) + contract_cols(grad_embed_rest, proj_low)
    )
    proj_grad = contract_rows(result_low, grad_embed_low) + contract_rows(
        result_low, grad_embed_rest
    )
    gain_two = jnp.sum(grad_result * unit_two, axis=0)
    shift_two = jnp.sum(grad_result, axis=0)
    grad_second = norm_backward(grad_result, unit_two, rstd_two, second_norm[0])
    grad_ffn = grad_second.astype(BF)
    down_bias = jnp.sum(grad_ffn.astype(F32), axis=0)
    other_ffn = swap(grad_ffn, "c")
    grad_ffn_all = jnp.concatenate([grad_ffn, other_ffn], axis=0)
    down_blocks = blocks_of(grad_ffn_all, activation)
    down_moved = exchange(*sum_moves(down_blocks, x, y))
    grad_up = (dot(grad_ffn_all, full_down) * slope.astype(F32)).astype(BF)
    up_bias = jnp.sum(grad_up.astype(F32), axis=0)
    up_blocks = blocks_of(normed_all, tie(grad_up, *down_moved))
    full_up = full_mid[:, :up_wide]
    grad_normed = (
        row_sum(lambda which: grad_up[which * share : (which + 1) * share], full_up, True)
        + grad_second
    )
    gain_one = jnp.sum(grad_normed * unit_one, axis=0)
    shift_one = jnp.sum(grad_normed, axis=0)
    grad_first = norm_backward(grad_normed, unit_one, rstd_one, gains[0])
    grad_attn = grad_first.astype(BF)
    out_bias = jnp.sum(grad_attn.astype(F32), axis=0)
    other_attn = swap(grad_attn, "c")
    grad_attn_all = jnp.where(
        c == 0,
        jnp.concatenate([grad_attn, other_attn], axis=0),
        jnp.concatenate([other_attn, grad_attn], axis=0),
    )
    grad_mixed = dot(grad_attn_all, full_out).astype(BF)
    out_blocks = blocks_of(grad_attn_all, mixed)
    down_parts = sum_parts(down_blocks, down_moved, x, y)
    moved = exchange(*line_moves(down_parts, x, y), *sum_moves(up_blocks, x, y))
    down_line = line_of(down_parts, moved, x, y)
    up_parts = sum_parts(up_blocks, moved[2:], x, y)
    grad_mixed, out_blocks, down_line, *up_parts = lax.optimization_barrier(
        (grad_mixed, out_blocks, down_line) + tuple(up_parts)
    )
    moved = exchange(
        near_move(down_line, z), *line_moves(up_parts, x, y), *sum_moves(out_blocks, x, y)
    )
    grads_one, sums_one = attend_back(bounds, 0, qkv, mixed, grad_mixed, lse, spans)
    down_pair = near_sum(down_line, moved[0], z)
    up_line = line_of(up_parts, moved[1:], x, y)
    out_parts = sum_parts(out_blocks, moved[3:], x, y)
    grad_mixed, down_pair, up_line, *out_parts = lax.optimization_barrier(
        (grad_mixed, down_pair, up_line) + tuple(out_parts)
    )
    up_line, losses = lax.optimization_barrier((up_line, losses))
    moved = exchange(
        far_move(down_pair, z), near_move(up_line, z), *line_moves(out_parts, x, y)
    )
    other_losses = swap(losses, "c")
    proj_given, other_losses, grad_mixed = lax.optimization_barrier(
        (rows_of(proj_grad, other_start, share), other_losses, grad_mixed)
    )
    proj_half = rows_of(proj_grad, own_start, share)
    other_proj = swap(proj_given, "c")
    grad_mixed, other_proj = lax.optimization_barrier((grad_mixed, other_proj))
    proj_half = proj_half + other_proj
    losses = jnp.where(c == y, losses, other_losses)
    loss_out = rows_of(losses, 4 * z + 2 * x + c, 1)
    grads_two, sums_two = attend_back(bounds, 1, qkv, mixed, grad_mixed, lse, spans)
    down_part = far_sum(down_pair, moved[0], z)
    up_pair = near_sum(up_line, moved[1], z)
    out_line = line_of(out_parts, moved[2:], x, y)
    grads_one, grads_two, down_part, up_pair, out_line = lax.optimization_barrier(
        (grads_one, grads_two, down_part, up_pair, out_line)
    )
    shared = jnp.stack([gain_one, gain_two, shift_one, shift_two, out_bias, down_bias])
    half_sums = jnp.concatenate(
        [
            sums_one[0],
            sums_two[0],
            sums_one[1],
            sums_two[1],
            up_bias,
        ]
    )
    small = jnp.concatenate([shared.reshape(-1, 128), half_sums.reshape(-1, 128), proj_half])

    qkv_blocks = jnp.concatenate(
        [blocks_of(row, grads_one), blocks_of(row, grads_two)], axis=4
    )
    qkv_blocks, up_pair, out_line, down_part, small = lax.optimization_barrier(
        (qkv_blocks, up_pair, out_line, down_part, small)
    )
    moved = exchange(
        *sum_moves(qkv_blocks, x, y),
        far_move(up_pair, z),
        near_move(out_line, z),
        (small.astype(BF), "z", NEAR),
    )
    qkv_parts = sum_parts(qkv_blocks, moved, x, y)
    up_part = far_sum(up_pair, moved[2], z)
    out_pair = near_sum(out_line, moved[3], z)
    small = small + moved[4].astype(F32)

    def input_terms(start):
        return contract_cols(
            rows_of(grads_one, start, share), full_qkv[:, : 3 * quarter]
        ) + contract_cols(rows_of(grads_two, start, share), full_qkv[:, 3 * quarter :])

    other_terms = swap(input_terms(other_start).astype(BF), "c")
    grad_input = (input_terms(own_start) + other_terms.astype(F32) + grad_first).astype(BF)
    moved = exchange(*line_moves(qkv_parts, x, y), far_move(out_pair, z), (small.astype(BF), "z", FAR))
    qkv_line = line_of(qkv_parts, moved, x, y)
    out_part = far_sum(out_pair, moved[2], z)
    small = small + moved[3].astype(F32)
    moved = exchange(
        near_move(qkv_line, z),
        (small.astype(BF), "x", SWAP),
        (tie(grad_input, qkv_line), CORES, TURN),
    )
    qkv_pair = near_sum(qkv_line, moved[0], z)
    small = small + moved[1].astype(F32)
    grad_input = moved[2]
    ffn_part = jnp.concatenate([down_part, up_part], axis=1).astype(BF)
    moved = exchange(
        far_move(qkv_pair, z), (small.astype(BF), "y", SWAP), (tie(ffn_part, qkv_pair), CORES, TURN)
    )
    attn_part = jnp.concatenate([far_sum(qkv_pair, moved[0], z), out_part], axis=1).astype(BF)
    small = small + moved[1].astype(F32)
    ffn_part = moved[2].astype(F32)
    down_part, up_part = ffn_part[:, :up_wide], ffn_part[:, up_wide:]
    attn_part, other_small = exchange((attn_part, CORES, TURN), (small.astype(BF), "c", SWAP))
    attn_part = attn_part.astype(F32)
    other_small = other_small.astype(F32)
    qkv_part, out_part = attn_part[:, : 3 * half_width], attn_part[:, 3 * half_width :]
    shared_rows = 6 * width // 128
    small_rows = small.shape[0] - share
    shared = (small[:shared_rows] + other_small[:shared_rows]).reshape(6, width)
    half_sums = jnp.where(
        c == y, small[shared_rows:small_rows], other_small[shared_rows:small_rows]
    ).reshape(-1)
    proj_sum = pair_up(small[small_rows:], other_small[small_rows:], c, 0).reshape(width, -1)
    qkv_part = qkv_part.reshape(64, 2, 3, quarter).transpose(2, 0, 1, 3).reshape(3, 64, half_width)
    return (
        y_out,
        loss_out,
        grad_input,
        qkv_part,
        half_sums[: 2 * half_width].reshape(2, half_width),
        out_part.T,
        shared[4],
        shared[0:2],
        shared[2:4],
        up_part,
        half_sums[2 * half_width :],
        down_part.T,
        shared[5],
        proj_sum,
    )


IN_SPECS = (
    P("dp", None),
    P(),
    P("dp", "tensor"),
    P(None, "dp", "tensor"),
    P(None, "tensor"),
    P("tensor", "dp"),
    P(),
    P(),
    P(),
    P("dp", "tensor"),
    P("tensor"),
    P("tensor", "dp"),
    P(),
    P(),
    P(("dp", "tensor"), None),
)
OUT_SPECS = (
    P(("dp", "tensor"), None),
    P("dp", "tensor"),
    P(("dp", "tensor"), None),
    P(None, "dp", "tensor"),
    P(None, "tensor"),
    P("tensor", "dp"),
    P(),
    P(),
    P(),
    P("dp", "tensor"),
    P("tensor"),
    P("tensor", "dp"),
    P(),
    P(),
)


def solution(mesh):
    if mesh.devices.shape != (16, 2):
        return jax.shard_map(
            local, mesh=mesh, in_specs=IN_SPECS, out_specs=OUT_SPECS, check_vma=False
        )
    names = {"dp": ("z", "x", "c"), "tensor": ("y",)}

    def respec(spec):
        parts = []
        for entry in spec:
            axes = () if entry is None else entry if isinstance(entry, tuple) else (entry,)
            parts.append(tuple(name for axis in axes for name in names[axis]) or None)
        return P(*parts)

    chips = Mesh(mesh.devices.reshape(4, 2, 2, 2), ("z", "x", "c", "y"))
    return jax.shard_map(
        local_chip,
        mesh=chips,
        in_specs=tuple(respec(spec) for spec in IN_SPECS),
        out_specs=tuple(respec(spec) for spec in OUT_SPECS),
        check_vma=False,
    )
```

```python
from functools import partial

import jax
import jax.numpy as jnp
from jax import lax
from jax.experimental import pallas as pl
from jax.experimental.pallas import tpu as pltpu
from jax.sharding import Mesh, PartitionSpec as P

HEAD_DIM = 64
QLEN = 32
NQ_ROW = 8
NDOC = 8


EPS_NORM = 1e-05
EPS_EMBED = 1e-06
POOL_TEMP = 0.1
LOSS_TEMP = 0.1
FULL_PRECISION = lax.Precision.HIGHEST
MASKED_SCORE = -1e30


def shortened(shard):

    def short(part):
        return part.astype(jnp.bfloat16) if part.dtype == jnp.float32 else part

    return jax.tree.map(short, shard)


def contract_rows(left, right, precision=None):
    return lax.dot_general(
        left,
        right,
        (((0,), (0,)), ((), ())),
        precision=precision,
        preferred_element_type=jnp.float32,
    )


def contract_cols(left, right, precision=None):
    return lax.dot_general(
        left,
        right,
        (((1,), (1,)), ((), ())),
        precision=precision,
        preferred_element_type=jnp.float32,
    )


def norm_forward(value, gain, shift):
    centred = value - jnp.mean(value, axis=1, keepdims=True)
    rstd = lax.rsqrt(jnp.mean(centred * centred, axis=1, keepdims=True) + EPS_NORM)
    unit = centred * rstd
    return (unit * gain + shift, unit, rstd)


def norm_backward(grad, unit, rstd, gain):
    scaled = grad * gain
    return rstd * (
        scaled
        - jnp.mean(scaled, axis=1, keepdims=True)
        - unit * jnp.mean(scaled * unit, axis=1, keepdims=True)
    )


def segments_of(row_lengths, token_count):
    position = jnp.arange(token_count, dtype=jnp.int32)
    query_span = NQ_ROW * QLEN
    ends = jnp.cumsum(row_lengths)
    passed = jnp.sum((position[:, None] - query_span >= ends[None, :]).astype(jnp.int32), axis=1)
    return jnp.where(position < query_span, position // QLEN, NQ_ROW + passed)


def normalize_cut(raw, width):
    part = raw[:, :width]
    scale = lax.rsqrt(jnp.sum(part * part, axis=1, keepdims=True) + EPS_EMBED)
    return (part * scale, part, scale)


def normalize_back(grad, part, scale, full_width):
    result = scale * grad - part * (scale * scale * scale) * jnp.sum(
        part * grad, axis=1, keepdims=True
    )
    return jnp.pad(result, ((0, 0), (0, full_width - grad.shape[1])))


def masked_scores(query_block, key_rows, block_segments, segments):
    scores = jnp.einsum(
        "qhd,khd->hqk", query_block, key_rows, preferred_element_type=jnp.float32
    ) * HEAD_DIM ** (-0.5)
    return jnp.where((block_segments[:, None] == segments[None, :])[None], scores, MASKED_SCORE)


def attend_forward(query_rows, key_rows, value_rows, segments, block_rows):
    token_count = query_rows.shape[0]

    def one_block(block_start):
        query_block = lax.dynamic_slice_in_dim(query_rows, block_start, block_rows, 0)
        block_segments = lax.dynamic_slice_in_dim(segments, block_start, block_rows, 0)
        scores = masked_scores(query_block, key_rows, block_segments, segments)
        highest = jnp.max(scores, axis=2, keepdims=True)
        expo = jnp.exp(scores - highest)
        totals = jnp.sum(expo, axis=2, keepdims=True)
        weights = (expo / totals).astype(jnp.bfloat16)
        mixed = jnp.einsum("hqk,khd->qhd", weights, value_rows, preferred_element_type=jnp.float32)
        return (mixed.astype(jnp.bfloat16), (highest + jnp.log(totals))[:, :, 0])

    starts = jnp.arange(token_count // block_rows, dtype=jnp.int32) * block_rows
    mixed, log_totals = lax.map(one_block, starts)
    return (mixed.reshape(token_count, -1), log_totals)


def attend_backward(query_rows, key_rows, value_rows, segments, log_totals, grad_mixed, block_rows):
    token_count, local_heads, head_size = query_rows.shape
    scale = HEAD_DIM ** (-0.5)
    grad_heads = grad_mixed.reshape(token_count, local_heads, head_size)

    def one_block(carried, inputs):
        grad_keys, grad_values = carried
        block_start, block_lse = inputs
        query_block = lax.dynamic_slice_in_dim(query_rows, block_start, block_rows, 0)
        grad_block = lax.dynamic_slice_in_dim(grad_heads, block_start, block_rows, 0)
        block_segments = lax.dynamic_slice_in_dim(segments, block_start, block_rows, 0)
        scores = masked_scores(query_block, key_rows, block_segments, segments)
        probs = jnp.exp(scores - block_lse[:, :, None])
        grad_probs = jnp.einsum(
            "qhd,khd->hqk", grad_block, value_rows, preferred_element_type=jnp.float32
        )
        inner = jnp.sum(probs * grad_probs, axis=2, keepdims=True)
        grad_scores = (probs * (grad_probs - inner)).astype(jnp.bfloat16)
        grad_query = (
            jnp.einsum("hqk,khd->qhd", grad_scores, key_rows, preferred_element_type=jnp.float32)
            * scale
        )
        grad_keys = (
            grad_keys
            + jnp.einsum(
                "hqk,qhd->khd", grad_scores, query_block, preferred_element_type=jnp.float32
            )
            * scale
        )
        grad_values = grad_values + jnp.einsum(
            "hqk,qhd->khd",
            probs.astype(jnp.bfloat16),
            grad_block,
            preferred_element_type=jnp.float32,
        )
        return ((grad_keys, grad_values), grad_query)

    starts = jnp.arange(token_count // block_rows, dtype=jnp.int32) * block_rows
    zero_rows = jnp.zeros(key_rows.shape, jnp.float32)
    (grad_keys, grad_values), grad_queries = lax.scan(
        one_block, (zero_rows, zero_rows), (starts, log_totals)
    )
    flat_width = local_heads * head_size
    return (
        grad_queries.reshape(token_count, flat_width),
        grad_keys.reshape(token_count, flat_width),
        grad_values.reshape(token_count, flat_width),
    )


def local(
    tokens,
    lengths,
    pairing,
    w_qkv,
    b_qv,
    w_out,
    b_out,
    ln_gain,
    ln_bias,
    w_up,
    b_up,
    w_down,
    b_down,
    w_proj,
    cot,
):
    tensor_count = lax.axis_size("tensor")
    tensor_index = lax.axis_index("tensor")
    data_index = lax.axis_index("dp")
    token_count = tokens.shape[0]
    share_rows = token_count // tensor_count
    block_rows = min(512, token_count)
    own_start = tensor_index * share_rows
    full_qkv, full_out, full_up, full_down = (
        lax.all_gather(w_qkv, "dp", axis=1, tiled=True),
        lax.all_gather(w_out, "dp", axis=1, tiled=True),
        lax.all_gather(w_up, "dp", axis=0, tiled=True),
        lax.all_gather(w_down, "dp", axis=1, tiled=True),
    )
    head_width = full_qkv.shape[2]
    local_heads = head_width // HEAD_DIM
    row_lengths = lax.dynamic_index_in_dim(lengths, data_index, 0, keepdims=False)
    segments = segments_of(row_lengths, token_count)
    projected = jnp.einsum("td,kdw->ktw", tokens, full_qkv, preferred_element_type=jnp.float32)
    qv_bias = b_qv.astype(jnp.float32)
    query_rows = (
        (projected[0] + qv_bias[0]).astype(jnp.bfloat16).reshape(token_count, local_heads, HEAD_DIM)
    )
    key_rows = projected[1].astype(jnp.bfloat16).reshape(token_count, local_heads, HEAD_DIM)
    value_rows = (
        (projected[2] + qv_bias[1]).astype(jnp.bfloat16).reshape(token_count, local_heads, HEAD_DIM)
    )
    mixed, log_totals = attend_forward(query_rows, key_rows, value_rows, segments, block_rows)
    attn_terms = jnp.dot(mixed, full_out, preferred_element_type=jnp.float32)
    attn_sum = lax.psum_scatter(
        attn_terms.astype(jnp.bfloat16), "tensor", scatter_dimension=0, tiled=True
    ).astype(jnp.float32)
    own_tokens = lax.dynamic_slice_in_dim(tokens, own_start, share_rows, 0).astype(jnp.float32)
    gains = ln_gain.astype(jnp.float32)
    shifts = ln_bias.astype(jnp.float32)
    normed, unit_one, rstd_one = norm_forward(
        own_tokens + attn_sum + b_out.astype(jnp.float32), gains[0], shifts[0]
    )
    normed_all = lax.all_gather(normed.astype(jnp.bfloat16), "tensor", axis=0, tiled=True)
    up_value = jnp.dot(normed_all, full_up, preferred_element_type=jnp.float32) + b_up.astype(
        jnp.float32
    )
    activation = jax.nn.gelu(up_value, approximate=False).astype(jnp.bfloat16)
    ffn_terms = jnp.dot(activation, full_down, preferred_element_type=jnp.float32)
    ffn_sum = lax.psum_scatter(
        ffn_terms.astype(jnp.bfloat16), "tensor", scatter_dimension=0, tiled=True
    ).astype(jnp.float32)
    result, unit_two, rstd_two = norm_forward(
        normed + ffn_sum + b_down.astype(jnp.float32), gains[1], shifts[1]
    )
    result_low = result.astype(jnp.bfloat16)
    embed = jnp.dot(result_low, w_proj, preferred_element_type=jnp.float32).astype(jnp.bfloat16)
    embed_all = lax.all_gather(embed, ("dp", "tensor"), axis=0, tiled=True)
    row_count = lengths.shape[0]
    proj_width = w_proj.shape[1]
    widths = (proj_width, 3 * proj_width // 4, proj_width // 2)
    per_device = pairing.shape[1]
    query_count = per_device * QLEN
    query_span = NQ_ROW * QLEN
    emb_rows = embed_all.reshape(row_count, token_count, proj_width)
    my_row = lax.dynamic_index_in_dim(emb_rows, data_index, 0, keepdims=False)
    query_raw = lax.dynamic_slice_in_dim(my_row, tensor_index * query_count, query_count, 0).astype(
        jnp.float32
    )
    query_levels = [normalize_cut(query_raw, width) for width in widths]
    query_units = [level_parts[0].astype(jnp.bfloat16) for level_parts in query_levels]
    doc_numbers = jnp.arange(NDOC, dtype=jnp.int32)

    def row_pool(carried, inputs):
        row_emb, lengths_row = inputs
        row_hot = (
            segments_of(lengths_row, token_count)[:, None] == NQ_ROW + doc_numbers[None, :]
        ).astype(jnp.float32)
        row_raw = row_emb.astype(jnp.float32)
        pooled_list = []
        sums_list = []
        for width, query_unit in zip(widths, query_units):
            doc_unit = normalize_cut(row_raw, width)[0].astype(jnp.bfloat16)
            expo = jnp.exp(contract_cols(query_unit, doc_unit) / POOL_TEMP)
            sums = jnp.dot(expo, row_hot, precision=FULL_PRECISION)
            pooled = POOL_TEMP * jnp.log(sums / lengths_row.astype(jnp.float32))
            pooled_list.append(jnp.sum(pooled.reshape(per_device, QLEN, NDOC), axis=1))
            sums_list.append(sums)
        return (carried, (jnp.stack(pooled_list), jnp.stack(sums_list)))

    _, (row_scores, row_sums) = lax.scan(row_pool, 0, (emb_rows, lengths))
    logits = (
        jnp.transpose(row_scores, (2, 1, 0, 3)).reshape(per_device, 3, row_count * NDOC) / LOSS_TEMP
    )
    own_pairs = pairing[0]
    target = jnp.take_along_axis(
        logits, jnp.broadcast_to(own_pairs[:, None, None], (per_device, 3, 1)), axis=2
    )[:, :, 0]
    loss_out = jnp.sum(jax.nn.logsumexp(logits, axis=2) - target, axis=1).reshape(1, per_device)
    picked = (
        jnp.arange(row_count * NDOC, dtype=jnp.int32)[None, None, :] == own_pairs[:, None, None]
    ).astype(jnp.float32)
    grad_logits = (jax.nn.softmax(logits, axis=2) - picked) / LOSS_TEMP
    grad_rows = jnp.transpose(grad_logits.reshape(per_device, 3, row_count, NDOC), (2, 1, 0, 3))
    coefficient = jnp.repeat(grad_rows, QLEN, axis=2) / row_sums

    def row_back(carried, inputs):
        row_emb, lengths_row, row_coef = inputs
        row_hot = (
            segments_of(lengths_row, token_count)[:, None] == NQ_ROW + doc_numbers[None, :]
        ).astype(jnp.float32)
        row_raw = row_emb.astype(jnp.float32)
        new_carried = []
        row_grad = jnp.zeros((token_count, proj_width), jnp.float32)
        for level_index in range(3):
            width = widths[level_index]
            doc_unit_f, doc_part, doc_scale = normalize_cut(row_raw, width)
            doc_unit = doc_unit_f.astype(jnp.bfloat16)
            expo = jnp.exp(contract_cols(query_units[level_index], doc_unit) / POOL_TEMP)
            spread = contract_cols(row_coef[level_index], row_hot, FULL_PRECISION)
            grad_sim = (expo * spread).astype(jnp.bfloat16)
            new_carried.append(
                carried[level_index]
                + jnp.dot(grad_sim, doc_unit, preferred_element_type=jnp.float32)
            )
        return (tuple(new_carried), row_grad)

    zero_query = tuple((jnp.zeros((query_count, width), jnp.float32) for width in widths))
    query_grads, doc_grads = lax.scan(row_back, zero_query, (emb_rows, lengths, coefficient))
    grad_query = jnp.zeros((query_count, proj_width), jnp.float32)
    for level_index in range(3):
        level_parts = query_levels[level_index]
        grad_query = grad_query + normalize_back(
            query_grads[level_index], level_parts[1], level_parts[2], proj_width
        )
    coef_mine = jnp.transpose(coefficient, (2, 1, 0, 3)).reshape(query_count, 3, row_count * NDOC)
    coef_all, grad_query_all = (
        lax.all_gather(shortened(coef_mine), ("dp", "tensor"), axis=0, tiled=True).astype(
            coef_mine.dtype
        ),
        lax.all_gather(
            grad_query.astype(jnp.bfloat16), ("dp", "tensor"), axis=0, tiled=True
        ).astype(grad_query.dtype),
    )
    own_raw = embed.astype(jnp.float32)
    own_segments = lax.dynamic_slice_in_dim(segments, own_start, share_rows, 0)
    own_docs = jnp.where(own_segments >= NQ_ROW, data_index * NDOC + own_segments - NQ_ROW, -1)
    own_hot = (own_docs[:, None] == jnp.arange(row_count * NDOC, dtype=jnp.int32)[None, :]).astype(
        jnp.float32
    )
    queries_all = (
        emb_rows[:, :query_span].reshape(row_count * query_span, proj_width).astype(jnp.float32)
    )
    grad_embed = jnp.zeros((share_rows, proj_width), jnp.float32)
    for level_index in range(3):
        width = widths[level_index]
        query_unit_all = normalize_cut(queries_all, width)[0].astype(jnp.bfloat16)
        doc_unit_f, doc_part, doc_scale = normalize_cut(own_raw, width)
        expo = jnp.exp(contract_cols(query_unit_all, doc_unit_f.astype(jnp.bfloat16)) / POOL_TEMP)
        spread = contract_cols(coef_all[:, level_index], own_hot, FULL_PRECISION)
        grad_sim = (expo * spread).astype(jnp.bfloat16)
        grad_doc = contract_rows(grad_sim, query_unit_all)
        grad_embed = grad_embed + normalize_back(grad_doc, doc_part, doc_scale, proj_width)
    row_query_grads = lax.dynamic_slice_in_dim(
        grad_query_all, data_index * query_span, query_span, 0
    )
    padded = jnp.pad(row_query_grads, ((0, token_count - query_span), (0, 0)))
    grad_embed = grad_embed + lax.dynamic_slice_in_dim(padded, own_start, share_rows, 0)
    proj_float = w_proj.astype(jnp.float32)
    grad_result = cot.astype(jnp.float32) + contract_cols(grad_embed, proj_float, FULL_PRECISION)
    proj_grad = contract_rows(result_low.astype(jnp.float32), grad_embed, FULL_PRECISION)
    gain_two = jnp.sum(grad_result * unit_two, axis=0)
    shift_two = jnp.sum(grad_result, axis=0)
    grad_second = norm_backward(grad_result, unit_two, rstd_two, gains[1])
    grad_ffn = grad_second.astype(jnp.bfloat16)
    down_bias = jnp.sum(grad_ffn.astype(jnp.float32), axis=0)
    grad_ffn_all = lax.all_gather(grad_ffn, "tensor", axis=0, tiled=True)
    grad_act = contract_cols(grad_ffn_all, full_down)
    down_grad = contract_rows(activation, grad_ffn_all)
    _, gelu_pull = jax.vjp(partial(jax.nn.gelu, approximate=False), up_value)
    grad_up = gelu_pull(grad_act)[0].astype(jnp.bfloat16)
    up_bias = jnp.sum(grad_up.astype(jnp.float32), axis=0)
    up_grad = contract_rows(normed_all, grad_up)
    normed_terms = contract_cols(grad_up, full_up)
    grad_normed = (
        lax.psum_scatter(
            normed_terms.astype(jnp.bfloat16), "tensor", scatter_dimension=0, tiled=True
        ).astype(jnp.float32)
        + grad_second
    )
    gain_one = jnp.sum(grad_normed * unit_one, axis=0)
    shift_one = jnp.sum(grad_normed, axis=0)
    grad_first = norm_backward(grad_normed, unit_one, rstd_one, gains[0])
    grad_attn = grad_first.astype(jnp.bfloat16)
    out_bias = jnp.sum(grad_attn.astype(jnp.float32), axis=0)
    grad_attn_all = lax.all_gather(grad_attn, "tensor", axis=0, tiled=True)
    out_grad = contract_rows(mixed, grad_attn_all)
    grad_mixed = contract_cols(grad_attn_all, full_out).astype(jnp.bfloat16)
    grad_q, grad_k, grad_v = attend_backward(
        query_rows, key_rows, value_rows, segments, log_totals, grad_mixed, block_rows
    )
    stacked_grads = jnp.stack(
        [grad_q.astype(jnp.bfloat16), grad_k.astype(jnp.bfloat16), grad_v.astype(jnp.bfloat16)]
    )
    qkv_grad = jnp.einsum("td,ktw->kdw", tokens, stacked_grads, preferred_element_type=jnp.float32)
    input_terms = jnp.einsum(
        "ktw,kdw->td", stacked_grads, full_qkv, preferred_element_type=jnp.float32
    )
    grad_input = (
        lax.psum_scatter(
            input_terms.astype(jnp.bfloat16), "tensor", scatter_dimension=0, tiled=True
        ).astype(jnp.float32)
        + grad_first
    )
    qv_grad = jnp.stack(
        [
            jnp.sum(stacked_grads[0].astype(jnp.float32), axis=0),
            jnp.sum(stacked_grads[2].astype(jnp.float32), axis=0),
        ]
    )
    qkv_part, out_part, up_part, down_part = (
        lax.psum_scatter(
            qkv_grad.astype(jnp.bfloat16), "dp", scatter_dimension=1, tiled=True
        ).astype(jnp.float32),
        lax.psum_scatter(
            out_grad.astype(jnp.bfloat16), "dp", scatter_dimension=1, tiled=True
        ).astype(jnp.float32),
        lax.psum_scatter(
            up_grad.astype(jnp.bfloat16), "dp", scatter_dimension=0, tiled=True
        ).astype(jnp.float32),
        lax.psum_scatter(
            down_grad.astype(jnp.bfloat16), "dp", scatter_dimension=1, tiled=True
        ).astype(jnp.float32),
    )
    gain_sum, shift_sum, out_bias_sum, down_bias_sum, proj_sum = lax.psum(
        (
            jnp.stack([gain_one, gain_two]),
            jnp.stack([shift_one, shift_two]),
            out_bias,
            down_bias,
            proj_grad,
        ),
        ("dp", "tensor"),
    )
    qv_sum, up_bias_sum = lax.psum((qv_grad, up_bias), "dp")
    return (
        result_low,
        loss_out,
        grad_input.astype(jnp.bfloat16),
        qkv_part,
        qv_sum,
        out_part,
        out_bias_sum,
        gain_sum,
        shift_sum,
        up_part,
        up_bias_sum,
        down_part,
        down_bias_sum,
        proj_sum,
    )


SWAP = [(0, 1), (1, 0)]
TURN = [(0, 0), (1, 2), (2, 1), (3, 3)]
FAR = [(0, 3), (3, 0), (1, 2), (2, 1)]
NEAR = [(0, 1), (1, 0), (2, 3), (3, 2)]
BF = jnp.bfloat16
F32 = jnp.float32


def dot(left, right):
    return jnp.dot(left, right, preferred_element_type=F32)


CORES = ("c", "y")


def tie(value, *others):
    return lax.optimization_barrier((value,) + others)[0]


def tie_all(values, *others):
    return lax.optimization_barrier(tuple(values) + others)[: len(values)]


def exchange(*moves):
    return lax.optimization_barrier(
        tuple(lax.ppermute(value, axis, steps) for value, axis, steps in moves)
    )


def swap(value, axis):
    return lax.ppermute(value, axis, SWAP)


def pair_up(first, second, own_index, axis):
    return jnp.where(
        own_index == 0, jnp.stack([first, second], axis), jnp.stack([second, first], axis)
    )


def far_pair(value, far, z):
    return jnp.where(z < 2, jnp.stack([value, far]), jnp.stack([far, value]))


def whole_line(pair, other, z):
    return jnp.where(
        (z == 0) | (z == 3),
        jnp.stack([pair[0], other[0], other[1], pair[1]]),
        jnp.stack([other[0], pair[0], pair[1], other[1]]),
    )


def first_moves(line):
    half = line.shape[1] // 2
    return ((line[:, :half], "x", SWAP), (line[:, half:], "y", SWAP))


def first_parts(line, moved, x, y):
    half = line.shape[1] // 2
    return (pair_up(line[:, :half], moved[0], x, 1), pair_up(line[:, half:], moved[1], y, 1))


def last_moves(parts):
    return ((parts[0], "y", SWAP), (parts[1], "x", SWAP))


def full_rows(parts, moved, x, y):
    low = pair_up(parts[0], moved[0], y, 2)
    high = pair_up(parts[1], moved[1], x, 1)
    return jnp.concatenate([low, high], axis=3).reshape(-1, low.shape[-1])


def at(blocks, index, axis):
    return lax.dynamic_index_in_dim(blocks, index, axis, keepdims=False)


def side_move(blocks, axis_name, own_index, axis):
    return (at(blocks, 1 - own_index, axis).astype(BF), axis_name, SWAP)


def side_sum(blocks, got, own_index, axis):
    return at(blocks, own_index, axis).astype(F32) + got.astype(F32)


def near_move(line, z):
    ends = (z == 0) | (z == 3)
    outer, inner = jnp.stack([line[0], line[3]]), line[1:3]
    return (jnp.where(ends, inner, outer).astype(BF), "z", NEAR)


def near_sum(line, got, z):
    ends = (z == 0) | (z == 3)
    return jnp.where(ends, jnp.stack([line[0], line[3]]), line[1:3]) + got.astype(F32)


def far_move(pair, z):
    return (jnp.where(z < 2, pair[1], pair[0]).astype(BF), "z", FAR)


def far_sum(pair, got, z):
    return jnp.where(z < 2, pair[0], pair[1]) + got.astype(F32)


def blocks_of(left, right):
    return contract_rows(left, right).astype(BF).reshape(4, 2, 2, 64, right.shape[1])


def sum_moves(blocks, x, y):
    half = blocks.shape[3] // 2
    return (
        side_move(blocks[..., :half, :], "x", x, 1),
        side_move(blocks[..., half:, :], "y", y, 2),
    )


def sum_parts(blocks, moved, x, y):
    half = blocks.shape[3] // 2
    return (
        side_sum(blocks[..., :half, :], moved[0], x, 1),
        side_sum(blocks[..., half:, :], moved[1], y, 2),
    )


def line_moves(parts, x, y):
    return (side_move(parts[0], "y", y, 1), side_move(parts[1], "x", x, 1))


def line_of(parts, moved, x, y):
    return jnp.concatenate(
        [side_sum(parts[0], moved[0], y, 1), side_sum(parts[1], moved[1], x, 1)], axis=1
    )


def tile_bounds(row_lengths, token_count):
    ends = jnp.cumsum(row_lengths)
    span = NQ_ROW * QLEN
    first = jnp.arange(token_count // TILE, dtype=jnp.int32) * TILE - span
    last = first + TILE - 1
    begin = jnp.max(jnp.where(ends[None, :] <= first[:, None], ends[None, :], 0), axis=1)
    end = jnp.min(jnp.where(ends[None, :] > last[:, None], ends[None, :], token_count), axis=1)
    low = jnp.where(first < 0, 0, (begin + span) // TILE)
    high = jnp.where(first < 0, 1, (end + span + TILE - 1) // TILE)
    return jnp.stack([low, high]).astype(jnp.int32)


def token_spans(row_lengths, token_count):
    ends = jnp.cumsum(row_lengths)[:, None]
    span = NQ_ROW * QLEN
    place = jnp.arange(token_count, dtype=jnp.int32)[None, :]
    doc = place - span
    begin = jnp.max(jnp.where(ends <= doc, ends, 0), axis=0) + span
    end = jnp.min(jnp.where(ends > doc, ends, token_count), axis=0) + span
    query = place[0] // QLEN * QLEN
    return jnp.stack(
        [jnp.where(doc[0] < 0, query, begin), jnp.where(doc[0] < 0, query + QLEN, end)]
    ).astype(jnp.int32)


def rows_of(value, start, count):
    return lax.dynamic_slice_in_dim(value, start, count, 0)


TILE = 256
KEYS = 256
LOSS_TILE = 1024
NEG = -1e30


def exact(left, right, dims):
    return lax.dot_general(left, right, (dims, ((), ())), preferred_element_type=F32)


def head_masks(value):
    lane = lax.broadcasted_iota(jnp.int32, value.shape, 1)
    zero = jnp.zeros_like(value)
    return (jnp.where(lane < HEAD_DIM, value, zero), jnp.where(lane < HEAD_DIM, zero, value))


def key_shift(step, spans):
    place = step * KEYS + lax.broadcasted_iota(jnp.int32, (KEYS, TILE), 0)
    inside = (place >= spans[0:1, :]) & (place < spans[1:2, :])
    return jnp.where(inside, 0.0, NEG)


def attend_kernel(bounds, own_ref, qkv_ref, spans, out_ref, lse_ref, held):
    block = pl.program_id(0)
    groups = 2
    pairs = out_ref.shape[1] // 128
    per_group = pairs // groups

    def column(pair, part):
        start = ((pair // per_group) * 3 + part) * per_group + pair % per_group
        return slice(start * 128, (start + 1) * 128)

    queries = [head_masks(own_ref[:, column(pair, 0)] * HEAD_DIM**-0.5) for pair in range(pairs)]
    heads = [(pair, head) for pair in range(pairs) for head in range(2)]

    def score(step, highest):
        rows = pl.ds(pl.multiple_of(step * KEYS, KEYS), KEYS)
        shift = key_shift(step, spans)
        fresh = []
        for index, (pair, head) in enumerate(heads):
            keys = qkv_ref[rows, column(pair, 1)]
            scores = exact(keys, queries[pair][head], ((1,), (1,))) + shift
            held[index, rows, :] = scores
            fresh.append(jnp.maximum(highest[index], jnp.max(scores, axis=0, keepdims=True)))
        return tuple(fresh)

    low = jnp.full((1, TILE), NEG, F32)
    highest = lax.fori_loop(bounds[0, block], bounds[1, block], score, (low,) * len(heads))

    def mix(step, carried):
        rows = pl.ds(pl.multiple_of(step * KEYS, KEYS), KEYS)
        fresh = []
        for index, (pair, head) in enumerate(heads):
            values = qkv_ref[rows, column(pair, 2)]
            total, mixed = carried[index]
            expo = jnp.exp(held[index, rows, :] - highest[index])
            product = exact(values, expo.astype(BF), ((0,), (0,)))
            fresh.append(
                (
                    total + jnp.sum(expo, axis=0, keepdims=True),
                    mixed + product[head * HEAD_DIM : (head + 1) * HEAD_DIM],
                )
            )
        return tuple(fresh)

    start = (jnp.zeros((1, TILE), F32), jnp.zeros((HEAD_DIM, TILE), F32))
    parts = lax.fori_loop(bounds[0, block], bounds[1, block], mix, (start,) * len(heads))
    for pair in range(pairs):
        both = [parts[2 * pair + head][1] / parts[2 * pair + head][0] for head in range(2)]
        mixed = jnp.transpose(jnp.concatenate(both, axis=0))
        out_ref[:, pair * 128 : (pair + 1) * 128] = mixed.astype(BF)
    for index in range(len(heads)):
        lse_ref[index : index + 1, :] = highest[index] + jnp.log(parts[index][0])


def attend(bounds, qkv, spans):
    count, wide = qkv.shape
    heads = wide // 3 // HEAD_DIM
    whole = lambda shape: pl.BlockSpec(shape, lambda i: (0, 0))
    return pl.pallas_call(
        attend_kernel,
        grid=(count // TILE,),
        in_specs=[
            pl.BlockSpec(memory_space=pltpu.SMEM),
            pl.BlockSpec((TILE, wide), lambda i: (i, 0)),
            whole((count, wide)),
            pl.BlockSpec((2, TILE), lambda i: (0, i)),
        ],
        out_specs=[
            pl.BlockSpec((TILE, wide // 3), lambda i: (i, 0)),
            pl.BlockSpec((heads, TILE), lambda i: (0, i)),
        ],
        out_shape=[
            jax.ShapeDtypeStruct((count, wide // 3), BF),
            jax.ShapeDtypeStruct((heads, count), F32),
        ],
        scratch_shapes=[pltpu.VMEM((heads, count, TILE), F32)],
        compiler_params=pltpu.CompilerParams(vmem_limit_bytes=40 << 20),
        cost_estimate=pl.CostEstimate(
            flops=4 * heads * count * count * 64,
            transcendentals=heads * count * count // 2,
            bytes_accessed=4 * count * wide * 2,
        ),
    )(bounds, qkv, qkv, spans)


def attend_back_kernel(
    first, bounds, own_ref, qkv_ref, out_ref, grad_ref, lse_ref, spans,
    grads_ref, sums_ref, key_sum, value_sum,
):
    block = pl.program_id(0)
    pairs = out_ref.shape[1] // 128
    heads = [(pair, head) for pair in range(pairs) for head in range(2)]
    cut = lambda index: slice(index * 128, (index + 1) * 128)

    @pl.when(block == 0)
    def _():
        key_sum[...] = jnp.zeros_like(key_sum)
        value_sum[...] = jnp.zeros_like(value_sum)
        sums_ref[...] = jnp.zeros_like(sums_ref)

    queries = [head_masks(own_ref[:, cut(pair)] * HEAD_DIM**-0.5) for pair in range(pairs)]
    grads = [head_masks(grad_ref[:, cut(pair)]) for pair in range(pairs)]
    picks = head_masks(jnp.ones((8, 128), BF))
    inner = []
    for pair, head in heads:
        product = grad_ref[:, cut(pair)].astype(F32) * out_ref[:, cut(pair)].astype(F32)
        high = product.astype(BF)
        rest = (product - high.astype(F32)).astype(BF)
        inner.append(
            (
                exact(picks[head], high, ((1,), (1,))) + exact(picks[head], rest, ((1,), (1,)))
            )[0:1]
        )
    lse = [lse_ref[first + index : first + index + 1, :] for index in range(len(heads))]

    def step_of(step, carried):
        rows = pl.ds(pl.multiple_of(step * KEYS, KEYS), KEYS)
        shift = key_shift(step, spans)
        fresh = []
        for pair in range(pairs):
            keys = qkv_ref[rows, cut(pairs + pair)]
            values = qkv_ref[rows, cut(2 * pairs + pair)]
            key_add = jnp.zeros((KEYS, 128), F32)
            value_add = jnp.zeros((KEYS, 128), F32)
            for head in range(2):
                index = 2 * pair + head
                scores = exact(keys, queries[pair][head], ((1,), (1,))) + shift
                probs = jnp.exp(scores - lse[index])
                grad_probs = exact(values, grads[pair][head], ((1,), (1,)))
                grad_scores = (probs * (grad_probs - inner[index])).astype(BF)
                value_add = value_add + exact(probs.astype(BF), grads[pair][head], ((1,), (0,)))
                key_add = key_add + exact(grad_scores, queries[pair][head], ((1,), (0,)))
                product = exact(keys, grad_scores, ((0,), (0,)))
                fresh.append(carried[index] + product[head * HEAD_DIM : (head + 1) * HEAD_DIM])
            key_sum[rows, cut(pair)] += key_add
            value_sum[rows, cut(pair)] += value_add
        return tuple(fresh)

    start = jnp.zeros((HEAD_DIM, TILE), F32)
    parts = lax.fori_loop(bounds[0, block], bounds[1, block], step_of, (start,) * len(heads))
    own = pl.ds(pl.multiple_of(block * TILE, TILE), TILE)
    for pair in range(pairs):
        grad_query = jnp.concatenate([parts[2 * pair], parts[2 * pair + 1]], axis=0)
        grad_query = jnp.transpose(grad_query * HEAD_DIM**-0.5).astype(BF)
        grads_ref[own, cut(pair)] = grad_query
        sums_ref[0:1, cut(pair)] += jnp.sum(grad_query.astype(F32), axis=0, keepdims=True)

    @pl.when(block == pl.num_programs(0) - 1)
    def _():
        wide = pairs * 128
        grad_value = value_sum[...].astype(BF)
        grads_ref[:, wide : 2 * wide] = key_sum[...].astype(BF)
        grads_ref[:, 2 * wide :] = grad_value
        sums_ref[1:2, :] = jnp.sum(grad_value.astype(F32), axis=0, keepdims=True)


def attend_back(bounds, group, qkv, mixed, grad_mixed, lse, spans):
    count = qkv.shape[0]
    wide = qkv.shape[1] // 2
    heads = wide // 3 // HEAD_DIM
    whole = lambda shape: pl.BlockSpec(shape, lambda i: (0, 0))
    return pl.pallas_call(
        partial(attend_back_kernel, group * heads),
        grid=(count // TILE,),
        in_specs=[
            pl.BlockSpec(memory_space=pltpu.SMEM),
            pl.BlockSpec((TILE, wide), lambda i: (i, group)),
            pl.BlockSpec((count, wide), lambda i: (0, group)),
            pl.BlockSpec((TILE, wide // 3), lambda i: (i, group)),
            pl.BlockSpec((TILE, wide // 3), lambda i: (i, group)),
            pl.BlockSpec((2 * heads, TILE), lambda i: (0, i)),
            pl.BlockSpec((2, TILE), lambda i: (0, i)),
        ],
        out_specs=[whole((count, wide)), whole((8, wide // 3))],
        out_shape=[
            jax.ShapeDtypeStruct((count, wide), BF),
            jax.ShapeDtypeStruct((8, wide // 3), F32),
        ],
        scratch_shapes=[
            pltpu.VMEM((count, wide // 3), F32),
            pltpu.VMEM((count, wide // 3), F32),
        ],
        compiler_params=pltpu.CompilerParams(vmem_limit_bytes=40 << 20),
        cost_estimate=pl.CostEstimate(
            flops=10 * heads * count * count * 64,
            transcendentals=heads * count * count // 2,
            bytes_accessed=8 * count * wide * 2,
        ),
    )(
        bounds, qkv, qkv, mixed, grad_mixed,
        lse, spans,
    )


ERFC = (
    -1.26551223, 1.00002368, 0.37409196, 0.09678418, -0.18628806,
    0.27886807, -1.13520398, 1.48851587, -0.82215223, 0.17087277,
)


def gelu_pair(value):
    size = jnp.abs(value) * 0.5**0.5
    ratio = 1.0 / (1.0 + 0.5 * size)
    series = jnp.full_like(value, ERFC[-1])
    for factor in ERFC[-2::-1]:
        series = series * ratio + factor
    bell = jnp.exp(-size * size)
    tail = 0.5 * ratio * bell * jnp.exp(series)
    phi = jnp.where(value < 0.0, tail, 1.0 - tail)
    return (value * phi, phi + value * bell * 0.3989422804014327)


def expand_kernel(x_ref, w_ref, b_ref, *refs):
    act_ref, slope_ref = refs[-2:]
    rows = 128
    for start in range(0, x_ref.shape[0], rows):
        part = slice(start, start + rows)
        value = exact(x_ref[part, :], w_ref[...], ((1,), (0,))) + b_ref[...]
        active, slope = gelu_pair(value)
        act_ref[part, :] = active.astype(BF)
        slope_ref[part, :] = slope.astype(BF)


def expand(value, weight, shift, first, tiles, filled=()):
    count, depth = value.shape
    width = shift.shape[1]
    tile = 256
    column = lambda rows: pl.BlockSpec((rows, tile), lambda i: (0, first + i))
    return pl.pallas_call(
        expand_kernel,
        grid=(tiles,),
        in_specs=[
            pl.BlockSpec((count, depth), lambda i: (0, 0)),
            column(depth),
            column(1),
        ]
        + [pl.BlockSpec(memory_space=pl.ANY)] * len(filled),
        out_specs=[column(count)] * 2,
        out_shape=[jax.ShapeDtypeStruct((count, width), BF)] * 2,
        input_output_aliases={3: 0, 4: 1} if filled else {},
        compiler_params=pltpu.CompilerParams(vmem_limit_bytes=32 << 20),
        cost_estimate=pl.CostEstimate(
            flops=2 * count * depth * tile * tiles,
            transcendentals=3 * count * tile * tiles,
            bytes_accessed=2 * (count * depth + depth * tile * tiles + 2 * count * tile * tiles),
        ),
    )(value, weight, shift, *filled)


def cut_levels(raw, cuts):
    lane = lax.broadcasted_iota(jnp.int32, raw.shape, 1)
    levels = []
    for cut in cuts:
        part = jnp.where(lane < cut, raw, 0.0)
        scale = lax.rsqrt(jnp.sum(part * part, axis=1, keepdims=True) + EPS_EMBED)
        levels.append(((part * scale).astype(BF), part, scale))
    return levels


def pool_kernel(cuts, span, q_ref, d_ref, seg_ref, out_ref, units, hot):
    @pl.when(pl.program_id(0) == 0)
    def _():
        raw = d_ref[span:, :].astype(F32)
        for level, parts in enumerate(cut_levels(raw, cuts)):
            units[level] = parts[0]
        doc = lax.broadcasted_iota(jnp.int32, hot.shape, 0)
        hot[...] = (seg_ref[:, span:] == NQ_ROW + doc).astype(F32).astype(BF)

    levels = cut_levels(q_ref[...].astype(F32), cuts)
    for level in range(len(cuts)):
        similar = exact(units[level], levels[level][0], ((1,), (1,)))
        expo = jnp.exp(similar * (1.0 / POOL_TEMP))
        high = expo.astype(BF)
        rest = (expo - high.astype(F32)).astype(BF)
        out_ref[level * NDOC : (level + 1) * NDOC, :] = exact(
            hot[...], high, ((1,), (0,))
        ) + exact(hot[...], rest, ((1,), (0,)))


def pool(cuts, span, queries, row_embed, seg_row):
    count, width = queries.shape
    tokens = row_embed.shape[0]
    whole = lambda shape: pl.BlockSpec(shape, lambda i: (0, 0))
    return pl.pallas_call(
        partial(pool_kernel, cuts, span),
        grid=(count // LOSS_TILE,),
        in_specs=[
            pl.BlockSpec((LOSS_TILE, width), lambda i: (i, 0)),
            whole((tokens, width)),
            whole((1, tokens)),
        ],
        out_specs=pl.BlockSpec((len(cuts) * NDOC, LOSS_TILE), lambda i: (0, i)),
        out_shape=jax.ShapeDtypeStruct((len(cuts) * NDOC, count), F32),
        scratch_shapes=[
            pltpu.VMEM((len(cuts), tokens - span, width), BF),
            pltpu.VMEM((NDOC, tokens - span), BF),
        ],
        compiler_params=pltpu.CompilerParams(vmem_limit_bytes=32 << 20),
        cost_estimate=pl.CostEstimate(
            flops=2 * len(cuts) * count * tokens * 256,
            transcendentals=len(cuts) * count * tokens,
            bytes_accessed=2 * (count + tokens) * width,
        ),
    )(queries, row_embed, seg_row)


def level_back(grad, part, scale):
    return scale * grad - part * (scale * scale * scale) * jnp.sum(
        part * grad, axis=1, keepdims=True
    )


def pool_back_kernel(
    cuts, span, q_ref, d_ref, seg_ref, coef_ref, q_out, d_out, units, units_t, hot, sums
):
    step = pl.program_id(0)

    @pl.when(step == 0)
    def _():
        raw = d_ref[span:, :].astype(F32)
        for level, parts in enumerate(cut_levels(raw, cuts)):
            units[level] = parts[0]
            units_t[level] = jnp.transpose(parts[0])
        doc = lax.broadcasted_iota(jnp.int32, hot.shape, 0)
        wanted = NQ_ROW + jnp.where(doc < NDOC, doc, doc - NDOC)
        hot[...] = (seg_ref[:, span:] == wanted).astype(F32).astype(BF)
        sums[...] = jnp.zeros_like(sums)

    levels = cut_levels(q_ref[...].astype(F32), cuts)
    total = jnp.zeros(q_ref.shape, F32)
    for level in range(len(cuts)):
        unit, part, scale = levels[level]
        similar = exact(units[level], unit, ((1,), (1,)))
        coef = coef_ref[level * NDOC : (level + 1) * NDOC, :]
        high = coef.astype(BF).astype(F32)
        both = jnp.concatenate([high, coef - high], axis=0).astype(BF)
        spread = exact(hot[...], both, ((0,), (0,)))
        grad = (jnp.exp(similar * (1.0 / POOL_TEMP)) * spread).astype(BF)
        sums[level] += exact(grad, unit, ((1,), (0,)))
        grad_unit = jnp.transpose(exact(units_t[level], grad, ((1,), (0,))))
        total = total + level_back(grad_unit, part, scale)
    q_out[...] = total.astype(BF)

    @pl.when(step == pl.num_programs(0) - 1)
    def _():
        raw = d_ref[span:, :].astype(F32)
        result = jnp.zeros(raw.shape, F32)
        for level, parts in enumerate(cut_levels(raw, cuts)):
            lane = lax.broadcasted_iota(jnp.int32, raw.shape, 1)
            grad = jnp.where(lane < cuts[level], sums[level], 0.0)
            result = result + level_back(grad, parts[1], parts[2])
        d_out[...] = result


def pool_back(cuts, span, queries, row_embed, seg_row, coef):
    count, width = queries.shape
    tokens = row_embed.shape[0]
    docs = tokens - span
    whole = lambda shape: pl.BlockSpec(shape, lambda i: (0, 0))
    return pl.pallas_call(
        partial(pool_back_kernel, cuts, span),
        grid=(count // LOSS_TILE,),
        in_specs=[
            pl.BlockSpec((LOSS_TILE, width), lambda i: (i, 0)),
            whole((tokens, width)),
            whole((1, tokens)),
            pl.BlockSpec((len(cuts) * NDOC, LOSS_TILE), lambda i: (0, i)),
        ],
        out_specs=[pl.BlockSpec((LOSS_TILE, width), lambda i: (i, 0)), whole((docs, width))],
        out_shape=[
            jax.ShapeDtypeStruct((count, width), BF),
            jax.ShapeDtypeStruct((docs, width), F32),
        ],
        scratch_shapes=[
            pltpu.VMEM((len(cuts), docs, width), BF),
            pltpu.VMEM((len(cuts), width, docs), BF),
            pltpu.VMEM((2 * NDOC, docs), BF),
            pltpu.VMEM((len(cuts), docs, width), F32),
        ],
        compiler_params=pltpu.CompilerParams(vmem_limit_bytes=32 << 20),
        cost_estimate=pl.CostEstimate(
            flops=2 * len(cuts) * count * docs * 512,
            transcendentals=len(cuts) * count * docs,
            bytes_accessed=4 * (count + tokens) * width,
        ),
    )(queries, row_embed, seg_row, coef)


def local_chip(
    tokens,
    lengths,
    pairing,
    w_qkv,
    b_qv,
    w_out,
    b_out,
    ln_gain,
    ln_bias,
    w_up,
    b_up,
    w_down,
    b_down,
    w_proj,
    cot,
):
    z, x, c, y = (lax.axis_index(name) for name in ("z", "x", "c", "y"))
    chip = 4 * z + 2 * x + y
    token_count, width = tokens.shape
    share = token_count // 2
    own_start, other_start = c * share, (1 - c) * share
    gains, shifts = ln_gain.astype(F32), ln_bias.astype(F32)

    half_width = w_qkv.shape[2]
    up_wide = w_up.shape[1]
    chip_count = lengths.shape[0]
    half_queries = NQ_ROW // 2
    query_total = chip_count * half_queries
    quarter = half_width // 2
    qkv_rows = jnp.concatenate(
        [w_qkv[k][:, g * quarter : (g + 1) * quarter] for g in range(2) for k in range(3)], axis=1
    )
    pair_rows = jnp.pad(pairing.astype(BF), ((0, 63), (0, 128 - half_queries)))
    mid_rows = jnp.concatenate([w_up, w_out.T, pair_rows], axis=1)
    bias = jnp.concatenate([b_qv.reshape(-1), b_up])[None].astype(F32)
    got = exchange(
        (qkv_rows, CORES, TURN), (tokens, "c", SWAP), (bias, "y", SWAP)
    )
    qkv_rows = got[0]
    row = jnp.where(c == y, tokens, got[1])
    bias = jnp.where(c == y, bias, got[2])
    (rest_rows,) = exchange(
        (tie(jnp.concatenate([mid_rows, w_down.T], axis=1), row), CORES, TURN)
    )
    (far,) = exchange((qkv_rows, "z", FAR))
    qkv_pair = far_pair(qkv_rows, far, z)
    mid_wide = mid_rows.shape[1]
    rest_rows = tie(rest_rows, qkv_pair)
    mid_rows, down_rows = rest_rows[:, :mid_wide], rest_rows[:, mid_wide:]
    (near,) = exchange((qkv_pair, "z", NEAR))
    qkv_line = whole_line(qkv_pair, near, z)
    (far,) = exchange((mid_rows, "z", FAR))
    mid_pair = far_pair(mid_rows, far, z)
    qkv_parts = first_parts(qkv_line, exchange(*first_moves(qkv_line)), x, y)
    (near,) = exchange((mid_pair, "z", NEAR))
    mid_line = whole_line(mid_pair, near, z)
    full_qkv = full_rows(qkv_parts, exchange(*last_moves(qkv_parts)), x, y)
    down_rows, mid_line = lax.optimization_barrier((down_rows, mid_line))
    (far,) = exchange((down_rows, "z", FAR))
    down_pair = far_pair(down_rows, far, z)
    (near,) = exchange((down_pair, "z", NEAR))
    down_line = whole_line(down_pair, near, z)
    mid_parts = first_parts(mid_line, exchange(*first_moves(mid_line)), x, y)
    full_mid = full_rows(mid_parts, exchange(*last_moves(mid_parts)), x, y)
    down_parts = first_parts(down_line, exchange(*first_moves(down_line)), x, y)
    full_out = full_mid[:, up_wide : up_wide + half_width]
    pairs = full_mid[:, up_wide + half_width :].reshape(chip_count, 64, 128)
    pairs = pairs[:, 0, :half_queries].astype(jnp.int32).reshape(1, query_total)
    row_lengths = lax.dynamic_index_in_dim(lengths, chip, 0, keepdims=False)
    segments = segments_of(row_lengths, token_count)
    seg_row, spans = segments[None, :], token_spans(row_lengths, token_count)
    query_span = NQ_ROW * QLEN
    bounds = tile_bounds(row_lengths, token_count)
    no_bias = jnp.zeros((1, quarter), F32)
    qkv_bias = jnp.concatenate(
        [
            part
            for g in range(2)
            for part in (
                bias[:, g * quarter : (g + 1) * quarter],
                no_bias,
                bias[:, half_width + g * quarter : half_width + (g + 1) * quarter],
            )
        ],
        axis=1,
    )
    qkv = (dot(row, full_qkv) + qkv_bias).astype(BF)
    mixed, lse = attend(bounds, tie(qkv, down_line), spans)

    def row_sum(left, weight_t, transposed):
        times = contract_cols if transposed else dot
        theirs = swap(times(left(1), weight_t).astype(BF), "c")
        return times(left(0), weight_t) + theirs.astype(F32)

    def mixed_half(which):
        return rows_of(mixed, other_start if which else own_start, share)

    other_attn = swap(contract_cols(mixed_half(1), full_out).astype(BF), "c")
    other_attn, second_norm = lax.optimization_barrier(
        (other_attn, jnp.stack([gains[1], shifts[1]]))
    )
    second_norm = swap(second_norm, "c")
    second_norm, *down_parts = lax.optimization_barrier((second_norm,) + tuple(down_parts))
    down_got = exchange(*last_moves(down_parts))
    attn_sum = contract_cols(mixed_half(0), full_out) + other_attn.astype(F32)
    own_tokens = rows_of(row, own_start, share).astype(F32)
    normed, unit_one, rstd_one = norm_forward(
        own_tokens + attn_sum + b_out.astype(F32), gains[0], shifts[0]
    )
    normed_low = normed.astype(BF)
    normed_all = jnp.concatenate([normed_low, swap(normed_low, "c")], axis=0)
    activation, slope = expand(
        normed_all, full_mid, bias[:, 2 * half_width :], 0, up_wide // 256
    )
    full_down = full_rows(down_parts, down_got, x, y)
    ffn_sum = row_sum(
        lambda which: activation[which * share : (which + 1) * share], full_down, True
    )
    result, unit_two, rstd_two = norm_forward(
        normed + ffn_sum + b_down.astype(F32), second_norm[0], second_norm[1]
    )
    result_low = result.astype(BF)
    embed = dot(result_low, w_proj).astype(BF)

    other_embed = swap(embed, "c")
    row_embed = jnp.where(
        c == 0,
        jnp.concatenate([embed, other_embed], axis=0),
        jnp.concatenate([other_embed, embed], axis=0),
    )
    half_span = query_span // 2
    own_queries = rows_of(row_embed, c * half_span, half_span)
    chips = ("z", "x", "y")
    queries = lax.all_to_all(
        jnp.broadcast_to(own_queries[None], (chip_count,) + own_queries.shape), chips, 0, 0
    ).reshape(chip_count * half_span, -1)
    queries, own_cot = lax.optimization_barrier((queries, lax.ppermute(cot, CORES, TURN)))
    proj_width = w_proj.shape[1]
    cuts = (proj_width, 3 * proj_width // 4, proj_width // 2)
    sums = pool(cuts, query_span, queries, row_embed, seg_row)
    doc_sizes = jnp.tile(row_lengths.astype(F32), 3)[:, None]
    group = (
        jnp.arange(query_total * QLEN, dtype=jnp.int32)[:, None] // QLEN
        == jnp.arange(query_total, dtype=jnp.int32)[None, :]
    ).astype(F32)
    pooled = POOL_TEMP * jnp.log(sums / doc_sizes)
    logits = jnp.dot(pooled, group, precision=FULL_PRECISION) / LOSS_TEMP
    logits = logits.reshape(3, NDOC, query_total)
    doc_numbers = chip * NDOC + jnp.arange(NDOC, dtype=jnp.int32)
    picked = (doc_numbers[:, None] == pairs).astype(F32)
    own_high = jnp.max(logits, axis=1)
    own_lse = own_high + jnp.log(jnp.sum(jnp.exp(logits - own_high[:, None]), axis=1))
    own_target = jnp.sum(logits * picked, axis=1)
    notes = jnp.pad(jnp.concatenate([own_lse, own_target], axis=1), ((0, 5), (0, 0)))
    notes = lax.all_to_all(
        jnp.broadcast_to(notes[None], (chip_count,) + notes.shape), chips, 0, 0
    )
    chip_lse = notes[:, :3, :query_total]
    high = jnp.max(chip_lse, axis=0)
    all_lse = high + jnp.log(jnp.sum(jnp.exp(chip_lse - high), axis=0))
    target = jnp.sum(notes[:, :3, query_total:], axis=0)
    losses = jnp.sum(all_lse - target, axis=0).reshape(chip_count, half_queries)
    grad_logits = (jnp.exp(logits - all_lse[:, None]) - picked) / LOSS_TEMP
    coefficient = (
        lax.dot_general(
            grad_logits.reshape(3 * NDOC, query_total),
            group,
            (((1,), (1,)), ((), ())),
            precision=FULL_PRECISION,
        )
        / sums
    )
    query_grad, doc_grad = pool_back(cuts, query_span, queries, row_embed, seg_row, coefficient)
    query_grad, y_out = lax.optimization_barrier(
        (query_grad, lax.ppermute(result_low, CORES, TURN))
    )
    grad_blocks = lax.all_to_all(
        query_grad.reshape(chip_count, half_span, proj_width), chips, 0, 0
    )
    own_query_grad = jnp.sum(grad_blocks.astype(F32), axis=0)
    row_grad = jnp.concatenate([jnp.zeros((query_span, proj_width), F32), doc_grad], axis=0)
    row_grad = lax.dynamic_update_slice_in_dim(row_grad, own_query_grad, c * half_span, 0)
    grad_embed = rows_of(row_grad, own_start, share) + swap(
        rows_of(row_grad, other_start, share), "c"
    )

    proj_low = w_proj
    grad_embed_low = grad_embed.astype(BF)
    grad_embed_rest = (grad_embed - grad_embed_low.astype(F32)).astype(BF)
    grad_result = own_cot.astype(F32) + (
        contract_cols(grad_embed_low, proj_low) + contract_cols(grad_embed_rest, proj_low)
    )
    proj_grad = contract_rows(result_low, grad_embed_low) + contract_rows(
        result_low, grad_embed_rest
    )
    gain_two = jnp.sum(grad_result * unit_two, axis=0)
    shift_two = jnp.sum(grad_result, axis=0)
    grad_second = norm_backward(grad_result, unit_two, rstd_two, second_norm[0])
    grad_ffn = grad_second.astype(BF)
    down_bias = jnp.sum(grad_ffn.astype(F32), axis=0)
    other_ffn = swap(grad_ffn, "c")
    grad_ffn_all = jnp.concatenate([grad_ffn, other_ffn], axis=0)
    down_blocks = blocks_of(grad_ffn_all, activation)
    down_moved = exchange(*sum_moves(down_blocks, x, y))
    grad_up = (dot(grad_ffn_all, full_down) * slope.astype(F32)).astype(BF)
    up_bias = jnp.sum(grad_up.astype(F32), axis=0)
    up_blocks = blocks_of(normed_all, tie(grad_up, *down_moved))
    full_up = full_mid[:, :up_wide]
    grad_normed = (
        row_sum(lambda which: grad_up[which * share : (which + 1) * share], full_up, True)
        + grad_second
    )
    gain_one = jnp.sum(grad_normed * unit_one, axis=0)
    shift_one = jnp.sum(grad_normed, axis=0)
    grad_first = norm_backward(grad_normed, unit_one, rstd_one, gains[0])
    grad_attn = grad_first.astype(BF)
    out_bias = jnp.sum(grad_attn.astype(F32), axis=0)
    other_attn = swap(grad_attn, "c")
    grad_attn_all = jnp.where(
        c == 0,
        jnp.concatenate([grad_attn, other_attn], axis=0),
        jnp.concatenate([other_attn, grad_attn], axis=0),
    )
    grad_mixed = dot(grad_attn_all, full_out).astype(BF)
    out_blocks = blocks_of(grad_attn_all, mixed)
    down_parts = sum_parts(down_blocks, down_moved, x, y)
    moved = exchange(*line_moves(down_parts, x, y), *sum_moves(up_blocks, x, y))
    down_line = line_of(down_parts, moved, x, y)
    up_parts = sum_parts(up_blocks, moved[2:], x, y)
    grad_mixed, out_blocks, down_line, *up_parts = lax.optimization_barrier(
        (grad_mixed, out_blocks, down_line) + tuple(up_parts)
    )
    moved = exchange(
        near_move(down_line, z), *line_moves(up_parts, x, y), *sum_moves(out_blocks, x, y)
    )
    grads_one, sums_one = attend_back(bounds, 0, qkv, mixed, grad_mixed, lse, spans)
    down_pair = near_sum(down_line, moved[0], z)
    up_line = line_of(up_parts, moved[1:], x, y)
    out_parts = sum_parts(out_blocks, moved[3:], x, y)
    grad_mixed, down_pair, up_line, *out_parts = lax.optimization_barrier(
        (grad_mixed, down_pair, up_line) + tuple(out_parts)
    )
    up_line, losses = lax.optimization_barrier((up_line, losses))
    moved = exchange(
        far_move(down_pair, z), near_move(up_line, z), *line_moves(out_parts, x, y)
    )
    other_losses = swap(losses, "c")
    proj_given, other_losses, grad_mixed = lax.optimization_barrier(
        (rows_of(proj_grad, other_start, share), other_losses, grad_mixed)
    )
    proj_half = rows_of(proj_grad, own_start, share)
    other_proj = swap(proj_given, "c")
    grad_mixed, other_proj = lax.optimization_barrier((grad_mixed, other_proj))
    proj_half = proj_half + other_proj
    losses = jnp.where(c == y, losses, other_losses)
    loss_out = rows_of(losses, 4 * z + 2 * x + c, 1)
    grads_two, sums_two = attend_back(bounds, 1, qkv, mixed, grad_mixed, lse, spans)
    down_part = far_sum(down_pair, moved[0], z)
    up_pair = near_sum(up_line, moved[1], z)
    out_line = line_of(out_parts, moved[2:], x, y)
    grads_one, grads_two, down_part, up_pair, out_line = lax.optimization_barrier(
        (grads_one, grads_two, down_part, up_pair, out_line)
    )
    shared = jnp.stack([gain_one, gain_two, shift_one, shift_two, out_bias, down_bias])
    half_sums = jnp.concatenate(
        [
            sums_one[0],
            sums_two[0],
            sums_one[1],
            sums_two[1],
            up_bias,
        ]
    )
    small = jnp.concatenate([shared.reshape(-1, 128), half_sums.reshape(-1, 128), proj_half])

    qkv_blocks = jnp.concatenate(
        [blocks_of(row, grads_one), blocks_of(row, grads_two)], axis=4
    )
    qkv_blocks, up_pair, out_line, down_part, small = lax.optimization_barrier(
        (qkv_blocks, up_pair, out_line, down_part, small)
    )
    moved = exchange(
        *sum_moves(qkv_blocks, x, y),
        far_move(up_pair, z),
        near_move(out_line, z),
        (small.astype(BF), "z", NEAR),
    )
    qkv_parts = sum_parts(qkv_blocks, moved, x, y)
    up_part = far_sum(up_pair, moved[2], z)
    out_pair = near_sum(out_line, moved[3], z)
    small = small + moved[4].astype(F32)

    def input_terms(start):
        return contract_cols(
            rows_of(grads_one, start, share), full_qkv[:, : 3 * quarter]
        ) + contract_cols(rows_of(grads_two, start, share), full_qkv[:, 3 * quarter :])

    other_terms = swap(input_terms(other_start).astype(BF), "c")
    grad_input = (input_terms(own_start) + other_terms.astype(F32) + grad_first).astype(BF)
    moved = exchange(*line_moves(qkv_parts, x, y), far_move(out_pair, z), (small.astype(BF), "z", FAR))
    qkv_line = line_of(qkv_parts, moved, x, y)
    out_part = far_sum(out_pair, moved[2], z)
    small = small + moved[3].astype(F32)
    moved = exchange(
        near_move(qkv_line, z),
        (small.astype(BF), "x", SWAP),
        (tie(grad_input, qkv_line), CORES, TURN),
    )
    qkv_pair = near_sum(qkv_line, moved[0], z)
    small = small + moved[1].astype(F32)
    grad_input = moved[2]
    ffn_part = jnp.concatenate([down_part, up_part], axis=1).astype(BF)
    moved = exchange(
        far_move(qkv_pair, z), (small.astype(BF), "y", SWAP), (tie(ffn_part, qkv_pair), CORES, TURN)
    )
    attn_part = jnp.concatenate([far_sum(qkv_pair, moved[0], z), out_part], axis=1).astype(BF)
    small = small + moved[1].astype(F32)
    ffn_part = moved[2].astype(F32)
    down_part, up_part = ffn_part[:, :up_wide], ffn_part[:, up_wide:]
    attn_part, other_small = exchange((attn_part, CORES, TURN), (small.astype(BF), "c", SWAP))
    attn_part = attn_part.astype(F32)
    other_small = other_small.astype(F32)
    qkv_part, out_part = attn_part[:, : 3 * half_width], attn_part[:, 3 * half_width :]
    shared_rows = 6 * width // 128
    small_rows = small.shape[0] - share
    shared = (small[:shared_rows] + other_small[:shared_rows]).reshape(6, width)
    half_sums = jnp.where(
        c == y, small[shared_rows:small_rows], other_small[shared_rows:small_rows]
    ).reshape(-1)
    proj_sum = pair_up(small[small_rows:], other_small[small_rows:], c, 0).reshape(width, -1)
    qkv_part = qkv_part.reshape(64, 2, 3, quarter).transpose(2, 0, 1, 3).reshape(3, 64, half_width)
    return (
        y_out,
        loss_out,
        grad_input,
        qkv_part,
        half_sums[: 2 * half_width].reshape(2, half_width),
        out_part.T,
        shared[4],
        shared[0:2],
        shared[2:4],
        up_part,
        half_sums[2 * half_width :],
        down_part.T,
        shared[5],
        proj_sum,
    )


IN_SPECS = (
    P("dp", None),
    P(),
    P("dp", "tensor"),
    P(None, "dp", "tensor"),
    P(None, "tensor"),
    P("tensor", "dp"),
    P(),
    P(),
    P(),
    P("dp", "tensor"),
    P("tensor"),
    P("tensor", "dp"),
    P(),
    P(),
    P(("dp", "tensor"), None),
)
OUT_SPECS = (
    P(("dp", "tensor"), None),
    P("dp", "tensor"),
    P(("dp", "tensor"), None),
    P(None, "dp", "tensor"),
    P(None, "tensor"),
    P("tensor", "dp"),
    P(),
    P(),
    P(),
    P("dp", "tensor"),
    P("tensor"),
    P("tensor", "dp"),
    P(),
    P(),
)


def solution(mesh):
    if mesh.devices.shape != (16, 2):
        return jax.shard_map(
            local, mesh=mesh, in_specs=IN_SPECS, out_specs=OUT_SPECS, check_vma=False
        )
    names = {"dp": ("z", "x", "c"), "tensor": ("y",)}

    def respec(spec):
        parts = []
        for entry in spec:
            axes = () if entry is None else entry if isinstance(entry, tuple) else (entry,)
            parts.append(tuple(name for axis in axes for name in names[axis]) or None)
        return P(*parts)

    chips = Mesh(mesh.devices.reshape(4, 2, 2, 2), ("z", "x", "c", "y"))
    return jax.shard_map(
        local_chip,
        mesh=chips,
        in_specs=tuple(respec(spec) for spec in IN_SPECS),
        out_specs=tuple(respec(spec) for spec in OUT_SPECS),
        check_vma=False,
    )
```

```python
from functools import partial

import jax
import jax.numpy as jnp
from jax import lax
from jax.experimental import pallas as pl
from jax.experimental.pallas import tpu as pltpu
from jax.sharding import Mesh, PartitionSpec as P

HEAD_DIM = 64
QLEN = 32
NQ_ROW = 8
NDOC = 8


EPS_NORM = 1e-05
EPS_EMBED = 1e-06
POOL_TEMP = 0.1
LOSS_TEMP = 0.1
FULL_PRECISION = lax.Precision.HIGHEST
MASKED_SCORE = -1e30


def shortened(shard):

    def short(part):
        return part.astype(jnp.bfloat16) if part.dtype == jnp.float32 else part

    return jax.tree.map(short, shard)


def contract_rows(left, right, precision=None):
    return lax.dot_general(
        left,
        right,
        (((0,), (0,)), ((), ())),
        precision=precision,
        preferred_element_type=jnp.float32,
    )


def contract_cols(left, right, precision=None):
    return lax.dot_general(
        left,
        right,
        (((1,), (1,)), ((), ())),
        precision=precision,
        preferred_element_type=jnp.float32,
    )


def norm_forward(value, gain, shift):
    centred = value - jnp.mean(value, axis=1, keepdims=True)
    rstd = lax.rsqrt(jnp.mean(centred * centred, axis=1, keepdims=True) + EPS_NORM)
    unit = centred * rstd
    return (unit * gain + shift, unit, rstd)


def norm_backward(grad, unit, rstd, gain):
    scaled = grad * gain
    return rstd * (
        scaled
        - jnp.mean(scaled, axis=1, keepdims=True)
        - unit * jnp.mean(scaled * unit, axis=1, keepdims=True)
    )


def segments_of(row_lengths, token_count):
    position = jnp.arange(token_count, dtype=jnp.int32)
    query_span = NQ_ROW * QLEN
    ends = jnp.cumsum(row_lengths)
    passed = jnp.sum((position[:, None] - query_span >= ends[None, :]).astype(jnp.int32), axis=1)
    return jnp.where(position < query_span, position // QLEN, NQ_ROW + passed)


def normalize_cut(raw, width):
    part = raw[:, :width]
    scale = lax.rsqrt(jnp.sum(part * part, axis=1, keepdims=True) + EPS_EMBED)
    return (part * scale, part, scale)


def normalize_back(grad, part, scale, full_width):
    result = scale * grad - part * (scale * scale * scale) * jnp.sum(
        part * grad, axis=1, keepdims=True
    )
    return jnp.pad(result, ((0, 0), (0, full_width - grad.shape[1])))


def masked_scores(query_block, key_rows, block_segments, segments):
    scores = jnp.einsum(
        "qhd,khd->hqk", query_block, key_rows, preferred_element_type=jnp.float32
    ) * HEAD_DIM ** (-0.5)
    return jnp.where((block_segments[:, None] == segments[None, :])[None], scores, MASKED_SCORE)


def attend_forward(query_rows, key_rows, value_rows, segments, block_rows):
    token_count = query_rows.shape[0]

    def one_block(block_start):
        query_block = lax.dynamic_slice_in_dim(query_rows, block_start, block_rows, 0)
        block_segments = lax.dynamic_slice_in_dim(segments, block_start, block_rows, 0)
        scores = masked_scores(query_block, key_rows, block_segments, segments)
        highest = jnp.max(scores, axis=2, keepdims=True)
        expo = jnp.exp(scores - highest)
        totals = jnp.sum(expo, axis=2, keepdims=True)
        weights = (expo / totals).astype(jnp.bfloat16)
        mixed = jnp.einsum("hqk,khd->qhd", weights, value_rows, preferred_element_type=jnp.float32)
        return (mixed.astype(jnp.bfloat16), (highest + jnp.log(totals))[:, :, 0])

    starts = jnp.arange(token_count // block_rows, dtype=jnp.int32) * block_rows
    mixed, log_totals = lax.map(one_block, starts)
    return (mixed.reshape(token_count, -1), log_totals)


def attend_backward(query_rows, key_rows, value_rows, segments, log_totals, grad_mixed, block_rows):
    token_count, local_heads, head_size = query_rows.shape
    scale = HEAD_DIM ** (-0.5)
    grad_heads = grad_mixed.reshape(token_count, local_heads, head_size)

    def one_block(carried, inputs):
        grad_keys, grad_values = carried
        block_start, block_lse = inputs
        query_block = lax.dynamic_slice_in_dim(query_rows, block_start, block_rows, 0)
        grad_block = lax.dynamic_slice_in_dim(grad_heads, block_start, block_rows, 0)
        block_segments = lax.dynamic_slice_in_dim(segments, block_start, block_rows, 0)
        scores = masked_scores(query_block, key_rows, block_segments, segments)
        probs = jnp.exp(scores - block_lse[:, :, None])
        grad_probs = jnp.einsum(
            "qhd,khd->hqk", grad_block, value_rows, preferred_element_type=jnp.float32
        )
        inner = jnp.sum(probs * grad_probs, axis=2, keepdims=True)
        grad_scores = (probs * (grad_probs - inner)).astype(jnp.bfloat16)
        grad_query = (
            jnp.einsum("hqk,khd->qhd", grad_scores, key_rows, preferred_element_type=jnp.float32)
            * scale
        )
        grad_keys = (
            grad_keys
            + jnp.einsum(
                "hqk,qhd->khd", grad_scores, query_block, preferred_element_type=jnp.float32
            )
            * scale
        )
        grad_values = grad_values + jnp.einsum(
            "hqk,qhd->khd",
            probs.astype(jnp.bfloat16),
            grad_block,
            preferred_element_type=jnp.float32,
        )
        return ((grad_keys, grad_values), grad_query)

    starts = jnp.arange(token_count // block_rows, dtype=jnp.int32) * block_rows
    zero_rows = jnp.zeros(key_rows.shape, jnp.float32)
    (grad_keys, grad_values), grad_queries = lax.scan(
        one_block, (zero_rows, zero_rows), (starts, log_totals)
    )
    flat_width = local_heads * head_size
    return (
        grad_queries.reshape(token_count, flat_width),
        grad_keys.reshape(token_count, flat_width),
        grad_values.reshape(token_count, flat_width),
    )


def local(
    tokens,
    lengths,
    pairing,
    w_qkv,
    b_qv,
    w_out,
    b_out,
    ln_gain,
    ln_bias,
    w_up,
    b_up,
    w_down,
    b_down,
    w_proj,
    cot,
):
    tensor_count = lax.axis_size("tensor")
    tensor_index = lax.axis_index("tensor")
    data_index = lax.axis_index("dp")
    token_count = tokens.shape[0]
    share_rows = token_count // tensor_count
    block_rows = min(512, token_count)
    own_start = tensor_index * share_rows
    full_qkv, full_out, full_up, full_down = (
        lax.all_gather(w_qkv, "dp", axis=1, tiled=True),
        lax.all_gather(w_out, "dp", axis=1, tiled=True),
        lax.all_gather(w_up, "dp", axis=0, tiled=True),
        lax.all_gather(w_down, "dp", axis=1, tiled=True),
    )
    head_width = full_qkv.shape[2]
    local_heads = head_width // HEAD_DIM
    row_lengths = lax.dynamic_index_in_dim(lengths, data_index, 0, keepdims=False)
    segments = segments_of(row_lengths, token_count)
    projected = jnp.einsum("td,kdw->ktw", tokens, full_qkv, preferred_element_type=jnp.float32)
    qv_bias = b_qv.astype(jnp.float32)
    query_rows = (
        (projected[0] + qv_bias[0]).astype(jnp.bfloat16).reshape(token_count, local_heads, HEAD_DIM)
    )
    key_rows = projected[1].astype(jnp.bfloat16).reshape(token_count, local_heads, HEAD_DIM)
    value_rows = (
        (projected[2] + qv_bias[1]).astype(jnp.bfloat16).reshape(token_count, local_heads, HEAD_DIM)
    )
    mixed, log_totals = attend_forward(query_rows, key_rows, value_rows, segments, block_rows)
    attn_terms = jnp.dot(mixed, full_out, preferred_element_type=jnp.float32)
    attn_sum = lax.psum_scatter(
        attn_terms.astype(jnp.bfloat16), "tensor", scatter_dimension=0, tiled=True
    ).astype(jnp.float32)
    own_tokens = lax.dynamic_slice_in_dim(tokens, own_start, share_rows, 0).astype(jnp.float32)
    gains = ln_gain.astype(jnp.float32)
    shifts = ln_bias.astype(jnp.float32)
    normed, unit_one, rstd_one = norm_forward(
        own_tokens + attn_sum + b_out.astype(jnp.float32), gains[0], shifts[0]
    )
    normed_all = lax.all_gather(normed.astype(jnp.bfloat16), "tensor", axis=0, tiled=True)
    up_value = jnp.dot(normed_all, full_up, preferred_element_type=jnp.float32) + b_up.astype(
        jnp.float32
    )
    activation = jax.nn.gelu(up_value, approximate=False).astype(jnp.bfloat16)
    ffn_terms = jnp.dot(activation, full_down, preferred_element_type=jnp.float32)
    ffn_sum = lax.psum_scatter(
        ffn_terms.astype(jnp.bfloat16), "tensor", scatter_dimension=0, tiled=True
    ).astype(jnp.float32)
    result, unit_two, rstd_two = norm_forward(
        normed + ffn_sum + b_down.astype(jnp.float32), gains[1], shifts[1]
    )
    result_low = result.astype(jnp.bfloat16)
    embed = jnp.dot(result_low, w_proj, preferred_element_type=jnp.float32).astype(jnp.bfloat16)
    embed_all = lax.all_gather(embed, ("dp", "tensor"), axis=0, tiled=True)
    row_count = lengths.shape[0]
    proj_width = w_proj.shape[1]
    widths = (proj_width, 3 * proj_width // 4, proj_width // 2)
    per_device = pairing.shape[1]
    query_count = per_device * QLEN
    query_span = NQ_ROW * QLEN
    emb_rows = embed_all.reshape(row_count, token_count, proj_width)
    my_row = lax.dynamic_index_in_dim(emb_rows, data_index, 0, keepdims=False)
    query_raw = lax.dynamic_slice_in_dim(my_row, tensor_index * query_count, query_count, 0).astype(
        jnp.float32
    )
    query_levels = [normalize_cut(query_raw, width) for width in widths]
    query_units = [level_parts[0].astype(jnp.bfloat16) for level_parts in query_levels]
    doc_numbers = jnp.arange(NDOC, dtype=jnp.int32)

    def row_pool(carried, inputs):
        row_emb, lengths_row = inputs
        row_hot = (
            segments_of(lengths_row, token_count)[:, None] == NQ_ROW + doc_numbers[None, :]
        ).astype(jnp.float32)
        row_raw = row_emb.astype(jnp.float32)
        pooled_list = []
        sums_list = []
        for width, query_unit in zip(widths, query_units):
            doc_unit = normalize_cut(row_raw, width)[0].astype(jnp.bfloat16)
            expo = jnp.exp(contract_cols(query_unit, doc_unit) / POOL_TEMP)
            sums = jnp.dot(expo, row_hot, precision=FULL_PRECISION)
            pooled = POOL_TEMP * jnp.log(sums / lengths_row.astype(jnp.float32))
            pooled_list.append(jnp.sum(pooled.reshape(per_device, QLEN, NDOC), axis=1))
            sums_list.append(sums)
        return (carried, (jnp.stack(pooled_list), jnp.stack(sums_list)))

    _, (row_scores, row_sums) = lax.scan(row_pool, 0, (emb_rows, lengths))
    logits = (
        jnp.transpose(row_scores, (2, 1, 0, 3)).reshape(per_device, 3, row_count * NDOC) / LOSS_TEMP
    )
    own_pairs = pairing[0]
    target = jnp.take_along_axis(
        logits, jnp.broadcast_to(own_pairs[:, None, None], (per_device, 3, 1)), axis=2
    )[:, :, 0]
    loss_out = jnp.sum(jax.nn.logsumexp(logits, axis=2) - target, axis=1).reshape(1, per_device)
    picked = (
        jnp.arange(row_count * NDOC, dtype=jnp.int32)[None, None, :] == own_pairs[:, None, None]
    ).astype(jnp.float32)
    grad_logits = (jax.nn.softmax(logits, axis=2) - picked) / LOSS_TEMP
    grad_rows = jnp.transpose(grad_logits.reshape(per_device, 3, row_count, NDOC), (2, 1, 0, 3))
    coefficient = jnp.repeat(grad_rows, QLEN, axis=2) / row_sums

    def row_back(carried, inputs):
        row_emb, lengths_row, row_coef = inputs
        row_hot = (
            segments_of(lengths_row, token_count)[:, None] == NQ_ROW + doc_numbers[None, :]
        ).astype(jnp.float32)
        row_raw = row_emb.astype(jnp.float32)
        new_carried = []
        row_grad = jnp.zeros((token_count, proj_width), jnp.float32)
        for level_index in range(3):
            width = widths[level_index]
            doc_unit_f, doc_part, doc_scale = normalize_cut(row_raw, width)
            doc_unit = doc_unit_f.astype(jnp.bfloat16)
            expo = jnp.exp(contract_cols(query_units[level_index], doc_unit) / POOL_TEMP)
            spread = contract_cols(row_coef[level_index], row_hot, FULL_PRECISION)
            grad_sim = (expo * spread).astype(jnp.bfloat16)
            new_carried.append(
                carried[level_index]
                + jnp.dot(grad_sim, doc_unit, preferred_element_type=jnp.float32)
            )
        return (tuple(new_carried), row_grad)

    zero_query = tuple((jnp.zeros((query_count, width), jnp.float32) for width in widths))
    query_grads, doc_grads = lax.scan(row_back, zero_query, (emb_rows, lengths, coefficient))
    grad_query = jnp.zeros((query_count, proj_width), jnp.float32)
    for level_index in range(3):
        level_parts = query_levels[level_index]
        grad_query = grad_query + normalize_back(
            query_grads[level_index], level_parts[1], level_parts[2], proj_width
        )
    coef_mine = jnp.transpose(coefficient, (2, 1, 0, 3)).reshape(query_count, 3, row_count * NDOC)
    coef_all, grad_query_all = (
        lax.all_gather(shortened(coef_mine), ("dp", "tensor"), axis=0, tiled=True).astype(
            coef_mine.dtype
        ),
        lax.all_gather(
            grad_query.astype(jnp.bfloat16), ("dp", "tensor"), axis=0, tiled=True
        ).astype(grad_query.dtype),
    )
    own_raw = embed.astype(jnp.float32)
    own_segments = lax.dynamic_slice_in_dim(segments, own_start, share_rows, 0)
    own_docs = jnp.where(own_segments >= NQ_ROW, data_index * NDOC + own_segments - NQ_ROW, -1)
    own_hot = (own_docs[:, None] == jnp.arange(row_count * NDOC, dtype=jnp.int32)[None, :]).astype(
        jnp.float32
    )
    queries_all = (
        emb_rows[:, :query_span].reshape(row_count * query_span, proj_width).astype(jnp.float32)
    )
    grad_embed = jnp.zeros((share_rows, proj_width), jnp.float32)
    for level_index in range(3):
        width = widths[level_index]
        query_unit_all = normalize_cut(queries_all, width)[0].astype(jnp.bfloat16)
        doc_unit_f, doc_part, doc_scale = normalize_cut(own_raw, width)
        expo = jnp.exp(contract_cols(query_unit_all, doc_unit_f.astype(jnp.bfloat16)) / POOL_TEMP)
        spread = contract_cols(coef_all[:, level_index], own_hot, FULL_PRECISION)
        grad_sim = (expo * spread).astype(jnp.bfloat16)
        grad_doc = contract_rows(grad_sim, query_unit_all)
        grad_embed = grad_embed + normalize_back(grad_doc, doc_part, doc_scale, proj_width)
    row_query_grads = lax.dynamic_slice_in_dim(
        grad_query_all, data_index * query_span, query_span, 0
    )
    padded = jnp.pad(row_query_grads, ((0, token_count - query_span), (0, 0)))
    grad_embed = grad_embed + lax.dynamic_slice_in_dim(padded, own_start, share_rows, 0)
    proj_float = w_proj.astype(jnp.float32)
    grad_result = cot.astype(jnp.float32) + contract_cols(grad_embed, proj_float, FULL_PRECISION)
    proj_grad = contract_rows(result_low.astype(jnp.float32), grad_embed, FULL_PRECISION)
    gain_two = jnp.sum(grad_result * unit_two, axis=0)
    shift_two = jnp.sum(grad_result, axis=0)
    grad_second = norm_backward(grad_result, unit_two, rstd_two, gains[1])
    grad_ffn = grad_second.astype(jnp.bfloat16)
    down_bias = jnp.sum(grad_ffn.astype(jnp.float32), axis=0)
    grad_ffn_all = lax.all_gather(grad_ffn, "tensor", axis=0, tiled=True)
    grad_act = contract_cols(grad_ffn_all, full_down)
    down_grad = contract_rows(activation, grad_ffn_all)
    _, gelu_pull = jax.vjp(partial(jax.nn.gelu, approximate=False), up_value)
    grad_up = gelu_pull(grad_act)[0].astype(jnp.bfloat16)
    up_bias = jnp.sum(grad_up.astype(jnp.float32), axis=0)
    up_grad = contract_rows(normed_all, grad_up)
    normed_terms = contract_cols(grad_up, full_up)
    grad_normed = (
        lax.psum_scatter(
            normed_terms.astype(jnp.bfloat16), "tensor", scatter_dimension=0, tiled=True
        ).astype(jnp.float32)
        + grad_second
    )
    gain_one = jnp.sum(grad_normed * unit_one, axis=0)
    shift_one = jnp.sum(grad_normed, axis=0)
    grad_first = norm_backward(grad_normed, unit_one, rstd_one, gains[0])
    grad_attn = grad_first.astype(jnp.bfloat16)
    out_bias = jnp.sum(grad_attn.astype(jnp.float32), axis=0)
    grad_attn_all = lax.all_gather(grad_attn, "tensor", axis=0, tiled=True)
    out_grad = contract_rows(mixed, grad_attn_all)
    grad_mixed = contract_cols(grad_attn_all, full_out).astype(jnp.bfloat16)
    grad_q, grad_k, grad_v = attend_backward(
        query_rows, key_rows, value_rows, segments, log_totals, grad_mixed, block_rows
    )
    stacked_grads = jnp.stack(
        [grad_q.astype(jnp.bfloat16), grad_k.astype(jnp.bfloat16), grad_v.astype(jnp.bfloat16)]
    )
    qkv_grad = jnp.einsum("td,ktw->kdw", tokens, stacked_grads, preferred_element_type=jnp.float32)
    input_terms = jnp.einsum(
        "ktw,kdw->td", stacked_grads, full_qkv, preferred_element_type=jnp.float32
    )
    grad_input = (
        lax.psum_scatter(
            input_terms.astype(jnp.bfloat16), "tensor", scatter_dimension=0, tiled=True
        ).astype(jnp.float32)
        + grad_first
    )
    qv_grad = jnp.stack(
        [
            jnp.sum(stacked_grads[0].astype(jnp.float32), axis=0),
            jnp.sum(stacked_grads[2].astype(jnp.float32), axis=0),
        ]
    )
    qkv_part, out_part, up_part, down_part = (
        lax.psum_scatter(
            qkv_grad.astype(jnp.bfloat16), "dp", scatter_dimension=1, tiled=True
        ).astype(jnp.float32),
        lax.psum_scatter(
            out_grad.astype(jnp.bfloat16), "dp", scatter_dimension=1, tiled=True
        ).astype(jnp.float32),
        lax.psum_scatter(
            up_grad.astype(jnp.bfloat16), "dp", scatter_dimension=0, tiled=True
        ).astype(jnp.float32),
        lax.psum_scatter(
            down_grad.astype(jnp.bfloat16), "dp", scatter_dimension=1, tiled=True
        ).astype(jnp.float32),
    )
    gain_sum, shift_sum, out_bias_sum, down_bias_sum, proj_sum = lax.psum(
        (
            jnp.stack([gain_one, gain_two]),
            jnp.stack([shift_one, shift_two]),
            out_bias,
            down_bias,
            proj_grad,
        ),
        ("dp", "tensor"),
    )
    qv_sum, up_bias_sum = lax.psum((qv_grad, up_bias), "dp")
    return (
        result_low,
        loss_out,
        grad_input.astype(jnp.bfloat16),
        qkv_part,
        qv_sum,
        out_part,
        out_bias_sum,
        gain_sum,
        shift_sum,
        up_part,
        up_bias_sum,
        down_part,
        down_bias_sum,
        proj_sum,
    )


SWAP = [(0, 1), (1, 0)]
TURN = [(0, 0), (1, 2), (2, 1), (3, 3)]
FAR = [(0, 3), (3, 0), (1, 2), (2, 1)]
NEAR = [(0, 1), (1, 0), (2, 3), (3, 2)]
BF = jnp.bfloat16
F32 = jnp.float32


def dot(left, right):
    return jnp.dot(left, right, preferred_element_type=F32)


CORES = ("c", "y")


def tie(value, *others):
    return lax.optimization_barrier((value,) + others)[0]


def tie_all(values, *others):
    return lax.optimization_barrier(tuple(values) + others)[: len(values)]


def exchange(*moves):
    return lax.optimization_barrier(
        tuple(lax.ppermute(value, axis, steps) for value, axis, steps in moves)
    )


def swap(value, axis):
    return lax.ppermute(value, axis, SWAP)


def pair_up(first, second, own_index, axis):
    return jnp.where(
        own_index == 0, jnp.stack([first, second], axis), jnp.stack([second, first], axis)
    )


def far_pair(value, far, z):
    return jnp.where(z < 2, jnp.stack([value, far]), jnp.stack([far, value]))


def whole_line(pair, other, z):
    return jnp.where(
        (z == 0) | (z == 3),
        jnp.stack([pair[0], other[0], other[1], pair[1]]),
        jnp.stack([other[0], pair[0], pair[1], other[1]]),
    )


def first_moves(line):
    half = line.shape[1] // 2
    return ((line[:, :half], "x", SWAP), (line[:, half:], "y", SWAP))


def first_parts(line, moved, x, y):
    half = line.shape[1] // 2
    return (pair_up(line[:, :half], moved[0], x, 1), pair_up(line[:, half:], moved[1], y, 1))


def last_moves(parts):
    return ((parts[0], "y", SWAP), (parts[1], "x", SWAP))


def full_rows(parts, moved, x, y):
    low = pair_up(parts[0], moved[0], y, 2)
    high = pair_up(parts[1], moved[1], x, 1)
    return jnp.concatenate([low, high], axis=3).reshape(-1, low.shape[-1])


def at(blocks, index, axis):
    return lax.dynamic_index_in_dim(blocks, index, axis, keepdims=False)


def side_move(blocks, axis_name, own_index, axis):
    return (at(blocks, 1 - own_index, axis).astype(BF), axis_name, SWAP)


def side_sum(blocks, got, own_index, axis):
    return at(blocks, own_index, axis).astype(F32) + got.astype(F32)


def near_move(line, z):
    ends = (z == 0) | (z == 3)
    outer, inner = jnp.stack([line[0], line[3]]), line[1:3]
    return (jnp.where(ends, inner, outer).astype(BF), "z", NEAR)


def near_sum(line, got, z):
    ends = (z == 0) | (z == 3)
    return jnp.where(ends, jnp.stack([line[0], line[3]]), line[1:3]) + got.astype(F32)


def far_move(pair, z):
    return (jnp.where(z < 2, pair[1], pair[0]).astype(BF), "z", FAR)


def far_sum(pair, got, z):
    return jnp.where(z < 2, pair[0], pair[1]) + got.astype(F32)


def blocks_of(left, right):
    return contract_rows(left, right).astype(BF).reshape(4, 2, 2, 64, right.shape[1])


def sum_moves(blocks, x, y):
    half = blocks.shape[3] // 2
    return (
        side_move(blocks[..., :half, :], "x", x, 1),
        side_move(blocks[..., half:, :], "y", y, 2),
    )


def sum_parts(blocks, moved, x, y):
    half = blocks.shape[3] // 2
    return (
        side_sum(blocks[..., :half, :], moved[0], x, 1),
        side_sum(blocks[..., half:, :], moved[1], y, 2),
    )


def line_moves(parts, x, y):
    return (side_move(parts[0], "y", y, 1), side_move(parts[1], "x", x, 1))


def line_of(parts, moved, x, y):
    return jnp.concatenate(
        [side_sum(parts[0], moved[0], y, 1), side_sum(parts[1], moved[1], x, 1)], axis=1
    )


def tile_bounds(row_lengths, token_count):
    ends = jnp.cumsum(row_lengths)
    span = NQ_ROW * QLEN
    first = jnp.arange(token_count // TILE, dtype=jnp.int32) * TILE - span
    last = first + TILE - 1
    begin = jnp.max(jnp.where(ends[None, :] <= first[:, None], ends[None, :], 0), axis=1)
    end = jnp.min(jnp.where(ends[None, :] > last[:, None], ends[None, :], token_count), axis=1)
    low = jnp.where(first < 0, 0, (begin + span) // TILE)
    high = jnp.where(first < 0, 1, (end + span + TILE - 1) // TILE)
    return jnp.stack([low, high]).astype(jnp.int32)


def token_spans(row_lengths, token_count):
    ends = jnp.cumsum(row_lengths)[:, None]
    span = NQ_ROW * QLEN
    place = jnp.arange(token_count, dtype=jnp.int32)[None, :]
    doc = place - span
    begin = jnp.max(jnp.where(ends <= doc, ends, 0), axis=0) + span
    end = jnp.min(jnp.where(ends > doc, ends, token_count), axis=0) + span
    query = place[0] // QLEN * QLEN
    return jnp.stack(
        [jnp.where(doc[0] < 0, query, begin), jnp.where(doc[0] < 0, query + QLEN, end)]
    ).astype(jnp.int32)


def rows_of(value, start, count):
    return lax.dynamic_slice_in_dim(value, start, count, 0)


TILE = 256
KEYS = 256
LOSS_TILE = 1024
NEG = -1e30


def exact(left, right, dims):
    return lax.dot_general(left, right, (dims, ((), ())), preferred_element_type=F32)


def head_masks(value):
    lane = lax.broadcasted_iota(jnp.int32, value.shape, 1)
    zero = jnp.zeros_like(value)
    return (jnp.where(lane < HEAD_DIM, value, zero), jnp.where(lane < HEAD_DIM, zero, value))


def key_shift(step, spans):
    place = step * KEYS + lax.broadcasted_iota(jnp.int32, (KEYS, TILE), 0)
    inside = (place >= spans[0:1, :]) & (place < spans[1:2, :])
    return jnp.where(inside, 0.0, NEG)


def attend_kernel(bounds, own_ref, qkv_ref, spans, out_ref, lse_ref, held):
    block = pl.program_id(0)
    groups = 2
    pairs = out_ref.shape[1] // 128
    per_group = pairs // groups

    def column(pair, part):
        start = ((pair // per_group) * 3 + part) * per_group + pair % per_group
        return slice(start * 128, (start + 1) * 128)

    queries = [head_masks(own_ref[:, column(pair, 0)] * HEAD_DIM**-0.5) for pair in range(pairs)]
    heads = [(pair, head) for pair in range(pairs) for head in range(2)]

    def score(step, highest):
        rows = pl.ds(pl.multiple_of(step * KEYS, KEYS), KEYS)
        shift = key_shift(step, spans)
        fresh = []
        for index, (pair, head) in enumerate(heads):
            keys = qkv_ref[rows, column(pair, 1)]
            scores = exact(keys, queries[pair][head], ((1,), (1,))) + shift
            held[index, rows, :] = scores
            fresh.append(jnp.maximum(highest[index], jnp.max(scores, axis=0, keepdims=True)))
        return tuple(fresh)

    low = jnp.full((1, TILE), NEG, F32)
    highest = lax.fori_loop(bounds[0, block], bounds[1, block], score, (low,) * len(heads))

    def mix(step, carried):
        rows = pl.ds(pl.multiple_of(step * KEYS, KEYS), KEYS)
        fresh = []
        for index, (pair, head) in enumerate(heads):
            values = qkv_ref[rows, column(pair, 2)]
            total, mixed = carried[index]
            expo = jnp.exp(held[index, rows, :] - highest[index])
            product = exact(values, expo.astype(BF), ((0,), (0,)))
            fresh.append(
                (
                    total + jnp.sum(expo, axis=0, keepdims=True),
                    mixed + product[head * HEAD_DIM : (head + 1) * HEAD_DIM],
                )
            )
        return tuple(fresh)

    start = (jnp.zeros((1, TILE), F32), jnp.zeros((HEAD_DIM, TILE), F32))
    parts = lax.fori_loop(bounds[0, block], bounds[1, block], mix, (start,) * len(heads))
    for pair in range(pairs):
        both = [parts[2 * pair + head][1] / parts[2 * pair + head][0] for head in range(2)]
        mixed = jnp.transpose(jnp.concatenate(both, axis=0))
        out_ref[:, pair * 128 : (pair + 1) * 128] = mixed.astype(BF)
    for index in range(len(heads)):
        lse_ref[index : index + 1, :] = highest[index] + jnp.log(parts[index][0])


def attend(bounds, qkv, spans):
    count, wide = qkv.shape
    heads = wide // 3 // HEAD_DIM
    whole = lambda shape: pl.BlockSpec(shape, lambda i: (0, 0))
    return pl.pallas_call(
        attend_kernel,
        grid=(count // TILE,),
        in_specs=[
            pl.BlockSpec(memory_space=pltpu.SMEM),
            pl.BlockSpec((TILE, wide), lambda i: (i, 0)),
            whole((count, wide)),
            pl.BlockSpec((2, TILE), lambda i: (0, i)),
        ],
        out_specs=[
            pl.BlockSpec((TILE, wide // 3), lambda i: (i, 0)),
            pl.BlockSpec((heads, TILE), lambda i: (0, i)),
        ],
        out_shape=[
            jax.ShapeDtypeStruct((count, wide // 3), BF),
            jax.ShapeDtypeStruct((heads, count), F32),
        ],
        scratch_shapes=[pltpu.VMEM((heads, count, TILE), F32)],
        compiler_params=pltpu.CompilerParams(vmem_limit_bytes=40 << 20),
        cost_estimate=pl.CostEstimate(
            flops=4 * heads * count * count * 64,
            transcendentals=heads * count * count // 2,
            bytes_accessed=4 * count * wide * 2,
        ),
    )(bounds, qkv, qkv, spans)


def attend_back_kernel(
    first, bounds, own_ref, qkv_ref, out_ref, grad_ref, lse_ref, spans,
    grads_ref, sums_ref, key_sum, value_sum,
):
    block = pl.program_id(0)
    pairs = out_ref.shape[1] // 128
    heads = [(pair, head) for pair in range(pairs) for head in range(2)]
    cut = lambda index: slice(index * 128, (index + 1) * 128)

    @pl.when(block == 0)
    def _():
        key_sum[...] = jnp.zeros_like(key_sum)
        value_sum[...] = jnp.zeros_like(value_sum)
        sums_ref[...] = jnp.zeros_like(sums_ref)

    queries = [head_masks(own_ref[:, cut(pair)] * HEAD_DIM**-0.5) for pair in range(pairs)]
    grads = [head_masks(grad_ref[:, cut(pair)]) for pair in range(pairs)]
    picks = head_masks(jnp.ones((8, 128), BF))
    inner = []
    for pair, head in heads:
        product = grad_ref[:, cut(pair)].astype(F32) * out_ref[:, cut(pair)].astype(F32)
        high = product.astype(BF)
        rest = (product - high.astype(F32)).astype(BF)
        inner.append(
            (
                exact(picks[head], high, ((1,), (1,))) + exact(picks[head], rest, ((1,), (1,)))
            )[0:1]
        )
    lse = [lse_ref[first + index : first + index + 1, :] for index in range(len(heads))]

    def step_of(step, carried):
        rows = pl.ds(pl.multiple_of(step * KEYS, KEYS), KEYS)
        shift = key_shift(step, spans)
        fresh = []
        for pair in range(pairs):
            keys = qkv_ref[rows, cut(pairs + pair)]
            values = qkv_ref[rows, cut(2 * pairs + pair)]
            key_add = jnp.zeros((KEYS, 128), F32)
            value_add = jnp.zeros((KEYS, 128), F32)
            for head in range(2):
                index = 2 * pair + head
                scores = exact(keys, queries[pair][head], ((1,), (1,))) + shift
                probs = jnp.exp(scores - lse[index])
                grad_probs = exact(values, grads[pair][head], ((1,), (1,)))
                grad_scores = (probs * (grad_probs - inner[index])).astype(BF)
                value_add = value_add + exact(probs.astype(BF), grads[pair][head], ((1,), (0,)))
                key_add = key_add + exact(grad_scores, queries[pair][head], ((1,), (0,)))
                product = exact(keys, grad_scores, ((0,), (0,)))
                fresh.append(carried[index] + product[head * HEAD_DIM : (head + 1) * HEAD_DIM])
            key_sum[rows, cut(pair)] += key_add
            value_sum[rows, cut(pair)] += value_add
        return tuple(fresh)

    start = jnp.zeros((HEAD_DIM, TILE), F32)
    parts = lax.fori_loop(bounds[0, block], bounds[1, block], step_of, (start,) * len(heads))
    own = pl.ds(pl.multiple_of(block * TILE, TILE), TILE)
    for pair in range(pairs):
        grad_query = jnp.concatenate([parts[2 * pair], parts[2 * pair + 1]], axis=0)
        grad_query = jnp.transpose(grad_query * HEAD_DIM**-0.5).astype(BF)
        grads_ref[own, cut(pair)] = grad_query
        sums_ref[0:1, cut(pair)] += jnp.sum(grad_query.astype(F32), axis=0, keepdims=True)

    @pl.when(block == pl.num_programs(0) - 1)
    def _():
        wide = pairs * 128
        grad_value = value_sum[...].astype(BF)
        grads_ref[:, wide : 2 * wide] = key_sum[...].astype(BF)
        grads_ref[:, 2 * wide :] = grad_value
        sums_ref[1:2, :] = jnp.sum(grad_value.astype(F32), axis=0, keepdims=True)


def attend_back(bounds, group, qkv, mixed, grad_mixed, lse, spans):
    count = qkv.shape[0]
    wide = qkv.shape[1] // 2
    heads = wide // 3 // HEAD_DIM
    whole = lambda shape: pl.BlockSpec(shape, lambda i: (0, 0))
    return pl.pallas_call(
        partial(attend_back_kernel, group * heads),
        grid=(count // TILE,),
        in_specs=[
            pl.BlockSpec(memory_space=pltpu.SMEM),
            pl.BlockSpec((TILE, wide), lambda i: (i, group)),
            pl.BlockSpec((count, wide), lambda i: (0, group)),
            pl.BlockSpec((TILE, wide // 3), lambda i: (i, group)),
            pl.BlockSpec((TILE, wide // 3), lambda i: (i, group)),
            pl.BlockSpec((2 * heads, TILE), lambda i: (0, i)),
            pl.BlockSpec((2, TILE), lambda i: (0, i)),
        ],
        out_specs=[whole((count, wide)), whole((8, wide // 3))],
        out_shape=[
            jax.ShapeDtypeStruct((count, wide), BF),
            jax.ShapeDtypeStruct((8, wide // 3), F32),
        ],
        scratch_shapes=[
            pltpu.VMEM((count, wide // 3), F32),
            pltpu.VMEM((count, wide // 3), F32),
        ],
        compiler_params=pltpu.CompilerParams(vmem_limit_bytes=40 << 20),
        cost_estimate=pl.CostEstimate(
            flops=10 * heads * count * count * 64,
            transcendentals=heads * count * count // 2,
            bytes_accessed=8 * count * wide * 2,
        ),
    )(
        bounds, qkv, qkv, mixed, grad_mixed,
        lse, spans,
    )


ERFC = (
    -1.26551223, 1.00002368, 0.37409196, 0.09678418, -0.18628806,
    0.27886807, -1.13520398, 1.48851587, -0.82215223, 0.17087277,
)


def gelu_pair(value):
    size = jnp.abs(value) * 0.5**0.5
    ratio = 1.0 / (1.0 + 0.5 * size)
    series = jnp.full_like(value, ERFC[-1])
    for factor in ERFC[-2::-1]:
        series = series * ratio + factor
    bell = jnp.exp(-size * size)
    tail = 0.5 * ratio * bell * jnp.exp(series)
    phi = jnp.where(value < 0.0, tail, 1.0 - tail)
    return (value * phi, phi + value * bell * 0.3989422804014327)


def expand_kernel(x_ref, w_ref, b_ref, *refs):
    act_ref, slope_ref = refs[-2:]
    rows = 128
    for start in range(0, x_ref.shape[0], rows):
        part = slice(start, start + rows)
        value = exact(x_ref[part, :], w_ref[...], ((1,), (0,))) + b_ref[...]
        active, slope = gelu_pair(value)
        act_ref[part, :] = active.astype(BF)
        slope_ref[part, :] = slope.astype(BF)


def expand(value, weight, shift, first, tiles, filled=()):
    count, depth = value.shape
    width = shift.shape[1]
    tile = 256
    column = lambda rows: pl.BlockSpec((rows, tile), lambda i: (0, first + i))
    return pl.pallas_call(
        expand_kernel,
        grid=(tiles,),
        in_specs=[
            pl.BlockSpec((count, depth), lambda i: (0, 0)),
            column(depth),
            column(1),
        ]
        + [pl.BlockSpec(memory_space=pl.ANY)] * len(filled),
        out_specs=[column(count)] * 2,
        out_shape=[jax.ShapeDtypeStruct((count, width), BF)] * 2,
        input_output_aliases={3: 0, 4: 1} if filled else {},
        compiler_params=pltpu.CompilerParams(vmem_limit_bytes=32 << 20),
        cost_estimate=pl.CostEstimate(
            flops=2 * count * depth * tile * tiles,
            transcendentals=3 * count * tile * tiles,
            bytes_accessed=2 * (count * depth + depth * tile * tiles + 2 * count * tile * tiles),
        ),
    )(value, weight, shift, *filled)


def cut_levels(raw, cuts):
    lane = lax.broadcasted_iota(jnp.int32, raw.shape, 1)
    levels = []
    for cut in cuts:
        part = jnp.where(lane < cut, raw, 0.0)
        scale = lax.rsqrt(jnp.sum(part * part, axis=1, keepdims=True) + EPS_EMBED)
        levels.append(((part * scale).astype(BF), part, scale))
    return levels


def pool_kernel(cuts, span, q_ref, d_ref, seg_ref, out_ref, units, hot):
    @pl.when(pl.program_id(0) == 0)
    def _():
        raw = d_ref[span:, :].astype(F32)
        for level, parts in enumerate(cut_levels(raw, cuts)):
            units[level] = parts[0]
        doc = lax.broadcasted_iota(jnp.int32, hot.shape, 0)
        hot[...] = (seg_ref[:, span:] == NQ_ROW + doc).astype(F32).astype(BF)

    levels = cut_levels(q_ref[...].astype(F32), cuts)
    for level in range(len(cuts)):
        similar = exact(units[level], levels[level][0], ((1,), (1,)))
        expo = jnp.exp(similar * (1.0 / POOL_TEMP))
        high = expo.astype(BF)
        rest = (expo - high.astype(F32)).astype(BF)
        out_ref[level * NDOC : (level + 1) * NDOC, :] = exact(
            hot[...], high, ((1,), (0,))
        ) + exact(hot[...], rest, ((1,), (0,)))


def pool(cuts, span, queries, row_embed, seg_row):
    count, width = queries.shape
    tokens = row_embed.shape[0]
    whole = lambda shape: pl.BlockSpec(shape, lambda i: (0, 0))
    return pl.pallas_call(
        partial(pool_kernel, cuts, span),
        grid=(count // LOSS_TILE,),
        in_specs=[
            pl.BlockSpec((LOSS_TILE, width), lambda i: (i, 0)),
            whole((tokens, width)),
            whole((1, tokens)),
        ],
        out_specs=pl.BlockSpec((len(cuts) * NDOC, LOSS_TILE), lambda i: (0, i)),
        out_shape=jax.ShapeDtypeStruct((len(cuts) * NDOC, count), F32),
        scratch_shapes=[
            pltpu.VMEM((len(cuts), tokens - span, width), BF),
            pltpu.VMEM((NDOC, tokens - span), BF),
        ],
        compiler_params=pltpu.CompilerParams(vmem_limit_bytes=32 << 20),
        cost_estimate=pl.CostEstimate(
            flops=2 * len(cuts) * count * tokens * 256,
            transcendentals=len(cuts) * count * tokens,
            bytes_accessed=2 * (count + tokens) * width,
        ),
    )(queries, row_embed, seg_row)


def level_back(grad, part, scale):
    return scale * grad - part * (scale * scale * scale) * jnp.sum(
        part * grad, axis=1, keepdims=True
    )


def pool_back_kernel(
    cuts, span, q_ref, d_ref, seg_ref, coef_ref, q_out, d_out, units, units_t, hot, sums
):
    step = pl.program_id(0)

    @pl.when(step == 0)
    def _():
        raw = d_ref[span:, :].astype(F32)
        for level, parts in enumerate(cut_levels(raw, cuts)):
            units[level] = parts[0]
            units_t[level] = jnp.transpose(parts[0])
        doc = lax.broadcasted_iota(jnp.int32, hot.shape, 0)
        wanted = NQ_ROW + jnp.where(doc < NDOC, doc, doc - NDOC)
        hot[...] = (seg_ref[:, span:] == wanted).astype(F32).astype(BF)
        sums[...] = jnp.zeros_like(sums)

    levels = cut_levels(q_ref[...].astype(F32), cuts)
    total = jnp.zeros(q_ref.shape, F32)
    for level in range(len(cuts)):
        unit, part, scale = levels[level]
        similar = exact(units[level], unit, ((1,), (1,)))
        coef = coef_ref[level * NDOC : (level + 1) * NDOC, :]
        high = coef.astype(BF).astype(F32)
        both = jnp.concatenate([high, coef - high], axis=0).astype(BF)
        spread = exact(hot[...], both, ((0,), (0,)))
        grad = (jnp.exp(similar * (1.0 / POOL_TEMP)) * spread).astype(BF)
        sums[level] += exact(grad, unit, ((1,), (0,)))
        grad_unit = jnp.transpose(exact(units_t[level], grad, ((1,), (0,))))
        total = total + level_back(grad_unit, part, scale)
    q_out[...] = total.astype(BF)

    @pl.when(step == pl.num_programs(0) - 1)
    def _():
        raw = d_ref[span:, :].astype(F32)
        result = jnp.zeros(raw.shape, F32)
        for level, parts in enumerate(cut_levels(raw, cuts)):
            lane = lax.broadcasted_iota(jnp.int32, raw.shape, 1)
            grad = jnp.where(lane < cuts[level], sums[level], 0.0)
            result = result + level_back(grad, parts[1], parts[2])
        d_out[...] = result


def pool_back(cuts, span, queries, row_embed, seg_row, coef):
    count, width = queries.shape
    tokens = row_embed.shape[0]
    docs = tokens - span
    whole = lambda shape: pl.BlockSpec(shape, lambda i: (0, 0))
    return pl.pallas_call(
        partial(pool_back_kernel, cuts, span),
        grid=(count // LOSS_TILE,),
        in_specs=[
            pl.BlockSpec((LOSS_TILE, width), lambda i: (i, 0)),
            whole((tokens, width)),
            whole((1, tokens)),
            pl.BlockSpec((len(cuts) * NDOC, LOSS_TILE), lambda i: (0, i)),
        ],
        out_specs=[pl.BlockSpec((LOSS_TILE, width), lambda i: (i, 0)), whole((docs, width))],
        out_shape=[
            jax.ShapeDtypeStruct((count, width), BF),
            jax.ShapeDtypeStruct((docs, width), F32),
        ],
        scratch_shapes=[
            pltpu.VMEM((len(cuts), docs, width), BF),
            pltpu.VMEM((len(cuts), width, docs), BF),
            pltpu.VMEM((2 * NDOC, docs), BF),
            pltpu.VMEM((len(cuts), docs, width), F32),
        ],
        compiler_params=pltpu.CompilerParams(vmem_limit_bytes=32 << 20),
        cost_estimate=pl.CostEstimate(
            flops=2 * len(cuts) * count * docs * 512,
            transcendentals=len(cuts) * count * docs,
            bytes_accessed=4 * (count + tokens) * width,
        ),
    )(queries, row_embed, seg_row, coef)


def local_chip(
    tokens,
    lengths,
    pairing,
    w_qkv,
    b_qv,
    w_out,
    b_out,
    ln_gain,
    ln_bias,
    w_up,
    b_up,
    w_down,
    b_down,
    w_proj,
    cot,
):
    z, x, c, y = (lax.axis_index(name) for name in ("z", "x", "c", "y"))
    chip = 4 * z + 2 * x + y
    token_count, width = tokens.shape
    share = token_count // 2
    own_start, other_start = c * share, (1 - c) * share
    gains, shifts = ln_gain.astype(F32), ln_bias.astype(F32)

    half_width = w_qkv.shape[2]
    up_wide = w_up.shape[1]
    chip_count = lengths.shape[0]
    half_queries = NQ_ROW // 2
    query_total = chip_count * half_queries
    quarter = half_width // 2
    qkv_rows = jnp.concatenate(
        [w_qkv[k][:, g * quarter : (g + 1) * quarter] for g in range(2) for k in range(3)], axis=1
    )
    pair_rows = jnp.pad(pairing.astype(BF), ((0, 63), (0, 128 - half_queries)))
    mid_rows = jnp.concatenate([w_up, w_out.T, pair_rows], axis=1)
    bias = jnp.concatenate([b_qv.reshape(-1), b_up])[None].astype(F32)
    got = exchange(
        (qkv_rows, CORES, TURN), (tokens, "c", SWAP), (bias, "y", SWAP)
    )
    qkv_rows = got[0]
    row = jnp.where(c == y, tokens, got[1])
    bias = jnp.where(c == y, bias, got[2])
    (rest_rows,) = exchange(
        (tie(jnp.concatenate([mid_rows, w_down.T], axis=1), row), CORES, TURN)
    )
    (far,) = exchange((qkv_rows, "z", FAR))
    qkv_pair = far_pair(qkv_rows, far, z)
    mid_wide = mid_rows.shape[1]
    rest_rows = tie(rest_rows, qkv_pair)
    mid_rows, down_rows = rest_rows[:, :mid_wide], rest_rows[:, mid_wide:]
    (near,) = exchange((qkv_pair, "z", NEAR))
    qkv_line = whole_line(qkv_pair, near, z)
    (far,) = exchange((mid_rows, "z", FAR))
    mid_pair = far_pair(mid_rows, far, z)
    qkv_parts = first_parts(qkv_line, exchange(*first_moves(qkv_line)), x, y)
    (near,) = exchange((mid_pair, "z", NEAR))
    mid_line = whole_line(mid_pair, near, z)
    full_qkv = full_rows(qkv_parts, exchange(*last_moves(qkv_parts)), x, y)
    down_rows, mid_line = lax.optimization_barrier((down_rows, mid_line))
    (far,) = exchange((down_rows, "z", FAR))
    down_pair = far_pair(down_rows, far, z)
    (near,) = exchange((down_pair, "z", NEAR))
    down_line = whole_line(down_pair, near, z)
    mid_parts = first_parts(mid_line, exchange(*first_moves(mid_line)), x, y)
    full_mid = full_rows(mid_parts, exchange(*last_moves(mid_parts)), x, y)
    down_parts = first_parts(down_line, exchange(*first_moves(down_line)), x, y)
    full_out = full_mid[:, up_wide : up_wide + half_width]
    pairs = full_mid[:, up_wide + half_width :].reshape(chip_count, 64, 128)
    pairs = pairs[:, 0, :half_queries].astype(jnp.int32).reshape(1, query_total)
    row_lengths = lax.dynamic_index_in_dim(lengths, chip, 0, keepdims=False)
    segments = segments_of(row_lengths, token_count)
    seg_row, spans = segments[None, :], token_spans(row_lengths, token_count)
    query_span = NQ_ROW * QLEN
    bounds = tile_bounds(row_lengths, token_count)
    no_bias = jnp.zeros((1, quarter), F32)
    qkv_bias = jnp.concatenate(
        [
            part
            for g in range(2)
            for part in (
                bias[:, g * quarter : (g + 1) * quarter],
                no_bias,
                bias[:, half_width + g * quarter : half_width + (g + 1) * quarter],
            )
        ],
        axis=1,
    )
    qkv = (dot(row, full_qkv) + qkv_bias).astype(BF)
    mixed, lse = attend(bounds, tie(qkv, down_line), spans)

    def row_sum(left, weight_t, transposed):
        times = contract_cols if transposed else dot
        theirs = swap(times(left(1), weight_t).astype(BF), "c")
        return times(left(0), weight_t) + theirs.astype(F32)

    def mixed_half(which):
        return rows_of(mixed, other_start if which else own_start, share)

    other_attn = swap(contract_cols(mixed_half(1), full_out).astype(BF), "c")
    other_attn, second_norm = lax.optimization_barrier(
        (other_attn, jnp.stack([gains[1], shifts[1]]))
    )
    second_norm = swap(second_norm, "c")
    second_norm, *down_parts = lax.optimization_barrier((second_norm,) + tuple(down_parts))
    down_got = exchange(*last_moves(down_parts))
    attn_sum = contract_cols(mixed_half(0), full_out) + other_attn.astype(F32)
    own_tokens = rows_of(row, own_start, share).astype(F32)
    normed, unit_one, rstd_one = norm_forward(
        own_tokens + attn_sum + b_out.astype(F32), gains[0], shifts[0]
    )
    normed_low = normed.astype(BF)
    normed_all = jnp.concatenate([normed_low, swap(normed_low, "c")], axis=0)
    activation, slope = expand(
        normed_all, full_mid, bias[:, 2 * half_width :], 0, up_wide // 256
    )
    full_down = full_rows(down_parts, down_got, x, y)
    ffn_sum = row_sum(
        lambda which: activation[which * share : (which + 1) * share], full_down, True
    )
    result, unit_two, rstd_two = norm_forward(
        normed + ffn_sum + b_down.astype(F32), second_norm[0], second_norm[1]
    )
    result_low = result.astype(BF)
    embed = dot(result_low, w_proj).astype(BF)

    other_embed = swap(embed, "c")
    row_embed = jnp.where(
        c == 0,
        jnp.concatenate([embed, other_embed], axis=0),
        jnp.concatenate([other_embed, embed], axis=0),
    )
    half_span = query_span // 2
    own_queries = rows_of(row_embed, c * half_span, half_span)
    chips = ("z", "x", "y")
    queries = lax.all_to_all(
        jnp.broadcast_to(own_queries[None], (chip_count,) + own_queries.shape), chips, 0, 0
    ).reshape(chip_count * half_span, -1)
    queries, own_cot = lax.optimization_barrier((queries, lax.ppermute(cot, CORES, TURN)))
    proj_width = w_proj.shape[1]
    cuts = (proj_width, 3 * proj_width // 4, proj_width // 2)
    sums = pool(cuts, query_span, queries, row_embed, seg_row)
    doc_sizes = jnp.tile(row_lengths.astype(F32), 3)[:, None]
    group = (
        jnp.arange(query_total * QLEN, dtype=jnp.int32)[:, None] // QLEN
        == jnp.arange(query_total, dtype=jnp.int32)[None, :]
    ).astype(F32)
    pooled = POOL_TEMP * jnp.log(sums / doc_sizes)
    logits = jnp.dot(pooled, group, precision=FULL_PRECISION) / LOSS_TEMP
    logits = logits.reshape(3, NDOC, query_total)
    doc_numbers = chip * NDOC + jnp.arange(NDOC, dtype=jnp.int32)
    picked = (doc_numbers[:, None] == pairs).astype(F32)
    own_high = jnp.max(logits, axis=1)
    own_lse = own_high + jnp.log(jnp.sum(jnp.exp(logits - own_high[:, None]), axis=1))
    own_target = jnp.sum(logits * picked, axis=1)
    notes = jnp.pad(jnp.concatenate([own_lse, own_target], axis=1), ((0, 5), (0, 0)))
    notes = lax.all_to_all(
        jnp.broadcast_to(notes[None], (chip_count,) + notes.shape), chips, 0, 0
    )
    chip_lse = notes[:, :3, :query_total]
    high = jnp.max(chip_lse, axis=0)
    all_lse = high + jnp.log(jnp.sum(jnp.exp(chip_lse - high), axis=0))
    target = jnp.sum(notes[:, :3, query_total:], axis=0)
    losses = jnp.sum(all_lse - target, axis=0).reshape(chip_count, half_queries)
    grad_logits = (jnp.exp(logits - all_lse[:, None]) - picked) / LOSS_TEMP
    coefficient = (
        lax.dot_general(
            grad_logits.reshape(3 * NDOC, query_total),
            group,
            (((1,), (1,)), ((), ())),
            precision=FULL_PRECISION,
        )
        / sums
    )
    query_grad, doc_grad = pool_back(cuts, query_span, queries, row_embed, seg_row, coefficient)
    query_grad, y_out = lax.optimization_barrier(
        (query_grad, lax.ppermute(result_low, CORES, TURN))
    )
    grad_blocks = lax.all_to_all(
        query_grad.reshape(chip_count, half_span, proj_width), chips, 0, 0
    )
    own_query_grad = jnp.sum(grad_blocks.astype(F32), axis=0)
    row_grad = jnp.concatenate([jnp.zeros((query_span, proj_width), F32), doc_grad], axis=0)
    row_grad = lax.dynamic_update_slice_in_dim(row_grad, own_query_grad, c * half_span, 0)
    grad_embed = rows_of(row_grad, own_start, share) + swap(
        rows_of(row_grad, other_start, share), "c"
    )

    proj_low = w_proj
    grad_embed_low = grad_embed.astype(BF)
    grad_embed_rest = (grad_embed - grad_embed_low.astype(F32)).astype(BF)
    grad_result = own_cot.astype(F32) + (
        contract_cols(grad_embed_low, proj_low) + contract_cols(grad_embed_rest, proj_low)
    )
    proj_grad = contract_rows(result_low, grad_embed_low) + contract_rows(
        result_low, grad_embed_rest
    )
    gain_two = jnp.sum(grad_result * unit_two, axis=0)
    shift_two = jnp.sum(grad_result, axis=0)
    grad_second = norm_backward(grad_result, unit_two, rstd_two, second_norm[0])
    grad_ffn = grad_second.astype(BF)
    down_bias = jnp.sum(grad_ffn.astype(F32), axis=0)
    other_ffn = swap(grad_ffn, "c")
    grad_ffn_all = jnp.concatenate([grad_ffn, other_ffn], axis=0)
    down_blocks = blocks_of(grad_ffn_all, activation)
    down_moved = exchange(*sum_moves(down_blocks, x, y))
    grad_up = (dot(grad_ffn_all, full_down) * slope.astype(F32)).astype(BF)
    up_bias = jnp.sum(grad_up.astype(F32), axis=0)
    up_blocks = blocks_of(normed_all, tie(grad_up, *down_moved))
    full_up = full_mid[:, :up_wide]
    grad_normed = (
        row_sum(lambda which: grad_up[which * share : (which + 1) * share], full_up, True)
        + grad_second
    )
    gain_one = jnp.sum(grad_normed * unit_one, axis=0)
    shift_one = jnp.sum(grad_normed, axis=0)
    grad_first = norm_backward(grad_normed, unit_one, rstd_one, gains[0])
    grad_attn = grad_first.astype(BF)
    out_bias = jnp.sum(grad_attn.astype(F32), axis=0)
    other_attn = swap(grad_attn, "c")
    grad_attn_all = jnp.where(
        c == 0,
        jnp.concatenate([grad_attn, other_attn], axis=0),
        jnp.concatenate([other_attn, grad_attn], axis=0),
    )
    grad_mixed = dot(grad_attn_all, full_out).astype(BF)
    out_blocks = blocks_of(grad_attn_all, mixed)
    down_parts = sum_parts(down_blocks, down_moved, x, y)
    moved = exchange(*line_moves(down_parts, x, y), *sum_moves(up_blocks, x, y))
    down_line = line_of(down_parts, moved, x, y)
    up_parts = sum_parts(up_blocks, moved[2:], x, y)
    grad_mixed, out_blocks, down_line, *up_parts = lax.optimization_barrier(
        (grad_mixed, out_blocks, down_line) + tuple(up_parts)
    )
    moved = exchange(
        near_move(down_line, z), *line_moves(up_parts, x, y), *sum_moves(out_blocks, x, y)
    )
    grads_one, sums_one = attend_back(bounds, 0, qkv, mixed, grad_mixed, lse, spans)
    down_pair = near_sum(down_line, moved[0], z)
    up_line = line_of(up_parts, moved[1:], x, y)
    out_parts = sum_parts(out_blocks, moved[3:], x, y)
    grad_mixed, down_pair, up_line, *out_parts = lax.optimization_barrier(
        (grad_mixed, down_pair, up_line) + tuple(out_parts)
    )
    up_line, losses = lax.optimization_barrier((up_line, losses))
    moved = exchange(
        far_move(down_pair, z), near_move(up_line, z), *line_moves(out_parts, x, y)
    )
    other_losses = swap(losses, "c")
    proj_given, other_losses, grad_mixed = lax.optimization_barrier(
        (rows_of(proj_grad, other_start, share), other_losses, grad_mixed)
    )
    proj_half = rows_of(proj_grad, own_start, share)
    other_proj = swap(proj_given, "c")
    grad_mixed, other_proj = lax.optimization_barrier((grad_mixed, other_proj))
    proj_half = proj_half + other_proj
    losses = jnp.where(c == y, losses, other_losses)
    loss_out = rows_of(losses, 4 * z + 2 * x + c, 1)
    grads_two, sums_two = attend_back(bounds, 1, qkv, mixed, grad_mixed, lse, spans)
    down_part = far_sum(down_pair, moved[0], z)
    up_pair = near_sum(up_line, moved[1], z)
    out_line = line_of(out_parts, moved[2:], x, y)
    grads_one, grads_two, down_part, up_pair, out_line = lax.optimization_barrier(
        (grads_one, grads_two, down_part, up_pair, out_line)
    )
    shared = jnp.stack([gain_one, gain_two, shift_one, shift_two, out_bias, down_bias])
    half_sums = jnp.concatenate(
        [
            sums_one[0],
            sums_two[0],
            sums_one[1],
            sums_two[1],
            up_bias,
        ]
    )
    small = jnp.concatenate([shared.reshape(-1, 128), half_sums.reshape(-1, 128), proj_half])

    qkv_blocks = jnp.concatenate(
        [blocks_of(row, grads_one), blocks_of(row, grads_two)], axis=4
    )
    qkv_blocks, up_pair, out_line, down_part, small = lax.optimization_barrier(
        (qkv_blocks, up_pair, out_line, down_part, small)
    )
    moved = exchange(
        *sum_moves(qkv_blocks, x, y),
        far_move(up_pair, z),
        near_move(out_line, z),
        (small.astype(BF), "z", NEAR),
    )
    qkv_parts = sum_parts(qkv_blocks, moved, x, y)
    up_part = far_sum(up_pair, moved[2], z)
    out_pair = near_sum(out_line, moved[3], z)
    small = small + moved[4].astype(F32)

    def input_terms(start):
        return contract_cols(
            rows_of(grads_one, start, share), full_qkv[:, : 3 * quarter]
        ) + contract_cols(rows_of(grads_two, start, share), full_qkv[:, 3 * quarter :])

    other_terms = swap(input_terms(other_start).astype(BF), "c")
    grad_input = (input_terms(own_start) + other_terms.astype(F32) + grad_first).astype(BF)
    moved = exchange(*line_moves(qkv_parts, x, y), far_move(out_pair, z), (small.astype(BF), "z", FAR))
    qkv_line = line_of(qkv_parts, moved, x, y)
    out_part = far_sum(out_pair, moved[2], z)
    small = small + moved[3].astype(F32)
    moved = exchange(
        near_move(qkv_line, z),
        (small.astype(BF), "x", SWAP),
        (tie(grad_input, qkv_line), CORES, TURN),
    )
    qkv_pair = near_sum(qkv_line, moved[0], z)
    small = small + moved[1].astype(F32)
    grad_input = moved[2]
    ffn_part = jnp.concatenate([down_part, up_part], axis=1).astype(BF)
    moved = exchange(
        far_move(qkv_pair, z), (tie(ffn_part, qkv_pair), CORES, TURN)
    )
    (other_side,) = exchange((small.astype(BF), "y", SWAP))
    attn_part = jnp.concatenate([far_sum(qkv_pair, moved[0], z), out_part], axis=1).astype(BF)
    small = small + other_side.astype(F32)
    ffn_part = moved[1].astype(F32)
    down_part, up_part = ffn_part[:, :up_wide], ffn_part[:, up_wide:]
    (attn_part,) = exchange((attn_part, CORES, TURN))
    (other_small,) = exchange((small.astype(BF), "c", SWAP))
    attn_part = attn_part.astype(F32)
    other_small = other_small.astype(F32)
    qkv_part, out_part = attn_part[:, : 3 * half_width], attn_part[:, 3 * half_width :]
    shared_rows = 6 * width // 128
    small_rows = small.shape[0] - share
    shared = (small[:shared_rows] + other_small[:shared_rows]).reshape(6, width)
    half_sums = jnp.where(
        c == y, small[shared_rows:small_rows], other_small[shared_rows:small_rows]
    ).reshape(-1)
    proj_sum = pair_up(small[small_rows:], other_small[small_rows:], c, 0).reshape(width, -1)
    qkv_part = qkv_part.reshape(64, 2, 3, quarter).transpose(2, 0, 1, 3).reshape(3, 64, half_width)
    return (
        y_out,
        loss_out,
        grad_input,
        qkv_part,
        half_sums[: 2 * half_width].reshape(2, half_width),
        out_part.T,
        shared[4],
        shared[0:2],
        shared[2:4],
        up_part,
        half_sums[2 * half_width :],
        down_part.T,
        shared[5],
        proj_sum,
    )


IN_SPECS = (
    P("dp", None),
    P(),
    P("dp", "tensor"),
    P(None, "dp", "tensor"),
    P(None, "tensor"),
    P("tensor", "dp"),
    P(),
    P(),
    P(),
    P("dp", "tensor"),
    P("tensor"),
    P("tensor", "dp"),
    P(),
    P(),
    P(("dp", "tensor"), None),
)
OUT_SPECS = (
    P(("dp", "tensor"), None),
    P("dp", "tensor"),
    P(("dp", "tensor"), None),
    P(None, "dp", "tensor"),
    P(None, "tensor"),
    P("tensor", "dp"),
    P(),
    P(),
    P(),
    P("dp", "tensor"),
    P("tensor"),
    P("tensor", "dp"),
    P(),
    P(),
)


def solution(mesh):
    if mesh.devices.shape != (16, 2):
        return jax.shard_map(
            local, mesh=mesh, in_specs=IN_SPECS, out_specs=OUT_SPECS, check_vma=False
        )
    names = {"dp": ("z", "x", "c"), "tensor": ("y",)}

    def respec(spec):
        parts = []
        for entry in spec:
            axes = () if entry is None else entry if isinstance(entry, tuple) else (entry,)
            parts.append(tuple(name for axis in axes for name in names[axis]) or None)
        return P(*parts)

    chips = Mesh(mesh.devices.reshape(4, 2, 2, 2), ("z", "x", "c", "y"))
    return jax.shard_map(
        local_chip,
        mesh=chips,
        in_specs=tuple(respec(spec) for spec in IN_SPECS),
        out_specs=tuple(respec(spec) for spec in OUT_SPECS),
        check_vma=False,
    )
```
